32 devices in a mesh: batch: 4 (over y, x), seq: 8 (over z, core).
Axes of the slice: x: 2, y: 2, z: 4, core: 2. Of those that a mesh axis runs over, the one named last changes fastest.
Arguments:
- layer_input: bfloat16 [4, 1024, 768], P('batch', 'seq'), may hold values from -6 to 6
- segment_ids: int32 [4, 1024], P('batch', 'seq'), may hold values from 0 to 3, never falling along the last dimension, each value on 1 to 640 neighbouring positions
- w_query: bfloat16 [768, 768], P('seq', 'batch'), may hold values from -0.21875 to 0.21875
- w_key: bfloat16 [768, 768], P('seq', 'batch'), may hold values from -0.21875 to 0.21875
- w_value: bfloat16 [768, 768], P('seq', 'batch'), may hold values from -0.21875 to 0.21875
- w_mix: bfloat16 [768, 768], P('seq', 'batch'), may hold values from -3.5 to 3.5
- rel_table: bfloat16 [512, 768], P('seq', 'batch'), may hold values from -6 to 6
- attn_biases: bfloat16 [4, 768], P(None, 'seq'), may hold values from -3 to 3
- norm_gains: bfloat16 [2, 768], P(None, 'seq'), may hold values from 0.5 to 1.5
- norm_shifts: bfloat16 [2, 768], P(None, 'seq'), may hold values from -3 to 3
- w_up: bfloat16 [768, 3072], P(None, 'seq'), may hold values from -0.21875 to 0.21875
- up_bias: bfloat16 [3072], P('seq'), may hold values from -3 to 3
- w_down: bfloat16 [3072, 768], P('seq'), may hold values from -0.109375 to 0.109375
- down_bias: bfloat16 [768], P('seq'), may hold values from -3 to 3
- out_grad: bfloat16 [4, 1024, 768], P('batch', 'seq'), may hold values from -6 to 6
Outputs:
- layer_output: bfloat16 [4, 1024, 768], P('batch', 'seq')
- input_grad: float32 [4, 1024, 768], P('batch', 'seq')
- query_grad: float32 [768, 768], P('seq', 'batch')
- key_grad: float32 [768, 768], P('seq', 'batch')
- value_grad: float32 [768, 768], P('seq', 'batch')
- mix_grad: float32 [768, 768], P('seq', 'batch')
- table_grad: float32 [512, 768], P('seq', 'batch')
- bias_grad: float32 [4, 768], P(None, 'seq')
- gain_grad: float32 [2, 768], P(None, 'seq')
- shift_grad: float32 [2, 768], P(None, 'seq')
- up_grad: float32 [768, 3072], P('batch', 'seq')
- up_bias_grad: float32 [3072], P('seq')
- down_grad: float32 [3072, 768], P('seq', 'batch')
- down_bias_grad: float32 [768], P('seq')
The draws below stay inside these ranges and needn't reach their ends.
Inputs may be any that keep to these rules, and one draw needn't show every extreme that they name: `segment_ids`: within a row the ids never fall; each id marks one document of 1 to 640 tokens, and a document of exactly that many tokens occurs.
All inputs are finite; a program needn't handle non-finite values.
Results may differ from the reference program's by a relative error of at most 0.014.
Values may be sent and summed in bfloat16 or wider, within the bound.
A program may use at most 256 MiB of HBM per device.

```python
import math
import jax
import jax.numpy as jnp
import numpy as np
from jax import lax

D = 768
DH = 64
FF = 3072
SPAN = 256
L = 1024
ROWS = 4
BUCKETS = 512


def level_of(stream_key, extent, cuts, low, largest):
    def one(position, shards_of):
        heights = jax.random.uniform(jax.random.fold_in(jax.random.fold_in(stream_key, 6), position), (shards_of,), jnp.float32, low / len(cuts), largest / len(cuts))
        return jnp.repeat(jnp.exp(heights), extent[position] // shards_of).reshape((-1,) + (1,) * (len(extent) - position - 1))

    factor_of = one(*cuts[0])
    for cut in cuts[1:]:
        factor_of = factor_of * one(*cut)
    return factor_of


def split_up(number_of, total, bound, slope):
    portions = [(1 << 20) // math.isqrt(grade ** slope) + 1 for grade in range(2, number_of + 1)]
    spare, counts = total - bound - (number_of - 1), [1] * (number_of - 1)
    while spare > 0:
        movable = [i for i in range(number_of - 1) if counts[i] < bound]
        pool, left = sum([portions[i] for i in movable]), spare
        for i in movable:
            more = min(bound - counts[i], max(1, left * portions[i] // pool), spare)
            counts[i] = counts[i] + more
            spare = spare - more
    return np.array([bound] + counts)


def ragged(stream_key, amount, total, reach, skew):
    if amount == 2:
        one = jax.random.randint(stream_key, (), max(1, total - reach), min(reach, total - 1) + 1)
        return jnp.stack([one, total - one])
    tallies = jnp.asarray(split_up(amount, total, reach, skew), jnp.int32)
    pairs = (amount - 1) // 2
    giver, receiver = tallies[1:1 + 2 * pairs:2], tallies[2:2 + 2 * pairs:2]
    slack = jnp.minimum(giver - 1, reach - receiver)
    passed = jax.random.randint(jax.random.fold_in(stream_key, 1), (pairs,), 0, 1 << 20) % (slack + 1)
    tallies = tallies.at[1:1 + 2 * pairs:2].set(giver - passed).at[2:2 + 2 * pairs:2].set(receiver + passed)
    return tallies[jax.random.permutation(jax.random.fold_in(stream_key, 2), amount)]


def bell_draw(rng, dims, width, limit, cuts=(), kind=jnp.bfloat16):
    factor_of = level_of(rng, dims, cuts, -0.22, 0.18) if cuts else 1.0
    entries = jax.random.normal(rng, dims, jnp.float32) * width * factor_of
    return jnp.minimum(jnp.maximum(entries, -limit), limit).astype(kind)


def setup_inputs(seed: int = 0) -> dict:
    streams_of = jax.random.split(jax.random.key(seed), 16)
    layer_input = bell_draw(streams_of[0], (ROWS, L, D), 1.0, 6.0, ((0, 4), (1, 8)))
    segment_ids = jax.vmap(lambda own: jnp.searchsorted(jnp.cumsum(ragged(own, 4, L, L // 2 + L // 8, 2)), jnp.arange(L), side="right"))(jax.random.split(streams_of[1], ROWS)).reshape((ROWS, L)).astype(jnp.int32)
    w_query = bell_draw(streams_of[2], (D, D), D ** -0.5, 0.21875, ((0, 8), (1, 4)))
    w_key = bell_draw(streams_of[3], (D, D), D ** -0.5, 0.21875, ((0, 8), (1, 4)))
    w_value = bell_draw(streams_of[4], (D, D), D ** -0.5, 0.21875, ((0, 8), (1, 4)))
    w_mix = bell_draw(streams_of[5], (D, D), (max(1, D // 256)) ** -0.5, 3.5, ((0, 8), (1, 4)))
    rel_table = bell_draw(streams_of[6], (BUCKETS, D), 1.0, 6.0, ((0, 8), (1, 4)))
    attn_biases = bell_draw(streams_of[7], (4, D), 0.5, 3.0, ((1, 8),))
    norm_gains = jnp.clip(1.0 + 0.1 * jax.random.normal(streams_of[8], (2, D), jnp.float32), 0.5, 1.5).astype(jnp.bfloat16)
    norm_shifts = bell_draw(streams_of[9], (2, D), 0.5, 3.0, ((1, 8),))
    w_up = bell_draw(streams_of[10], (D, FF), D ** -0.5, 0.21875, ((1, 8),))
    up_bias = bell_draw(streams_of[11], (FF,), 0.5, 3.0, ((0, 8),))
    w_down = bell_draw(streams_of[12], (FF, D), FF ** -0.5, 0.109375, ((0, 8),))
    down_bias = bell_draw(streams_of[13], (D,), 0.5, 3.0, ((0, 8),))
    out_grad = bell_draw(streams_of[14], (ROWS, L, D), 1.0, 6.0, ((0, 4), (1, 8)))
    return dict(layer_input=layer_input, segment_ids=segment_ids, w_query=w_query, w_key=w_key, w_value=w_value, w_mix=w_mix, rel_table=rel_table, attn_biases=attn_biases, norm_gains=norm_gains, norm_shifts=norm_shifts, w_up=w_up, up_bias=up_bias, w_down=w_down, down_bias=down_bias, out_grad=out_grad)


masked_score = -1e+30
norm_eps = 1e-06

@jax.custom_vjp
def low(v):
    return lax.optimization_barrier(v.astype(jnp.bfloat16)).astype(jnp.float32)

@jax.custom_vjp
def low_back(v):
    return v

def low_keep(v):
    return (low(v), None)

def low_pass(kept, grad):
    return (grad,)

def back_keep(v):
    return (v, None)

def back_low(kept, grad):
    return (low(grad),)
low.defvjp(low_keep, low_pass)
low_back.defvjp(back_keep, back_low)

def matmul(left, right):
    return jnp.dot(left, right, precision=lax.Precision.HIGHEST, preferred_element_type=jnp.float32)

def normalize(values, gain, shift):
    average = lax.optimization_barrier(jnp.mean(values, axis=-1, keepdims=True))
    centered = values - average
    variance = lax.optimization_barrier(jnp.mean(centered * centered, axis=-1, keepdims=True))
    return centered * lax.rsqrt(variance + norm_eps) * gain + shift

def bucket_table(length):
    place = jnp.arange(length, dtype=jnp.int32)
    return (jnp.clip(place[:, None] - place[None, :], -SPAN, SPAN - 1) + SPAN).astype(jnp.int32)

def head_attend(head_item, buckets, same_doc, score_scale):
    queries, keys, values, query_rel, key_rel = head_item
    content = matmul(queries, keys.T)
    content_pos = jnp.take_along_axis(matmul(queries, key_rel.T), buckets, axis=1)
    pos_content = jnp.take_along_axis(matmul(keys, query_rel.T), buckets, axis=1).T
    scores = low_back(jnp.where(same_doc, (content + content_pos + pos_content) * score_scale, masked_score))
    highest = lax.optimization_barrier(jnp.max(scores, axis=-1, keepdims=True))
    exponent = jnp.exp(scores - highest)
    probs = exponent / lax.optimization_barrier(jnp.sum(exponent, axis=-1, keepdims=True))
    return matmul(low(probs), values)

def row_layer(row_tokens, row_segments, weights, query_rel, key_rel):
    w_query, w_key, w_value, w_mix, rel_table, biases, gains, shifts, w_up, up_bias, w_down, down_bias = weights
    length = row_tokens.shape[0]
    heads = w_query.shape[1] // DH
    queries = low_back(low(matmul(row_tokens, w_query) + biases[0]))
    keys = low_back(low(matmul(row_tokens, w_key) + biases[1]))
    values = low_back(low(matmul(row_tokens, w_value) + biases[2]))

    def split(matrix):
        return matrix.reshape(matrix.shape[0], heads, DH).transpose(1, 0, 2)
    buckets = bucket_table(length)
    same_doc = row_segments[:, None] == row_segments[None, :]
    score_scale = 1.0 / math.sqrt(3.0 * DH)

    def one_head(head_item):
        return head_attend(head_item, buckets, same_doc, score_scale)
    context = lax.map(jax.checkpoint(one_head), (split(queries), split(keys), split(values), split(query_rel), split(key_rel)))
    context = low_back(low(context.transpose(1, 0, 2).reshape(length, heads * DH)))
    hidden = normalize(row_tokens + low_back(matmul(context, w_mix)) + biases[3], gains[0], shifts[0])
    inner = low_back(matmul(low(hidden), w_up) + up_bias)
    act = low(jax.nn.gelu(inner, approximate=False))
    mixed = hidden + low_back(matmul(act, w_down)) + down_bias
    return normalize(mixed, gains[1], shifts[1])

def reference(layer_input, segment_ids, w_query, w_key, w_value, w_mix, rel_table, attn_biases, norm_gains, norm_shifts, w_up, up_bias, w_down, down_bias, out_grad):
    params = tuple((p.astype(jnp.float32) for p in (w_query, w_key, w_value, w_mix, rel_table, attn_biases, norm_gains, norm_shifts, w_up, up_bias, w_down, down_bias)))

    def forward(inputs, weights):
        query_rel = low(matmul(weights[4], weights[0]) + weights[5][0])
        key_rel = low(matmul(weights[4], weights[1]) + weights[5][1])

        def one_row(pair):
            return row_layer(pair[0], pair[1], weights, query_rel, key_rel)
        return lax.map(jax.checkpoint(one_row), (inputs, segment_ids))
    outputs, pullback = jax.vjp(forward, layer_input.astype(jnp.float32), params)
    input_grad, grads = pullback(out_grad.astype(jnp.float32))
    return (outputs.astype(jnp.bfloat16), input_grad, grads[0], grads[1], grads[2], grads[3], grads[4], grads[5], grads[6], grads[7], grads[8], grads[9], grads[10], grads[11])
```

```python
import math

import jax
import jax.numpy as jnp
from jax import lax
from jax.experimental import pallas as pl
from jax.experimental.pallas import tpu as pltpu
from jax.sharding import PartitionSpec as P

DH = 64


masked_score = -1e30
norm_eps = 1e-06
pair_heads = 2


def normalize(values, gain, shift):
    average = jnp.mean(values, axis=-1, keepdims=True)
    centered = values - average
    variance = jnp.mean(centered * centered, axis=-1, keepdims=True)
    return centered * lax.rsqrt(variance + norm_eps) * gain + shift


def exact_gelu(values):
    return jax.nn.gelu(values, approximate=False)


def split_heads(matrix):
    length, rows, width = matrix.shape
    groups = width // (pair_heads * DH)
    return matrix.reshape(length, rows, groups, pair_heads, DH).transpose(2, 1, 3, 0, 4)


def join_heads(matrix):
    groups, rows, pair, length, depth = matrix.shape
    return matrix.transpose(3, 1, 0, 2, 4).reshape(length, rows, groups * pair * depth)


def split_table(matrix):
    buckets, width = matrix.shape
    return matrix.reshape(buckets, width // (pair_heads * DH), pair_heads, DH).transpose(1, 2, 0, 3)


def join_table(matrix):
    groups, pair, buckets, depth = matrix.shape
    return matrix.transpose(2, 0, 1, 3).reshape(buckets, groups * pair * depth)


def table_ends(table):
    return jnp.stack([table[:, 0], table[:, -1]], axis=1)


def near_skew(table_prod, offset, full_len):
    lead = table_prod.shape[:-2]
    count, buckets = table_prod.shape[-2:]
    span = buckets // 2
    lead_pad = [(0, 0)] * len(lead)
    flipped = jnp.pad(table_prod[..., ::-1], lead_pad + [(0, 0), (0, count)])
    sheared = flipped.reshape(lead + (count * (buckets + count),))[
        ..., : count * (buckets + count - 1)
    ]
    sheared = sheared.reshape(lead + (count, buckets + count - 1))
    spread = jnp.pad(sheared, lead_pad + [(0, 0), (full_len, full_len)])
    band = lax.dynamic_slice_in_dim(
        spread, full_len + span - 1 - offset, full_len, axis=len(lead) + 1
    )
    distance = (offset + jnp.arange(count, dtype=jnp.int32))[:, None] - jnp.arange(
        full_len, dtype=jnp.int32
    )[None, :]
    return jnp.where(
        distance <= -span,
        table_prod[..., 0:1],
        jnp.where(distance >= span - 1, table_prod[..., buckets - 1 :], band),
    )


def far_place(cross, end_vals, offset, count, full_len):
    lead = cross.shape[:-2]
    band_len, buckets = cross.shape[-2:]
    span = buckets // 2
    lead_pad = [(0, 0)] * len(lead)
    turned = jnp.swapaxes(cross, -1, -2).reshape(lead + (buckets * band_len,))
    turned = jnp.pad(turned, lead_pad + [(0, buckets)])
    diagonal = turned.reshape(lead + (buckets, band_len + 1))[..., :count]
    aligned = jnp.pad(jnp.swapaxes(diagonal, -1, -2), lead_pad + [(0, 0), (0, count)])
    sheared = aligned.reshape(lead + (count * (buckets + count),))[
        ..., : count * (buckets + count - 1)
    ]
    sheared = sheared.reshape(lead + (count, buckets + count - 1))
    spread = jnp.pad(sheared, lead_pad + [(0, 0), (full_len, full_len)])
    band = lax.dynamic_slice_in_dim(spread, full_len + span - offset, full_len, axis=len(lead) + 1)
    distance = (
        jnp.arange(full_len, dtype=jnp.int32)[None, :]
        - (offset + jnp.arange(count, dtype=jnp.int32))[:, None]
    )
    return jnp.where(
        distance <= -span,
        end_vals[..., 0:1, :],
        jnp.where(distance >= span - 1, end_vals[..., 1:2, :], band),
    )


def band_rows(all_rows, offset, count, span):
    padded = jnp.pad(all_rows, [(0, 0), (0, 0), (span, span), (0, 0)])
    return lax.dynamic_slice_in_dim(padded, offset, count + 2 * span - 1, axis=2)


def unband(values, offset, full_len, span):
    lead = values.shape[:2]
    room = jnp.zeros(lead + (full_len + 2 * span, values.shape[3]), jnp.float32)
    placed = lax.dynamic_update_slice_in_dim(room, values, offset, axis=2)
    return placed[:, :, span : span + full_len]


def relative_scores(own_rows, all_rows, own_table, all_table, offset, full_len):
    count = own_rows.shape[2]
    content = jnp.einsum("rgid,rgjd->rgij", own_rows, all_rows, preferred_element_type=jnp.float32)
    own_prod = jnp.einsum("rgid,gbd->rgib", own_rows, own_table, preferred_element_type=jnp.float32)
    window = band_rows(all_rows, offset, count, all_table.shape[1] // 2)
    cross = jnp.einsum("rgmd,gbd->rgmb", window, all_table, preferred_element_type=jnp.float32)
    end_vals = jnp.einsum(
        "rgjd,ged->rgej", all_rows, table_ends(all_table), preferred_element_type=jnp.float32
    )
    near_vals, near_pull = jax.vjp(lambda product: near_skew(product, offset, full_len), own_prod)
    far_vals, far_pull = jax.vjp(
        lambda part, ends: far_place(part, ends, offset, count, full_len), cross, end_vals
    )
    return (content + near_vals + far_vals, near_pull, far_pull, window)


def end_columns(grad):
    return jnp.stack([grad[..., 0], grad[..., -1]], axis=2)


def end_terms(ends, table):
    return jnp.einsum(
        "rgei,ged->rgid",
        ends,
        table_ends(table),
        precision=lax.Precision.HIGHEST,
        preferred_element_type=jnp.float32,
    )


def end_rows(ends, rows_low):
    return jnp.einsum(
        "rgei,rgid->ged",
        ends,
        rows_low,
        precision=lax.Precision.HIGHEST,
        preferred_element_type=jnp.float32,
    )


def with_ends(inner_part, edge_rows):
    buckets = inner_part.shape[1]
    place = jnp.arange(buckets, dtype=jnp.int32)[None, :, None]
    return (
        inner_part
        + jnp.where(place == 0, edge_rows[:, 0:1], 0.0)
        + jnp.where(place == buckets - 1, edge_rows[:, 1:2], 0.0)
    )


BLOCK = 128


def dot_nn(a, b):
    return lax.dot_general(a, b, (((1,), (0,)), ((), ())), preferred_element_type=jnp.float32)


def dot_nt(a, b):
    return lax.dot_general(a, b, (((1,), (1,)), ((), ())), preferred_element_type=jnp.float32)


def dot_tn(a, b):
    return lax.dot_general(a, b, (((0,), (0,)), ((), ())), preferred_element_type=jnp.float32)


def turn_matrix(buckets):
    row = lax.broadcasted_iota(jnp.int32, (buckets, buckets), 0)
    col = lax.broadcasted_iota(jnp.int32, (buckets, buckets), 1)
    return (row + col == buckets - 1).astype(jnp.bfloat16)


def skew_band(product):
    count, buckets = product.shape
    row = lax.broadcasted_iota(jnp.int32, (count, BLOCK), 0)
    lane = lax.broadcasted_iota(jnp.int32, (count, BLOCK), 1)
    edge = jnp.where(row + lane <= BLOCK - 2, product[:, buckets - 1 :], product[:, 0:1])
    wide = jnp.concatenate([product, edge], axis=1)
    return pltpu.roll(wide, 1, 1, stride=1, stride_axis=0)


def skew_back(turned, buckets):
    return pltpu.roll(turned, turned.shape[1] - BLOCK, 1, stride=1, stride_axis=0)[:, :buckets]


def attend_kernel(
    first_ref,
    x_ref,
    w_ref,
    bias_ref,
    table_ref,
    segc_ref,
    segr_ref,
    q_ref,
    k_ref,
    v_ref,
    qrev_ref,
    krev_ref,
    p_ref,
    ctx_ref,
    place_ref,
    wide_ref,
    ends_ref,
    held_ref,
):
    full_len = x_ref.shape[0]
    buckets = table_ref.shape[0]
    blocks = full_len // BLOCK
    span = buckets // 2
    side = span // BLOCK
    band_width = buckets + BLOCK
    band_blocks = band_width // BLOCK
    group = 2 * DH
    scale = 1.0 / math.sqrt(3.0 * DH)
    units = p_ref.shape[0]
    proj = (dot_nn(x_ref[...], w_ref[...]) + bias_ref[...]).astype(jnp.bfloat16)
    rel = (dot_nn(table_ref[...], w_ref[:, : 2 * group]) + bias_ref[:, : 2 * group]).astype(
        jnp.bfloat16
    )
    rel = dot_nn(turn_matrix(buckets), rel).astype(jnp.bfloat16)
    for slot in range(2):
        lo, hi = slot * DH, (slot + 1) * DH
        q_ref[slot] = proj[:, lo:hi]
        k_ref[slot] = proj[:, group + lo : group + hi]
        v_ref[slot] = proj[:, 2 * group + lo : 2 * group + hi]
        qrev_ref[slot] = rel[:, lo:hi]
        krev_ref[slot] = rel[:, group + lo : group + hi]
    held_ref[...] = jnp.zeros_like(held_ref)
    for slot in range(2):
        ends_ref[slot, 0] = dot_nt(qrev_ref[slot, 0:16], k_ref[slot])
        ends_ref[slot, 1] = dot_nt(qrev_ref[slot, buckets - 16 : buckets], k_ref[slot])

        def key_block(kb, carry):
            rows = k_ref[slot, pl.ds(pl.multiple_of(kb * BLOCK, BLOCK), BLOCK)]
            band = skew_band(dot_nt(rows, qrev_ref[slot]))
            for e in range(band_blocks):
                place_ref[
                    slot,
                    kb + e,
                    :,
                    (band_blocks - 1 - e) * BLOCK : (band_blocks - e) * BLOCK,
                ] = band[:, e * BLOCK : (e + 1) * BLOCK].T
            return carry

        lax.fori_loop(0, blocks, key_block, 0)

    first = first_ref[0]

    def unit(u, carry):
        g = u + first
        slot = g // blocks
        qb = g % blocks
        start = pl.multiple_of(qb * BLOCK, BLOCK)
        rows = q_ref[slot, pl.ds(start, BLOCK)]
        own = dot_nt(rows, krev_ref[slot])
        band = skew_band(own) + place_ref[slot, qb + side]
        wide_ref[:, pl.ds(start, band_width)] = band
        content = dot_nt(rows, k_ref[slot])
        lane = lax.broadcasted_iota(jnp.int32, (BLOCK, full_len), 1)
        near = jnp.where(
            lane < start - span,
            own[:, 0:1] + ends_ref[slot, 1, 15:16],
            jnp.where(
                lane >= start + band_width - span,
                own[:, buckets - 1 :] + ends_ref[slot, 0, 0:1],
                wide_ref[:, span : span + full_len],
            ),
        )
        same = segc_ref[pl.ds(start, BLOCK)] == segr_ref[...]
        scores = jnp.where(same, (content + near) * scale, masked_score)
        highest = jnp.max(scores, axis=-1, keepdims=True)
        exponent = jnp.exp(scores - highest)
        total = jnp.sum(exponent, axis=-1, keepdims=True)
        probs = (exponent / total).astype(jnp.bfloat16)
        p_ref[u] = probs
        held_ref[slot, pl.ds(start, BLOCK)] = dot_nn(probs, v_ref[slot]).astype(jnp.bfloat16)
        return carry

    lax.fori_loop(0, units, unit, 0)
    ctx_ref[...] = jnp.concatenate([held_ref[0], held_ref[1]], axis=1)


def attend(first, x_all, w_cat, bias_cat, table, seg_col, seg_row):
    full_len, width = x_all.shape
    buckets = table.shape[0]
    blocks = full_len // BLOCK
    units = 3 * blocks // 2
    band_width = buckets + BLOCK
    low, wide = jnp.bfloat16, jnp.float32
    pad_blocks = blocks + band_width // BLOCK - 1
    return pl.pallas_call(
        attend_kernel,
        out_shape=(
            jax.ShapeDtypeStruct((2, full_len, DH), low),
            jax.ShapeDtypeStruct((2, full_len, DH), low),
            jax.ShapeDtypeStruct((2, full_len, DH), low),
            jax.ShapeDtypeStruct((2, buckets, DH), low),
            jax.ShapeDtypeStruct((2, buckets, DH), low),
            jax.ShapeDtypeStruct((units, BLOCK, full_len), low),
            jax.ShapeDtypeStruct((full_len, 2 * DH), low),
        ),
        in_specs=[pl.BlockSpec(memory_space=pltpu.SMEM)]
        + [pl.BlockSpec(memory_space=pltpu.VMEM)] * 6,
        out_specs=[pl.BlockSpec(memory_space=pltpu.VMEM)] * 7,
        scratch_shapes=[
            pltpu.VMEM((2, pad_blocks, BLOCK, band_width), wide),
            pltpu.VMEM((BLOCK, full_len + buckets), wide),
            pltpu.VMEM((2, 2, 16, full_len), wide),
            pltpu.VMEM((2, full_len, DH), low),
        ],
        compiler_params=pltpu.CompilerParams(vmem_limit_bytes=60 * 1024 * 1024),
        name="attend",
    )(first, x_all, w_cat, bias_cat, table, seg_col, seg_row)


def attend_back_kernel(
    first_ref,
    q_ref,
    k_ref,
    v_ref,
    qrev_ref,
    krev_ref,
    p_ref,
    dctx_ref,
    dcat_ref,
    rel_ref,
    sum_ref,
    heads_ref,
    wide_ref,
    low_ref,
    place_ref,
    dq_ref,
    dkt_ref,
    dvt_ref,
    far_ref,
    dkr_ref,
    dqr_ref,
):
    full_len = q_ref.shape[1]
    buckets = qrev_ref.shape[1]
    blocks = full_len // BLOCK
    span = buckets // 2
    side = span // BLOCK
    band_width = buckets + BLOCK
    band_blocks = band_width // BLOCK
    scale = 1.0 / math.sqrt(3.0 * DH)
    units = p_ref.shape[0]
    for ref in (wide_ref, low_ref, place_ref, dq_ref, dkt_ref, dvt_ref, far_ref, dkr_ref, dqr_ref):
        ref[...] = jnp.zeros_like(ref)
    for slot in range(2):
        heads_ref[slot] = dctx_ref[:, slot * DH : (slot + 1) * DH]
    first = first_ref[0]
    turn = turn_matrix(BLOCK)
    place8 = lax.broadcasted_iota(jnp.int32, (8, full_len), 0)

    def unit(u, carry):
        g = u + first
        slot = g // blocks
        qb = g % blocks
        start = pl.multiple_of(qb * BLOCK, BLOCK)
        rows = q_ref[slot, pl.ds(start, BLOCK)]
        grad = heads_ref[slot, pl.ds(start, BLOCK)]
        probs = p_ref[u]
        wide_probs = probs.astype(jnp.float32)
        prob_grad = dot_nt(grad, v_ref[slot])
        inner = jnp.sum(wide_probs * prob_grad, axis=-1, keepdims=True)
        low_grad = (wide_probs * (prob_grad - inner)).astype(jnp.bfloat16)
        score_grad = low_grad.astype(jnp.float32)
        wide_ref[:, span : span + full_len] = dot_nn(turn, low_grad)
        low_ref[:, span : span + full_len] = low_grad
        dvt_ref[slot] += dot_tn(grad, probs)
        dkt_ref[slot] += dot_tn(rows, low_grad)
        row = lax.broadcasted_iota(jnp.int32, (BLOCK, full_len), 0)
        lane = lax.broadcasted_iota(jnp.int32, (BLOCK, full_len), 1)
        gap = lane - row - start
        right = jnp.where(gap > span, score_grad, 0.0)
        left = jnp.where(gap < 1 - span, score_grad, 0.0)
        end_right = jnp.sum(right, axis=-1, keepdims=True)
        end_left = jnp.sum(left, axis=-1, keepdims=True)
        far_right = jnp.sum(jnp.where(gap >= span, score_grad, 0.0), axis=0, keepdims=True)
        far_left = jnp.sum(jnp.where(gap < -span, score_grad, 0.0), axis=0, keepdims=True)
        far_ref[slot] += jnp.where(place8 == 0, far_right, jnp.where(place8 == 1, far_left, 0.0))
        band = wide_ref[:, pl.ds(start, band_width)]
        near = dot_nn(turn, skew_back(band, buckets).astype(jnp.bfloat16))
        bucket = lax.broadcasted_iota(jnp.int32, (BLOCK, buckets), 1)
        near = near + jnp.where(
            bucket == 0, end_left, jnp.where(bucket == buckets - 1, end_right, 0.0)
        )
        near_low = near.astype(jnp.bfloat16)
        dq = dot_nn(low_grad, k_ref[slot]) + dot_nn(near_low, krev_ref[slot])
        dq_ref[slot, pl.ds(start, BLOCK)] = dq
        dkr_ref[slot] += dot_tn(rows, near_low)
        for e in range(band_blocks):
            keys_at = pl.multiple_of(start + e * BLOCK, BLOCK)
            place_ref[
                slot, qb + e, :, (band_blocks - 1 - e) * BLOCK : (band_blocks - e) * BLOCK
            ] = dot_nt(turn, low_ref[:, pl.ds(keys_at, BLOCK)])
        return carry

    lax.fori_loop(0, units, unit, 0)
    parts_q, parts_k, parts_v = [], [], []
    parts_r = [None] * 4
    for slot in range(2):
        far_low = far_ref[slot].astype(jnp.bfloat16)
        mark = lax.broadcasted_iota(jnp.int32, (8, DH), 0)
        ends = jnp.where(
            mark == 0,
            qrev_ref[slot, 0:1].astype(jnp.float32),
            jnp.where(mark == 1, qrev_ref[slot, buckets - 1 : buckets].astype(jnp.float32), 0.0),
        ).astype(jnp.bfloat16)
        end_keys = dot_tn(ends, far_low)
        end_rows = dot_nn(far_low, k_ref[slot])

        whole_k = (dkt_ref[slot] + end_keys).T

        def key_side(kb, carry):
            start = pl.multiple_of(kb * BLOCK, BLOCK)
            far = skew_back(place_ref[slot, kb + side], buckets).astype(jnp.bfloat16)
            far = dot_nn(turn, far).astype(jnp.bfloat16)
            keys = k_ref[slot, pl.ds(start, BLOCK)]
            dqr_ref[slot] += dot_tn(keys, far)
            dq_ref[2 + slot, pl.ds(start, BLOCK)] = dot_nn(far, qrev_ref[slot])
            return carry

        lax.fori_loop(0, blocks, key_side, 0)
        parts_q.append((dq_ref[slot] * scale).astype(jnp.bfloat16))
        parts_k.append(((dq_ref[2 + slot] + whole_k) * scale).astype(jnp.bfloat16))
        parts_v.append(dvt_ref[slot].T.astype(jnp.bfloat16))
        bucket = lax.broadcasted_iota(jnp.int32, (buckets, DH), 0)
        qr = dqr_ref[slot].T + jnp.where(
            bucket == 0, end_rows[0:1], jnp.where(bucket == buckets - 1, end_rows[1:2], 0.0)
        )
        dqr_out = qr * scale
        dkr_out = dkr_ref[slot].T * scale
        parts_r[slot] = dqr_out
        parts_r[2 + slot] = dkr_out
    dcat = jnp.concatenate(parts_q + parts_k + parts_v, axis=1)
    dcat_ref[...] = dcat
    rel = jnp.concatenate(parts_r, axis=1)
    rel_ref[...] = dot_nn(turn_matrix(buckets), rel.astype(jnp.bfloat16)).astype(jnp.bfloat16)
    rel_sum = jnp.sum(rel, axis=0, keepdims=True)
    rel_sum = jnp.concatenate([rel_sum, jnp.zeros((1, 2 * DH), jnp.float32)], axis=1)
    sum_ref[...] = jnp.sum(dcat.astype(jnp.float32), axis=0, keepdims=True) + rel_sum


def attend_back(first, q, k, v, qrev, krev, probs, dctx):
    full_len = q.shape[1]
    buckets = qrev.shape[1]
    blocks = full_len // BLOCK
    band_width = buckets + BLOCK
    low, wide = jnp.bfloat16, jnp.float32
    pad_blocks = blocks + band_width // BLOCK - 1
    return pl.pallas_call(
        attend_back_kernel,
        out_shape=(
            jax.ShapeDtypeStruct((full_len, 6 * DH), low),
            jax.ShapeDtypeStruct((buckets, 4 * DH), low),
            jax.ShapeDtypeStruct((1, 6 * DH), wide),
        ),
        in_specs=[pl.BlockSpec(memory_space=pltpu.SMEM)]
        + [pl.BlockSpec(memory_space=pltpu.VMEM)] * 7,
        out_specs=[pl.BlockSpec(memory_space=pltpu.VMEM)] * 3,
        scratch_shapes=[
            pltpu.VMEM((2, full_len, DH), low),
            pltpu.VMEM((BLOCK, full_len + buckets), wide),
            pltpu.VMEM((BLOCK, full_len + buckets), low),
            pltpu.VMEM((2, pad_blocks, BLOCK, band_width), wide),
            pltpu.VMEM((4, full_len, DH), wide),
            pltpu.VMEM((2, DH, full_len), wide),
            pltpu.VMEM((2, DH, full_len), wide),
            pltpu.VMEM((2, 8, full_len), wide),
            pltpu.VMEM((2, DH, buckets), wide),
            pltpu.VMEM((2, DH, buckets), wide),
        ],
        compiler_params=pltpu.CompilerParams(vmem_limit_bytes=60 * 1024 * 1024),
        name="attend_back",
    )(first, q, k, v, qrev, krev, probs, dctx)


MESH = pl.DeviceIdType.MESH
VMEM_SPEC = pl.BlockSpec(memory_space=pltpu.VMEM)
ANY_SPEC = pl.BlockSpec(memory_space=pl.ANY)


class Place:
    def __init__(self):
        self.batches = lax.axis_size("batch")
        self.tokens = lax.axis_size("seq")
        self.chips = self.tokens // 2
        self.row = lax.axis_index("batch")
        self.part = lax.axis_index("seq")
        self.chip = self.part // 2
        self.core = self.part % 2

    def along_chips(self, k):
        chip = lax.rem(self.chip + k, self.chips)
        return chip, (self.row, 2 * chip + self.core)

    def from_chips(self, k):
        return lax.rem(self.chip + self.chips - k, self.chips)

    def partner(self):
        return (self.row, self.part + 1 - 2 * self.core)

    def along_rows(self, k):
        row = lax.rem(self.row + k, self.batches)
        return row, (row, self.part)

    def from_rows(self, k):
        return lax.rem(self.row + self.batches - k, self.batches)

    def along_seq(self, k):
        part = lax.rem(self.part + k, self.tokens)
        return part, (self.row, part)

    def along_plane(self, k):
        index = lax.rem(2 * self.row + self.core + k, 2 * self.batches)
        row, core = index // 2, index % 2
        return row, core, (row, 2 * self.chip + core)

    def chip_peers(self):
        return [self.along_chips(k)[1] for k in range(1, self.chips)]

    def row_peers(self):
        return [self.along_rows(k)[1] for k in range(1, self.batches)]

    def cross_peers(self):
        other = self.part + 1 - 2 * self.core
        return [(self.along_rows(k)[0], other) for k in range(1, self.batches)]

    def seq_peers(self):
        return [self.along_seq(k)[1] for k in range(1, self.tokens)]

    def plane_peers(self):
        return [self.along_plane(k)[2] for k in range(1, 2 * self.batches)]


def meet(peers):
    barrier = pltpu.get_barrier_semaphore()
    for peer in peers:
        pl.semaphore_signal(barrier, inc=1, device_id=peer, device_id_type=MESH)
    pl.semaphore_wait(barrier, len(peers))


class Wires:
    def __init__(self, send_sems, recv_sems, local_sems):
        self.sems = (send_sems, recv_sems, local_sems)
        self.used = [0, 0]
        self.ends = []

    def send(self, src, dst, peer):
        k = self.used[0]
        self.used[0] += 1
        copy = pltpu.make_async_remote_copy(
            src_ref=src,
            dst_ref=dst,
            send_sem=self.sems[0].at[k],
            recv_sem=self.sems[1].at[k],
            device_id=peer,
            device_id_type=MESH,
        )
        copy.start()
        self.ends.append(copy.wait_send)
        return copy

    def local(self, src, dst):
        k = self.used[1]
        self.used[1] += 1
        copy = pltpu.make_async_copy(src, dst, self.sems[2].at[k])
        copy.start()
        return copy

    def finish(self):
        for end in self.ends:
            end()


def wire_scratch(sends, locals_count):
    return [
        pltpu.SemaphoreType.DMA((sends,)),
        pltpu.SemaphoreType.DMA((sends,)),
        pltpu.SemaphoreType.DMA((locals_count,)),
    ]


def comm_call(kernel, name, ident, out_shapes, inputs, sends, locals_count, scratch=()):
    return pl.pallas_call(
        kernel,
        out_shape=tuple(out_shapes),
        in_specs=[VMEM_SPEC] * len(inputs),
        out_specs=tuple([ANY_SPEC] * len(out_shapes)),
        scratch_shapes=list(scratch) + wire_scratch(sends, locals_count),
        compiler_params=pltpu.CompilerParams(
            collective_id=ident, has_side_effects=True, vmem_limit_bytes=40 * 1024 * 1024
        ),
        name=name,
    )(*inputs)


def like(array, *lead):
    return jax.ShapeDtypeStruct(tuple(lead) + tuple(array.shape), array.dtype)


def gather_kernel(
    x_ref, qkv_ref, mt_ref, vec_ref, up_ref, down_ref,
    xs_ref, qkvs_ref, mts_ref, vecs_ref, up2_ref, down2_ref, *sems,
):
    at = Place()
    wires = Wires(*sems)
    b, s, z, c = at.row, at.part, at.chip, at.core
    off_diagonal = b != z
    turned = (z, 2 * b + c)
    barrier = pltpu.get_barrier_semaphore()
    peers = at.chip_peers() + at.plane_peers()
    for peer in peers:
        pl.semaphore_signal(barrier, inc=1, device_id=peer, device_id_type=MESH)

    @pl.when(off_diagonal)
    def _():
        pl.semaphore_signal(barrier, inc=1, device_id=turned, device_id_type=MESH)

    pl.semaphore_wait(barrier, len(peers) + off_diagonal.astype(jnp.int32))

    k = wires.used[0]
    wires.used[0] += 1
    swap = pltpu.make_async_remote_copy(
        src_ref=qkv_ref,
        dst_ref=qkvs_ref.at[2 * z + c],
        send_sem=sems[0].at[k],
        recv_sem=sems[1].at[k],
        device_id=turned,
        device_id_type=MESH,
    )
    stay = pltpu.make_async_copy(qkv_ref, qkvs_ref.at[2 * b + c], sems[2].at[0])
    wires.used[1] += 1

    @pl.when(off_diagonal)
    def _():
        swap.start()

    @pl.when(jnp.logical_not(off_diagonal))
    def _():
        stay.start()

    mt_sends = []
    for k in range(1, at.chips):
        peer = at.along_chips(k)[1]
        mt_sends.append(wires.send(mt_ref, mts_ref.at[c, b, z], peer))
    x_sends, vec_sends = [], []
    for k in range(1, at.chips):
        peer = at.along_chips(k)[1]
        x_sends.append(wires.send(x_ref, xs_ref.at[s], peer))
        vec_sends.append(wires.send(vec_ref, vecs_ref.at[s], peer))
    own = [
        wires.local(x_ref, xs_ref.at[s]),
        wires.local(mt_ref, mts_ref.at[c, b, z]),
        wires.local(vec_ref, vecs_ref.at[s]),
    ]
    last = [
        wires.send(x_ref, xs_ref.at[s], at.partner()),
        wires.send(vec_ref, vecs_ref.at[s], at.partner()),
        wires.send(up_ref, up2_ref, at.partner()),
        wires.send(down_ref, down2_ref, at.partner()),
    ]

    @pl.when(off_diagonal)
    def _():
        swap.wait_recv()

    @pl.when(jnp.logical_not(off_diagonal))
    def _():
        stay.wait()

    for k in range(1, 2 * at.batches):
        peer = at.along_plane(k)[2]
        last.append(wires.send(qkvs_ref.at[2 * b + c], qkvs_ref.at[2 * b + c], peer))
    for copy in mt_sends:
        copy.wait_recv()
    for copy in own:
        copy.wait()
    row_sends = []
    for k in range(1, at.batches):
        peer = at.along_rows(k)[1]
        row_sends.append(wires.send(mts_ref.at[c, b], mts_ref.at[c, b], peer))
    last.append(wires.send(mts_ref.at[c, b], mts_ref.at[c, b], at.partner()))
    for k in range(1, at.batches):
        row = at.from_rows(k)
        row_sends[k - 1].wait_recv()
        last.append(wires.send(mts_ref.at[c, row], mts_ref.at[c, row], at.partner()))
    for k in range(1, at.chips):
        index = 2 * at.from_chips(k) + c
        x_sends[k - 1].wait_recv()
        last.append(wires.send(xs_ref.at[index], xs_ref.at[index], at.partner()))
        vec_sends[k - 1].wait_recv()
        last.append(wires.send(vecs_ref.at[index], vecs_ref.at[index], at.partner()))
    for copy in last:
        copy.wait_recv()
    wires.finish()

    @pl.when(off_diagonal)
    def _():
        swap.wait_send()


def gather_inputs(x, qkv, mt, vec, up, down):
    tokens, batches = lax.axis_size("seq"), lax.axis_size("batch")
    chips = tokens // 2
    outs = (
        like(x, tokens),
        like(qkv, tokens),
        like(mt, 2, batches, chips),
        like(vec, tokens),
        like(up),
        like(down),
    )
    sends = 1 + 3 * (chips - 1) + 4 + 2 * batches - 1 + 2 * (batches - 1) + 1 + 2 * (chips - 1)
    return comm_call(
        gather_kernel, "gather_inputs", 0, outs, (x, qkv, mt, vec, up, down), sends, 4
    )


def swap_kernel(src_ref, dst_ref, *sems):
    at = Place()
    wires = Wires(*sems)
    meet(at.seq_peers())
    copies = []
    for k in range(1, at.tokens):
        part, peer = at.along_seq(k)
        copies.append(wires.send(src_ref.at[part], dst_ref.at[at.part], peer))
    own = wires.local(src_ref.at[at.part], dst_ref.at[at.part])
    for copy in copies:
        copy.wait_recv()
    own.wait()
    wires.finish()


def swap_seq(blocks, ident):
    tokens = lax.axis_size("seq")
    return comm_call(
        swap_kernel, "swap_seq", ident, (like(blocks),), (blocks,), tokens - 1, 1
    )[0]


def class_gather_kernel(src_ref, dst_ref, *sems):
    at = Place()
    wires = Wires(*sems)
    meet(at.chip_peers())
    copies = [
        wires.send(src_ref, dst_ref.at[at.chip], at.along_chips(k)[1])
        for k in range(1, at.chips)
    ]
    own = wires.local(src_ref, dst_ref.at[at.chip])
    for copy in copies:
        copy.wait_recv()
    own.wait()
    wires.finish()


def class_gather(block, ident):
    chips = lax.axis_size("seq") // 2
    return comm_call(
        class_gather_kernel, "class_gather", ident, (like(block, chips),), (block,), chips - 1, 1
    )[0]


def class_scatter_kernel(src_ref, dst_ref, *sems):
    at = Place()
    wires = Wires(*sems)
    meet(at.chip_peers())
    copies = []
    for k in range(1, at.chips):
        chip, peer = at.along_chips(k)
        copies.append(wires.send(src_ref.at[chip], dst_ref.at[at.chip], peer))
    own = wires.local(src_ref.at[at.chip], dst_ref.at[at.chip])
    for copy in copies:
        copy.wait_recv()
    own.wait()
    wires.finish()


def class_scatter(blocks, ident):
    chips = lax.axis_size("seq") // 2
    return comm_call(
        class_scatter_kernel, "class_scatter", ident, (like(blocks),), (blocks,), chips - 1, 1
    )[0]


def plane_sends(at, wires, src_ref, dst_ref):
    mine = 2 * at.row + at.core
    copies = []
    for k in range(1, 2 * at.batches):
        row, core, peer = at.along_plane(k)
        other = lax.rem(core + at.core, 2)
        copies.append(wires.send(src_ref.at[other, row], dst_ref.at[mine], peer))
    return copies, wires.local(src_ref.at[0, at.row], dst_ref.at[mine])


def spread_kernel(src_ref, up_ref, upb_ref, dst_ref, ups_ref, upbs_ref, *sems):
    at = Place()
    wires = Wires(*sems)
    meet(at.chip_peers() + at.plane_peers())
    copies = [
        wires.send(src_ref, dst_ref.at[at.part], at.along_chips(k)[1])
        for k in range(1, at.chips)
    ]
    last = [wires.send(src_ref, dst_ref.at[at.part], at.partner())]
    own = [wires.local(src_ref, dst_ref.at[at.part])]
    for src, dst in ((up_ref, ups_ref), (upb_ref, upbs_ref)):
        more, kept = plane_sends(at, wires, src, dst)
        last += more
        own.append(kept)
    for k in range(1, at.chips):
        index = 2 * at.from_chips(k) + at.core
        copies[k - 1].wait_recv()
        last.append(wires.send(dst_ref.at[index], dst_ref.at[index], at.partner()))
    for copy in last:
        copy.wait_recv()
    for copy in own:
        copy.wait()
    wires.finish()


def spread_grads(block, up, upb, ident):
    tokens, batches = lax.axis_size("seq"), lax.axis_size("batch")
    chips = tokens // 2
    outs = (
        like(block, tokens),
        jax.ShapeDtypeStruct((2 * batches,) + up.shape[2:], up.dtype),
        jax.ShapeDtypeStruct((2 * batches,) + upb.shape[2:], upb.dtype),
    )
    sends = 2 * (chips - 1) + 1 + 2 * (2 * batches - 1)
    return comm_call(spread_kernel, "spread_grads", ident, outs, (block, up, upb), sends, 3)


def reduce_kernel(
    in_ref, vec_ref, dw_ref, tab_ref, mix_ref,
    ins_ref, vecs_ref, dws_ref, tabs_ref, mixs_ref, half_ref, sum_ref, *sems,
):
    at = Place()
    wires = Wires(*sems)
    meet(at.seq_peers() + at.row_peers())
    c = at.core
    halves = [
        wires.send(in_ref.at[chip, 1 - c], half_ref.at[chip], at.partner())
        for chip in range(at.chips)
    ]
    last, own = [], []
    for k in range(1, at.batches):
        row, peer = at.along_rows(k)
        for src, dst in ((dw_ref, dws_ref), (tab_ref, tabs_ref), (mix_ref, mixs_ref)):
            last.append(wires.send(src.at[row], dst.at[at.row], peer))
    for src, dst in ((dw_ref, dws_ref), (tab_ref, tabs_ref), (mix_ref, mixs_ref)):
        own.append(wires.local(src.at[at.row], dst.at[at.row]))
    for k in range(1, at.tokens):
        part, peer = at.along_seq(k)
        last.append(wires.send(vec_ref.at[part], vecs_ref.at[at.part], peer))
    own.append(wires.local(vec_ref.at[at.part], vecs_ref.at[at.part]))
    for copy in halves:
        copy.wait_recv()
    sum_ref[...] = (
        in_ref[:, c].astype(jnp.float32) + half_ref[...].astype(jnp.float32)
    ).astype(jnp.bfloat16)
    for k in range(1, at.chips):
        chip, peer = at.along_chips(k)
        last.append(wires.send(sum_ref.at[chip], ins_ref.at[at.chip], peer))
    own.append(wires.local(sum_ref.at[at.chip], ins_ref.at[at.chip]))
    for copy in last:
        copy.wait_recv()
    for copy in own:
        copy.wait()
    wires.finish()


def reduce_grads(in_part, vec, dw, tab, mix, ident):
    tokens, batches = lax.axis_size("seq"), lax.axis_size("batch")
    chips = tokens // 2
    half = (chips,) + in_part.shape[2:]
    outs = (jax.ShapeDtypeStruct(half, in_part.dtype), like(vec), like(dw), like(tab), like(mix))
    sends = chips + 3 * (batches - 1) + tokens - 1 + chips - 1
    return comm_call(
        reduce_kernel,
        "reduce_grads",
        ident,
        outs,
        (in_part, vec, dw, tab, mix),
        sends,
        5,
        scratch=(pltpu.VMEM(half, in_part.dtype), pltpu.VMEM(half, in_part.dtype)),
    )


def settle_kernel(
    dw_ref, tab_ref, mix_ref, vec_ref, down_ref,
    dws_ref, tabs_ref, mixs_ref, vecs_ref, downs_ref, *sems,
):
    at = Place()
    wires = Wires(*sems)
    b, z, c = at.row, at.chip, at.core
    off_diagonal = b != z
    same, cross = (z, 2 * b + c), (z, 2 * b + 1 - c)
    peers = at.seq_peers() + at.row_peers() + at.cross_peers()
    barrier = pltpu.get_barrier_semaphore()
    for peer in peers:
        pl.semaphore_signal(barrier, inc=1, device_id=peer, device_id_type=MESH)

    @pl.when(off_diagonal)
    def _():
        pl.semaphore_signal(barrier, inc=1, device_id=same, device_id_type=MESH)
        pl.semaphore_signal(barrier, inc=1, device_id=cross, device_id_type=MESH)

    pl.semaphore_wait(barrier, len(peers) + 2 * off_diagonal.astype(jnp.int32))

    k = wires.used[0]
    wires.used[0] += 1
    move = pltpu.make_async_remote_copy(
        src_ref=dw_ref.at[c],
        dst_ref=dws_ref.at[c],
        send_sem=sems[0].at[k],
        recv_sem=sems[1].at[k],
        device_id=same,
        device_id_type=MESH,
    )
    stay = pltpu.make_async_copy(dw_ref.at[c], dws_ref.at[c], sems[2].at[0])
    wires.used[1] += 1

    @pl.when(off_diagonal)
    def _():
        move.start()

    @pl.when(jnp.logical_not(off_diagonal))
    def _():
        stay.start()

    last, own = [wires.send(dw_ref.at[1 - c], dws_ref.at[c], cross)], []
    for k in range(1, at.tokens):
        part, peer = at.along_seq(k)
        last.append(wires.send(tab_ref.at[part], tabs_ref.at[at.part], peer))
    own.append(wires.local(tab_ref.at[at.part], tabs_ref.at[at.part]))
    last.append(wires.send(mix_ref, mixs_ref, at.partner()))
    for k in range(1, at.batches):
        last.append(wires.send(vec_ref, vecs_ref.at[b], at.along_rows(k)[1]))
    own.append(wires.local(vec_ref, vecs_ref.at[b]))
    more, kept = plane_sends(at, wires, down_ref, downs_ref)
    last += more
    own.append(kept)
    for copy in last:
        copy.wait_recv()
    for copy in own:
        copy.wait()
    wires.finish()

    @pl.when(off_diagonal)
    def _():
        move.wait()

    @pl.when(jnp.logical_not(off_diagonal))
    def _():
        stay.wait()


def settle_grads(dw, tab, mix, vec, down, ident):
    tokens, batches = lax.axis_size("seq"), lax.axis_size("batch")
    outs = (
        like(dw),
        like(tab),
        like(mix),
        like(vec, batches),
        jax.ShapeDtypeStruct((2 * batches,) + down.shape[2:], down.dtype),
    )
    sends = 2 + tokens - 1 + 1 + batches - 1 + 2 * batches - 1
    return comm_call(
        settle_kernel, "settle_grads", ident, outs, (dw, tab, mix, vec, down), sends, 4
    )


def fits_fast(layer_input, table_shard, w_query):
    rows, local_len, width = layer_input.shape
    tokens, batches = lax.axis_size("seq"), lax.axis_size("batch")
    return (
        rows == 1
        and local_len == BLOCK
        and tokens == 2 * batches
        and width == 3 * DH * batches
        and (table_shard.shape[0] * tokens) % (4 * BLOCK) == 0
        and tokens % 4 == 0
    )


def fast_body(
    layer_input, segment_ids, w_query, w_key, w_value, w_mix, rel_table, attn_biases,
    norm_gains, norm_shifts, w_up, up_bias, w_down, down_bias, out_grad,
):
    local_len, width = layer_input.shape[1:]
    at = Place()
    tokens, batches, chips = at.tokens, at.batches, at.chips
    full_len = local_len * tokens
    low, wide = jnp.bfloat16, jnp.float32
    pair = 2 * DH
    shard_rows, shard_cols = w_query.shape
    table_rows = rel_table.shape[0]
    lanes = attn_biases.shape[1]
    hidden_here = w_up.shape[1]
    x = layer_input[0]

    pack = jnp.concatenate([attn_biases, norm_gains, norm_shifts, down_bias[None]], axis=0)
    pack = jnp.pad(pack, ((0, 0), (0, BLOCK - lanes)))
    pack = jnp.concatenate(
        [pack, segment_ids.astype(low), up_bias.reshape(hidden_here // BLOCK, BLOCK)], axis=0
    )
    used = pack.shape[0]
    pack = jnp.pad(pack, ((0, 16 - used), (0, 0)))
    qkv = jnp.stack([w_query, w_key, w_value])
    mt = jnp.concatenate([w_mix, rel_table], axis=0)
    x_all, qkv_all, mt_all, vec_all, up_other, down_other = gather_inputs(
        x, qkv, mt, pack, w_up, w_down
    )
    x_all = x_all.reshape(full_len, width)
    vecs = vec_all[:, :9, :lanes].transpose(1, 0, 2).reshape(9, width)
    biases, gains, shifts = vecs[0:4], vecs[4:6].astype(wide), vecs[6:8].astype(wide)
    bias_down = vecs[8]
    seg = vec_all[:, 9].reshape(full_len).astype(wide)
    other_vec = lax.dynamic_index_in_dim(
        vec_all, at.part + 1 - 2 * at.core, axis=0, keepdims=False
    )
    bias_up = jnp.concatenate([up_bias, other_vec[10:used].reshape(hidden_here)])
    column = at.core * DH
    wcols = qkv_all.transpose(0, 2, 1, 3).reshape(width, 3, shard_cols)
    w_cat = lax.dynamic_slice_in_dim(wcols, column, pair, axis=2).reshape(width, 3 * pair)
    first_col = at.chip * shard_cols + column
    bias_cat = (
        lax.dynamic_slice_in_dim(biases[:3], first_col, pair, axis=1)
        .reshape(1, 3 * pair)
        .astype(wide)
    )
    m_mix = mt_all[..., :shard_rows, :].transpose(2, 0, 3, 1, 4).reshape(width, width)
    table = (
        mt_all[..., shard_rows:, :].transpose(2, 0, 3, 1, 4).reshape(tokens * table_rows, width)
    )

    first = (at.core * (full_len // BLOCK // 2)).astype(jnp.int32).reshape(1)
    q, k, v, qrev, krev, probs, ctx = attend(
        first, x_all, w_cat, bias_cat, table, seg[:, None], seg[None, :]
    )
    got = swap_seq(ctx.reshape(tokens, local_len, pair), 1)
    got = got.reshape(chips, 2, local_len, pair)
    left, right = got[:, 0], got[:, 1]
    context = jnp.concatenate(
        [left[..., :DH], left[..., DH:] + right[..., :DH], right[..., DH:]], axis=-1
    )
    context_low = context.transpose(1, 0, 2).reshape(local_len, width)
    pre_norm = (
        x.astype(wide) + jnp.dot(context_low, m_mix, preferred_element_type=wide) + biases[3]
    )
    hidden, norm1_pull = jax.vjp(normalize, pre_norm, gains[0], shifts[0])
    hidden_rows = class_gather(hidden.astype(low), 2).reshape(chips * local_len, width)
    up_pair = jnp.concatenate([w_up, up_other], axis=1)
    down_pair = jnp.concatenate([w_down, down_other], axis=0)
    inner = jnp.dot(hidden_rows, up_pair, preferred_element_type=wide) + bias_up
    act, gelu_pull = jax.vjp(exact_gelu, inner)
    act_low = act.astype(low)
    ffn_part = jnp.dot(act_low, down_pair, preferred_element_type=wide).astype(low)
    ffn_parts = class_scatter(ffn_part.reshape(chips, local_len, width), 3)
    mixed = hidden + jnp.sum(ffn_parts.astype(wide), axis=0) + bias_down
    output, norm2_pull = jax.vjp(normalize, mixed, gains[1], shifts[1])
    mixed_grad, gain2_grad, shift2_grad = norm2_pull(out_grad[0].astype(wide))
    grad_rows = class_gather(mixed_grad.astype(low), 4).reshape(chips * local_len, width)
    act_grad = jnp.einsum("nd,fd->nf", grad_rows, down_pair, preferred_element_type=wide)
    inner_low = gelu_pull(act_grad)[0].astype(low)
    back_part = jnp.einsum("nf,df->nd", inner_low, up_pair, preferred_element_type=wide).astype(
        low
    )
    back_parts = class_scatter(back_part.reshape(chips, local_len, width), 5)
    hidden_grad = mixed_grad + jnp.sum(back_parts.astype(wide), axis=0)
    pre_grad, gain1_grad, shift1_grad = norm1_pull(hidden_grad)
    up_part = jnp.einsum(
        "nd,nkf->kdf",
        hidden_rows,
        inner_low.reshape(-1, 2, hidden_here),
        preferred_element_type=wide,
    ).astype(low)
    up_part = up_part.reshape(2, batches, width // batches, hidden_here)
    upb_part = jnp.sum(inner_low.astype(wide), axis=0).reshape(2, 1, 1, hidden_here)
    upb_part = jnp.broadcast_to(upb_part, (2, batches, 8, hidden_here))
    down_part = jnp.einsum(
        "nkf,nge->kgfe",
        act_low.reshape(-1, 2, hidden_here),
        grad_rows.reshape(-1, batches, width // batches),
        preferred_element_type=wide,
    ).astype(low)
    attn_all, up_parts, upb_parts = spread_grads(pre_grad.astype(low), up_part, upb_part, 6)
    attn_all = attn_all.reshape(full_len, width)
    mix_rows = lax.dynamic_slice_in_dim(m_mix, first_col, pair, axis=0)
    context_grad = jnp.einsum(
        "ne,de->nd", attn_all, mix_rows, preferred_element_type=wide
    ).astype(low)
    dcat, rel_grad, col_sums = attend_back(first, q, k, v, qrev, krev, probs, context_grad)
    in_part = jnp.einsum("ne,de->nd", dcat, w_cat, preferred_element_type=wide).astype(low)
    in_part = in_part.reshape(chips, 2, local_len, width)
    dw_part = jnp.einsum("nd,ne->de", x_all, dcat, preferred_element_type=wide)
    dw_rel = jnp.einsum("bd,be->de", table, rel_grad, preferred_element_type=wide)
    dw_part = dw_part + jnp.pad(dw_rel, ((0, 0), (0, pair)))
    dw_part = dw_part.astype(low).reshape(batches, width // batches, 3 * pair)
    tab_part = jnp.einsum(
        "be,gde->gbd",
        rel_grad,
        w_cat[:, : 2 * pair].reshape(batches, width // batches, 2 * pair),
        preferred_element_type=wide,
    ).astype(low)
    mix_part = jnp.einsum(
        "nk,nge->gke",
        ctx,
        attn_all.reshape(full_len, batches, width // batches),
        preferred_element_type=wide,
    ).astype(low)
    bias_rows = lax.dynamic_update_slice(
        jnp.zeros((3, width), wide), col_sums.reshape(3, pair), (jnp.int32(0), first_col)
    )
    vec_part = jnp.concatenate(
        [
            bias_rows,
            jnp.sum(pre_grad, axis=0)[None],
            gain1_grad[None],
            gain2_grad[None],
            shift1_grad[None],
            shift2_grad[None],
            jnp.sum(mixed_grad, axis=0)[None],
        ],
        axis=0,
    )
    vec_part = jnp.pad(
        vec_part.reshape(9, tokens, lanes).transpose(1, 0, 2), ((0, 0), (0, 7), (0, BLOCK - lanes))
    )
    ins, vec_parts, dws, tabs, mixs = reduce_grads(in_part, vec_part, dw_part, tab_part, mix_part, 7)
    input_grad = pre_grad + jnp.sum(ins.astype(wide), axis=0)
    dw_sum = jnp.sum(dws.astype(wide), axis=0).astype(low)
    tab_sum = jnp.sum(tabs.astype(wide), axis=0).astype(low)
    mix_sum = jnp.sum(mixs.astype(wide), axis=0).astype(low)
    vec_sum = jnp.sum(vec_parts, axis=0)
    dw_got, tab_got, mix_other, vec_got, downs = settle_grads(
        dw_sum.reshape(2, shard_rows, 3 * pair),
        tab_sum.reshape(tokens, table_rows, shard_cols),
        mix_sum,
        vec_sum,
        down_part,
        8,
    )
    dw_got = dw_got.astype(wide).reshape(2, shard_rows, 3, pair)
    dw_all = jnp.pad(dw_got[0], ((0, 0), (0, 0), (0, DH))) + jnp.pad(
        dw_got[1], ((0, 0), (0, 0), (DH, 0))
    )
    table_grad = jnp.sum(tab_got.astype(wide), axis=0)
    mix_own, mix_other = mix_sum.astype(wide), mix_other.astype(wide)
    lower = jnp.where(at.core == 0, mix_own, mix_other)
    upper = jnp.where(at.core == 0, mix_other, mix_own)
    mix_grad = jnp.pad(lower, ((0, DH), (0, 0))) + jnp.pad(upper, ((DH, 0), (0, 0)))
    mix_grad = lax.dynamic_slice_in_dim(mix_grad, at.core * shard_rows, shard_rows, axis=0)
    small = jnp.sum(vec_got, axis=0)[:, :lanes]
    return (
        output.astype(low)[None],
        input_grad[None],
        dw_all[:, 0],
        dw_all[:, 1],
        dw_all[:, 2],
        mix_grad,
        table_grad,
        small[0:4],
        small[4:6],
        small[6:8],
        jnp.sum(up_parts.astype(wide), axis=0),
        jnp.sum(upb_parts[:, 0], axis=0),
        jnp.sum(downs.astype(wide), axis=0),
        small[8],
    )


def body(
    layer_input,
    segment_ids,
    w_query,
    w_key,
    w_value,
    w_mix,
    rel_table,
    attn_biases,
    norm_gains,
    norm_shifts,
    w_up,
    up_bias,
    w_down,
    down_bias,
    out_grad,
):
    if fits_fast(layer_input, rel_table, w_query):
        return fast_body(
            layer_input, segment_ids, w_query, w_key, w_value, w_mix, rel_table, attn_biases,
            norm_gains, norm_shifts, w_up, up_bias, w_down, down_bias, out_grad,
        )
    rows, local_len, width = layer_input.shape
    full_len = local_len * lax.axis_size("seq")
    tokens_here = local_len * rows
    highest_prec = lax.Precision.HIGHEST
    parts = (
        lax.all_gather(w_query, "batch", axis=1, tiled=True),
        lax.all_gather(w_key, "batch", axis=1, tiled=True),
        lax.all_gather(w_value, "batch", axis=1, tiled=True),
        lax.all_gather(w_mix, "batch", axis=1, tiled=True),
        lax.all_gather(rel_table, "batch", axis=1, tiled=True),
    )
    whole = (
        lax.all_gather(parts[0], "seq", axis=0, tiled=True),
        lax.all_gather(parts[1], "seq", axis=0, tiled=True),
        lax.all_gather(parts[2], "seq", axis=0, tiled=True),
        lax.all_gather(parts[3], "seq", axis=0, tiled=True),
        lax.all_gather(parts[4], "seq", axis=0, tiled=True),
        lax.all_gather(attn_biases, "seq", axis=1, tiled=True),
        lax.all_gather(norm_gains, "seq", axis=1, tiled=True),
        lax.all_gather(norm_shifts, "seq", axis=1, tiled=True),
        lax.all_gather(down_bias, "seq", axis=0, tiled=True),
    )
    m_query, m_key, m_value, m_mix, table, biases, gains, shifts, bias_down = whole
    flat_input = jnp.swapaxes(layer_input, 0, 1).reshape(tokens_here, width)
    queries = (jnp.dot(flat_input, m_query, preferred_element_type=jnp.float32) + biases[0]).astype(
        jnp.bfloat16
    )
    keys_here = (jnp.dot(flat_input, m_key, preferred_element_type=jnp.float32) + biases[1]).astype(
        jnp.bfloat16
    )
    values_here = (
        jnp.dot(flat_input, m_value, preferred_element_type=jnp.float32) + biases[2]
    ).astype(jnp.bfloat16)
    query_rel = (jnp.dot(table, m_query, preferred_element_type=jnp.float32) + biases[0]).astype(
        jnp.bfloat16
    )
    key_rel = (jnp.dot(table, m_key, preferred_element_type=jnp.float32) + biases[1]).astype(
        jnp.bfloat16
    )
    local_seg = jnp.swapaxes(segment_ids, 0, 1).astype(jnp.bfloat16)
    keys_all, values_all, seg_all = (
        lax.all_gather(keys_here.reshape(local_len, rows, width), "seq", axis=0, tiled=True),
        lax.all_gather(values_here.reshape(local_len, rows, width), "seq", axis=0, tiled=True),
        lax.all_gather(local_seg, "seq", axis=0, tiled=True),
    )
    buckets = table.shape[0]
    offset = lax.axis_index("seq") * local_len
    bucket_iota = jnp.arange(buckets, dtype=jnp.int32)
    inner_cols = (bucket_iota > 0) & (bucket_iota < buckets - 1)
    same_doc = (
        jnp.swapaxes(local_seg, 0, 1)[:, None, :, None]
        == jnp.swapaxes(seg_all, 0, 1)[:, None, None, :]
    )
    score_scale = 1.0 / math.sqrt(3.0 * DH)
    head_queries = split_heads(queries.reshape(local_len, rows, width))
    head_keys = split_heads(keys_all)
    head_values = split_heads(values_all)
    rel_queries = split_table(query_rel)
    rel_keys = split_table(key_rel)

    def forward_group(carry, group):
        g_query, g_key, g_value, g_qrel, g_krel = group
        total, near_pull, far_pull, window = relative_scores(
            g_query, g_key, g_krel, g_qrel, offset, full_len
        )
        scores = jnp.where(same_doc, total * score_scale, masked_score)
        highest = jnp.max(scores, axis=-1, keepdims=True)
        exponent = jnp.exp(scores - highest)
        denominator = jnp.sum(exponent, axis=-1, keepdims=True)
        weights_low = (exponent / denominator).astype(jnp.bfloat16)
        context = jnp.einsum(
            "rgij,rgjd->rgid", weights_low, g_value, preferred_element_type=jnp.float32
        )
        return (carry, (context, (highest + jnp.log(denominator))[..., 0]))

    unused, (context_groups, log_totals) = lax.scan(
        forward_group, None, (head_queries, head_keys, head_values, rel_queries, rel_keys)
    )
    context_low = join_heads(context_groups).reshape(tokens_here, width).astype(jnp.bfloat16)
    pre_norm = (
        flat_input.astype(jnp.float32)
        + jnp.dot(context_low, m_mix, preferred_element_type=jnp.float32)
        + biases[3]
    )
    hidden, norm1_pull = jax.vjp(
        normalize, pre_norm, gains[0].astype(jnp.float32), shifts[0].astype(jnp.float32)
    )
    hidden_low = hidden.astype(jnp.bfloat16)

    def spread_rows(rows_low):
        return lax.all_gather(rows_low, "seq", axis=0, tiled=True)

    def hidden_sums(make_term):
        return lax.psum_scatter(
            make_term(jnp.int32(0), tokens_here * lax.axis_size("seq")),
            "seq",
            scatter_dimension=0,
            tiled=True,
        )

    hidden_rows = spread_rows(hidden_low)
    inner = jnp.dot(hidden_rows, w_up, preferred_element_type=jnp.float32) + up_bias
    act, gelu_pull = jax.vjp(exact_gelu, inner)
    act_low = act.astype(jnp.bfloat16)

    def down_rows(start, count):
        return jnp.dot(act_low, w_down, preferred_element_type=jnp.float32)

    ffn_result = hidden_sums(down_rows)
    mixed = hidden + ffn_result + bias_down
    output, norm2_pull = jax.vjp(
        normalize, mixed, gains[1].astype(jnp.float32), shifts[1].astype(jnp.float32)
    )
    flat_grad = jnp.swapaxes(out_grad, 0, 1).reshape(tokens_here, width).astype(jnp.float32)
    mixed_grad, gain2_grad, shift2_grad = norm2_pull(flat_grad)
    ffn_grad_low = mixed_grad.astype(jnp.bfloat16)
    grad_rows = spread_rows(ffn_grad_low)
    act_grad = jnp.einsum("nd,fd->nf", grad_rows, w_down, preferred_element_type=jnp.float32)
    inner_low = gelu_pull(act_grad)[0].astype(jnp.bfloat16)
    up_part = jnp.einsum("nd,nf->df", hidden_rows, inner_low, preferred_element_type=jnp.float32)
    upb_part = jnp.sum(inner_low.astype(jnp.float32), axis=0)
    down_part = jnp.einsum("nf,nd->fd", act_low, grad_rows, preferred_element_type=jnp.float32)

    def back_rows(start, count):
        return jnp.einsum("nf,df->nd", inner_low, w_up, preferred_element_type=jnp.float32)

    hidden_grad = mixed_grad + hidden_sums(back_rows)
    pre_grad, gain1_grad, shift1_grad = norm1_pull(hidden_grad)
    attn_low = pre_grad.astype(jnp.bfloat16)
    mix_whole = jnp.einsum("nd,ne->de", context_low, attn_low, preferred_element_type=jnp.float32)
    context_grad = jnp.einsum(
        "ne,de->nd", attn_low, m_mix, preferred_element_type=jnp.float32
    ).astype(jnp.bfloat16)
    head_context_grad = split_heads(context_grad.reshape(local_len, rows, width))

    def query_side(group):
        g_query, g_key, g_value, g_qrel, g_krel, g_dctx, g_lse = group
        total, near_pull, far_pull, window = relative_scores(
            g_query, g_key, g_krel, g_qrel, offset, full_len
        )
        scores = jnp.where(same_doc, total * score_scale, masked_score)
        weights_now = jnp.exp(scores - g_lse[..., None])
        prob_grad = jnp.einsum(
            "rgid,rgjd->rgij", g_dctx, g_value, preferred_element_type=jnp.float32
        )
        inner_sum = jnp.sum(weights_now * prob_grad, axis=-1)
        score_grad = (weights_now * (prob_grad - inner_sum[..., None])).astype(jnp.bfloat16)
        grad_wide = score_grad.astype(jnp.float32)
        near_grad = near_pull(grad_wide)[0]
        near_low = jnp.where(inner_cols, near_grad, 0.0).astype(jnp.bfloat16)
        near_ends = end_columns(near_grad)
        query_part = jnp.einsum(
            "rgij,rgjd->rgid", score_grad, g_key, preferred_element_type=jnp.float32
        )
        query_part = (
            query_part
            + jnp.einsum("rgib,gbd->rgid", near_low, g_krel, preferred_element_type=jnp.float32)
            + end_terms(near_ends, g_krel)
        )
        krel_part = with_ends(
            jnp.einsum("rgib,rgid->gbd", near_low, g_query, preferred_element_type=jnp.float32),
            end_rows(near_ends, g_query),
        )
        return (
            weights_now,
            score_grad,
            grad_wide,
            far_pull,
            window,
            inner_sum,
            query_part * score_scale,
            krel_part * score_scale,
        )

    query_groups = (
        head_queries,
        head_keys,
        head_values,
        rel_queries,
        rel_keys,
        head_context_grad,
        log_totals,
    )

    def all_grads(carry, group):
        weights_now, score_grad, grad_wide, far_pull, window, inner_sum, query_part, krel_part = (
            query_side(group)
        )
        g_query, g_key, g_value, g_qrel, g_krel, g_dctx, g_lse = group
        cross_grad, end_grad = far_pull(grad_wide)
        cross_low = cross_grad.astype(jnp.bfloat16)
        key_part = jnp.einsum(
            "rgij,rgid->rgjd", score_grad, g_query, preferred_element_type=jnp.float32
        )
        band_part = jnp.einsum(
            "rgmb,gbd->rgmd", cross_low, g_qrel, preferred_element_type=jnp.float32
        )
        key_part = (
            key_part
            + unband(band_part, offset, full_len, buckets // 2)
            + end_terms(end_grad, g_qrel)
        )
        value_part = jnp.einsum(
            "rgij,rgid->rgjd",
            weights_now.astype(jnp.bfloat16),
            g_dctx,
            preferred_element_type=jnp.float32,
        )
        qrel_part = with_ends(
            jnp.einsum("rgmb,rgmd->gbd", cross_low, window, preferred_element_type=jnp.float32),
            end_rows(end_grad, g_key),
        )
        return (
            carry,
            (query_part, key_part * score_scale, value_part, qrel_part * score_scale, krel_part),
        )

    unused, (dq_groups, dk_groups, dv_groups, dqrel_groups, dkrel_groups) = lax.scan(
        all_grads, None, query_groups
    )
    key_sum, value_sum = (
        lax.psum_scatter(join_heads(dk_groups), "seq", scatter_dimension=0, tiled=True),
        lax.psum_scatter(join_heads(dv_groups), "seq", scatter_dimension=0, tiled=True),
    )
    key_grads = key_sum.reshape(tokens_here, width).astype(jnp.bfloat16)
    value_grads = value_sum.reshape(tokens_here, width).astype(jnp.bfloat16)
    query_grads = join_heads(dq_groups).reshape(tokens_here, width).astype(jnp.bfloat16)
    qrel_grad = join_table(dqrel_groups)
    krel_grad = join_table(dkrel_groups)
    input_grad = pre_grad + jnp.einsum(
        "ne,de->nd", query_grads, m_query, preferred_element_type=jnp.float32
    )
    input_grad = input_grad + jnp.einsum(
        "ne,de->nd", key_grads, m_key, preferred_element_type=jnp.float32
    )
    input_grad = input_grad + jnp.einsum(
        "ne,de->nd", value_grads, m_value, preferred_element_type=jnp.float32
    )
    query_whole = jnp.einsum(
        "nd,ne->de", flat_input, query_grads, preferred_element_type=jnp.float32
    ) + jnp.einsum(
        "bd,be->de", table, qrel_grad, precision=highest_prec, preferred_element_type=jnp.float32
    )
    key_whole = jnp.einsum(
        "nd,ne->de", flat_input, key_grads, preferred_element_type=jnp.float32
    ) + jnp.einsum(
        "bd,be->de", table, krel_grad, precision=highest_prec, preferred_element_type=jnp.float32
    )
    value_whole = jnp.einsum(
        "nd,ne->de", flat_input, value_grads, preferred_element_type=jnp.float32
    )
    table_whole = jnp.einsum(
        "be,de->bd", qrel_grad, m_query, precision=highest_prec, preferred_element_type=jnp.float32
    ) + jnp.einsum(
        "be,de->bd", krel_grad, m_key, precision=highest_prec, preferred_element_type=jnp.float32
    )
    bias_whole = jnp.stack(
        [
            jnp.sum(query_grads.astype(jnp.float32), axis=0) + jnp.sum(qrel_grad, axis=0),
            jnp.sum(key_grads.astype(jnp.float32), axis=0) + jnp.sum(krel_grad, axis=0),
            jnp.sum(value_grads.astype(jnp.float32), axis=0),
            jnp.sum(pre_grad, axis=0),
        ]
    )
    gain_whole = jnp.stack([gain1_grad, gain2_grad])
    shift_whole = jnp.stack([shift1_grad, shift2_grad])
    downb_whole = jnp.sum(mixed_grad, axis=0)
    seq_parts = (
        lax.psum_scatter(query_whole, "seq", scatter_dimension=0, tiled=True),
        lax.psum_scatter(key_whole, "seq", scatter_dimension=0, tiled=True),
        lax.psum_scatter(value_whole, "seq", scatter_dimension=0, tiled=True),
        lax.psum_scatter(mix_whole, "seq", scatter_dimension=0, tiled=True),
        lax.psum_scatter(table_whole, "seq", scatter_dimension=0, tiled=True),
        lax.psum_scatter(bias_whole, "seq", scatter_dimension=1, tiled=True),
        lax.psum_scatter(gain_whole, "seq", scatter_dimension=1, tiled=True),
        lax.psum_scatter(shift_whole, "seq", scatter_dimension=1, tiled=True),
        lax.psum_scatter(downb_whole, "seq", scatter_dimension=0, tiled=True),
    )
    batch_parts = (
        lax.psum_scatter(seq_parts[0], "batch", scatter_dimension=1, tiled=True),
        lax.psum_scatter(seq_parts[1], "batch", scatter_dimension=1, tiled=True),
        lax.psum_scatter(seq_parts[2], "batch", scatter_dimension=1, tiled=True),
        lax.psum_scatter(seq_parts[3], "batch", scatter_dimension=1, tiled=True),
        lax.psum_scatter(seq_parts[4], "batch", scatter_dimension=1, tiled=True),
        lax.psum_scatter(up_part, "batch", scatter_dimension=0, tiled=True),
        lax.psum_scatter(down_part, "batch", scatter_dimension=1, tiled=True),
    )
    small_parts = lax.psum(
        (seq_parts[5], seq_parts[6], seq_parts[7], seq_parts[8], upb_part), "batch"
    )
    layer_output = jnp.swapaxes(output.reshape(local_len, rows, width), 0, 1).astype(jnp.bfloat16)
    input_back = jnp.swapaxes(input_grad.reshape(local_len, rows, width), 0, 1)
    return (
        layer_output,
        input_back,
        batch_parts[0],
        batch_parts[1],
        batch_parts[2],
        batch_parts[3],
        batch_parts[4],
        small_parts[0],
        small_parts[1],
        small_parts[2],
        batch_parts[5],
        small_parts[4],
        batch_parts[6],
        small_parts[3],
    )


def solution(mesh):
    return jax.shard_map(
        body,
        mesh=mesh,
        in_specs=(
            P("batch", "seq", None),
            P("batch", "seq"),
            P("seq", "batch"),
            P("seq", "batch"),
            P("seq", "batch"),
            P("seq", "batch"),
            P("seq", "batch"),
            P(None, "seq"),
            P(None, "seq"),
            P(None, "seq"),
            P(None, "seq"),
            P("seq"),
            P("seq", None),
            P("seq"),
            P("batch", "seq", None),
        ),
        out_specs=(
            P("batch", "seq", None),
            P("batch", "seq", None),
            P("seq", "batch"),
            P("seq", "batch"),
            P("seq", "batch"),
            P("seq", "batch"),
            P("seq", "batch"),
            P(None, "seq"),
            P(None, "seq"),
            P(None, "seq"),
            P("batch", "seq"),
            P("seq"),
            P("seq", "batch"),
            P("seq"),
        ),
        check_vma=False,
    )
```

```python
import math

import jax
import jax.numpy as jnp
from jax import lax
from jax.experimental import pallas as pl
from jax.experimental.pallas import tpu as pltpu
from jax.sharding import PartitionSpec as P

DH = 64


masked_score = -1e30
norm_eps = 1e-06
pair_heads = 2


def normalize(values, gain, shift):
    average = jnp.mean(values, axis=-1, keepdims=True)
    centered = values - average
    variance = jnp.mean(centered * centered, axis=-1, keepdims=True)
    return centered * lax.rsqrt(variance + norm_eps) * gain + shift


def exact_gelu(values):
    return jax.nn.gelu(values, approximate=False)


def split_heads(matrix):
    length, rows, width = matrix.shape
    groups = width // (pair_heads * DH)
    return matrix.reshape(length, rows, groups, pair_heads, DH).transpose(2, 1, 3, 0, 4)


def join_heads(matrix):
    groups, rows, pair, length, depth = matrix.shape
    return matrix.transpose(3, 1, 0, 2, 4).reshape(length, rows, groups * pair * depth)


def split_table(matrix):
    buckets, width = matrix.shape
    return matrix.reshape(buckets, width // (pair_heads * DH), pair_heads, DH).transpose(1, 2, 0, 3)


def join_table(matrix):
    groups, pair, buckets, depth = matrix.shape
    return matrix.transpose(2, 0, 1, 3).reshape(buckets, groups * pair * depth)


def table_ends(table):
    return jnp.stack([table[:, 0], table[:, -1]], axis=1)


def near_skew(table_prod, offset, full_len):
    lead = table_prod.shape[:-2]
    count, buckets = table_prod.shape[-2:]
    span = buckets // 2
    lead_pad = [(0, 0)] * len(lead)
    flipped = jnp.pad(table_prod[..., ::-1], lead_pad + [(0, 0), (0, count)])
    sheared = flipped.reshape(lead + (count * (buckets + count),))[
        ..., : count * (buckets + count - 1)
    ]
    sheared = sheared.reshape(lead + (count, buckets + count - 1))
    spread = jnp.pad(sheared, lead_pad + [(0, 0), (full_len, full_len)])
    band = lax.dynamic_slice_in_dim(
        spread, full_len + span - 1 - offset, full_len, axis=len(lead) + 1
    )
    distance = (offset + jnp.arange(count, dtype=jnp.int32))[:, None] - jnp.arange(
        full_len, dtype=jnp.int32
    )[None, :]
    return jnp.where(
        distance <= -span,
        table_prod[..., 0:1],
        jnp.where(distance >= span - 1, table_prod[..., buckets - 1 :], band),
    )


def far_place(cross, end_vals, offset, count, full_len):
    lead = cross.shape[:-2]
    band_len, buckets = cross.shape[-2:]
    span = buckets // 2
    lead_pad = [(0, 0)] * len(lead)
    turned = jnp.swapaxes(cross, -1, -2).reshape(lead + (buckets * band_len,))
    turned = jnp.pad(turned, lead_pad + [(0, buckets)])
    diagonal = turned.reshape(lead + (buckets, band_len + 1))[..., :count]
    aligned = jnp.pad(jnp.swapaxes(diagonal, -1, -2), lead_pad + [(0, 0), (0, count)])
    sheared = aligned.reshape(lead + (count * (buckets + count),))[
        ..., : count * (buckets + count - 1)
    ]
    sheared = sheared.reshape(lead + (count, buckets + count - 1))
    spread = jnp.pad(sheared, lead_pad + [(0, 0), (full_len, full_len)])
    band = lax.dynamic_slice_in_dim(spread, full_len + span - offset, full_len, axis=len(lead) + 1)
    distance = (
        jnp.arange(full_len, dtype=jnp.int32)[None, :]
        - (offset + jnp.arange(count, dtype=jnp.int32))[:, None]
    )
    return jnp.where(
        distance <= -span,
        end_vals[..., 0:1, :],
        jnp.where(distance >= span - 1, end_vals[..., 1:2, :], band),
    )


def band_rows(all_rows, offset, count, span):
    padded = jnp.pad(all_rows, [(0, 0), (0, 0), (span, span), (0, 0)])
    return lax.dynamic_slice_in_dim(padded, offset, count + 2 * span - 1, axis=2)


def unband(values, offset, full_len, span):
    lead = values.shape[:2]
    room = jnp.zeros(lead + (full_len + 2 * span, values.shape[3]), jnp.float32)
    placed = lax.dynamic_update_slice_in_dim(room, values, offset, axis=2)
    return placed[:, :, span : span + full_len]


def relative_scores(own_rows, all_rows, own_table, all_table, offset, full_len):
    count = own_rows.shape[2]
    content = jnp.einsum("rgid,rgjd->rgij", own_rows, all_rows, preferred_element_type=jnp.float32)
    own_prod = jnp.einsum("rgid,gbd->rgib", own_rows, own_table, preferred_element_type=jnp.float32)
    window = band_rows(all_rows, offset, count, all_table.shape[1] // 2)
    cross = jnp.einsum("rgmd,gbd->rgmb", window, all_table, preferred_element_type=jnp.float32)
    end_vals = jnp.einsum(
        "rgjd,ged->rgej", all_rows, table_ends(all_table), preferred_element_type=jnp.float32
    )
    near_vals, near_pull = jax.vjp(lambda product: near_skew(product, offset, full_len), own_prod)
    far_vals, far_pull = jax.vjp(
        lambda part, ends: far_place(part, ends, offset, count, full_len), cross, end_vals
    )
    return (content + near_vals + far_vals, near_pull, far_pull, window)


def end_columns(grad):
    return jnp.stack([grad[..., 0], grad[..., -1]], axis=2)


def end_terms(ends, table):
    return jnp.einsum(
        "rgei,ged->rgid",
        ends,
        table_ends(table),
        precision=lax.Precision.HIGHEST,
        preferred_element_type=jnp.float32,
    )


def end_rows(ends, rows_low):
    return jnp.einsum(
        "rgei,rgid->ged",
        ends,
        rows_low,
        precision=lax.Precision.HIGHEST,
        preferred_element_type=jnp.float32,
    )


def with_ends(inner_part, edge_rows):
    buckets = inner_part.shape[1]
    place = jnp.arange(buckets, dtype=jnp.int32)[None, :, None]
    return (
        inner_part
        + jnp.where(place == 0, edge_rows[:, 0:1], 0.0)
        + jnp.where(place == buckets - 1, edge_rows[:, 1:2], 0.0)
    )


BLOCK = 128


def dot_nn(a, b):
    return lax.dot_general(a, b, (((1,), (0,)), ((), ())), preferred_element_type=jnp.float32)


def dot_nt(a, b):
    return lax.dot_general(a, b, (((1,), (1,)), ((), ())), preferred_element_type=jnp.float32)


def dot_tn(a, b):
    return lax.dot_general(a, b, (((0,), (0,)), ((), ())), preferred_element_type=jnp.float32)


def turn_matrix(buckets):
    row = lax.broadcasted_iota(jnp.int32, (buckets, buckets), 0)
    col = lax.broadcasted_iota(jnp.int32, (buckets, buckets), 1)
    return (row + col == buckets - 1).astype(jnp.bfloat16)


def skew_band(product):
    count, buckets = product.shape
    row = lax.broadcasted_iota(jnp.int32, (count, BLOCK), 0)
    lane = lax.broadcasted_iota(jnp.int32, (count, BLOCK), 1)
    edge = jnp.where(row + lane <= BLOCK - 2, product[:, buckets - 1 :], product[:, 0:1])
    wide = jnp.concatenate([product, edge], axis=1)
    return pltpu.roll(wide, 1, 1, stride=1, stride_axis=0)


def skew_back(turned, buckets):
    return pltpu.roll(turned, turned.shape[1] - BLOCK, 1, stride=1, stride_axis=0)[:, :buckets]


def chip_columns(vec_ref, chip, index, core):
    width = 3 * DH // 2
    both = jnp.concatenate(
        [
            vec_ref[2 * chip, index : index + 1, :width].astype(jnp.float32),
            vec_ref[2 * chip + 1, index : index + 1, :width].astype(jnp.float32),
        ],
        axis=1,
    )
    return jnp.where(core == 0, both[:, : 2 * DH], both[:, DH:])


def attend_kernel(
    xs_ref,
    qkvs_ref,
    mts_ref,
    vecs_ref,
    q_ref,
    k_ref,
    v_ref,
    qrev_ref,
    krev_ref,
    p_ref,
    ctx_ref,
    w_ref,
    mix_ref,
    table_ref,
    x_ref,
    segc_ref,
    place_ref,
    wide_ref,
    ends_ref,
    held_ref,
):
    at = Place()
    full_len = x_ref.shape[0]
    buckets = table_ref.shape[0]
    blocks = full_len // BLOCK
    span = buckets // 2
    side = span // BLOCK
    band_width = buckets + BLOCK
    band_blocks = band_width // BLOCK
    group = 2 * DH
    scale = 1.0 / math.sqrt(3.0 * DH)
    units = p_ref.shape[0]
    shard_rows = qkvs_ref.shape[2]
    table_rows = mts_ref.shape[3] - shard_rows
    batches = mts_ref.shape[1]
    for part in range(at.tokens):
        pieces = []
        for i in range(3):
            piece = qkvs_ref[part, i]
            pieces.append(jnp.where(at.core == 0, piece[:, :group], piece[:, DH:]))
        w_ref[part * shard_rows : (part + 1) * shard_rows] = jnp.concatenate(pieces, axis=1)
        core, chip = part % 2, part // 2
        whole = [mts_ref[core, row, chip] for row in range(batches)]
        mix_ref[part * shard_rows : (part + 1) * shard_rows] = jnp.concatenate(
            [piece[:shard_rows] for piece in whole], axis=1
        )
        table_ref[part * table_rows : (part + 1) * table_rows] = jnp.concatenate(
            [piece[shard_rows:] for piece in whole], axis=1
        )
        x_ref[part * BLOCK : (part + 1) * BLOCK] = xs_ref[part]
        own_seg = vecs_ref[part, 9:10].astype(jnp.float32)
        segc_ref[part * BLOCK : (part + 1) * BLOCK] = jnp.broadcast_to(own_seg, (BLOCK, BLOCK)).T
    seg_row = jnp.concatenate(
        [vecs_ref[part, 9:10].astype(jnp.float32) for part in range(at.tokens)], axis=1
    )
    bias = jnp.concatenate(
        [chip_columns(vecs_ref, at.chip, i, at.core) for i in range(3)], axis=1
    )
    proj = (dot_nn(x_ref[...], w_ref[...]) + bias).astype(jnp.bfloat16)
    rel = (dot_nn(table_ref[...], w_ref[:, : 2 * group]) + bias[:, : 2 * group]).astype(
        jnp.bfloat16
    )
    rel = dot_nn(turn_matrix(buckets), rel).astype(jnp.bfloat16)
    for slot in range(2):
        lo, hi = slot * DH, (slot + 1) * DH
        q_ref[slot] = proj[:, lo:hi]
        k_ref[slot] = proj[:, group + lo : group + hi]
        v_ref[slot] = proj[:, 2 * group + lo : 2 * group + hi]
        qrev_ref[slot] = rel[:, lo:hi]
        krev_ref[slot] = rel[:, group + lo : group + hi]
    held_ref[...] = jnp.zeros_like(held_ref)
    for slot in range(2):
        ends_ref[slot, 0] = dot_nt(qrev_ref[slot, 0:16], k_ref[slot])
        ends_ref[slot, 1] = dot_nt(qrev_ref[slot, buckets - 16 : buckets], k_ref[slot])

        def key_block(kb, carry):
            rows = k_ref[slot, pl.ds(pl.multiple_of(kb * BLOCK, BLOCK), BLOCK)]
            band = skew_band(dot_nt(rows, qrev_ref[slot]))
            for e in range(band_blocks):
                place_ref[
                    slot,
                    kb + e,
                    :,
                    (band_blocks - 1 - e) * BLOCK : (band_blocks - e) * BLOCK,
                ] = band[:, e * BLOCK : (e + 1) * BLOCK].T
            return carry

        lax.fori_loop(0, blocks, key_block, 0)

    first = at.core * (blocks // 2)

    def unit(u, carry):
        g = u + first
        slot = g // blocks
        qb = g % blocks
        start = pl.multiple_of(qb * BLOCK, BLOCK)
        rows = q_ref[slot, pl.ds(start, BLOCK)]
        own = dot_nt(rows, krev_ref[slot])
        band = skew_band(own) + place_ref[slot, qb + side]
        wide_ref[:, pl.ds(start, band_width)] = band
        content = dot_nt(rows, k_ref[slot])
        lane = lax.broadcasted_iota(jnp.int32, (BLOCK, full_len), 1)
        near = jnp.where(
            lane < start - span,
            own[:, 0:1] + ends_ref[slot, 1, 15:16],
            jnp.where(
                lane >= start + band_width - span,
                own[:, buckets - 1 :] + ends_ref[slot, 0, 0:1],
                wide_ref[:, span : span + full_len],
            ),
        )
        same = segc_ref[pl.ds(start, BLOCK), 0:1] == seg_row
        scores = jnp.where(same, (content + near) * scale, masked_score)
        highest = jnp.max(scores, axis=-1, keepdims=True)
        exponent = jnp.exp(scores - highest)
        total = jnp.sum(exponent, axis=-1, keepdims=True)
        probs = (exponent / total).astype(jnp.bfloat16)
        p_ref[u] = probs
        held_ref[slot, pl.ds(start, BLOCK)] = dot_nn(probs, v_ref[slot]).astype(jnp.bfloat16)
        return carry

    lax.fori_loop(0, units, unit, 0)
    for part in range(at.tokens):
        rows = slice(part * BLOCK, (part + 1) * BLOCK)
        ctx_ref[part] = jnp.concatenate([held_ref[0, rows], held_ref[1, rows]], axis=1)


def attend(xs, qkvs, mts, vecs):
    tokens, local_len, width = xs.shape
    full_len = tokens * local_len
    shard_rows = qkvs.shape[2]
    buckets = tokens * (mts.shape[3] - shard_rows)
    blocks = full_len // BLOCK
    units = 3 * blocks // 2
    band_width = buckets + BLOCK
    low, wide = jnp.bfloat16, jnp.float32
    pad_blocks = blocks + band_width // BLOCK - 1
    return pl.pallas_call(
        attend_kernel,
        out_shape=(
            jax.ShapeDtypeStruct((2, full_len, DH), low),
            jax.ShapeDtypeStruct((2, full_len, DH), low),
            jax.ShapeDtypeStruct((2, full_len, DH), low),
            jax.ShapeDtypeStruct((2, buckets, DH), low),
            jax.ShapeDtypeStruct((2, buckets, DH), low),
            jax.ShapeDtypeStruct((units, BLOCK, full_len), low),
            jax.ShapeDtypeStruct((tokens, local_len, 2 * DH), low),
            jax.ShapeDtypeStruct((width, 6 * DH), low),
            jax.ShapeDtypeStruct((width, width), low),
            jax.ShapeDtypeStruct((buckets, width), low),
        ),
        in_specs=[pl.BlockSpec(memory_space=pltpu.VMEM)] * 4,
        out_specs=[pl.BlockSpec(memory_space=pltpu.VMEM)] * 10,
        scratch_shapes=[
            pltpu.VMEM((full_len, width), low),
            pltpu.VMEM((full_len, BLOCK), wide),
            pltpu.VMEM((2, pad_blocks, BLOCK, band_width), wide),
            pltpu.VMEM((BLOCK, full_len + buckets), wide),
            pltpu.VMEM((2, 2, 16, full_len), wide),
            pltpu.VMEM((2, full_len, DH), low),
        ],
        compiler_params=pltpu.CompilerParams(vmem_limit_bytes=60 * 1024 * 1024),
        name="attend",
    )(xs, qkvs, mts, vecs)


def attend_back_kernel(
    q_ref,
    k_ref,
    v_ref,
    qrev_ref,
    krev_ref,
    p_ref,
    ctx_ref,
    w_ref,
    mix_ref,
    table_ref,
    xs_ref,
    attn_ref,
    in_ref,
    dw_ref,
    tab_ref,
    mixpart_ref,
    sum_ref,
    x_ref,
    heads_ref,
    wide_ref,
    low_ref,
    place_ref,
    dq_ref,
    dkt_ref,
    dvt_ref,
    far_ref,
    dkr_ref,
    dqr_ref,
):
    full_len = q_ref.shape[1]
    buckets = qrev_ref.shape[1]
    blocks = full_len // BLOCK
    span = buckets // 2
    side = span // BLOCK
    band_width = buckets + BLOCK
    band_blocks = band_width // BLOCK
    scale = 1.0 / math.sqrt(3.0 * DH)
    units = p_ref.shape[0]
    for ref in (wide_ref, low_ref, place_ref, dq_ref, dkt_ref, dvt_ref, far_ref, dkr_ref, dqr_ref):
        ref[...] = jnp.zeros_like(ref)
    at = Place()
    group = 2 * DH
    width = x_ref.shape[1]
    first_row = pl.multiple_of((3 * at.chip + at.core) * DH, DH)
    mix_rows = mix_ref[pl.ds(first_row, group)]
    mix_part = jnp.zeros((group, width), jnp.float32)
    for part in range(at.tokens):
        x_ref[part * BLOCK : (part + 1) * BLOCK] = xs_ref[part]
        low_part = attn_ref[part]
        mix_part = mix_part + dot_tn(ctx_ref[part], low_part)
        dctx = dot_nt(low_part, mix_rows).astype(jnp.bfloat16)
        for slot in range(2):
            heads_ref[slot, part * BLOCK : (part + 1) * BLOCK] = dctx[
                :, slot * DH : (slot + 1) * DH
            ]
    columns = width // at.batches
    for row in range(at.batches):
        mixpart_ref[row] = mix_part[:, row * columns : (row + 1) * columns].astype(jnp.bfloat16)
    first = at.core * (blocks // 2)
    turn = turn_matrix(BLOCK)
    place8 = lax.broadcasted_iota(jnp.int32, (8, full_len), 0)

    def unit(u, carry):
        g = u + first
        slot = g // blocks
        qb = g % blocks
        start = pl.multiple_of(qb * BLOCK, BLOCK)
        rows = q_ref[slot, pl.ds(start, BLOCK)]
        grad = heads_ref[slot, pl.ds(start, BLOCK)]
        probs = p_ref[u]
        wide_probs = probs.astype(jnp.float32)
        prob_grad = dot_nt(grad, v_ref[slot])
        inner = jnp.sum(wide_probs * prob_grad, axis=-1, keepdims=True)
        low_grad = (wide_probs * (prob_grad - inner)).astype(jnp.bfloat16)
        score_grad = low_grad.astype(jnp.float32)
        wide_ref[:, span : span + full_len] = dot_nn(turn, low_grad)
        low_ref[:, span : span + full_len] = low_grad
        dvt_ref[slot] += dot_tn(grad, probs)
        dkt_ref[slot] += dot_tn(rows, low_grad)
        row = lax.broadcasted_iota(jnp.int32, (BLOCK, full_len), 0)
        lane = lax.broadcasted_iota(jnp.int32, (BLOCK, full_len), 1)
        gap = lane - row - start
        right = jnp.where(gap > span, score_grad, 0.0)
        left = jnp.where(gap < 1 - span, score_grad, 0.0)
        end_right = jnp.sum(right, axis=-1, keepdims=True)
        end_left = jnp.sum(left, axis=-1, keepdims=True)
        far_right = jnp.sum(jnp.where(gap >= span, score_grad, 0.0), axis=0, keepdims=True)
        far_left = jnp.sum(jnp.where(gap < -span, score_grad, 0.0), axis=0, keepdims=True)
        far_ref[slot] += jnp.where(place8 == 0, far_right, jnp.where(place8 == 1, far_left, 0.0))
        band = wide_ref[:, pl.ds(start, band_width)]
        near = dot_nn(turn, skew_back(band, buckets).astype(jnp.bfloat16))
        bucket = lax.broadcasted_iota(jnp.int32, (BLOCK, buckets), 1)
        near = near + jnp.where(
            bucket == 0, end_left, jnp.where(bucket == buckets - 1, end_right, 0.0)
        )
        near_low = near.astype(jnp.bfloat16)
        dq = dot_nn(low_grad, k_ref[slot]) + dot_nn(near_low, krev_ref[slot])
        dq_ref[slot, pl.ds(start, BLOCK)] = dq
        dkr_ref[slot] += dot_tn(rows, near_low)
        for e in range(band_blocks):
            keys_at = pl.multiple_of(start + e * BLOCK, BLOCK)
            place_ref[
                slot, qb + e, :, (band_blocks - 1 - e) * BLOCK : (band_blocks - e) * BLOCK
            ] = dot_nt(turn, low_ref[:, pl.ds(keys_at, BLOCK)])
        return carry

    lax.fori_loop(0, units, unit, 0)
    parts_q, parts_k, parts_v = [], [], []
    parts_r = [None] * 4
    for slot in range(2):
        far_low = far_ref[slot].astype(jnp.bfloat16)
        mark = lax.broadcasted_iota(jnp.int32, (8, DH), 0)
        ends = jnp.where(
            mark == 0,
            qrev_ref[slot, 0:1].astype(jnp.float32),
            jnp.where(mark == 1, qrev_ref[slot, buckets - 1 : buckets].astype(jnp.float32), 0.0),
        ).astype(jnp.bfloat16)
        end_keys = dot_tn(ends, far_low)
        end_rows = dot_nn(far_low, k_ref[slot])

        whole_k = (dkt_ref[slot] + end_keys).T

        def key_side(kb, carry):
            start = pl.multiple_of(kb * BLOCK, BLOCK)
            far = skew_back(place_ref[slot, kb + side], buckets).astype(jnp.bfloat16)
            far = dot_nn(turn, far).astype(jnp.bfloat16)
            keys = k_ref[slot, pl.ds(start, BLOCK)]
            dqr_ref[slot] += dot_tn(keys, far)
            dq_ref[2 + slot, pl.ds(start, BLOCK)] = dot_nn(far, qrev_ref[slot])
            return carry

        lax.fori_loop(0, blocks, key_side, 0)
        parts_q.append((dq_ref[slot] * scale).astype(jnp.bfloat16))
        parts_k.append(((dq_ref[2 + slot] + whole_k) * scale).astype(jnp.bfloat16))
        parts_v.append(dvt_ref[slot].T.astype(jnp.bfloat16))
        bucket = lax.broadcasted_iota(jnp.int32, (buckets, DH), 0)
        qr = dqr_ref[slot].T + jnp.where(
            bucket == 0, end_rows[0:1], jnp.where(bucket == buckets - 1, end_rows[1:2], 0.0)
        )
        dqr_out = qr * scale
        dkr_out = dkr_ref[slot].T * scale
        parts_r[slot] = dqr_out
        parts_r[2 + slot] = dkr_out
    dcat = jnp.concatenate(parts_q + parts_k + parts_v, axis=1)
    in_part = dot_nt(dcat, w_ref[...]).astype(jnp.bfloat16)
    for part in range(at.tokens):
        in_ref[part // 2, part % 2] = in_part[part * BLOCK : (part + 1) * BLOCK]
    rel = jnp.concatenate(parts_r, axis=1)
    rel_low = dot_nn(turn_matrix(buckets), rel.astype(jnp.bfloat16)).astype(jnp.bfloat16)
    dw = dot_tn(x_ref[...], dcat)
    dw_rel = dot_tn(table_ref[...], rel_low)
    dw = jnp.concatenate([dw[:, : 2 * group] + dw_rel, dw[:, 2 * group :]], axis=1)
    dw_low = dw.astype(jnp.bfloat16)
    for row in range(at.batches):
        rows = slice(row * columns, (row + 1) * columns)
        dw_ref[row] = dw_low[rows]
        tab_ref[row] = dot_nt(rel_low, w_ref[rows, : 2 * group]).astype(jnp.bfloat16)
    rel_sum = jnp.sum(rel, axis=0, keepdims=True)
    rel_sum = jnp.concatenate([rel_sum, jnp.zeros((1, 2 * DH), jnp.float32)], axis=1)
    sums = jnp.sum(dcat.astype(jnp.float32), axis=0, keepdims=True) + rel_sum
    sum_ref[...] = jnp.broadcast_to(sums, sum_ref.shape)


def attend_back(q, k, v, qrev, krev, probs, ctx, w_cat, m_mix, table, xs, attn_all):
    full_len = q.shape[1]
    buckets, width = table.shape
    blocks = full_len // BLOCK
    tokens, batches = lax.axis_size("seq"), lax.axis_size("batch")
    columns = width // batches
    band_width = buckets + BLOCK
    low, wide = jnp.bfloat16, jnp.float32
    pad_blocks = blocks + band_width // BLOCK - 1
    return pl.pallas_call(
        attend_back_kernel,
        out_shape=(
            jax.ShapeDtypeStruct((tokens // 2, 2, BLOCK, width), low),
            jax.ShapeDtypeStruct((batches, columns, 6 * DH), low),
            jax.ShapeDtypeStruct((batches, buckets, columns), low),
            jax.ShapeDtypeStruct((batches, 2 * DH, columns), low),
            jax.ShapeDtypeStruct((8, 6 * DH), wide),
        ),
        in_specs=[pl.BlockSpec(memory_space=pltpu.VMEM)] * 12,
        out_specs=[pl.BlockSpec(memory_space=pltpu.VMEM)] * 5,
        scratch_shapes=[
            pltpu.VMEM((full_len, width), low),
            pltpu.VMEM((2, full_len, DH), low),
            pltpu.VMEM((BLOCK, full_len + buckets), wide),
            pltpu.VMEM((BLOCK, full_len + buckets), low),
            pltpu.VMEM((2, pad_blocks, BLOCK, band_width), wide),
            pltpu.VMEM((4, full_len, DH), wide),
            pltpu.VMEM((2, DH, full_len), wide),
            pltpu.VMEM((2, DH, full_len), wide),
            pltpu.VMEM((2, 8, full_len), wide),
            pltpu.VMEM((2, DH, buckets), wide),
            pltpu.VMEM((2, DH, buckets), wide),
        ],
        compiler_params=pltpu.CompilerParams(vmem_limit_bytes=60 * 1024 * 1024),
        name="attend_back",
    )(q, k, v, qrev, krev, probs, ctx, w_cat, m_mix, table, xs, attn_all)


MESH = pl.DeviceIdType.MESH
VMEM_SPEC = pl.BlockSpec(memory_space=pltpu.VMEM)
ANY_SPEC = pl.BlockSpec(memory_space=pl.ANY)


class Place:
    def __init__(self):
        self.batches = lax.axis_size("batch")
        self.tokens = lax.axis_size("seq")
        self.chips = self.tokens // 2
        self.row = lax.axis_index("batch")
        self.part = lax.axis_index("seq")
        self.chip = self.part // 2
        self.core = self.part % 2

    def along_chips(self, k):
        chip = lax.rem(self.chip + k, self.chips)
        return chip, (self.row, 2 * chip + self.core)

    def from_chips(self, k):
        return lax.rem(self.chip + self.chips - k, self.chips)

    def partner(self):
        return (self.row, self.part + 1 - 2 * self.core)

    def along_rows(self, k):
        row = lax.rem(self.row + k, self.batches)
        return row, (row, self.part)

    def from_rows(self, k):
        return lax.rem(self.row + self.batches - k, self.batches)

    def along_seq(self, k):
        part = lax.rem(self.part + k, self.tokens)
        return part, (self.row, part)

    def along_plane(self, k):
        index = lax.rem(2 * self.row + self.core + k, 2 * self.batches)
        row, core = index // 2, index % 2
        return row, core, (row, 2 * self.chip + core)

    def chip_peers(self):
        return [self.along_chips(k)[1] for k in range(1, self.chips)]

    def row_peers(self):
        return [self.along_rows(k)[1] for k in range(1, self.batches)]

    def cross_peers(self):
        other = self.part + 1 - 2 * self.core
        return [(self.along_rows(k)[0], other) for k in range(1, self.batches)]

    def cross_row_peers(self):
        return self.row_peers() + self.cross_peers()

    def seq_peers(self):
        return [self.along_seq(k)[1] for k in range(1, self.tokens)]

    def plane_peers(self):
        return [self.along_plane(k)[2] for k in range(1, 2 * self.batches)]


def meet(peers):
    barrier = pltpu.get_barrier_semaphore()
    for peer in peers:
        pl.semaphore_signal(barrier, inc=1, device_id=peer, device_id_type=MESH)
    pl.semaphore_wait(barrier, len(peers))


class Wires:
    def __init__(self, send_sems, recv_sems, local_sems):
        self.sems = (send_sems, recv_sems, local_sems)
        self.used = [0, 0]
        self.ends = []

    def send(self, src, dst, peer):
        k = self.used[0]
        self.used[0] += 1
        copy = pltpu.make_async_remote_copy(
            src_ref=src,
            dst_ref=dst,
            send_sem=self.sems[0].at[k],
            recv_sem=self.sems[1].at[k],
            device_id=peer,
            device_id_type=MESH,
        )
        copy.start()
        self.ends.append(copy.wait_send)
        return copy

    def local(self, src, dst):
        k = self.used[1]
        self.used[1] += 1
        copy = pltpu.make_async_copy(src, dst, self.sems[2].at[k])
        copy.start()
        return copy

    def finish(self):
        for end in self.ends:
            end()


def wire_scratch(sends, locals_count):
    return [
        pltpu.SemaphoreType.DMA((sends,)),
        pltpu.SemaphoreType.DMA((sends,)),
        pltpu.SemaphoreType.DMA((locals_count,)),
    ]


def comm_call(kernel, name, ident, out_shapes, inputs, sends, locals_count, scratch=()):
    return pl.pallas_call(
        kernel,
        out_shape=tuple(out_shapes),
        in_specs=[VMEM_SPEC] * len(inputs),
        out_specs=tuple([ANY_SPEC] * len(out_shapes)),
        scratch_shapes=list(scratch) + wire_scratch(sends, locals_count),
        compiler_params=pltpu.CompilerParams(
            collective_id=ident, has_side_effects=True, vmem_limit_bytes=40 * 1024 * 1024
        ),
        name=name,
    )(*inputs)


def like(array, *lead):
    return jax.ShapeDtypeStruct(tuple(lead) + tuple(array.shape), array.dtype)


def gather_kernel(
    x_ref, wq_ref, wk_ref, wv_ref, mix_ref, table_ref, vec_ref, up_ref, down_ref,
    xs_ref, qkvs_ref, mts_ref, vecs_ref, up2_ref, down2_ref, *sems,
):
    at = Place()
    wires = Wires(*sems)
    b, s, z, c = at.row, at.part, at.chip, at.core
    off_diagonal = b != z
    turned = (z, 2 * b + c)
    barrier = pltpu.get_barrier_semaphore()
    peers = at.chip_peers() + at.plane_peers()
    for peer in peers:
        pl.semaphore_signal(barrier, inc=1, device_id=peer, device_id_type=MESH)

    @pl.when(off_diagonal)
    def _():
        pl.semaphore_signal(barrier, inc=1, device_id=turned, device_id_type=MESH)

    pl.semaphore_wait(barrier, len(peers) + off_diagonal.astype(jnp.int32))

    swaps, stays = [], []
    for i, ref in enumerate((wq_ref, wk_ref, wv_ref)):
        k = wires.used[0]
        wires.used[0] += 1
        swaps.append(
            pltpu.make_async_remote_copy(
                src_ref=ref,
                dst_ref=qkvs_ref.at[2 * z + c, i],
                send_sem=sems[0].at[k],
                recv_sem=sems[1].at[k],
                device_id=turned,
                device_id_type=MESH,
            )
        )
        stays.append(pltpu.make_async_copy(ref, qkvs_ref.at[2 * b + c, i], sems[2].at[i]))
        wires.used[1] += 1

    @pl.when(off_diagonal)
    def _():
        for swap in swaps:
            swap.start()

    @pl.when(jnp.logical_not(off_diagonal))
    def _():
        for stay in stays:
            stay.start()

    rows = mix_ref.shape[0]
    table_rows = table_ref.shape[0]
    mix_home = mts_ref.at[c, b, z, pl.ds(0, rows)]
    table_home = mts_ref.at[c, b, z, pl.ds(rows, table_rows)]
    mt_sends = []
    for k in range(1, at.chips):
        peer = at.along_chips(k)[1]
        mt_sends.append(wires.send(mix_ref, mix_home, peer))
        mt_sends.append(wires.send(table_ref, table_home, peer))
    x_sends, vec_sends = [], []
    for k in range(1, at.chips):
        peer = at.along_chips(k)[1]
        x_sends.append(wires.send(x_ref, xs_ref.at[s], peer))
        vec_sends.append(wires.send(vec_ref, vecs_ref.at[s], peer))
    own = [
        wires.local(x_ref, xs_ref.at[s]),
        wires.local(mix_ref, mix_home),
        wires.local(table_ref, table_home),
        wires.local(vec_ref, vecs_ref.at[s]),
    ]
    last = [
        wires.send(x_ref, xs_ref.at[s], at.partner()),
        wires.send(vec_ref, vecs_ref.at[s], at.partner()),
        wires.send(up_ref, up2_ref, at.partner()),
        wires.send(down_ref, down2_ref, at.partner()),
    ]

    @pl.when(off_diagonal)
    def _():
        for swap in swaps:
            swap.wait_recv()

    @pl.when(jnp.logical_not(off_diagonal))
    def _():
        for stay in stays:
            stay.wait()

    for k in range(1, 2 * at.batches):
        peer = at.along_plane(k)[2]
        last.append(wires.send(qkvs_ref.at[2 * b + c], qkvs_ref.at[2 * b + c], peer))
    for copy in mt_sends:
        copy.wait_recv()
    for copy in own:
        copy.wait()
    row_sends = []
    for k in range(1, at.batches):
        peer = at.along_rows(k)[1]
        row_sends.append(wires.send(mts_ref.at[c, b], mts_ref.at[c, b], peer))
    last.append(wires.send(mts_ref.at[c, b], mts_ref.at[c, b], at.partner()))
    for k in range(1, at.batches):
        row = at.from_rows(k)
        row_sends[k - 1].wait_recv()
        last.append(wires.send(mts_ref.at[c, row], mts_ref.at[c, row], at.partner()))
    for k in range(1, at.chips):
        index = 2 * at.from_chips(k) + c
        x_sends[k - 1].wait_recv()
        last.append(wires.send(xs_ref.at[index], xs_ref.at[index], at.partner()))
        vec_sends[k - 1].wait_recv()
        last.append(wires.send(vecs_ref.at[index], vecs_ref.at[index], at.partner()))
    for copy in last:
        copy.wait_recv()
    wires.finish()

    @pl.when(off_diagonal)
    def _():
        for swap in swaps:
            swap.wait_send()


def gather_inputs(x, w_query, w_key, w_value, w_mix, rel_table, vec, up, down):
    tokens, batches = lax.axis_size("seq"), lax.axis_size("batch")
    chips = tokens // 2
    rows, columns = w_mix.shape
    outs = (
        like(x, tokens),
        like(w_query, tokens, 3),
        jax.ShapeDtypeStruct(
            (2, batches, chips, rows + rel_table.shape[0], columns), w_mix.dtype
        ),
        like(vec, tokens),
        like(up),
        like(down),
    )
    sends = 3 + 4 * (chips - 1) + 4 + 2 * batches - 1 + 2 * (batches - 1) + 1 + 2 * (chips - 1)
    inputs = (x, w_query, w_key, w_value, w_mix, rel_table, vec, up, down)
    return comm_call(gather_kernel, "gather_inputs", 0, outs, inputs, sends, 7)


def norm_parts(values):
    average = jnp.mean(values, axis=-1, keepdims=True)
    centered = values - average
    variance = jnp.mean(centered * centered, axis=-1, keepdims=True)
    scale = lax.rsqrt(variance + norm_eps)
    return centered * scale, scale


def norm_back(grad, gain, unit, scale):
    inner = grad * gain
    mean = jnp.mean(inner, axis=-1, keepdims=True)
    slope = jnp.mean(inner * unit, axis=-1, keepdims=True)
    return scale * (inner - mean - unit * slope)


def feed_kernel(
    ctx_ref, x_ref, mix_ref, vecs_ref, up_ref, down_ref, up2_ref, down2_ref, out_grad_ref,
    output_ref, pre_grad_ref, sums_ref, attn_ref, ups_ref, downs_ref, upbs_ref,
    got_ref, hid_ref, act_ref, slope_ref, part_ref, ffn_ref, grad_ref, inner_ref,
    back_ref, backs_ref, low_ref, upg_ref, downg_ref, upb_ref, vec_ref, *sems,
):
    at = Place()
    wires = Wires(*sems)
    low, wide = jnp.bfloat16, jnp.float32
    s, z, c = at.part, at.chip, at.core
    meet(at.seq_peers() + at.cross_row_peers())
    last, own = [], []
    swaps = []
    for k in range(1, at.tokens):
        part, peer = at.along_seq(k)
        swaps.append(wires.send(ctx_ref.at[part], got_ref.at[s], peer))
    kept = wires.local(ctx_ref.at[s], got_ref.at[s])
    lanes = x_ref.shape[1] // at.tokens
    hidden_here = up_ref.shape[1]
    vec_ref[...] = jnp.concatenate(
        [vecs_ref[part, :, :lanes].astype(wide) for part in range(at.tokens)], axis=1
    )
    bias3 = vec_ref[3:4]
    gain1, gain2 = vec_ref[4:5], vec_ref[5:6]
    shift1, shift2 = vec_ref[6:7], vec_ref[7:8]
    bias_down = vec_ref[8:9]
    partner = s + 1 - 2 * c
    up_rows = hidden_here // BLOCK
    bias_up = jnp.concatenate(
        [vecs_ref[s, 10 + i : 11 + i].astype(wide) for i in range(up_rows)]
        + [vecs_ref[partner, 10 + i : 11 + i].astype(wide) for i in range(up_rows)],
        axis=1,
    )
    for copy in swaps:
        copy.wait_recv()
    kept.wait()
    pieces = []
    for chip in range(at.chips):
        left, right = got_ref[2 * chip], got_ref[2 * chip + 1]
        middle = left[:, DH:].astype(wide) + right[:, :DH].astype(wide)
        pieces += [left[:, :DH], middle.astype(low), right[:, DH:]]
    context = jnp.concatenate(pieces, axis=1)
    pre_norm = x_ref[...].astype(wide) + dot_nn(context, mix_ref[...]) + bias3
    unit1, scale1 = norm_parts(pre_norm)
    hidden = unit1 * gain1 + shift1
    hid_ref[z] = hidden.astype(low)
    spread = [
        wires.send(hid_ref.at[z], hid_ref.at[z], at.along_chips(k)[1]) for k in range(1, at.chips)
    ]

    ffn_sends = []
    for k in range(at.chips):
        chip = at.from_chips(k)
        if k:
            spread[k - 1].wait_recv()
        rows = hid_ref[chip]
        inner = jnp.concatenate(
            [dot_nn(rows, up_ref[...]), dot_nn(rows, up2_ref[...])], axis=1
        )
        inner = inner + bias_up
        cdf = 0.5 * (1.0 + lax.erf(inner * math.sqrt(0.5)))
        act = (inner * cdf).astype(low)
        slope_ref[chip] = cdf + inner * (
            jnp.exp(-0.5 * inner * inner) * (1.0 / math.sqrt(2.0 * math.pi))
        )
        act_ref[chip] = act
        part_ref[chip] = (
            dot_nn(act[:, :hidden_here], down_ref[...])
            + dot_nn(act[:, hidden_here:], down2_ref[...])
        ).astype(low)
        if k:
            peer = (at.row, 2 * chip + c)
            ffn_sends.append(wires.send(part_ref.at[chip], ffn_ref.at[at.chips - 1 - k], peer))
    total = part_ref[z].astype(wide)
    for k in range(1, at.chips):
        ffn_sends[k - 1].wait_recv()
        total = total + ffn_ref[at.chips - 1 - k].astype(wide)
    mixed = hidden + total + bias_down
    unit2, scale2 = norm_parts(mixed)
    output_ref[...] = (unit2 * gain2 + shift2).astype(low)
    out_grad = out_grad_ref[...].astype(wide)
    mixed_grad = norm_back(out_grad, gain2, unit2, scale2)
    grad_ref[z] = mixed_grad.astype(low)
    spread = [
        wires.send(grad_ref.at[z], grad_ref.at[z], at.along_chips(k)[1])
        for k in range(1, at.chips)
    ]
    gain2_grad = jnp.sum(out_grad * unit2, axis=0, keepdims=True)
    shift2_grad = jnp.sum(out_grad, axis=0, keepdims=True)
    downb_grad = jnp.sum(mixed_grad, axis=0, keepdims=True)

    back_sends = []
    for k in range(at.chips):
        chip = at.from_chips(k)
        if k:
            spread[k - 1].wait_recv()
        rows = grad_ref[chip]
        act_grad = jnp.concatenate(
            [dot_nt(rows, down_ref[...]), dot_nt(rows, down2_ref[...])], axis=1
        )
        inner_low = (act_grad * slope_ref[chip]).astype(low)
        inner_ref[chip] = inner_low
        back_ref[chip] = (
            dot_nt(inner_low[:, :hidden_here], up_ref[...])
            + dot_nt(inner_low[:, hidden_here:], up2_ref[...])
        ).astype(low)
        if k:
            peer = (at.row, 2 * chip + c)
            back_sends.append(wires.send(back_ref.at[chip], backs_ref.at[at.chips - 1 - k], peer))

    width = x_ref.shape[1]
    columns = width // at.batches
    inner_all = inner_ref[...].reshape(at.chips * BLOCK, 2 * hidden_here)
    act_all = act_ref[...].reshape(at.chips * BLOCK, 2 * hidden_here)
    hid_all = hid_ref[...].reshape(at.chips * BLOCK, width)
    grad_all = grad_ref[...].reshape(at.chips * BLOCK, width)
    up_grad = dot_tn(hid_all, inner_all).astype(low)
    down_grad = dot_tn(act_all, grad_all).astype(low)
    upb_grad = jnp.sum(inner_all.astype(wide), axis=0, keepdims=True)
    for d in range(2):
        half = slice(d * hidden_here, (d + 1) * hidden_here)
        upb_ref[d] = jnp.broadcast_to(upb_grad[:, half], upb_ref.shape[1:])
        for row in range(at.batches):
            piece = slice(row * columns, (row + 1) * columns)
            upg_ref[d, row] = up_grad[piece, half]
            downg_ref[d, row] = down_grad[half, piece]
    mine = 2 * at.row + c
    for k in range(1, 2 * at.batches):
        row, core, peer = at.along_plane(k)
        other = lax.rem(core + c, 2)
        last.append(wires.send(upg_ref.at[other, row], ups_ref.at[mine], peer))
        last.append(wires.send(downg_ref.at[other, row], downs_ref.at[mine], peer))
        last.append(wires.send(upb_ref.at[other], upbs_ref.at[mine], peer))
    own.append(wires.local(upg_ref.at[0, at.row], ups_ref.at[mine]))
    own.append(wires.local(downg_ref.at[0, at.row], downs_ref.at[mine]))
    own.append(wires.local(upb_ref.at[0], upbs_ref.at[mine]))

    total = back_ref[z].astype(wide)
    for k in range(1, at.chips):
        back_sends[k - 1].wait_recv()
        total = total + backs_ref[at.chips - 1 - k].astype(wide)
    hidden_grad = mixed_grad + total
    pre_grad = norm_back(hidden_grad, gain1, unit1, scale1)
    low_ref[...] = pre_grad.astype(low)
    spread = [
        wires.send(low_ref, attn_ref.at[s], at.along_chips(k)[1]) for k in range(1, at.chips)
    ]
    last.append(wires.send(low_ref, attn_ref.at[s], at.partner()))
    own.append(wires.local(low_ref, attn_ref.at[s]))
    pre_grad_ref[...] = pre_grad
    gain1_grad = jnp.sum(hidden_grad * unit1, axis=0, keepdims=True)
    shift1_grad = jnp.sum(hidden_grad, axis=0, keepdims=True)
    bias3_grad = jnp.sum(pre_grad, axis=0, keepdims=True)
    sums = jnp.concatenate(
        [bias3_grad, gain1_grad, gain2_grad, shift1_grad, shift2_grad, downb_grad]
        + [jnp.zeros((2, width), wide)],
        axis=0,
    )
    spare = jnp.zeros((8, BLOCK - lanes), wide)
    for part in range(at.tokens):
        sums_ref[part] = jnp.concatenate(
            [sums[:, part * lanes : (part + 1) * lanes], spare], axis=1
        )
    for k in range(1, at.chips):
        index = 2 * at.from_chips(k) + c
        spread[k - 1].wait_recv()
        last.append(wires.send(attn_ref.at[index], attn_ref.at[index], at.partner()))
    for copy in last:
        copy.wait_recv()
    for copy in own:
        copy.wait()
    wires.finish()


def feed_forward(ctx, x, m_mix, vecs, up, down, up2, down2, out_grad, ident):
    tokens, batches = lax.axis_size("seq"), lax.axis_size("batch")
    chips = tokens // 2
    width = x.shape[1]
    columns = width // batches
    hidden_here = up.shape[1]
    low, wide = jnp.bfloat16, jnp.float32
    outs = (
        jax.ShapeDtypeStruct(x.shape, low),
        jax.ShapeDtypeStruct(x.shape, wide),
        jax.ShapeDtypeStruct((tokens, 8, BLOCK), wide),
        jax.ShapeDtypeStruct((tokens,) + x.shape, low),
        jax.ShapeDtypeStruct((2 * batches, columns, hidden_here), low),
        jax.ShapeDtypeStruct((2 * batches, hidden_here, columns), low),
        jax.ShapeDtypeStruct((2 * batches, 8, hidden_here), wide),
    )
    block = (chips,) + x.shape
    wide_block = (chips, x.shape[0], 2 * hidden_here)
    others = (chips - 1,) + x.shape
    scratch = (
        pltpu.VMEM(ctx.shape, low),
        pltpu.VMEM(block, low),
        pltpu.VMEM(wide_block, low),
        pltpu.VMEM(wide_block, wide),
        pltpu.VMEM(block, low),
        pltpu.VMEM(others, low),
        pltpu.VMEM(block, low),
        pltpu.VMEM(wide_block, low),
        pltpu.VMEM(block, low),
        pltpu.VMEM(others, low),
        pltpu.VMEM(x.shape, low),
        pltpu.VMEM((2, batches, columns, hidden_here), low),
        pltpu.VMEM((2, batches, hidden_here, columns), low),
        pltpu.VMEM((2, 8, hidden_here), wide),
        pltpu.VMEM((16, width), wide),
    )
    inputs = (ctx, x, m_mix, vecs, up, down, up2, down2, out_grad)
    sends = tokens - 1 + 4 * (chips - 1) + 3 * (2 * batches - 1) + 2 * (chips - 1) + 1
    return pl.pallas_call(
        feed_kernel,
        out_shape=outs,
        in_specs=[VMEM_SPEC] * len(inputs),
        out_specs=(VMEM_SPEC,) * 3 + (ANY_SPEC,) * 4,
        scratch_shapes=list(scratch) + wire_scratch(sends, 5),
        compiler_params=pltpu.CompilerParams(
            collective_id=ident, has_side_effects=True, vmem_limit_bytes=60 * 1024 * 1024
        ),
        name="feed_forward",
    )(*inputs)


def settle_kernel(
    in_ref, vec_ref, col_ref, dw_ref, tab_ref, mix_ref,
    ins_ref, vec_all_ref, cols_ref, dw_all_ref, tab_all_ref, mix_all_ref,
    half_ref, sum_ref, vecs_ref, vec_low_ref, dws_ref, dw_low_ref, tabs_ref, tab_low_ref,
    mixs_ref, mix_low_ref, *sems,
):
    at = Place()
    wires = Wires(*sems)
    low, wide = jnp.bfloat16, jnp.float32
    b, s, z, c = at.row, at.part, at.chip, at.core
    off_diagonal = b != z
    same, cross = (z, 2 * b + c), (z, 2 * b + 1 - c)
    peers = at.seq_peers() + at.cross_row_peers()
    barrier = pltpu.get_barrier_semaphore()
    for peer in peers:
        pl.semaphore_signal(barrier, inc=1, device_id=peer, device_id_type=MESH)

    @pl.when(off_diagonal)
    def _():
        pl.semaphore_signal(barrier, inc=1, device_id=same, device_id_type=MESH)
        pl.semaphore_signal(barrier, inc=1, device_id=cross, device_id_type=MESH)

    pl.semaphore_wait(barrier, len(peers) + 2 * off_diagonal.astype(jnp.int32))

    dw_sends, tab_sends, mix_sends, vec_sends, last, own = [], [], [], [], [], []
    for k in range(1, at.batches):
        row, peer = at.along_rows(k)
        dw_sends.append(wires.send(dw_ref.at[row], dws_ref.at[k - 1], peer))
    halves = [
        wires.send(in_ref.at[chip, 1 - c], half_ref.at[chip], at.partner())
        for chip in range(at.chips)
    ]
    for k in range(1, at.batches):
        row, peer = at.along_rows(k)
        tab_sends.append(wires.send(tab_ref.at[row], tabs_ref.at[k - 1], peer))
    for k in range(1, at.batches):
        row, peer = at.along_rows(k)
        mix_sends.append(wires.send(mix_ref.at[row], mixs_ref.at[k - 1], peer))
    for k in range(1, at.tokens):
        part, peer = at.along_seq(k)
        vec_sends.append(wires.send(vec_ref.at[part], vecs_ref.at[k - 1], peer))
    mine = 2 * b + c
    for k in range(1, 2 * at.batches):
        last.append(wires.send(col_ref, cols_ref.at[mine], at.along_plane(k)[2]))
    own.append(wires.local(col_ref, cols_ref.at[mine]))

    total = dw_ref[b].astype(wide)
    for k in range(1, at.batches):
        dw_sends[k - 1].wait_recv()
        total = total + dws_ref[k - 1].astype(wide)
    shard_rows = dw_low_ref.shape[1]
    for half in range(2):
        dw_low_ref[half] = total[half * shard_rows : (half + 1) * shard_rows].astype(low)
    k = wires.used[0]
    wires.used[0] += 1
    move = pltpu.make_async_remote_copy(
        src_ref=dw_low_ref.at[c],
        dst_ref=dw_all_ref.at[c],
        send_sem=sems[0].at[k],
        recv_sem=sems[1].at[k],
        device_id=same,
        device_id_type=MESH,
    )
    stay = pltpu.make_async_copy(
        dw_low_ref.at[c], dw_all_ref.at[c], sems[2].at[wires.used[1]]
    )
    wires.used[1] += 1

    @pl.when(off_diagonal)
    def _():
        move.start()

    @pl.when(jnp.logical_not(off_diagonal))
    def _():
        stay.start()

    last.append(wires.send(dw_low_ref.at[1 - c], dw_all_ref.at[c], cross))

    for chip in range(at.chips):
        halves[chip].wait_recv()
        sum_ref[chip] = (in_ref[chip, c].astype(wide) + half_ref[chip].astype(wide)).astype(low)
    for k in range(1, at.chips):
        chip, peer = at.along_chips(k)
        last.append(wires.send(sum_ref.at[chip], ins_ref.at[z], peer))
    own.append(wires.local(sum_ref.at[z], ins_ref.at[z]))

    total = tab_ref[b].astype(wide)
    for k in range(1, at.batches):
        tab_sends[k - 1].wait_recv()
        total = total + tabs_ref[k - 1].astype(wide)
    table_rows = tab_low_ref.shape[1]
    for part in range(at.tokens):
        tab_low_ref[part] = total[part * table_rows : (part + 1) * table_rows].astype(low)
    for k in range(1, at.tokens):
        part, peer = at.along_seq(k)
        last.append(wires.send(tab_low_ref.at[part], tab_all_ref.at[s], peer))
    own.append(wires.local(tab_low_ref.at[s], tab_all_ref.at[s]))

    total = mix_ref[b].astype(wide)
    for k in range(1, at.batches):
        mix_sends[k - 1].wait_recv()
        total = total + mixs_ref[k - 1].astype(wide)
    mix_low_ref[...] = total.astype(low)
    last.append(wires.send(mix_low_ref, mix_all_ref.at[c], at.partner()))
    own.append(wires.local(mix_low_ref, mix_all_ref.at[c]))

    total = vec_ref[s]
    for k in range(1, at.tokens):
        vec_sends[k - 1].wait_recv()
        total = total + vecs_ref[k - 1]
    vec_low_ref[...] = total
    for k in range(1, at.batches):
        last.append(wires.send(vec_low_ref, vec_all_ref.at[b], at.along_rows(k)[1]))
    own.append(wires.local(vec_low_ref, vec_all_ref.at[b]))

    for copy in last:
        copy.wait_recv()
    for copy in own:
        copy.wait()
    wires.finish()

    @pl.when(off_diagonal)
    def _():
        move.wait()

    @pl.when(jnp.logical_not(off_diagonal))
    def _():
        stay.wait()


def settle_grads(in_part, vec, cols, dw, tab, mix, ident):
    tokens, batches = lax.axis_size("seq"), lax.axis_size("batch")
    chips = tokens // 2
    low, wide = jnp.bfloat16, jnp.float32
    half = (chips,) + in_part.shape[2:]
    columns, group = dw.shape[1:]
    buckets, table_cols = tab.shape[1:]
    dw_pieces = (2, columns // 2, group)
    tab_pieces = (tokens, buckets // tokens, table_cols)
    mix_piece = mix.shape[1:]
    outs = (
        jax.ShapeDtypeStruct(half, low),
        jax.ShapeDtypeStruct((batches,) + vec.shape[1:], wide),
        like(cols, 2 * batches),
        jax.ShapeDtypeStruct(dw_pieces, low),
        jax.ShapeDtypeStruct(tab_pieces, low),
        jax.ShapeDtypeStruct((2,) + mix_piece, low),
    )
    scratch = (
        pltpu.VMEM(half, low),
        pltpu.VMEM(half, low),
        pltpu.VMEM((tokens - 1,) + vec.shape[1:], wide),
        pltpu.VMEM(vec.shape[1:], wide),
        pltpu.VMEM((batches - 1,) + dw.shape[1:], low),
        pltpu.VMEM(dw_pieces, low),
        pltpu.VMEM((batches - 1,) + tab.shape[1:], low),
        pltpu.VMEM(tab_pieces, low),
        pltpu.VMEM((batches - 1,) + mix_piece, low),
        pltpu.VMEM(mix_piece, low),
    )
    sends = (
        3 * (batches - 1) + chips + tokens - 1 + 2 * batches - 1
        + 2 + chips - 1 + tokens - 1 + 1 + batches - 1
    )
    inputs = (in_part, vec, cols, dw, tab, mix)
    return comm_call(settle_kernel, "settle_grads", ident, outs, inputs, sends, 6, scratch=scratch)


def finish_kernel(
    pre_ref, ins_ref, vecs_ref, cols_ref, dws_ref, tabs_ref, mixs_ref, ups_ref, downs_ref,
    upbs_ref,
    input_ref, dq_ref, dk_ref, dv_ref, mix_ref, table_ref, bias_ref, gain_ref, shift_ref,
    up_ref, upb_ref, down_ref, downb_ref,
):
    at = Place()
    wide = jnp.float32

    def total(ref):
        out = ref[0].astype(wide)
        for k in range(1, ref.shape[0]):
            out = out + ref[k].astype(wide)
        return out

    input_ref[...] = pre_ref[...] + total(ins_ref)
    up_ref[...] = total(ups_ref)
    down_ref[...] = total(downs_ref)
    upb_ref[...] = total(upbs_ref)[0:1]
    table_ref[...] = total(tabs_ref)
    group = 2 * DH
    spare = jnp.zeros((dws_ref.shape[1], DH), wide)
    for i, ref in enumerate((dq_ref, dk_ref, dv_ref)):
        lower = dws_ref[0, :, i * group : (i + 1) * group].astype(wide)
        upper = dws_ref[1, :, i * group : (i + 1) * group].astype(wide)
        ref[...] = jnp.concatenate([lower, spare], axis=1) + jnp.concatenate(
            [spare, upper], axis=1
        )
    rows = mix_ref.shape[0]
    lower, upper = mixs_ref[0].astype(wide), mixs_ref[1].astype(wide)
    spare = jnp.zeros((DH, lower.shape[1]), wide)
    whole = jnp.concatenate([lower, spare], axis=0) + jnp.concatenate([spare, upper], axis=0)
    mix_ref[...] = jnp.where(at.core == 0, whole[:rows], whole[rows:])
    small = total(vecs_ref)
    lanes = bias_ref.shape[1]
    cols = [cols_ref[core, 0:1] for core in range(2)]
    for row in range(1, at.batches):
        cols = [cols[core] + cols_ref[2 * row + core, 0:1] for core in range(2)]
    spare = jnp.zeros((1, DH), wide)
    biases = []
    for i in range(3):
        lower, upper = [part[:, i * group : (i + 1) * group] for part in cols]
        both = jnp.concatenate([lower, spare], axis=1) + jnp.concatenate([spare, upper], axis=1)
        biases.append(jnp.where(at.core == 0, both[:, :lanes], both[:, lanes:]))
    bias_ref[...] = jnp.concatenate(biases + [small[0:1, :lanes]], axis=0)
    gain_ref[...] = small[1:3, :lanes]
    shift_ref[...] = small[3:5, :lanes]
    downb_ref[...] = small[5:6, :lanes]


def finish(pre_grad, parts, shapes):
    inputs = (pre_grad,) + tuple(parts)
    return pl.pallas_call(
        finish_kernel,
        out_shape=tuple(jax.ShapeDtypeStruct(shape, jnp.float32) for shape in shapes),
        in_specs=[VMEM_SPEC] * len(inputs),
        out_specs=(VMEM_SPEC,) * len(shapes),
        compiler_params=pltpu.CompilerParams(vmem_limit_bytes=40 * 1024 * 1024),
        name="finish",
    )(*inputs)


def fits_fast(layer_input, table_shard, hidden_here):
    rows, local_len, width = layer_input.shape
    tokens, batches = lax.axis_size("seq"), lax.axis_size("batch")
    return (
        rows == 1
        and local_len == BLOCK
        and tokens == 2 * batches
        and width == 3 * DH * batches
        and (table_shard.shape[0] * tokens) % (4 * BLOCK) == 0
        and tokens % 4 == 0
        and 10 + hidden_here // BLOCK <= 16
        and hidden_here % BLOCK == 0
    )


def fast_body(
    layer_input, segment_ids, w_query, w_key, w_value, w_mix, rel_table, attn_biases,
    norm_gains, norm_shifts, w_up, up_bias, w_down, down_bias, out_grad,
):
    local_len, width = layer_input.shape[1:]
    low = jnp.bfloat16
    shard_rows, shard_cols = w_query.shape
    lanes = attn_biases.shape[1]
    hidden_here = w_up.shape[1]
    x = layer_input[0]
    pack = jnp.concatenate([attn_biases, norm_gains, norm_shifts, down_bias[None]], axis=0)
    pack = jnp.pad(pack, ((0, 0), (0, BLOCK - lanes)))
    pack = jnp.concatenate(
        [pack, segment_ids.astype(low), up_bias.reshape(hidden_here // BLOCK, BLOCK)], axis=0
    )
    pack = jnp.pad(pack, ((0, 16 - pack.shape[0]), (0, 0)))
    xs, qkvs, mts, vecs, up2, down2 = gather_inputs(
        x, w_query, w_key, w_value, w_mix, rel_table, pack, w_up, w_down
    )
    q, k, v, qrev, krev, probs, ctx, w_cat, m_mix, table = attend(xs, qkvs, mts, vecs)
    output, pre_grad, sums, attn_all, ups, downs, upbs = feed_forward(
        ctx, x, m_mix, vecs, w_up, w_down, up2, down2, out_grad[0], 1
    )
    in_part, dw_part, tab_part, mix_part, cols = attend_back(
        q, k, v, qrev, krev, probs, ctx, w_cat, m_mix, table, xs, attn_all
    )
    ins, vec_all, cols_all, dw_all, tab_all, mix_all = settle_grads(
        in_part, sums, cols, dw_part, tab_part, mix_part, 2
    )
    shard = (shard_rows, shard_cols)
    shapes = (
        x.shape, shard, shard, shard, shard, rel_table.shape, (4, lanes), (2, lanes), (2, lanes),
        (width // lax.axis_size("batch"), hidden_here), (1, hidden_here),
        (hidden_here, width // lax.axis_size("batch")), (1, lanes),
    )
    grads = finish(
        pre_grad,
        (ins, vec_all, cols_all, dw_all, tab_all, mix_all, ups, downs, upbs),
        shapes,
    )
    input_grad, dq, dk, dv, dmix, dtable, dbias, dgain, dshift, dup, dupb, ddown, ddownb = grads
    return (
        output[None], input_grad[None], dq, dk, dv, dmix, dtable, dbias, dgain, dshift,
        dup, dupb[0], ddown, ddownb[0],
    )


def body(
    layer_input,
    segment_ids,
    w_query,
    w_key,
    w_value,
    w_mix,
    rel_table,
    attn_biases,
    norm_gains,
    norm_shifts,
    w_up,
    up_bias,
    w_down,
    down_bias,
    out_grad,
):
    if fits_fast(layer_input, rel_table, w_up.shape[1]):
        return fast_body(
            layer_input, segment_ids, w_query, w_key, w_value, w_mix, rel_table, attn_biases,
            norm_gains, norm_shifts, w_up, up_bias, w_down, down_bias, out_grad,
        )
    rows, local_len, width = layer_input.shape
    full_len = local_len * lax.axis_size("seq")
    tokens_here = local_len * rows
    highest_prec = lax.Precision.HIGHEST
    parts = (
        lax.all_gather(w_query, "batch", axis=1, tiled=True),
        lax.all_gather(w_key, "batch", axis=1, tiled=True),
        lax.all_gather(w_value, "batch", axis=1, tiled=True),
        lax.all_gather(w_mix, "batch", axis=1, tiled=True),
        lax.all_gather(rel_table, "batch", axis=1, tiled=True),
    )
    whole = (
        lax.all_gather(parts[0], "seq", axis=0, tiled=True),
        lax.all_gather(parts[1], "seq", axis=0, tiled=True),
        lax.all_gather(parts[2], "seq", axis=0, tiled=True),
        lax.all_gather(parts[3], "seq", axis=0, tiled=True),
        lax.all_gather(parts[4], "seq", axis=0, tiled=True),
        lax.all_gather(attn_biases, "seq", axis=1, tiled=True),
        lax.all_gather(norm_gains, "seq", axis=1, tiled=True),
        lax.all_gather(norm_shifts, "seq", axis=1, tiled=True),
        lax.all_gather(down_bias, "seq", axis=0, tiled=True),
    )
    m_query, m_key, m_value, m_mix, table, biases, gains, shifts, bias_down = whole
    flat_input = jnp.swapaxes(layer_input, 0, 1).reshape(tokens_here, width)
    queries = (jnp.dot(flat_input, m_query, preferred_element_type=jnp.float32) + biases[0]).astype(
        jnp.bfloat16
    )
    keys_here = (jnp.dot(flat_input, m_key, preferred_element_type=jnp.float32) + biases[1]).astype(
        jnp.bfloat16
    )
    values_here = (
        jnp.dot(flat_input, m_value, preferred_element_type=jnp.float32) + biases[2]
    ).astype(jnp.bfloat16)
    query_rel = (jnp.dot(table, m_query, preferred_element_type=jnp.float32) + biases[0]).astype(
        jnp.bfloat16
    )
    key_rel = (jnp.dot(table, m_key, preferred_element_type=jnp.float32) + biases[1]).astype(
        jnp.bfloat16
    )
    local_seg = jnp.swapaxes(segment_ids, 0, 1).astype(jnp.bfloat16)
    keys_all, values_all, seg_all = (
        lax.all_gather(keys_here.reshape(local_len, rows, width), "seq", axis=0, tiled=True),
        lax.all_gather(values_here.reshape(local_len, rows, width), "seq", axis=0, tiled=True),
        lax.all_gather(local_seg, "seq", axis=0, tiled=True),
    )
    buckets = table.shape[0]
    offset = lax.axis_index("seq") * local_len
    bucket_iota = jnp.arange(buckets, dtype=jnp.int32)
    inner_cols = (bucket_iota > 0) & (bucket_iota < buckets - 1)
    same_doc = (
        jnp.swapaxes(local_seg, 0, 1)[:, None, :, None]
        == jnp.swapaxes(seg_all, 0, 1)[:, None, None, :]
    )
    score_scale = 1.0 / math.sqrt(3.0 * DH)
    head_queries = split_heads(queries.reshape(local_len, rows, width))
    head_keys = split_heads(keys_all)
    head_values = split_heads(values_all)
    rel_queries = split_table(query_rel)
    rel_keys = split_table(key_rel)

    def forward_group(carry, group):
        g_query, g_key, g_value, g_qrel, g_krel = group
        total, near_pull, far_pull, window = relative_scores(
            g_query, g_key, g_krel, g_qrel, offset, full_len
        )
        scores = jnp.where(same_doc, total * score_scale, masked_score)
        highest = jnp.max(scores, axis=-1, keepdims=True)
        exponent = jnp.exp(scores - highest)
        denominator = jnp.sum(exponent, axis=-1, keepdims=True)
        weights_low = (exponent / denominator).astype(jnp.bfloat16)
        context = jnp.einsum(
            "rgij,rgjd->rgid", weights_low, g_value, preferred_element_type=jnp.float32
        )
        return (carry, (context, (highest + jnp.log(denominator))[..., 0]))

    unused, (context_groups, log_totals) = lax.scan(
        forward_group, None, (head_queries, head_keys, head_values, rel_queries, rel_keys)
    )
    context_low = join_heads(context_groups).reshape(tokens_here, width).astype(jnp.bfloat16)
    pre_norm = (
        flat_input.astype(jnp.float32)
        + jnp.dot(context_low, m_mix, preferred_element_type=jnp.float32)
        + biases[3]
    )
    hidden, norm1_pull = jax.vjp(
        normalize, pre_norm, gains[0].astype(jnp.float32), shifts[0].astype(jnp.float32)
    )
    hidden_low = hidden.astype(jnp.bfloat16)

    def spread_rows(rows_low):
        return lax.all_gather(rows_low, "seq", axis=0, tiled=True)

    def hidden_sums(make_term):
        return lax.psum_scatter(
            make_term(jnp.int32(0), tokens_here * lax.axis_size("seq")),
            "seq",
            scatter_dimension=0,
            tiled=True,
        )

    hidden_rows = spread_rows(hidden_low)
    inner = jnp.dot(hidden_rows, w_up, preferred_element_type=jnp.float32) + up_bias
    act, gelu_pull = jax.vjp(exact_gelu, inner)
    act_low = act.astype(jnp.bfloat16)

    def down_rows(start, count):
        return jnp.dot(act_low, w_down, preferred_element_type=jnp.float32)

    ffn_result = hidden_sums(down_rows)
    mixed = hidden + ffn_result + bias_down
    output, norm2_pull = jax.vjp(
        normalize, mixed, gains[1].astype(jnp.float32), shifts[1].astype(jnp.float32)
    )
    flat_grad = jnp.swapaxes(out_grad, 0, 1).reshape(tokens_here, width).astype(jnp.float32)
    mixed_grad, gain2_grad, shift2_grad = norm2_pull(flat_grad)
    ffn_grad_low = mixed_grad.astype(jnp.bfloat16)
    grad_rows = spread_rows(ffn_grad_low)
    act_grad = jnp.einsum("nd,fd->nf", grad_rows, w_down, preferred_element_type=jnp.float32)
    inner_low = gelu_pull(act_grad)[0].astype(jnp.bfloat16)
    up_part = jnp.einsum("nd,nf->df", hidden_rows, inner_low, preferred_element_type=jnp.float32)
    upb_part = jnp.sum(inner_low.astype(jnp.float32), axis=0)
    down_part = jnp.einsum("nf,nd->fd", act_low, grad_rows, preferred_element_type=jnp.float32)

    def back_rows(start, count):
        return jnp.einsum("nf,df->nd", inner_low, w_up, preferred_element_type=jnp.float32)

    hidden_grad = mixed_grad + hidden_sums(back_rows)
    pre_grad, gain1_grad, shift1_grad = norm1_pull(hidden_grad)
    attn_low = pre_grad.astype(jnp.bfloat16)
    mix_whole = jnp.einsum("nd,ne->de", context_low, attn_low, preferred_element_type=jnp.float32)
    context_grad = jnp.einsum(
        "ne,de->nd", attn_low, m_mix, preferred_element_type=jnp.float32
    ).astype(jnp.bfloat16)
    head_context_grad = split_heads(context_grad.reshape(local_len, rows, width))

    def query_side(group):
        g_query, g_key, g_value, g_qrel, g_krel, g_dctx, g_lse = group
        total, near_pull, far_pull, window = relative_scores(
            g_query, g_key, g_krel, g_qrel, offset, full_len
        )
        scores = jnp.where(same_doc, total * score_scale, masked_score)
        weights_now = jnp.exp(scores - g_lse[..., None])
        prob_grad = jnp.einsum(
            "rgid,rgjd->rgij", g_dctx, g_value, preferred_element_type=jnp.float32
        )
        inner_sum = jnp.sum(weights_now * prob_grad, axis=-1)
        score_grad = (weights_now * (prob_grad - inner_sum[..., None])).astype(jnp.bfloat16)
        grad_wide = score_grad.astype(jnp.float32)
        near_grad = near_pull(grad_wide)[0]
        near_low = jnp.where(inner_cols, near_grad, 0.0).astype(jnp.bfloat16)
        near_ends = end_columns(near_grad)
        query_part = jnp.einsum(
            "rgij,rgjd->rgid", score_grad, g_key, preferred_element_type=jnp.float32
        )
        query_part = (
            query_part
            + jnp.einsum("rgib,gbd->rgid", near_low, g_krel, preferred_element_type=jnp.float32)
            + end_terms(near_ends, g_krel)
        )
        krel_part = with_ends(
            jnp.einsum("rgib,rgid->gbd", near_low, g_query, preferred_element_type=jnp.float32),
            end_rows(near_ends, g_query),
        )
        return (
            weights_now,
            score_grad,
            grad_wide,
            far_pull,
            window,
            inner_sum,
            query_part * score_scale,
            krel_part * score_scale,
        )

    query_groups = (
        head_queries,
        head_keys,
        head_values,
        rel_queries,
        rel_keys,
        head_context_grad,
        log_totals,
    )

    def all_grads(carry, group):
        weights_now, score_grad, grad_wide, far_pull, window, inner_sum, query_part, krel_part = (
            query_side(group)
        )
        g_query, g_key, g_value, g_qrel, g_krel, g_dctx, g_lse = group
        cross_grad, end_grad = far_pull(grad_wide)
        cross_low = cross_grad.astype(jnp.bfloat16)
        key_part = jnp.einsum(
            "rgij,rgid->rgjd", score_grad, g_query, preferred_element_type=jnp.float32
        )
        band_part = jnp.einsum(
            "rgmb,gbd->rgmd", cross_low, g_qrel, preferred_element_type=jnp.float32
        )
        key_part = (
            key_part
            + unband(band_part, offset, full_len, buckets // 2)
            + end_terms(end_grad, g_qrel)
        )
        value_part = jnp.einsum(
            "rgij,rgid->rgjd",
            weights_now.astype(jnp.bfloat16),
            g_dctx,
            preferred_element_type=jnp.float32,
        )
        qrel_part = with_ends(
            jnp.einsum("rgmb,rgmd->gbd", cross_low, window, preferred_element_type=jnp.float32),
            end_rows(end_grad, g_key),
        )
        return (
            carry,
            (query_part, key_part * score_scale, value_part, qrel_part * score_scale, krel_part),
        )

    unused, (dq_groups, dk_groups, dv_groups, dqrel_groups, dkrel_groups) = lax.scan(
        all_grads, None, query_groups
    )
    key_sum, value_sum = (
        lax.psum_scatter(join_heads(dk_groups), "seq", scatter_dimension=0, tiled=True),
        lax.psum_scatter(join_heads(dv_groups), "seq", scatter_dimension=0, tiled=True),
    )
    key_grads = key_sum.reshape(tokens_here, width).astype(jnp.bfloat16)
    value_grads = value_sum.reshape(tokens_here, width).astype(jnp.bfloat16)
    query_grads = join_heads(dq_groups).reshape(tokens_here, width).astype(jnp.bfloat16)
    qrel_grad = join_table(dqrel_groups)
    krel_grad = join_table(dkrel_groups)
    input_grad = pre_grad + jnp.einsum(
        "ne,de->nd", query_grads, m_query, preferred_element_type=jnp.float32
    )
    input_grad = input_grad + jnp.einsum(
        "ne,de->nd", key_grads, m_key, preferred_element_type=jnp.float32
    )
    input_grad = input_grad + jnp.einsum(
        "ne,de->nd", value_grads, m_value, preferred_element_type=jnp.float32
    )
    query_whole = jnp.einsum(
        "nd,ne->de", flat_input, query_grads, preferred_element_type=jnp.float32
    ) + jnp.einsum(
        "bd,be->de", table, qrel_grad, precision=highest_prec, preferred_element_type=jnp.float32
    )
    key_whole = jnp.einsum(
        "nd,ne->de", flat_input, key_grads, preferred_element_type=jnp.float32
    ) + jnp.einsum(
        "bd,be->de", table, krel_grad, precision=highest_prec, preferred_element_type=jnp.float32
    )
    value_whole = jnp.einsum(
        "nd,ne->de", flat_input, value_grads, preferred_element_type=jnp.float32
    )
    table_whole = jnp.einsum(
        "be,de->bd", qrel_grad, m_query, precision=highest_prec, preferred_element_type=jnp.float32
    ) + jnp.einsum(
        "be,de->bd", krel_grad, m_key, precision=highest_prec, preferred_element_type=jnp.float32
    )
    bias_whole = jnp.stack(
        [
            jnp.sum(query_grads.astype(jnp.float32), axis=0) + jnp.sum(qrel_grad, axis=0),
            jnp.sum(key_grads.astype(jnp.float32), axis=0) + jnp.sum(krel_grad, axis=0),
            jnp.sum(value_grads.astype(jnp.float32), axis=0),
            jnp.sum(pre_grad, axis=0),
        ]
    )
    gain_whole = jnp.stack([gain1_grad, gain2_grad])
    shift_whole = jnp.stack([shift1_grad, shift2_grad])
    downb_whole = jnp.sum(mixed_grad, axis=0)
    seq_parts = (
        lax.psum_scatter(query_whole, "seq", scatter_dimension=0, tiled=True),
        lax.psum_scatter(key_whole, "seq", scatter_dimension=0, tiled=True),
        lax.psum_scatter(value_whole, "seq", scatter_dimension=0, tiled=True),
        lax.psum_scatter(mix_whole, "seq", scatter_dimension=0, tiled=True),
        lax.psum_scatter(table_whole, "seq", scatter_dimension=0, tiled=True),
        lax.psum_scatter(bias_whole, "seq", scatter_dimension=1, tiled=True),
        lax.psum_scatter(gain_whole, "seq", scatter_dimension=1, tiled=True),
        lax.psum_scatter(shift_whole, "seq", scatter_dimension=1, tiled=True),
        lax.psum_scatter(downb_whole, "seq", scatter_dimension=0, tiled=True),
    )
    batch_parts = (
        lax.psum_scatter(seq_parts[0], "batch", scatter_dimension=1, tiled=True),
        lax.psum_scatter(seq_parts[1], "batch", scatter_dimension=1, tiled=True),
        lax.psum_scatter(seq_parts[2], "batch", scatter_dimension=1, tiled=True),
        lax.psum_scatter(seq_parts[3], "batch", scatter_dimension=1, tiled=True),
        lax.psum_scatter(seq_parts[4], "batch", scatter_dimension=1, tiled=True),
        lax.psum_scatter(up_part, "batch", scatter_dimension=0, tiled=True),
        lax.psum_scatter(down_part, "batch", scatter_dimension=1, tiled=True),
    )
    small_parts = lax.psum(
        (seq_parts[5], seq_parts[6], seq_parts[7], seq_parts[8], upb_part), "batch"
    )
    layer_output = jnp.swapaxes(output.reshape(local_len, rows, width), 0, 1).astype(jnp.bfloat16)
    input_back = jnp.swapaxes(input_grad.reshape(local_len, rows, width), 0, 1)
    return (
        layer_output,
        input_back,
        batch_parts[0],
        batch_parts[1],
        batch_parts[2],
        batch_parts[3],
        batch_parts[4],
        small_parts[0],
        small_parts[1],
        small_parts[2],
        batch_parts[5],
        small_parts[4],
        batch_parts[6],
        small_parts[3],
    )


def solution(mesh):
    return jax.shard_map(
        body,
        mesh=mesh,
        in_specs=(
            P("batch", "seq", None),
            P("batch", "seq"),
            P("seq", "batch"),
            P("seq", "batch"),
            P("seq", "batch"),
            P("seq", "batch"),
            P("seq", "batch"),
            P(None, "seq"),
            P(None, "seq"),
            P(None, "seq"),
            P(None, "seq"),
            P("seq"),
            P("seq", None),
            P("seq"),
            P("batch", "seq", None),
        ),
        out_specs=(
            P("batch", "seq", None),
            P("batch", "seq", None),
            P("seq", "batch"),
            P("seq", "batch"),
            P("seq", "batch"),
            P("seq", "batch"),
            P("seq", "batch"),
            P(None, "seq"),
            P(None, "seq"),
            P(None, "seq"),
            P("batch", "seq"),
            P("seq"),
            P("seq", "batch"),
            P("seq"),
        ),
        check_vma=False,
    )
```

```python
import math

import jax
import jax.numpy as jnp
from jax import lax
from jax.experimental import pallas as pl
from jax.experimental.pallas import tpu as pltpu
from jax.sharding import PartitionSpec as P

DH = 64


masked_score = -1e30
norm_eps = 1e-06
pair_heads = 2


def normalize(values, gain, shift):
    average = jnp.mean(values, axis=-1, keepdims=True)
    centered = values - average
    variance = jnp.mean(centered * centered, axis=-1, keepdims=True)
    return centered * lax.rsqrt(variance + norm_eps) * gain + shift


def exact_gelu(values):
    return jax.nn.gelu(values, approximate=False)


def split_heads(matrix):
    length, rows, width = matrix.shape
    groups = width // (pair_heads * DH)
    return matrix.reshape(length, rows, groups, pair_heads, DH).transpose(2, 1, 3, 0, 4)


def join_heads(matrix):
    groups, rows, pair, length, depth = matrix.shape
    return matrix.transpose(3, 1, 0, 2, 4).reshape(length, rows, groups * pair * depth)


def split_table(matrix):
    buckets, width = matrix.shape
    return matrix.reshape(buckets, width // (pair_heads * DH), pair_heads, DH).transpose(1, 2, 0, 3)


def join_table(matrix):
    groups, pair, buckets, depth = matrix.shape
    return matrix.transpose(2, 0, 1, 3).reshape(buckets, groups * pair * depth)


def table_ends(table):
    return jnp.stack([table[:, 0], table[:, -1]], axis=1)


def near_skew(table_prod, offset, full_len):
    lead = table_prod.shape[:-2]
    count, buckets = table_prod.shape[-2:]
    span = buckets // 2
    lead_pad = [(0, 0)] * len(lead)
    flipped = jnp.pad(table_prod[..., ::-1], lead_pad + [(0, 0), (0, count)])
    sheared = flipped.reshape(lead + (count * (buckets + count),))[
        ..., : count * (buckets + count - 1)
    ]
    sheared = sheared.reshape(lead + (count, buckets + count - 1))
    spread = jnp.pad(sheared, lead_pad + [(0, 0), (full_len, full_len)])
    band = lax.dynamic_slice_in_dim(
        spread, full_len + span - 1 - offset, full_len, axis=len(lead) + 1
    )
    distance = (offset + jnp.arange(count, dtype=jnp.int32))[:, None] - jnp.arange(
        full_len, dtype=jnp.int32
    )[None, :]
    return jnp.where(
        distance <= -span,
        table_prod[..., 0:1],
        jnp.where(distance >= span - 1, table_prod[..., buckets - 1 :], band),
    )


def far_place(cross, end_vals, offset, count, full_len):
    lead = cross.shape[:-2]
    band_len, buckets = cross.shape[-2:]
    span = buckets // 2
    lead_pad = [(0, 0)] * len(lead)
    turned = jnp.swapaxes(cross, -1, -2).reshape(lead + (buckets * band_len,))
    turned = jnp.pad(turned, lead_pad + [(0, buckets)])
    diagonal = turned.reshape(lead + (buckets, band_len + 1))[..., :count]
    aligned = jnp.pad(jnp.swapaxes(diagonal, -1, -2), lead_pad + [(0, 0), (0, count)])
    sheared = aligned.reshape(lead + (count * (buckets + count),))[
        ..., : count * (buckets + count - 1)
    ]
    sheared = sheared.reshape(lead + (count, buckets + count - 1))
    spread = jnp.pad(sheared, lead_pad + [(0, 0), (full_len, full_len)])
    band = lax.dynamic_slice_in_dim(spread, full_len + span - offset, full_len, axis=len(lead) + 1)
    distance = (
        jnp.arange(full_len, dtype=jnp.int32)[None, :]
        - (offset + jnp.arange(count, dtype=jnp.int32))[:, None]
    )
    return jnp.where(
        distance <= -span,
        end_vals[..., 0:1, :],
        jnp.where(distance >= span - 1, end_vals[..., 1:2, :], band),
    )


def band_rows(all_rows, offset, count, span):
    padded = jnp.pad(all_rows, [(0, 0), (0, 0), (span, span), (0, 0)])
    return lax.dynamic_slice_in_dim(padded, offset, count + 2 * span - 1, axis=2)


def unband(values, offset, full_len, span):
    lead = values.shape[:2]
    room = jnp.zeros(lead + (full_len + 2 * span, values.shape[3]), jnp.float32)
    placed = lax.dynamic_update_slice_in_dim(room, values, offset, axis=2)
    return placed[:, :, span : span + full_len]


def relative_scores(own_rows, all_rows, own_table, all_table, offset, full_len):
    count = own_rows.shape[2]
    content = jnp.einsum("rgid,rgjd->rgij", own_rows, all_rows, preferred_element_type=jnp.float32)
    own_prod = jnp.einsum("rgid,gbd->rgib", own_rows, own_table, preferred_element_type=jnp.float32)
    window = band_rows(all_rows, offset, count, all_table.shape[1] // 2)
    cross = jnp.einsum("rgmd,gbd->rgmb", window, all_table, preferred_element_type=jnp.float32)
    end_vals = jnp.einsum(
        "rgjd,ged->rgej", all_rows, table_ends(all_table), preferred_element_type=jnp.float32
    )
    near_vals, near_pull = jax.vjp(lambda product: near_skew(product, offset, full_len), own_prod)
    far_vals, far_pull = jax.vjp(
        lambda part, ends: far_place(part, ends, offset, count, full_len), cross, end_vals
    )
    return (content + near_vals + far_vals, near_pull, far_pull, window)


def end_columns(grad):
    return jnp.stack([grad[..., 0], grad[..., -1]], axis=2)


def end_terms(ends, table):
    return jnp.einsum(
        "rgei,ged->rgid",
        ends,
        table_ends(table),
        precision=lax.Precision.HIGHEST,
        preferred_element_type=jnp.float32,
    )


def end_rows(ends, rows_low):
    return jnp.einsum(
        "rgei,rgid->ged",
        ends,
        rows_low,
        precision=lax.Precision.HIGHEST,
        preferred_element_type=jnp.float32,
    )


def with_ends(inner_part, edge_rows):
    buckets = inner_part.shape[1]
    place = jnp.arange(buckets, dtype=jnp.int32)[None, :, None]
    return (
        inner_part
        + jnp.where(place == 0, edge_rows[:, 0:1], 0.0)
        + jnp.where(place == buckets - 1, edge_rows[:, 1:2], 0.0)
    )


BLOCK = 128
MIB = 1024 * 1024
ATTEND_VMEM = 26 * MIB
BACK_VMEM = 26 * MIB
FEED_VMEM = 26 * MIB
COMM_VMEM = 16 * MIB


def dot_nn(a, b):
    return lax.dot_general(a, b, (((1,), (0,)), ((), ())), preferred_element_type=jnp.float32)


def dot_nt(a, b):
    return lax.dot_general(a, b, (((1,), (1,)), ((), ())), preferred_element_type=jnp.float32)


def dot_tn(a, b):
    return lax.dot_general(a, b, (((0,), (0,)), ((), ())), preferred_element_type=jnp.float32)


def turn_matrix(buckets):
    row = lax.broadcasted_iota(jnp.int32, (buckets, buckets), 0)
    col = lax.broadcasted_iota(jnp.int32, (buckets, buckets), 1)
    return (row + col == buckets - 1).astype(jnp.bfloat16)


def skew_band(product):
    count, buckets = product.shape
    row = lax.broadcasted_iota(jnp.int32, (count, BLOCK), 0)
    lane = lax.broadcasted_iota(jnp.int32, (count, BLOCK), 1)
    edge = jnp.where(row + lane <= BLOCK - 2, product[:, buckets - 1 :], product[:, 0:1])
    wide = jnp.concatenate([product, edge], axis=1)
    return pltpu.roll(wide, 1, 1, stride=1, stride_axis=0)


def skew_back(turned, buckets):
    return pltpu.roll(turned, turned.shape[1] - BLOCK, 1, stride=1, stride_axis=0)[:, :buckets]


def chip_columns(vec_ref, chip, index, core):
    width = 3 * DH // 2
    both = jnp.concatenate(
        [
            vec_ref[2 * chip, index : index + 1, :width].astype(jnp.float32),
            vec_ref[2 * chip + 1, index : index + 1, :width].astype(jnp.float32),
        ],
        axis=1,
    )
    return jnp.where(core == 0, both[:, : 2 * DH], both[:, DH:])


def attend_kernel(
    xs_ref,
    qkvs_ref,
    mts_ref,
    vecs_ref,
    q_ref,
    k_ref,
    v_ref,
    qrev_ref,
    krev_ref,
    p_ref,
    ctx_ref,
    w_ref,
    mix_ref,
    table_ref,
    segc_ref,
    place_ref,
    wide_ref,
    ends_ref,
    held_ref,
):
    at = Place()
    full_len = xs_ref.shape[0] * xs_ref.shape[1]
    buckets = table_ref.shape[0]
    blocks = full_len // BLOCK
    span = buckets // 2
    side = span // BLOCK
    band_width = buckets + BLOCK
    band_blocks = band_width // BLOCK
    group = 2 * DH
    scale = 1.0 / math.sqrt(3.0 * DH)
    units = p_ref.shape[0]
    shard_rows = qkvs_ref.shape[2]
    table_rows = mts_ref.shape[3] - shard_rows
    batches = mts_ref.shape[1]
    for part in range(at.tokens):
        pieces = []
        for i in range(3):
            piece = qkvs_ref[part, i]
            pieces.append(jnp.where(at.core == 0, piece[:, :group], piece[:, DH:]))
        w_ref[part * shard_rows : (part + 1) * shard_rows] = jnp.concatenate(pieces, axis=1)
        core, chip = part % 2, part // 2
        whole = [mts_ref[core, row, chip] for row in range(batches)]
        mix_ref[part * shard_rows : (part + 1) * shard_rows] = jnp.concatenate(
            [piece[:shard_rows] for piece in whole], axis=1
        )
        table_ref[part * table_rows : (part + 1) * table_rows] = jnp.concatenate(
            [piece[shard_rows:] for piece in whole], axis=1
        )
        own_seg = vecs_ref[part, 9:10].astype(jnp.float32)
        segc_ref[part * BLOCK : (part + 1) * BLOCK] = jnp.broadcast_to(own_seg, (BLOCK, BLOCK)).T
    seg_row = jnp.concatenate(
        [vecs_ref[part, 9:10].astype(jnp.float32) for part in range(at.tokens)], axis=1
    )
    bias = jnp.concatenate(
        [chip_columns(vecs_ref, at.chip, i, at.core) for i in range(3)], axis=1
    )
    tokens_all = xs_ref[...].reshape(full_len, xs_ref.shape[2])
    proj = (dot_nn(tokens_all, w_ref[...]) + bias).astype(jnp.bfloat16)
    rel = (dot_nn(table_ref[...], w_ref[:, : 2 * group]) + bias[:, : 2 * group]).astype(
        jnp.bfloat16
    )
    rel = dot_nn(turn_matrix(buckets), rel).astype(jnp.bfloat16)
    for slot in range(2):
        lo, hi = slot * DH, (slot + 1) * DH
        q_ref[slot] = proj[:, lo:hi]
        k_ref[slot] = proj[:, group + lo : group + hi]
        v_ref[slot] = proj[:, 2 * group + lo : 2 * group + hi]
        qrev_ref[slot] = rel[:, lo:hi]
        krev_ref[slot] = rel[:, group + lo : group + hi]
    held_ref[...] = jnp.zeros_like(held_ref)
    for slot in range(2):
        ends_ref[slot, 0] = dot_nt(qrev_ref[slot, 0:16], k_ref[slot])
        ends_ref[slot, 1] = dot_nt(qrev_ref[slot, buckets - 16 : buckets], k_ref[slot])

        def key_block(kb, carry):
            rows = k_ref[slot, pl.ds(pl.multiple_of(kb * BLOCK, BLOCK), BLOCK)]
            band = skew_band(dot_nt(rows, qrev_ref[slot]))
            for e in range(band_blocks):
                place_ref[
                    slot,
                    kb + e,
                    :,
                    (band_blocks - 1 - e) * BLOCK : (band_blocks - e) * BLOCK,
                ] = band[:, e * BLOCK : (e + 1) * BLOCK].T
            return carry

        lax.fori_loop(0, blocks, key_block, 0)

    first = at.core * (blocks // 2)

    def unit(u, carry):
        g = u + first
        slot = g // blocks
        qb = g % blocks
        start = pl.multiple_of(qb * BLOCK, BLOCK)
        rows = q_ref[slot, pl.ds(start, BLOCK)]
        own = dot_nt(rows, krev_ref[slot])
        band = skew_band(own) + place_ref[slot, qb + side]
        wide_ref[:, pl.ds(start, band_width)] = band
        content = dot_nt(rows, k_ref[slot])
        lane = lax.broadcasted_iota(jnp.int32, (BLOCK, full_len), 1)
        near = jnp.where(
            lane < start - span,
            own[:, 0:1] + ends_ref[slot, 1, 15:16],
            jnp.where(
                lane >= start + band_width - span,
                own[:, buckets - 1 :] + ends_ref[slot, 0, 0:1],
                wide_ref[:, span : span + full_len],
            ),
        )
        same = segc_ref[pl.ds(start, BLOCK), 0:1] == seg_row
        scores = jnp.where(same, (content + near) * scale, masked_score)
        highest = jnp.max(scores, axis=-1, keepdims=True)
        exponent = jnp.exp(scores - highest)
        total = jnp.sum(exponent, axis=-1, keepdims=True)
        probs = (exponent / total).astype(jnp.bfloat16)
        p_ref[u] = probs
        held_ref[slot, pl.ds(start, BLOCK)] = dot_nn(probs, v_ref[slot]).astype(jnp.bfloat16)
        return carry

    lax.fori_loop(0, units, unit, 0)
    for part in range(at.tokens):
        rows = slice(part * BLOCK, (part + 1) * BLOCK)
        ctx_ref[part] = jnp.concatenate([held_ref[0, rows], held_ref[1, rows]], axis=1)


def attend(xs, qkvs, mts, vecs):
    tokens, local_len, width = xs.shape
    full_len = tokens * local_len
    shard_rows = qkvs.shape[2]
    buckets = tokens * (mts.shape[3] - shard_rows)
    blocks = full_len // BLOCK
    units = 3 * blocks // 2
    band_width = buckets + BLOCK
    low, wide = jnp.bfloat16, jnp.float32
    pad_blocks = blocks + band_width // BLOCK - 1
    return pl.pallas_call(
        attend_kernel,
        out_shape=(
            jax.ShapeDtypeStruct((2, full_len, DH), low),
            jax.ShapeDtypeStruct((2, full_len, DH), low),
            jax.ShapeDtypeStruct((2, full_len, DH), low),
            jax.ShapeDtypeStruct((2, buckets, DH), low),
            jax.ShapeDtypeStruct((2, buckets, DH), low),
            jax.ShapeDtypeStruct((units, BLOCK, full_len), low),
            jax.ShapeDtypeStruct((tokens, local_len, 2 * DH), low),
            jax.ShapeDtypeStruct((width, 6 * DH), low),
            jax.ShapeDtypeStruct((width, width), low),
            jax.ShapeDtypeStruct((buckets, width), low),
        ),
        in_specs=[pl.BlockSpec(memory_space=pltpu.VMEM)] * 4,
        out_specs=[pl.BlockSpec(memory_space=pltpu.VMEM)] * 10,
        scratch_shapes=[
            pltpu.VMEM((full_len, BLOCK), wide),
            pltpu.VMEM((2, pad_blocks, BLOCK, band_width), wide),
            pltpu.VMEM((BLOCK, full_len + buckets), wide),
            pltpu.VMEM((2, 2, 16, full_len), wide),
            pltpu.VMEM((2, full_len, DH), low),
        ],
        compiler_params=pltpu.CompilerParams(vmem_limit_bytes=ATTEND_VMEM),
        name="attend",
    )(xs, qkvs, mts, vecs)


def attend_back_kernel(
    q_ref,
    k_ref,
    v_ref,
    qrev_ref,
    krev_ref,
    p_ref,
    mix_ref,
    attn_ref,
    dcat_ref,
    rel_ref,
    sum_ref,
    heads_ref,
    wide_ref,
    low_ref,
    place_ref,
    dq_ref,
    dkt_ref,
    dvt_ref,
    far_ref,
    dkr_ref,
    dqr_ref,
):
    full_len = q_ref.shape[1]
    buckets = qrev_ref.shape[1]
    blocks = full_len // BLOCK
    span = buckets // 2
    side = span // BLOCK
    band_width = buckets + BLOCK
    band_blocks = band_width // BLOCK
    scale = 1.0 / math.sqrt(3.0 * DH)
    units = p_ref.shape[0]
    for ref in (wide_ref, low_ref, place_ref, dq_ref, dkt_ref, dvt_ref, far_ref, dkr_ref, dqr_ref):
        ref[...] = jnp.zeros_like(ref)
    at = Place()
    group = 2 * DH
    first_row = pl.multiple_of((3 * at.chip + at.core) * DH, DH)
    mix_rows = mix_ref[pl.ds(first_row, group)]
    dctx = dot_nt(attn_ref[...].reshape(full_len, attn_ref.shape[2]), mix_rows)
    for slot in range(2):
        heads_ref[slot] = dctx[:, slot * DH : (slot + 1) * DH].astype(jnp.bfloat16)
    first = at.core * (blocks // 2)
    turn = turn_matrix(BLOCK)
    place8 = lax.broadcasted_iota(jnp.int32, (8, full_len), 0)

    def unit(u, carry):
        g = u + first
        slot = g // blocks
        qb = g % blocks
        start = pl.multiple_of(qb * BLOCK, BLOCK)
        rows = q_ref[slot, pl.ds(start, BLOCK)]
        grad = heads_ref[slot, pl.ds(start, BLOCK)]
        probs = p_ref[u]
        wide_probs = probs.astype(jnp.float32)
        prob_grad = dot_nt(grad, v_ref[slot])
        inner = jnp.sum(wide_probs * prob_grad, axis=-1, keepdims=True)
        low_grad = (wide_probs * (prob_grad - inner)).astype(jnp.bfloat16)
        score_grad = low_grad.astype(jnp.float32)
        wide_ref[:, span : span + full_len] = dot_nn(turn, low_grad)
        low_ref[:, span : span + full_len] = low_grad
        dvt_ref[slot] += dot_tn(grad, probs)
        dkt_ref[slot] += dot_tn(rows, low_grad)
        row = lax.broadcasted_iota(jnp.int32, (BLOCK, full_len), 0)
        lane = lax.broadcasted_iota(jnp.int32, (BLOCK, full_len), 1)
        gap = lane - row - start
        right = jnp.where(gap > span, score_grad, 0.0)
        left = jnp.where(gap < 1 - span, score_grad, 0.0)
        end_right = jnp.sum(right, axis=-1, keepdims=True)
        end_left = jnp.sum(left, axis=-1, keepdims=True)
        far_right = jnp.sum(jnp.where(gap >= span, score_grad, 0.0), axis=0, keepdims=True)
        far_left = jnp.sum(jnp.where(gap < -span, score_grad, 0.0), axis=0, keepdims=True)
        far_ref[slot] += jnp.where(place8 == 0, far_right, jnp.where(place8 == 1, far_left, 0.0))
        band = wide_ref[:, pl.ds(start, band_width)]
        near = dot_nn(turn, skew_back(band, buckets).astype(jnp.bfloat16))
        bucket = lax.broadcasted_iota(jnp.int32, (BLOCK, buckets), 1)
        near = near + jnp.where(
            bucket == 0, end_left, jnp.where(bucket == buckets - 1, end_right, 0.0)
        )
        near_low = near.astype(jnp.bfloat16)
        dq = dot_nn(low_grad, k_ref[slot]) + dot_nn(near_low, krev_ref[slot])
        dq_ref[slot, pl.ds(start, BLOCK)] = dq
        dkr_ref[slot] += dot_tn(rows, near_low)
        for e in range(band_blocks):
            keys_at = pl.multiple_of(start + e * BLOCK, BLOCK)
            place_ref[
                slot, qb + e, :, (band_blocks - 1 - e) * BLOCK : (band_blocks - e) * BLOCK
            ] = dot_nt(turn, low_ref[:, pl.ds(keys_at, BLOCK)])
        return carry

    lax.fori_loop(0, units, unit, 0)
    parts_q, parts_k, parts_v = [], [], []
    parts_r = [None] * 4
    for slot in range(2):
        far_low = far_ref[slot].astype(jnp.bfloat16)
        mark = lax.broadcasted_iota(jnp.int32, (8, DH), 0)
        ends = jnp.where(
            mark == 0,
            qrev_ref[slot, 0:1].astype(jnp.float32),
            jnp.where(mark == 1, qrev_ref[slot, buckets - 1 : buckets].astype(jnp.float32), 0.0),
        ).astype(jnp.bfloat16)
        end_keys = dot_tn(ends, far_low)
        end_rows = dot_nn(far_low, k_ref[slot])

        whole_k = (dkt_ref[slot] + end_keys).T

        def key_side(kb, carry):
            start = pl.multiple_of(kb * BLOCK, BLOCK)
            far = skew_back(place_ref[slot, kb + side], buckets).astype(jnp.bfloat16)
            far = dot_nn(turn, far).astype(jnp.bfloat16)
            keys = k_ref[slot, pl.ds(start, BLOCK)]
            dqr_ref[slot] += dot_tn(keys, far)
            dq_ref[2 + slot, pl.ds(start, BLOCK)] = dot_nn(far, qrev_ref[slot])
            return carry

        lax.fori_loop(0, blocks, key_side, 0)
        parts_q.append((dq_ref[slot] * scale).astype(jnp.bfloat16))
        parts_k.append(((dq_ref[2 + slot] + whole_k) * scale).astype(jnp.bfloat16))
        parts_v.append(dvt_ref[slot].T.astype(jnp.bfloat16))
        bucket = lax.broadcasted_iota(jnp.int32, (buckets, DH), 0)
        qr = dqr_ref[slot].T + jnp.where(
            bucket == 0, end_rows[0:1], jnp.where(bucket == buckets - 1, end_rows[1:2], 0.0)
        )
        dqr_out = qr * scale
        dkr_out = dkr_ref[slot].T * scale
        parts_r[slot] = dqr_out
        parts_r[2 + slot] = dkr_out
    dcat = jnp.concatenate(parts_q + parts_k + parts_v, axis=1)
    dcat_ref[...] = dcat
    rel = jnp.concatenate(parts_r, axis=1)
    rel_ref[...] = dot_nn(turn_matrix(buckets), rel.astype(jnp.bfloat16)).astype(jnp.bfloat16)
    rel_sum = jnp.sum(rel, axis=0, keepdims=True)
    rel_sum = jnp.concatenate([rel_sum, jnp.zeros((1, 2 * DH), jnp.float32)], axis=1)
    sums = jnp.sum(dcat.astype(jnp.float32), axis=0, keepdims=True) + rel_sum
    sum_ref[...] = jnp.broadcast_to(sums, sum_ref.shape)


def attend_back(q, k, v, qrev, krev, probs, m_mix, attn_all):
    full_len = q.shape[1]
    buckets = qrev.shape[1]
    blocks = full_len // BLOCK
    band_width = buckets + BLOCK
    low, wide = jnp.bfloat16, jnp.float32
    pad_blocks = blocks + band_width // BLOCK - 1
    return pl.pallas_call(
        attend_back_kernel,
        out_shape=(
            jax.ShapeDtypeStruct((full_len, 6 * DH), low),
            jax.ShapeDtypeStruct((buckets, 4 * DH), low),
            jax.ShapeDtypeStruct((8, 6 * DH), wide),
        ),
        in_specs=[pl.BlockSpec(memory_space=pltpu.VMEM)] * 8,
        out_specs=[pl.BlockSpec(memory_space=pltpu.VMEM)] * 3,
        scratch_shapes=[
            pltpu.VMEM((2, full_len, DH), low),
            pltpu.VMEM((BLOCK, full_len + buckets), wide),
            pltpu.VMEM((BLOCK, full_len + buckets), low),
            pltpu.VMEM((2, pad_blocks, BLOCK, band_width), wide),
            pltpu.VMEM((4, full_len, DH), wide),
            pltpu.VMEM((2, DH, full_len), wide),
            pltpu.VMEM((2, DH, full_len), wide),
            pltpu.VMEM((2, 8, full_len), wide),
            pltpu.VMEM((2, DH, buckets), wide),
            pltpu.VMEM((2, DH, buckets), wide),
        ],
        compiler_params=pltpu.CompilerParams(vmem_limit_bytes=BACK_VMEM),
        name="attend_back",
    )(q, k, v, qrev, krev, probs, m_mix, attn_all)


MESH = pl.DeviceIdType.MESH
VMEM_SPEC = pl.BlockSpec(memory_space=pltpu.VMEM)
ANY_SPEC = pl.BlockSpec(memory_space=pl.ANY)


class Place:
    def __init__(self):
        self.batches = lax.axis_size("batch")
        self.tokens = lax.axis_size("seq")
        self.chips = self.tokens // 2
        self.row = lax.axis_index("batch")
        self.part = lax.axis_index("seq")
        self.chip = self.part // 2
        self.core = self.part % 2

    def along_chips(self, k):
        chip = lax.rem(self.chip + k, self.chips)
        return chip, (self.row, 2 * chip + self.core)

    def from_chips(self, k):
        return lax.rem(self.chip + self.chips - k, self.chips)

    def partner(self):
        return (self.row, self.part + 1 - 2 * self.core)

    def along_rows(self, k):
        row = lax.rem(self.row + k, self.batches)
        return row, (row, self.part)

    def from_rows(self, k):
        return lax.rem(self.row + self.batches - k, self.batches)

    def along_seq(self, k):
        part = lax.rem(self.part + k, self.tokens)
        return part, (self.row, part)

    def along_plane(self, k):
        index = lax.rem(2 * self.row + self.core + k, 2 * self.batches)
        row, core = index // 2, index % 2
        return row, core, (row, 2 * self.chip + core)

    def chip_peers(self):
        return [self.along_chips(k)[1] for k in range(1, self.chips)]

    def row_peers(self):
        return [self.along_rows(k)[1] for k in range(1, self.batches)]

    def cross_peers(self):
        other = self.part + 1 - 2 * self.core
        return [(self.along_rows(k)[0], other) for k in range(1, self.batches)]

    def cross_row_peers(self):
        return self.row_peers() + self.cross_peers()

    def seq_peers(self):
        return [self.along_seq(k)[1] for k in range(1, self.tokens)]

    def plane_peers(self):
        return [self.along_plane(k)[2] for k in range(1, 2 * self.batches)]


def meet(peers):
    barrier = pltpu.get_barrier_semaphore()
    for peer in peers:
        pl.semaphore_signal(barrier, inc=1, device_id=peer, device_id_type=MESH)
    pl.semaphore_wait(barrier, len(peers))


class Wires:
    def __init__(self, send_sems, recv_sems, local_sems):
        self.sems = (send_sems, recv_sems, local_sems)
        self.used = [0, 0]
        self.ends = []

    def send(self, src, dst, peer):
        k = self.used[0]
        self.used[0] += 1
        copy = pltpu.make_async_remote_copy(
            src_ref=src,
            dst_ref=dst,
            send_sem=self.sems[0].at[k],
            recv_sem=self.sems[1].at[k],
            device_id=peer,
            device_id_type=MESH,
        )
        copy.start()
        self.ends.append(copy.wait_send)
        return copy

    def local(self, src, dst):
        k = self.used[1]
        self.used[1] += 1
        copy = pltpu.make_async_copy(src, dst, self.sems[2].at[k])
        copy.start()
        return copy

    def finish(self):
        for end in self.ends:
            end()


def wire_scratch(sends, locals_count):
    return [
        pltpu.SemaphoreType.DMA((sends,)),
        pltpu.SemaphoreType.DMA((sends,)),
        pltpu.SemaphoreType.DMA((locals_count,)),
    ]


def comm_call(kernel, name, ident, out_shapes, inputs, sends, locals_count, scratch=(), spec=VMEM_SPEC):
    return pl.pallas_call(
        kernel,
        out_shape=tuple(out_shapes),
        in_specs=[spec] * len(inputs),
        out_specs=tuple([VMEM_SPEC] * len(out_shapes)),
        scratch_shapes=list(scratch) + wire_scratch(sends, locals_count),
        compiler_params=pltpu.CompilerParams(
            collective_id=ident, has_side_effects=True, vmem_limit_bytes=COMM_VMEM
        ),
        name=name,
    )(*inputs)


def like(array, *lead):
    return jax.ShapeDtypeStruct(tuple(lead) + tuple(array.shape), array.dtype)


def gather_kernel(
    x_ref, wq_ref, wk_ref, wv_ref, mix_ref, table_ref, vec_ref, up_ref, down_ref,
    xs_ref, qkvs_ref, mts_ref, vecs_ref, up2_ref, down2_ref, *sems,
):
    at = Place()
    wires = Wires(*sems)
    b, s, z, c = at.row, at.part, at.chip, at.core
    off_diagonal = b != z
    turned = (z, 2 * b + c)
    barrier = pltpu.get_barrier_semaphore()
    peers = at.chip_peers() + at.plane_peers()
    for peer in peers:
        pl.semaphore_signal(barrier, inc=1, device_id=peer, device_id_type=MESH)

    @pl.when(off_diagonal)
    def _():
        pl.semaphore_signal(barrier, inc=1, device_id=turned, device_id_type=MESH)

    pl.semaphore_wait(barrier, len(peers) + off_diagonal.astype(jnp.int32))

    swaps, stays = [], []
    for i, ref in enumerate((wq_ref, wk_ref, wv_ref)):
        k = wires.used[0]
        wires.used[0] += 1
        swaps.append(
            pltpu.make_async_remote_copy(
                src_ref=ref,
                dst_ref=qkvs_ref.at[2 * z + c, i],
                send_sem=sems[0].at[k],
                recv_sem=sems[1].at[k],
                device_id=turned,
                device_id_type=MESH,
            )
        )
        stays.append(pltpu.make_async_copy(ref, qkvs_ref.at[2 * b + c, i], sems[2].at[i]))
        wires.used[1] += 1

    @pl.when(off_diagonal)
    def _():
        for swap in swaps:
            swap.start()

    @pl.when(jnp.logical_not(off_diagonal))
    def _():
        for stay in stays:
            stay.start()

    rows = mix_ref.shape[0]
    table_rows = table_ref.shape[0]
    mix_home = mts_ref.at[c, b, z, pl.ds(0, rows)]
    table_home = mts_ref.at[c, b, z, pl.ds(rows, table_rows)]
    mt_sends = []
    for k in range(1, at.chips):
        peer = at.along_chips(k)[1]
        mt_sends.append(wires.send(mix_ref, mix_home, peer))
        mt_sends.append(wires.send(table_ref, table_home, peer))
    x_sends, vec_sends = [], []
    for k in range(1, at.chips):
        peer = at.along_chips(k)[1]
        x_sends.append(wires.send(x_ref, xs_ref.at[s], peer))
        vec_sends.append(wires.send(vec_ref, vecs_ref.at[s], peer))
    own = [
        wires.local(x_ref, xs_ref.at[s]),
        wires.local(mix_ref, mix_home),
        wires.local(table_ref, table_home),
        wires.local(vec_ref, vecs_ref.at[s]),
    ]
    last = [
        wires.send(x_ref, xs_ref.at[s], at.partner()),
        wires.send(vec_ref, vecs_ref.at[s], at.partner()),
        wires.send(up_ref, up2_ref, at.partner()),
        wires.send(down_ref, down2_ref, at.partner()),
    ]

    @pl.when(off_diagonal)
    def _():
        for swap in swaps:
            swap.wait_recv()

    @pl.when(jnp.logical_not(off_diagonal))
    def _():
        for stay in stays:
            stay.wait()

    for k in range(1, 2 * at.batches):
        peer = at.along_plane(k)[2]
        last.append(wires.send(qkvs_ref.at[2 * b + c], qkvs_ref.at[2 * b + c], peer))
    for copy in mt_sends:
        copy.wait_recv()
    for copy in own:
        copy.wait()
    row_sends = []
    for k in range(1, at.batches):
        peer = at.along_rows(k)[1]
        row_sends.append(wires.send(mts_ref.at[c, b], mts_ref.at[c, b], peer))
    last.append(wires.send(mts_ref.at[c, b], mts_ref.at[c, b], at.partner()))
    for k in range(1, at.batches):
        row = at.from_rows(k)
        row_sends[k - 1].wait_recv()
        last.append(wires.send(mts_ref.at[c, row], mts_ref.at[c, row], at.partner()))
    for k in range(1, at.chips):
        index = 2 * at.from_chips(k) + c
        x_sends[k - 1].wait_recv()
        last.append(wires.send(xs_ref.at[index], xs_ref.at[index], at.partner()))
        vec_sends[k - 1].wait_recv()
        last.append(wires.send(vecs_ref.at[index], vecs_ref.at[index], at.partner()))
    for copy in last:
        copy.wait_recv()
    wires.finish()

    @pl.when(off_diagonal)
    def _():
        for swap in swaps:
            swap.wait_send()


def gather_inputs(x, w_query, w_key, w_value, w_mix, rel_table, vec, up, down):
    tokens, batches = lax.axis_size("seq"), lax.axis_size("batch")
    chips = tokens // 2
    rows, columns = w_mix.shape
    outs = (
        like(x, tokens),
        like(w_query, tokens, 3),
        jax.ShapeDtypeStruct(
            (2, batches, chips, rows + rel_table.shape[0], columns), w_mix.dtype
        ),
        like(vec, tokens),
        like(up),
        like(down),
    )
    sends = 3 + 4 * (chips - 1) + 4 + 2 * batches - 1 + 2 * (batches - 1) + 1 + 2 * (chips - 1)
    inputs = (x, w_query, w_key, w_value, w_mix, rel_table, vec, up, down)
    return comm_call(gather_kernel, "gather_inputs", 0, outs, inputs, sends, 7, spec=ANY_SPEC)


def norm_parts(values):
    average = jnp.mean(values, axis=-1, keepdims=True)
    centered = values - average
    variance = jnp.mean(centered * centered, axis=-1, keepdims=True)
    scale = lax.rsqrt(variance + norm_eps)
    return centered * scale, scale


def norm_back(grad, gain, unit, scale):
    inner = grad * gain
    mean = jnp.mean(inner, axis=-1, keepdims=True)
    slope = jnp.mean(inner * unit, axis=-1, keepdims=True)
    return scale * (inner - mean - unit * slope)


def feed_kernel(
    ctx_ref, x_ref, mix_ref, vecs_ref, up_ref, down_ref, up2_ref, down2_ref, out_grad_ref,
    output_ref, pre_grad_ref, sums_ref, attn_ref, ups_ref, downs_ref, upbs_ref,
    got_ref, hid_ref, act_ref, slope_ref, part_ref, ffn_ref, grad_ref, inner_ref,
    back_ref, backs_ref, low_ref, upg_ref, downg_ref, upb_ref, vec_ref, *sems,
):
    at = Place()
    wires = Wires(*sems)
    low, wide = jnp.bfloat16, jnp.float32
    s, z, c = at.part, at.chip, at.core
    meet(at.seq_peers() + at.cross_row_peers())
    last, own = [], []
    swaps = []
    for k in range(1, at.tokens):
        part, peer = at.along_seq(k)
        swaps.append(wires.send(ctx_ref.at[part], got_ref.at[s], peer))
    kept = wires.local(ctx_ref.at[s], got_ref.at[s])
    lanes = x_ref.shape[1] // at.tokens
    hidden_here = up_ref.shape[1]
    vec_ref[...] = jnp.concatenate(
        [vecs_ref[part, :, :lanes].astype(wide) for part in range(at.tokens)], axis=1
    )
    bias3 = vec_ref[3:4]
    gain1, gain2 = vec_ref[4:5], vec_ref[5:6]
    shift1, shift2 = vec_ref[6:7], vec_ref[7:8]
    bias_down = vec_ref[8:9]
    partner = s + 1 - 2 * c
    up_rows = hidden_here // BLOCK
    bias_up = jnp.concatenate(
        [vecs_ref[s, 10 + i : 11 + i].astype(wide) for i in range(up_rows)]
        + [vecs_ref[partner, 10 + i : 11 + i].astype(wide) for i in range(up_rows)],
        axis=1,
    )
    for copy in swaps:
        copy.wait_recv()
    kept.wait()
    pieces = []
    for chip in range(at.chips):
        left, right = got_ref[2 * chip], got_ref[2 * chip + 1]
        middle = left[:, DH:].astype(wide) + right[:, :DH].astype(wide)
        pieces += [left[:, :DH], middle.astype(low), right[:, DH:]]
    context = jnp.concatenate(pieces, axis=1)
    pre_norm = x_ref[...].astype(wide) + dot_nn(context, mix_ref[...]) + bias3
    unit1, scale1 = norm_parts(pre_norm)
    hidden = unit1 * gain1 + shift1
    hid_ref[z] = hidden.astype(low)
    spread = [
        wires.send(hid_ref.at[z], hid_ref.at[z], at.along_chips(k)[1]) for k in range(1, at.chips)
    ]

    ffn_sends = []
    for k in range(at.chips):
        chip = at.from_chips(k)
        if k:
            spread[k - 1].wait_recv()
        rows = hid_ref[chip]
        inner = jnp.concatenate(
            [dot_nn(rows, up_ref[...]), dot_nn(rows, up2_ref[...])], axis=1
        )
        inner = inner + bias_up
        cdf = 0.5 * (1.0 + lax.erf(inner * math.sqrt(0.5)))
        act = (inner * cdf).astype(low)
        slope_ref[chip] = cdf + inner * (
            jnp.exp(-0.5 * inner * inner) * (1.0 / math.sqrt(2.0 * math.pi))
        )
        act_ref[chip] = act
        part_ref[chip] = (
            dot_nn(act[:, :hidden_here], down_ref[...])
            + dot_nn(act[:, hidden_here:], down2_ref[...])
        ).astype(low)
        if k:
            peer = (at.row, 2 * chip + c)
            ffn_sends.append(wires.send(part_ref.at[chip], ffn_ref.at[at.chips - 1 - k], peer))
    total = part_ref[z].astype(wide)
    for k in range(1, at.chips):
        ffn_sends[k - 1].wait_recv()
        total = total + ffn_ref[at.chips - 1 - k].astype(wide)
    mixed = hidden + total + bias_down
    unit2, scale2 = norm_parts(mixed)
    output_ref[...] = (unit2 * gain2 + shift2).astype(low)
    out_grad = out_grad_ref[...].astype(wide)
    mixed_grad = norm_back(out_grad, gain2, unit2, scale2)
    grad_ref[z] = mixed_grad.astype(low)
    spread = [
        wires.send(grad_ref.at[z], grad_ref.at[z], at.along_chips(k)[1])
        for k in range(1, at.chips)
    ]
    gain2_grad = jnp.sum(out_grad * unit2, axis=0, keepdims=True)
    shift2_grad = jnp.sum(out_grad, axis=0, keepdims=True)
    downb_grad = jnp.sum(mixed_grad, axis=0, keepdims=True)

    back_sends = []
    for k in range(at.chips):
        chip = at.from_chips(k)
        if k:
            spread[k - 1].wait_recv()
        rows = grad_ref[chip]
        act_grad = jnp.concatenate(
            [dot_nt(rows, down_ref[...]), dot_nt(rows, down2_ref[...])], axis=1
        )
        inner_low = (act_grad * slope_ref[chip]).astype(low)
        inner_ref[chip] = inner_low
        back_ref[chip] = (
            dot_nt(inner_low[:, :hidden_here], up_ref[...])
            + dot_nt(inner_low[:, hidden_here:], up2_ref[...])
        ).astype(low)
        if k:
            peer = (at.row, 2 * chip + c)
            back_sends.append(wires.send(back_ref.at[chip], backs_ref.at[at.chips - 1 - k], peer))

    width = x_ref.shape[1]
    columns = width // at.batches
    inner_all = inner_ref[...].reshape(at.chips * BLOCK, 2 * hidden_here)
    act_all = act_ref[...].reshape(at.chips * BLOCK, 2 * hidden_here)
    hid_all = hid_ref[...].reshape(at.chips * BLOCK, width)
    grad_all = grad_ref[...].reshape(at.chips * BLOCK, width)
    up_grad = dot_tn(hid_all, inner_all).astype(low)
    down_grad = dot_tn(act_all, grad_all).astype(low)
    upb_grad = jnp.sum(inner_all.astype(wide), axis=0, keepdims=True)
    for d in range(2):
        half = slice(d * hidden_here, (d + 1) * hidden_here)
        upb_ref[d] = jnp.broadcast_to(upb_grad[:, half], upb_ref.shape[1:])
        for row in range(at.batches):
            piece = slice(row * columns, (row + 1) * columns)
            upg_ref[d, row] = up_grad[piece, half]
            downg_ref[d, row] = down_grad[half, piece]
    mine = 2 * at.row + c
    for k in range(1, 2 * at.batches):
        row, core, peer = at.along_plane(k)
        other = lax.rem(core + c, 2)
        last.append(wires.send(upg_ref.at[other, row], ups_ref.at[mine], peer))
        last.append(wires.send(downg_ref.at[other, row], downs_ref.at[mine], peer))
        last.append(wires.send(upb_ref.at[other], upbs_ref.at[mine], peer))
    own.append(wires.local(upg_ref.at[0, at.row], ups_ref.at[mine]))
    own.append(wires.local(downg_ref.at[0, at.row], downs_ref.at[mine]))
    own.append(wires.local(upb_ref.at[0], upbs_ref.at[mine]))

    total = back_ref[z].astype(wide)
    for k in range(1, at.chips):
        back_sends[k - 1].wait_recv()
        total = total + backs_ref[at.chips - 1 - k].astype(wide)
    hidden_grad = mixed_grad + total
    pre_grad = norm_back(hidden_grad, gain1, unit1, scale1)
    low_ref[...] = pre_grad.astype(low)
    spread = [
        wires.send(low_ref, attn_ref.at[s], at.along_chips(k)[1]) for k in range(1, at.chips)
    ]
    last.append(wires.send(low_ref, attn_ref.at[s], at.partner()))
    own.append(wires.local(low_ref, attn_ref.at[s]))
    pre_grad_ref[...] = pre_grad
    gain1_grad = jnp.sum(hidden_grad * unit1, axis=0, keepdims=True)
    shift1_grad = jnp.sum(hidden_grad, axis=0, keepdims=True)
    bias3_grad = jnp.sum(pre_grad, axis=0, keepdims=True)
    sums = jnp.concatenate(
        [bias3_grad, gain1_grad, gain2_grad, shift1_grad, shift2_grad, downb_grad]
        + [jnp.zeros((2, width), wide)],
        axis=0,
    )
    spare = jnp.zeros((8, BLOCK - lanes), wide)
    for part in range(at.tokens):
        sums_ref[part] = jnp.concatenate(
            [sums[:, part * lanes : (part + 1) * lanes], spare], axis=1
        )
    for k in range(1, at.chips):
        index = 2 * at.from_chips(k) + c
        spread[k - 1].wait_recv()
        last.append(wires.send(attn_ref.at[index], attn_ref.at[index], at.partner()))
    for copy in last:
        copy.wait_recv()
    for copy in own:
        copy.wait()
    wires.finish()


def feed_forward(ctx, x, m_mix, vecs, up, down, up2, down2, out_grad, ident):
    tokens, batches = lax.axis_size("seq"), lax.axis_size("batch")
    chips = tokens // 2
    width = x.shape[1]
    columns = width // batches
    hidden_here = up.shape[1]
    low, wide = jnp.bfloat16, jnp.float32
    outs = (
        jax.ShapeDtypeStruct(x.shape, low),
        jax.ShapeDtypeStruct(x.shape, wide),
        jax.ShapeDtypeStruct((tokens, 8, BLOCK), wide),
        jax.ShapeDtypeStruct((tokens,) + x.shape, low),
        jax.ShapeDtypeStruct((2 * batches, columns, hidden_here), low),
        jax.ShapeDtypeStruct((2 * batches, hidden_here, columns), low),
        jax.ShapeDtypeStruct((2 * batches, 8, hidden_here), wide),
    )
    block = (chips,) + x.shape
    wide_block = (chips, x.shape[0], 2 * hidden_here)
    others = (chips - 1,) + x.shape
    scratch = (
        pltpu.VMEM(ctx.shape, low),
        pltpu.VMEM(block, low),
        pltpu.VMEM(wide_block, low),
        pltpu.VMEM(wide_block, wide),
        pltpu.VMEM(block, low),
        pltpu.VMEM(others, low),
        pltpu.VMEM(block, low),
        pltpu.VMEM(wide_block, low),
        pltpu.VMEM(block, low),
        pltpu.VMEM(others, low),
        pltpu.VMEM(x.shape, low),
        pltpu.VMEM((2, batches, columns, hidden_here), low),
        pltpu.VMEM((2, batches, hidden_here, columns), low),
        pltpu.VMEM((2, 8, hidden_here), wide),
        pltpu.VMEM((16, width), wide),
    )
    inputs = (ctx, x, m_mix, vecs, up, down, up2, down2, out_grad)
    sends = tokens - 1 + 4 * (chips - 1) + 3 * (2 * batches - 1) + 2 * (chips - 1) + 1
    return pl.pallas_call(
        feed_kernel,
        out_shape=outs,
        in_specs=[VMEM_SPEC] * len(inputs),
        out_specs=(VMEM_SPEC,) * len(outs),
        scratch_shapes=list(scratch) + wire_scratch(sends, 5),
        compiler_params=pltpu.CompilerParams(
            collective_id=ident, has_side_effects=True, vmem_limit_bytes=FEED_VMEM
        ),
        name="feed_forward",
    )(*inputs)


def settle_kernel(
    vec_ref, col_ref, dcat_ref, rel_ref, w_ref, xs_ref, table_ref, ctx_ref, attn_ref,
    ins_ref, vec_all_ref, cols_ref, dw_all_ref, tab_all_ref, mix_all_ref,
    in_ref, dw_ref, tab_ref, mix_ref, half_ref, sum_ref, vecs_ref, vec_low_ref, dws_ref, dw_low_ref, tabs_ref, tab_low_ref,
    mixs_ref, mix_low_ref, *sems,
):
    at = Place()
    wires = Wires(*sems)
    low, wide = jnp.bfloat16, jnp.float32
    b, s, z, c = at.row, at.part, at.chip, at.core
    off_diagonal = b != z
    same, cross = (z, 2 * b + c), (z, 2 * b + 1 - c)
    peers = at.seq_peers() + at.cross_row_peers()
    barrier = pltpu.get_barrier_semaphore()
    for peer in peers:
        pl.semaphore_signal(barrier, inc=1, device_id=peer, device_id_type=MESH)

    @pl.when(off_diagonal)
    def _():
        pl.semaphore_signal(barrier, inc=1, device_id=same, device_id_type=MESH)
        pl.semaphore_signal(barrier, inc=1, device_id=cross, device_id_type=MESH)

    pl.semaphore_wait(barrier, len(peers) + 2 * off_diagonal.astype(jnp.int32))

    dw_sends, tab_sends, mix_sends, vec_sends, last, own = [], [], [], [], [], []
    width = w_ref.shape[0]
    columns = width // at.batches
    full_len = dcat_ref.shape[0]
    group = 2 * DH

    def input_part(chip, core):
        start = pl.multiple_of((2 * chip + core) * BLOCK, BLOCK)
        in_ref[chip, core] = dot_nt(dcat_ref[pl.ds(start, BLOCK)], w_ref[...]).astype(low)

    halves = []
    for chip in range(at.chips):
        input_part(chip, 1 - c)
        halves.append(wires.send(in_ref.at[chip, 1 - c], half_ref.at[chip], at.partner()))
    for k in range(1, at.tokens):
        part, peer = at.along_seq(k)
        vec_sends.append(wires.send(vec_ref.at[part], vecs_ref.at[k - 1], peer))
    mine = 2 * b + c
    for k in range(1, 2 * at.batches):
        last.append(wires.send(col_ref, cols_ref.at[mine], at.along_plane(k)[2]))
    own.append(wires.local(col_ref, cols_ref.at[mine]))

    for chip in range(at.chips):
        input_part(chip, c)
        halves[chip].wait_recv()
        sum_ref[chip] = (in_ref[chip, c].astype(wide) + half_ref[chip].astype(wide)).astype(low)
    for k in range(1, at.chips):
        chip, peer = at.along_chips(k)
        last.append(wires.send(sum_ref.at[chip], ins_ref.at[z], peer))
    own.append(wires.local(sum_ref.at[z], ins_ref.at[z]))

    whole = xs_ref[...].reshape(full_len, width)
    dw = dot_tn(whole, dcat_ref[...])
    dw_rel = dot_tn(table_ref[...], rel_ref[...])
    dw = jnp.concatenate([dw[:, : 2 * group] + dw_rel, dw[:, 2 * group :]], axis=1)
    for row in range(at.batches):
        dw_ref[row] = dw[row * columns : (row + 1) * columns].astype(low)
    for k in range(1, at.batches):
        row, peer = at.along_rows(k)
        dw_sends.append(wires.send(dw_ref.at[row], dws_ref.at[k - 1], peer))
    for row in range(at.batches):
        rows = slice(row * columns, (row + 1) * columns)
        tab_ref[row] = dot_nt(rel_ref[...], w_ref[rows, : 2 * group]).astype(low)
    for k in range(1, at.batches):
        row, peer = at.along_rows(k)
        tab_sends.append(wires.send(tab_ref.at[row], tabs_ref.at[k - 1], peer))
    mix = dot_tn(
        ctx_ref[...].reshape(full_len, group), attn_ref[...].reshape(full_len, width)
    )
    for row in range(at.batches):
        mix_ref[row] = mix[:, row * columns : (row + 1) * columns].astype(low)
    for k in range(1, at.batches):
        row, peer = at.along_rows(k)
        mix_sends.append(wires.send(mix_ref.at[row], mixs_ref.at[k - 1], peer))

    total = dw_ref[b].astype(wide)
    for k in range(1, at.batches):
        dw_sends[k - 1].wait_recv()
        total = total + dws_ref[k - 1].astype(wide)
    shard_rows = dw_low_ref.shape[1]
    for half in range(2):
        dw_low_ref[half] = total[half * shard_rows : (half + 1) * shard_rows].astype(low)
    k = wires.used[0]
    wires.used[0] += 1
    move = pltpu.make_async_remote_copy(
        src_ref=dw_low_ref.at[c],
        dst_ref=dw_all_ref.at[c],
        send_sem=sems[0].at[k],
        recv_sem=sems[1].at[k],
        device_id=same,
        device_id_type=MESH,
    )
    stay = pltpu.make_async_copy(
        dw_low_ref.at[c], dw_all_ref.at[c], sems[2].at[wires.used[1]]
    )
    wires.used[1] += 1

    @pl.when(off_diagonal)
    def _():
        move.start()

    @pl.when(jnp.logical_not(off_diagonal))
    def _():
        stay.start()

    last.append(wires.send(dw_low_ref.at[1 - c], dw_all_ref.at[c], cross))

    total = tab_ref[b].astype(wide)
    for k in range(1, at.batches):
        tab_sends[k - 1].wait_recv()
        total = total + tabs_ref[k - 1].astype(wide)
    table_rows = tab_low_ref.shape[1]
    for part in range(at.tokens):
        tab_low_ref[part] = total[part * table_rows : (part + 1) * table_rows].astype(low)
    for k in range(1, at.tokens):
        part, peer = at.along_seq(k)
        last.append(wires.send(tab_low_ref.at[part], tab_all_ref.at[s], peer))
    own.append(wires.local(tab_low_ref.at[s], tab_all_ref.at[s]))

    total = mix_ref[b].astype(wide)
    for k in range(1, at.batches):
        mix_sends[k - 1].wait_recv()
        total = total + mixs_ref[k - 1].astype(wide)
    mix_low_ref[...] = total.astype(low)
    last.append(wires.send(mix_low_ref, mix_all_ref.at[c], at.partner()))
    own.append(wires.local(mix_low_ref, mix_all_ref.at[c]))

    total = vec_ref[s]
    for k in range(1, at.tokens):
        vec_sends[k - 1].wait_recv()
        total = total + vecs_ref[k - 1]
    vec_low_ref[...] = total
    for k in range(1, at.batches):
        last.append(wires.send(vec_low_ref, vec_all_ref.at[b], at.along_rows(k)[1]))
    own.append(wires.local(vec_low_ref, vec_all_ref.at[b]))

    for copy in last:
        copy.wait_recv()
    for copy in own:
        copy.wait()
    wires.finish()

    @pl.when(off_diagonal)
    def _():
        move.wait()

    @pl.when(jnp.logical_not(off_diagonal))
    def _():
        stay.wait()


def settle_grads(vec, cols, dcat, rel, w_cat, xs, table, ctx, attn_all, ident):
    tokens, batches = lax.axis_size("seq"), lax.axis_size("batch")
    chips = tokens // 2
    low, wide = jnp.bfloat16, jnp.float32
    local_len, width = xs.shape[1:]
    columns, group = width // batches, dcat.shape[1]
    buckets = table.shape[0]
    half = (chips, local_len, width)
    dw_pieces = (2, columns // 2, group)
    tab_pieces = (tokens, buckets // tokens, columns)
    mix_piece = (2 * DH, columns)
    dw_piece, tab_piece = (columns, group), (buckets, columns)
    outs = (
        jax.ShapeDtypeStruct(half, low),
        jax.ShapeDtypeStruct((batches,) + vec.shape[1:], wide),
        like(cols, 2 * batches),
        jax.ShapeDtypeStruct(dw_pieces, low),
        jax.ShapeDtypeStruct(tab_pieces, low),
        jax.ShapeDtypeStruct((2,) + mix_piece, low),
    )
    scratch = (
        pltpu.VMEM((chips, 2, local_len, width), low),
        pltpu.VMEM((batches,) + dw_piece, low),
        pltpu.VMEM((batches,) + tab_piece, low),
        pltpu.VMEM((batches,) + mix_piece, low),
        pltpu.VMEM(half, low),
        pltpu.VMEM(half, low),
        pltpu.VMEM((tokens - 1,) + vec.shape[1:], wide),
        pltpu.VMEM(vec.shape[1:], wide),
        pltpu.VMEM((batches - 1,) + dw_piece, low),
        pltpu.VMEM(dw_pieces, low),
        pltpu.VMEM((batches - 1,) + tab_piece, low),
        pltpu.VMEM(tab_pieces, low),
        pltpu.VMEM((batches - 1,) + mix_piece, low),
        pltpu.VMEM(mix_piece, low),
    )
    sends = (
        3 * (batches - 1) + chips + tokens - 1 + 2 * batches - 1
        + 2 + chips - 1 + tokens - 1 + 1 + batches - 1
    )
    inputs = (vec, cols, dcat, rel, w_cat, xs, table, ctx, attn_all)
    return comm_call(settle_kernel, "settle_grads", ident, outs, inputs, sends, 6, scratch=scratch)


def finish_kernel(
    pre_ref, ins_ref, vecs_ref, cols_ref, dws_ref, tabs_ref, mixs_ref, ups_ref, downs_ref,
    upbs_ref,
    input_ref, dq_ref, dk_ref, dv_ref, mix_ref, table_ref, bias_ref, gain_ref, shift_ref,
    up_ref, upb_ref, down_ref, downb_ref,
):
    at = Place()
    wide = jnp.float32

    def total(ref):
        out = ref[0].astype(wide)
        for k in range(1, ref.shape[0]):
            out = out + ref[k].astype(wide)
        return out

    input_ref[...] = pre_ref[...] + total(ins_ref)
    up_ref[...] = total(ups_ref)
    down_ref[...] = total(downs_ref)
    upb_ref[...] = total(upbs_ref)[0:1]
    table_ref[...] = total(tabs_ref)
    group = 2 * DH
    spare = jnp.zeros((dws_ref.shape[1], DH), wide)
    for i, ref in enumerate((dq_ref, dk_ref, dv_ref)):
        lower = dws_ref[0, :, i * group : (i + 1) * group].astype(wide)
        upper = dws_ref[1, :, i * group : (i + 1) * group].astype(wide)
        ref[...] = jnp.concatenate([lower, spare], axis=1) + jnp.concatenate(
            [spare, upper], axis=1
        )
    rows = mix_ref.shape[0]
    lower, upper = mixs_ref[0].astype(wide), mixs_ref[1].astype(wide)
    spare = jnp.zeros((DH, lower.shape[1]), wide)
    whole = jnp.concatenate([lower, spare], axis=0) + jnp.concatenate([spare, upper], axis=0)
    mix_ref[...] = jnp.where(at.core == 0, whole[:rows], whole[rows:])
    small = total(vecs_ref)
    lanes = bias_ref.shape[1]
    cols = [cols_ref[core, 0:1] for core in range(2)]
    for row in range(1, at.batches):
        cols = [cols[core] + cols_ref[2 * row + core, 0:1] for core in range(2)]
    spare = jnp.zeros((1, DH), wide)
    biases = []
    for i in range(3):
        lower, upper = [part[:, i * group : (i + 1) * group] for part in cols]
        both = jnp.concatenate([lower, spare], axis=1) + jnp.concatenate([spare, upper], axis=1)
        biases.append(jnp.where(at.core == 0, both[:, :lanes], both[:, lanes:]))
    bias_ref[...] = jnp.concatenate(biases + [small[0:1, :lanes]], axis=0)
    gain_ref[...] = small[1:3, :lanes]
    shift_ref[...] = small[3:5, :lanes]
    downb_ref[...] = small[5:6, :lanes]


def finish(pre_grad, parts, shapes):
    inputs = (pre_grad,) + tuple(parts)
    return pl.pallas_call(
        finish_kernel,
        out_shape=tuple(jax.ShapeDtypeStruct(shape, jnp.float32) for shape in shapes),
        in_specs=[VMEM_SPEC] * len(inputs),
        out_specs=(VMEM_SPEC,) * len(shapes),
        compiler_params=pltpu.CompilerParams(vmem_limit_bytes=COMM_VMEM),
        name="finish",
    )(*inputs)


def fits_fast(layer_input, table_shard, hidden_here):
    rows, local_len, width = layer_input.shape
    tokens, batches = lax.axis_size("seq"), lax.axis_size("batch")
    return (
        rows == 1
        and local_len == BLOCK
        and tokens == 2 * batches
        and width == 3 * DH * batches
        and (table_shard.shape[0] * tokens) % (4 * BLOCK) == 0
        and tokens % 4 == 0
        and 10 + hidden_here // BLOCK <= 16
        and hidden_here % BLOCK == 0
    )


def fast_body(
    layer_input, segment_ids, w_query, w_key, w_value, w_mix, rel_table, attn_biases,
    norm_gains, norm_shifts, w_up, up_bias, w_down, down_bias, out_grad,
):
    local_len, width = layer_input.shape[1:]
    low = jnp.bfloat16
    shard_rows, shard_cols = w_query.shape
    lanes = attn_biases.shape[1]
    hidden_here = w_up.shape[1]
    x = layer_input[0]
    pack = jnp.concatenate([attn_biases, norm_gains, norm_shifts, down_bias[None]], axis=0)
    pack = jnp.pad(pack, ((0, 0), (0, BLOCK - lanes)))
    pack = jnp.concatenate(
        [pack, segment_ids.astype(low), up_bias.reshape(hidden_here // BLOCK, BLOCK)], axis=0
    )
    pack = jnp.pad(pack, ((0, 16 - pack.shape[0]), (0, 0)))
    xs, qkvs, mts, vecs, up2, down2 = gather_inputs(
        x, w_query, w_key, w_value, w_mix, rel_table, pack, w_up, w_down
    )
    q, k, v, qrev, krev, probs, ctx, w_cat, m_mix, table = attend(xs, qkvs, mts, vecs)
    output, pre_grad, sums, attn_all, ups, downs, upbs = feed_forward(
        ctx, x, m_mix, vecs, w_up, w_down, up2, down2, out_grad[0], 1
    )
    dcat, rel_grad, cols = attend_back(q, k, v, qrev, krev, probs, m_mix, attn_all)
    ins, vec_all, cols_all, dw_all, tab_all, mix_all = settle_grads(
        sums, cols, dcat, rel_grad, w_cat, xs, table, ctx, attn_all, 2
    )
    shard = (shard_rows, shard_cols)
    shapes = (
        x.shape, shard, shard, shard, shard, rel_table.shape, (4, lanes), (2, lanes), (2, lanes),
        (width // lax.axis_size("batch"), hidden_here), (1, hidden_here),
        (hidden_here, width // lax.axis_size("batch")), (1, lanes),
    )
    grads = finish(
        pre_grad,
        (ins, vec_all, cols_all, dw_all, tab_all, mix_all, ups, downs, upbs),
        shapes,
    )
    input_grad, dq, dk, dv, dmix, dtable, dbias, dgain, dshift, dup, dupb, ddown, ddownb = grads
    return (
        output[None], input_grad[None], dq, dk, dv, dmix, dtable, dbias, dgain, dshift,
        dup, dupb[0], ddown, ddownb[0],
    )


def body(
    layer_input,
    segment_ids,
    w_query,
    w_key,
    w_value,
    w_mix,
    rel_table,
    attn_biases,
    norm_gains,
    norm_shifts,
    w_up,
    up_bias,
    w_down,
    down_bias,
    out_grad,
):
    if fits_fast(layer_input, rel_table, w_up.shape[1]):
        return fast_body(
            layer_input, segment_ids, w_query, w_key, w_value, w_mix, rel_table, attn_biases,
            norm_gains, norm_shifts, w_up, up_bias, w_down, down_bias, out_grad,
        )
    rows, local_len, width = layer_input.shape
    full_len = local_len * lax.axis_size("seq")
    tokens_here = local_len * rows
    highest_prec = lax.Precision.HIGHEST
    parts = (
        lax.all_gather(w_query, "batch", axis=1, tiled=True),
        lax.all_gather(w_key, "batch", axis=1, tiled=True),
        lax.all_gather(w_value, "batch", axis=1, tiled=True),
        lax.all_gather(w_mix, "batch", axis=1, tiled=True),
        lax.all_gather(rel_table, "batch", axis=1, tiled=True),
    )
    whole = (
        lax.all_gather(parts[0], "seq", axis=0, tiled=True),
        lax.all_gather(parts[1], "seq", axis=0, tiled=True),
        lax.all_gather(parts[2], "seq", axis=0, tiled=True),
        lax.all_gather(parts[3], "seq", axis=0, tiled=True),
        lax.all_gather(parts[4], "seq", axis=0, tiled=True),
        lax.all_gather(attn_biases, "seq", axis=1, tiled=True),
        lax.all_gather(norm_gains, "seq", axis=1, tiled=True),
        lax.all_gather(norm_shifts, "seq", axis=1, tiled=True),
        lax.all_gather(down_bias, "seq", axis=0, tiled=True),
    )
    m_query, m_key, m_value, m_mix, table, biases, gains, shifts, bias_down = whole
    flat_input = jnp.swapaxes(layer_input, 0, 1).reshape(tokens_here, width)
    queries = (jnp.dot(flat_input, m_query, preferred_element_type=jnp.float32) + biases[0]).astype(
        jnp.bfloat16
    )
    keys_here = (jnp.dot(flat_input, m_key, preferred_element_type=jnp.float32) + biases[1]).astype(
        jnp.bfloat16
    )
    values_here = (
        jnp.dot(flat_input, m_value, preferred_element_type=jnp.float32) + biases[2]
    ).astype(jnp.bfloat16)
    query_rel = (jnp.dot(table, m_query, preferred_element_type=jnp.float32) + biases[0]).astype(
        jnp.bfloat16
    )
    key_rel = (jnp.dot(table, m_key, preferred_element_type=jnp.float32) + biases[1]).astype(
        jnp.bfloat16
    )
    local_seg = jnp.swapaxes(segment_ids, 0, 1).astype(jnp.bfloat16)
    keys_all, values_all, seg_all = (
        lax.all_gather(keys_here.reshape(local_len, rows, width), "seq", axis=0, tiled=True),
        lax.all_gather(values_here.reshape(local_len, rows, width), "seq", axis=0, tiled=True),
        lax.all_gather(local_seg, "seq", axis=0, tiled=True),
    )
    buckets = table.shape[0]
    offset = lax.axis_index("seq") * local_len
    bucket_iota = jnp.arange(buckets, dtype=jnp.int32)
    inner_cols = (bucket_iota > 0) & (bucket_iota < buckets - 1)
    same_doc = (
        jnp.swapaxes(local_seg, 0, 1)[:, None, :, None]
        == jnp.swapaxes(seg_all, 0, 1)[:, None, None, :]
    )
    score_scale = 1.0 / math.sqrt(3.0 * DH)
    head_queries = split_heads(queries.reshape(local_len, rows, width))
    head_keys = split_heads(keys_all)
    head_values = split_heads(values_all)
    rel_queries = split_table(query_rel)
    rel_keys = split_table(key_rel)

    def forward_group(carry, group):
        g_query, g_key, g_value, g_qrel, g_krel = group
        total, near_pull, far_pull, window = relative_scores(
            g_query, g_key, g_krel, g_qrel, offset, full_len
        )
        scores = jnp.where(same_doc, total * score_scale, masked_score)
        highest = jnp.max(scores, axis=-1, keepdims=True)
        exponent = jnp.exp(scores - highest)
        denominator = jnp.sum(exponent, axis=-1, keepdims=True)
        weights_low = (exponent / denominator).astype(jnp.bfloat16)
        context = jnp.einsum(
            "rgij,rgjd->rgid", weights_low, g_value, preferred_element_type=jnp.float32
        )
        return (carry, (context, (highest + jnp.log(denominator))[..., 0]))

    unused, (context_groups, log_totals) = lax.scan(
        forward_group, None, (head_queries, head_keys, head_values, rel_queries, rel_keys)
    )
    context_low = join_heads(context_groups).reshape(tokens_here, width).astype(jnp.bfloat16)
    pre_norm = (
        flat_input.astype(jnp.float32)
        + jnp.dot(context_low, m_mix, preferred_element_type=jnp.float32)
        + biases[3]
    )
    hidden, norm1_pull = jax.vjp(
        normalize, pre_norm, gains[0].astype(jnp.float32), shifts[0].astype(jnp.float32)
    )
    hidden_low = hidden.astype(jnp.bfloat16)

    def spread_rows(rows_low):
        return lax.all_gather(rows_low, "seq", axis=0, tiled=True)

    def hidden_sums(make_term):
        return lax.psum_scatter(
            make_term(jnp.int32(0), tokens_here * lax.axis_size("seq")),
            "seq",
            scatter_dimension=0,
            tiled=True,
        )

    hidden_rows = spread_rows(hidden_low)
    inner = jnp.dot(hidden_rows, w_up, preferred_element_type=jnp.float32) + up_bias
    act, gelu_pull = jax.vjp(exact_gelu, inner)
    act_low = act.astype(jnp.bfloat16)

    def down_rows(start, count):
        return jnp.dot(act_low, w_down, preferred_element_type=jnp.float32)

    ffn_result = hidden_sums(down_rows)
    mixed = hidden + ffn_result + bias_down
    output, norm2_pull = jax.vjp(
        normalize, mixed, gains[1].astype(jnp.float32), shifts[1].astype(jnp.float32)
    )
    flat_grad = jnp.swapaxes(out_grad, 0, 1).reshape(tokens_here, width).astype(jnp.float32)
    mixed_grad, gain2_grad, shift2_grad = norm2_pull(flat_grad)
    ffn_grad_low = mixed_grad.astype(jnp.bfloat16)
    grad_rows = spread_rows(ffn_grad_low)
    act_grad = jnp.einsum("nd,fd->nf", grad_rows, w_down, preferred_element_type=jnp.float32)
    inner_low = gelu_pull(act_grad)[0].astype(jnp.bfloat16)
    up_part = jnp.einsum("nd,nf->df", hidden_rows, inner_low, preferred_element_type=jnp.float32)
    upb_part = jnp.sum(inner_low.astype(jnp.float32), axis=0)
    down_part = jnp.einsum("nf,nd->fd", act_low, grad_rows, preferred_element_type=jnp.float32)

    def back_rows(start, count):
        return jnp.einsum("nf,df->nd", inner_low, w_up, preferred_element_type=jnp.float32)

    hidden_grad = mixed_grad + hidden_sums(back_rows)
    pre_grad, gain1_grad, shift1_grad = norm1_pull(hidden_grad)
    attn_low = pre_grad.astype(jnp.bfloat16)
    mix_whole = jnp.einsum("nd,ne->de", context_low, attn_low, preferred_element_type=jnp.float32)
    context_grad = jnp.einsum(
        "ne,de->nd", attn_low, m_mix, preferred_element_type=jnp.float32
    ).astype(jnp.bfloat16)
    head_context_grad = split_heads(context_grad.reshape(local_len, rows, width))

    def query_side(group):
        g_query, g_key, g_value, g_qrel, g_krel, g_dctx, g_lse = group
        total, near_pull, far_pull, window = relative_scores(
            g_query, g_key, g_krel, g_qrel, offset, full_len
        )
        scores = jnp.where(same_doc, total * score_scale, masked_score)
        weights_now = jnp.exp(scores - g_lse[..., None])
        prob_grad = jnp.einsum(
            "rgid,rgjd->rgij", g_dctx, g_value, preferred_element_type=jnp.float32
        )
        inner_sum = jnp.sum(weights_now * prob_grad, axis=-1)
        score_grad = (weights_now * (prob_grad - inner_sum[..., None])).astype(jnp.bfloat16)
        grad_wide = score_grad.astype(jnp.float32)
        near_grad = near_pull(grad_wide)[0]
        near_low = jnp.where(inner_cols, near_grad, 0.0).astype(jnp.bfloat16)
        near_ends = end_columns(near_grad)
        query_part = jnp.einsum(
            "rgij,rgjd->rgid", score_grad, g_key, preferred_element_type=jnp.float32
        )
        query_part = (
            query_part
            + jnp.einsum("rgib,gbd->rgid", near_low, g_krel, preferred_element_type=jnp.float32)
            + end_terms(near_ends, g_krel)
        )
        krel_part = with_ends(
            jnp.einsum("rgib,rgid->gbd", near_low, g_query, preferred_element_type=jnp.float32),
            end_rows(near_ends, g_query),
        )
        return (
            weights_now,
            score_grad,
            grad_wide,
            far_pull,
            window,
            inner_sum,
            query_part * score_scale,
            krel_part * score_scale,
        )

    query_groups = (
        head_queries,
        head_keys,
        head_values,
        rel_queries,
        rel_keys,
        head_context_grad,
        log_totals,
    )

    def all_grads(carry, group):
        weights_now, score_grad, grad_wide, far_pull, window, inner_sum, query_part, krel_part = (
            query_side(group)
        )
        g_query, g_key, g_value, g_qrel, g_krel, g_dctx, g_lse = group
        cross_grad, end_grad = far_pull(grad_wide)
        cross_low = cross_grad.astype(jnp.bfloat16)
        key_part = jnp.einsum(
            "rgij,rgid->rgjd", score_grad, g_query, preferred_element_type=jnp.float32
        )
        band_part = jnp.einsum(
            "rgmb,gbd->rgmd", cross_low, g_qrel, preferred_element_type=jnp.float32
        )
        key_part = (
            key_part
            + unband(band_part, offset, full_len, buckets // 2)
            + end_terms(end_grad, g_qrel)
        )
        value_part = jnp.einsum(
            "rgij,rgid->rgjd",
            weights_now.astype(jnp.bfloat16),
            g_dctx,
            preferred_element_type=jnp.float32,
        )
        qrel_part = with_ends(
            jnp.einsum("rgmb,rgmd->gbd", cross_low, window, preferred_element_type=jnp.float32),
            end_rows(end_grad, g_key),
        )
        return (
            carry,
            (query_part, key_part * score_scale, value_part, qrel_part * score_scale, krel_part),
        )

    unused, (dq_groups, dk_groups, dv_groups, dqrel_groups, dkrel_groups) = lax.scan(
        all_grads, None, query_groups
    )
    key_sum, value_sum = (
        lax.psum_scatter(join_heads(dk_groups), "seq", scatter_dimension=0, tiled=True),
        lax.psum_scatter(join_heads(dv_groups), "seq", scatter_dimension=0, tiled=True),
    )
    key_grads = key_sum.reshape(tokens_here, width).astype(jnp.bfloat16)
    value_grads = value_sum.reshape(tokens_here, width).astype(jnp.bfloat16)
    query_grads = join_heads(dq_groups).reshape(tokens_here, width).astype(jnp.bfloat16)
    qrel_grad = join_table(dqrel_groups)
    krel_grad = join_table(dkrel_groups)
    input_grad = pre_grad + jnp.einsum(
        "ne,de->nd", query_grads, m_query, preferred_element_type=jnp.float32
    )
    input_grad = input_grad + jnp.einsum(
        "ne,de->nd", key_grads, m_key, preferred_element_type=jnp.float32
    )
    input_grad = input_grad + jnp.einsum(
        "ne,de->nd", value_grads, m_value, preferred_element_type=jnp.float32
    )
    query_whole = jnp.einsum(
        "nd,ne->de", flat_input, query_grads, preferred_element_type=jnp.float32
    ) + jnp.einsum(
        "bd,be->de", table, qrel_grad, precision=highest_prec, preferred_element_type=jnp.float32
    )
    key_whole = jnp.einsum(
        "nd,ne->de", flat_input, key_grads, preferred_element_type=jnp.float32
    ) + jnp.einsum(
        "bd,be->de", table, krel_grad, precision=highest_prec, preferred_element_type=jnp.float32
    )
    value_whole = jnp.einsum(
        "nd,ne->de", flat_input, value_grads, preferred_element_type=jnp.float32
    )
    table_whole = jnp.einsum(
        "be,de->bd", qrel_grad, m_query, precision=highest_prec, preferred_element_type=jnp.float32
    ) + jnp.einsum(
        "be,de->bd", krel_grad, m_key, precision=highest_prec, preferred_element_type=jnp.float32
    )
    bias_whole = jnp.stack(
        [
            jnp.sum(query_grads.astype(jnp.float32), axis=0) + jnp.sum(qrel_grad, axis=0),
            jnp.sum(key_grads.astype(jnp.float32), axis=0) + jnp.sum(krel_grad, axis=0),
            jnp.sum(value_grads.astype(jnp.float32), axis=0),
            jnp.sum(pre_grad, axis=0),
        ]
    )
    gain_whole = jnp.stack([gain1_grad, gain2_grad])
    shift_whole = jnp.stack([shift1_grad, shift2_grad])
    downb_whole = jnp.sum(mixed_grad, axis=0)
    seq_parts = (
        lax.psum_scatter(query_whole, "seq", scatter_dimension=0, tiled=True),
        lax.psum_scatter(key_whole, "seq", scatter_dimension=0, tiled=True),
        lax.psum_scatter(value_whole, "seq", scatter_dimension=0, tiled=True),
        lax.psum_scatter(mix_whole, "seq", scatter_dimension=0, tiled=True),
        lax.psum_scatter(table_whole, "seq", scatter_dimension=0, tiled=True),
        lax.psum_scatter(bias_whole, "seq", scatter_dimension=1, tiled=True),
        lax.psum_scatter(gain_whole, "seq", scatter_dimension=1, tiled=True),
        lax.psum_scatter(shift_whole, "seq", scatter_dimension=1, tiled=True),
        lax.psum_scatter(downb_whole, "seq", scatter_dimension=0, tiled=True),
    )
    batch_parts = (
        lax.psum_scatter(seq_parts[0], "batch", scatter_dimension=1, tiled=True),
        lax.psum_scatter(seq_parts[1], "batch", scatter_dimension=1, tiled=True),
        lax.psum_scatter(seq_parts[2], "batch", scatter_dimension=1, tiled=True),
        lax.psum_scatter(seq_parts[3], "batch", scatter_dimension=1, tiled=True),
        lax.psum_scatter(seq_parts[4], "batch", scatter_dimension=1, tiled=True),
        lax.psum_scatter(up_part, "batch", scatter_dimension=0, tiled=True),
        lax.psum_scatter(down_part, "batch", scatter_dimension=1, tiled=True),
    )
    small_parts = lax.psum(
        (seq_parts[5], seq_parts[6], seq_parts[7], seq_parts[8], upb_part), "batch"
    )
    layer_output = jnp.swapaxes(output.reshape(local_len, rows, width), 0, 1).astype(jnp.bfloat16)
    input_back = jnp.swapaxes(input_grad.reshape(local_len, rows, width), 0, 1)
    return (
        layer_output,
        input_back,
        batch_parts[0],
        batch_parts[1],
        batch_parts[2],
        batch_parts[3],
        batch_parts[4],
        small_parts[0],
        small_parts[1],
        small_parts[2],
        batch_parts[5],
        small_parts[4],
        batch_parts[6],
        small_parts[3],
    )


def solution(mesh):
    return jax.shard_map(
        body,
        mesh=mesh,
        in_specs=(
            P("batch", "seq", None),
            P("batch", "seq"),
            P("seq", "batch"),
            P("seq", "batch"),
            P("seq", "batch"),
            P("seq", "batch"),
            P("seq", "batch"),
            P(None, "seq"),
            P(None, "seq"),
            P(None, "seq"),
            P(None, "seq"),
            P("seq"),
            P("seq", None),
            P("seq"),
            P("batch", "seq", None),
        ),
        out_specs=(
            P("batch", "seq", None),
            P("batch", "seq", None),
            P("seq", "batch"),
            P("seq", "batch"),
            P("seq", "batch"),
            P("seq", "batch"),
            P("seq", "batch"),
            P(None, "seq"),
            P(None, "seq"),
            P(None, "seq"),
            P("batch", "seq"),
            P("seq"),
            P("seq", "batch"),
            P("seq"),
        ),
        check_vma=False,
    )
```

```python
import math

import jax
import jax.numpy as jnp
from jax import lax
from jax.experimental import pallas as pl
from jax.experimental.pallas import tpu as pltpu
from jax.sharding import PartitionSpec as P

DH = 64


masked_score = -1e30
norm_eps = 1e-06
pair_heads = 2


def normalize(values, gain, shift):
    average = jnp.mean(values, axis=-1, keepdims=True)
    centered = values - average
    variance = jnp.mean(centered * centered, axis=-1, keepdims=True)
    return centered * lax.rsqrt(variance + norm_eps) * gain + shift


def exact_gelu(values):
    return jax.nn.gelu(values, approximate=False)


def split_heads(matrix):
    length, rows, width = matrix.shape
    groups = width // (pair_heads * DH)
    return matrix.reshape(length, rows, groups, pair_heads, DH).transpose(2, 1, 3, 0, 4)


def join_heads(matrix):
    groups, rows, pair, length, depth = matrix.shape
    return matrix.transpose(3, 1, 0, 2, 4).reshape(length, rows, groups * pair * depth)


def split_table(matrix):
    buckets, width = matrix.shape
    return matrix.reshape(buckets, width // (pair_heads * DH), pair_heads, DH).transpose(1, 2, 0, 3)


def join_table(matrix):
    groups, pair, buckets, depth = matrix.shape
    return matrix.transpose(2, 0, 1, 3).reshape(buckets, groups * pair * depth)


def table_ends(table):
    return jnp.stack([table[:, 0], table[:, -1]], axis=1)


def near_skew(table_prod, offset, full_len):
    lead = table_prod.shape[:-2]
    count, buckets = table_prod.shape[-2:]
    span = buckets // 2
    lead_pad = [(0, 0)] * len(lead)
    flipped = jnp.pad(table_prod[..., ::-1], lead_pad + [(0, 0), (0, count)])
    sheared = flipped.reshape(lead + (count * (buckets + count),))[
        ..., : count * (buckets + count - 1)
    ]
    sheared = sheared.reshape(lead + (count, buckets + count - 1))
    spread = jnp.pad(sheared, lead_pad + [(0, 0), (full_len, full_len)])
    band = lax.dynamic_slice_in_dim(
        spread, full_len + span - 1 - offset, full_len, axis=len(lead) + 1
    )
    distance = (offset + jnp.arange(count, dtype=jnp.int32))[:, None] - jnp.arange(
        full_len, dtype=jnp.int32
    )[None, :]
    return jnp.where(
        distance <= -span,
        table_prod[..., 0:1],
        jnp.where(distance >= span - 1, table_prod[..., buckets - 1 :], band),
    )


def far_place(cross, end_vals, offset, count, full_len):
    lead = cross.shape[:-2]
    band_len, buckets = cross.shape[-2:]
    span = buckets // 2
    lead_pad = [(0, 0)] * len(lead)
    turned = jnp.swapaxes(cross, -1, -2).reshape(lead + (buckets * band_len,))
    turned = jnp.pad(turned, lead_pad + [(0, buckets)])
    diagonal = turned.reshape(lead + (buckets, band_len + 1))[..., :count]
    aligned = jnp.pad(jnp.swapaxes(diagonal, -1, -2), lead_pad + [(0, 0), (0, count)])
    sheared = aligned.reshape(lead + (count * (buckets + count),))[
        ..., : count * (buckets + count - 1)
    ]
    sheared = sheared.reshape(lead + (count, buckets + count - 1))
    spread = jnp.pad(sheared, lead_pad + [(0, 0), (full_len, full_len)])
    band = lax.dynamic_slice_in_dim(spread, full_len + span - offset, full_len, axis=len(lead) + 1)
    distance = (
        jnp.arange(full_len, dtype=jnp.int32)[None, :]
        - (offset + jnp.arange(count, dtype=jnp.int32))[:, None]
    )
    return jnp.where(
        distance <= -span,
        end_vals[..., 0:1, :],
        jnp.where(distance >= span - 1, end_vals[..., 1:2, :], band),
    )


def band_rows(all_rows, offset, count, span):
    padded = jnp.pad(all_rows, [(0, 0), (0, 0), (span, span), (0, 0)])
    return lax.dynamic_slice_in_dim(padded, offset, count + 2 * span - 1, axis=2)


def unband(values, offset, full_len, span):
    lead = values.shape[:2]
    room = jnp.zeros(lead + (full_len + 2 * span, values.shape[3]), jnp.float32)
    placed = lax.dynamic_update_slice_in_dim(room, values, offset, axis=2)
    return placed[:, :, span : span + full_len]


def relative_scores(own_rows, all_rows, own_table, all_table, offset, full_len):
    count = own_rows.shape[2]
    content = jnp.einsum("rgid,rgjd->rgij", own_rows, all_rows, preferred_element_type=jnp.float32)
    own_prod = jnp.einsum("rgid,gbd->rgib", own_rows, own_table, preferred_element_type=jnp.float32)
    window = band_rows(all_rows, offset, count, all_table.shape[1] // 2)
    cross = jnp.einsum("rgmd,gbd->rgmb", window, all_table, preferred_element_type=jnp.float32)
    end_vals = jnp.einsum(
        "rgjd,ged->rgej", all_rows, table_ends(all_table), preferred_element_type=jnp.float32
    )
    near_vals, near_pull = jax.vjp(lambda product: near_skew(product, offset, full_len), own_prod)
    far_vals, far_pull = jax.vjp(
        lambda part, ends: far_place(part, ends, offset, count, full_len), cross, end_vals
    )
    return (content + near_vals + far_vals, near_pull, far_pull, window)


def end_columns(grad):
    return jnp.stack([grad[..., 0], grad[..., -1]], axis=2)


def end_terms(ends, table):
    return jnp.einsum(
        "rgei,ged->rgid",
        ends,
        table_ends(table),
        precision=lax.Precision.HIGHEST,
        preferred_element_type=jnp.float32,
    )


def end_rows(ends, rows_low):
    return jnp.einsum(
        "rgei,rgid->ged",
        ends,
        rows_low,
        precision=lax.Precision.HIGHEST,
        preferred_element_type=jnp.float32,
    )


def with_ends(inner_part, edge_rows):
    buckets = inner_part.shape[1]
    place = jnp.arange(buckets, dtype=jnp.int32)[None, :, None]
    return (
        inner_part
        + jnp.where(place == 0, edge_rows[:, 0:1], 0.0)
        + jnp.where(place == buckets - 1, edge_rows[:, 1:2], 0.0)
    )


BLOCK = 128
MIB = 1024 * 1024
ATTEND_VMEM = 26 * MIB
BACK_VMEM = 26 * MIB
FEED_VMEM = 26 * MIB
COMM_VMEM = 16 * MIB


def dot_nn(a, b):
    return lax.dot_general(a, b, (((1,), (0,)), ((), ())), preferred_element_type=jnp.float32)


def dot_nt(a, b):
    return lax.dot_general(a, b, (((1,), (1,)), ((), ())), preferred_element_type=jnp.float32)


def dot_tn(a, b):
    return lax.dot_general(a, b, (((0,), (0,)), ((), ())), preferred_element_type=jnp.float32)


def turn_matrix(buckets):
    row = lax.broadcasted_iota(jnp.int32, (buckets, buckets), 0)
    col = lax.broadcasted_iota(jnp.int32, (buckets, buckets), 1)
    return (row + col == buckets - 1).astype(jnp.bfloat16)


def skew_band(product):
    count, buckets = product.shape
    row = lax.broadcasted_iota(jnp.int32, (count, BLOCK), 0)
    lane = lax.broadcasted_iota(jnp.int32, (count, BLOCK), 1)
    edge = jnp.where(row + lane <= BLOCK - 2, product[:, buckets - 1 :], product[:, 0:1])
    wide = jnp.concatenate([product, edge], axis=1)
    return pltpu.roll(wide, 1, 1, stride=1, stride_axis=0)


def skew_back(turned, buckets):
    return pltpu.roll(turned, turned.shape[1] - BLOCK, 1, stride=1, stride_axis=0)[:, :buckets]


def chip_columns(vec_ref, chip, index, core):
    width = 3 * DH // 2
    both = jnp.concatenate(
        [
            vec_ref[2 * chip, index : index + 1, :width].astype(jnp.float32),
            vec_ref[2 * chip + 1, index : index + 1, :width].astype(jnp.float32),
        ],
        axis=1,
    )
    return jnp.where(core == 0, both[:, : 2 * DH], both[:, DH:])


def attend_kernel(
    xs_ref,
    qkvs_ref,
    tables_ref,
    vecs_ref,
    q_ref,
    k_ref,
    v_ref,
    qrev_ref,
    krev_ref,
    p_ref,
    ctx_ref,
    w_ref,
    table_ref,
    segc_ref,
    place_ref,
    wide_ref,
    ends_ref,
    held_ref,
):
    at = Place()
    full_len = xs_ref.shape[0] * xs_ref.shape[1]
    buckets = table_ref.shape[0]
    blocks = full_len // BLOCK
    span = buckets // 2
    side = span // BLOCK
    band_width = buckets + BLOCK
    band_blocks = band_width // BLOCK
    group = 2 * DH
    scale = 1.0 / math.sqrt(3.0 * DH)
    units = p_ref.shape[0]
    shard_rows = qkvs_ref.shape[2]
    table_rows = tables_ref.shape[3]
    batches = tables_ref.shape[1]
    for part in range(at.tokens):
        pieces = []
        for i in range(3):
            piece = qkvs_ref[part, i]
            pieces.append(jnp.where(at.core == 0, piece[:, :group], piece[:, DH:]))
        w_ref[part * shard_rows : (part + 1) * shard_rows] = jnp.concatenate(pieces, axis=1)
        core, chip = part % 2, part // 2
        table_ref[part * table_rows : (part + 1) * table_rows] = jnp.concatenate(
            [tables_ref[core, row, chip] for row in range(batches)], axis=1
        )
        own_seg = vecs_ref[part, 9:10].astype(jnp.float32)
        segc_ref[part * BLOCK : (part + 1) * BLOCK] = jnp.broadcast_to(own_seg, (BLOCK, BLOCK)).T
    seg_row = jnp.concatenate(
        [vecs_ref[part, 9:10].astype(jnp.float32) for part in range(at.tokens)], axis=1
    )
    bias = jnp.concatenate(
        [chip_columns(vecs_ref, at.chip, i, at.core) for i in range(3)], axis=1
    )
    tokens_all = xs_ref[...].reshape(full_len, xs_ref.shape[2])
    proj = (dot_nn(tokens_all, w_ref[...]) + bias).astype(jnp.bfloat16)
    rel = (dot_nn(table_ref[...], w_ref[:, : 2 * group]) + bias[:, : 2 * group]).astype(
        jnp.bfloat16
    )
    rel = dot_nn(turn_matrix(buckets), rel).astype(jnp.bfloat16)
    for slot in range(2):
        lo, hi = slot * DH, (slot + 1) * DH
        q_ref[slot] = proj[:, lo:hi]
        k_ref[slot] = proj[:, group + lo : group + hi]
        v_ref[slot] = proj[:, 2 * group + lo : 2 * group + hi]
        qrev_ref[slot] = rel[:, lo:hi]
        krev_ref[slot] = rel[:, group + lo : group + hi]
    held_ref[...] = jnp.zeros_like(held_ref)
    for slot in range(2):
        ends_ref[slot, 0] = dot_nt(qrev_ref[slot, 0:16], k_ref[slot])
        ends_ref[slot, 1] = dot_nt(qrev_ref[slot, buckets - 16 : buckets], k_ref[slot])

        def key_block(kb, carry):
            rows = k_ref[slot, pl.ds(pl.multiple_of(kb * BLOCK, BLOCK), BLOCK)]
            band = skew_band(dot_nt(rows, qrev_ref[slot]))
            for e in range(band_blocks):
                place_ref[
                    slot,
                    kb + e,
                    :,
                    (band_blocks - 1 - e) * BLOCK : (band_blocks - e) * BLOCK,
                ] = band[:, e * BLOCK : (e + 1) * BLOCK].T
            return carry

        lax.fori_loop(0, blocks, key_block, 0)

    first = at.core * (blocks // 2)

    def unit(u, carry):
        g = u + first
        slot = g // blocks
        qb = g % blocks
        start = pl.multiple_of(qb * BLOCK, BLOCK)
        rows = q_ref[slot, pl.ds(start, BLOCK)]
        own = dot_nt(rows, krev_ref[slot])
        band = skew_band(own) + place_ref[slot, qb + side]
        wide_ref[:, pl.ds(start, band_width)] = band
        content = dot_nt(rows, k_ref[slot])
        lane = lax.broadcasted_iota(jnp.int32, (BLOCK, full_len), 1)
        near = jnp.where(
            lane < start - span,
            own[:, 0:1] + ends_ref[slot, 1, 15:16],
            jnp.where(
                lane >= start + band_width - span,
                own[:, buckets - 1 :] + ends_ref[slot, 0, 0:1],
                wide_ref[:, span : span + full_len],
            ),
        )
        same = segc_ref[pl.ds(start, BLOCK), 0:1] == seg_row
        scores = jnp.where(same, (content + near) * scale, masked_score)
        highest = jnp.max(scores, axis=-1, keepdims=True)
        exponent = jnp.exp(scores - highest)
        total = jnp.sum(exponent, axis=-1, keepdims=True)
        probs = (exponent / total).astype(jnp.bfloat16)
        p_ref[u] = probs
        held_ref[slot, pl.ds(start, BLOCK)] = dot_nn(probs, v_ref[slot]).astype(jnp.bfloat16)
        return carry

    lax.fori_loop(0, units, unit, 0)
    for part in range(at.tokens):
        rows = slice(part * BLOCK, (part + 1) * BLOCK)
        ctx_ref[part] = jnp.concatenate([held_ref[0, rows], held_ref[1, rows]], axis=1)


def attend(xs, qkvs, tables, vecs):
    tokens, local_len, width = xs.shape
    full_len = tokens * local_len
    buckets = tokens * tables.shape[3]
    blocks = full_len // BLOCK
    units = 3 * blocks // 2
    band_width = buckets + BLOCK
    low, wide = jnp.bfloat16, jnp.float32
    pad_blocks = blocks + band_width // BLOCK - 1
    return pl.pallas_call(
        attend_kernel,
        out_shape=(
            jax.ShapeDtypeStruct((2, full_len, DH), low),
            jax.ShapeDtypeStruct((2, full_len, DH), low),
            jax.ShapeDtypeStruct((2, full_len, DH), low),
            jax.ShapeDtypeStruct((2, buckets, DH), low),
            jax.ShapeDtypeStruct((2, buckets, DH), low),
            jax.ShapeDtypeStruct((units, BLOCK, full_len), low),
            jax.ShapeDtypeStruct((tokens, local_len, 2 * DH), low),
            jax.ShapeDtypeStruct((width, 6 * DH), low),
            jax.ShapeDtypeStruct((buckets, width), low),
        ),
        in_specs=[pl.BlockSpec(memory_space=pltpu.VMEM)] * 4,
        out_specs=[pl.BlockSpec(memory_space=pltpu.VMEM)] * 9,
        scratch_shapes=[
            pltpu.VMEM((full_len, BLOCK), wide),
            pltpu.VMEM((2, pad_blocks, BLOCK, band_width), wide),
            pltpu.VMEM((BLOCK, full_len + buckets), wide),
            pltpu.VMEM((2, 2, 16, full_len), wide),
            pltpu.VMEM((2, full_len, DH), low),
        ],
        compiler_params=pltpu.CompilerParams(vmem_limit_bytes=ATTEND_VMEM),
        name="attend",
    )(xs, qkvs, tables, vecs)


def attend_back_kernel(
    q_ref,
    k_ref,
    v_ref,
    qrev_ref,
    krev_ref,
    p_ref,
    mix_ref,
    attn_ref,
    dcat_ref,
    rel_ref,
    sum_ref,
    heads_ref,
    wide_ref,
    low_ref,
    place_ref,
    dq_ref,
    dkt_ref,
    dvt_ref,
    far_ref,
    dkr_ref,
    dqr_ref,
):
    full_len = q_ref.shape[1]
    buckets = qrev_ref.shape[1]
    blocks = full_len // BLOCK
    span = buckets // 2
    side = span // BLOCK
    band_width = buckets + BLOCK
    band_blocks = band_width // BLOCK
    scale = 1.0 / math.sqrt(3.0 * DH)
    units = p_ref.shape[0]
    for ref in (wide_ref, low_ref, place_ref, dq_ref, dkt_ref, dvt_ref, far_ref, dkr_ref, dqr_ref):
        ref[...] = jnp.zeros_like(ref)
    at = Place()
    group = 2 * DH
    first_row = pl.multiple_of((3 * at.chip + at.core) * DH, DH)
    mix_rows = mix_ref[pl.ds(first_row, group)]
    dctx = dot_nt(attn_ref[...].reshape(full_len, attn_ref.shape[2]), mix_rows)
    for slot in range(2):
        heads_ref[slot] = dctx[:, slot * DH : (slot + 1) * DH].astype(jnp.bfloat16)
    first = at.core * (blocks // 2)
    turn = turn_matrix(BLOCK)
    place8 = lax.broadcasted_iota(jnp.int32, (8, full_len), 0)

    def unit(u, carry):
        g = u + first
        slot = g // blocks
        qb = g % blocks
        start = pl.multiple_of(qb * BLOCK, BLOCK)
        rows = q_ref[slot, pl.ds(start, BLOCK)]
        grad = heads_ref[slot, pl.ds(start, BLOCK)]
        probs = p_ref[u]
        wide_probs = probs.astype(jnp.float32)
        prob_grad = dot_nt(grad, v_ref[slot])
        inner = jnp.sum(wide_probs * prob_grad, axis=-1, keepdims=True)
        low_grad = (wide_probs * (prob_grad - inner)).astype(jnp.bfloat16)
        score_grad = low_grad.astype(jnp.float32)
        wide_ref[:, span : span + full_len] = dot_nn(turn, low_grad)
        low_ref[:, span : span + full_len] = low_grad
        dvt_ref[slot] += dot_tn(grad, probs)
        dkt_ref[slot] += dot_tn(rows, low_grad)
        row = lax.broadcasted_iota(jnp.int32, (BLOCK, full_len), 0)
        lane = lax.broadcasted_iota(jnp.int32, (BLOCK, full_len), 1)
        gap = lane - row - start
        right = jnp.where(gap > span, score_grad, 0.0)
        left = jnp.where(gap < 1 - span, score_grad, 0.0)
        end_right = jnp.sum(right, axis=-1, keepdims=True)
        end_left = jnp.sum(left, axis=-1, keepdims=True)
        far_right = jnp.sum(jnp.where(gap >= span, score_grad, 0.0), axis=0, keepdims=True)
        far_left = jnp.sum(jnp.where(gap < -span, score_grad, 0.0), axis=0, keepdims=True)
        far_ref[slot] += jnp.where(place8 == 0, far_right, jnp.where(place8 == 1, far_left, 0.0))
        band = wide_ref[:, pl.ds(start, band_width)]
        near = dot_nn(turn, skew_back(band, buckets).astype(jnp.bfloat16))
        bucket = lax.broadcasted_iota(jnp.int32, (BLOCK, buckets), 1)
        near = near + jnp.where(
            bucket == 0, end_left, jnp.where(bucket == buckets - 1, end_right, 0.0)
        )
        near_low = near.astype(jnp.bfloat16)
        dq = dot_nn(low_grad, k_ref[slot]) + dot_nn(near_low, krev_ref[slot])
        dq_ref[slot, pl.ds(start, BLOCK)] = dq
        dkr_ref[slot] += dot_tn(rows, near_low)
        for e in range(band_blocks):
            keys_at = pl.multiple_of(start + e * BLOCK, BLOCK)
            place_ref[
                slot, qb + e, :, (band_blocks - 1 - e) * BLOCK : (band_blocks - e) * BLOCK
            ] = dot_nt(turn, low_ref[:, pl.ds(keys_at, BLOCK)])
        return carry

    lax.fori_loop(0, units, unit, 0)
    parts_q, parts_k, parts_v = [], [], []
    parts_r = [None] * 4
    for slot in range(2):
        far_low = far_ref[slot].astype(jnp.bfloat16)
        mark = lax.broadcasted_iota(jnp.int32, (8, DH), 0)
        ends = jnp.where(
            mark == 0,
            qrev_ref[slot, 0:1].astype(jnp.float32),
            jnp.where(mark == 1, qrev_ref[slot, buckets - 1 : buckets].astype(jnp.float32), 0.0),
        ).astype(jnp.bfloat16)
        end_keys = dot_tn(ends, far_low)
        end_rows = dot_nn(far_low, k_ref[slot])

        whole_k = (dkt_ref[slot] + end_keys).T

        def key_side(kb, carry):
            start = pl.multiple_of(kb * BLOCK, BLOCK)
            far = skew_back(place_ref[slot, kb + side], buckets).astype(jnp.bfloat16)
            far = dot_nn(turn, far).astype(jnp.bfloat16)
            keys = k_ref[slot, pl.ds(start, BLOCK)]
            dqr_ref[slot] += dot_tn(keys, far)
            dq_ref[2 + slot, pl.ds(start, BLOCK)] = dot_nn(far, qrev_ref[slot])
            return carry

        lax.fori_loop(0, blocks, key_side, 0)
        parts_q.append((dq_ref[slot] * scale).astype(jnp.bfloat16))
        parts_k.append(((dq_ref[2 + slot] + whole_k) * scale).astype(jnp.bfloat16))
        parts_v.append(dvt_ref[slot].T.astype(jnp.bfloat16))
        bucket = lax.broadcasted_iota(jnp.int32, (buckets, DH), 0)
        qr = dqr_ref[slot].T + jnp.where(
            bucket == 0, end_rows[0:1], jnp.where(bucket == buckets - 1, end_rows[1:2], 0.0)
        )
        dqr_out = qr * scale
        dkr_out = dkr_ref[slot].T * scale
        parts_r[slot] = dqr_out
        parts_r[2 + slot] = dkr_out
    dcat = jnp.concatenate(parts_q + parts_k + parts_v, axis=1)
    dcat_ref[...] = dcat
    rel = jnp.concatenate(parts_r, axis=1)
    rel_ref[...] = dot_nn(turn_matrix(buckets), rel.astype(jnp.bfloat16)).astype(jnp.bfloat16)
    rel_sum = jnp.sum(rel, axis=0, keepdims=True)
    rel_sum = jnp.concatenate([rel_sum, jnp.zeros((1, 2 * DH), jnp.float32)], axis=1)
    sums = jnp.sum(dcat.astype(jnp.float32), axis=0, keepdims=True) + rel_sum
    sum_ref[...] = jnp.broadcast_to(sums, sum_ref.shape)


def attend_back(q, k, v, qrev, krev, probs, m_mix, attn_all):
    full_len = q.shape[1]
    buckets = qrev.shape[1]
    blocks = full_len // BLOCK
    band_width = buckets + BLOCK
    low, wide = jnp.bfloat16, jnp.float32
    pad_blocks = blocks + band_width // BLOCK - 1
    return pl.pallas_call(
        attend_back_kernel,
        out_shape=(
            jax.ShapeDtypeStruct((full_len, 6 * DH), low),
            jax.ShapeDtypeStruct((buckets, 4 * DH), low),
            jax.ShapeDtypeStruct((8, 6 * DH), wide),
        ),
        in_specs=[pl.BlockSpec(memory_space=pltpu.VMEM)] * 8,
        out_specs=[pl.BlockSpec(memory_space=pltpu.VMEM)] * 3,
        scratch_shapes=[
            pltpu.VMEM((2, full_len, DH), low),
            pltpu.VMEM((BLOCK, full_len + buckets), wide),
            pltpu.VMEM((BLOCK, full_len + buckets), low),
            pltpu.VMEM((2, pad_blocks, BLOCK, band_width), wide),
            pltpu.VMEM((4, full_len, DH), wide),
            pltpu.VMEM((2, DH, full_len), wide),
            pltpu.VMEM((2, DH, full_len), wide),
            pltpu.VMEM((2, 8, full_len), wide),
            pltpu.VMEM((2, DH, buckets), wide),
            pltpu.VMEM((2, DH, buckets), wide),
        ],
        compiler_params=pltpu.CompilerParams(vmem_limit_bytes=BACK_VMEM),
        name="attend_back",
    )(q, k, v, qrev, krev, probs, m_mix, attn_all)


MESH = pl.DeviceIdType.MESH
VMEM_SPEC = pl.BlockSpec(memory_space=pltpu.VMEM)
HBM_SPEC = pl.BlockSpec(memory_space=pltpu.HBM)
CHUNKS = 2


class Place:
    def __init__(self):
        self.batches = lax.axis_size("batch")
        self.tokens = lax.axis_size("seq")
        self.chips = self.tokens // 2
        self.row = lax.axis_index("batch")
        self.part = lax.axis_index("seq")
        self.chip = self.part // 2
        self.core = self.part % 2

    def along_chips(self, k):
        chip = lax.rem(self.chip + k, self.chips)
        return chip, (self.row, 2 * chip + self.core)

    def from_chips(self, k):
        return lax.rem(self.chip + self.chips - k, self.chips)

    def partner(self):
        return (self.row, self.part + 1 - 2 * self.core)

    def along_rows(self, k):
        row = lax.rem(self.row + k, self.batches)
        return row, (row, self.part)

    def from_rows(self, k):
        return lax.rem(self.row + self.batches - k, self.batches)

    def along_seq(self, k):
        part = lax.rem(self.part + k, self.tokens)
        return part, (self.row, part)

    def along_plane(self, k):
        index = lax.rem(2 * self.row + self.core + k, 2 * self.batches)
        row, core = index // 2, index % 2
        return row, core, (row, 2 * self.chip + core)

    def chip_peers(self):
        return [self.along_chips(k)[1] for k in range(1, self.chips)]

    def row_peers(self):
        return [self.along_rows(k)[1] for k in range(1, self.batches)]

    def cross_peers(self):
        other = self.part + 1 - 2 * self.core
        return [(self.along_rows(k)[0], other) for k in range(1, self.batches)]

    def cross_row_peers(self):
        return self.row_peers() + self.cross_peers()

    def seq_peers(self):
        return [self.along_seq(k)[1] for k in range(1, self.tokens)]

    def plane_peers(self):
        return [self.along_plane(k)[2] for k in range(1, 2 * self.batches)]


def meet(peers):
    barrier = pltpu.get_barrier_semaphore()
    for peer in peers:
        pl.semaphore_signal(barrier, inc=1, device_id=peer, device_id_type=MESH)
    pl.semaphore_wait(barrier, len(peers))


class Wires:
    def __init__(self, send_sems, recv_sems, local_sems):
        self.sems = (send_sems, recv_sems, local_sems)
        self.used = [0, 0]
        self.ends = []

    def send(self, src, dst, peer):
        k = self.used[0]
        self.used[0] += 1
        copy = pltpu.make_async_remote_copy(
            src_ref=src,
            dst_ref=dst,
            send_sem=self.sems[0].at[k],
            recv_sem=self.sems[1].at[k],
            device_id=peer,
            device_id_type=MESH,
        )
        copy.start()
        self.ends.append(copy.wait_send)
        return copy

    def local(self, src, dst):
        k = self.used[1]
        self.used[1] += 1
        copy = pltpu.make_async_copy(src, dst, self.sems[2].at[k])
        copy.start()
        return copy

    def finish(self):
        for end in self.ends:
            end()


def wire_scratch(sends, locals_count):
    return [
        pltpu.SemaphoreType.DMA((sends,)),
        pltpu.SemaphoreType.DMA((sends,)),
        pltpu.SemaphoreType.DMA((locals_count,)),
    ]


def comm_call(kernel, name, ident, out_shapes, inputs, sends, locals_count, scratch=(), spec=VMEM_SPEC):
    return pl.pallas_call(
        kernel,
        out_shape=tuple(out_shapes),
        in_specs=[spec] * len(inputs),
        out_specs=tuple([VMEM_SPEC] * len(out_shapes)),
        scratch_shapes=list(scratch) + wire_scratch(sends, locals_count),
        compiler_params=pltpu.CompilerParams(
            collective_id=ident, has_side_effects=True, vmem_limit_bytes=COMM_VMEM
        ),
        name=name,
    )(*inputs)


def like(array, *lead):
    return jax.ShapeDtypeStruct(tuple(lead) + tuple(array.shape), array.dtype)


def pick(values, index):
    out = jnp.int32(values[0])
    for i in range(1, len(values)):
        out = jnp.where(index == i, jnp.int32(values[i]), out)
    return out


def arrival_order(at):
    chips = range(at.chips)
    lists = [sorted((j for j in chips if j != z), key=lambda j: (abs(j - z), j)) for z in chips]
    return [pick([lists[z][t] for z in chips], at.chip) for t in range(at.chips - 1)]


def return_order(at):
    chips = range(at.chips)

    def away(j, z):
        end = at.chips - 1 if j < z else 0
        return (abs(j - end) + abs(end - z), j)

    lists = [sorted((j for j in chips if j != z), key=lambda j: away(j, z)) for z in chips]
    return [pick([lists[z][t] for z in chips], at.chip) for t in range(at.chips - 1)]


def goes_on(at, j):
    above = jnp.logical_and(j < at.chip, at.chip < at.chips - 1)
    below = jnp.logical_and(j > at.chip, at.chip > 0)
    return jnp.logical_or(above, below)


def line_peer(at, step):
    return (at.row, 2 * (at.chip + step) + at.core)


class LineGather:
    def __init__(self, at, buf, slot, sems, own=None):
        self.at, self.buf, self.slot, self.own = at, buf, slot, own
        self.send_sems, self.recv_sems = sems
        self.rows = buf.shape[1] // CHUNKS

    def copy(self, j, h, step, k, own=False):
        window = pl.ds(h * self.rows, self.rows)
        home = self.buf.at[self.slot(j), window]
        src = self.own.at[window] if own and self.own is not None else home
        return pltpu.make_async_remote_copy(
            src_ref=src,
            dst_ref=home,
            send_sem=self.send_sems.at[k * CHUNKS + h],
            recv_sem=self.recv_sems.at[j * CHUNKS + h],
            device_id=line_peer(self.at, step),
            device_id_type=MESH,
        )

    def own_each(self, act):
        z, n = self.at.chip, self.at.chips
        for h in range(CHUNKS):

            @pl.when(z < n - 1)
            def _():
                act(self.copy(z, h, 1, z, own=True))

            @pl.when(z > 0)
            def _():
                act(self.copy(z, h, -1, n, own=True))

    def start(self):
        self.own_each(lambda copy: copy.start())

    def arrive(self, j):
        step = jnp.where(j < self.at.chip, 1, -1)
        for h in range(CHUNKS):
            self.copy(j, h, -step, j).wait_recv()

            @pl.when(goes_on(self.at, j))
            def _():
                self.copy(j, h, step, j).start()

    def drain(self, order):
        self.own_each(lambda copy: copy.wait_send())
        for j in order:
            step = jnp.where(j < self.at.chip, 1, -1)

            @pl.when(goes_on(self.at, j))
            def _():
                for h in range(CHUNKS):
                    self.copy(j, h, step, j).wait_send()


class LineReduce:
    def __init__(self, at, part, got, sems):
        self.at, self.part, self.got = at, part, got
        self.send_sems, self.recv_sems = sems
        self.rows = part.shape[1] // CHUNKS

    def copy(self, j, h):
        z, n = self.at.chip, self.at.chips
        window = pl.ds(h * self.rows, self.rows)
        slot = jnp.where(z + 1 == j, n, j)
        return pltpu.make_async_remote_copy(
            src_ref=self.part.at[j, window],
            dst_ref=self.got.at[slot, window],
            send_sem=self.send_sems.at[j * CHUNKS + h],
            recv_sem=self.recv_sems.at[slot * CHUNKS + h],
            device_id=line_peer(self.at, jnp.where(j < z, -1, 1)),
            device_id_type=MESH,
        )

    def landed(self, slot, h, step):
        window = pl.ds(h * self.rows, self.rows)
        return pltpu.make_async_remote_copy(
            src_ref=self.got.at[slot, window],
            dst_ref=self.got.at[slot, window],
            send_sem=self.send_sems.at[h],
            recv_sem=self.recv_sems.at[slot * CHUNKS + h],
            device_id=line_peer(self.at, step),
            device_id_type=MESH,
        )

    def send(self, j):
        for h in range(CHUNKS):
            self.copy(j, h).start()

    def send_last(self, j):
        @pl.when(jnp.logical_not(goes_on(self.at, j)))
        def _():
            self.send(j)

    def pass_on(self, order):
        z, n = self.at.chip, self.at.chips
        wide = jnp.float32

        @pl.when(jnp.logical_and(z > 0, z < n - 1))
        def _():
            for j in order:
                step = jnp.where(j < z, 1, -1)
                for h in range(CHUNKS):
                    self.landed(j, h, step).wait_recv()
                    window = pl.ds(h * self.rows, self.rows)
                    total = self.part[j, window].astype(wide) + self.got[j, window].astype(wide)
                    self.part[j, window] = total.astype(self.part.dtype)
                    self.copy(j, h).start()

    def clear(self):
        z, n = self.at.chip, self.at.chips

        @pl.when(z == n - 1)
        def _():
            self.got[z] = jnp.zeros(self.got.shape[1:], self.got.dtype)

        @pl.when(z == 0)
        def _():
            self.got[n] = jnp.zeros(self.got.shape[1:], self.got.dtype)

    def collect(self):
        z, n = self.at.chip, self.at.chips
        for h in range(CHUNKS):

            @pl.when(z < n - 1)
            def _():
                self.landed(z, h, 1).wait_recv()

            @pl.when(z > 0)
            def _():
                self.landed(n, h, -1).wait_recv()

        return self.got[z].astype(jnp.float32) + self.got[n].astype(jnp.float32)

    def drain(self, order):
        for j in order:
            for h in range(CHUNKS):
                self.copy(j, h).wait_send()


def gather_sems(chips):
    return [
        pltpu.SemaphoreType.DMA(((chips + 1) * CHUNKS,)),
        pltpu.SemaphoreType.DMA((chips * CHUNKS,)),
    ]


def reduce_sems(chips):
    return [
        pltpu.SemaphoreType.DMA((chips * CHUNKS,)),
        pltpu.SemaphoreType.DMA(((chips + 1) * CHUNKS,)),
    ]


def gather_kernel(
    x_ref, wq_ref, wk_ref, wv_ref, mix_ref, table_ref, vec_ref, up_ref, down_ref,
    xs_ref, qkvs_ref, mixs_ref, tables_ref, vecs_ref, up2_ref, down2_ref,
    line_send, line_recv, *sems,
):
    at = Place()
    wires = Wires(*sems)
    b, s, z, c = at.row, at.part, at.chip, at.core
    off_diagonal = b != z
    turned = (z, 2 * b + c)
    peers = at.seq_peers() + at.row_peers()
    barrier = pltpu.get_barrier_semaphore()
    for peer in peers:
        pl.semaphore_signal(barrier, inc=1, device_id=peer, device_id_type=MESH)

    @pl.when(off_diagonal)
    def _():
        pl.semaphore_signal(barrier, inc=1, device_id=turned, device_id_type=MESH)

    pl.semaphore_wait(barrier, len(peers) + off_diagonal.astype(jnp.int32))

    swaps, stays = [], []
    for i, ref in enumerate((wq_ref, wk_ref, wv_ref)):
        k = wires.used[0]
        wires.used[0] += 1
        swaps.append(
            pltpu.make_async_remote_copy(
                src_ref=ref,
                dst_ref=qkvs_ref.at[2 * z + c, i],
                send_sem=sems[0].at[k],
                recv_sem=sems[1].at[k],
                device_id=turned,
                device_id_type=MESH,
            )
        )
        stays.append(pltpu.make_async_copy(ref, qkvs_ref.at[2 * b + c, i], sems[2].at[i]))
        wires.used[1] += 1

    @pl.when(off_diagonal)
    def _():
        for swap in swaps:
            swap.start()

    @pl.when(jnp.logical_not(off_diagonal))
    def _():
        for stay in stays:
            stay.start()

    table_home = tables_ref.at[c, b, z]
    table_sends = [
        wires.send(table_ref, table_home, at.along_chips(k)[1]) for k in range(1, at.chips)
    ]
    kept = wires.local(table_ref, table_home)
    line = LineGather(at, xs_ref, lambda j: 2 * j + c, (line_send, line_recv), own=x_ref)
    line.start()
    last = [wires.send(vec_ref, vecs_ref.at[s], at.along_seq(k)[1]) for k in range(1, at.tokens)]
    last += [
        wires.send(mix_ref, mixs_ref.at[z], at.along_chips(k)[1]) for k in range(1, at.chips)
    ]
    last += [
        wires.send(x_ref, xs_ref.at[s], at.partner()),
        wires.send(up_ref, up2_ref, at.partner()),
        wires.send(down_ref, down2_ref, at.partner()),
    ]
    own = [
        wires.local(x_ref, xs_ref.at[s]),
        wires.local(mix_ref, mixs_ref.at[z]),
        wires.local(vec_ref, vecs_ref.at[s]),
    ]

    @pl.when(off_diagonal)
    def _():
        for swap in swaps:
            swap.wait_recv()

    @pl.when(jnp.logical_not(off_diagonal))
    def _():
        for stay in stays:
            stay.wait()

    mine = qkvs_ref.at[2 * b + c]
    qkv_sends = [wires.send(mine, mine, at.along_rows(k)[1]) for k in range(1, at.batches)]
    last.append(wires.send(mine, mine, at.partner()))
    for copy in table_sends:
        copy.wait_recv()
    kept.wait()
    mine = tables_ref.at[c, b]
    row_sends = [wires.send(mine, mine, at.along_rows(k)[1]) for k in range(1, at.batches)]
    last.append(wires.send(mine, mine, at.partner()))
    order = arrival_order(at)

    def arrived(j):
        line.arrive(j)
        home = xs_ref.at[2 * j + c]
        last.append(wires.send(home, home, at.partner()))

    for j in order[:2]:
        arrived(j)
    for k in range(1, at.batches):
        qkv_sends[k - 1].wait_recv()
        home = qkvs_ref.at[2 * at.from_rows(k) + c]
        last.append(wires.send(home, home, at.partner()))
    for k in range(1, at.batches):
        row_sends[k - 1].wait_recv()
        home = tables_ref.at[c, at.from_rows(k)]
        last.append(wires.send(home, home, at.partner()))
    for j in order[2:]:
        arrived(j)
    for copy in last:
        copy.wait_recv()
    for copy in own:
        copy.wait()
    wires.finish()
    line.drain(order)

    @pl.when(off_diagonal)
    def _():
        for swap in swaps:
            swap.wait_send()


def gather_inputs(x, w_query, w_key, w_value, w_mix, rel_table, vec, up, down):
    tokens, batches = lax.axis_size("seq"), lax.axis_size("batch")
    chips = tokens // 2
    outs = (
        like(x, tokens),
        like(w_query, tokens, 3),
        like(w_mix, chips),
        like(rel_table, 2, batches, chips),
        like(vec, tokens),
        like(up),
        like(down),
    )
    sends = 3 + 2 * (chips - 1) + tokens - 1 + 3 + 4 * (batches - 1) + 2 + chips - 1
    inputs = (x, w_query, w_key, w_value, w_mix, rel_table, vec, up, down)
    return comm_call(
        gather_kernel,
        "gather_inputs",
        0,
        outs,
        inputs,
        sends,
        7,
        scratch=gather_sems(chips),
        spec=HBM_SPEC,
    )


def norm_parts(values):
    average = jnp.mean(values, axis=-1, keepdims=True)
    centered = values - average
    variance = jnp.mean(centered * centered, axis=-1, keepdims=True)
    scale = lax.rsqrt(variance + norm_eps)
    return centered * scale, scale


def norm_back(grad, gain, unit, scale):
    inner = grad * gain
    mean = jnp.mean(inner, axis=-1, keepdims=True)
    slope = jnp.mean(inner * unit, axis=-1, keepdims=True)
    return scale * (inner - mean - unit * slope)


def line_pass(gather, reduce, order, work):
    def finish(j):
        work(j)
        reduce.send_last(j)

    gather.arrive(order[0])
    gather.arrive(order[1])
    finish(order[0])
    gather.arrive(order[2])
    finish(order[1])
    finish(order[2])


def feed_kernel(
    ctx_ref, x_ref, mixs_ref, vecs_ref, up_ref, down_ref, up2_ref, down2_ref, out_grad_ref,
    output_ref, pre_grad_ref, sums_ref, attn_ref, mix_ref, ups_ref, downs_ref, upbs_ref,
    got_ref, mixall_ref, hid_ref, act_ref, slope_ref, part_ref, ffn_ref, grad_ref, inner_ref,
    back_ref, backs_ref, up_away_ref, down_away_ref, upb_away_ref,
    up_got_ref, down_got_ref, upb_got_ref, upg_ref, downg_ref, upb_ref, vec_ref,
    hid_send, hid_recv, ffn_send, ffn_recv, grad_send, grad_recv, back_send, back_recv,
    attn_send, attn_recv, *sems,
):
    at = Place()
    wires = Wires(*sems)
    low, wide = jnp.bfloat16, jnp.float32
    b, s, z, c = at.row, at.part, at.chip, at.core
    order, returns = arrival_order(at), return_order(at)
    meet(at.seq_peers() + at.row_peers())
    last, own = [], []
    swaps = []
    for k in range(1, at.tokens):
        part, peer = at.along_seq(k)
        swaps.append(wires.send(ctx_ref.at[part], got_ref.at[s], peer))
    kept = wires.local(ctx_ref.at[s], got_ref.at[s])
    mix_sends = [
        wires.send(mixs_ref, mixall_ref.at[c, b], at.along_rows(k)[1])
        for k in range(1, at.batches)
    ]
    mix_lasts = [wires.send(mixs_ref, mixall_ref.at[c, b], at.partner())]
    mix_kept = wires.local(mixs_ref, mixall_ref.at[c, b])
    lanes = x_ref.shape[1] // at.tokens
    hidden_here = up_ref.shape[1]
    vec_ref[...] = jnp.concatenate(
        [vecs_ref[part, :, :lanes].astype(wide) for part in range(at.tokens)], axis=1
    )
    bias3 = vec_ref[3:4]
    gain1, gain2 = vec_ref[4:5], vec_ref[5:6]
    shift1, shift2 = vec_ref[6:7], vec_ref[7:8]
    bias_down = vec_ref[8:9]
    partner = s + 1 - 2 * c
    up_rows = hidden_here // BLOCK
    bias_up = jnp.concatenate(
        [vecs_ref[s, 10 + i : 11 + i].astype(wide) for i in range(up_rows)]
        + [vecs_ref[partner, 10 + i : 11 + i].astype(wide) for i in range(up_rows)],
        axis=1,
    )
    for k in range(1, at.batches):
        mix_sends[k - 1].wait_recv()
        home = mixall_ref.at[c, at.from_rows(k)]
        mix_lasts.append(wires.send(home, home, at.partner()))
    for copy in mix_lasts:
        copy.wait_recv()
    mix_kept.wait()
    shard_rows = mixs_ref.shape[1]
    for part in range(at.tokens):
        mix_ref[part * shard_rows : (part + 1) * shard_rows] = jnp.concatenate(
            [mixall_ref[part % 2, row, part // 2] for row in range(at.batches)], axis=1
        )
    for copy in swaps:
        copy.wait_recv()
    kept.wait()
    pieces = []
    for chip in range(at.chips):
        left, right = got_ref[2 * chip], got_ref[2 * chip + 1]
        middle = left[:, DH:].astype(wide) + right[:, :DH].astype(wide)
        pieces += [left[:, :DH], middle.astype(low), right[:, DH:]]
    context = jnp.concatenate(pieces, axis=1)
    pre_norm = x_ref[...].astype(wide) + dot_nn(context, mix_ref[...]) + bias3
    unit1, scale1 = norm_parts(pre_norm)
    hidden = unit1 * gain1 + shift1
    hid_ref[z] = hidden.astype(low)
    hid_line = LineGather(at, hid_ref, lambda j: j, (hid_send, hid_recv))
    ffn_line = LineReduce(at, part_ref, ffn_ref, (ffn_send, ffn_recv))
    hid_line.start()
    ffn_line.clear()

    def ffn(chip):
        rows = hid_ref[chip]
        inner = jnp.concatenate(
            [dot_nn(rows, up_ref[...]), dot_nn(rows, up2_ref[...])], axis=1
        )
        inner = inner + bias_up
        cdf = 0.5 * (1.0 + lax.erf(inner * math.sqrt(0.5)))
        act = (inner * cdf).astype(low)
        slope_ref[chip] = cdf + inner * (
            jnp.exp(-0.5 * inner * inner) * (1.0 / math.sqrt(2.0 * math.pi))
        )
        act_ref[chip] = act
        part_ref[chip] = (
            dot_nn(act[:, :hidden_here], down_ref[...])
            + dot_nn(act[:, hidden_here:], down2_ref[...])
        ).astype(low)

    ffn(z)
    line_pass(hid_line, ffn_line, order, ffn)
    ffn_line.pass_on(returns)
    total = part_ref[z].astype(wide) + ffn_line.collect()
    mixed = hidden + total + bias_down
    unit2, scale2 = norm_parts(mixed)
    output_ref[...] = (unit2 * gain2 + shift2).astype(low)
    out_grad = out_grad_ref[...].astype(wide)
    mixed_grad = norm_back(out_grad, gain2, unit2, scale2)
    grad_ref[z] = mixed_grad.astype(low)
    grad_line = LineGather(at, grad_ref, lambda j: j, (grad_send, grad_recv))
    back_line = LineReduce(at, back_ref, backs_ref, (back_send, back_recv))
    grad_line.start()
    back_line.clear()
    gain2_grad = jnp.sum(out_grad * unit2, axis=0, keepdims=True)
    shift2_grad = jnp.sum(out_grad, axis=0, keepdims=True)
    downb_grad = jnp.sum(mixed_grad, axis=0, keepdims=True)

    def back(chip):
        rows = grad_ref[chip]
        act_grad = jnp.concatenate(
            [dot_nt(rows, down_ref[...]), dot_nt(rows, down2_ref[...])], axis=1
        )
        inner_low = (act_grad * slope_ref[chip]).astype(low)
        inner_ref[chip] = inner_low
        back_ref[chip] = (
            dot_nt(inner_low[:, :hidden_here], up_ref[...])
            + dot_nt(inner_low[:, hidden_here:], up2_ref[...])
        ).astype(low)

    back(z)
    line_pass(grad_line, back_line, order, back)
    width = x_ref.shape[1]
    columns = width // at.batches
    inner_all = inner_ref[...].reshape(at.chips * BLOCK, 2 * hidden_here)
    act_all = act_ref[...].reshape(at.chips * BLOCK, 2 * hidden_here)
    hid_all = hid_ref[...].reshape(at.chips * BLOCK, width)
    grad_all = grad_ref[...].reshape(at.chips * BLOCK, width)
    near, away = slice(0, hidden_here), slice(hidden_here, 2 * hidden_here)
    up_away_ref[...] = dot_tn(hid_all, inner_all[:, away]).astype(low)
    down_grad = dot_tn(act_all, grad_all)
    for row in range(at.batches):
        piece = slice(row * columns, (row + 1) * columns)
        down_away_ref[row] = down_grad[away, piece].astype(low)
    upb_grad = jnp.sum(inner_all.astype(wide), axis=0, keepdims=True)
    upb_away_ref[...] = jnp.broadcast_to(upb_grad[:, away], upb_away_ref.shape)
    halves = [
        wires.send(up_away_ref, up_got_ref, at.partner()),
        wires.send(down_away_ref, down_got_ref, at.partner()),
        wires.send(upb_away_ref, upb_got_ref, at.partner()),
    ]
    back_line.pass_on(returns)
    up_own = dot_tn(hid_all, inner_all[:, near])
    for copy in halves:
        copy.wait_recv()
    upb_ref[...] = jnp.broadcast_to(upb_grad[:, near], upb_ref.shape) + upb_got_ref[...]
    up_sum = (up_own + up_got_ref[...].astype(wide)).astype(low)
    for row in range(at.batches):
        upg_ref[row] = up_sum[row * columns : (row + 1) * columns]
        piece = slice(row * columns, (row + 1) * columns)
        downg_ref[row] = (down_grad[near, piece] + down_got_ref[row].astype(wide)).astype(low)
    for k in range(1, at.batches):
        row, peer = at.along_rows(k)
        last.append(wires.send(upg_ref.at[row], ups_ref.at[b], peer))
        last.append(wires.send(downg_ref.at[row], downs_ref.at[b], peer))
        last.append(wires.send(upb_ref, upbs_ref.at[b], peer))
    own.append(wires.local(upg_ref.at[b], ups_ref.at[b]))
    own.append(wires.local(downg_ref.at[b], downs_ref.at[b]))
    own.append(wires.local(upb_ref, upbs_ref.at[b]))
    total = back_ref[z].astype(wide) + back_line.collect()
    hidden_grad = mixed_grad + total
    pre_grad = norm_back(hidden_grad, gain1, unit1, scale1)
    attn_ref[s] = pre_grad.astype(low)
    attn_line = LineGather(at, attn_ref, lambda j: 2 * j + c, (attn_send, attn_recv))
    attn_line.start()
    last.append(wires.send(attn_ref.at[s], attn_ref.at[s], at.partner()))
    pre_grad_ref[...] = pre_grad
    gain1_grad = jnp.sum(hidden_grad * unit1, axis=0, keepdims=True)
    shift1_grad = jnp.sum(hidden_grad, axis=0, keepdims=True)
    bias3_grad = jnp.sum(pre_grad, axis=0, keepdims=True)
    sums = jnp.concatenate(
        [bias3_grad, gain1_grad, gain2_grad, shift1_grad, shift2_grad, downb_grad]
        + [jnp.zeros((2, width), wide)],
        axis=0,
    )
    spare = jnp.zeros((8, BLOCK - lanes), wide)
    for part in range(at.tokens):
        sums_ref[part] = jnp.concatenate(
            [sums[:, part * lanes : (part + 1) * lanes], spare], axis=1
        )
    for j in order:
        attn_line.arrive(j)
        home = attn_ref.at[2 * j + c]
        last.append(wires.send(home, home, at.partner()))
    for copy in last:
        copy.wait_recv()
    for copy in own:
        copy.wait()
    wires.finish()
    for line in (hid_line, ffn_line, grad_line, back_line, attn_line):
        line.drain(order)


def feed_forward(ctx, x, mixs, vecs, up, down, up2, down2, out_grad, ident):
    tokens, batches = lax.axis_size("seq"), lax.axis_size("batch")
    chips = tokens // 2
    width = x.shape[1]
    columns = width // batches
    hidden_here = up.shape[1]
    low, wide = jnp.bfloat16, jnp.float32
    outs = (
        jax.ShapeDtypeStruct(x.shape, low),
        jax.ShapeDtypeStruct(x.shape, wide),
        jax.ShapeDtypeStruct((tokens, 8, BLOCK), wide),
        jax.ShapeDtypeStruct((tokens,) + x.shape, low),
        jax.ShapeDtypeStruct((width, width), low),
        jax.ShapeDtypeStruct((batches, columns, hidden_here), low),
        jax.ShapeDtypeStruct((batches, hidden_here, columns), low),
        jax.ShapeDtypeStruct((batches, 8, hidden_here), wide),
    )
    block = (chips,) + x.shape
    wide_block = (chips, x.shape[0], 2 * hidden_here)
    slots = (chips + 1,) + x.shape
    up_half, bias_half = (width, hidden_here), (8, hidden_here)
    down_half = (batches, hidden_here, columns)
    scratch = [
        pltpu.VMEM(ctx.shape, low),
        pltpu.VMEM((2, batches) + mixs.shape, low),
        pltpu.VMEM(block, low),
        pltpu.VMEM(wide_block, low),
        pltpu.VMEM(wide_block, wide),
        pltpu.VMEM(block, low),
        pltpu.VMEM(slots, low),
        pltpu.VMEM(block, low),
        pltpu.VMEM(wide_block, low),
        pltpu.VMEM(block, low),
        pltpu.VMEM(slots, low),
        pltpu.VMEM(up_half, low),
        pltpu.VMEM(down_half, low),
        pltpu.VMEM(bias_half, wide),
        pltpu.VMEM(up_half, low),
        pltpu.VMEM(down_half, low),
        pltpu.VMEM(bias_half, wide),
        pltpu.VMEM((batches, columns, hidden_here), low),
        pltpu.VMEM((batches, hidden_here, columns), low),
        pltpu.VMEM(bias_half, wide),
        pltpu.VMEM((16, width), wide),
    ]
    scratch += (gather_sems(chips) + reduce_sems(chips)) * 2 + gather_sems(chips)
    inputs = (ctx, x, mixs, vecs, up, down, up2, down2, out_grad)
    sends = tokens - 1 + 2 * batches - 1 + 3 + 3 * (batches - 1) + chips
    return pl.pallas_call(
        feed_kernel,
        out_shape=outs,
        in_specs=[VMEM_SPEC] * len(inputs),
        out_specs=(VMEM_SPEC,) * len(outs),
        scratch_shapes=scratch + wire_scratch(sends, 5),
        compiler_params=pltpu.CompilerParams(
            collective_id=ident, has_side_effects=True, vmem_limit_bytes=FEED_VMEM
        ),
        name="feed_forward",
    )(*inputs)


def settle_kernel(
    vec_ref, col_ref, dcat_ref, rel_ref, w_ref, xs_ref, table_ref, ctx_ref, attn_ref,
    ins_ref, vec_all_ref, cols_ref, dw_all_ref, tab_all_ref, mix_all_ref,
    in_ref, dw_ref, tab_ref, mix_ref, half_ref, sum_ref, vecs_ref, vec_low_ref, dws_ref, dw_low_ref, tabs_ref, tab_low_ref,
    mixs_ref, mix_low_ref, *sems,
):
    at = Place()
    wires = Wires(*sems)
    low, wide = jnp.bfloat16, jnp.float32
    b, s, z, c = at.row, at.part, at.chip, at.core
    off_diagonal = b != z
    same, cross = (z, 2 * b + c), (z, 2 * b + 1 - c)
    peers = at.seq_peers() + at.cross_row_peers()
    barrier = pltpu.get_barrier_semaphore()
    for peer in peers:
        pl.semaphore_signal(barrier, inc=1, device_id=peer, device_id_type=MESH)

    @pl.when(off_diagonal)
    def _():
        pl.semaphore_signal(barrier, inc=1, device_id=same, device_id_type=MESH)
        pl.semaphore_signal(barrier, inc=1, device_id=cross, device_id_type=MESH)

    pl.semaphore_wait(barrier, len(peers) + 2 * off_diagonal.astype(jnp.int32))

    dw_sends, tab_sends, mix_sends, vec_sends, last, own = [], [], [], [], [], []
    width = w_ref.shape[0]
    columns = width // at.batches
    full_len = dcat_ref.shape[0]
    group = 2 * DH

    def input_part(chip, core):
        start = pl.multiple_of((2 * chip + core) * BLOCK, BLOCK)
        in_ref[chip, core] = dot_nt(dcat_ref[pl.ds(start, BLOCK)], w_ref[...]).astype(low)

    halves = []
    for chip in range(at.chips):
        input_part(chip, 1 - c)
        halves.append(wires.send(in_ref.at[chip, 1 - c], half_ref.at[chip], at.partner()))
    for k in range(1, at.tokens):
        part, peer = at.along_seq(k)
        vec_sends.append(wires.send(vec_ref.at[part], vecs_ref.at[k - 1], peer))
    mine = 2 * b + c
    for k in range(1, 2 * at.batches):
        last.append(wires.send(col_ref, cols_ref.at[mine], at.along_plane(k)[2]))
    own.append(wires.local(col_ref, cols_ref.at[mine]))

    for chip in range(at.chips):
        input_part(chip, c)
        halves[chip].wait_recv()
        sum_ref[chip] = (in_ref[chip, c].astype(wide) + half_ref[chip].astype(wide)).astype(low)
    for k in range(1, at.chips):
        chip, peer = at.along_chips(k)
        last.append(wires.send(sum_ref.at[chip], ins_ref.at[z], peer))
    own.append(wires.local(sum_ref.at[z], ins_ref.at[z]))

    whole = xs_ref[...].reshape(full_len, width)
    dw = dot_tn(whole, dcat_ref[...])
    dw_rel = dot_tn(table_ref[...], rel_ref[...])
    dw = jnp.concatenate([dw[:, : 2 * group] + dw_rel, dw[:, 2 * group :]], axis=1)
    for row in range(at.batches):
        dw_ref[row] = dw[row * columns : (row + 1) * columns].astype(low)
    for k in range(1, at.batches):
        row, peer = at.along_rows(k)
        dw_sends.append(wires.send(dw_ref.at[row], dws_ref.at[k - 1], peer))
    for row in range(at.batches):
        rows = slice(row * columns, (row + 1) * columns)
        tab_ref[row] = dot_nt(rel_ref[...], w_ref[rows, : 2 * group]).astype(low)
    for k in range(1, at.batches):
        row, peer = at.along_rows(k)
        tab_sends.append(wires.send(tab_ref.at[row], tabs_ref.at[k - 1], peer))
    mix = dot_tn(
        ctx_ref[...].reshape(full_len, group), attn_ref[...].reshape(full_len, width)
    )
    for row in range(at.batches):
        mix_ref[row] = mix[:, row * columns : (row + 1) * columns].astype(low)
    for k in range(1, at.batches):
        row, peer = at.along_rows(k)
        mix_sends.append(wires.send(mix_ref.at[row], mixs_ref.at[k - 1], peer))

    total = dw_ref[b].astype(wide)
    for k in range(1, at.batches):
        dw_sends[k - 1].wait_recv()
        total = total + dws_ref[k - 1].astype(wide)
    shard_rows = dw_low_ref.shape[1]
    for half in range(2):
        dw_low_ref[half] = total[half * shard_rows : (half + 1) * shard_rows].astype(low)
    k = wires.used[0]
    wires.used[0] += 1
    move = pltpu.make_async_remote_copy(
        src_ref=dw_low_ref.at[c],
        dst_ref=dw_all_ref.at[c],
        send_sem=sems[0].at[k],
        recv_sem=sems[1].at[k],
        device_id=same,
        device_id_type=MESH,
    )
    stay = pltpu.make_async_copy(
        dw_low_ref.at[c], dw_all_ref.at[c], sems[2].at[wires.used[1]]
    )
    wires.used[1] += 1

    @pl.when(off_diagonal)
    def _():
        move.start()

    @pl.when(jnp.logical_not(off_diagonal))
    def _():
        stay.start()

    last.append(wires.send(dw_low_ref.at[1 - c], dw_all_ref.at[c], cross))

    total = tab_ref[b].astype(wide)
    for k in range(1, at.batches):
        tab_sends[k - 1].wait_recv()
        total = total + tabs_ref[k - 1].astype(wide)
    table_rows = tab_low_ref.shape[1]
    for part in range(at.tokens):
        tab_low_ref[part] = total[part * table_rows : (part + 1) * table_rows].astype(low)
    for k in range(1, at.tokens):
        part, peer = at.along_seq(k)
        last.append(wires.send(tab_low_ref.at[part], tab_all_ref.at[s], peer))
    own.append(wires.local(tab_low_ref.at[s], tab_all_ref.at[s]))

    total = mix_ref[b].astype(wide)
    for k in range(1, at.batches):
        mix_sends[k - 1].wait_recv()
        total = total + mixs_ref[k - 1].astype(wide)
    mix_low_ref[...] = total.astype(low)
    last.append(wires.send(mix_low_ref, mix_all_ref.at[c], at.partner()))
    own.append(wires.local(mix_low_ref, mix_all_ref.at[c]))

    total = vec_ref[s]
    for k in range(1, at.tokens):
        vec_sends[k - 1].wait_recv()
        total = total + vecs_ref[k - 1]
    vec_low_ref[...] = total
    for k in range(1, at.batches):
        last.append(wires.send(vec_low_ref, vec_all_ref.at[b], at.along_rows(k)[1]))
    own.append(wires.local(vec_low_ref, vec_all_ref.at[b]))

    for copy in last:
        copy.wait_recv()
    for copy in own:
        copy.wait()
    wires.finish()

    @pl.when(off_diagonal)
    def _():
        move.wait()

    @pl.when(jnp.logical_not(off_diagonal))
    def _():
        stay.wait()


def settle_grads(vec, cols, dcat, rel, w_cat, xs, table, ctx, attn_all, ident):
    tokens, batches = lax.axis_size("seq"), lax.axis_size("batch")
    chips = tokens // 2
    low, wide = jnp.bfloat16, jnp.float32
    local_len, width = xs.shape[1:]
    columns, group = width // batches, dcat.shape[1]
    buckets = table.shape[0]
    half = (chips, local_len, width)
    dw_pieces = (2, columns // 2, group)
    tab_pieces = (tokens, buckets // tokens, columns)
    mix_piece = (2 * DH, columns)
    dw_piece, tab_piece = (columns, group), (buckets, columns)
    outs = (
        jax.ShapeDtypeStruct(half, low),
        jax.ShapeDtypeStruct((batches,) + vec.shape[1:], wide),
        like(cols, 2 * batches),
        jax.ShapeDtypeStruct(dw_pieces, low),
        jax.ShapeDtypeStruct(tab_pieces, low),
        jax.ShapeDtypeStruct((2,) + mix_piece, low),
    )
    scratch = (
        pltpu.VMEM((chips, 2, local_len, width), low),
        pltpu.VMEM((batches,) + dw_piece, low),
        pltpu.VMEM((batches,) + tab_piece, low),
        pltpu.VMEM((batches,) + mix_piece, low),
        pltpu.VMEM(half, low),
        pltpu.VMEM(half, low),
        pltpu.VMEM((tokens - 1,) + vec.shape[1:], wide),
        pltpu.VMEM(vec.shape[1:], wide),
        pltpu.VMEM((batches - 1,) + dw_piece, low),
        pltpu.VMEM(dw_pieces, low),
        pltpu.VMEM((batches - 1,) + tab_piece, low),
        pltpu.VMEM(tab_pieces, low),
        pltpu.VMEM((batches - 1,) + mix_piece, low),
        pltpu.VMEM(mix_piece, low),
    )
    sends = (
        3 * (batches - 1) + chips + tokens - 1 + 2 * batches - 1
        + 2 + chips - 1 + tokens - 1 + 1 + batches - 1
    )
    inputs = (vec, cols, dcat, rel, w_cat, xs, table, ctx, attn_all)
    return comm_call(settle_kernel, "settle_grads", ident, outs, inputs, sends, 6, scratch=scratch)


def finish_kernel(
    pre_ref, ins_ref, vecs_ref, cols_ref, dws_ref, tabs_ref, mixs_ref, ups_ref, downs_ref,
    upbs_ref,
    input_ref, dq_ref, dk_ref, dv_ref, mix_ref, table_ref, bias_ref, gain_ref, shift_ref,
    up_ref, upb_ref, down_ref, downb_ref,
):
    at = Place()
    wide = jnp.float32

    def total(ref):
        out = ref[0].astype(wide)
        for k in range(1, ref.shape[0]):
            out = out + ref[k].astype(wide)
        return out

    input_ref[...] = pre_ref[...] + total(ins_ref)
    up_ref[...] = total(ups_ref)
    down_ref[...] = total(downs_ref)
    upb_ref[...] = total(upbs_ref)[0:1]
    table_ref[...] = total(tabs_ref)
    group = 2 * DH
    spare = jnp.zeros((dws_ref.shape[1], DH), wide)
    for i, ref in enumerate((dq_ref, dk_ref, dv_ref)):
        lower = dws_ref[0, :, i * group : (i + 1) * group].astype(wide)
        upper = dws_ref[1, :, i * group : (i + 1) * group].astype(wide)
        ref[...] = jnp.concatenate([lower, spare], axis=1) + jnp.concatenate(
            [spare, upper], axis=1
        )
    rows = mix_ref.shape[0]
    lower, upper = mixs_ref[0].astype(wide), mixs_ref[1].astype(wide)
    spare = jnp.zeros((DH, lower.shape[1]), wide)
    whole = jnp.concatenate([lower, spare], axis=0) + jnp.concatenate([spare, upper], axis=0)
    mix_ref[...] = jnp.where(at.core == 0, whole[:rows], whole[rows:])
    small = total(vecs_ref)
    lanes = bias_ref.shape[1]
    cols = [cols_ref[core, 0:1] for core in range(2)]
    for row in range(1, at.batches):
        cols = [cols[core] + cols_ref[2 * row + core, 0:1] for core in range(2)]
    spare = jnp.zeros((1, DH), wide)
    biases = []
    for i in range(3):
        lower, upper = [part[:, i * group : (i + 1) * group] for part in cols]
        both = jnp.concatenate([lower, spare], axis=1) + jnp.concatenate([spare, upper], axis=1)
        biases.append(jnp.where(at.core == 0, both[:, :lanes], both[:, lanes:]))
    bias_ref[...] = jnp.concatenate(biases + [small[0:1, :lanes]], axis=0)
    gain_ref[...] = small[1:3, :lanes]
    shift_ref[...] = small[3:5, :lanes]
    downb_ref[...] = small[5:6, :lanes]


def finish(pre_grad, parts, shapes):
    inputs = (pre_grad,) + tuple(parts)
    return pl.pallas_call(
        finish_kernel,
        out_shape=tuple(jax.ShapeDtypeStruct(shape, jnp.float32) for shape in shapes),
        in_specs=[VMEM_SPEC] * len(inputs),
        out_specs=(VMEM_SPEC,) * len(shapes),
        compiler_params=pltpu.CompilerParams(vmem_limit_bytes=COMM_VMEM),
        name="finish",
    )(*inputs)


def fits_fast(layer_input, table_shard, hidden_here):
    rows, local_len, width = layer_input.shape
    tokens, batches = lax.axis_size("seq"), lax.axis_size("batch")
    return (
        rows == 1
        and local_len == BLOCK
        and tokens == 2 * batches
        and width == 3 * DH * batches
        and (table_shard.shape[0] * tokens) % (4 * BLOCK) == 0
        and tokens == 8
        and 10 + hidden_here // BLOCK <= 16
        and hidden_here % BLOCK == 0
    )


def fast_body(
    layer_input, segment_ids, w_query, w_key, w_value, w_mix, rel_table, attn_biases,
    norm_gains, norm_shifts, w_up, up_bias, w_down, down_bias, out_grad,
):
    local_len, width = layer_input.shape[1:]
    low = jnp.bfloat16
    shard_rows, shard_cols = w_query.shape
    lanes = attn_biases.shape[1]
    hidden_here = w_up.shape[1]
    x = layer_input[0]
    pack = jnp.concatenate([attn_biases, norm_gains, norm_shifts, down_bias[None]], axis=0)
    pack = jnp.pad(pack, ((0, 0), (0, BLOCK - lanes)))
    pack = jnp.concatenate(
        [pack, segment_ids.astype(low), up_bias.reshape(hidden_here // BLOCK, BLOCK)], axis=0
    )
    pack = jnp.pad(pack, ((0, 16 - pack.shape[0]), (0, 0)))
    xs, qkvs, mixs, tables, vecs, up2, down2 = gather_inputs(
        x, w_query, w_key, w_value, w_mix, rel_table, pack, w_up, w_down
    )
    q, k, v, qrev, krev, probs, ctx, w_cat, table = attend(xs, qkvs, tables, vecs)
    output, pre_grad, sums, attn_all, m_mix, ups, downs, upbs = feed_forward(
        ctx, x, mixs, vecs, w_up, w_down, up2, down2, out_grad[0], 1
    )
    dcat, rel_grad, cols = attend_back(q, k, v, qrev, krev, probs, m_mix, attn_all)
    ins, vec_all, cols_all, dw_all, tab_all, mix_all = settle_grads(
        sums, cols, dcat, rel_grad, w_cat, xs, table, ctx, attn_all, 2
    )
    shard = (shard_rows, shard_cols)
    shapes = (
        x.shape, shard, shard, shard, shard, rel_table.shape, (4, lanes), (2, lanes), (2, lanes),
        (width // lax.axis_size("batch"), hidden_here), (1, hidden_here),
        (hidden_here, width // lax.axis_size("batch")), (1, lanes),
    )
    grads = finish(
        pre_grad,
        (ins, vec_all, cols_all, dw_all, tab_all, mix_all, ups, downs, upbs),
        shapes,
    )
    input_grad, dq, dk, dv, dmix, dtable, dbias, dgain, dshift, dup, dupb, ddown, ddownb = grads
    return (
        output[None], input_grad[None], dq, dk, dv, dmix, dtable, dbias, dgain, dshift,
        dup, dupb[0], ddown, ddownb[0],
    )


def body(
    layer_input,
    segment_ids,
    w_query,
    w_key,
    w_value,
    w_mix,
    rel_table,
    attn_biases,
    norm_gains,
    norm_shifts,
    w_up,
    up_bias,
    w_down,
    down_bias,
    out_grad,
):
    if fits_fast(layer_input, rel_table, w_up.shape[1]):
        return fast_body(
            layer_input, segment_ids, w_query, w_key, w_value, w_mix, rel_table, attn_biases,
            norm_gains, norm_shifts, w_up, up_bias, w_down, down_bias, out_grad,
        )
    rows, local_len, width = layer_input.shape
    full_len = local_len * lax.axis_size("seq")
    tokens_here = local_len * rows
    highest_prec = lax.Precision.HIGHEST
    parts = (
        lax.all_gather(w_query, "batch", axis=1, tiled=True),
        lax.all_gather(w_key, "batch", axis=1, tiled=True),
        lax.all_gather(w_value, "batch", axis=1, tiled=True),
        lax.all_gather(w_mix, "batch", axis=1, tiled=True),
        lax.all_gather(rel_table, "batch", axis=1, tiled=True),
    )
    whole = (
        lax.all_gather(parts[0], "seq", axis=0, tiled=True),
        lax.all_gather(parts[1], "seq", axis=0, tiled=True),
        lax.all_gather(parts[2], "seq", axis=0, tiled=True),
        lax.all_gather(parts[3], "seq", axis=0, tiled=True),
        lax.all_gather(parts[4], "seq", axis=0, tiled=True),
        lax.all_gather(attn_biases, "seq", axis=1, tiled=True),
        lax.all_gather(norm_gains, "seq", axis=1, tiled=True),
        lax.all_gather(norm_shifts, "seq", axis=1, tiled=True),
        lax.all_gather(down_bias, "seq", axis=0, tiled=True),
    )
    m_query, m_key, m_value, m_mix, table, biases, gains, shifts, bias_down = whole
    flat_input = jnp.swapaxes(layer_input, 0, 1).reshape(tokens_here, width)
    queries = (jnp.dot(flat_input, m_query, preferred_element_type=jnp.float32) + biases[0]).astype(
        jnp.bfloat16
    )
    keys_here = (jnp.dot(flat_input, m_key, preferred_element_type=jnp.float32) + biases[1]).astype(
        jnp.bfloat16
    )
    values_here = (
        jnp.dot(flat_input, m_value, preferred_element_type=jnp.float32) + biases[2]
    ).astype(jnp.bfloat16)
    query_rel = (jnp.dot(table, m_query, preferred_element_type=jnp.float32) + biases[0]).astype(
        jnp.bfloat16
    )
    key_rel = (jnp.dot(table, m_key, preferred_element_type=jnp.float32) + biases[1]).astype(
        jnp.bfloat16
    )
    local_seg = jnp.swapaxes(segment_ids, 0, 1).astype(jnp.bfloat16)
    keys_all, values_all, seg_all = (
        lax.all_gather(keys_here.reshape(local_len, rows, width), "seq", axis=0, tiled=True),
        lax.all_gather(values_here.reshape(local_len, rows, width), "seq", axis=0, tiled=True),
        lax.all_gather(local_seg, "seq", axis=0, tiled=True),
    )
    buckets = table.shape[0]
    offset = lax.axis_index("seq") * local_len
    bucket_iota = jnp.arange(buckets, dtype=jnp.int32)
    inner_cols = (bucket_iota > 0) & (bucket_iota < buckets - 1)
    same_doc = (
        jnp.swapaxes(local_seg, 0, 1)[:, None, :, None]
        == jnp.swapaxes(seg_all, 0, 1)[:, None, None, :]
    )
    score_scale = 1.0 / math.sqrt(3.0 * DH)
    head_queries = split_heads(queries.reshape(local_len, rows, width))
    head_keys = split_heads(keys_all)
    head_values = split_heads(values_all)
    rel_queries = split_table(query_rel)
    rel_keys = split_table(key_rel)

    def forward_group(carry, group):
        g_query, g_key, g_value, g_qrel, g_krel = group
        total, near_pull, far_pull, window = relative_scores(
            g_query, g_key, g_krel, g_qrel, offset, full_len
        )
        scores = jnp.where(same_doc, total * score_scale, masked_score)
        highest = jnp.max(scores, axis=-1, keepdims=True)
        exponent = jnp.exp(scores - highest)
        denominator = jnp.sum(exponent, axis=-1, keepdims=True)
        weights_low = (exponent / denominator).astype(jnp.bfloat16)
        context = jnp.einsum(
            "rgij,rgjd->rgid", weights_low, g_value, preferred_element_type=jnp.float32
        )
        return (carry, (context, (highest + jnp.log(denominator))[..., 0]))

    unused, (context_groups, log_totals) = lax.scan(
        forward_group, None, (head_queries, head_keys, head_values, rel_queries, rel_keys)
    )
    context_low = join_heads(context_groups).reshape(tokens_here, width).astype(jnp.bfloat16)
    pre_norm = (
        flat_input.astype(jnp.float32)
        + jnp.dot(context_low, m_mix, preferred_element_type=jnp.float32)
        + biases[3]
    )
    hidden, norm1_pull = jax.vjp(
        normalize, pre_norm, gains[0].astype(jnp.float32), shifts[0].astype(jnp.float32)
    )
    hidden_low = hidden.astype(jnp.bfloat16)

    def spread_rows(rows_low):
        return lax.all_gather(rows_low, "seq", axis=0, tiled=True)

    def hidden_sums(make_term):
        return lax.psum_scatter(
            make_term(jnp.int32(0), tokens_here * lax.axis_size("seq")),
            "seq",
            scatter_dimension=0,
            tiled=True,
        )

    hidden_rows = spread_rows(hidden_low)
    inner = jnp.dot(hidden_rows, w_up, preferred_element_type=jnp.float32) + up_bias
    act, gelu_pull = jax.vjp(exact_gelu, inner)
    act_low = act.astype(jnp.bfloat16)

    def down_rows(start, count):
        return jnp.dot(act_low, w_down, preferred_element_type=jnp.float32)

    ffn_result = hidden_sums(down_rows)
    mixed = hidden + ffn_result + bias_down
    output, norm2_pull = jax.vjp(
        normalize, mixed, gains[1].astype(jnp.float32), shifts[1].astype(jnp.float32)
    )
    flat_grad = jnp.swapaxes(out_grad, 0, 1).reshape(tokens_here, width).astype(jnp.float32)
    mixed_grad, gain2_grad, shift2_grad = norm2_pull(flat_grad)
    ffn_grad_low = mixed_grad.astype(jnp.bfloat16)
    grad_rows = spread_rows(ffn_grad_low)
    act_grad = jnp.einsum("nd,fd->nf", grad_rows, w_down, preferred_element_type=jnp.float32)
    inner_low = gelu_pull(act_grad)[0].astype(jnp.bfloat16)
    up_part = jnp.einsum("nd,nf->df", hidden_rows, inner_low, preferred_element_type=jnp.float32)
    upb_part = jnp.sum(inner_low.astype(jnp.float32), axis=0)
    down_part = jnp.einsum("nf,nd->fd", act_low, grad_rows, preferred_element_type=jnp.float32)

    def back_rows(start, count):
        return jnp.einsum("nf,df->nd", inner_low, w_up, preferred_element_type=jnp.float32)

    hidden_grad = mixed_grad + hidden_sums(back_rows)
    pre_grad, gain1_grad, shift1_grad = norm1_pull(hidden_grad)
    attn_low = pre_grad.astype(jnp.bfloat16)
    mix_whole = jnp.einsum("nd,ne->de", context_low, attn_low, preferred_element_type=jnp.float32)
    context_grad = jnp.einsum(
        "ne,de->nd", attn_low, m_mix, preferred_element_type=jnp.float32
    ).astype(jnp.bfloat16)
    head_context_grad = split_heads(context_grad.reshape(local_len, rows, width))

    def query_side(group):
        g_query, g_key, g_value, g_qrel, g_krel, g_dctx, g_lse = group
        total, near_pull, far_pull, window = relative_scores(
            g_query, g_key, g_krel, g_qrel, offset, full_len
        )
        scores = jnp.where(same_doc, total * score_scale, masked_score)
        weights_now = jnp.exp(scores - g_lse[..., None])
        prob_grad = jnp.einsum(
            "rgid,rgjd->rgij", g_dctx, g_value, preferred_element_type=jnp.float32
        )
        inner_sum = jnp.sum(weights_now * prob_grad, axis=-1)
        score_grad = (weights_now * (prob_grad - inner_sum[..., None])).astype(jnp.bfloat16)
        grad_wide = score_grad.astype(jnp.float32)
        near_grad = near_pull(grad_wide)[0]
        near_low = jnp.where(inner_cols, near_grad, 0.0).astype(jnp.bfloat16)
        near_ends = end_columns(near_grad)
        query_part = jnp.einsum(
            "rgij,rgjd->rgid", score_grad, g_key, preferred_element_type=jnp.float32
        )
        query_part = (
            query_part
            + jnp.einsum("rgib,gbd->rgid", near_low, g_krel, preferred_element_type=jnp.float32)
            + end_terms(near_ends, g_krel)
        )
        krel_part = with_ends(
            jnp.einsum("rgib,rgid->gbd", near_low, g_query, preferred_element_type=jnp.float32),
            end_rows(near_ends, g_query),
        )
        return (
            weights_now,
            score_grad,
            grad_wide,
            far_pull,
            window,
            inner_sum,
            query_part * score_scale,
            krel_part * score_scale,
        )

    query_groups = (
        head_queries,
        head_keys,
        head_values,
        rel_queries,
        rel_keys,
        head_context_grad,
        log_totals,
    )

    def all_grads(carry, group):
        weights_now, score_grad, grad_wide, far_pull, window, inner_sum, query_part, krel_part = (
            query_side(group)
        )
        g_query, g_key, g_value, g_qrel, g_krel, g_dctx, g_lse = group
        cross_grad, end_grad = far_pull(grad_wide)
        cross_low = cross_grad.astype(jnp.bfloat16)
        key_part = jnp.einsum(
            "rgij,rgid->rgjd", score_grad, g_query, preferred_element_type=jnp.float32
        )
        band_part = jnp.einsum(
            "rgmb,gbd->rgmd", cross_low, g_qrel, preferred_element_type=jnp.float32
        )
        key_part = (
            key_part
            + unband(band_part, offset, full_len, buckets // 2)
            + end_terms(end_grad, g_qrel)
        )
        value_part = jnp.einsum(
            "rgij,rgid->rgjd",
            weights_now.astype(jnp.bfloat16),
            g_dctx,
            preferred_element_type=jnp.float32,
        )
        qrel_part = with_ends(
            jnp.einsum("rgmb,rgmd->gbd", cross_low, window, preferred_element_type=jnp.float32),
            end_rows(end_grad, g_key),
        )
        return (
            carry,
            (query_part, key_part * score_scale, value_part, qrel_part * score_scale, krel_part),
        )

    unused, (dq_groups, dk_groups, dv_groups, dqrel_groups, dkrel_groups) = lax.scan(
        all_grads, None, query_groups
    )
    key_sum, value_sum = (
        lax.psum_scatter(join_heads(dk_groups), "seq", scatter_dimension=0, tiled=True),
        lax.psum_scatter(join_heads(dv_groups), "seq", scatter_dimension=0, tiled=True),
    )
    key_grads = key_sum.reshape(tokens_here, width).astype(jnp.bfloat16)
    value_grads = value_sum.reshape(tokens_here, width).astype(jnp.bfloat16)
    query_grads = join_heads(dq_groups).reshape(tokens_here, width).astype(jnp.bfloat16)
    qrel_grad = join_table(dqrel_groups)
    krel_grad = join_table(dkrel_groups)
    input_grad = pre_grad + jnp.einsum(
        "ne,de->nd", query_grads, m_query, preferred_element_type=jnp.float32
    )
    input_grad = input_grad + jnp.einsum(
        "ne,de->nd", key_grads, m_key, preferred_element_type=jnp.float32
    )
    input_grad = input_grad + jnp.einsum(
        "ne,de->nd", value_grads, m_value, preferred_element_type=jnp.float32
    )
    query_whole = jnp.einsum(
        "nd,ne->de", flat_input, query_grads, preferred_element_type=jnp.float32
    ) + jnp.einsum(
        "bd,be->de", table, qrel_grad, precision=highest_prec, preferred_element_type=jnp.float32
    )
    key_whole = jnp.einsum(
        "nd,ne->de", flat_input, key_grads, preferred_element_type=jnp.float32
    ) + jnp.einsum(
        "bd,be->de", table, krel_grad, precision=highest_prec, preferred_element_type=jnp.float32
    )
    value_whole = jnp.einsum(
        "nd,ne->de", flat_input, value_grads, preferred_element_type=jnp.float32
    )
    table_whole = jnp.einsum(
        "be,de->bd", qrel_grad, m_query, precision=highest_prec, preferred_element_type=jnp.float32
    ) + jnp.einsum(
        "be,de->bd", krel_grad, m_key, precision=highest_prec, preferred_element_type=jnp.float32
    )
    bias_whole = jnp.stack(
        [
            jnp.sum(query_grads.astype(jnp.float32), axis=0) + jnp.sum(qrel_grad, axis=0),
            jnp.sum(key_grads.astype(jnp.float32), axis=0) + jnp.sum(krel_grad, axis=0),
            jnp.sum(value_grads.astype(jnp.float32), axis=0),
            jnp.sum(pre_grad, axis=0),
        ]
    )
    gain_whole = jnp.stack([gain1_grad, gain2_grad])
    shift_whole = jnp.stack([shift1_grad, shift2_grad])
    downb_whole = jnp.sum(mixed_grad, axis=0)
    seq_parts = (
        lax.psum_scatter(query_whole, "seq", scatter_dimension=0, tiled=True),
        lax.psum_scatter(key_whole, "seq", scatter_dimension=0, tiled=True),
        lax.psum_scatter(value_whole, "seq", scatter_dimension=0, tiled=True),
        lax.psum_scatter(mix_whole, "seq", scatter_dimension=0, tiled=True),
        lax.psum_scatter(table_whole, "seq", scatter_dimension=0, tiled=True),
        lax.psum_scatter(bias_whole, "seq", scatter_dimension=1, tiled=True),
        lax.psum_scatter(gain_whole, "seq", scatter_dimension=1, tiled=True),
        lax.psum_scatter(shift_whole, "seq", scatter_dimension=1, tiled=True),
        lax.psum_scatter(downb_whole, "seq", scatter_dimension=0, tiled=True),
    )
    batch_parts = (
        lax.psum_scatter(seq_parts[0], "batch", scatter_dimension=1, tiled=True),
        lax.psum_scatter(seq_parts[1], "batch", scatter_dimension=1, tiled=True),
        lax.psum_scatter(seq_parts[2], "batch", scatter_dimension=1, tiled=True),
        lax.psum_scatter(seq_parts[3], "batch", scatter_dimension=1, tiled=True),
        lax.psum_scatter(seq_parts[4], "batch", scatter_dimension=1, tiled=True),
        lax.psum_scatter(up_part, "batch", scatter_dimension=0, tiled=True),
        lax.psum_scatter(down_part, "batch", scatter_dimension=1, tiled=True),
    )
    small_parts = lax.psum(
        (seq_parts[5], seq_parts[6], seq_parts[7], seq_parts[8], upb_part), "batch"
    )
    layer_output = jnp.swapaxes(output.reshape(local_len, rows, width), 0, 1).astype(jnp.bfloat16)
    input_back = jnp.swapaxes(input_grad.reshape(local_len, rows, width), 0, 1)
    return (
        layer_output,
        input_back,
        batch_parts[0],
        batch_parts[1],
        batch_parts[2],
        batch_parts[3],
        batch_parts[4],
        small_parts[0],
        small_parts[1],
        small_parts[2],
        batch_parts[5],
        small_parts[4],
        batch_parts[6],
        small_parts[3],
    )


def solution(mesh):
    return jax.shard_map(
        body,
        mesh=mesh,
        in_specs=(
            P("batch", "seq", None),
            P("batch", "seq"),
            P("seq", "batch"),
            P("seq", "batch"),
            P("seq", "batch"),
            P("seq", "batch"),
            P("seq", "batch"),
            P(None, "seq"),
            P(None, "seq"),
            P(None, "seq"),
            P(None, "seq"),
            P("seq"),
            P("seq", None),
            P("seq"),
            P("batch", "seq", None),
        ),
        out_specs=(
            P("batch", "seq", None),
            P("batch", "seq", None),
            P("seq", "batch"),
            P("seq", "batch"),
            P("seq", "batch"),
            P("seq", "batch"),
            P("seq", "batch"),
            P(None, "seq"),
            P(None, "seq"),
            P(None, "seq"),
            P("batch", "seq"),
            P("seq"),
            P("seq", "batch"),
            P("seq"),
        ),
        check_vma=False,
    )
```

```python
import math

import jax
import jax.numpy as jnp
from jax import lax
from jax.experimental import pallas as pl
from jax.experimental.pallas import tpu as pltpu
from jax.sharding import PartitionSpec as P

DH = 64


masked_score = -1e30
norm_eps = 1e-06
pair_heads = 2


def normalize(values, gain, shift):
    average = jnp.mean(values, axis=-1, keepdims=True)
    centered = values - average
    variance = jnp.mean(centered * centered, axis=-1, keepdims=True)
    return centered * lax.rsqrt(variance + norm_eps) * gain + shift


def exact_gelu(values):
    return jax.nn.gelu(values, approximate=False)


def split_heads(matrix):
    length, rows, width = matrix.shape
    groups = width // (pair_heads * DH)
    return matrix.reshape(length, rows, groups, pair_heads, DH).transpose(2, 1, 3, 0, 4)


def join_heads(matrix):
    groups, rows, pair, length, depth = matrix.shape
    return matrix.transpose(3, 1, 0, 2, 4).reshape(length, rows, groups * pair * depth)


def split_table(matrix):
    buckets, width = matrix.shape
    return matrix.reshape(buckets, width // (pair_heads * DH), pair_heads, DH).transpose(1, 2, 0, 3)


def join_table(matrix):
    groups, pair, buckets, depth = matrix.shape
    return matrix.transpose(2, 0, 1, 3).reshape(buckets, groups * pair * depth)


def table_ends(table):
    return jnp.stack([table[:, 0], table[:, -1]], axis=1)


def near_skew(table_prod, offset, full_len):
    lead = table_prod.shape[:-2]
    count, buckets = table_prod.shape[-2:]
    span = buckets // 2
    lead_pad = [(0, 0)] * len(lead)
    flipped = jnp.pad(table_prod[..., ::-1], lead_pad + [(0, 0), (0, count)])
    sheared = flipped.reshape(lead + (count * (buckets + count),))[
        ..., : count * (buckets + count - 1)
    ]
    sheared = sheared.reshape(lead + (count, buckets + count - 1))
    spread = jnp.pad(sheared, lead_pad + [(0, 0), (full_len, full_len)])
    band = lax.dynamic_slice_in_dim(
        spread, full_len + span - 1 - offset, full_len, axis=len(lead) + 1
    )
    distance = (offset + jnp.arange(count, dtype=jnp.int32))[:, None] - jnp.arange(
        full_len, dtype=jnp.int32
    )[None, :]
    return jnp.where(
        distance <= -span,
        table_prod[..., 0:1],
        jnp.where(distance >= span - 1, table_prod[..., buckets - 1 :], band),
    )


def far_place(cross, end_vals, offset, count, full_len):
    lead = cross.shape[:-2]
    band_len, buckets = cross.shape[-2:]
    span = buckets // 2
    lead_pad = [(0, 0)] * len(lead)
    turned = jnp.swapaxes(cross, -1, -2).reshape(lead + (buckets * band_len,))
    turned = jnp.pad(turned, lead_pad + [(0, buckets)])
    diagonal = turned.reshape(lead + (buckets, band_len + 1))[..., :count]
    aligned = jnp.pad(jnp.swapaxes(diagonal, -1, -2), lead_pad + [(0, 0), (0, count)])
    sheared = aligned.reshape(lead + (count * (buckets + count),))[
        ..., : count * (buckets + count - 1)
    ]
    sheared = sheared.reshape(lead + (count, buckets + count - 1))
    spread = jnp.pad(sheared, lead_pad + [(0, 0), (full_len, full_len)])
    band = lax.dynamic_slice_in_dim(spread, full_len + span - offset, full_len, axis=len(lead) + 1)
    distance = (
        jnp.arange(full_len, dtype=jnp.int32)[None, :]
        - (offset + jnp.arange(count, dtype=jnp.int32))[:, None]
    )
    return jnp.where(
        distance <= -span,
        end_vals[..., 0:1, :],
        jnp.where(distance >= span - 1, end_vals[..., 1:2, :], band),
    )


def band_rows(all_rows, offset, count, span):
    padded = jnp.pad(all_rows, [(0, 0), (0, 0), (span, span), (0, 0)])
    return lax.dynamic_slice_in_dim(padded, offset, count + 2 * span - 1, axis=2)


def unband(values, offset, full_len, span):
    lead = values.shape[:2]
    room = jnp.zeros(lead + (full_len + 2 * span, values.shape[3]), jnp.float32)
    placed = lax.dynamic_update_slice_in_dim(room, values, offset, axis=2)
    return placed[:, :, span : span + full_len]


def relative_scores(own_rows, all_rows, own_table, all_table, offset, full_len):
    count = own_rows.shape[2]
    content = jnp.einsum("rgid,rgjd->rgij", own_rows, all_rows, preferred_element_type=jnp.float32)
    own_prod = jnp.einsum("rgid,gbd->rgib", own_rows, own_table, preferred_element_type=jnp.float32)
    window = band_rows(all_rows, offset, count, all_table.shape[1] // 2)
    cross = jnp.einsum("rgmd,gbd->rgmb", window, all_table, preferred_element_type=jnp.float32)
    end_vals = jnp.einsum(
        "rgjd,ged->rgej", all_rows, table_ends(all_table), preferred_element_type=jnp.float32
    )
    near_vals, near_pull = jax.vjp(lambda product: near_skew(product, offset, full_len), own_prod)
    far_vals, far_pull = jax.vjp(
        lambda part, ends: far_place(part, ends, offset, count, full_len), cross, end_vals
    )
    return (content + near_vals + far_vals, near_pull, far_pull, window)


def end_columns(grad):
    return jnp.stack([grad[..., 0], grad[..., -1]], axis=2)


def end_terms(ends, table):
    return jnp.einsum(
        "rgei,ged->rgid",
        ends,
        table_ends(table),
        precision=lax.Precision.HIGHEST,
        preferred_element_type=jnp.float32,
    )


def end_rows(ends, rows_low):
    return jnp.einsum(
        "rgei,rgid->ged",
        ends,
        rows_low,
        precision=lax.Precision.HIGHEST,
        preferred_element_type=jnp.float32,
    )


def with_ends(inner_part, edge_rows):
    buckets = inner_part.shape[1]
    place = jnp.arange(buckets, dtype=jnp.int32)[None, :, None]
    return (
        inner_part
        + jnp.where(place == 0, edge_rows[:, 0:1], 0.0)
        + jnp.where(place == buckets - 1, edge_rows[:, 1:2], 0.0)
    )


BLOCK = 128
MIB = 1024 * 1024
ATTEND_VMEM = 26 * MIB
BACK_VMEM = 26 * MIB
FEED_VMEM = 26 * MIB
COMM_VMEM = 16 * MIB


def dot_nn(a, b):
    return lax.dot_general(a, b, (((1,), (0,)), ((), ())), preferred_element_type=jnp.float32)


def dot_nt(a, b):
    return lax.dot_general(a, b, (((1,), (1,)), ((), ())), preferred_element_type=jnp.float32)


def dot_tn(a, b):
    return lax.dot_general(a, b, (((0,), (0,)), ((), ())), preferred_element_type=jnp.float32)


def turn_matrix(buckets):
    row = lax.broadcasted_iota(jnp.int32, (buckets, buckets), 0)
    col = lax.broadcasted_iota(jnp.int32, (buckets, buckets), 1)
    return (row + col == buckets - 1).astype(jnp.bfloat16)


def skew_band(product):
    count, buckets = product.shape
    row = lax.broadcasted_iota(jnp.int32, (count, BLOCK), 0)
    lane = lax.broadcasted_iota(jnp.int32, (count, BLOCK), 1)
    edge = jnp.where(row + lane <= BLOCK - 2, product[:, buckets - 1 :], product[:, 0:1])
    wide = jnp.concatenate([product, edge], axis=1)
    return pltpu.roll(wide, 1, 1, stride=1, stride_axis=0)


def skew_back(turned, buckets):
    return pltpu.roll(turned, turned.shape[1] - BLOCK, 1, stride=1, stride_axis=0)[:, :buckets]


def chip_columns(vec_ref, chip, index, core):
    width = 3 * DH // 2
    both = jnp.concatenate(
        [
            vec_ref[2 * chip, index : index + 1, :width].astype(jnp.float32),
            vec_ref[2 * chip + 1, index : index + 1, :width].astype(jnp.float32),
        ],
        axis=1,
    )
    return jnp.where(core == 0, both[:, : 2 * DH], both[:, DH:])


def attend_kernel(
    xs_ref,
    qkvs_ref,
    tables_ref,
    vecs_ref,
    q_ref,
    k_ref,
    v_ref,
    qrev_ref,
    krev_ref,
    p_ref,
    ctx_ref,
    w_ref,
    table_ref,
    segc_ref,
    place_ref,
    wide_ref,
    ends_ref,
    held_ref,
):
    at = Place()
    full_len = xs_ref.shape[0] * xs_ref.shape[1]
    buckets = table_ref.shape[0]
    blocks = full_len // BLOCK
    span = buckets // 2
    side = span // BLOCK
    band_width = buckets + BLOCK
    band_blocks = band_width // BLOCK
    group = 2 * DH
    scale = 1.0 / math.sqrt(3.0 * DH)
    units = p_ref.shape[0]
    shard_rows = qkvs_ref.shape[2]
    table_rows = tables_ref.shape[3]
    batches = tables_ref.shape[1]
    for part in range(at.tokens):
        pieces = []
        for i in range(3):
            piece = qkvs_ref[part, i]
            pieces.append(jnp.where(at.core == 0, piece[:, :group], piece[:, DH:]))
        w_ref[part * shard_rows : (part + 1) * shard_rows] = jnp.concatenate(pieces, axis=1)
        core, chip = part % 2, part // 2
        table_ref[part * table_rows : (part + 1) * table_rows] = jnp.concatenate(
            [tables_ref[core, row, chip] for row in range(batches)], axis=1
        )
        own_seg = vecs_ref[part, 9:10].astype(jnp.float32)
        segc_ref[part * BLOCK : (part + 1) * BLOCK] = jnp.broadcast_to(own_seg, (BLOCK, BLOCK)).T
    seg_row = jnp.concatenate(
        [vecs_ref[part, 9:10].astype(jnp.float32) for part in range(at.tokens)], axis=1
    )
    bias = jnp.concatenate(
        [chip_columns(vecs_ref, at.chip, i, at.core) for i in range(3)], axis=1
    )
    tokens_all = xs_ref[...].reshape(full_len, xs_ref.shape[2])
    proj = (dot_nn(tokens_all, w_ref[...]) + bias).astype(jnp.bfloat16)
    rel = (dot_nn(table_ref[...], w_ref[:, : 2 * group]) + bias[:, : 2 * group]).astype(
        jnp.bfloat16
    )
    rel = dot_nn(turn_matrix(buckets), rel).astype(jnp.bfloat16)
    for slot in range(2):
        lo, hi = slot * DH, (slot + 1) * DH
        q_ref[slot] = proj[:, lo:hi]
        k_ref[slot] = proj[:, group + lo : group + hi]
        v_ref[slot] = proj[:, 2 * group + lo : 2 * group + hi]
        qrev_ref[slot] = rel[:, lo:hi]
        krev_ref[slot] = rel[:, group + lo : group + hi]
    held_ref[...] = jnp.zeros_like(held_ref)
    for slot in range(2):
        ends_ref[slot, 0] = dot_nt(qrev_ref[slot, 0:16], k_ref[slot])
        ends_ref[slot, 1] = dot_nt(qrev_ref[slot, buckets - 16 : buckets], k_ref[slot])

        def key_block(kb, carry):
            rows = k_ref[slot, pl.ds(pl.multiple_of(kb * BLOCK, BLOCK), BLOCK)]
            band = skew_band(dot_nt(rows, qrev_ref[slot]))
            for e in range(band_blocks):
                place_ref[
                    slot,
                    kb + e,
                    :,
                    (band_blocks - 1 - e) * BLOCK : (band_blocks - e) * BLOCK,
                ] = band[:, e * BLOCK : (e + 1) * BLOCK].T
            return carry

        lax.fori_loop(0, blocks, key_block, 0)

    first = at.core * (blocks // 2)

    def unit(u, carry):
        g = u + first
        slot = g // blocks
        qb = g % blocks
        start = pl.multiple_of(qb * BLOCK, BLOCK)
        rows = q_ref[slot, pl.ds(start, BLOCK)]
        own = dot_nt(rows, krev_ref[slot])
        band = skew_band(own) + place_ref[slot, qb + side]
        wide_ref[:, pl.ds(start, band_width)] = band
        content = dot_nt(rows, k_ref[slot])
        lane = lax.broadcasted_iota(jnp.int32, (BLOCK, full_len), 1)
        near = jnp.where(
            lane < start - span,
            own[:, 0:1] + ends_ref[slot, 1, 15:16],
            jnp.where(
                lane >= start + band_width - span,
                own[:, buckets - 1 :] + ends_ref[slot, 0, 0:1],
                wide_ref[:, span : span + full_len],
            ),
        )
        same = segc_ref[pl.ds(start, BLOCK), 0:1] == seg_row
        scores = jnp.where(same, (content + near) * scale, masked_score)
        highest = jnp.max(scores, axis=-1, keepdims=True)
        exponent = jnp.exp(scores - highest)
        total = jnp.sum(exponent, axis=-1, keepdims=True)
        probs = (exponent / total).astype(jnp.bfloat16)
        p_ref[u] = probs
        held_ref[slot, pl.ds(start, BLOCK)] = dot_nn(probs, v_ref[slot]).astype(jnp.bfloat16)
        return carry

    lax.fori_loop(0, units, unit, 0)
    for part in range(at.tokens):
        rows = slice(part * BLOCK, (part + 1) * BLOCK)
        ctx_ref[part] = jnp.concatenate([held_ref[0, rows], held_ref[1, rows]], axis=1)


def attend(xs, qkvs, tables, vecs):
    tokens, local_len, width = xs.shape
    full_len = tokens * local_len
    buckets = tokens * tables.shape[3]
    blocks = full_len // BLOCK
    units = 3 * blocks // 2
    band_width = buckets + BLOCK
    low, wide = jnp.bfloat16, jnp.float32
    pad_blocks = blocks + band_width // BLOCK - 1
    return pl.pallas_call(
        attend_kernel,
        out_shape=(
            jax.ShapeDtypeStruct((2, full_len, DH), low),
            jax.ShapeDtypeStruct((2, full_len, DH), low),
            jax.ShapeDtypeStruct((2, full_len, DH), low),
            jax.ShapeDtypeStruct((2, buckets, DH), low),
            jax.ShapeDtypeStruct((2, buckets, DH), low),
            jax.ShapeDtypeStruct((units, BLOCK, full_len), low),
            jax.ShapeDtypeStruct((tokens, local_len, 2 * DH), low),
            jax.ShapeDtypeStruct((width, 6 * DH), low),
            jax.ShapeDtypeStruct((buckets, width), low),
        ),
        in_specs=[pl.BlockSpec(memory_space=pltpu.VMEM)] * 4,
        out_specs=[pl.BlockSpec(memory_space=pltpu.VMEM)] * 9,
        scratch_shapes=[
            pltpu.VMEM((full_len, BLOCK), wide),
            pltpu.VMEM((2, pad_blocks, BLOCK, band_width), wide),
            pltpu.VMEM((BLOCK, full_len + buckets), wide),
            pltpu.VMEM((2, 2, 16, full_len), wide),
            pltpu.VMEM((2, full_len, DH), low),
        ],
        compiler_params=pltpu.CompilerParams(vmem_limit_bytes=ATTEND_VMEM),
        name="attend",
    )(xs, qkvs, tables, vecs)


def attend_back_kernel(
    q_ref,
    k_ref,
    v_ref,
    qrev_ref,
    krev_ref,
    p_ref,
    mix_ref,
    attn_ref,
    dcat_ref,
    rel_ref,
    sum_ref,
    heads_ref,
    wide_ref,
    low_ref,
    place_ref,
    dq_ref,
    dkt_ref,
    dvt_ref,
    far_ref,
    dkr_ref,
    dqr_ref,
):
    full_len = q_ref.shape[1]
    buckets = qrev_ref.shape[1]
    blocks = full_len // BLOCK
    span = buckets // 2
    side = span // BLOCK
    band_width = buckets + BLOCK
    band_blocks = band_width // BLOCK
    scale = 1.0 / math.sqrt(3.0 * DH)
    units = p_ref.shape[0]
    for ref in (wide_ref, low_ref, place_ref, dq_ref, dkt_ref, dvt_ref, far_ref, dkr_ref, dqr_ref):
        ref[...] = jnp.zeros_like(ref)
    at = Place()
    group = 2 * DH
    first_row = pl.multiple_of((3 * at.chip + at.core) * DH, DH)
    mix_rows = mix_ref[pl.ds(first_row, group)]
    dctx = dot_nt(attn_ref[...].reshape(full_len, attn_ref.shape[2]), mix_rows)
    for slot in range(2):
        heads_ref[slot] = dctx[:, slot * DH : (slot + 1) * DH].astype(jnp.bfloat16)
    first = at.core * (blocks // 2)
    turn = turn_matrix(BLOCK)
    place8 = lax.broadcasted_iota(jnp.int32, (8, full_len), 0)

    def unit(u, carry):
        g = u + first
        slot = g // blocks
        qb = g % blocks
        start = pl.multiple_of(qb * BLOCK, BLOCK)
        rows = q_ref[slot, pl.ds(start, BLOCK)]
        grad = heads_ref[slot, pl.ds(start, BLOCK)]
        probs = p_ref[u]
        wide_probs = probs.astype(jnp.float32)
        prob_grad = dot_nt(grad, v_ref[slot])
        inner = jnp.sum(wide_probs * prob_grad, axis=-1, keepdims=True)
        low_grad = (wide_probs * (prob_grad - inner)).astype(jnp.bfloat16)
        score_grad = low_grad.astype(jnp.float32)
        wide_ref[:, span : span + full_len] = dot_nn(turn, low_grad)
        low_ref[:, span : span + full_len] = low_grad
        dvt_ref[slot] += dot_tn(grad, probs)
        dkt_ref[slot] += dot_tn(rows, low_grad)
        row = lax.broadcasted_iota(jnp.int32, (BLOCK, full_len), 0)
        lane = lax.broadcasted_iota(jnp.int32, (BLOCK, full_len), 1)
        gap = lane - row - start
        right = jnp.where(gap > span, score_grad, 0.0)
        left = jnp.where(gap < 1 - span, score_grad, 0.0)
        end_right = jnp.sum(right, axis=-1, keepdims=True)
        end_left = jnp.sum(left, axis=-1, keepdims=True)
        far_right = jnp.sum(jnp.where(gap >= span, score_grad, 0.0), axis=0, keepdims=True)
        far_left = jnp.sum(jnp.where(gap < -span, score_grad, 0.0), axis=0, keepdims=True)
        far_ref[slot] += jnp.where(place8 == 0, far_right, jnp.where(place8 == 1, far_left, 0.0))
        band = wide_ref[:, pl.ds(start, band_width)]
        near = dot_nn(turn, skew_back(band, buckets).astype(jnp.bfloat16))
        bucket = lax.broadcasted_iota(jnp.int32, (BLOCK, buckets), 1)
        near = near + jnp.where(
            bucket == 0, end_left, jnp.where(bucket == buckets - 1, end_right, 0.0)
        )
        near_low = near.astype(jnp.bfloat16)
        dq = dot_nn(low_grad, k_ref[slot]) + dot_nn(near_low, krev_ref[slot])
        dq_ref[slot, pl.ds(start, BLOCK)] = dq
        dkr_ref[slot] += dot_tn(rows, near_low)
        for e in range(band_blocks):
            keys_at = pl.multiple_of(start + e * BLOCK, BLOCK)
            place_ref[
                slot, qb + e, :, (band_blocks - 1 - e) * BLOCK : (band_blocks - e) * BLOCK
            ] = dot_nt(turn, low_ref[:, pl.ds(keys_at, BLOCK)])
        return carry

    lax.fori_loop(0, units, unit, 0)
    parts_q, parts_k, parts_v = [], [], []
    parts_r = [None] * 4
    for slot in range(2):
        far_low = far_ref[slot].astype(jnp.bfloat16)
        mark = lax.broadcasted_iota(jnp.int32, (8, DH), 0)
        ends = jnp.where(
            mark == 0,
            qrev_ref[slot, 0:1].astype(jnp.float32),
            jnp.where(mark == 1, qrev_ref[slot, buckets - 1 : buckets].astype(jnp.float32), 0.0),
        ).astype(jnp.bfloat16)
        end_keys = dot_tn(ends, far_low)
        end_rows = dot_nn(far_low, k_ref[slot])

        whole_k = (dkt_ref[slot] + end_keys).T

        def key_side(kb, carry):
            start = pl.multiple_of(kb * BLOCK, BLOCK)
            far = skew_back(place_ref[slot, kb + side], buckets).astype(jnp.bfloat16)
            far = dot_nn(turn, far).astype(jnp.bfloat16)
            keys = k_ref[slot, pl.ds(start, BLOCK)]
            dqr_ref[slot] += dot_tn(keys, far)
            dq_ref[2 + slot, pl.ds(start, BLOCK)] = dot_nn(far, qrev_ref[slot])
            return carry

        lax.fori_loop(0, blocks, key_side, 0)
        parts_q.append((dq_ref[slot] * scale).astype(jnp.bfloat16))
        parts_k.append(((dq_ref[2 + slot] + whole_k) * scale).astype(jnp.bfloat16))
        parts_v.append(dvt_ref[slot].T.astype(jnp.bfloat16))
        bucket = lax.broadcasted_iota(jnp.int32, (buckets, DH), 0)
        qr = dqr_ref[slot].T + jnp.where(
            bucket == 0, end_rows[0:1], jnp.where(bucket == buckets - 1, end_rows[1:2], 0.0)
        )
        dqr_out = qr * scale
        dkr_out = dkr_ref[slot].T * scale
        parts_r[slot] = dqr_out
        parts_r[2 + slot] = dkr_out
    dcat = jnp.concatenate(parts_q + parts_k + parts_v, axis=1)
    dcat_ref[...] = dcat
    rel = jnp.concatenate(parts_r, axis=1)
    rel_ref[...] = dot_nn(turn_matrix(buckets), rel.astype(jnp.bfloat16)).astype(jnp.bfloat16)
    rel_sum = jnp.sum(rel, axis=0, keepdims=True)
    rel_sum = jnp.concatenate([rel_sum, jnp.zeros((1, 2 * DH), jnp.float32)], axis=1)
    sums = jnp.sum(dcat.astype(jnp.float32), axis=0, keepdims=True) + rel_sum
    sum_ref[...] = jnp.broadcast_to(sums, sum_ref.shape)


def attend_back(q, k, v, qrev, krev, probs, m_mix, attn_all):
    full_len = q.shape[1]
    buckets = qrev.shape[1]
    blocks = full_len // BLOCK
    band_width = buckets + BLOCK
    low, wide = jnp.bfloat16, jnp.float32
    pad_blocks = blocks + band_width // BLOCK - 1
    return pl.pallas_call(
        attend_back_kernel,
        out_shape=(
            jax.ShapeDtypeStruct((full_len, 6 * DH), low),
            jax.ShapeDtypeStruct((buckets, 4 * DH), low),
            jax.ShapeDtypeStruct((8, 6 * DH), wide),
        ),
        in_specs=[pl.BlockSpec(memory_space=pltpu.VMEM)] * 8,
        out_specs=[pl.BlockSpec(memory_space=pltpu.VMEM)] * 3,
        scratch_shapes=[
            pltpu.VMEM((2, full_len, DH), low),
            pltpu.VMEM((BLOCK, full_len + buckets), wide),
            pltpu.VMEM((BLOCK, full_len + buckets), low),
            pltpu.VMEM((2, pad_blocks, BLOCK, band_width), wide),
            pltpu.VMEM((4, full_len, DH), wide),
            pltpu.VMEM((2, DH, full_len), wide),
            pltpu.VMEM((2, DH, full_len), wide),
            pltpu.VMEM((2, 8, full_len), wide),
            pltpu.VMEM((2, DH, buckets), wide),
            pltpu.VMEM((2, DH, buckets), wide),
        ],
        compiler_params=pltpu.CompilerParams(vmem_limit_bytes=BACK_VMEM),
        name="attend_back",
    )(q, k, v, qrev, krev, probs, m_mix, attn_all)


MESH = pl.DeviceIdType.MESH
VMEM_SPEC = pl.BlockSpec(memory_space=pltpu.VMEM)
HBM_SPEC = pl.BlockSpec(memory_space=pltpu.HBM)
CHUNKS = 2


class Place:
    def __init__(self):
        self.batches = lax.axis_size("batch")
        self.tokens = lax.axis_size("seq")
        self.chips = self.tokens // 2
        self.row = lax.axis_index("batch")
        self.part = lax.axis_index("seq")
        self.chip = self.part // 2
        self.core = self.part % 2

    def along_chips(self, k):
        chip = lax.rem(self.chip + k, self.chips)
        return chip, (self.row, 2 * chip + self.core)

    def from_chips(self, k):
        return lax.rem(self.chip + self.chips - k, self.chips)

    def partner(self):
        return (self.row, self.part + 1 - 2 * self.core)

    def along_rows(self, k):
        row = lax.rem(self.row + k, self.batches)
        return row, (row, self.part)

    def from_rows(self, k):
        return lax.rem(self.row + self.batches - k, self.batches)

    def along_seq(self, k):
        part = lax.rem(self.part + k, self.tokens)
        return part, (self.row, part)

    def along_plane(self, k):
        index = lax.rem(2 * self.row + self.core + k, 2 * self.batches)
        row, core = index // 2, index % 2
        return row, core, (row, 2 * self.chip + core)

    def chip_peers(self):
        return [self.along_chips(k)[1] for k in range(1, self.chips)]

    def row_peers(self):
        return [self.along_rows(k)[1] for k in range(1, self.batches)]

    def cross_peers(self):
        other = self.part + 1 - 2 * self.core
        return [(self.along_rows(k)[0], other) for k in range(1, self.batches)]

    def cross_row_peers(self):
        return self.row_peers() + self.cross_peers()

    def seq_peers(self):
        return [self.along_seq(k)[1] for k in range(1, self.tokens)]

    def plane_peers(self):
        return [self.along_plane(k)[2] for k in range(1, 2 * self.batches)]


def meet(peers):
    barrier = pltpu.get_barrier_semaphore()
    for peer in peers:
        pl.semaphore_signal(barrier, inc=1, device_id=peer, device_id_type=MESH)
    pl.semaphore_wait(barrier, len(peers))


class Wires:
    def __init__(self, send_sems, recv_sems, local_sems):
        self.sems = (send_sems, recv_sems, local_sems)
        self.used = [0, 0]
        self.ends = []

    def send(self, src, dst, peer):
        k = self.used[0]
        self.used[0] += 1
        copy = pltpu.make_async_remote_copy(
            src_ref=src,
            dst_ref=dst,
            send_sem=self.sems[0].at[k],
            recv_sem=self.sems[1].at[k],
            device_id=peer,
            device_id_type=MESH,
        )
        copy.start()
        self.ends.append(copy.wait_send)
        return copy

    def local(self, src, dst):
        k = self.used[1]
        self.used[1] += 1
        copy = pltpu.make_async_copy(src, dst, self.sems[2].at[k])
        copy.start()
        return copy

    def finish(self):
        for end in self.ends:
            end()


def wire_scratch(sends, locals_count):
    return [
        pltpu.SemaphoreType.DMA((sends,)),
        pltpu.SemaphoreType.DMA((sends,)),
        pltpu.SemaphoreType.DMA((locals_count,)),
    ]


def comm_call(kernel, name, ident, out_shapes, inputs, sends, locals_count, scratch=(), spec=VMEM_SPEC):
    return pl.pallas_call(
        kernel,
        out_shape=tuple(out_shapes),
        in_specs=[spec] * len(inputs),
        out_specs=tuple([VMEM_SPEC] * len(out_shapes)),
        scratch_shapes=list(scratch) + wire_scratch(sends, locals_count),
        compiler_params=pltpu.CompilerParams(
            collective_id=ident, has_side_effects=True, vmem_limit_bytes=COMM_VMEM
        ),
        name=name,
    )(*inputs)


def like(array, *lead):
    return jax.ShapeDtypeStruct(tuple(lead) + tuple(array.shape), array.dtype)


def pick(values, index):
    out = jnp.int32(values[0])
    for i in range(1, len(values)):
        out = jnp.where(index == i, jnp.int32(values[i]), out)
    return out


def arrival_order(at):
    chips = range(at.chips)
    lists = [sorted((j for j in chips if j != z), key=lambda j: (abs(j - z), j)) for z in chips]
    return [pick([lists[z][t] for z in chips], at.chip) for t in range(at.chips - 1)]


def return_order(at):
    chips = range(at.chips)

    def away(j, z):
        end = at.chips - 1 if j < z else 0
        return (abs(j - end) + abs(end - z), j)

    lists = [sorted((j for j in chips if j != z), key=lambda j: away(j, z)) for z in chips]
    return [pick([lists[z][t] for z in chips], at.chip) for t in range(at.chips - 1)]


def goes_on(at, j):
    above = jnp.logical_and(j < at.chip, at.chip < at.chips - 1)
    below = jnp.logical_and(j > at.chip, at.chip > 0)
    return jnp.logical_or(above, below)


def line_peer(at, step):
    return (at.row, 2 * (at.chip + step) + at.core)


class LineGather:
    def __init__(self, at, buf, slot, sems, own=None):
        self.at, self.buf, self.slot, self.own = at, buf, slot, own
        self.send_sems, self.recv_sems = sems
        self.rows = buf.shape[1] // CHUNKS

    def copy(self, j, h, step, k, own=False):
        window = pl.ds(h * self.rows, self.rows)
        home = self.buf.at[self.slot(j), window]
        src = self.own.at[window] if own and self.own is not None else home
        return pltpu.make_async_remote_copy(
            src_ref=src,
            dst_ref=home,
            send_sem=self.send_sems.at[k * CHUNKS + h],
            recv_sem=self.recv_sems.at[j * CHUNKS + h],
            device_id=line_peer(self.at, step),
            device_id_type=MESH,
        )

    def own_each(self, act):
        z, n = self.at.chip, self.at.chips
        for h in range(CHUNKS):

            @pl.when(z < n - 1)
            def _():
                act(self.copy(z, h, 1, z, own=True))

            @pl.when(z > 0)
            def _():
                act(self.copy(z, h, -1, n, own=True))

    def start(self):
        self.own_each(lambda copy: copy.start())

    def arrive(self, j):
        step = jnp.where(j < self.at.chip, 1, -1)
        for h in range(CHUNKS):
            self.copy(j, h, -step, j).wait_recv()

            @pl.when(goes_on(self.at, j))
            def _():
                self.copy(j, h, step, j).start()

    def drain(self, order):
        self.own_each(lambda copy: copy.wait_send())
        for j in order:
            step = jnp.where(j < self.at.chip, 1, -1)

            @pl.when(goes_on(self.at, j))
            def _():
                for h in range(CHUNKS):
                    self.copy(j, h, step, j).wait_send()


class LineReduce:
    def __init__(self, at, part, got, sems):
        self.at, self.part, self.got = at, part, got
        self.send_sems, self.recv_sems = sems
        self.rows = part.shape[1] // CHUNKS

    def copy(self, j, h):
        z, n = self.at.chip, self.at.chips
        window = pl.ds(h * self.rows, self.rows)
        slot = jnp.where(z + 1 == j, n, j)
        return pltpu.make_async_remote_copy(
            src_ref=self.part.at[j, window],
            dst_ref=self.got.at[slot, window],
            send_sem=self.send_sems.at[j * CHUNKS + h],
            recv_sem=self.recv_sems.at[slot * CHUNKS + h],
            device_id=line_peer(self.at, jnp.where(j < z, -1, 1)),
            device_id_type=MESH,
        )

    def landed(self, slot, h, step):
        window = pl.ds(h * self.rows, self.rows)
        return pltpu.make_async_remote_copy(
            src_ref=self.got.at[slot, window],
            dst_ref=self.got.at[slot, window],
            send_sem=self.send_sems.at[h],
            recv_sem=self.recv_sems.at[slot * CHUNKS + h],
            device_id=line_peer(self.at, step),
            device_id_type=MESH,
        )

    def send(self, j):
        for h in range(CHUNKS):
            self.copy(j, h).start()

    def send_last(self, j):
        @pl.when(jnp.logical_not(goes_on(self.at, j)))
        def _():
            self.send(j)

    def pass_on(self, order):
        z, n = self.at.chip, self.at.chips
        wide = jnp.float32

        @pl.when(jnp.logical_and(z > 0, z < n - 1))
        def _():
            for j in order:
                step = jnp.where(j < z, 1, -1)
                for h in range(CHUNKS):
                    self.landed(j, h, step).wait_recv()
                    window = pl.ds(h * self.rows, self.rows)
                    total = self.part[j, window].astype(wide) + self.got[j, window].astype(wide)
                    self.part[j, window] = total.astype(self.part.dtype)
                    self.copy(j, h).start()

    def clear(self):
        z, n = self.at.chip, self.at.chips

        @pl.when(z == n - 1)
        def _():
            self.got[z] = jnp.zeros(self.got.shape[1:], self.got.dtype)

        @pl.when(z == 0)
        def _():
            self.got[n] = jnp.zeros(self.got.shape[1:], self.got.dtype)

    def collect(self):
        z, n = self.at.chip, self.at.chips
        for h in range(CHUNKS):

            @pl.when(z < n - 1)
            def _():
                self.landed(z, h, 1).wait_recv()

            @pl.when(z > 0)
            def _():
                self.landed(n, h, -1).wait_recv()

        return self.got[z].astype(jnp.float32) + self.got[n].astype(jnp.float32)

    def drain(self, order):
        for j in order:
            for h in range(CHUNKS):
                self.copy(j, h).wait_send()


def gather_sems(chips):
    return [
        pltpu.SemaphoreType.DMA(((chips + 1) * CHUNKS,)),
        pltpu.SemaphoreType.DMA((chips * CHUNKS,)),
    ]


def reduce_sems(chips):
    return [
        pltpu.SemaphoreType.DMA((chips * CHUNKS,)),
        pltpu.SemaphoreType.DMA(((chips + 1) * CHUNKS,)),
    ]


def gather_kernel(
    x_ref, wq_ref, wk_ref, wv_ref, mix_ref, table_ref, vec_ref, up_ref, down_ref,
    xs_ref, qkvs_ref, mixs_ref, tables_ref, vecs_ref, up2_ref, down2_ref,
    line_send, line_recv, *sems,
):
    at = Place()
    wires = Wires(*sems)
    b, s, z, c = at.row, at.part, at.chip, at.core
    off_diagonal = b != z
    turned = (z, 2 * b + c)
    peers = at.seq_peers() + at.row_peers()
    barrier = pltpu.get_barrier_semaphore()
    for peer in peers:
        pl.semaphore_signal(barrier, inc=1, device_id=peer, device_id_type=MESH)

    @pl.when(off_diagonal)
    def _():
        pl.semaphore_signal(barrier, inc=1, device_id=turned, device_id_type=MESH)

    pl.semaphore_wait(barrier, len(peers) + off_diagonal.astype(jnp.int32))

    swaps, stays = [], []
    for i, ref in enumerate((wq_ref, wk_ref, wv_ref)):
        k = wires.used[0]
        wires.used[0] += 1
        swaps.append(
            pltpu.make_async_remote_copy(
                src_ref=ref,
                dst_ref=qkvs_ref.at[2 * z + c, i],
                send_sem=sems[0].at[k],
                recv_sem=sems[1].at[k],
                device_id=turned,
                device_id_type=MESH,
            )
        )
        stays.append(pltpu.make_async_copy(ref, qkvs_ref.at[2 * b + c, i], sems[2].at[i]))
        wires.used[1] += 1

    @pl.when(off_diagonal)
    def _():
        for swap in swaps:
            swap.start()

    @pl.when(jnp.logical_not(off_diagonal))
    def _():
        for stay in stays:
            stay.start()

    table_home = tables_ref.at[c, b, z]
    mix_home = mixs_ref.at[c, b, z]
    table_sends = [
        wires.send(table_ref, table_home, at.along_chips(k)[1]) for k in range(1, at.chips)
    ]
    kept = [wires.local(table_ref, table_home), wires.local(mix_ref, mix_home)]
    line = LineGather(at, xs_ref, lambda j: 2 * j + c, (line_send, line_recv), own=x_ref)
    line.start()
    last = [wires.send(vec_ref, vecs_ref.at[s], at.along_seq(k)[1]) for k in range(1, at.tokens)]
    mix_sends = [
        wires.send(mix_ref, mix_home, at.along_chips(k)[1]) for k in range(1, at.chips)
    ]
    last += [
        wires.send(x_ref, xs_ref.at[s], at.partner()),
        wires.send(up_ref, up2_ref, at.partner()),
        wires.send(down_ref, down2_ref, at.partner()),
    ]
    own = [
        wires.local(x_ref, xs_ref.at[s]),
        wires.local(vec_ref, vecs_ref.at[s]),
    ]

    @pl.when(off_diagonal)
    def _():
        for swap in swaps:
            swap.wait_recv()

    @pl.when(jnp.logical_not(off_diagonal))
    def _():
        for stay in stays:
            stay.wait()

    mine = qkvs_ref.at[2 * b + c]
    qkv_sends = [wires.send(mine, mine, at.along_rows(k)[1]) for k in range(1, at.batches)]
    last.append(wires.send(mine, mine, at.partner()))
    for copy in table_sends:
        copy.wait_recv()
    for copy in kept:
        copy.wait()
    mine = tables_ref.at[c, b]
    row_sends = [wires.send(mine, mine, at.along_rows(k)[1]) for k in range(1, at.batches)]
    last.append(wires.send(mine, mine, at.partner()))
    order = arrival_order(at)

    def arrived(j):
        line.arrive(j)
        home = xs_ref.at[2 * j + c]
        last.append(wires.send(home, home, at.partner()))

    arrived(order[0])
    for copy in mix_sends:
        copy.wait_recv()
    mine = mixs_ref.at[c, b]
    mix_rows = [wires.send(mine, mine, at.along_rows(k)[1]) for k in range(1, at.batches)]
    last.append(wires.send(mine, mine, at.partner()))
    arrived(order[1])
    for k in range(1, at.batches):
        qkv_sends[k - 1].wait_recv()
        home = qkvs_ref.at[2 * at.from_rows(k) + c]
        last.append(wires.send(home, home, at.partner()))
    for k in range(1, at.batches):
        row_sends[k - 1].wait_recv()
        home = tables_ref.at[c, at.from_rows(k)]
        last.append(wires.send(home, home, at.partner()))
    for j in order[2:]:
        arrived(j)
    for k in range(1, at.batches):
        mix_rows[k - 1].wait_recv()
        home = mixs_ref.at[c, at.from_rows(k)]
        last.append(wires.send(home, home, at.partner()))
    for copy in last:
        copy.wait_recv()
    for copy in own:
        copy.wait()
    wires.finish()
    line.drain(order)

    @pl.when(off_diagonal)
    def _():
        for swap in swaps:
            swap.wait_send()


def gather_inputs(x, w_query, w_key, w_value, w_mix, rel_table, vec, up, down):
    tokens, batches = lax.axis_size("seq"), lax.axis_size("batch")
    chips = tokens // 2
    outs = (
        like(x, tokens),
        like(w_query, tokens, 3),
        like(w_mix, 2, batches, chips),
        like(rel_table, 2, batches, chips),
        like(vec, tokens),
        like(up),
        like(down),
    )
    sends = 3 + 2 * (chips - 1) + tokens - 1 + 3 + 6 * (batches - 1) + 3 + chips - 1
    inputs = (x, w_query, w_key, w_value, w_mix, rel_table, vec, up, down)
    return comm_call(
        gather_kernel,
        "gather_inputs",
        0,
        outs,
        inputs,
        sends,
        7,
        scratch=gather_sems(chips),
        spec=HBM_SPEC,
    )


def norm_parts(values):
    average = jnp.mean(values, axis=-1, keepdims=True)
    centered = values - average
    variance = jnp.mean(centered * centered, axis=-1, keepdims=True)
    scale = lax.rsqrt(variance + norm_eps)
    return centered * scale, scale


def norm_back(grad, gain, unit, scale):
    inner = grad * gain
    mean = jnp.mean(inner, axis=-1, keepdims=True)
    slope = jnp.mean(inner * unit, axis=-1, keepdims=True)
    return scale * (inner - mean - unit * slope)


def line_pass(gather, reduce, order, work):
    def finish(j):
        work(j)
        reduce.send_last(j)

    for j in order:
        gather.arrive(j)
        finish(j)


def feed_kernel(
    ctx_ref, x_ref, mixs_ref, vecs_ref, up_ref, down_ref, up2_ref, down2_ref, out_grad_ref,
    output_ref, pre_grad_ref, sums_ref, attn_ref, mix_ref, ups_ref, downs_ref, upbs_ref,
    got_ref, hid_ref, act_ref, slope_ref, part_ref, ffn_ref, grad_ref, inner_ref,
    back_ref, backs_ref, up_away_ref, down_away_ref, upb_away_ref,
    up_got_ref, down_got_ref, upb_got_ref, upg_ref, downg_ref, upb_ref, vec_ref,
    hid_send, hid_recv, ffn_send, ffn_recv, grad_send, grad_recv, back_send, back_recv,
    attn_send, attn_recv, *sems,
):
    at = Place()
    wires = Wires(*sems)
    low, wide = jnp.bfloat16, jnp.float32
    b, s, z, c = at.row, at.part, at.chip, at.core
    order, returns = arrival_order(at), return_order(at)
    meet(at.seq_peers() + at.row_peers())
    last, own = [], []
    swaps = []
    for k in range(1, at.tokens):
        part, peer = at.along_seq(k)
        swaps.append(wires.send(ctx_ref.at[part], got_ref.at[s], peer))
    kept = wires.local(ctx_ref.at[s], got_ref.at[s])
    lanes = x_ref.shape[1] // at.tokens
    hidden_here = up_ref.shape[1]
    vec_ref[...] = jnp.concatenate(
        [vecs_ref[part, :, :lanes].astype(wide) for part in range(at.tokens)], axis=1
    )
    bias3 = vec_ref[3:4]
    gain1, gain2 = vec_ref[4:5], vec_ref[5:6]
    shift1, shift2 = vec_ref[6:7], vec_ref[7:8]
    bias_down = vec_ref[8:9]
    partner = s + 1 - 2 * c
    up_rows = hidden_here // BLOCK
    bias_up = jnp.concatenate(
        [vecs_ref[s, 10 + i : 11 + i].astype(wide) for i in range(up_rows)]
        + [vecs_ref[partner, 10 + i : 11 + i].astype(wide) for i in range(up_rows)],
        axis=1,
    )
    shard_rows = mixs_ref.shape[3]
    for part in range(at.tokens):
        mix_ref[part * shard_rows : (part + 1) * shard_rows] = jnp.concatenate(
            [mixs_ref[part % 2, row, part // 2] for row in range(at.batches)], axis=1
        )
    for copy in swaps:
        copy.wait_recv()
    kept.wait()
    pieces = []
    for chip in range(at.chips):
        left, right = got_ref[2 * chip], got_ref[2 * chip + 1]
        middle = left[:, DH:].astype(wide) + right[:, :DH].astype(wide)
        pieces += [left[:, :DH], middle.astype(low), right[:, DH:]]
    context = jnp.concatenate(pieces, axis=1)
    pre_norm = x_ref[...].astype(wide) + dot_nn(context, mix_ref[...]) + bias3
    unit1, scale1 = norm_parts(pre_norm)
    hidden = unit1 * gain1 + shift1
    hid_ref[z] = hidden.astype(low)
    hid_line = LineGather(at, hid_ref, lambda j: j, (hid_send, hid_recv))
    ffn_line = LineReduce(at, part_ref, ffn_ref, (ffn_send, ffn_recv))
    hid_line.start()
    ffn_line.clear()

    def ffn(chip):
        rows = hid_ref[chip]
        inner = jnp.concatenate(
            [dot_nn(rows, up_ref[...]), dot_nn(rows, up2_ref[...])], axis=1
        )
        inner = inner + bias_up
        cdf = 0.5 * (1.0 + lax.erf(inner * math.sqrt(0.5)))
        act = (inner * cdf).astype(low)
        slope_ref[chip] = cdf + inner * (
            jnp.exp(-0.5 * inner * inner) * (1.0 / math.sqrt(2.0 * math.pi))
        )
        act_ref[chip] = act
        part_ref[chip] = (
            dot_nn(act[:, :hidden_here], down_ref[...])
            + dot_nn(act[:, hidden_here:], down2_ref[...])
        ).astype(low)

    ffn(z)
    line_pass(hid_line, ffn_line, order, ffn)
    ffn_line.pass_on(returns)
    total = part_ref[z].astype(wide) + ffn_line.collect()
    mixed = hidden + total + bias_down
    unit2, scale2 = norm_parts(mixed)
    output_ref[...] = (unit2 * gain2 + shift2).astype(low)
    out_grad = out_grad_ref[...].astype(wide)
    mixed_grad = norm_back(out_grad, gain2, unit2, scale2)
    grad_ref[z] = mixed_grad.astype(low)
    grad_line = LineGather(at, grad_ref, lambda j: j, (grad_send, grad_recv))
    back_line = LineReduce(at, back_ref, backs_ref, (back_send, back_recv))
    grad_line.start()
    back_line.clear()
    gain2_grad = jnp.sum(out_grad * unit2, axis=0, keepdims=True)
    shift2_grad = jnp.sum(out_grad, axis=0, keepdims=True)
    downb_grad = jnp.sum(mixed_grad, axis=0, keepdims=True)

    def back(chip):
        rows = grad_ref[chip]
        act_grad = jnp.concatenate(
            [dot_nt(rows, down_ref[...]), dot_nt(rows, down2_ref[...])], axis=1
        )
        inner_low = (act_grad * slope_ref[chip]).astype(low)
        inner_ref[chip] = inner_low
        back_ref[chip] = (
            dot_nt(inner_low[:, :hidden_here], up_ref[...])
            + dot_nt(inner_low[:, hidden_here:], up2_ref[...])
        ).astype(low)

    back(z)
    line_pass(grad_line, back_line, order, back)
    width = x_ref.shape[1]
    columns = width // at.batches
    inner_all = inner_ref[...].reshape(at.chips * BLOCK, 2 * hidden_here)
    act_all = act_ref[...].reshape(at.chips * BLOCK, 2 * hidden_here)
    hid_all = hid_ref[...].reshape(at.chips * BLOCK, width)
    grad_all = grad_ref[...].reshape(at.chips * BLOCK, width)
    near, away = slice(0, hidden_here), slice(hidden_here, 2 * hidden_here)
    up_grad = dot_tn(hid_all, inner_all)
    up_away_ref[...] = up_grad[:, away].astype(low)
    down_grad = dot_tn(grad_all, act_all)
    down_away_ref[...] = down_grad[:, away].astype(low)
    upb_grad = jnp.sum(inner_all.astype(wide), axis=0, keepdims=True)
    upb_away_ref[...] = jnp.broadcast_to(upb_grad[:, away], upb_away_ref.shape)
    halves = [
        wires.send(up_away_ref, up_got_ref, at.partner()),
        wires.send(down_away_ref, down_got_ref, at.partner()),
        wires.send(upb_away_ref, upb_got_ref, at.partner()),
    ]
    back_line.pass_on(returns)
    for copy in halves:
        copy.wait_recv()
    upb_ref[...] = jnp.broadcast_to(upb_grad[:, near], upb_ref.shape) + upb_got_ref[...]
    up_sum = (up_grad[:, near] + up_got_ref[...].astype(wide)).astype(low)
    down_sum = (down_grad[:, near] + down_got_ref[...].astype(wide)).astype(low)
    for row in range(at.batches):
        upg_ref[row] = up_sum[row * columns : (row + 1) * columns]
        downg_ref[row] = down_sum[row * columns : (row + 1) * columns]
    for k in range(1, at.batches):
        row, peer = at.along_rows(k)
        last.append(wires.send(upg_ref.at[row], ups_ref.at[b], peer))
        last.append(wires.send(downg_ref.at[row], downs_ref.at[b], peer))
        last.append(wires.send(upb_ref, upbs_ref.at[b], peer))
    own.append(wires.local(upg_ref.at[b], ups_ref.at[b]))
    own.append(wires.local(downg_ref.at[b], downs_ref.at[b]))
    own.append(wires.local(upb_ref, upbs_ref.at[b]))
    total = back_ref[z].astype(wide) + back_line.collect()
    hidden_grad = mixed_grad + total
    pre_grad = norm_back(hidden_grad, gain1, unit1, scale1)
    attn_ref[s] = pre_grad.astype(low)
    attn_line = LineGather(at, attn_ref, lambda j: 2 * j + c, (attn_send, attn_recv))
    attn_line.start()
    last.append(wires.send(attn_ref.at[s], attn_ref.at[s], at.partner()))
    pre_grad_ref[...] = pre_grad
    gain1_grad = jnp.sum(hidden_grad * unit1, axis=0, keepdims=True)
    shift1_grad = jnp.sum(hidden_grad, axis=0, keepdims=True)
    bias3_grad = jnp.sum(pre_grad, axis=0, keepdims=True)
    sums = jnp.concatenate(
        [bias3_grad, gain1_grad, gain2_grad, shift1_grad, shift2_grad, downb_grad]
        + [jnp.zeros((2, width), wide)],
        axis=0,
    )
    spare = jnp.zeros((8, BLOCK - lanes), wide)
    for part in range(at.tokens):
        sums_ref[part] = jnp.concatenate(
            [sums[:, part * lanes : (part + 1) * lanes], spare], axis=1
        )
    for j in order:
        attn_line.arrive(j)
        home = attn_ref.at[2 * j + c]
        last.append(wires.send(home, home, at.partner()))
    for copy in last:
        copy.wait_recv()
    for copy in own:
        copy.wait()
    wires.finish()
    for line in (hid_line, ffn_line, grad_line, back_line, attn_line):
        line.drain(order)


def feed_forward(ctx, x, mixs, vecs, up, down, up2, down2, out_grad, ident):
    tokens, batches = lax.axis_size("seq"), lax.axis_size("batch")
    chips = tokens // 2
    width = x.shape[1]
    columns = width // batches
    hidden_here = up.shape[1]
    low, wide = jnp.bfloat16, jnp.float32
    outs = (
        jax.ShapeDtypeStruct(x.shape, low),
        jax.ShapeDtypeStruct(x.shape, wide),
        jax.ShapeDtypeStruct((tokens, 8, BLOCK), wide),
        jax.ShapeDtypeStruct((tokens,) + x.shape, low),
        jax.ShapeDtypeStruct((width, width), low),
        jax.ShapeDtypeStruct((batches, columns, hidden_here), low),
        jax.ShapeDtypeStruct((batches, columns, hidden_here), low),
        jax.ShapeDtypeStruct((batches, 8, hidden_here), wide),
    )
    block = (chips,) + x.shape
    wide_block = (chips, x.shape[0], 2 * hidden_here)
    slots = (chips + 1,) + x.shape
    up_half, bias_half = (width, hidden_here), (8, hidden_here)
    down_half = up_half
    scratch = [
        pltpu.VMEM(ctx.shape, low),
        pltpu.VMEM(block, low),
        pltpu.VMEM(wide_block, low),
        pltpu.VMEM(wide_block, wide),
        pltpu.VMEM(block, low),
        pltpu.VMEM(slots, low),
        pltpu.VMEM(block, low),
        pltpu.VMEM(wide_block, low),
        pltpu.VMEM(block, low),
        pltpu.VMEM(slots, low),
        pltpu.VMEM(up_half, low),
        pltpu.VMEM(down_half, low),
        pltpu.VMEM(bias_half, wide),
        pltpu.VMEM(up_half, low),
        pltpu.VMEM(down_half, low),
        pltpu.VMEM(bias_half, wide),
        pltpu.VMEM((batches, columns, hidden_here), low),
        pltpu.VMEM((batches, columns, hidden_here), low),
        pltpu.VMEM(bias_half, wide),
        pltpu.VMEM((16, width), wide),
    ]
    scratch += (gather_sems(chips) + reduce_sems(chips)) * 2 + gather_sems(chips)
    inputs = (ctx, x, mixs, vecs, up, down, up2, down2, out_grad)
    sends = tokens - 1 + 2 * batches - 1 + 3 + 3 * (batches - 1) + chips
    return pl.pallas_call(
        feed_kernel,
        out_shape=outs,
        in_specs=[VMEM_SPEC] * len(inputs),
        out_specs=(VMEM_SPEC,) * len(outs),
        scratch_shapes=scratch + wire_scratch(sends, 5),
        compiler_params=pltpu.CompilerParams(
            collective_id=ident, has_side_effects=True, vmem_limit_bytes=FEED_VMEM
        ),
        name="feed_forward",
    )(*inputs)


def settle_kernel(
    vec_ref, col_ref, dcat_ref, rel_ref, w_ref, xs_ref, table_ref, ctx_ref, attn_ref,
    ins_ref, vec_all_ref, cols_ref, dw_all_ref, tab_all_ref, mix_all_ref,
    in_ref, dw_ref, tab_ref, mix_ref, half_ref, sum_ref, vecs_ref, vec_low_ref, dws_ref, dw_low_ref, tabs_ref, tab_low_ref,
    mixs_ref, mix_low_ref, *sems,
):
    at = Place()
    wires = Wires(*sems)
    low, wide = jnp.bfloat16, jnp.float32
    b, s, z, c = at.row, at.part, at.chip, at.core
    off_diagonal = b != z
    same, cross = (z, 2 * b + c), (z, 2 * b + 1 - c)
    peers = at.seq_peers() + at.cross_row_peers()
    barrier = pltpu.get_barrier_semaphore()
    for peer in peers:
        pl.semaphore_signal(barrier, inc=1, device_id=peer, device_id_type=MESH)

    @pl.when(off_diagonal)
    def _():
        pl.semaphore_signal(barrier, inc=1, device_id=same, device_id_type=MESH)
        pl.semaphore_signal(barrier, inc=1, device_id=cross, device_id_type=MESH)

    pl.semaphore_wait(barrier, len(peers) + 2 * off_diagonal.astype(jnp.int32))

    dw_sends, tab_sends, mix_sends, vec_sends, last, own = [], [], [], [], [], []
    width = w_ref.shape[0]
    columns = width // at.batches
    full_len = dcat_ref.shape[0]
    group = 2 * DH

    def input_part(chip, core):
        start = pl.multiple_of((2 * chip + core) * BLOCK, BLOCK)
        in_ref[chip, core] = dot_nt(dcat_ref[pl.ds(start, BLOCK)], w_ref[...]).astype(low)

    halves = []
    for chip in range(at.chips):
        input_part(chip, 1 - c)
        halves.append(wires.send(in_ref.at[chip, 1 - c], half_ref.at[chip], at.partner()))
    for k in range(1, at.tokens):
        part, peer = at.along_seq(k)
        vec_sends.append(wires.send(vec_ref.at[part], vecs_ref.at[k - 1], peer))
    mine = 2 * b + c
    for k in range(1, 2 * at.batches):
        last.append(wires.send(col_ref, cols_ref.at[mine], at.along_plane(k)[2]))
    own.append(wires.local(col_ref, cols_ref.at[mine]))

    for chip in range(at.chips):
        input_part(chip, c)
        halves[chip].wait_recv()
        sum_ref[chip] = (in_ref[chip, c].astype(wide) + half_ref[chip].astype(wide)).astype(low)
    for k in range(1, at.chips):
        chip, peer = at.along_chips(k)
        last.append(wires.send(sum_ref.at[chip], ins_ref.at[z], peer))
    own.append(wires.local(sum_ref.at[z], ins_ref.at[z]))

    whole = xs_ref[...].reshape(full_len, width)
    dw = dot_tn(whole, dcat_ref[...])
    dw_rel = dot_tn(table_ref[...], rel_ref[...])
    dw = jnp.concatenate([dw[:, : 2 * group] + dw_rel, dw[:, 2 * group :]], axis=1)
    for row in range(at.batches):
        dw_ref[row] = dw[row * columns : (row + 1) * columns].astype(low)
    for k in range(1, at.batches):
        row, peer = at.along_rows(k)
        dw_sends.append(wires.send(dw_ref.at[row], dws_ref.at[k - 1], peer))
    for row in range(at.batches):
        rows = slice(row * columns, (row + 1) * columns)
        tab_ref[row] = dot_nt(rel_ref[...], w_ref[rows, : 2 * group]).astype(low)
    for k in range(1, at.batches):
        row, peer = at.along_rows(k)
        tab_sends.append(wires.send(tab_ref.at[row], tabs_ref.at[k - 1], peer))
    mix = dot_tn(
        ctx_ref[...].reshape(full_len, group), attn_ref[...].reshape(full_len, width)
    )
    for row in range(at.batches):
        mix_ref[row] = mix[:, row * columns : (row + 1) * columns].astype(low)
    for k in range(1, at.batches):
        row, peer = at.along_rows(k)
        mix_sends.append(wires.send(mix_ref.at[row], mixs_ref.at[k - 1], peer))

    total = dw_ref[b].astype(wide)
    for k in range(1, at.batches):
        dw_sends[k - 1].wait_recv()
        total = total + dws_ref[k - 1].astype(wide)
    shard_rows = dw_low_ref.shape[1]
    for half in range(2):
        dw_low_ref[half] = total[half * shard_rows : (half + 1) * shard_rows].astype(low)
    k = wires.used[0]
    wires.used[0] += 1
    move = pltpu.make_async_remote_copy(
        src_ref=dw_low_ref.at[c],
        dst_ref=dw_all_ref.at[c],
        send_sem=sems[0].at[k],
        recv_sem=sems[1].at[k],
        device_id=same,
        device_id_type=MESH,
    )
    stay = pltpu.make_async_copy(
        dw_low_ref.at[c], dw_all_ref.at[c], sems[2].at[wires.used[1]]
    )
    wires.used[1] += 1

    @pl.when(off_diagonal)
    def _():
        move.start()

    @pl.when(jnp.logical_not(off_diagonal))
    def _():
        stay.start()

    last.append(wires.send(dw_low_ref.at[1 - c], dw_all_ref.at[c], cross))

    total = tab_ref[b].astype(wide)
    for k in range(1, at.batches):
        tab_sends[k - 1].wait_recv()
        total = total + tabs_ref[k - 1].astype(wide)
    table_rows = tab_low_ref.shape[1]
    for part in range(at.tokens):
        tab_low_ref[part] = total[part * table_rows : (part + 1) * table_rows].astype(low)
    for k in range(1, at.tokens):
        part, peer = at.along_seq(k)
        last.append(wires.send(tab_low_ref.at[part], tab_all_ref.at[s], peer))
    own.append(wires.local(tab_low_ref.at[s], tab_all_ref.at[s]))

    total = mix_ref[b].astype(wide)
    for k in range(1, at.batches):
        mix_sends[k - 1].wait_recv()
        total = total + mixs_ref[k - 1].astype(wide)
    mix_low_ref[...] = total.astype(low)
    last.append(wires.send(mix_low_ref, mix_all_ref.at[c], at.partner()))
    own.append(wires.local(mix_low_ref, mix_all_ref.at[c]))

    total = vec_ref[s]
    for k in range(1, at.tokens):
        vec_sends[k - 1].wait_recv()
        total = total + vecs_ref[k - 1]
    vec_low_ref[...] = total
    for k in range(1, at.batches):
        last.append(wires.send(vec_low_ref, vec_all_ref.at[b], at.along_rows(k)[1]))
    own.append(wires.local(vec_low_ref, vec_all_ref.at[b]))

    for copy in last:
        copy.wait_recv()
    for copy in own:
        copy.wait()
    wires.finish()

    @pl.when(off_diagonal)
    def _():
        move.wait()

    @pl.when(jnp.logical_not(off_diagonal))
    def _():
        stay.wait()


def settle_grads(vec, cols, dcat, rel, w_cat, xs, table, ctx, attn_all, ident):
    tokens, batches = lax.axis_size("seq"), lax.axis_size("batch")
    chips = tokens // 2
    low, wide = jnp.bfloat16, jnp.float32
    local_len, width = xs.shape[1:]
    columns, group = width // batches, dcat.shape[1]
    buckets = table.shape[0]
    half = (chips, local_len, width)
    dw_pieces = (2, columns // 2, group)
    tab_pieces = (tokens, buckets // tokens, columns)
    mix_piece = (2 * DH, columns)
    dw_piece, tab_piece = (columns, group), (buckets, columns)
    outs = (
        jax.ShapeDtypeStruct(half, low),
        jax.ShapeDtypeStruct((batches,) + vec.shape[1:], wide),
        like(cols, 2 * batches),
        jax.ShapeDtypeStruct(dw_pieces, low),
        jax.ShapeDtypeStruct(tab_pieces, low),
        jax.ShapeDtypeStruct((2,) + mix_piece, low),
    )
    scratch = (
        pltpu.VMEM((chips, 2, local_len, width), low),
        pltpu.VMEM((batches,) + dw_piece, low),
        pltpu.VMEM((batches,) + tab_piece, low),
        pltpu.VMEM((batches,) + mix_piece, low),
        pltpu.VMEM(half, low),
        pltpu.VMEM(half, low),
        pltpu.VMEM((tokens - 1,) + vec.shape[1:], wide),
        pltpu.VMEM(vec.shape[1:], wide),
        pltpu.VMEM((batches - 1,) + dw_piece, low),
        pltpu.VMEM(dw_pieces, low),
        pltpu.VMEM((batches - 1,) + tab_piece, low),
        pltpu.VMEM(tab_pieces, low),
        pltpu.VMEM((batches - 1,) + mix_piece, low),
        pltpu.VMEM(mix_piece, low),
    )
    sends = (
        3 * (batches - 1) + chips + tokens - 1 + 2 * batches - 1
        + 2 + chips - 1 + tokens - 1 + 1 + batches - 1
    )
    inputs = (vec, cols, dcat, rel, w_cat, xs, table, ctx, attn_all)
    return comm_call(settle_kernel, "settle_grads", ident, outs, inputs, sends, 6, scratch=scratch)


def finish_kernel(
    pre_ref, ins_ref, vecs_ref, cols_ref, dws_ref, tabs_ref, mixs_ref, ups_ref, downs_ref,
    upbs_ref, last_ref,
    output_ref, input_ref, dq_ref, dk_ref, dv_ref, mix_ref, table_ref, bias_ref, gain_ref, shift_ref,
    up_ref, upb_ref, down_ref, downb_ref,
):
    at = Place()
    wide = jnp.float32

    def total(ref):
        out = ref[0].astype(wide)
        for k in range(1, ref.shape[0]):
            out = out + ref[k].astype(wide)
        return out

    output_ref[...] = last_ref[...]
    input_ref[...] = pre_ref[...] + total(ins_ref)
    up_ref[...] = total(ups_ref)
    down_ref[...] = total(downs_ref)
    upb_ref[...] = total(upbs_ref)[0:1]
    table_ref[...] = total(tabs_ref)
    group = 2 * DH
    spare = jnp.zeros((dws_ref.shape[1], DH), wide)
    for i, ref in enumerate((dq_ref, dk_ref, dv_ref)):
        lower = dws_ref[0, :, i * group : (i + 1) * group].astype(wide)
        upper = dws_ref[1, :, i * group : (i + 1) * group].astype(wide)
        ref[...] = jnp.concatenate([lower, spare], axis=1) + jnp.concatenate(
            [spare, upper], axis=1
        )
    rows = mix_ref.shape[0]
    lower, upper = mixs_ref[0].astype(wide), mixs_ref[1].astype(wide)
    spare = jnp.zeros((DH, lower.shape[1]), wide)
    whole = jnp.concatenate([lower, spare], axis=0) + jnp.concatenate([spare, upper], axis=0)
    mix_ref[...] = jnp.where(at.core == 0, whole[:rows], whole[rows:])
    small = total(vecs_ref)
    lanes = bias_ref.shape[1]
    cols = [cols_ref[core, 0:1] for core in range(2)]
    for row in range(1, at.batches):
        cols = [cols[core] + cols_ref[2 * row + core, 0:1] for core in range(2)]
    spare = jnp.zeros((1, DH), wide)
    biases = []
    for i in range(3):
        lower, upper = [part[:, i * group : (i + 1) * group] for part in cols]
        both = jnp.concatenate([lower, spare], axis=1) + jnp.concatenate([spare, upper], axis=1)
        biases.append(jnp.where(at.core == 0, both[:, :lanes], both[:, lanes:]))
    bias_ref[...] = jnp.concatenate(biases + [small[0:1, :lanes]], axis=0)
    gain_ref[...] = small[1:3, :lanes]
    shift_ref[...] = small[3:5, :lanes]
    downb_ref[...] = small[5:6, :lanes]


def finish(pre_grad, parts, shapes):
    inputs = (pre_grad,) + tuple(parts)
    return pl.pallas_call(
        finish_kernel,
        out_shape=(like(parts[-1]),)
        + tuple(jax.ShapeDtypeStruct(shape, jnp.float32) for shape in shapes),
        in_specs=[VMEM_SPEC] * len(inputs),
        out_specs=(VMEM_SPEC,) * (len(shapes) + 1),
        compiler_params=pltpu.CompilerParams(vmem_limit_bytes=COMM_VMEM),
        name="finish",
    )(*inputs)


def fits_fast(layer_input, table_shard, hidden_here):
    rows, local_len, width = layer_input.shape
    tokens, batches = lax.axis_size("seq"), lax.axis_size("batch")
    return (
        rows == 1
        and local_len == BLOCK
        and tokens == 2 * batches
        and width == 3 * DH * batches
        and (table_shard.shape[0] * tokens) % (4 * BLOCK) == 0
        and tokens == 8
        and 10 + hidden_here // BLOCK <= 16
        and hidden_here % BLOCK == 0
    )


def fast_body(
    layer_input, segment_ids, w_query, w_key, w_value, w_mix, rel_table, attn_biases,
    norm_gains, norm_shifts, w_up, up_bias, w_down, down_bias, out_grad,
):
    local_len, width = layer_input.shape[1:]
    low = jnp.bfloat16
    shard_rows, shard_cols = w_query.shape
    lanes = attn_biases.shape[1]
    hidden_here = w_up.shape[1]
    x = layer_input[0]
    pack = jnp.concatenate([attn_biases, norm_gains, norm_shifts, down_bias[None]], axis=0)
    pack = jnp.pad(pack, ((0, 0), (0, BLOCK - lanes)))
    pack = jnp.concatenate(
        [pack, segment_ids.astype(low), up_bias.reshape(hidden_here // BLOCK, BLOCK)], axis=0
    )
    pack = jnp.pad(pack, ((0, 16 - pack.shape[0]), (0, 0)))
    weights = (w_query, w_key, w_value, w_mix, rel_table, pack, w_up, w_down)
    xs, qkvs, mixs, tables, vecs, up2, down2 = gather_inputs(
        *[pltpu.with_memory_space_constraint(a, pltpu.HBM) for a in (x,) + weights]
    )
    q, k, v, qrev, krev, probs, ctx, w_cat, table = attend(xs, qkvs, tables, vecs)
    output, pre_grad, sums, attn_all, m_mix, ups, downs, upbs = feed_forward(
        ctx, x, mixs, vecs, w_up, w_down, up2, down2, out_grad[0], 1
    )
    dcat, rel_grad, cols = attend_back(q, k, v, qrev, krev, probs, m_mix, attn_all)
    ins, vec_all, cols_all, dw_all, tab_all, mix_all = settle_grads(
        sums, cols, dcat, rel_grad, w_cat, xs, table, ctx, attn_all, 2
    )
    shard = (shard_rows, shard_cols)
    shapes = (
        x.shape, shard, shard, shard, shard, rel_table.shape, (4, lanes), (2, lanes), (2, lanes),
        (width // lax.axis_size("batch"), hidden_here), (1, hidden_here),
        (width // lax.axis_size("batch"), hidden_here), (1, lanes),
    )
    grads = finish(
        pre_grad,
        (ins, vec_all, cols_all, dw_all, tab_all, mix_all, ups, downs, upbs, output),
        shapes,
    )
    output, input_grad, dq, dk, dv, dmix, dtable = grads[:7]
    dbias, dgain, dshift, dup, dupb, ddown, ddownb = grads[7:]
    return (
        output[None], input_grad[None], dq, dk, dv, dmix, dtable, dbias, dgain, dshift,
        dup, dupb.reshape(hidden_here), ddown.T, ddownb.reshape(lanes),
    )


def body(
    layer_input,
    segment_ids,
    w_query,
    w_key,
    w_value,
    w_mix,
    rel_table,
    attn_biases,
    norm_gains,
    norm_shifts,
    w_up,
    up_bias,
    w_down,
    down_bias,
    out_grad,
):
    if fits_fast(layer_input, rel_table, w_up.shape[1]):
        return fast_body(
            layer_input, segment_ids, w_query, w_key, w_value, w_mix, rel_table, attn_biases,
            norm_gains, norm_shifts, w_up, up_bias, w_down, down_bias, out_grad,
        )
    rows, local_len, width = layer_input.shape
    full_len = local_len * lax.axis_size("seq")
    tokens_here = local_len * rows
    highest_prec = lax.Precision.HIGHEST
    parts = (
        lax.all_gather(w_query, "batch", axis=1, tiled=True),
        lax.all_gather(w_key, "batch", axis=1, tiled=True),
        lax.all_gather(w_value, "batch", axis=1, tiled=True),
        lax.all_gather(w_mix, "batch", axis=1, tiled=True),
        lax.all_gather(rel_table, "batch", axis=1, tiled=True),
    )
    whole = (
        lax.all_gather(parts[0], "seq", axis=0, tiled=True),
        lax.all_gather(parts[1], "seq", axis=0, tiled=True),
        lax.all_gather(parts[2], "seq", axis=0, tiled=True),
        lax.all_gather(parts[3], "seq", axis=0, tiled=True),
        lax.all_gather(parts[4], "seq", axis=0, tiled=True),
        lax.all_gather(attn_biases, "seq", axis=1, tiled=True),
        lax.all_gather(norm_gains, "seq", axis=1, tiled=True),
        lax.all_gather(norm_shifts, "seq", axis=1, tiled=True),
        lax.all_gather(down_bias, "seq", axis=0, tiled=True),
    )
    m_query, m_key, m_value, m_mix, table, biases, gains, shifts, bias_down = whole
    flat_input = jnp.swapaxes(layer_input, 0, 1).reshape(tokens_here, width)
    queries = (jnp.dot(flat_input, m_query, preferred_element_type=jnp.float32) + biases[0]).astype(
        jnp.bfloat16
    )
    keys_here = (jnp.dot(flat_input, m_key, preferred_element_type=jnp.float32) + biases[1]).astype(
        jnp.bfloat16
    )
    values_here = (
        jnp.dot(flat_input, m_value, preferred_element_type=jnp.float32) + biases[2]
    ).astype(jnp.bfloat16)
    query_rel = (jnp.dot(table, m_query, preferred_element_type=jnp.float32) + biases[0]).astype(
        jnp.bfloat16
    )
    key_rel = (jnp.dot(table, m_key, preferred_element_type=jnp.float32) + biases[1]).astype(
        jnp.bfloat16
    )
    local_seg = jnp.swapaxes(segment_ids, 0, 1).astype(jnp.bfloat16)
    keys_all, values_all, seg_all = (
        lax.all_gather(keys_here.reshape(local_len, rows, width), "seq", axis=0, tiled=True),
        lax.all_gather(values_here.reshape(local_len, rows, width), "seq", axis=0, tiled=True),
        lax.all_gather(local_seg, "seq", axis=0, tiled=True),
    )
    buckets = table.shape[0]
    offset = lax.axis_index("seq") * local_len
    bucket_iota = jnp.arange(buckets, dtype=jnp.int32)
    inner_cols = (bucket_iota > 0) & (bucket_iota < buckets - 1)
    same_doc = (
        jnp.swapaxes(local_seg, 0, 1)[:, None, :, None]
        == jnp.swapaxes(seg_all, 0, 1)[:, None, None, :]
    )
    score_scale = 1.0 / math.sqrt(3.0 * DH)
    head_queries = split_heads(queries.reshape(local_len, rows, width))
    head_keys = split_heads(keys_all)
    head_values = split_heads(values_all)
    rel_queries = split_table(query_rel)
    rel_keys = split_table(key_rel)

    def forward_group(carry, group):
        g_query, g_key, g_value, g_qrel, g_krel = group
        total, near_pull, far_pull, window = relative_scores(
            g_query, g_key, g_krel, g_qrel, offset, full_len
        )
        scores = jnp.where(same_doc, total * score_scale, masked_score)
        highest = jnp.max(scores, axis=-1, keepdims=True)
        exponent = jnp.exp(scores - highest)
        denominator = jnp.sum(exponent, axis=-1, keepdims=True)
        weights_low = (exponent / denominator).astype(jnp.bfloat16)
        context = jnp.einsum(
            "rgij,rgjd->rgid", weights_low, g_value, preferred_element_type=jnp.float32
        )
        return (carry, (context, (highest + jnp.log(denominator))[..., 0]))

    unused, (context_groups, log_totals) = lax.scan(
        forward_group, None, (head_queries, head_keys, head_values, rel_queries, rel_keys)
    )
    context_low = join_heads(context_groups).reshape(tokens_here, width).astype(jnp.bfloat16)
    pre_norm = (
        flat_input.astype(jnp.float32)
        + jnp.dot(context_low, m_mix, preferred_element_type=jnp.float32)
        + biases[3]
    )
    hidden, norm1_pull = jax.vjp(
        normalize, pre_norm, gains[0].astype(jnp.float32), shifts[0].astype(jnp.float32)
    )
    hidden_low = hidden.astype(jnp.bfloat16)

    def spread_rows(rows_low):
        return lax.all_gather(rows_low, "seq", axis=0, tiled=True)

    def hidden_sums(make_term):
        return lax.psum_scatter(
            make_term(jnp.int32(0), tokens_here * lax.axis_size("seq")),
            "seq",
            scatter_dimension=0,
            tiled=True,
        )

    hidden_rows = spread_rows(hidden_low)
    inner = jnp.dot(hidden_rows, w_up, preferred_element_type=jnp.float32) + up_bias
    act, gelu_pull = jax.vjp(exact_gelu, inner)
    act_low = act.astype(jnp.bfloat16)

    def down_rows(start, count):
        return jnp.dot(act_low, w_down, preferred_element_type=jnp.float32)

    ffn_result = hidden_sums(down_rows)
    mixed = hidden + ffn_result + bias_down
    output, norm2_pull = jax.vjp(
        normalize, mixed, gains[1].astype(jnp.float32), shifts[1].astype(jnp.float32)
    )
    flat_grad = jnp.swapaxes(out_grad, 0, 1).reshape(tokens_here, width).astype(jnp.float32)
    mixed_grad, gain2_grad, shift2_grad = norm2_pull(flat_grad)
    ffn_grad_low = mixed_grad.astype(jnp.bfloat16)
    grad_rows = spread_rows(ffn_grad_low)
    act_grad = jnp.einsum("nd,fd->nf", grad_rows, w_down, preferred_element_type=jnp.float32)
    inner_low = gelu_pull(act_grad)[0].astype(jnp.bfloat16)
    up_part = jnp.einsum("nd,nf->df", hidden_rows, inner_low, preferred_element_type=jnp.float32)
    upb_part = jnp.sum(inner_low.astype(jnp.float32), axis=0)
    down_part = jnp.einsum("nf,nd->fd", act_low, grad_rows, preferred_element_type=jnp.float32)

    def back_rows(start, count):
        return jnp.einsum("nf,df->nd", inner_low, w_up, preferred_element_type=jnp.float32)

    hidden_grad = mixed_grad + hidden_sums(back_rows)
    pre_grad, gain1_grad, shift1_grad = norm1_pull(hidden_grad)
    attn_low = pre_grad.astype(jnp.bfloat16)
    mix_whole = jnp.einsum("nd,ne->de", context_low, attn_low, preferred_element_type=jnp.float32)
    context_grad = jnp.einsum(
        "ne,de->nd", attn_low, m_mix, preferred_element_type=jnp.float32
    ).astype(jnp.bfloat16)
    head_context_grad = split_heads(context_grad.reshape(local_len, rows, width))

    def query_side(group):
        g_query, g_key, g_value, g_qrel, g_krel, g_dctx, g_lse = group
        total, near_pull, far_pull, window = relative_scores(
            g_query, g_key, g_krel, g_qrel, offset, full_len
        )
        scores = jnp.where(same_doc, total * score_scale, masked_score)
        weights_now = jnp.exp(scores - g_lse[..., None])
        prob_grad = jnp.einsum(
            "rgid,rgjd->rgij", g_dctx, g_value, preferred_element_type=jnp.float32
        )
        inner_sum = jnp.sum(weights_now * prob_grad, axis=-1)
        score_grad = (weights_now * (prob_grad - inner_sum[..., None])).astype(jnp.bfloat16)
        grad_wide = score_grad.astype(jnp.float32)
        near_grad = near_pull(grad_wide)[0]
        near_low = jnp.where(inner_cols, near_grad, 0.0).astype(jnp.bfloat16)
        near_ends = end_columns(near_grad)
        query_part = jnp.einsum(
            "rgij,rgjd->rgid", score_grad, g_key, preferred_element_type=jnp.float32
        )
        query_part = (
            query_part
            + jnp.einsum("rgib,gbd->rgid", near_low, g_krel, preferred_element_type=jnp.float32)
            + end_terms(near_ends, g_krel)
        )
        krel_part = with_ends(
            jnp.einsum("rgib,rgid->gbd", near_low, g_query, preferred_element_type=jnp.float32),
            end_rows(near_ends, g_query),
        )
        return (
            weights_now,
            score_grad,
            grad_wide,
            far_pull,
            window,
            inner_sum,
            query_part * score_scale,
            krel_part * score_scale,
        )

    query_groups = (
        head_queries,
        head_keys,
        head_values,
        rel_queries,
        rel_keys,
        head_context_grad,
        log_totals,
    )

    def all_grads(carry, group):
        weights_now, score_grad, grad_wide, far_pull, window, inner_sum, query_part, krel_part = (
            query_side(group)
        )
        g_query, g_key, g_value, g_qrel, g_krel, g_dctx, g_lse = group
        cross_grad, end_grad = far_pull(grad_wide)
        cross_low = cross_grad.astype(jnp.bfloat16)
        key_part = jnp.einsum(
            "rgij,rgid->rgjd", score_grad, g_query, preferred_element_type=jnp.float32
        )
        band_part = jnp.einsum(
            "rgmb,gbd->rgmd", cross_low, g_qrel, preferred_element_type=jnp.float32
        )
        key_part = (
            key_part
            + unband(band_part, offset, full_len, buckets // 2)
            + end_terms(end_grad, g_qrel)
        )
        value_part = jnp.einsum(
            "rgij,rgid->rgjd",
            weights_now.astype(jnp.bfloat16),
            g_dctx,
            preferred_element_type=jnp.float32,
        )
        qrel_part = with_ends(
            jnp.einsum("rgmb,rgmd->gbd", cross_low, window, preferred_element_type=jnp.float32),
            end_rows(end_grad, g_key),
        )
        return (
            carry,
            (query_part, key_part * score_scale, value_part, qrel_part * score_scale, krel_part),
        )

    unused, (dq_groups, dk_groups, dv_groups, dqrel_groups, dkrel_groups) = lax.scan(
        all_grads, None, query_groups
    )
    key_sum, value_sum = (
        lax.psum_scatter(join_heads(dk_groups), "seq", scatter_dimension=0, tiled=True),
        lax.psum_scatter(join_heads(dv_groups), "seq", scatter_dimension=0, tiled=True),
    )
    key_grads = key_sum.reshape(tokens_here, width).astype(jnp.bfloat16)
    value_grads = value_sum.reshape(tokens_here, width).astype(jnp.bfloat16)
    query_grads = join_heads(dq_groups).reshape(tokens_here, width).astype(jnp.bfloat16)
    qrel_grad = join_table(dqrel_groups)
    krel_grad = join_table(dkrel_groups)
    input_grad = pre_grad + jnp.einsum(
        "ne,de->nd", query_grads, m_query, preferred_element_type=jnp.float32
    )
    input_grad = input_grad + jnp.einsum(
        "ne,de->nd", key_grads, m_key, preferred_element_type=jnp.float32
    )
    input_grad = input_grad + jnp.einsum(
        "ne,de->nd", value_grads, m_value, preferred_element_type=jnp.float32
    )
    query_whole = jnp.einsum(
        "nd,ne->de", flat_input, query_grads, preferred_element_type=jnp.float32
    ) + jnp.einsum(
        "bd,be->de", table, qrel_grad, precision=highest_prec, preferred_element_type=jnp.float32
    )
    key_whole = jnp.einsum(
        "nd,ne->de", flat_input, key_grads, preferred_element_type=jnp.float32
    ) + jnp.einsum(
        "bd,be->de", table, krel_grad, precision=highest_prec, preferred_element_type=jnp.float32
    )
    value_whole = jnp.einsum(
        "nd,ne->de", flat_input, value_grads, preferred_element_type=jnp.float32
    )
    table_whole = jnp.einsum(
        "be,de->bd", qrel_grad, m_query, precision=highest_prec, preferred_element_type=jnp.float32
    ) + jnp.einsum(
        "be,de->bd", krel_grad, m_key, precision=highest_prec, preferred_element_type=jnp.float32
    )
    bias_whole = jnp.stack(
        [
            jnp.sum(query_grads.astype(jnp.float32), axis=0) + jnp.sum(qrel_grad, axis=0),
            jnp.sum(key_grads.astype(jnp.float32), axis=0) + jnp.sum(krel_grad, axis=0),
            jnp.sum(value_grads.astype(jnp.float32), axis=0),
            jnp.sum(pre_grad, axis=0),
        ]
    )
    gain_whole = jnp.stack([gain1_grad, gain2_grad])
    shift_whole = jnp.stack([shift1_grad, shift2_grad])
    downb_whole = jnp.sum(mixed_grad, axis=0)
    seq_parts = (
        lax.psum_scatter(query_whole, "seq", scatter_dimension=0, tiled=True),
        lax.psum_scatter(key_whole, "seq", scatter_dimension=0, tiled=True),
        lax.psum_scatter(value_whole, "seq", scatter_dimension=0, tiled=True),
        lax.psum_scatter(mix_whole, "seq", scatter_dimension=0, tiled=True),
        lax.psum_scatter(table_whole, "seq", scatter_dimension=0, tiled=True),
        lax.psum_scatter(bias_whole, "seq", scatter_dimension=1, tiled=True),
        lax.psum_scatter(gain_whole, "seq", scatter_dimension=1, tiled=True),
        lax.psum_scatter(shift_whole, "seq", scatter_dimension=1, tiled=True),
        lax.psum_scatter(downb_whole, "seq", scatter_dimension=0, tiled=True),
    )
    batch_parts = (
        lax.psum_scatter(seq_parts[0], "batch", scatter_dimension=1, tiled=True),
        lax.psum_scatter(seq_parts[1], "batch", scatter_dimension=1, tiled=True),
        lax.psum_scatter(seq_parts[2], "batch", scatter_dimension=1, tiled=True),
        lax.psum_scatter(seq_parts[3], "batch", scatter_dimension=1, tiled=True),
        lax.psum_scatter(seq_parts[4], "batch", scatter_dimension=1, tiled=True),
        lax.psum_scatter(up_part, "batch", scatter_dimension=0, tiled=True),
        lax.psum_scatter(down_part, "batch", scatter_dimension=1, tiled=True),
    )
    small_parts = lax.psum(
        (seq_parts[5], seq_parts[6], seq_parts[7], seq_parts[8], upb_part), "batch"
    )
    layer_output = jnp.swapaxes(output.reshape(local_len, rows, width), 0, 1).astype(jnp.bfloat16)
    input_back = jnp.swapaxes(input_grad.reshape(local_len, rows, width), 0, 1)
    return (
        layer_output,
        input_back,
        batch_parts[0],
        batch_parts[1],
        batch_parts[2],
        batch_parts[3],
        batch_parts[4],
        small_parts[0],
        small_parts[1],
        small_parts[2],
        batch_parts[5],
        small_parts[4],
        batch_parts[6],
        small_parts[3],
    )


def solution(mesh):
    return jax.shard_map(
        body,
        mesh=mesh,
        in_specs=(
            P("batch", "seq", None),
            P("batch", "seq"),
            P("seq", "batch"),
            P("seq", "batch"),
            P("seq", "batch"),
            P("seq", "batch"),
            P("seq", "batch"),
            P(None, "seq"),
            P(None, "seq"),
            P(None, "seq"),
            P(None, "seq"),
            P("seq"),
            P("seq", None),
            P("seq"),
            P("batch", "seq", None),
        ),
        out_specs=(
            P("batch", "seq", None),
            P("batch", "seq", None),
            P("seq", "batch"),
            P("seq", "batch"),
            P("seq", "batch"),
            P("seq", "batch"),
            P("seq", "batch"),
            P(None, "seq"),
            P(None, "seq"),
            P(None, "seq"),
            P("batch", "seq"),
            P("seq"),
            P("seq", "batch"),
            P("seq"),
        ),
        check_vma=False,
    )
```

```python
import math

import jax
import jax.numpy as jnp
from jax import lax
from jax.experimental import pallas as pl
from jax.experimental.pallas import tpu as pltpu
from jax.sharding import PartitionSpec as P

DH = 64


masked_score = -1e30
norm_eps = 1e-06
pair_heads = 2


def normalize(values, gain, shift):
    average = jnp.mean(values, axis=-1, keepdims=True)
    centered = values - average
    variance = jnp.mean(centered * centered, axis=-1, keepdims=True)
    return centered * lax.rsqrt(variance + norm_eps) * gain + shift


def exact_gelu(values):
    return jax.nn.gelu(values, approximate=False)


def split_heads(matrix):
    length, rows, width = matrix.shape
    groups = width // (pair_heads * DH)
    return matrix.reshape(length, rows, groups, pair_heads, DH).transpose(2, 1, 3, 0, 4)


def join_heads(matrix):
    groups, rows, pair, length, depth = matrix.shape
    return matrix.transpose(3, 1, 0, 2, 4).reshape(length, rows, groups * pair * depth)


def split_table(matrix):
    buckets, width = matrix.shape
    return matrix.reshape(buckets, width // (pair_heads * DH), pair_heads, DH).transpose(1, 2, 0, 3)


def join_table(matrix):
    groups, pair, buckets, depth = matrix.shape
    return matrix.transpose(2, 0, 1, 3).reshape(buckets, groups * pair * depth)


def table_ends(table):
    return jnp.stack([table[:, 0], table[:, -1]], axis=1)


def near_skew(table_prod, offset, full_len):
    lead = table_prod.shape[:-2]
    count, buckets = table_prod.shape[-2:]
    span = buckets // 2
    lead_pad = [(0, 0)] * len(lead)
    flipped = jnp.pad(table_prod[..., ::-1], lead_pad + [(0, 0), (0, count)])
    sheared = flipped.reshape(lead + (count * (buckets + count),))[
        ..., : count * (buckets + count - 1)
    ]
    sheared = sheared.reshape(lead + (count, buckets + count - 1))
    spread = jnp.pad(sheared, lead_pad + [(0, 0), (full_len, full_len)])
    band = lax.dynamic_slice_in_dim(
        spread, full_len + span - 1 - offset, full_len, axis=len(lead) + 1
    )
    distance = (offset + jnp.arange(count, dtype=jnp.int32))[:, None] - jnp.arange(
        full_len, dtype=jnp.int32
    )[None, :]
    return jnp.where(
        distance <= -span,
        table_prod[..., 0:1],
        jnp.where(distance >= span - 1, table_prod[..., buckets - 1 :], band),
    )


def far_place(cross, end_vals, offset, count, full_len):
    lead = cross.shape[:-2]
    band_len, buckets = cross.shape[-2:]
    span = buckets // 2
    lead_pad = [(0, 0)] * len(lead)
    turned = jnp.swapaxes(cross, -1, -2).reshape(lead + (buckets * band_len,))
    turned = jnp.pad(turned, lead_pad + [(0, buckets)])
    diagonal = turned.reshape(lead + (buckets, band_len + 1))[..., :count]
    aligned = jnp.pad(jnp.swapaxes(diagonal, -1, -2), lead_pad + [(0, 0), (0, count)])
    sheared = aligned.reshape(lead + (count * (buckets + count),))[
        ..., : count * (buckets + count - 1)
    ]
    sheared = sheared.reshape(lead + (count, buckets + count - 1))
    spread = jnp.pad(sheared, lead_pad + [(0, 0), (full_len, full_len)])
    band = lax.dynamic_slice_in_dim(spread, full_len + span - offset, full_len, axis=len(lead) + 1)
    distance = (
        jnp.arange(full_len, dtype=jnp.int32)[None, :]
        - (offset + jnp.arange(count, dtype=jnp.int32))[:, None]
    )
    return jnp.where(
        distance <= -span,
        end_vals[..., 0:1, :],
        jnp.where(distance >= span - 1, end_vals[..., 1:2, :], band),
    )


def band_rows(all_rows, offset, count, span):
    padded = jnp.pad(all_rows, [(0, 0), (0, 0), (span, span), (0, 0)])
    return lax.dynamic_slice_in_dim(padded, offset, count + 2 * span - 1, axis=2)


def unband(values, offset, full_len, span):
    lead = values.shape[:2]
    room = jnp.zeros(lead + (full_len + 2 * span, values.shape[3]), jnp.float32)
    placed = lax.dynamic_update_slice_in_dim(room, values, offset, axis=2)
    return placed[:, :, span : span + full_len]


def relative_scores(own_rows, all_rows, own_table, all_table, offset, full_len):
    count = own_rows.shape[2]
    content = jnp.einsum("rgid,rgjd->rgij", own_rows, all_rows, preferred_element_type=jnp.float32)
    own_prod = jnp.einsum("rgid,gbd->rgib", own_rows, own_table, preferred_element_type=jnp.float32)
    window = band_rows(all_rows, offset, count, all_table.shape[1] // 2)
    cross = jnp.einsum("rgmd,gbd->rgmb", window, all_table, preferred_element_type=jnp.float32)
    end_vals = jnp.einsum(
        "rgjd,ged->rgej", all_rows, table_ends(all_table), preferred_element_type=jnp.float32
    )
    near_vals, near_pull = jax.vjp(lambda product: near_skew(product, offset, full_len), own_prod)
    far_vals, far_pull = jax.vjp(
        lambda part, ends: far_place(part, ends, offset, count, full_len), cross, end_vals
    )
    return (content + near_vals + far_vals, near_pull, far_pull, window)


def end_columns(grad):
    return jnp.stack([grad[..., 0], grad[..., -1]], axis=2)


def end_terms(ends, table):
    return jnp.einsum(
        "rgei,ged->rgid",
        ends,
        table_ends(table),
        precision=lax.Precision.HIGHEST,
        preferred_element_type=jnp.float32,
    )


def end_rows(ends, rows_low):
    return jnp.einsum(
        "rgei,rgid->ged",
        ends,
        rows_low,
        precision=lax.Precision.HIGHEST,
        preferred_element_type=jnp.float32,
    )


def with_ends(inner_part, edge_rows):
    buckets = inner_part.shape[1]
    place = jnp.arange(buckets, dtype=jnp.int32)[None, :, None]
    return (
        inner_part
        + jnp.where(place == 0, edge_rows[:, 0:1], 0.0)
        + jnp.where(place == buckets - 1, edge_rows[:, 1:2], 0.0)
    )


BLOCK = 128
MIB = 1024 * 1024
ATTEND_VMEM = 26 * MIB
BACK_VMEM = 26 * MIB
FEED_VMEM = 26 * MIB
COMM_VMEM = 16 * MIB


def dot_nn(a, b):
    return lax.dot_general(a, b, (((1,), (0,)), ((), ())), preferred_element_type=jnp.float32)


def dot_nt(a, b):
    return lax.dot_general(a, b, (((1,), (1,)), ((), ())), preferred_element_type=jnp.float32)


def dot_tn(a, b):
    return lax.dot_general(a, b, (((0,), (0,)), ((), ())), preferred_element_type=jnp.float32)


def turn_matrix(buckets):
    row = lax.broadcasted_iota(jnp.int32, (buckets, buckets), 0)
    col = lax.broadcasted_iota(jnp.int32, (buckets, buckets), 1)
    return (row + col == buckets - 1).astype(jnp.bfloat16)


def skew_band(product):
    count, buckets = product.shape
    row = lax.broadcasted_iota(jnp.int32, (count, BLOCK), 0)
    lane = lax.broadcasted_iota(jnp.int32, (count, BLOCK), 1)
    edge = jnp.where(row + lane <= BLOCK - 2, product[:, buckets - 1 :], product[:, 0:1])
    wide = jnp.concatenate([product, edge], axis=1)
    return pltpu.roll(wide, 1, 1, stride=1, stride_axis=0)


def skew_back(turned, buckets):
    return pltpu.roll(turned, turned.shape[1] - BLOCK, 1, stride=1, stride_axis=0)[:, :buckets]


def chip_columns(vec_ref, chip, index, core):
    width = 3 * DH // 2
    both = jnp.concatenate(
        [
            vec_ref[2 * chip, index : index + 1, :width].astype(jnp.float32),
            vec_ref[2 * chip + 1, index : index + 1, :width].astype(jnp.float32),
        ],
        axis=1,
    )
    return jnp.where(core == 0, both[:, : 2 * DH], both[:, DH:])


def attend_kernel(
    xs_ref,
    qkvs_ref,
    tables_ref,
    vecs_ref,
    q_ref,
    k_ref,
    v_ref,
    qrev_ref,
    krev_ref,
    p_ref,
    ctx_ref,
    w_ref,
    table_ref,
    segc_ref,
    place_ref,
    wide_ref,
    ends_ref,
    held_ref,
):
    at = Place()
    full_len = xs_ref.shape[0] * xs_ref.shape[1]
    buckets = table_ref.shape[0]
    blocks = full_len // BLOCK
    span = buckets // 2
    side = span // BLOCK
    band_width = buckets + BLOCK
    band_blocks = band_width // BLOCK
    group = 2 * DH
    scale = 1.0 / math.sqrt(3.0 * DH)
    units = p_ref.shape[0]
    shard_rows = qkvs_ref.shape[2]
    table_rows = tables_ref.shape[3]
    batches = tables_ref.shape[1]
    for part in range(at.tokens):
        pieces = []
        for i in range(3):
            piece = qkvs_ref[part, i]
            pieces.append(jnp.where(at.core == 0, piece[:, :group], piece[:, DH:]))
        w_ref[part * shard_rows : (part + 1) * shard_rows] = jnp.concatenate(pieces, axis=1)
        core, chip = part % 2, part // 2
        table_ref[part * table_rows : (part + 1) * table_rows] = jnp.concatenate(
            [tables_ref[core, row, chip] for row in range(batches)], axis=1
        )
        own_seg = vecs_ref[part, 9:10].astype(jnp.float32)
        segc_ref[part * BLOCK : (part + 1) * BLOCK] = jnp.broadcast_to(own_seg, (BLOCK, BLOCK)).T
    seg_row = jnp.concatenate(
        [vecs_ref[part, 9:10].astype(jnp.float32) for part in range(at.tokens)], axis=1
    )
    bias = jnp.concatenate(
        [chip_columns(vecs_ref, at.chip, i, at.core) for i in range(3)], axis=1
    )
    tokens_all = xs_ref[...].reshape(full_len, xs_ref.shape[2])
    proj = (dot_nn(tokens_all, w_ref[...]) + bias).astype(jnp.bfloat16)
    rel = (dot_nn(table_ref[...], w_ref[:, : 2 * group]) + bias[:, : 2 * group]).astype(
        jnp.bfloat16
    )
    rel = dot_nn(turn_matrix(buckets), rel).astype(jnp.bfloat16)
    for slot in range(2):
        lo, hi = slot * DH, (slot + 1) * DH
        q_ref[slot] = proj[:, lo:hi]
        k_ref[slot] = proj[:, group + lo : group + hi]
        v_ref[slot] = proj[:, 2 * group + lo : 2 * group + hi]
        qrev_ref[slot] = rel[:, lo:hi]
        krev_ref[slot] = rel[:, group + lo : group + hi]
    held_ref[...] = jnp.zeros_like(held_ref)
    for slot in range(2):
        ends_ref[slot, 0] = dot_nt(qrev_ref[slot, 0:16], k_ref[slot])
        ends_ref[slot, 1] = dot_nt(qrev_ref[slot, buckets - 16 : buckets], k_ref[slot])

        def key_block(kb, carry):
            rows = k_ref[slot, pl.ds(pl.multiple_of(kb * BLOCK, BLOCK), BLOCK)]
            band = skew_band(dot_nt(rows, qrev_ref[slot]))
            for e in range(band_blocks):
                place_ref[
                    slot,
                    kb + e,
                    :,
                    (band_blocks - 1 - e) * BLOCK : (band_blocks - e) * BLOCK,
                ] = band[:, e * BLOCK : (e + 1) * BLOCK].T
            return carry

        lax.fori_loop(0, blocks, key_block, 0)

    first = at.core * (blocks // 2)

    def unit(u, carry):
        g = u + first
        slot = g // blocks
        qb = g % blocks
        start = pl.multiple_of(qb * BLOCK, BLOCK)
        rows = q_ref[slot, pl.ds(start, BLOCK)]
        own = dot_nt(rows, krev_ref[slot])
        band = skew_band(own) + place_ref[slot, qb + side]
        wide_ref[:, pl.ds(start, band_width)] = band
        content = dot_nt(rows, k_ref[slot])
        lane = lax.broadcasted_iota(jnp.int32, (BLOCK, full_len), 1)
        near = jnp.where(
            lane < start - span,
            own[:, 0:1] + ends_ref[slot, 1, 15:16],
            jnp.where(
                lane >= start + band_width - span,
                own[:, buckets - 1 :] + ends_ref[slot, 0, 0:1],
                wide_ref[:, span : span + full_len],
            ),
        )
        same = segc_ref[pl.ds(start, BLOCK), 0:1] == seg_row
        scores = jnp.where(same, (content + near) * scale, masked_score)
        highest = jnp.max(scores, axis=-1, keepdims=True)
        exponent = jnp.exp(scores - highest)
        total = jnp.sum(exponent, axis=-1, keepdims=True)
        probs = (exponent / total).astype(jnp.bfloat16)
        p_ref[u] = probs
        held_ref[slot, pl.ds(start, BLOCK)] = dot_nn(probs, v_ref[slot]).astype(jnp.bfloat16)
        return carry

    lax.fori_loop(0, units, unit, 0)
    for part in range(at.tokens):
        rows = slice(part * BLOCK, (part + 1) * BLOCK)
        ctx_ref[part] = jnp.concatenate([held_ref[0, rows], held_ref[1, rows]], axis=1)


def attend(xs, qkvs, tables, vecs):
    tokens, local_len, width = xs.shape
    full_len = tokens * local_len
    buckets = tokens * tables.shape[3]
    blocks = full_len // BLOCK
    units = 3 * blocks // 2
    band_width = buckets + BLOCK
    low, wide = jnp.bfloat16, jnp.float32
    pad_blocks = blocks + band_width // BLOCK - 1
    return pl.pallas_call(
        attend_kernel,
        out_shape=(
            jax.ShapeDtypeStruct((2, full_len, DH), low),
            jax.ShapeDtypeStruct((2, full_len, DH), low),
            jax.ShapeDtypeStruct((2, full_len, DH), low),
            jax.ShapeDtypeStruct((2, buckets, DH), low),
            jax.ShapeDtypeStruct((2, buckets, DH), low),
            jax.ShapeDtypeStruct((units, BLOCK, full_len), low),
            jax.ShapeDtypeStruct((tokens, local_len, 2 * DH), low),
            jax.ShapeDtypeStruct((width, 6 * DH), low),
            jax.ShapeDtypeStruct((buckets, width), low),
        ),
        in_specs=[pl.BlockSpec(memory_space=pltpu.VMEM)] * 4,
        out_specs=[pl.BlockSpec(memory_space=pltpu.VMEM)] * 9,
        scratch_shapes=[
            pltpu.VMEM((full_len, BLOCK), wide),
            pltpu.VMEM((2, pad_blocks, BLOCK, band_width), wide),
            pltpu.VMEM((BLOCK, full_len + buckets), wide),
            pltpu.VMEM((2, 2, 16, full_len), wide),
            pltpu.VMEM((2, full_len, DH), low),
        ],
        compiler_params=pltpu.CompilerParams(vmem_limit_bytes=ATTEND_VMEM),
        name="attend",
    )(xs, qkvs, tables, vecs)


def attend_back_kernel(
    q_ref,
    k_ref,
    v_ref,
    qrev_ref,
    krev_ref,
    p_ref,
    mix_ref,
    attn_ref,
    dcat_ref,
    rel_ref,
    sum_ref,
    heads_ref,
    wide_ref,
    low_ref,
    place_ref,
    dq_ref,
    dkt_ref,
    dvt_ref,
    far_ref,
    dkr_ref,
    dqr_ref,
):
    full_len = q_ref.shape[1]
    buckets = qrev_ref.shape[1]
    blocks = full_len // BLOCK
    span = buckets // 2
    side = span // BLOCK
    band_width = buckets + BLOCK
    band_blocks = band_width // BLOCK
    scale = 1.0 / math.sqrt(3.0 * DH)
    units = p_ref.shape[0]
    for ref in (wide_ref, low_ref, place_ref, dq_ref, dkt_ref, dvt_ref, far_ref, dkr_ref, dqr_ref):
        ref[...] = jnp.zeros_like(ref)
    at = Place()
    group = 2 * DH
    first_row = pl.multiple_of((3 * at.chip + at.core) * DH, DH)
    mix_rows = mix_ref[pl.ds(first_row, group)]
    dctx = dot_nt(attn_ref[...].reshape(full_len, attn_ref.shape[2]), mix_rows)
    for slot in range(2):
        heads_ref[slot] = dctx[:, slot * DH : (slot + 1) * DH].astype(jnp.bfloat16)
    first = at.core * (blocks // 2)
    turn = turn_matrix(BLOCK)
    place8 = lax.broadcasted_iota(jnp.int32, (8, full_len), 0)

    def unit(u, carry):
        g = u + first
        slot = g // blocks
        qb = g % blocks
        start = pl.multiple_of(qb * BLOCK, BLOCK)
        rows = q_ref[slot, pl.ds(start, BLOCK)]
        grad = heads_ref[slot, pl.ds(start, BLOCK)]
        probs = p_ref[u]
        wide_probs = probs.astype(jnp.float32)
        prob_grad = dot_nt(grad, v_ref[slot])
        inner = jnp.sum(wide_probs * prob_grad, axis=-1, keepdims=True)
        low_grad = (wide_probs * (prob_grad - inner)).astype(jnp.bfloat16)
        score_grad = low_grad.astype(jnp.float32)
        wide_ref[:, span : span + full_len] = dot_nn(turn, low_grad)
        low_ref[:, span : span + full_len] = low_grad
        dvt_ref[slot] += dot_tn(grad, probs)
        dkt_ref[slot] += dot_tn(rows, low_grad)
        row = lax.broadcasted_iota(jnp.int32, (BLOCK, full_len), 0)
        lane = lax.broadcasted_iota(jnp.int32, (BLOCK, full_len), 1)
        gap = lane - row - start
        right = jnp.where(gap > span, score_grad, 0.0)
        left = jnp.where(gap < 1 - span, score_grad, 0.0)
        end_right = jnp.sum(right, axis=-1, keepdims=True)
        end_left = jnp.sum(left, axis=-1, keepdims=True)
        far_right = jnp.sum(jnp.where(gap >= span, score_grad, 0.0), axis=0, keepdims=True)
        far_left = jnp.sum(jnp.where(gap < -span, score_grad, 0.0), axis=0, keepdims=True)
        far_ref[slot] += jnp.where(place8 == 0, far_right, jnp.where(place8 == 1, far_left, 0.0))
        band = wide_ref[:, pl.ds(start, band_width)]
        near = dot_nn(turn, skew_back(band, buckets).astype(jnp.bfloat16))
        bucket = lax.broadcasted_iota(jnp.int32, (BLOCK, buckets), 1)
        near = near + jnp.where(
            bucket == 0, end_left, jnp.where(bucket == buckets - 1, end_right, 0.0)
        )
        near_low = near.astype(jnp.bfloat16)
        dq = dot_nn(low_grad, k_ref[slot]) + dot_nn(near_low, krev_ref[slot])
        dq_ref[slot, pl.ds(start, BLOCK)] = dq
        dkr_ref[slot] += dot_tn(rows, near_low)
        for e in range(band_blocks):
            keys_at = pl.multiple_of(start + e * BLOCK, BLOCK)
            place_ref[
                slot, qb + e, :, (band_blocks - 1 - e) * BLOCK : (band_blocks - e) * BLOCK
            ] = dot_nt(turn, low_ref[:, pl.ds(keys_at, BLOCK)])
        return carry

    lax.fori_loop(0, units, unit, 0)
    parts_q, parts_k, parts_v = [], [], []
    parts_r = [None] * 4
    for slot in range(2):
        far_low = far_ref[slot].astype(jnp.bfloat16)
        mark = lax.broadcasted_iota(jnp.int32, (8, DH), 0)
        ends = jnp.where(
            mark == 0,
            qrev_ref[slot, 0:1].astype(jnp.float32),
            jnp.where(mark == 1, qrev_ref[slot, buckets - 1 : buckets].astype(jnp.float32), 0.0),
        ).astype(jnp.bfloat16)
        end_keys = dot_tn(ends, far_low)
        end_rows = dot_nn(far_low, k_ref[slot])

        whole_k = (dkt_ref[slot] + end_keys).T

        def key_side(kb, carry):
            start = pl.multiple_of(kb * BLOCK, BLOCK)
            far = skew_back(place_ref[slot, kb + side], buckets).astype(jnp.bfloat16)
            far = dot_nn(turn, far).astype(jnp.bfloat16)
            keys = k_ref[slot, pl.ds(start, BLOCK)]
            dqr_ref[slot] += dot_tn(keys, far)
            dq_ref[2 + slot, pl.ds(start, BLOCK)] = dot_nn(far, qrev_ref[slot])
            return carry

        lax.fori_loop(0, blocks, key_side, 0)
        parts_q.append((dq_ref[slot] * scale).astype(jnp.bfloat16))
        parts_k.append(((dq_ref[2 + slot] + whole_k) * scale).astype(jnp.bfloat16))
        parts_v.append(dvt_ref[slot].T.astype(jnp.bfloat16))
        bucket = lax.broadcasted_iota(jnp.int32, (buckets, DH), 0)
        qr = dqr_ref[slot].T + jnp.where(
            bucket == 0, end_rows[0:1], jnp.where(bucket == buckets - 1, end_rows[1:2], 0.0)
        )
        dqr_out = qr * scale
        dkr_out = dkr_ref[slot].T * scale
        parts_r[slot] = dqr_out
        parts_r[2 + slot] = dkr_out
    dcat = jnp.concatenate(parts_q + parts_k + parts_v, axis=1)
    dcat_ref[...] = dcat
    rel = jnp.concatenate(parts_r, axis=1)
    rel_ref[...] = dot_nn(turn_matrix(buckets), rel.astype(jnp.bfloat16)).astype(jnp.bfloat16)
    rel_sum = jnp.sum(rel, axis=0, keepdims=True)
    rel_sum = jnp.concatenate([rel_sum, jnp.zeros((1, 2 * DH), jnp.float32)], axis=1)
    sums = jnp.sum(dcat.astype(jnp.float32), axis=0, keepdims=True) + rel_sum
    sum_ref[...] = jnp.broadcast_to(sums, sum_ref.shape)


def attend_back(q, k, v, qrev, krev, probs, m_mix, attn_all):
    full_len = q.shape[1]
    buckets = qrev.shape[1]
    blocks = full_len // BLOCK
    band_width = buckets + BLOCK
    low, wide = jnp.bfloat16, jnp.float32
    pad_blocks = blocks + band_width // BLOCK - 1
    return pl.pallas_call(
        attend_back_kernel,
        out_shape=(
            jax.ShapeDtypeStruct((full_len, 6 * DH), low),
            jax.ShapeDtypeStruct((buckets, 4 * DH), low),
            jax.ShapeDtypeStruct((8, 6 * DH), wide),
        ),
        in_specs=[pl.BlockSpec(memory_space=pltpu.VMEM)] * 8,
        out_specs=[pl.BlockSpec(memory_space=pltpu.VMEM)] * 3,
        scratch_shapes=[
            pltpu.VMEM((2, full_len, DH), low),
            pltpu.VMEM((BLOCK, full_len + buckets), wide),
            pltpu.VMEM((BLOCK, full_len + buckets), low),
            pltpu.VMEM((2, pad_blocks, BLOCK, band_width), wide),
            pltpu.VMEM((4, full_len, DH), wide),
            pltpu.VMEM((2, DH, full_len), wide),
            pltpu.VMEM((2, DH, full_len), wide),
            pltpu.VMEM((2, 8, full_len), wide),
            pltpu.VMEM((2, DH, buckets), wide),
            pltpu.VMEM((2, DH, buckets), wide),
        ],
        compiler_params=pltpu.CompilerParams(vmem_limit_bytes=BACK_VMEM),
        name="attend_back",
    )(q, k, v, qrev, krev, probs, m_mix, attn_all)


MESH = pl.DeviceIdType.MESH
VMEM_SPEC = pl.BlockSpec(memory_space=pltpu.VMEM)
HBM_SPEC = pl.BlockSpec(memory_space=pltpu.HBM)
CHUNKS = 2


class Place:
    def __init__(self):
        self.batches = lax.axis_size("batch")
        self.tokens = lax.axis_size("seq")
        self.chips = self.tokens // 2
        self.row = lax.axis_index("batch")
        self.part = lax.axis_index("seq")
        self.chip = self.part // 2
        self.core = self.part % 2

    def along_chips(self, k):
        chip = lax.rem(self.chip + k, self.chips)
        return chip, (self.row, 2 * chip + self.core)

    def from_chips(self, k):
        return lax.rem(self.chip + self.chips - k, self.chips)

    def partner(self):
        return (self.row, self.part + 1 - 2 * self.core)

    def along_rows(self, k):
        row = lax.rem(self.row + k, self.batches)
        return row, (row, self.part)

    def from_rows(self, k):
        return lax.rem(self.row + self.batches - k, self.batches)

    def along_seq(self, k):
        part = lax.rem(self.part + k, self.tokens)
        return part, (self.row, part)

    def along_plane(self, k):
        index = lax.rem(2 * self.row + self.core + k, 2 * self.batches)
        row, core = index // 2, index % 2
        return row, core, (row, 2 * self.chip + core)

    def chip_peers(self):
        return [self.along_chips(k)[1] for k in range(1, self.chips)]

    def row_peers(self):
        return [self.along_rows(k)[1] for k in range(1, self.batches)]

    def cross_peers(self):
        other = self.part + 1 - 2 * self.core
        return [(self.along_rows(k)[0], other) for k in range(1, self.batches)]

    def cross_row_peers(self):
        return self.row_peers() + self.cross_peers()

    def all_peers(self):
        peers = []
        for i in range(self.batches):
            row = lax.rem(self.row + i, self.batches)
            for j in range(self.tokens):
                if i or j:
                    peers.append((row, lax.rem(self.part + j, self.tokens)))
        return peers

    def seq_peers(self):
        return [self.along_seq(k)[1] for k in range(1, self.tokens)]

    def plane_peers(self):
        return [self.along_plane(k)[2] for k in range(1, 2 * self.batches)]


def meet(peers):
    barrier = pltpu.get_barrier_semaphore()
    for peer in peers:
        pl.semaphore_signal(barrier, inc=1, device_id=peer, device_id_type=MESH)
    pl.semaphore_wait(barrier, len(peers))


class Wires:
    def __init__(self, send_sems, recv_sems, local_sems):
        self.sems = (send_sems, recv_sems, local_sems)
        self.used = [0, 0]
        self.ends = []

    def send(self, src, dst, peer):
        k = self.used[0]
        self.used[0] += 1
        copy = pltpu.make_async_remote_copy(
            src_ref=src,
            dst_ref=dst,
            send_sem=self.sems[0].at[k],
            recv_sem=self.sems[1].at[k],
            device_id=peer,
            device_id_type=MESH,
        )
        copy.start()
        self.ends.append(copy.wait_send)
        return copy

    def local(self, src, dst):
        k = self.used[1]
        self.used[1] += 1
        copy = pltpu.make_async_copy(src, dst, self.sems[2].at[k])
        copy.start()
        return copy

    def finish(self):
        for end in self.ends:
            end()


def wire_scratch(sends, locals_count):
    return [
        pltpu.SemaphoreType.DMA((sends,)),
        pltpu.SemaphoreType.DMA((sends,)),
        pltpu.SemaphoreType.DMA((locals_count,)),
    ]


def comm_call(kernel, name, ident, out_shapes, inputs, sends, locals_count, scratch=(), spec=VMEM_SPEC):
    return pl.pallas_call(
        kernel,
        out_shape=tuple(out_shapes),
        in_specs=[spec] * len(inputs),
        out_specs=tuple([VMEM_SPEC] * len(out_shapes)),
        scratch_shapes=list(scratch) + wire_scratch(sends, locals_count),
        compiler_params=pltpu.CompilerParams(
            collective_id=ident, has_side_effects=True, vmem_limit_bytes=COMM_VMEM
        ),
        name=name,
    )(*inputs)


def like(array, *lead):
    return jax.ShapeDtypeStruct(tuple(lead) + tuple(array.shape), array.dtype)


def pick(values, index):
    out = jnp.int32(values[0])
    for i in range(1, len(values)):
        out = jnp.where(index == i, jnp.int32(values[i]), out)
    return out


def arrival_order(at):
    chips = range(at.chips)
    lists = [sorted((j for j in chips if j != z), key=lambda j: (abs(j - z), j)) for z in chips]
    return [pick([lists[z][t] for z in chips], at.chip) for t in range(at.chips - 1)]


def return_order(at):
    chips = range(at.chips)

    def away(j, z):
        end = at.chips - 1 if j < z else 0
        return (abs(j - end) + abs(end - z), j)

    lists = [sorted((j for j in chips if j != z), key=lambda j: away(j, z)) for z in chips]
    return [pick([lists[z][t] for z in chips], at.chip) for t in range(at.chips - 1)]


def far_order(at):
    chips = range(at.chips)
    lists = [sorted((j for j in chips if j != z), key=lambda j: (-abs(j - z), j)) for z in chips]
    return [pick([lists[z][t] for z in chips], at.chip) for t in range(at.chips - 1)]


def goes_on(at, j):
    above = jnp.logical_and(j < at.chip, at.chip < at.chips - 1)
    below = jnp.logical_and(j > at.chip, at.chip > 0)
    return jnp.logical_or(above, below)


def line_peer(at, step):
    return (at.row, 2 * (at.chip + step) + at.core)


class LineGather:
    def __init__(self, at, buf, slot, sems, own=None):
        self.at, self.buf, self.slot, self.own = at, buf, slot, own
        self.send_sems, self.recv_sems = sems
        self.rows = buf.shape[1] // CHUNKS

    def copy(self, j, h, step, k, own=False):
        window = pl.ds(h * self.rows, self.rows)
        home = self.buf.at[self.slot(j), window]
        src = self.own.at[window] if own and self.own is not None else home
        return pltpu.make_async_remote_copy(
            src_ref=src,
            dst_ref=home,
            send_sem=self.send_sems.at[k * CHUNKS + h],
            recv_sem=self.recv_sems.at[j * CHUNKS + h],
            device_id=line_peer(self.at, step),
            device_id_type=MESH,
        )

    def own_each(self, act):
        z, n = self.at.chip, self.at.chips
        for h in range(CHUNKS):

            @pl.when(z < n - 1)
            def _():
                act(self.copy(z, h, 1, z, own=True))

            @pl.when(z > 0)
            def _():
                act(self.copy(z, h, -1, n, own=True))

    def start(self):
        self.own_each(lambda copy: copy.start())

    def arrive(self, j):
        step = jnp.where(j < self.at.chip, 1, -1)
        for h in range(CHUNKS):
            self.copy(j, h, -step, j).wait_recv()

            @pl.when(goes_on(self.at, j))
            def _():
                self.copy(j, h, step, j).start()

    def drain(self, order):
        self.own_each(lambda copy: copy.wait_send())
        for j in order:
            step = jnp.where(j < self.at.chip, 1, -1)

            @pl.when(goes_on(self.at, j))
            def _():
                for h in range(CHUNKS):
                    self.copy(j, h, step, j).wait_send()


class LineReduce:
    def __init__(self, at, part, got, sems):
        self.at, self.part, self.got = at, part, got
        self.send_sems, self.recv_sems = sems
        self.rows = part.shape[1] // CHUNKS

    def copy(self, j, h):
        z, n = self.at.chip, self.at.chips
        window = pl.ds(h * self.rows, self.rows)
        slot = jnp.where(z + 1 == j, n, j)
        return pltpu.make_async_remote_copy(
            src_ref=self.part.at[j, window],
            dst_ref=self.got.at[slot, window],
            send_sem=self.send_sems.at[j * CHUNKS + h],
            recv_sem=self.recv_sems.at[slot * CHUNKS + h],
            device_id=line_peer(self.at, jnp.where(j < z, -1, 1)),
            device_id_type=MESH,
        )

    def landed(self, slot, h, step):
        window = pl.ds(h * self.rows, self.rows)
        return pltpu.make_async_remote_copy(
            src_ref=self.got.at[slot, window],
            dst_ref=self.got.at[slot, window],
            send_sem=self.send_sems.at[h],
            recv_sem=self.recv_sems.at[slot * CHUNKS + h],
            device_id=line_peer(self.at, step),
            device_id_type=MESH,
        )

    def send(self, j):
        for h in range(CHUNKS):
            self.copy(j, h).start()

    def send_last(self, j):
        @pl.when(jnp.logical_not(goes_on(self.at, j)))
        def _():
            self.send(j)

    def pass_on(self, order):
        z, n = self.at.chip, self.at.chips
        wide = jnp.float32

        @pl.when(jnp.logical_and(z > 0, z < n - 1))
        def _():
            for j in order:
                step = jnp.where(j < z, 1, -1)
                for h in range(CHUNKS):
                    self.landed(j, h, step).wait_recv()
                    window = pl.ds(h * self.rows, self.rows)
                    total = self.part[j, window].astype(wide) + self.got[j, window].astype(wide)
                    self.part[j, window] = total.astype(self.part.dtype)
                    self.copy(j, h).start()

    def clear(self):
        z, n = self.at.chip, self.at.chips

        @pl.when(z == n - 1)
        def _():
            self.got[z] = jnp.zeros(self.got.shape[1:], self.got.dtype)

        @pl.when(z == 0)
        def _():
            self.got[n] = jnp.zeros(self.got.shape[1:], self.got.dtype)

    def collect(self):
        z, n = self.at.chip, self.at.chips
        for h in range(CHUNKS):

            @pl.when(z < n - 1)
            def _():
                self.landed(z, h, 1).wait_recv()

            @pl.when(z > 0)
            def _():
                self.landed(n, h, -1).wait_recv()

        return self.got[z].astype(jnp.float32) + self.got[n].astype(jnp.float32)

    def drain(self, order):
        for j in order:
            for h in range(CHUNKS):
                self.copy(j, h).wait_send()


def gather_sems(chips):
    return [
        pltpu.SemaphoreType.DMA(((chips + 1) * CHUNKS,)),
        pltpu.SemaphoreType.DMA((chips * CHUNKS,)),
    ]


def reduce_sems(chips):
    return [
        pltpu.SemaphoreType.DMA((chips * CHUNKS,)),
        pltpu.SemaphoreType.DMA(((chips + 1) * CHUNKS,)),
    ]


def gather_kernel(
    x_ref, wq_ref, wk_ref, wv_ref, mix_ref, table_ref, vec_ref, up_ref, down_ref,
    xs_ref, qkvs_ref, mixs_ref, tables_ref, vecs_ref, up2_ref, down2_ref,
    line_send, line_recv, *sems,
):
    at = Place()
    wires = Wires(*sems)
    b, s, z, c = at.row, at.part, at.chip, at.core
    off_diagonal = b != z
    turned = (z, 2 * b + c)
    peers = at.seq_peers() + at.row_peers()
    barrier = pltpu.get_barrier_semaphore()
    for peer in peers:
        pl.semaphore_signal(barrier, inc=1, device_id=peer, device_id_type=MESH)

    @pl.when(off_diagonal)
    def _():
        pl.semaphore_signal(barrier, inc=1, device_id=turned, device_id_type=MESH)

    pl.semaphore_wait(barrier, len(peers) + off_diagonal.astype(jnp.int32))

    swaps, stays = [], []
    for i, ref in enumerate((wq_ref, wk_ref, wv_ref)):
        k = wires.used[0]
        wires.used[0] += 1
        swaps.append(
            pltpu.make_async_remote_copy(
                src_ref=ref,
                dst_ref=qkvs_ref.at[2 * z + c, i],
                send_sem=sems[0].at[k],
                recv_sem=sems[1].at[k],
                device_id=turned,
                device_id_type=MESH,
            )
        )
        stays.append(pltpu.make_async_copy(ref, qkvs_ref.at[2 * b + c, i], sems[2].at[i]))
        wires.used[1] += 1

    @pl.when(off_diagonal)
    def _():
        for swap in swaps:
            swap.start()

    @pl.when(jnp.logical_not(off_diagonal))
    def _():
        for stay in stays:
            stay.start()

    table_home = tables_ref.at[c, b, z]
    mix_home = mixs_ref.at[c, b, z]
    table_sends = [
        wires.send(table_ref, table_home, at.along_chips(k)[1]) for k in range(1, at.chips)
    ]
    kept = [wires.local(table_ref, table_home), wires.local(mix_ref, mix_home)]
    line = LineGather(at, xs_ref, lambda j: 2 * j + c, (line_send, line_recv), own=x_ref)
    line.start()
    last = [wires.send(vec_ref, vecs_ref.at[s], at.along_seq(k)[1]) for k in range(1, at.tokens)]
    mix_sends = [
        wires.send(mix_ref, mix_home, at.along_chips(k)[1]) for k in range(1, at.chips)
    ]
    last += [
        wires.send(x_ref, xs_ref.at[s], at.partner()),
        wires.send(up_ref, up2_ref, at.partner()),
        wires.send(down_ref, down2_ref, at.partner()),
    ]
    own = [
        wires.local(x_ref, xs_ref.at[s]),
        wires.local(vec_ref, vecs_ref.at[s]),
    ]

    @pl.when(off_diagonal)
    def _():
        for swap in swaps:
            swap.wait_recv()

    @pl.when(jnp.logical_not(off_diagonal))
    def _():
        for stay in stays:
            stay.wait()

    mine = qkvs_ref.at[2 * b + c]
    qkv_sends = [wires.send(mine, mine, at.along_rows(k)[1]) for k in range(1, at.batches)]
    last.append(wires.send(mine, mine, at.partner()))
    for copy in table_sends:
        copy.wait_recv()
    for copy in kept:
        copy.wait()
    mine = tables_ref.at[c, b]
    row_sends = [wires.send(mine, mine, at.along_rows(k)[1]) for k in range(1, at.batches)]
    last.append(wires.send(mine, mine, at.partner()))
    order = arrival_order(at)

    def arrived(j):
        line.arrive(j)
        home = xs_ref.at[2 * j + c]
        last.append(wires.send(home, home, at.partner()))

    arrived(order[0])
    for copy in mix_sends:
        copy.wait_recv()
    mine = mixs_ref.at[c, b]
    mix_rows = [wires.send(mine, mine, at.along_rows(k)[1]) for k in range(1, at.batches)]
    last.append(wires.send(mine, mine, at.partner()))
    arrived(order[1])
    for k in range(1, at.batches):
        qkv_sends[k - 1].wait_recv()
        home = qkvs_ref.at[2 * at.from_rows(k) + c]
        last.append(wires.send(home, home, at.partner()))
    for k in range(1, at.batches):
        row_sends[k - 1].wait_recv()
        home = tables_ref.at[c, at.from_rows(k)]
        last.append(wires.send(home, home, at.partner()))
    for j in order[2:]:
        arrived(j)
    for k in range(1, at.batches):
        mix_rows[k - 1].wait_recv()
        home = mixs_ref.at[c, at.from_rows(k)]
        last.append(wires.send(home, home, at.partner()))
    for copy in last:
        copy.wait_recv()
    for copy in own:
        copy.wait()
    wires.finish()
    line.drain(order)

    @pl.when(off_diagonal)
    def _():
        for swap in swaps:
            swap.wait_send()


def gather_inputs(x, w_query, w_key, w_value, w_mix, rel_table, vec, up, down):
    tokens, batches = lax.axis_size("seq"), lax.axis_size("batch")
    chips = tokens // 2
    outs = (
        like(x, tokens),
        like(w_query, tokens, 3),
        like(w_mix, 2, batches, chips),
        like(rel_table, 2, batches, chips),
        like(vec, tokens),
        like(up),
        like(down),
    )
    sends = 3 + 2 * (chips - 1) + tokens - 1 + 3 + 6 * (batches - 1) + 3 + chips - 1
    inputs = (x, w_query, w_key, w_value, w_mix, rel_table, vec, up, down)
    return comm_call(
        gather_kernel,
        "gather_inputs",
        0,
        outs,
        inputs,
        sends,
        7,
        scratch=gather_sems(chips),
        spec=HBM_SPEC,
    )


def norm_parts(values):
    average = jnp.mean(values, axis=-1, keepdims=True)
    centered = values - average
    variance = jnp.mean(centered * centered, axis=-1, keepdims=True)
    scale = lax.rsqrt(variance + norm_eps)
    return centered * scale, scale


def norm_back(grad, gain, unit, scale):
    inner = grad * gain
    mean = jnp.mean(inner, axis=-1, keepdims=True)
    slope = jnp.mean(inner * unit, axis=-1, keepdims=True)
    return scale * (inner - mean - unit * slope)


def line_pass(gather, reduce, order, work):
    def finish(j):
        work(j)
        reduce.send_last(j)

    for j in order:
        gather.arrive(j)
        finish(j)


def feed_kernel(
    ctx_ref, x_ref, mixs_ref, vecs_ref, up_ref, down_ref, up2_ref, down2_ref, out_grad_ref,
    output_ref, pre_grad_ref, sums_ref, attn_ref, mix_ref, ups_ref, downs_ref, upbs_ref,
    got_ref, hid_ref, act_ref, slope_ref, part_ref, ffn_ref, grad_ref, inner_ref,
    back_ref, backs_ref, up_away_ref, down_away_ref, upb_away_ref,
    up_got_ref, down_got_ref, upb_got_ref, upg_ref, downg_ref, upb_ref, vec_ref,
    hid_send, hid_recv, ffn_send, ffn_recv, grad_send, grad_recv, back_send, back_recv,
    attn_send, attn_recv, *sems,
):
    at = Place()
    wires = Wires(*sems)
    low, wide = jnp.bfloat16, jnp.float32
    b, s, z, c = at.row, at.part, at.chip, at.core
    order, returns = arrival_order(at), return_order(at)
    meet(at.seq_peers() + at.row_peers())
    last, own = [], []
    swaps = []
    for k in range(1, at.tokens):
        part, peer = at.along_seq(k)
        swaps.append(wires.send(ctx_ref.at[part], got_ref.at[s], peer))
    kept = wires.local(ctx_ref.at[s], got_ref.at[s])
    lanes = x_ref.shape[1] // at.tokens
    hidden_here = up_ref.shape[1]
    vec_ref[...] = jnp.concatenate(
        [vecs_ref[part, :, :lanes].astype(wide) for part in range(at.tokens)], axis=1
    )
    bias3 = vec_ref[3:4]
    gain1, gain2 = vec_ref[4:5], vec_ref[5:6]
    shift1, shift2 = vec_ref[6:7], vec_ref[7:8]
    bias_down = vec_ref[8:9]
    partner = s + 1 - 2 * c
    up_rows = hidden_here // BLOCK
    bias_up = jnp.concatenate(
        [vecs_ref[s, 10 + i : 11 + i].astype(wide) for i in range(up_rows)]
        + [vecs_ref[partner, 10 + i : 11 + i].astype(wide) for i in range(up_rows)],
        axis=1,
    )
    shard_rows = mixs_ref.shape[3]
    for part in range(at.tokens):
        mix_ref[part * shard_rows : (part + 1) * shard_rows] = jnp.concatenate(
            [mixs_ref[part % 2, row, part // 2] for row in range(at.batches)], axis=1
        )
    for copy in swaps:
        copy.wait_recv()
    kept.wait()
    pieces = []
    for chip in range(at.chips):
        left, right = got_ref[2 * chip], got_ref[2 * chip + 1]
        middle = left[:, DH:].astype(wide) + right[:, :DH].astype(wide)
        pieces += [left[:, :DH], middle.astype(low), right[:, DH:]]
    context = jnp.concatenate(pieces, axis=1)
    pre_norm = x_ref[...].astype(wide) + dot_nn(context, mix_ref[...]) + bias3
    unit1, scale1 = norm_parts(pre_norm)
    hidden = unit1 * gain1 + shift1
    hid_ref[z] = hidden.astype(low)
    hid_line = LineGather(at, hid_ref, lambda j: j, (hid_send, hid_recv))
    ffn_line = LineReduce(at, part_ref, ffn_ref, (ffn_send, ffn_recv))
    hid_line.start()
    ffn_line.clear()

    def ffn(chip):
        rows = hid_ref[chip]
        inner = jnp.concatenate(
            [dot_nn(rows, up_ref[...]), dot_nn(rows, up2_ref[...])], axis=1
        )
        inner = inner + bias_up
        cdf = 0.5 * (1.0 + lax.erf(inner * math.sqrt(0.5)))
        act = (inner * cdf).astype(low)
        slope_ref[chip] = cdf + inner * (
            jnp.exp(-0.5 * inner * inner) * (1.0 / math.sqrt(2.0 * math.pi))
        )
        act_ref[chip] = act
        part_ref[chip] = (
            dot_nn(act[:, :hidden_here], down_ref[...])
            + dot_nn(act[:, hidden_here:], down2_ref[...])
        ).astype(low)

    ffn(z)
    line_pass(hid_line, ffn_line, order, ffn)
    ffn_line.pass_on(returns)
    total = part_ref[z].astype(wide) + ffn_line.collect()
    mixed = hidden + total + bias_down
    unit2, scale2 = norm_parts(mixed)
    output_ref[...] = (unit2 * gain2 + shift2).astype(low)
    out_grad = out_grad_ref[...].astype(wide)
    mixed_grad = norm_back(out_grad, gain2, unit2, scale2)
    grad_ref[z] = mixed_grad.astype(low)
    grad_line = LineGather(at, grad_ref, lambda j: j, (grad_send, grad_recv))
    back_line = LineReduce(at, back_ref, backs_ref, (back_send, back_recv))
    grad_line.start()
    back_line.clear()
    gain2_grad = jnp.sum(out_grad * unit2, axis=0, keepdims=True)
    shift2_grad = jnp.sum(out_grad, axis=0, keepdims=True)
    downb_grad = jnp.sum(mixed_grad, axis=0, keepdims=True)

    def back(chip):
        rows = grad_ref[chip]
        act_grad = jnp.concatenate(
            [dot_nt(rows, down_ref[...]), dot_nt(rows, down2_ref[...])], axis=1
        )
        inner_low = (act_grad * slope_ref[chip]).astype(low)
        inner_ref[chip] = inner_low
        back_ref[chip] = (
            dot_nt(inner_low[:, :hidden_here], up_ref[...])
            + dot_nt(inner_low[:, hidden_here:], up2_ref[...])
        ).astype(low)

    back(z)
    line_pass(grad_line, back_line, order, back)
    width = x_ref.shape[1]
    columns = width // at.batches
    inner_all = inner_ref[...].reshape(at.chips * BLOCK, 2 * hidden_here)
    act_all = act_ref[...].reshape(at.chips * BLOCK, 2 * hidden_here)
    hid_all = hid_ref[...].reshape(at.chips * BLOCK, width)
    grad_all = grad_ref[...].reshape(at.chips * BLOCK, width)
    near, away = slice(0, hidden_here), slice(hidden_here, 2 * hidden_here)
    up_grad = dot_tn(hid_all, inner_all)
    up_away_ref[...] = up_grad[:, away].astype(low)
    down_grad = dot_tn(grad_all, act_all)
    down_away_ref[...] = down_grad[:, away].astype(low)
    upb_grad = jnp.sum(inner_all.astype(wide), axis=0, keepdims=True)
    upb_away_ref[...] = jnp.broadcast_to(upb_grad[:, away], upb_away_ref.shape)
    halves = [
        wires.send(up_away_ref, up_got_ref, at.partner()),
        wires.send(down_away_ref, down_got_ref, at.partner()),
        wires.send(upb_away_ref, upb_got_ref, at.partner()),
    ]
    back_line.pass_on(returns)
    for copy in halves:
        copy.wait_recv()
    upb_ref[...] = jnp.broadcast_to(upb_grad[:, near], upb_ref.shape) + upb_got_ref[...]
    up_sum = (up_grad[:, near] + up_got_ref[...].astype(wide)).astype(low)
    down_sum = (down_grad[:, near] + down_got_ref[...].astype(wide)).astype(low)
    for row in range(at.batches):
        upg_ref[row] = up_sum[row * columns : (row + 1) * columns]
        downg_ref[row] = down_sum[row * columns : (row + 1) * columns]
    for k in range(1, at.batches):
        row, peer = at.along_rows(k)
        last.append(wires.send(upg_ref.at[row], ups_ref.at[b], peer))
        last.append(wires.send(downg_ref.at[row], downs_ref.at[b], peer))
        last.append(wires.send(upb_ref, upbs_ref.at[b], peer))
    own.append(wires.local(upg_ref.at[b], ups_ref.at[b]))
    own.append(wires.local(downg_ref.at[b], downs_ref.at[b]))
    own.append(wires.local(upb_ref, upbs_ref.at[b]))
    total = back_ref[z].astype(wide) + back_line.collect()
    hidden_grad = mixed_grad + total
    pre_grad = norm_back(hidden_grad, gain1, unit1, scale1)
    attn_ref[s] = pre_grad.astype(low)
    attn_line = LineGather(at, attn_ref, lambda j: 2 * j + c, (attn_send, attn_recv))
    attn_line.start()
    last.append(wires.send(attn_ref.at[s], attn_ref.at[s], at.partner()))
    pre_grad_ref[...] = pre_grad
    gain1_grad = jnp.sum(hidden_grad * unit1, axis=0, keepdims=True)
    shift1_grad = jnp.sum(hidden_grad, axis=0, keepdims=True)
    bias3_grad = jnp.sum(pre_grad, axis=0, keepdims=True)
    sums = jnp.concatenate(
        [bias3_grad, gain1_grad, gain2_grad, shift1_grad, shift2_grad, downb_grad]
        + [jnp.zeros((2, width), wide)],
        axis=0,
    )
    spare = jnp.zeros((8, BLOCK - lanes), wide)
    for part in range(at.tokens):
        sums_ref[part] = jnp.concatenate(
            [sums[:, part * lanes : (part + 1) * lanes], spare], axis=1
        )
    for j in order:
        attn_line.arrive(j)
        home = attn_ref.at[2 * j + c]
        last.append(wires.send(home, home, at.partner()))
    for copy in last:
        copy.wait_recv()
    for copy in own:
        copy.wait()
    wires.finish()
    for line in (hid_line, ffn_line, grad_line, back_line, attn_line):
        line.drain(order)


def feed_forward(ctx, x, mixs, vecs, up, down, up2, down2, out_grad, ident):
    tokens, batches = lax.axis_size("seq"), lax.axis_size("batch")
    chips = tokens // 2
    width = x.shape[1]
    columns = width // batches
    hidden_here = up.shape[1]
    low, wide = jnp.bfloat16, jnp.float32
    outs = (
        jax.ShapeDtypeStruct(x.shape, low),
        jax.ShapeDtypeStruct(x.shape, wide),
        jax.ShapeDtypeStruct((tokens, 8, BLOCK), wide),
        jax.ShapeDtypeStruct((tokens,) + x.shape, low),
        jax.ShapeDtypeStruct((width, width), low),
        jax.ShapeDtypeStruct((batches, columns, hidden_here), low),
        jax.ShapeDtypeStruct((batches, columns, hidden_here), low),
        jax.ShapeDtypeStruct((batches, 8, hidden_here), wide),
    )
    block = (chips,) + x.shape
    wide_block = (chips, x.shape[0], 2 * hidden_here)
    slots = (chips + 1,) + x.shape
    up_half, bias_half = (width, hidden_here), (8, hidden_here)
    down_half = up_half
    scratch = [
        pltpu.VMEM(ctx.shape, low),
        pltpu.VMEM(block, low),
        pltpu.VMEM(wide_block, low),
        pltpu.VMEM(wide_block, wide),
        pltpu.VMEM(block, low),
        pltpu.VMEM(slots, low),
        pltpu.VMEM(block, low),
        pltpu.VMEM(wide_block, low),
        pltpu.VMEM(block, low),
        pltpu.VMEM(slots, low),
        pltpu.VMEM(up_half, low),
        pltpu.VMEM(down_half, low),
        pltpu.VMEM(bias_half, wide),
        pltpu.VMEM(up_half, low),
        pltpu.VMEM(down_half, low),
        pltpu.VMEM(bias_half, wide),
        pltpu.VMEM((batches, columns, hidden_here), low),
        pltpu.VMEM((batches, columns, hidden_here), low),
        pltpu.VMEM(bias_half, wide),
        pltpu.VMEM((16, width), wide),
    ]
    scratch += (gather_sems(chips) + reduce_sems(chips)) * 2 + gather_sems(chips)
    inputs = (ctx, x, mixs, vecs, up, down, up2, down2, out_grad)
    sends = tokens - 1 + 2 * batches - 1 + 3 + 3 * (batches - 1) + chips
    return pl.pallas_call(
        feed_kernel,
        out_shape=outs,
        in_specs=[VMEM_SPEC] * len(inputs),
        out_specs=(VMEM_SPEC,) * len(outs),
        scratch_shapes=scratch + wire_scratch(sends, 5),
        compiler_params=pltpu.CompilerParams(
            collective_id=ident, has_side_effects=True, vmem_limit_bytes=FEED_VMEM
        ),
        name="feed_forward",
    )(*inputs)


def settle_kernel(
    vec_ref, col_ref, dcat_ref, rel_ref, w_ref, xs_ref, table_ref, ctx_ref, attn_ref,
    ins_ref, vec_all_ref, cols_ref, dw_all_ref, tab_all_ref, mix_all_ref,
    in_ref, dw_ref, tab_ref, mix_ref, half_ref, sum_ref, got_ref, vecs_ref, vec_low_ref,
    dws_ref, dw_low_ref, rels_ref, rel_low_ref, mixs_ref, mix_low_ref,
    line_send, line_recv, tab_send, tab_recv, *sems,
):
    at = Place()
    wires = Wires(*sems)
    low, wide = jnp.bfloat16, jnp.float32
    b, s, z, c = at.row, at.part, at.chip, at.core
    off_diagonal = b != z
    same, cross = (z, 2 * b + c), (z, 2 * b + 1 - c)
    meet(at.all_peers())
    width = w_ref.shape[0]
    columns = width // at.batches
    full_len = dcat_ref.shape[0]
    group = 2 * DH
    buckets = table_ref.shape[0]
    bucket_rows = buckets // at.batches

    dw_sends, mix_sends, vec_sends, rel_sends, last, own = [], [], [], [], [], []
    for k in range(1, at.batches):
        row, peer = at.along_rows(k)
        rows = pl.ds(pl.multiple_of(row * bucket_rows, bucket_rows), bucket_rows)
        rel_sends.append(wires.send(rel_ref.at[rows], rels_ref.at[k - 1], peer))

    def input_part(chip, core):
        start = pl.multiple_of((2 * chip + core) * BLOCK, BLOCK)
        in_ref[chip, core] = dot_nt(dcat_ref[pl.ds(start, BLOCK)], w_ref[...]).astype(low)

    order = far_order(at)
    places = order + [z]
    halves = []
    for chip in places:
        input_part(chip, 1 - c)
        halves.append(wires.send(in_ref.at[chip, 1 - c], half_ref.at[chip], at.partner()))
    line = LineReduce(at, sum_ref, got_ref, (line_send, line_recv))
    line.clear()
    for i, chip in enumerate(places):
        input_part(chip, c)
        halves[i].wait_recv()
        total = in_ref[chip, c].astype(wide) + half_ref[chip].astype(wide)
        sum_ref[chip] = total.astype(low)
        if i < len(order):
            line.send_last(chip)

    for k in range(1, at.tokens):
        part, peer = at.along_seq(k)
        vec_sends.append(wires.send(vec_ref.at[part], vecs_ref.at[k - 1], peer))
    mine = 2 * b + c
    for k in range(1, 2 * at.batches):
        last.append(wires.send(col_ref, cols_ref.at[mine], at.along_plane(k)[2]))
    own.append(wires.local(col_ref, cols_ref.at[mine]))

    whole = xs_ref[...].reshape(full_len, width)
    dw = dot_tn(whole, dcat_ref[...])
    dw_rel = dot_tn(table_ref[...], rel_ref[...])
    dw = jnp.concatenate([dw[:, : 2 * group] + dw_rel, dw[:, 2 * group :]], axis=1)
    for row in range(at.batches):
        dw_ref[row] = dw[row * columns : (row + 1) * columns].astype(low)
    for k in range(1, at.batches):
        row, peer = at.along_rows(k)
        dw_sends.append(wires.send(dw_ref.at[row], dws_ref.at[k - 1], peer))
    line.pass_on(order)

    rows = pl.ds(pl.multiple_of(b * bucket_rows, bucket_rows), bucket_rows)
    total = rel_ref[rows].astype(wide)
    for k in range(1, at.batches):
        rel_sends[k - 1].wait_recv()
        total = total + rels_ref[k - 1].astype(wide)
    rel_low_ref[...] = total.astype(low)
    table_rows = bucket_rows // 2
    for row in range(at.batches):
        piece = dot_nt(rel_low_ref[...], w_ref[row * columns : (row + 1) * columns, : 2 * group])
        for core in range(2):
            tab_ref[core, row] = piece[core * table_rows : (core + 1) * table_rows].astype(low)

    def tab_copy(k, d):
        row = lax.rem(b + k, at.batches)
        core = jnp.where(d == 0, c, 1 - c)
        return pltpu.make_async_remote_copy(
            src_ref=tab_ref.at[core, row],
            dst_ref=tab_all_ref.at[s],
            send_sem=tab_send.at[2 * k + d],
            recv_sem=tab_recv.at[s],
            device_id=(row, 2 * b + core),
            device_id_type=MESH,
        )

    tab_stay = pltpu.make_async_copy(
        tab_ref.at[c, b], tab_all_ref.at[s], sems[2].at[wires.used[1]]
    )
    wires.used[1] += 1
    for k in range(at.batches):
        for d in range(2):
            if k or d:
                tab_copy(k, d).start()

    @pl.when(off_diagonal)
    def _():
        tab_copy(0, 0).start()

    @pl.when(jnp.logical_not(off_diagonal))
    def _():
        tab_stay.start()

    mix = dot_tn(
        ctx_ref[...].reshape(full_len, group), attn_ref[...].reshape(full_len, width)
    )
    for row in range(at.batches):
        mix_ref[row] = mix[:, row * columns : (row + 1) * columns].astype(low)
    for k in range(1, at.batches):
        row, peer = at.along_rows(k)
        mix_sends.append(wires.send(mix_ref.at[row], mixs_ref.at[k - 1], peer))

    total = vec_ref[s]
    for k in range(1, at.tokens):
        vec_sends[k - 1].wait_recv()
        total = total + vecs_ref[k - 1]
    vec_low_ref[...] = total
    for k in range(1, at.batches):
        last.append(wires.send(vec_low_ref, vec_all_ref.at[b], at.along_rows(k)[1]))
    own.append(wires.local(vec_low_ref, vec_all_ref.at[b]))

    total = dw_ref[b].astype(wide)
    for k in range(1, at.batches):
        dw_sends[k - 1].wait_recv()
        total = total + dws_ref[k - 1].astype(wide)
    shard_rows = dw_low_ref.shape[1]
    for half in range(2):
        dw_low_ref[half] = total[half * shard_rows : (half + 1) * shard_rows].astype(low)
    k = wires.used[0]
    wires.used[0] += 1
    move = pltpu.make_async_remote_copy(
        src_ref=dw_low_ref.at[c],
        dst_ref=dw_all_ref.at[c],
        send_sem=sems[0].at[k],
        recv_sem=sems[1].at[k],
        device_id=same,
        device_id_type=MESH,
    )
    stay = pltpu.make_async_copy(
        dw_low_ref.at[c], dw_all_ref.at[c], sems[2].at[wires.used[1]]
    )
    wires.used[1] += 1

    @pl.when(off_diagonal)
    def _():
        move.start()

    @pl.when(jnp.logical_not(off_diagonal))
    def _():
        stay.start()

    last.append(wires.send(dw_low_ref.at[1 - c], dw_all_ref.at[c], cross))

    total = mix_ref[b].astype(wide)
    for k in range(1, at.batches):
        mix_sends[k - 1].wait_recv()
        total = total + mixs_ref[k - 1].astype(wide)
    mix_low_ref[...] = total.astype(low)
    last.append(wires.send(mix_low_ref, mix_all_ref.at[c], at.partner()))
    own.append(wires.local(mix_low_ref, mix_all_ref.at[c]))

    ins_ref[...] = sum_ref[z].astype(wide) + line.collect()
    for copy in last:
        copy.wait_recv()
    for copy in own:
        copy.wait()
    wires.finish()
    line.drain(order)
    for part in range(at.tokens):
        landed = pltpu.make_async_remote_copy(
            src_ref=tab_all_ref.at[part],
            dst_ref=tab_all_ref.at[part],
            send_sem=tab_send.at[0],
            recv_sem=tab_recv.at[part],
            device_id=at.partner(),
            device_id_type=MESH,
        )

        @pl.when(jnp.logical_or(off_diagonal, s != part))
        def _():
            landed.wait_recv()

    for k in range(at.batches):
        for d in range(2):
            if k or d:
                tab_copy(k, d).wait_send()

    @pl.when(off_diagonal)
    def _():
        tab_copy(0, 0).wait_send()
        move.wait()

    @pl.when(jnp.logical_not(off_diagonal))
    def _():
        tab_stay.wait()
        stay.wait()


def settle_grads(vec, cols, dcat, rel, w_cat, xs, table, ctx, attn_all, ident):
    tokens, batches = lax.axis_size("seq"), lax.axis_size("batch")
    chips = tokens // 2
    low, wide = jnp.bfloat16, jnp.float32
    local_len, width = xs.shape[1:]
    columns, group = width // batches, dcat.shape[1]
    buckets = table.shape[0]
    half = (chips, local_len, width)
    dw_pieces = (2, columns // 2, group)
    mix_piece = (2 * DH, columns)
    dw_piece, rel_piece = (columns, group), (buckets // batches, rel.shape[1])
    outs = (
        jax.ShapeDtypeStruct((local_len, width), wide),
        jax.ShapeDtypeStruct((batches,) + vec.shape[1:], wide),
        like(cols, 2 * batches),
        jax.ShapeDtypeStruct(dw_pieces, low),
        jax.ShapeDtypeStruct((tokens, buckets // tokens, columns), low),
        jax.ShapeDtypeStruct((2,) + mix_piece, low),
    )
    scratch = [
        pltpu.VMEM((chips, 2, local_len, width), low),
        pltpu.VMEM((batches,) + dw_piece, low),
        pltpu.VMEM((2, batches, buckets // tokens, columns), low),
        pltpu.VMEM((batches,) + mix_piece, low),
        pltpu.VMEM(half, low),
        pltpu.VMEM(half, low),
        pltpu.VMEM((chips + 1, local_len, width), low),
        pltpu.VMEM((tokens - 1,) + vec.shape[1:], wide),
        pltpu.VMEM(vec.shape[1:], wide),
        pltpu.VMEM((batches - 1,) + dw_piece, low),
        pltpu.VMEM(dw_pieces, low),
        pltpu.VMEM((batches - 1,) + rel_piece, low),
        pltpu.VMEM(rel_piece, low),
        pltpu.VMEM((batches - 1,) + mix_piece, low),
        pltpu.VMEM(mix_piece, low),
    ]
    scratch += reduce_sems(chips)
    scratch += [pltpu.SemaphoreType.DMA((2 * batches,)), pltpu.SemaphoreType.DMA((tokens,))]
    sends = 4 * (batches - 1) + chips + tokens - 1 + 2 * batches - 1 + 3
    inputs = (vec, cols, dcat, rel, w_cat, xs, table, ctx, attn_all)
    return comm_call(settle_kernel, "settle_grads", ident, outs, inputs, sends, 6, scratch=scratch)


def finish_kernel(
    pre_ref, ins_ref, vecs_ref, cols_ref, dws_ref, tabs_ref, mixs_ref, ups_ref, downs_ref,
    upbs_ref, last_ref,
    output_ref, input_ref, dq_ref, dk_ref, dv_ref, mix_ref, table_ref, bias_ref, gain_ref, shift_ref,
    up_ref, upb_ref, down_ref, downb_ref,
):
    at = Place()
    wide = jnp.float32

    def total(ref):
        out = ref[0].astype(wide)
        for k in range(1, ref.shape[0]):
            out = out + ref[k].astype(wide)
        return out

    output_ref[...] = last_ref[...]
    input_ref[...] = pre_ref[...] + ins_ref[...]
    up_ref[...] = total(ups_ref)
    down_ref[...] = total(downs_ref)
    upb_ref[...] = total(upbs_ref)[0:1]
    table_ref[...] = total(tabs_ref)
    group = 2 * DH
    spare = jnp.zeros((dws_ref.shape[1], DH), wide)
    for i, ref in enumerate((dq_ref, dk_ref, dv_ref)):
        lower = dws_ref[0, :, i * group : (i + 1) * group].astype(wide)
        upper = dws_ref[1, :, i * group : (i + 1) * group].astype(wide)
        ref[...] = jnp.concatenate([lower, spare], axis=1) + jnp.concatenate(
            [spare, upper], axis=1
        )
    rows = mix_ref.shape[0]
    lower, upper = mixs_ref[0].astype(wide), mixs_ref[1].astype(wide)
    spare = jnp.zeros((DH, lower.shape[1]), wide)
    whole = jnp.concatenate([lower, spare], axis=0) + jnp.concatenate([spare, upper], axis=0)
    mix_ref[...] = jnp.where(at.core == 0, whole[:rows], whole[rows:])
    small = total(vecs_ref)
    lanes = bias_ref.shape[1]
    cols = [cols_ref[core, 0:1] for core in range(2)]
    for row in range(1, at.batches):
        cols = [cols[core] + cols_ref[2 * row + core, 0:1] for core in range(2)]
    spare = jnp.zeros((1, DH), wide)
    biases = []
    for i in range(3):
        lower, upper = [part[:, i * group : (i + 1) * group] for part in cols]
        both = jnp.concatenate([lower, spare], axis=1) + jnp.concatenate([spare, upper], axis=1)
        biases.append(jnp.where(at.core == 0, both[:, :lanes], both[:, lanes:]))
    bias_ref[...] = jnp.concatenate(biases + [small[0:1, :lanes]], axis=0)
    gain_ref[...] = small[1:3, :lanes]
    shift_ref[...] = small[3:5, :lanes]
    downb_ref[...] = small[5:6, :lanes]


def finish(pre_grad, parts, shapes):
    inputs = (pre_grad,) + tuple(parts)
    return pl.pallas_call(
        finish_kernel,
        out_shape=(like(parts[-1]),)
        + tuple(jax.ShapeDtypeStruct(shape, jnp.float32) for shape in shapes),
        in_specs=[VMEM_SPEC] * len(inputs),
        out_specs=(VMEM_SPEC,) * (len(shapes) + 1),
        compiler_params=pltpu.CompilerParams(vmem_limit_bytes=COMM_VMEM),
        name="finish",
    )(*inputs)


def fits_fast(layer_input, table_shard, hidden_here):
    rows, local_len, width = layer_input.shape
    tokens, batches = lax.axis_size("seq"), lax.axis_size("batch")
    return (
        rows == 1
        and local_len == BLOCK
        and tokens == 2 * batches
        and width == 3 * DH * batches
        and (table_shard.shape[0] * tokens) % (4 * BLOCK) == 0
        and tokens == 8
        and 10 + hidden_here // BLOCK <= 16
        and hidden_here % BLOCK == 0
    )


def fast_body(
    layer_input, segment_ids, w_query, w_key, w_value, w_mix, rel_table, attn_biases,
    norm_gains, norm_shifts, w_up, up_bias, w_down, down_bias, out_grad,
):
    local_len, width = layer_input.shape[1:]
    low = jnp.bfloat16
    shard_rows, shard_cols = w_query.shape
    lanes = attn_biases.shape[1]
    hidden_here = w_up.shape[1]
    x = layer_input[0]
    pack = jnp.concatenate([attn_biases, norm_gains, norm_shifts, down_bias[None]], axis=0)
    pack = jnp.pad(pack, ((0, 0), (0, BLOCK - lanes)))
    pack = jnp.concatenate(
        [pack, segment_ids.astype(low), up_bias.reshape(hidden_here // BLOCK, BLOCK)], axis=0
    )
    pack = jnp.pad(pack, ((0, 16 - pack.shape[0]), (0, 0)))
    weights = (w_query, w_key, w_value, w_mix, rel_table, pack, w_up, w_down)
    xs, qkvs, mixs, tables, vecs, up2, down2 = gather_inputs(
        *[pltpu.with_memory_space_constraint(a, pltpu.HBM) for a in (x,) + weights]
    )
    q, k, v, qrev, krev, probs, ctx, w_cat, table = attend(xs, qkvs, tables, vecs)
    output, pre_grad, sums, attn_all, m_mix, ups, downs, upbs = feed_forward(
        ctx, x, mixs, vecs, w_up, w_down, up2, down2, out_grad[0], 1
    )
    dcat, rel_grad, cols = attend_back(q, k, v, qrev, krev, probs, m_mix, attn_all)
    ins, vec_all, cols_all, dw_all, tab_all, mix_all = settle_grads(
        sums, cols, dcat, rel_grad, w_cat, xs, table, ctx, attn_all, 2
    )
    shard = (shard_rows, shard_cols)
    shapes = (
        x.shape, shard, shard, shard, shard, rel_table.shape, (4, lanes), (2, lanes), (2, lanes),
        (width // lax.axis_size("batch"), hidden_here), (1, hidden_here),
        (width // lax.axis_size("batch"), hidden_here), (1, lanes),
    )
    grads = finish(
        pre_grad,
        (ins, vec_all, cols_all, dw_all, tab_all, mix_all, ups, downs, upbs, output),
        shapes,
    )
    output, input_grad, dq, dk, dv, dmix, dtable = grads[:7]
    dbias, dgain, dshift, dup, dupb, ddown, ddownb = grads[7:]
    return (
        output[None], input_grad[None], dq, dk, dv, dmix, dtable, dbias, dgain, dshift,
        dup, dupb.reshape(hidden_here), ddown.T, ddownb.reshape(lanes),
    )


def body(
    layer_input,
    segment_ids,
    w_query,
    w_key,
    w_value,
    w_mix,
    rel_table,
    attn_biases,
    norm_gains,
    norm_shifts,
    w_up,
    up_bias,
    w_down,
    down_bias,
    out_grad,
):
    if fits_fast(layer_input, rel_table, w_up.shape[1]):
        return fast_body(
            layer_input, segment_ids, w_query, w_key, w_value, w_mix, rel_table, attn_biases,
            norm_gains, norm_shifts, w_up, up_bias, w_down, down_bias, out_grad,
        )
    rows, local_len, width = layer_input.shape
    full_len = local_len * lax.axis_size("seq")
    tokens_here = local_len * rows
    highest_prec = lax.Precision.HIGHEST
    parts = (
        lax.all_gather(w_query, "batch", axis=1, tiled=True),
        lax.all_gather(w_key, "batch", axis=1, tiled=True),
        lax.all_gather(w_value, "batch", axis=1, tiled=True),
        lax.all_gather(w_mix, "batch", axis=1, tiled=True),
        lax.all_gather(rel_table, "batch", axis=1, tiled=True),
    )
    whole = (
        lax.all_gather(parts[0], "seq", axis=0, tiled=True),
        lax.all_gather(parts[1], "seq", axis=0, tiled=True),
        lax.all_gather(parts[2], "seq", axis=0, tiled=True),
        lax.all_gather(parts[3], "seq", axis=0, tiled=True),
        lax.all_gather(parts[4], "seq", axis=0, tiled=True),
        lax.all_gather(attn_biases, "seq", axis=1, tiled=True),
        lax.all_gather(norm_gains, "seq", axis=1, tiled=True),
        lax.all_gather(norm_shifts, "seq", axis=1, tiled=True),
        lax.all_gather(down_bias, "seq", axis=0, tiled=True),
    )
    m_query, m_key, m_value, m_mix, table, biases, gains, shifts, bias_down = whole
    flat_input = jnp.swapaxes(layer_input, 0, 1).reshape(tokens_here, width)
    queries = (jnp.dot(flat_input, m_query, preferred_element_type=jnp.float32) + biases[0]).astype(
        jnp.bfloat16
    )
    keys_here = (jnp.dot(flat_input, m_key, preferred_element_type=jnp.float32) + biases[1]).astype(
        jnp.bfloat16
    )
    values_here = (
        jnp.dot(flat_input, m_value, preferred_element_type=jnp.float32) + biases[2]
    ).astype(jnp.bfloat16)
    query_rel = (jnp.dot(table, m_query, preferred_element_type=jnp.float32) + biases[0]).astype(
        jnp.bfloat16
    )
    key_rel = (jnp.dot(table, m_key, preferred_element_type=jnp.float32) + biases[1]).astype(
        jnp.bfloat16
    )
    local_seg = jnp.swapaxes(segment_ids, 0, 1).astype(jnp.bfloat16)
    keys_all, values_all, seg_all = (
        lax.all_gather(keys_here.reshape(local_len, rows, width), "seq", axis=0, tiled=True),
        lax.all_gather(values_here.reshape(local_len, rows, width), "seq", axis=0, tiled=True),
        lax.all_gather(local_seg, "seq", axis=0, tiled=True),
    )
    buckets = table.shape[0]
    offset = lax.axis_index("seq") * local_len
    bucket_iota = jnp.arange(buckets, dtype=jnp.int32)
    inner_cols = (bucket_iota > 0) & (bucket_iota < buckets - 1)
    same_doc = (
        jnp.swapaxes(local_seg, 0, 1)[:, None, :, None]
        == jnp.swapaxes(seg_all, 0, 1)[:, None, None, :]
    )
    score_scale = 1.0 / math.sqrt(3.0 * DH)
    head_queries = split_heads(queries.reshape(local_len, rows, width))
    head_keys = split_heads(keys_all)
    head_values = split_heads(values_all)
    rel_queries = split_table(query_rel)
    rel_keys = split_table(key_rel)

    def forward_group(carry, group):
        g_query, g_key, g_value, g_qrel, g_krel = group
        total, near_pull, far_pull, window = relative_scores(
            g_query, g_key, g_krel, g_qrel, offset, full_len
        )
        scores = jnp.where(same_doc, total * score_scale, masked_score)
        highest = jnp.max(scores, axis=-1, keepdims=True)
        exponent = jnp.exp(scores - highest)
        denominator = jnp.sum(exponent, axis=-1, keepdims=True)
        weights_low = (exponent / denominator).astype(jnp.bfloat16)
        context = jnp.einsum(
            "rgij,rgjd->rgid", weights_low, g_value, preferred_element_type=jnp.float32
        )
        return (carry, (context, (highest + jnp.log(denominator))[..., 0]))

    unused, (context_groups, log_totals) = lax.scan(
        forward_group, None, (head_queries, head_keys, head_values, rel_queries, rel_keys)
    )
    context_low = join_heads(context_groups).reshape(tokens_here, width).astype(jnp.bfloat16)
    pre_norm = (
        flat_input.astype(jnp.float32)
        + jnp.dot(context_low, m_mix, preferred_element_type=jnp.float32)
        + biases[3]
    )
    hidden, norm1_pull = jax.vjp(
        normalize, pre_norm, gains[0].astype(jnp.float32), shifts[0].astype(jnp.float32)
    )
    hidden_low = hidden.astype(jnp.bfloat16)

    def spread_rows(rows_low):
        return lax.all_gather(rows_low, "seq", axis=0, tiled=True)

    def hidden_sums(make_term):
        return lax.psum_scatter(
            make_term(jnp.int32(0), tokens_here * lax.axis_size("seq")),
            "seq",
            scatter_dimension=0,
            tiled=True,
        )

    hidden_rows = spread_rows(hidden_low)
    inner = jnp.dot(hidden_rows, w_up, preferred_element_type=jnp.float32) + up_bias
    act, gelu_pull = jax.vjp(exact_gelu, inner)
    act_low = act.astype(jnp.bfloat16)

    def down_rows(start, count):
        return jnp.dot(act_low, w_down, preferred_element_type=jnp.float32)

    ffn_result = hidden_sums(down_rows)
    mixed = hidden + ffn_result + bias_down
    output, norm2_pull = jax.vjp(
        normalize, mixed, gains[1].astype(jnp.float32), shifts[1].astype(jnp.float32)
    )
    flat_grad = jnp.swapaxes(out_grad, 0, 1).reshape(tokens_here, width).astype(jnp.float32)
    mixed_grad, gain2_grad, shift2_grad = norm2_pull(flat_grad)
    ffn_grad_low = mixed_grad.astype(jnp.bfloat16)
    grad_rows = spread_rows(ffn_grad_low)
    act_grad = jnp.einsum("nd,fd->nf", grad_rows, w_down, preferred_element_type=jnp.float32)
    inner_low = gelu_pull(act_grad)[0].astype(jnp.bfloat16)
    up_part = jnp.einsum("nd,nf->df", hidden_rows, inner_low, preferred_element_type=jnp.float32)
    upb_part = jnp.sum(inner_low.astype(jnp.float32), axis=0)
    down_part = jnp.einsum("nf,nd->fd", act_low, grad_rows, preferred_element_type=jnp.float32)

    def back_rows(start, count):
        return jnp.einsum("nf,df->nd", inner_low, w_up, preferred_element_type=jnp.float32)

    hidden_grad = mixed_grad + hidden_sums(back_rows)
    pre_grad, gain1_grad, shift1_grad = norm1_pull(hidden_grad)
    attn_low = pre_grad.astype(jnp.bfloat16)
    mix_whole = jnp.einsum("nd,ne->de", context_low, attn_low, preferred_element_type=jnp.float32)
    context_grad = jnp.einsum(
        "ne,de->nd", attn_low, m_mix, preferred_element_type=jnp.float32
    ).astype(jnp.bfloat16)
    head_context_grad = split_heads(context_grad.reshape(local_len, rows, width))

    def query_side(group):
        g_query, g_key, g_value, g_qrel, g_krel, g_dctx, g_lse = group
        total, near_pull, far_pull, window = relative_scores(
            g_query, g_key, g_krel, g_qrel, offset, full_len
        )
        scores = jnp.where(same_doc, total * score_scale, masked_score)
        weights_now = jnp.exp(scores - g_lse[..., None])
        prob_grad = jnp.einsum(
            "rgid,rgjd->rgij", g_dctx, g_value, preferred_element_type=jnp.float32
        )
        inner_sum = jnp.sum(weights_now * prob_grad, axis=-1)
        score_grad = (weights_now * (prob_grad - inner_sum[..., None])).astype(jnp.bfloat16)
        grad_wide = score_grad.astype(jnp.float32)
        near_grad = near_pull(grad_wide)[0]
        near_low = jnp.where(inner_cols, near_grad, 0.0).astype(jnp.bfloat16)
        near_ends = end_columns(near_grad)
        query_part = jnp.einsum(
            "rgij,rgjd->rgid", score_grad, g_key, preferred_element_type=jnp.float32
        )
        query_part = (
            query_part
            + jnp.einsum("rgib,gbd->rgid", near_low, g_krel, preferred_element_type=jnp.float32)
            + end_terms(near_ends, g_krel)
        )
        krel_part = with_ends(
            jnp.einsum("rgib,rgid->gbd", near_low, g_query, preferred_element_type=jnp.float32),
            end_rows(near_ends, g_query),
        )
        return (
            weights_now,
            score_grad,
            grad_wide,
            far_pull,
            window,
            inner_sum,
            query_part * score_scale,
            krel_part * score_scale,
        )

    query_groups = (
        head_queries,
        head_keys,
        head_values,
        rel_queries,
        rel_keys,
        head_context_grad,
        log_totals,
    )

    def all_grads(carry, group):
        weights_now, score_grad, grad_wide, far_pull, window, inner_sum, query_part, krel_part = (
            query_side(group)
        )
        g_query, g_key, g_value, g_qrel, g_krel, g_dctx, g_lse = group
        cross_grad, end_grad = far_pull(grad_wide)
        cross_low = cross_grad.astype(jnp.bfloat16)
        key_part = jnp.einsum(
            "rgij,rgid->rgjd", score_grad, g_query, preferred_element_type=jnp.float32
        )
        band_part = jnp.einsum(
            "rgmb,gbd->rgmd", cross_low, g_qrel, preferred_element_type=jnp.float32
        )
        key_part = (
            key_part
            + unband(band_part, offset, full_len, buckets // 2)
            + end_terms(end_grad, g_qrel)
        )
        value_part = jnp.einsum(
            "rgij,rgid->rgjd",
            weights_now.astype(jnp.bfloat16),
            g_dctx,
            preferred_element_type=jnp.float32,
        )
        qrel_part = with_ends(
            jnp.einsum("rgmb,rgmd->gbd", cross_low, window, preferred_element_type=jnp.float32),
            end_rows(end_grad, g_key),
        )
        return (
            carry,
            (query_part, key_part * score_scale, value_part, qrel_part * score_scale, krel_part),
        )

    unused, (dq_groups, dk_groups, dv_groups, dqrel_groups, dkrel_groups) = lax.scan(
        all_grads, None, query_groups
    )
    key_sum, value_sum = (
        lax.psum_scatter(join_heads(dk_groups), "seq", scatter_dimension=0, tiled=True),
        lax.psum_scatter(join_heads(dv_groups), "seq", scatter_dimension=0, tiled=True),
    )
    key_grads = key_sum.reshape(tokens_here, width).astype(jnp.bfloat16)
    value_grads = value_sum.reshape(tokens_here, width).astype(jnp.bfloat16)
    query_grads = join_heads(dq_groups).reshape(tokens_here, width).astype(jnp.bfloat16)
    qrel_grad = join_table(dqrel_groups)
    krel_grad = join_table(dkrel_groups)
    input_grad = pre_grad + jnp.einsum(
        "ne,de->nd", query_grads, m_query, preferred_element_type=jnp.float32
    )
    input_grad = input_grad + jnp.einsum(
        "ne,de->nd", key_grads, m_key, preferred_element_type=jnp.float32
    )
    input_grad = input_grad + jnp.einsum(
        "ne,de->nd", value_grads, m_value, preferred_element_type=jnp.float32
    )
    query_whole = jnp.einsum(
        "nd,ne->de", flat_input, query_grads, preferred_element_type=jnp.float32
    ) + jnp.einsum(
        "bd,be->de", table, qrel_grad, precision=highest_prec, preferred_element_type=jnp.float32
    )
    key_whole = jnp.einsum(
        "nd,ne->de", flat_input, key_grads, preferred_element_type=jnp.float32
    ) + jnp.einsum(
        "bd,be->de", table, krel_grad, precision=highest_prec, preferred_element_type=jnp.float32
    )
    value_whole = jnp.einsum(
        "nd,ne->de", flat_input, value_grads, preferred_element_type=jnp.float32
    )
    table_whole = jnp.einsum(
        "be,de->bd", qrel_grad, m_query, precision=highest_prec, preferred_element_type=jnp.float32
    ) + jnp.einsum(
        "be,de->bd", krel_grad, m_key, precision=highest_prec, preferred_element_type=jnp.float32
    )
    bias_whole = jnp.stack(
        [
            jnp.sum(query_grads.astype(jnp.float32), axis=0) + jnp.sum(qrel_grad, axis=0),
            jnp.sum(key_grads.astype(jnp.float32), axis=0) + jnp.sum(krel_grad, axis=0),
            jnp.sum(value_grads.astype(jnp.float32), axis=0),
            jnp.sum(pre_grad, axis=0),
        ]
    )
    gain_whole = jnp.stack([gain1_grad, gain2_grad])
    shift_whole = jnp.stack([shift1_grad, shift2_grad])
    downb_whole = jnp.sum(mixed_grad, axis=0)
    seq_parts = (
        lax.psum_scatter(query_whole, "seq", scatter_dimension=0, tiled=True),
        lax.psum_scatter(key_whole, "seq", scatter_dimension=0, tiled=True),
        lax.psum_scatter(value_whole, "seq", scatter_dimension=0, tiled=True),
        lax.psum_scatter(mix_whole, "seq", scatter_dimension=0, tiled=True),
        lax.psum_scatter(table_whole, "seq", scatter_dimension=0, tiled=True),
        lax.psum_scatter(bias_whole, "seq", scatter_dimension=1, tiled=True),
        lax.psum_scatter(gain_whole, "seq", scatter_dimension=1, tiled=True),
        lax.psum_scatter(shift_whole, "seq", scatter_dimension=1, tiled=True),
        lax.psum_scatter(downb_whole, "seq", scatter_dimension=0, tiled=True),
    )
    batch_parts = (
        lax.psum_scatter(seq_parts[0], "batch", scatter_dimension=1, tiled=True),
        lax.psum_scatter(seq_parts[1], "batch", scatter_dimension=1, tiled=True),
        lax.psum_scatter(seq_parts[2], "batch", scatter_dimension=1, tiled=True),
        lax.psum_scatter(seq_parts[3], "batch", scatter_dimension=1, tiled=True),
        lax.psum_scatter(seq_parts[4], "batch", scatter_dimension=1, tiled=True),
        lax.psum_scatter(up_part, "batch", scatter_dimension=0, tiled=True),
        lax.psum_scatter(down_part, "batch", scatter_dimension=1, tiled=True),
    )
    small_parts = lax.psum(
        (seq_parts[5], seq_parts[6], seq_parts[7], seq_parts[8], upb_part), "batch"
    )
    layer_output = jnp.swapaxes(output.reshape(local_len, rows, width), 0, 1).astype(jnp.bfloat16)
    input_back = jnp.swapaxes(input_grad.reshape(local_len, rows, width), 0, 1)
    return (
        layer_output,
        input_back,
        batch_parts[0],
        batch_parts[1],
        batch_parts[2],
        batch_parts[3],
        batch_parts[4],
        small_parts[0],
        small_parts[1],
        small_parts[2],
        batch_parts[5],
        small_parts[4],
        batch_parts[6],
        small_parts[3],
    )


def solution(mesh):
    return jax.shard_map(
        body,
        mesh=mesh,
        in_specs=(
            P("batch", "seq", None),
            P("batch", "seq"),
            P("seq", "batch"),
            P("seq", "batch"),
            P("seq", "batch"),
            P("seq", "batch"),
            P("seq", "batch"),
            P(None, "seq"),
            P(None, "seq"),
            P(None, "seq"),
            P(None, "seq"),
            P("seq"),
            P("seq", None),
            P("seq"),
            P("batch", "seq", None),
        ),
        out_specs=(
            P("batch", "seq", None),
            P("batch", "seq", None),
            P("seq", "batch"),
            P("seq", "batch"),
            P("seq", "batch"),
            P("seq", "batch"),
            P("seq", "batch"),
            P(None, "seq"),
            P(None, "seq"),
            P(None, "seq"),
            P("batch", "seq"),
            P("seq"),
            P("seq", "batch"),
            P("seq"),
        ),
        check_vma=False,
    )
```

```python
import math

import jax
import jax.numpy as jnp
from jax import lax
from jax.experimental import pallas as pl
from jax.experimental.pallas import tpu as pltpu
from jax.sharding import PartitionSpec as P

DH = 64


masked_score = -1e30
norm_eps = 1e-06
pair_heads = 2


def normalize(values, gain, shift):
    average = jnp.mean(values, axis=-1, keepdims=True)
    centered = values - average
    variance = jnp.mean(centered * centered, axis=-1, keepdims=True)
    return centered * lax.rsqrt(variance + norm_eps) * gain + shift


def exact_gelu(values):
    return jax.nn.gelu(values, approximate=False)


def split_heads(matrix):
    length, rows, width = matrix.shape
    groups = width // (pair_heads * DH)
    return matrix.reshape(length, rows, groups, pair_heads, DH).transpose(2, 1, 3, 0, 4)


def join_heads(matrix):
    groups, rows, pair, length, depth = matrix.shape
    return matrix.transpose(3, 1, 0, 2, 4).reshape(length, rows, groups * pair * depth)


def split_table(matrix):
    buckets, width = matrix.shape
    return matrix.reshape(buckets, width // (pair_heads * DH), pair_heads, DH).transpose(1, 2, 0, 3)


def join_table(matrix):
    groups, pair, buckets, depth = matrix.shape
    return matrix.transpose(2, 0, 1, 3).reshape(buckets, groups * pair * depth)


def table_ends(table):
    return jnp.stack([table[:, 0], table[:, -1]], axis=1)


def near_skew(table_prod, offset, full_len):
    lead = table_prod.shape[:-2]
    count, buckets = table_prod.shape[-2:]
    span = buckets // 2
    lead_pad = [(0, 0)] * len(lead)
    flipped = jnp.pad(table_prod[..., ::-1], lead_pad + [(0, 0), (0, count)])
    sheared = flipped.reshape(lead + (count * (buckets + count),))[
        ..., : count * (buckets + count - 1)
    ]
    sheared = sheared.reshape(lead + (count, buckets + count - 1))
    spread = jnp.pad(sheared, lead_pad + [(0, 0), (full_len, full_len)])
    band = lax.dynamic_slice_in_dim(
        spread, full_len + span - 1 - offset, full_len, axis=len(lead) + 1
    )
    distance = (offset + jnp.arange(count, dtype=jnp.int32))[:, None] - jnp.arange(
        full_len, dtype=jnp.int32
    )[None, :]
    return jnp.where(
        distance <= -span,
        table_prod[..., 0:1],
        jnp.where(distance >= span - 1, table_prod[..., buckets - 1 :], band),
    )


def far_place(cross, end_vals, offset, count, full_len):
    lead = cross.shape[:-2]
    band_len, buckets = cross.shape[-2:]
    span = buckets // 2
    lead_pad = [(0, 0)] * len(lead)
    turned = jnp.swapaxes(cross, -1, -2).reshape(lead + (buckets * band_len,))
    turned = jnp.pad(turned, lead_pad + [(0, buckets)])
    diagonal = turned.reshape(lead + (buckets, band_len + 1))[..., :count]
    aligned = jnp.pad(jnp.swapaxes(diagonal, -1, -2), lead_pad + [(0, 0), (0, count)])
    sheared = aligned.reshape(lead + (count * (buckets + count),))[
        ..., : count * (buckets + count - 1)
    ]
    sheared = sheared.reshape(lead + (count, buckets + count - 1))
    spread = jnp.pad(sheared, lead_pad + [(0, 0), (full_len, full_len)])
    band = lax.dynamic_slice_in_dim(spread, full_len + span - offset, full_len, axis=len(lead) + 1)
    distance = (
        jnp.arange(full_len, dtype=jnp.int32)[None, :]
        - (offset + jnp.arange(count, dtype=jnp.int32))[:, None]
    )
    return jnp.where(
        distance <= -span,
        end_vals[..., 0:1, :],
        jnp.where(distance >= span - 1, end_vals[..., 1:2, :], band),
    )


def band_rows(all_rows, offset, count, span):
    padded = jnp.pad(all_rows, [(0, 0), (0, 0), (span, span), (0, 0)])
    return lax.dynamic_slice_in_dim(padded, offset, count + 2 * span - 1, axis=2)


def unband(values, offset, full_len, span):
    lead = values.shape[:2]
    room = jnp.zeros(lead + (full_len + 2 * span, values.shape[3]), jnp.float32)
    placed = lax.dynamic_update_slice_in_dim(room, values, offset, axis=2)
    return placed[:, :, span : span + full_len]


def relative_scores(own_rows, all_rows, own_table, all_table, offset, full_len):
    count = own_rows.shape[2]
    content = jnp.einsum("rgid,rgjd->rgij", own_rows, all_rows, preferred_element_type=jnp.float32)
    own_prod = jnp.einsum("rgid,gbd->rgib", own_rows, own_table, preferred_element_type=jnp.float32)
    window = band_rows(all_rows, offset, count, all_table.shape[1] // 2)
    cross = jnp.einsum("rgmd,gbd->rgmb", window, all_table, preferred_element_type=jnp.float32)
    end_vals = jnp.einsum(
        "rgjd,ged->rgej", all_rows, table_ends(all_table), preferred_element_type=jnp.float32
    )
    near_vals, near_pull = jax.vjp(lambda product: near_skew(product, offset, full_len), own_prod)
    far_vals, far_pull = jax.vjp(
        lambda part, ends: far_place(part, ends, offset, count, full_len), cross, end_vals
    )
    return (content + near_vals + far_vals, near_pull, far_pull, window)


def end_columns(grad):
    return jnp.stack([grad[..., 0], grad[..., -1]], axis=2)


def end_terms(ends, table):
    return jnp.einsum(
        "rgei,ged->rgid",
        ends,
        table_ends(table),
        precision=lax.Precision.HIGHEST,
        preferred_element_type=jnp.float32,
    )


def end_rows(ends, rows_low):
    return jnp.einsum(
        "rgei,rgid->ged",
        ends,
        rows_low,
        precision=lax.Precision.HIGHEST,
        preferred_element_type=jnp.float32,
    )


def with_ends(inner_part, edge_rows):
    buckets = inner_part.shape[1]
    place = jnp.arange(buckets, dtype=jnp.int32)[None, :, None]
    return (
        inner_part
        + jnp.where(place == 0, edge_rows[:, 0:1], 0.0)
        + jnp.where(place == buckets - 1, edge_rows[:, 1:2], 0.0)
    )


BLOCK = 128
MIB = 1024 * 1024
ATTEND_VMEM = 26 * MIB
BACK_VMEM = 26 * MIB
FEED_VMEM = 40 * MIB
COMM_VMEM = 16 * MIB


def dot_nn(a, b):
    return lax.dot_general(a, b, (((1,), (0,)), ((), ())), preferred_element_type=jnp.float32)


def dot_nt(a, b):
    return lax.dot_general(a, b, (((1,), (1,)), ((), ())), preferred_element_type=jnp.float32)


def dot_tn(a, b):
    return lax.dot_general(a, b, (((0,), (0,)), ((), ())), preferred_element_type=jnp.float32)


def turn_matrix(buckets):
    row = lax.broadcasted_iota(jnp.int32, (buckets, buckets), 0)
    col = lax.broadcasted_iota(jnp.int32, (buckets, buckets), 1)
    return (row + col == buckets - 1).astype(jnp.bfloat16)


def skew_band(product):
    count, buckets = product.shape
    row = lax.broadcasted_iota(jnp.int32, (count, BLOCK), 0)
    lane = lax.broadcasted_iota(jnp.int32, (count, BLOCK), 1)
    edge = jnp.where(row + lane <= BLOCK - 2, product[:, buckets - 1 :], product[:, 0:1])
    wide = jnp.concatenate([product, edge], axis=1)
    return pltpu.roll(wide, 1, 1, stride=1, stride_axis=0)


def skew_back(turned, buckets):
    return pltpu.roll(turned, turned.shape[1] - BLOCK, 1, stride=1, stride_axis=0)[:, :buckets]


def chip_columns(vec_ref, chip, index, core):
    width = 3 * DH // 2
    both = jnp.concatenate(
        [
            vec_ref[2 * chip, index : index + 1, :width].astype(jnp.float32),
            vec_ref[2 * chip + 1, index : index + 1, :width].astype(jnp.float32),
        ],
        axis=1,
    )
    return jnp.where(core == 0, both[:, : 2 * DH], both[:, DH:])


def attend_kernel(
    xs_ref,
    qkvs_ref,
    tables_ref,
    vecs_ref,
    q_ref,
    k_ref,
    v_ref,
    qrev_ref,
    krev_ref,
    p_ref,
    ctx_ref,
    w_ref,
    table_ref,
    segc_ref,
    place_ref,
    wide_ref,
    ends_ref,
    held_ref,
    ready,
    leave,
):
    at = Place()
    full_len = xs_ref.shape[0] * xs_ref.shape[1]
    buckets = table_ref.shape[0]
    blocks = full_len // BLOCK
    span = buckets // 2
    side = span // BLOCK
    band_width = buckets + BLOCK
    band_blocks = band_width // BLOCK
    group = 2 * DH
    scale = 1.0 / math.sqrt(3.0 * DH)
    units = p_ref.shape[0]
    shard_rows = qkvs_ref.shape[2]
    table_rows = tables_ref.shape[3]
    batches = tables_ref.shape[1]
    for part in range(at.tokens):
        pieces = []
        for i in range(3):
            piece = qkvs_ref[part, i]
            pieces.append(jnp.where(at.core == 0, piece[:, :group], piece[:, DH:]))
        w_ref[part * shard_rows : (part + 1) * shard_rows] = jnp.concatenate(pieces, axis=1)
        core, chip = part % 2, part // 2
        table_ref[part * table_rows : (part + 1) * table_rows] = jnp.concatenate(
            [tables_ref[core, row, chip] for row in range(batches)], axis=1
        )
        own_seg = vecs_ref[part, 9:10].astype(jnp.float32)
        segc_ref[part * BLOCK : (part + 1) * BLOCK] = jnp.broadcast_to(own_seg, (BLOCK, BLOCK)).T
    seg_row = jnp.concatenate(
        [vecs_ref[part, 9:10].astype(jnp.float32) for part in range(at.tokens)], axis=1
    )
    bias = jnp.concatenate(
        [chip_columns(vecs_ref, at.chip, i, at.core) for i in range(3)], axis=1
    )
    tokens_all = xs_ref[...].reshape(full_len, xs_ref.shape[2])
    proj = (dot_nn(tokens_all, w_ref[...]) + bias).astype(jnp.bfloat16)
    rel = (dot_nn(table_ref[...], w_ref[:, : 2 * group]) + bias[:, : 2 * group]).astype(
        jnp.bfloat16
    )
    rel = dot_nn(turn_matrix(buckets), rel).astype(jnp.bfloat16)
    for slot in range(2):
        lo, hi = slot * DH, (slot + 1) * DH
        q_ref[slot] = proj[:, lo:hi]
        k_ref[slot] = proj[:, group + lo : group + hi]
        v_ref[slot] = proj[:, 2 * group + lo : 2 * group + hi]
        qrev_ref[slot] = rel[:, lo:hi]
        krev_ref[slot] = rel[:, group + lo : group + hi]
    held_ref[...] = jnp.zeros_like(held_ref)
    for slot in range(2):
        ends_ref[slot, 0] = dot_nt(qrev_ref[slot, 0:16], k_ref[slot])
        ends_ref[slot, 1] = dot_nt(qrev_ref[slot, buckets - 16 : buckets], k_ref[slot])

        def key_block(kb, carry):
            rows = k_ref[slot, pl.ds(pl.multiple_of(kb * BLOCK, BLOCK), BLOCK)]
            band = skew_band(dot_nt(rows, qrev_ref[slot]))
            for e in range(band_blocks):
                place_ref[
                    slot,
                    kb + e,
                    :,
                    (band_blocks - 1 - e) * BLOCK : (band_blocks - e) * BLOCK,
                ] = band[:, e * BLOCK : (e + 1) * BLOCK].T
            return carry

        lax.fori_loop(0, blocks, key_block, 0)

    first = at.core * (blocks // 2)
    ready()

    def unit(u, carry):
        g = u + first
        slot = g // blocks
        qb = g % blocks

        @pl.when(u > 0)
        def _():
            leave(u - 1)

        start = pl.multiple_of(qb * BLOCK, BLOCK)
        rows = q_ref[slot, pl.ds(start, BLOCK)]
        own = dot_nt(rows, krev_ref[slot])
        band = skew_band(own) + place_ref[slot, qb + side]
        wide_ref[:, pl.ds(start, band_width)] = band
        content = dot_nt(rows, k_ref[slot])
        lane = lax.broadcasted_iota(jnp.int32, (BLOCK, full_len), 1)
        near = jnp.where(
            lane < start - span,
            own[:, 0:1] + ends_ref[slot, 1, 15:16],
            jnp.where(
                lane >= start + band_width - span,
                own[:, buckets - 1 :] + ends_ref[slot, 0, 0:1],
                wide_ref[:, span : span + full_len],
            ),
        )
        same = segc_ref[pl.ds(start, BLOCK), 0:1] == seg_row
        scores = jnp.where(same, (content + near) * scale, masked_score)
        highest = jnp.max(scores, axis=-1, keepdims=True)
        exponent = jnp.exp(scores - highest)
        total = jnp.sum(exponent, axis=-1, keepdims=True)
        probs = (exponent / total).astype(jnp.bfloat16)
        p_ref[u] = probs
        held_ref[slot, pl.ds(start, BLOCK)] = dot_nn(probs, v_ref[slot]).astype(jnp.bfloat16)
        return carry

    lax.fori_loop(0, units, unit, 0)
    for part in range(at.tokens):
        rows = slice(part * BLOCK, (part + 1) * BLOCK)
        ctx_ref[part] = jnp.concatenate([held_ref[0, rows], held_ref[1, rows]], axis=1)
    leave(units - 1)


def attend_back_kernel(
    q_ref,
    k_ref,
    v_ref,
    qrev_ref,
    krev_ref,
    p_ref,
    mix_ref,
    attn_ref,
    dcat_ref,
    rel_ref,
    sum_ref,
    heads_ref,
    wide_ref,
    low_ref,
    place_ref,
    dq_ref,
    dkt_ref,
    dvt_ref,
    far_ref,
    dkr_ref,
    dqr_ref,
):
    full_len = q_ref.shape[1]
    buckets = qrev_ref.shape[1]
    blocks = full_len // BLOCK
    span = buckets // 2
    side = span // BLOCK
    band_width = buckets + BLOCK
    band_blocks = band_width // BLOCK
    scale = 1.0 / math.sqrt(3.0 * DH)
    units = p_ref.shape[0]
    for ref in (wide_ref, low_ref, place_ref, dq_ref, dkt_ref, dvt_ref, far_ref, dkr_ref, dqr_ref):
        ref[...] = jnp.zeros_like(ref)
    at = Place()
    group = 2 * DH
    first_row = pl.multiple_of((3 * at.chip + at.core) * DH, DH)
    mix_rows = mix_ref[pl.ds(first_row, group)]
    dctx = dot_nt(attn_ref[...].reshape(full_len, attn_ref.shape[2]), mix_rows)
    for slot in range(2):
        heads_ref[slot] = dctx[:, slot * DH : (slot + 1) * DH].astype(jnp.bfloat16)
    first = at.core * (blocks // 2)
    turn = turn_matrix(BLOCK)
    place8 = lax.broadcasted_iota(jnp.int32, (8, full_len), 0)

    def unit(u, carry):
        g = u + first
        slot = g // blocks
        qb = g % blocks
        start = pl.multiple_of(qb * BLOCK, BLOCK)
        rows = q_ref[slot, pl.ds(start, BLOCK)]
        grad = heads_ref[slot, pl.ds(start, BLOCK)]
        probs = p_ref[u]
        wide_probs = probs.astype(jnp.float32)
        prob_grad = dot_nt(grad, v_ref[slot])
        inner = jnp.sum(wide_probs * prob_grad, axis=-1, keepdims=True)
        low_grad = (wide_probs * (prob_grad - inner)).astype(jnp.bfloat16)
        score_grad = low_grad.astype(jnp.float32)
        wide_ref[:, span : span + full_len] = dot_nn(turn, low_grad)
        low_ref[:, span : span + full_len] = low_grad
        dvt_ref[slot] += dot_tn(grad, probs)
        dkt_ref[slot] += dot_tn(rows, low_grad)
        row = lax.broadcasted_iota(jnp.int32, (BLOCK, full_len), 0)
        lane = lax.broadcasted_iota(jnp.int32, (BLOCK, full_len), 1)
        gap = lane - row - start
        right = jnp.where(gap > span, score_grad, 0.0)
        left = jnp.where(gap < 1 - span, score_grad, 0.0)
        end_right = jnp.sum(right, axis=-1, keepdims=True)
        end_left = jnp.sum(left, axis=-1, keepdims=True)
        far_right = jnp.sum(jnp.where(gap >= span, score_grad, 0.0), axis=0, keepdims=True)
        far_left = jnp.sum(jnp.where(gap < -span, score_grad, 0.0), axis=0, keepdims=True)
        far_ref[slot] += jnp.where(place8 == 0, far_right, jnp.where(place8 == 1, far_left, 0.0))
        band = wide_ref[:, pl.ds(start, band_width)]
        near = dot_nn(turn, skew_back(band, buckets).astype(jnp.bfloat16))
        bucket = lax.broadcasted_iota(jnp.int32, (BLOCK, buckets), 1)
        near = near + jnp.where(
            bucket == 0, end_left, jnp.where(bucket == buckets - 1, end_right, 0.0)
        )
        near_low = near.astype(jnp.bfloat16)
        dq = dot_nn(low_grad, k_ref[slot]) + dot_nn(near_low, krev_ref[slot])
        dq_ref[slot, pl.ds(start, BLOCK)] = dq
        dkr_ref[slot] += dot_tn(rows, near_low)
        for e in range(band_blocks):
            keys_at = pl.multiple_of(start + e * BLOCK, BLOCK)
            place_ref[
                slot, qb + e, :, (band_blocks - 1 - e) * BLOCK : (band_blocks - e) * BLOCK
            ] = dot_nt(turn, low_ref[:, pl.ds(keys_at, BLOCK)])
        return carry

    lax.fori_loop(0, units, unit, 0)
    parts_q, parts_k, parts_v = [], [], []
    parts_r = [None] * 4
    for slot in range(2):
        far_low = far_ref[slot].astype(jnp.bfloat16)
        mark = lax.broadcasted_iota(jnp.int32, (8, DH), 0)
        ends = jnp.where(
            mark == 0,
            qrev_ref[slot, 0:1].astype(jnp.float32),
            jnp.where(mark == 1, qrev_ref[slot, buckets - 1 : buckets].astype(jnp.float32), 0.0),
        ).astype(jnp.bfloat16)
        end_keys = dot_tn(ends, far_low)
        end_rows = dot_nn(far_low, k_ref[slot])

        whole_k = (dkt_ref[slot] + end_keys).T

        def key_side(kb, carry):
            start = pl.multiple_of(kb * BLOCK, BLOCK)
            far = skew_back(place_ref[slot, kb + side], buckets).astype(jnp.bfloat16)
            far = dot_nn(turn, far).astype(jnp.bfloat16)
            keys = k_ref[slot, pl.ds(start, BLOCK)]
            dqr_ref[slot] += dot_tn(keys, far)
            dq_ref[2 + slot, pl.ds(start, BLOCK)] = dot_nn(far, qrev_ref[slot])
            return carry

        lax.fori_loop(0, blocks, key_side, 0)
        parts_q.append((dq_ref[slot] * scale).astype(jnp.bfloat16))
        parts_k.append(((dq_ref[2 + slot] + whole_k) * scale).astype(jnp.bfloat16))
        parts_v.append(dvt_ref[slot].T.astype(jnp.bfloat16))
        bucket = lax.broadcasted_iota(jnp.int32, (buckets, DH), 0)
        qr = dqr_ref[slot].T + jnp.where(
            bucket == 0, end_rows[0:1], jnp.where(bucket == buckets - 1, end_rows[1:2], 0.0)
        )
        dqr_out = qr * scale
        dkr_out = dkr_ref[slot].T * scale
        parts_r[slot] = dqr_out
        parts_r[2 + slot] = dkr_out
    dcat = jnp.concatenate(parts_q + parts_k + parts_v, axis=1)
    dcat_ref[...] = dcat
    rel = jnp.concatenate(parts_r, axis=1)
    rel_ref[...] = dot_nn(turn_matrix(buckets), rel.astype(jnp.bfloat16)).astype(jnp.bfloat16)
    rel_sum = jnp.sum(rel, axis=0, keepdims=True)
    rel_sum = jnp.concatenate([rel_sum, jnp.zeros((1, 2 * DH), jnp.float32)], axis=1)
    sums = jnp.sum(dcat.astype(jnp.float32), axis=0, keepdims=True) + rel_sum
    sum_ref[...] = jnp.broadcast_to(sums, sum_ref.shape)


def attend_back(q, k, v, qrev, krev, probs, m_mix, attn_all):
    full_len = q.shape[1]
    buckets = qrev.shape[1]
    blocks = full_len // BLOCK
    band_width = buckets + BLOCK
    low, wide = jnp.bfloat16, jnp.float32
    pad_blocks = blocks + band_width // BLOCK - 1
    return pl.pallas_call(
        attend_back_kernel,
        out_shape=(
            jax.ShapeDtypeStruct((full_len, 6 * DH), low),
            jax.ShapeDtypeStruct((buckets, 4 * DH), low),
            jax.ShapeDtypeStruct((8, 6 * DH), wide),
        ),
        in_specs=[pl.BlockSpec(memory_space=pltpu.VMEM)] * 8,
        out_specs=[pl.BlockSpec(memory_space=pltpu.VMEM)] * 3,
        scratch_shapes=[
            pltpu.VMEM((2, full_len, DH), low),
            pltpu.VMEM((BLOCK, full_len + buckets), wide),
            pltpu.VMEM((BLOCK, full_len + buckets), low),
            pltpu.VMEM((2, pad_blocks, BLOCK, band_width), wide),
            pltpu.VMEM((4, full_len, DH), wide),
            pltpu.VMEM((2, DH, full_len), wide),
            pltpu.VMEM((2, DH, full_len), wide),
            pltpu.VMEM((2, 8, full_len), wide),
            pltpu.VMEM((2, DH, buckets), wide),
            pltpu.VMEM((2, DH, buckets), wide),
        ],
        compiler_params=pltpu.CompilerParams(vmem_limit_bytes=BACK_VMEM),
        name="attend_back",
    )(q, k, v, qrev, krev, probs, m_mix, attn_all)


MESH = pl.DeviceIdType.MESH
VMEM_SPEC = pl.BlockSpec(memory_space=pltpu.VMEM)
HBM_SPEC = pl.BlockSpec(memory_space=pltpu.HBM)
CHUNKS = 2


class Place:
    def __init__(self):
        self.batches = lax.axis_size("batch")
        self.tokens = lax.axis_size("seq")
        self.chips = self.tokens // 2
        self.row = lax.axis_index("batch")
        self.part = lax.axis_index("seq")
        self.chip = self.part // 2
        self.core = self.part % 2

    def along_chips(self, k):
        chip = lax.rem(self.chip + k, self.chips)
        return chip, (self.row, 2 * chip + self.core)

    def from_chips(self, k):
        return lax.rem(self.chip + self.chips - k, self.chips)

    def partner(self):
        return (self.row, self.part + 1 - 2 * self.core)

    def along_rows(self, k):
        row = lax.rem(self.row + k, self.batches)
        return row, (row, self.part)

    def from_rows(self, k):
        return lax.rem(self.row + self.batches - k, self.batches)

    def along_seq(self, k):
        part = lax.rem(self.part + k, self.tokens)
        return part, (self.row, part)

    def along_plane(self, k):
        index = lax.rem(2 * self.row + self.core + k, 2 * self.batches)
        row, core = index // 2, index % 2
        return row, core, (row, 2 * self.chip + core)

    def chip_peers(self):
        return [self.along_chips(k)[1] for k in range(1, self.chips)]

    def row_peers(self):
        return [self.along_rows(k)[1] for k in range(1, self.batches)]

    def cross_peers(self):
        other = self.part + 1 - 2 * self.core
        return [(self.along_rows(k)[0], other) for k in range(1, self.batches)]

    def cross_row_peers(self):
        return self.row_peers() + self.cross_peers()

    def all_peers(self):
        peers = []
        for i in range(self.batches):
            row = lax.rem(self.row + i, self.batches)
            for j in range(self.tokens):
                if i or j:
                    peers.append((row, lax.rem(self.part + j, self.tokens)))
        return peers

    def seq_peers(self):
        return [self.along_seq(k)[1] for k in range(1, self.tokens)]

    def plane_peers(self):
        return [self.along_plane(k)[2] for k in range(1, 2 * self.batches)]


def meet(peers):
    barrier = pltpu.get_barrier_semaphore()
    for peer in peers:
        pl.semaphore_signal(barrier, inc=1, device_id=peer, device_id_type=MESH)
    pl.semaphore_wait(barrier, len(peers))


class Wires:
    def __init__(self, send_sems, recv_sems, local_sems):
        self.sems = (send_sems, recv_sems, local_sems)
        self.used = [0, 0]
        self.ends = []

    def send(self, src, dst, peer):
        k = self.used[0]
        self.used[0] += 1
        copy = pltpu.make_async_remote_copy(
            src_ref=src,
            dst_ref=dst,
            send_sem=self.sems[0].at[k],
            recv_sem=self.sems[1].at[k],
            device_id=peer,
            device_id_type=MESH,
        )
        copy.start()
        self.ends.append(copy.wait_send)
        return copy

    def local(self, src, dst):
        k = self.used[1]
        self.used[1] += 1
        copy = pltpu.make_async_copy(src, dst, self.sems[2].at[k])
        copy.start()
        return copy

    def finish(self):
        for end in self.ends:
            end()


def wire_scratch(sends, locals_count):
    return [
        pltpu.SemaphoreType.DMA((sends,)),
        pltpu.SemaphoreType.DMA((sends,)),
        pltpu.SemaphoreType.DMA((locals_count,)),
    ]


def comm_call(kernel, name, ident, out_shapes, inputs, sends, locals_count, scratch=(), spec=VMEM_SPEC):
    return pl.pallas_call(
        kernel,
        out_shape=tuple(out_shapes),
        in_specs=[spec] * len(inputs),
        out_specs=tuple([VMEM_SPEC] * len(out_shapes)),
        scratch_shapes=list(scratch) + wire_scratch(sends, locals_count),
        compiler_params=pltpu.CompilerParams(
            collective_id=ident, has_side_effects=True, vmem_limit_bytes=COMM_VMEM
        ),
        name=name,
    )(*inputs)


def like(array, *lead):
    return jax.ShapeDtypeStruct(tuple(lead) + tuple(array.shape), array.dtype)


def pick(values, index):
    out = jnp.int32(values[0])
    for i in range(1, len(values)):
        out = jnp.where(index == i, jnp.int32(values[i]), out)
    return out


def arrival_order(at):
    chips = range(at.chips)
    lists = [sorted((j for j in chips if j != z), key=lambda j: (abs(j - z), j)) for z in chips]
    return [pick([lists[z][t] for z in chips], at.chip) for t in range(at.chips - 1)]


def return_order(at):
    chips = range(at.chips)

    def away(j, z):
        end = at.chips - 1 if j < z else 0
        return (abs(j - end) + abs(end - z), j)

    lists = [sorted((j for j in chips if j != z), key=lambda j: away(j, z)) for z in chips]
    return [pick([lists[z][t] for z in chips], at.chip) for t in range(at.chips - 1)]


def far_order(at):
    chips = range(at.chips)
    lists = [sorted((j for j in chips if j != z), key=lambda j: (-abs(j - z), j)) for z in chips]
    return [pick([lists[z][t] for z in chips], at.chip) for t in range(at.chips - 1)]


def goes_on(at, j):
    above = jnp.logical_and(j < at.chip, at.chip < at.chips - 1)
    below = jnp.logical_and(j > at.chip, at.chip > 0)
    return jnp.logical_or(above, below)


def line_peer(at, step):
    return (at.row, 2 * (at.chip + step) + at.core)


class LineGather:
    def __init__(self, at, buf, slot, sems, own=None):
        self.at, self.buf, self.slot, self.own = at, buf, slot, own
        self.send_sems, self.recv_sems = sems
        self.rows = buf.shape[1] // CHUNKS

    def copy(self, j, h, step, k, own=False):
        window = pl.ds(h * self.rows, self.rows)
        home = self.buf.at[self.slot(j), window]
        src = self.own.at[window] if own and self.own is not None else home
        return pltpu.make_async_remote_copy(
            src_ref=src,
            dst_ref=home,
            send_sem=self.send_sems.at[k * CHUNKS + h],
            recv_sem=self.recv_sems.at[j * CHUNKS + h],
            device_id=line_peer(self.at, step),
            device_id_type=MESH,
        )

    def own_each(self, act):
        z, n = self.at.chip, self.at.chips
        for h in range(CHUNKS):

            @pl.when(z < n - 1)
            def _():
                act(self.copy(z, h, 1, z, own=True))

            @pl.when(z > 0)
            def _():
                act(self.copy(z, h, -1, n, own=True))

    def start(self):
        self.own_each(lambda copy: copy.start())

    def arrive(self, j):
        step = jnp.where(j < self.at.chip, 1, -1)
        for h in range(CHUNKS):
            self.copy(j, h, -step, j).wait_recv()

            @pl.when(goes_on(self.at, j))
            def _():
                self.copy(j, h, step, j).start()

    def drain(self, order):
        self.own_each(lambda copy: copy.wait_send())
        for j in order:
            step = jnp.where(j < self.at.chip, 1, -1)

            @pl.when(goes_on(self.at, j))
            def _():
                for h in range(CHUNKS):
                    self.copy(j, h, step, j).wait_send()


class LineReduce:
    def __init__(self, at, part, got, sems):
        self.at, self.part, self.got = at, part, got
        self.send_sems, self.recv_sems = sems
        self.rows = part.shape[1] // CHUNKS

    def copy(self, j, h):
        z, n = self.at.chip, self.at.chips
        window = pl.ds(h * self.rows, self.rows)
        slot = jnp.where(z + 1 == j, n, j)
        return pltpu.make_async_remote_copy(
            src_ref=self.part.at[j, window],
            dst_ref=self.got.at[slot, window],
            send_sem=self.send_sems.at[j * CHUNKS + h],
            recv_sem=self.recv_sems.at[slot * CHUNKS + h],
            device_id=line_peer(self.at, jnp.where(j < z, -1, 1)),
            device_id_type=MESH,
        )

    def landed(self, slot, h, step):
        window = pl.ds(h * self.rows, self.rows)
        return pltpu.make_async_remote_copy(
            src_ref=self.got.at[slot, window],
            dst_ref=self.got.at[slot, window],
            send_sem=self.send_sems.at[h],
            recv_sem=self.recv_sems.at[slot * CHUNKS + h],
            device_id=line_peer(self.at, step),
            device_id_type=MESH,
        )

    def send(self, j):
        for h in range(CHUNKS):
            self.copy(j, h).start()

    def send_last(self, j):
        @pl.when(jnp.logical_not(goes_on(self.at, j)))
        def _():
            self.send(j)

    def pass_on(self, order):
        z, n = self.at.chip, self.at.chips
        wide = jnp.float32

        @pl.when(jnp.logical_and(z > 0, z < n - 1))
        def _():
            for j in order:
                step = jnp.where(j < z, 1, -1)
                for h in range(CHUNKS):
                    self.landed(j, h, step).wait_recv()
                    window = pl.ds(h * self.rows, self.rows)
                    total = self.part[j, window].astype(wide) + self.got[j, window].astype(wide)
                    self.part[j, window] = total.astype(self.part.dtype)
                    self.copy(j, h).start()

    def clear(self):
        z, n = self.at.chip, self.at.chips

        @pl.when(z == n - 1)
        def _():
            self.got[z] = jnp.zeros(self.got.shape[1:], self.got.dtype)

        @pl.when(z == 0)
        def _():
            self.got[n] = jnp.zeros(self.got.shape[1:], self.got.dtype)

    def collect(self):
        z, n = self.at.chip, self.at.chips
        for h in range(CHUNKS):

            @pl.when(z < n - 1)
            def _():
                self.landed(z, h, 1).wait_recv()

            @pl.when(z > 0)
            def _():
                self.landed(n, h, -1).wait_recv()

        return self.got[z].astype(jnp.float32) + self.got[n].astype(jnp.float32)

    def drain(self, order):
        for j in order:
            for h in range(CHUNKS):
                self.copy(j, h).wait_send()


def gather_sems(chips):
    return [
        pltpu.SemaphoreType.DMA(((chips + 1) * CHUNKS,)),
        pltpu.SemaphoreType.DMA((chips * CHUNKS,)),
    ]


def reduce_sems(chips):
    return [
        pltpu.SemaphoreType.DMA((chips * CHUNKS,)),
        pltpu.SemaphoreType.DMA(((chips + 1) * CHUNKS,)),
    ]


def gather_kernel(
    x_ref, wq_ref, wk_ref, wv_ref, mix_ref, table_ref, vec_ref, up_ref, down_ref,
    xs_ref, qkvs_ref, mixs_ref, tables_ref, vecs_ref, up2_ref, down2_ref,
    line_send, line_recv, *sems,
):
    at = Place()
    wires = Wires(*sems)
    b, s, z, c = at.row, at.part, at.chip, at.core
    off_diagonal = b != z
    turned = (z, 2 * b + c)
    peers = at.seq_peers() + at.row_peers()
    barrier = pltpu.get_barrier_semaphore()
    for peer in peers:
        pl.semaphore_signal(barrier, inc=1, device_id=peer, device_id_type=MESH)

    @pl.when(off_diagonal)
    def _():
        pl.semaphore_signal(barrier, inc=1, device_id=turned, device_id_type=MESH)

    pl.semaphore_wait(barrier, len(peers) + off_diagonal.astype(jnp.int32))

    swaps, stays = [], []
    for i, ref in enumerate((wq_ref, wk_ref, wv_ref)):
        k = wires.used[0]
        wires.used[0] += 1
        swaps.append(
            pltpu.make_async_remote_copy(
                src_ref=ref,
                dst_ref=qkvs_ref.at[2 * z + c, i],
                send_sem=sems[0].at[k],
                recv_sem=sems[1].at[k],
                device_id=turned,
                device_id_type=MESH,
            )
        )
        stays.append(pltpu.make_async_copy(ref, qkvs_ref.at[2 * b + c, i], sems[2].at[i]))
        wires.used[1] += 1

    @pl.when(off_diagonal)
    def _():
        for swap in swaps:
            swap.start()

    @pl.when(jnp.logical_not(off_diagonal))
    def _():
        for stay in stays:
            stay.start()

    table_home = tables_ref.at[c, b, z]
    mix_home = mixs_ref.at[c, b, z]
    table_sends = [
        wires.send(table_ref, table_home, at.along_chips(k)[1]) for k in range(1, at.chips)
    ]
    kept = [wires.local(table_ref, table_home), wires.local(mix_ref, mix_home)]
    line = LineGather(at, xs_ref, lambda j: 2 * j + c, (line_send, line_recv), own=x_ref)
    line.start()
    last = [wires.send(vec_ref, vecs_ref.at[s], at.along_seq(k)[1]) for k in range(1, at.tokens)]
    mix_sends = [
        wires.send(mix_ref, mix_home, at.along_chips(k)[1]) for k in range(1, at.chips)
    ]
    last += [
        wires.send(x_ref, xs_ref.at[s], at.partner()),
        wires.send(up_ref, up2_ref, at.partner()),
        wires.send(down_ref, down2_ref, at.partner()),
    ]
    own = [
        wires.local(x_ref, xs_ref.at[s]),
        wires.local(vec_ref, vecs_ref.at[s]),
    ]

    @pl.when(off_diagonal)
    def _():
        for swap in swaps:
            swap.wait_recv()

    @pl.when(jnp.logical_not(off_diagonal))
    def _():
        for stay in stays:
            stay.wait()

    mine = qkvs_ref.at[2 * b + c]
    qkv_sends = [wires.send(mine, mine, at.along_rows(k)[1]) for k in range(1, at.batches)]
    last.append(wires.send(mine, mine, at.partner()))
    for copy in table_sends:
        copy.wait_recv()
    for copy in kept:
        copy.wait()
    mine = tables_ref.at[c, b]
    row_sends = [wires.send(mine, mine, at.along_rows(k)[1]) for k in range(1, at.batches)]
    last.append(wires.send(mine, mine, at.partner()))
    order = arrival_order(at)

    def arrived(j):
        line.arrive(j)
        home = xs_ref.at[2 * j + c]
        last.append(wires.send(home, home, at.partner()))

    arrived(order[0])
    for copy in mix_sends:
        copy.wait_recv()
    mine = mixs_ref.at[c, b]
    mix_rows = [wires.send(mine, mine, at.along_rows(k)[1]) for k in range(1, at.batches)]
    last.append(wires.send(mine, mine, at.partner()))
    arrived(order[1])
    for k in range(1, at.batches):
        qkv_sends[k - 1].wait_recv()
        home = qkvs_ref.at[2 * at.from_rows(k) + c]
        last.append(wires.send(home, home, at.partner()))
    for k in range(1, at.batches):
        row_sends[k - 1].wait_recv()
        home = tables_ref.at[c, at.from_rows(k)]
        last.append(wires.send(home, home, at.partner()))
    for j in order[2:]:
        arrived(j)
    for k in range(1, at.batches):
        mix_rows[k - 1].wait_recv()
        home = mixs_ref.at[c, at.from_rows(k)]
        last.append(wires.send(home, home, at.partner()))
    for copy in last:
        copy.wait_recv()
    for copy in own:
        copy.wait()
    wires.finish()
    line.drain(order)

    @pl.when(off_diagonal)
    def _():
        for swap in swaps:
            swap.wait_send()


def gather_inputs(x, w_query, w_key, w_value, w_mix, rel_table, vec, up, down):
    tokens, batches = lax.axis_size("seq"), lax.axis_size("batch")
    chips = tokens // 2
    outs = (
        like(x, tokens),
        like(w_query, tokens, 3),
        like(w_mix, 2, batches, chips),
        like(rel_table, 2, batches, chips),
        like(vec, tokens),
        like(up),
        like(down),
    )
    sends = 3 + 2 * (chips - 1) + tokens - 1 + 3 + 6 * (batches - 1) + 3 + chips - 1
    inputs = (x, w_query, w_key, w_value, w_mix, rel_table, vec, up, down)
    return comm_call(
        gather_kernel,
        "gather_inputs",
        0,
        outs,
        inputs,
        sends,
        7,
        scratch=gather_sems(chips),
        spec=HBM_SPEC,
    )


def norm_parts(values):
    average = jnp.mean(values, axis=-1, keepdims=True)
    centered = values - average
    variance = jnp.mean(centered * centered, axis=-1, keepdims=True)
    scale = lax.rsqrt(variance + norm_eps)
    return centered * scale, scale


def norm_back(grad, gain, unit, scale):
    inner = grad * gain
    mean = jnp.mean(inner, axis=-1, keepdims=True)
    slope = jnp.mean(inner * unit, axis=-1, keepdims=True)
    return scale * (inner - mean - unit * slope)


def line_pass(gather, reduce, order, work):
    def finish(j):
        work(j)
        reduce.send_last(j)

    for j in order:
        gather.arrive(j)
        finish(j)


def feed_kernel(
    xs_ref, qkvs_ref, tables_ref, x_ref, mixs_ref, vecs_ref, up_ref, down_ref, up2_ref,
    down2_ref, out_grad_ref,
    q_ref, k_ref, v_ref, qrev_ref, krev_ref, p_ref, ctx_ref, w_ref, table_ref,
    output_ref, pre_grad_ref, sums_ref, attn_ref, mix_ref, ups_ref, downs_ref, upbs_ref,
    segc_ref, place_ref, wide_ref, ends_ref, held_ref,
    got_ref, hid_ref, act_ref, slope_ref, part_ref, ffn_ref, grad_ref, inner_ref,
    back_ref, backs_ref, up_away_ref, down_away_ref, upb_away_ref,
    up_got_ref, down_got_ref, upb_got_ref, upg_ref, downg_ref, upb_ref, vec_ref,
    hid_send, hid_recv, ffn_send, ffn_recv, grad_send, grad_recv, back_send, back_recv,
    attn_send, attn_recv, ctx_send, ctx_recv, *sems,
):
    at = Place()
    wires = Wires(*sems)
    low, wide = jnp.bfloat16, jnp.float32
    b, s, z, c = at.row, at.part, at.chip, at.core
    order, returns = arrival_order(at), return_order(at)
    peers = at.seq_peers() + at.row_peers()
    barrier = pltpu.get_barrier_semaphore()
    for peer in peers:
        pl.semaphore_signal(barrier, inc=1, device_id=peer, device_id_type=MESH)
    last, own = [], []
    blocks = at.tokens
    units = p_ref.shape[0]

    def context_copy(u):
        g = u + c * (blocks // 2)
        slot, qb = g // blocks, g % blocks
        rows = pl.ds(pl.multiple_of(qb * BLOCK, BLOCK), BLOCK)
        head = 3 * z + c + slot
        src, dst = held_ref.at[slot, rows], got_ref.at[head]
        remote = pltpu.make_async_remote_copy(
            src_ref=src,
            dst_ref=dst,
            send_sem=ctx_send.at[u],
            recv_sem=ctx_recv.at[head],
            device_id=(b, qb),
            device_id_type=MESH,
        )
        return qb != s, remote, pltpu.make_async_copy(src, dst, ctx_recv.at[head])

    def leave(u):
        away, remote, here = context_copy(u)

        @pl.when(away)
        def _():
            remote.start()

        @pl.when(jnp.logical_not(away))
        def _():
            here.start()

    attend_kernel(
        xs_ref, qkvs_ref, tables_ref, vecs_ref, q_ref, k_ref, v_ref, qrev_ref, krev_ref, p_ref,
        ctx_ref, w_ref, table_ref, segc_ref, place_ref, wide_ref, ends_ref, held_ref,
        lambda: pl.semaphore_wait(barrier, len(peers)), leave,
    )
    lanes = x_ref.shape[1] // at.tokens
    hidden_here = up_ref.shape[1]
    vec_ref[...] = jnp.concatenate(
        [vecs_ref[part, :, :lanes].astype(wide) for part in range(at.tokens)], axis=1
    )
    bias3 = vec_ref[3:4]
    gain1, gain2 = vec_ref[4:5], vec_ref[5:6]
    shift1, shift2 = vec_ref[6:7], vec_ref[7:8]
    bias_down = vec_ref[8:9]
    partner = s + 1 - 2 * c
    up_rows = hidden_here // BLOCK
    bias_up = jnp.concatenate(
        [vecs_ref[s, 10 + i : 11 + i].astype(wide) for i in range(up_rows)]
        + [vecs_ref[partner, 10 + i : 11 + i].astype(wide) for i in range(up_rows)],
        axis=1,
    )
    shard_rows = mixs_ref.shape[3]
    for part in range(at.tokens):
        mix_ref[part * shard_rows : (part + 1) * shard_rows] = jnp.concatenate(
            [mixs_ref[part % 2, row, part // 2] for row in range(at.batches)], axis=1
        )
    for head in range(3 * at.chips):
        pltpu.make_async_copy(got_ref.at[head], got_ref.at[head], ctx_recv.at[head]).wait()
    pieces = [got_ref[head] for head in range(3 * at.chips)]
    context = jnp.concatenate(pieces, axis=1)
    pre_norm = x_ref[...].astype(wide) + dot_nn(context, mix_ref[...]) + bias3
    unit1, scale1 = norm_parts(pre_norm)
    hidden = unit1 * gain1 + shift1
    hid_ref[z] = hidden.astype(low)
    hid_line = LineGather(at, hid_ref, lambda j: j, (hid_send, hid_recv))
    ffn_line = LineReduce(at, part_ref, ffn_ref, (ffn_send, ffn_recv))
    hid_line.start()
    ffn_line.clear()

    def ffn(chip):
        rows = hid_ref[chip]
        inner = jnp.concatenate(
            [dot_nn(rows, up_ref[...]), dot_nn(rows, up2_ref[...])], axis=1
        )
        inner = inner + bias_up
        cdf = 0.5 * (1.0 + lax.erf(inner * math.sqrt(0.5)))
        act = (inner * cdf).astype(low)
        slope_ref[chip] = cdf + inner * (
            jnp.exp(-0.5 * inner * inner) * (1.0 / math.sqrt(2.0 * math.pi))
        )
        act_ref[chip] = act
        part_ref[chip] = (
            dot_nn(act[:, :hidden_here], down_ref[...])
            + dot_nn(act[:, hidden_here:], down2_ref[...])
        ).astype(low)

    ffn(z)
    line_pass(hid_line, ffn_line, order, ffn)
    ffn_line.pass_on(returns)
    total = part_ref[z].astype(wide) + ffn_line.collect()
    mixed = hidden + total + bias_down
    unit2, scale2 = norm_parts(mixed)
    output_ref[...] = (unit2 * gain2 + shift2).astype(low)
    out_grad = out_grad_ref[...].astype(wide)
    mixed_grad = norm_back(out_grad, gain2, unit2, scale2)
    grad_ref[z] = mixed_grad.astype(low)
    grad_line = LineGather(at, grad_ref, lambda j: j, (grad_send, grad_recv))
    back_line = LineReduce(at, back_ref, backs_ref, (back_send, back_recv))
    grad_line.start()
    back_line.clear()
    gain2_grad = jnp.sum(out_grad * unit2, axis=0, keepdims=True)
    shift2_grad = jnp.sum(out_grad, axis=0, keepdims=True)
    downb_grad = jnp.sum(mixed_grad, axis=0, keepdims=True)

    def back(chip):
        rows = grad_ref[chip]
        act_grad = jnp.concatenate(
            [dot_nt(rows, down_ref[...]), dot_nt(rows, down2_ref[...])], axis=1
        )
        inner_low = (act_grad * slope_ref[chip]).astype(low)
        inner_ref[chip] = inner_low
        back_ref[chip] = (
            dot_nt(inner_low[:, :hidden_here], up_ref[...])
            + dot_nt(inner_low[:, hidden_here:], up2_ref[...])
        ).astype(low)

    back(z)
    line_pass(grad_line, back_line, order, back)
    width = x_ref.shape[1]
    columns = width // at.batches
    inner_all = inner_ref[...].reshape(at.chips * BLOCK, 2 * hidden_here)
    act_all = act_ref[...].reshape(at.chips * BLOCK, 2 * hidden_here)
    hid_all = hid_ref[...].reshape(at.chips * BLOCK, width)
    grad_all = grad_ref[...].reshape(at.chips * BLOCK, width)
    near, away = slice(0, hidden_here), slice(hidden_here, 2 * hidden_here)
    up_grad = dot_tn(hid_all, inner_all)
    up_away_ref[...] = up_grad[:, away].astype(low)
    down_grad = dot_tn(grad_all, act_all)
    down_away_ref[...] = down_grad[:, away].astype(low)
    upb_grad = jnp.sum(inner_all.astype(wide), axis=0, keepdims=True)
    upb_away_ref[...] = jnp.broadcast_to(upb_grad[:, away], upb_away_ref.shape)
    halves = [
        wires.send(up_away_ref, up_got_ref, at.partner()),
        wires.send(down_away_ref, down_got_ref, at.partner()),
        wires.send(upb_away_ref, upb_got_ref, at.partner()),
    ]
    back_line.pass_on(returns)
    for copy in halves:
        copy.wait_recv()
    upb_ref[...] = jnp.broadcast_to(upb_grad[:, near], upb_ref.shape) + upb_got_ref[...]
    up_sum = (up_grad[:, near] + up_got_ref[...].astype(wide)).astype(low)
    down_sum = (down_grad[:, near] + down_got_ref[...].astype(wide)).astype(low)
    for row in range(at.batches):
        upg_ref[row] = up_sum[row * columns : (row + 1) * columns]
        downg_ref[row] = down_sum[row * columns : (row + 1) * columns]
    for k in range(1, at.batches):
        row, peer = at.along_rows(k)
        last.append(wires.send(upg_ref.at[row], ups_ref.at[b], peer))
        last.append(wires.send(downg_ref.at[row], downs_ref.at[b], peer))
        last.append(wires.send(upb_ref, upbs_ref.at[b], peer))
    own.append(wires.local(upg_ref.at[b], ups_ref.at[b]))
    own.append(wires.local(downg_ref.at[b], downs_ref.at[b]))
    own.append(wires.local(upb_ref, upbs_ref.at[b]))
    total = back_ref[z].astype(wide) + back_line.collect()
    hidden_grad = mixed_grad + total
    pre_grad = norm_back(hidden_grad, gain1, unit1, scale1)
    attn_ref[s] = pre_grad.astype(low)
    attn_line = LineGather(at, attn_ref, lambda j: 2 * j + c, (attn_send, attn_recv))
    attn_line.start()
    last.append(wires.send(attn_ref.at[s], attn_ref.at[s], at.partner()))
    pre_grad_ref[...] = pre_grad
    gain1_grad = jnp.sum(hidden_grad * unit1, axis=0, keepdims=True)
    shift1_grad = jnp.sum(hidden_grad, axis=0, keepdims=True)
    bias3_grad = jnp.sum(pre_grad, axis=0, keepdims=True)
    sums = jnp.concatenate(
        [bias3_grad, gain1_grad, gain2_grad, shift1_grad, shift2_grad, downb_grad]
        + [jnp.zeros((2, width), wide)],
        axis=0,
    )
    spare = jnp.zeros((8, BLOCK - lanes), wide)
    for part in range(at.tokens):
        sums_ref[part] = jnp.concatenate(
            [sums[:, part * lanes : (part + 1) * lanes], spare], axis=1
        )
    for j in order:
        attn_line.arrive(j)
        home = attn_ref.at[2 * j + c]
        last.append(wires.send(home, home, at.partner()))
    for copy in last:
        copy.wait_recv()
    for copy in own:
        copy.wait()
    wires.finish()
    for line in (hid_line, ffn_line, grad_line, back_line, attn_line):
        line.drain(order)

    def left(u, carry):
        away, remote, _ = context_copy(u)

        @pl.when(away)
        def _():
            remote.wait_send()

        return carry

    lax.fori_loop(0, units, left, 0)


def feed_forward(xs, qkvs, tables, x, mixs, vecs, up, down, up2, down2, out_grad, ident):
    tokens, batches = lax.axis_size("seq"), lax.axis_size("batch")
    chips = tokens // 2
    local_len, width = x.shape
    full_len = tokens * local_len
    columns = width // batches
    hidden_here = up.shape[1]
    buckets = tokens * tables.shape[3]
    blocks = full_len // BLOCK
    units = 3 * blocks // 2
    band_width = buckets + BLOCK
    pad_blocks = blocks + band_width // BLOCK - 1
    low, wide = jnp.bfloat16, jnp.float32
    outs = (
        jax.ShapeDtypeStruct((2, full_len, DH), low),
        jax.ShapeDtypeStruct((2, full_len, DH), low),
        jax.ShapeDtypeStruct((2, full_len, DH), low),
        jax.ShapeDtypeStruct((2, buckets, DH), low),
        jax.ShapeDtypeStruct((2, buckets, DH), low),
        jax.ShapeDtypeStruct((units, BLOCK, full_len), low),
        jax.ShapeDtypeStruct((tokens, local_len, 2 * DH), low),
        jax.ShapeDtypeStruct((width, 6 * DH), low),
        jax.ShapeDtypeStruct((buckets, width), low),
        jax.ShapeDtypeStruct(x.shape, low),
        jax.ShapeDtypeStruct(x.shape, wide),
        jax.ShapeDtypeStruct((tokens, 8, BLOCK), wide),
        jax.ShapeDtypeStruct((tokens,) + x.shape, low),
        jax.ShapeDtypeStruct((width, width), low),
        jax.ShapeDtypeStruct((batches, columns, hidden_here), low),
        jax.ShapeDtypeStruct((batches, columns, hidden_here), low),
        jax.ShapeDtypeStruct((batches, 8, hidden_here), wide),
    )
    block = (chips,) + x.shape
    wide_block = (chips, x.shape[0], 2 * hidden_here)
    slots = (chips + 1,) + x.shape
    up_half, bias_half = (width, hidden_here), (8, hidden_here)
    down_half = up_half
    scratch = [
        pltpu.VMEM((full_len, BLOCK), wide),
        pltpu.VMEM((2, pad_blocks, BLOCK, band_width), wide),
        pltpu.VMEM((BLOCK, full_len + buckets), wide),
        pltpu.VMEM((2, 2, 16, full_len), wide),
        pltpu.VMEM((2, full_len, DH), low),
        pltpu.VMEM((3 * chips, local_len, DH), low),
        pltpu.VMEM(block, low),
        pltpu.VMEM(wide_block, low),
        pltpu.VMEM(wide_block, wide),
        pltpu.VMEM(block, low),
        pltpu.VMEM(slots, low),
        pltpu.VMEM(block, low),
        pltpu.VMEM(wide_block, low),
        pltpu.VMEM(block, low),
        pltpu.VMEM(slots, low),
        pltpu.VMEM(up_half, low),
        pltpu.VMEM(down_half, low),
        pltpu.VMEM(bias_half, wide),
        pltpu.VMEM(up_half, low),
        pltpu.VMEM(down_half, low),
        pltpu.VMEM(bias_half, wide),
        pltpu.VMEM((batches, columns, hidden_here), low),
        pltpu.VMEM((batches, columns, hidden_here), low),
        pltpu.VMEM(bias_half, wide),
        pltpu.VMEM((16, width), wide),
    ]
    scratch += (gather_sems(chips) + reduce_sems(chips)) * 2 + gather_sems(chips)
    scratch += [pltpu.SemaphoreType.DMA((units,)), pltpu.SemaphoreType.DMA((3 * chips,))]
    inputs = (xs, qkvs, tables, x, mixs, vecs, up, down, up2, down2, out_grad)
    sends = 3 + 3 * (batches - 1) + chips
    return pl.pallas_call(
        feed_kernel,
        out_shape=outs,
        in_specs=[VMEM_SPEC] * len(inputs),
        out_specs=(VMEM_SPEC,) * len(outs),
        scratch_shapes=scratch + wire_scratch(sends, 5),
        compiler_params=pltpu.CompilerParams(
            collective_id=ident, has_side_effects=True, vmem_limit_bytes=FEED_VMEM
        ),
        name="feed_forward",
    )(*inputs)


def settle_kernel(
    vec_ref, col_ref, dcat_ref, rel_ref, w_ref, xs_ref, table_ref, ctx_ref, attn_ref,
    ins_ref, vec_all_ref, cols_ref, dw_all_ref, tab_all_ref, mix_all_ref,
    in_ref, dw_ref, tab_ref, mix_ref, half_ref, sum_ref, got_ref, vecs_ref, vec_low_ref,
    dws_ref, dw_low_ref, rels_ref, rel_low_ref, mixs_ref, mix_low_ref,
    line_send, line_recv, tab_send, tab_recv, *sems,
):
    at = Place()
    wires = Wires(*sems)
    low, wide = jnp.bfloat16, jnp.float32
    b, s, z, c = at.row, at.part, at.chip, at.core
    off_diagonal = b != z
    same, cross = (z, 2 * b + c), (z, 2 * b + 1 - c)
    meet(at.all_peers())
    width = w_ref.shape[0]
    columns = width // at.batches
    full_len = dcat_ref.shape[0]
    group = 2 * DH
    buckets = table_ref.shape[0]
    bucket_rows = buckets // at.batches

    dw_sends, mix_sends, vec_sends, rel_sends, last, own = [], [], [], [], [], []
    for k in range(1, at.batches):
        row, peer = at.along_rows(k)
        rows = pl.ds(pl.multiple_of(row * bucket_rows, bucket_rows), bucket_rows)
        rel_sends.append(wires.send(rel_ref.at[rows], rels_ref.at[k - 1], peer))

    for k in range(1, at.tokens):
        part, peer = at.along_seq(k)
        vec_sends.append(wires.send(vec_ref.at[part], vecs_ref.at[k - 1], peer))
    mine = 2 * b + c
    for k in range(1, 2 * at.batches):
        last.append(wires.send(col_ref, cols_ref.at[mine], at.along_plane(k)[2]))
    own.append(wires.local(col_ref, cols_ref.at[mine]))

    def input_part(chip, core):
        start = pl.multiple_of((2 * chip + core) * BLOCK, BLOCK)
        in_ref[chip, core] = dot_nt(dcat_ref[pl.ds(start, BLOCK)], w_ref[...]).astype(low)

    order = far_order(at)
    places = order + [z]
    halves = []
    for chip in places:
        input_part(chip, 1 - c)
        halves.append(wires.send(in_ref.at[chip, 1 - c], half_ref.at[chip], at.partner()))
    line = LineReduce(at, sum_ref, got_ref, (line_send, line_recv))
    line.clear()
    for i, chip in enumerate(places):
        input_part(chip, c)
        halves[i].wait_recv()
        total = in_ref[chip, c].astype(wide) + half_ref[chip].astype(wide)
        sum_ref[chip] = total.astype(low)
        if i < len(order):
            line.send_last(chip)

    whole = xs_ref[...].reshape(full_len, width)
    dw = dot_tn(whole, dcat_ref[...])
    dw_rel = dot_tn(table_ref[...], rel_ref[...])
    dw = jnp.concatenate([dw[:, : 2 * group] + dw_rel, dw[:, 2 * group :]], axis=1)
    for row in range(at.batches):
        dw_ref[row] = dw[row * columns : (row + 1) * columns].astype(low)
    for k in range(1, at.batches):
        row, peer = at.along_rows(k)
        dw_sends.append(wires.send(dw_ref.at[row], dws_ref.at[k - 1], peer))

    rows = pl.ds(pl.multiple_of(b * bucket_rows, bucket_rows), bucket_rows)
    total = rel_ref[rows].astype(wide)
    for k in range(1, at.batches):
        rel_sends[k - 1].wait_recv()
        total = total + rels_ref[k - 1].astype(wide)
    rel_low_ref[...] = total.astype(low)
    table_rows = bucket_rows // 2
    for row in range(at.batches):
        piece = dot_nt(rel_low_ref[...], w_ref[row * columns : (row + 1) * columns, : 2 * group])
        for core in range(2):
            tab_ref[core, row] = piece[core * table_rows : (core + 1) * table_rows].astype(low)

    def tab_copy(k, d):
        row = lax.rem(b + k, at.batches)
        core = jnp.where(d == 0, c, 1 - c)
        return pltpu.make_async_remote_copy(
            src_ref=tab_ref.at[core, row],
            dst_ref=tab_all_ref.at[s],
            send_sem=tab_send.at[2 * k + d],
            recv_sem=tab_recv.at[s],
            device_id=(row, 2 * b + core),
            device_id_type=MESH,
        )

    tab_stay = pltpu.make_async_copy(
        tab_ref.at[c, b], tab_all_ref.at[s], sems[2].at[wires.used[1]]
    )
    wires.used[1] += 1
    for k in range(at.batches):
        for d in range(2):
            if k or d:
                tab_copy(k, d).start()

    @pl.when(off_diagonal)
    def _():
        tab_copy(0, 0).start()

    @pl.when(jnp.logical_not(off_diagonal))
    def _():
        tab_stay.start()

    line.pass_on(order[:1])
    mix = dot_tn(
        ctx_ref[...].reshape(full_len, group), attn_ref[...].reshape(full_len, width)
    )
    for row in range(at.batches):
        mix_ref[row] = mix[:, row * columns : (row + 1) * columns].astype(low)
    for k in range(1, at.batches):
        row, peer = at.along_rows(k)
        mix_sends.append(wires.send(mix_ref.at[row], mixs_ref.at[k - 1], peer))

    line.pass_on(order[1:2])
    total = dw_ref[b].astype(wide)
    for k in range(1, at.batches):
        dw_sends[k - 1].wait_recv()
        total = total + dws_ref[k - 1].astype(wide)
    shard_rows = dw_low_ref.shape[1]
    for half in range(2):
        dw_low_ref[half] = total[half * shard_rows : (half + 1) * shard_rows].astype(low)
    k = wires.used[0]
    wires.used[0] += 1
    move = pltpu.make_async_remote_copy(
        src_ref=dw_low_ref.at[c],
        dst_ref=dw_all_ref.at[c],
        send_sem=sems[0].at[k],
        recv_sem=sems[1].at[k],
        device_id=same,
        device_id_type=MESH,
    )
    stay = pltpu.make_async_copy(
        dw_low_ref.at[c], dw_all_ref.at[c], sems[2].at[wires.used[1]]
    )
    wires.used[1] += 1

    @pl.when(off_diagonal)
    def _():
        move.start()

    @pl.when(jnp.logical_not(off_diagonal))
    def _():
        stay.start()

    last.append(wires.send(dw_low_ref.at[1 - c], dw_all_ref.at[c], cross))

    line.pass_on(order[2:])
    total = mix_ref[b].astype(wide)
    for k in range(1, at.batches):
        mix_sends[k - 1].wait_recv()
        total = total + mixs_ref[k - 1].astype(wide)
    mix_low_ref[...] = total.astype(low)
    last.append(wires.send(mix_low_ref, mix_all_ref.at[c], at.partner()))
    own.append(wires.local(mix_low_ref, mix_all_ref.at[c]))

    total = vec_ref[s]
    for k in range(1, at.tokens):
        vec_sends[k - 1].wait_recv()
        total = total + vecs_ref[k - 1]
    vec_low_ref[...] = total
    for k in range(1, at.batches):
        last.append(wires.send(vec_low_ref, vec_all_ref.at[b], at.along_rows(k)[1]))
    own.append(wires.local(vec_low_ref, vec_all_ref.at[b]))

    ins_ref[...] = sum_ref[z].astype(wide) + line.collect()
    for copy in last:
        copy.wait_recv()
    for copy in own:
        copy.wait()
    wires.finish()
    line.drain(order)
    for part in range(at.tokens):
        landed = pltpu.make_async_remote_copy(
            src_ref=tab_all_ref.at[part],
            dst_ref=tab_all_ref.at[part],
            send_sem=tab_send.at[0],
            recv_sem=tab_recv.at[part],
            device_id=at.partner(),
            device_id_type=MESH,
        )

        @pl.when(jnp.logical_or(off_diagonal, s != part))
        def _():
            landed.wait_recv()

    for k in range(at.batches):
        for d in range(2):
            if k or d:
                tab_copy(k, d).wait_send()

    @pl.when(off_diagonal)
    def _():
        tab_copy(0, 0).wait_send()
        move.wait()

    @pl.when(jnp.logical_not(off_diagonal))
    def _():
        tab_stay.wait()
        stay.wait()


def settle_grads(vec, cols, dcat, rel, w_cat, xs, table, ctx, attn_all, ident):
    tokens, batches = lax.axis_size("seq"), lax.axis_size("batch")
    chips = tokens // 2
    low, wide = jnp.bfloat16, jnp.float32
    local_len, width = xs.shape[1:]
    columns, group = width // batches, dcat.shape[1]
    buckets = table.shape[0]
    half = (chips, local_len, width)
    dw_pieces = (2, columns // 2, group)
    mix_piece = (2 * DH, columns)
    dw_piece, rel_piece = (columns, group), (buckets // batches, rel.shape[1])
    outs = (
        jax.ShapeDtypeStruct((local_len, width), wide),
        jax.ShapeDtypeStruct((batches,) + vec.shape[1:], wide),
        like(cols, 2 * batches),
        jax.ShapeDtypeStruct(dw_pieces, low),
        jax.ShapeDtypeStruct((tokens, buckets // tokens, columns), low),
        jax.ShapeDtypeStruct((2,) + mix_piece, low),
    )
    scratch = [
        pltpu.VMEM((chips, 2, local_len, width), low),
        pltpu.VMEM((batches,) + dw_piece, low),
        pltpu.VMEM((2, batches, buckets // tokens, columns), low),
        pltpu.VMEM((batches,) + mix_piece, low),
        pltpu.VMEM(half, low),
        pltpu.VMEM(half, low),
        pltpu.VMEM((chips + 1, local_len, width), low),
        pltpu.VMEM((tokens - 1,) + vec.shape[1:], wide),
        pltpu.VMEM(vec.shape[1:], wide),
        pltpu.VMEM((batches - 1,) + dw_piece, low),
        pltpu.VMEM(dw_pieces, low),
        pltpu.VMEM((batches - 1,) + rel_piece, low),
        pltpu.VMEM(rel_piece, low),
        pltpu.VMEM((batches - 1,) + mix_piece, low),
        pltpu.VMEM(mix_piece, low),
    ]
    scratch += reduce_sems(chips)
    scratch += [pltpu.SemaphoreType.DMA((2 * batches,)), pltpu.SemaphoreType.DMA((tokens,))]
    sends = 4 * (batches - 1) + chips + tokens - 1 + 2 * batches - 1 + 3
    inputs = (vec, cols, dcat, rel, w_cat, xs, table, ctx, attn_all)
    return comm_call(settle_kernel, "settle_grads", ident, outs, inputs, sends, 6, scratch=scratch)


def finish_kernel(
    pre_ref, ins_ref, vecs_ref, cols_ref, dws_ref, tabs_ref, mixs_ref, ups_ref, downs_ref,
    upbs_ref, last_ref,
    output_ref, input_ref, dq_ref, dk_ref, dv_ref, mix_ref, table_ref, bias_ref, gain_ref, shift_ref,
    up_ref, upb_ref, down_ref, downb_ref,
):
    at = Place()
    wide = jnp.float32

    def total(ref):
        out = ref[0].astype(wide)
        for k in range(1, ref.shape[0]):
            out = out + ref[k].astype(wide)
        return out

    output_ref[...] = last_ref[...]
    input_ref[...] = pre_ref[...] + ins_ref[...]
    up_ref[...] = total(ups_ref)
    down_ref[...] = total(downs_ref)
    upb_ref[...] = total(upbs_ref)[0:1]
    table_ref[...] = total(tabs_ref)
    group = 2 * DH
    spare = jnp.zeros((dws_ref.shape[1], DH), wide)
    for i, ref in enumerate((dq_ref, dk_ref, dv_ref)):
        lower = dws_ref[0, :, i * group : (i + 1) * group].astype(wide)
        upper = dws_ref[1, :, i * group : (i + 1) * group].astype(wide)
        ref[...] = jnp.concatenate([lower, spare], axis=1) + jnp.concatenate(
            [spare, upper], axis=1
        )
    rows = mix_ref.shape[0]
    lower, upper = mixs_ref[0].astype(wide), mixs_ref[1].astype(wide)
    spare = jnp.zeros((DH, lower.shape[1]), wide)
    whole = jnp.concatenate([lower, spare], axis=0) + jnp.concatenate([spare, upper], axis=0)
    mix_ref[...] = jnp.where(at.core == 0, whole[:rows], whole[rows:])
    small = total(vecs_ref)
    lanes = bias_ref.shape[1]
    cols = [cols_ref[core, 0:1] for core in range(2)]
    for row in range(1, at.batches):
        cols = [cols[core] + cols_ref[2 * row + core, 0:1] for core in range(2)]
    spare = jnp.zeros((1, DH), wide)
    biases = []
    for i in range(3):
        lower, upper = [part[:, i * group : (i + 1) * group] for part in cols]
        both = jnp.concatenate([lower, spare], axis=1) + jnp.concatenate([spare, upper], axis=1)
        biases.append(jnp.where(at.core == 0, both[:, :lanes], both[:, lanes:]))
    bias_ref[...] = jnp.concatenate(biases + [small[0:1, :lanes]], axis=0)
    gain_ref[...] = small[1:3, :lanes]
    shift_ref[...] = small[3:5, :lanes]
    downb_ref[...] = small[5:6, :lanes]


def finish(pre_grad, parts, shapes):
    inputs = (pre_grad,) + tuple(parts)
    return pl.pallas_call(
        finish_kernel,
        out_shape=(like(parts[-1]),)
        + tuple(jax.ShapeDtypeStruct(shape, jnp.float32) for shape in shapes),
        in_specs=[VMEM_SPEC] * len(inputs),
        out_specs=(VMEM_SPEC,) * (len(shapes) + 1),
        compiler_params=pltpu.CompilerParams(vmem_limit_bytes=COMM_VMEM),
        name="finish",
    )(*inputs)


def fits_fast(layer_input, table_shard, hidden_here):
    rows, local_len, width = layer_input.shape
    tokens, batches = lax.axis_size("seq"), lax.axis_size("batch")
    return (
        rows == 1
        and local_len == BLOCK
        and tokens == 2 * batches
        and width == 3 * DH * batches
        and (table_shard.shape[0] * tokens) % (4 * BLOCK) == 0
        and tokens == 8
        and 10 + hidden_here // BLOCK <= 16
        and hidden_here % BLOCK == 0
    )


def fast_body(
    layer_input, segment_ids, w_query, w_key, w_value, w_mix, rel_table, attn_biases,
    norm_gains, norm_shifts, w_up, up_bias, w_down, down_bias, out_grad,
):
    local_len, width = layer_input.shape[1:]
    low = jnp.bfloat16
    shard_rows, shard_cols = w_query.shape
    lanes = attn_biases.shape[1]
    hidden_here = w_up.shape[1]
    x = layer_input[0]
    pack = jnp.concatenate([attn_biases, norm_gains, norm_shifts, down_bias[None]], axis=0)
    pack = jnp.pad(pack, ((0, 0), (0, BLOCK - lanes)))
    pack = jnp.concatenate(
        [pack, segment_ids.astype(low), up_bias.reshape(hidden_here // BLOCK, BLOCK)], axis=0
    )
    pack = jnp.pad(pack, ((0, 16 - pack.shape[0]), (0, 0)))
    weights = (w_query, w_key, w_value, w_mix, rel_table, pack, w_up, w_down)
    xs, qkvs, mixs, tables, vecs, up2, down2 = gather_inputs(
        *[pltpu.with_memory_space_constraint(a, pltpu.HBM) for a in (x,) + weights]
    )
    forward = feed_forward(
        xs, qkvs, tables, x, mixs, vecs, w_up, w_down, up2, down2, out_grad[0], 1
    )
    q, k, v, qrev, krev, probs, ctx, w_cat, table = forward[:9]
    output, pre_grad, sums, attn_all, m_mix, ups, downs, upbs = forward[9:]
    dcat, rel_grad, cols = attend_back(q, k, v, qrev, krev, probs, m_mix, attn_all)
    ins, vec_all, cols_all, dw_all, tab_all, mix_all = settle_grads(
        sums, cols, dcat, rel_grad, w_cat, xs, table, ctx, attn_all, 2
    )
    shard = (shard_rows, shard_cols)
    shapes = (
        x.shape, shard, shard, shard, shard, rel_table.shape, (4, lanes), (2, lanes), (2, lanes),
        (width // lax.axis_size("batch"), hidden_here), (1, hidden_here),
        (width // lax.axis_size("batch"), hidden_here), (1, lanes),
    )
    grads = finish(
        pre_grad,
        (ins, vec_all, cols_all, dw_all, tab_all, mix_all, ups, downs, upbs, output),
        shapes,
    )
    output, input_grad, dq, dk, dv, dmix, dtable = grads[:7]
    dbias, dgain, dshift, dup, dupb, ddown, ddownb = grads[7:]
    return (
        output[None], input_grad[None], dq, dk, dv, dmix, dtable, dbias, dgain, dshift,
        dup, dupb.reshape(hidden_here), ddown.T, ddownb.reshape(lanes),
    )


def body(
    layer_input,
    segment_ids,
    w_query,
    w_key,
    w_value,
    w_mix,
    rel_table,
    attn_biases,
    norm_gains,
    norm_shifts,
    w_up,
    up_bias,
    w_down,
    down_bias,
    out_grad,
):
    if fits_fast(layer_input, rel_table, w_up.shape[1]):
        return fast_body(
            layer_input, segment_ids, w_query, w_key, w_value, w_mix, rel_table, attn_biases,
            norm_gains, norm_shifts, w_up, up_bias, w_down, down_bias, out_grad,
        )
    rows, local_len, width = layer_input.shape
    full_len = local_len * lax.axis_size("seq")
    tokens_here = local_len * rows
    highest_prec = lax.Precision.HIGHEST
    parts = (
        lax.all_gather(w_query, "batch", axis=1, tiled=True),
        lax.all_gather(w_key, "batch", axis=1, tiled=True),
        lax.all_gather(w_value, "batch", axis=1, tiled=True),
        lax.all_gather(w_mix, "batch", axis=1, tiled=True),
        lax.all_gather(rel_table, "batch", axis=1, tiled=True),
    )
    whole = (
        lax.all_gather(parts[0], "seq", axis=0, tiled=True),
        lax.all_gather(parts[1], "seq", axis=0, tiled=True),
        lax.all_gather(parts[2], "seq", axis=0, tiled=True),
        lax.all_gather(parts[3], "seq", axis=0, tiled=True),
        lax.all_gather(parts[4], "seq", axis=0, tiled=True),
        lax.all_gather(attn_biases, "seq", axis=1, tiled=True),
        lax.all_gather(norm_gains, "seq", axis=1, tiled=True),
        lax.all_gather(norm_shifts, "seq", axis=1, tiled=True),
        lax.all_gather(down_bias, "seq", axis=0, tiled=True),
    )
    m_query, m_key, m_value, m_mix, table, biases, gains, shifts, bias_down = whole
    flat_input = jnp.swapaxes(layer_input, 0, 1).reshape(tokens_here, width)
    queries = (jnp.dot(flat_input, m_query, preferred_element_type=jnp.float32) + biases[0]).astype(
        jnp.bfloat16
    )
    keys_here = (jnp.dot(flat_input, m_key, preferred_element_type=jnp.float32) + biases[1]).astype(
        jnp.bfloat16
    )
    values_here = (
        jnp.dot(flat_input, m_value, preferred_element_type=jnp.float32) + biases[2]
    ).astype(jnp.bfloat16)
    query_rel = (jnp.dot(table, m_query, preferred_element_type=jnp.float32) + biases[0]).astype(
        jnp.bfloat16
    )
    key_rel = (jnp.dot(table, m_key, preferred_element_type=jnp.float32) + biases[1]).astype(
        jnp.bfloat16
    )
    local_seg = jnp.swapaxes(segment_ids, 0, 1).astype(jnp.bfloat16)
    keys_all, values_all, seg_all = (
        lax.all_gather(keys_here.reshape(local_len, rows, width), "seq", axis=0, tiled=True),
        lax.all_gather(values_here.reshape(local_len, rows, width), "seq", axis=0, tiled=True),
        lax.all_gather(local_seg, "seq", axis=0, tiled=True),
    )
    buckets = table.shape[0]
    offset = lax.axis_index("seq") * local_len
    bucket_iota = jnp.arange(buckets, dtype=jnp.int32)
    inner_cols = (bucket_iota > 0) & (bucket_iota < buckets - 1)
    same_doc = (
        jnp.swapaxes(local_seg, 0, 1)[:, None, :, None]
        == jnp.swapaxes(seg_all, 0, 1)[:, None, None, :]
    )
    score_scale = 1.0 / math.sqrt(3.0 * DH)
    head_queries = split_heads(queries.reshape(local_len, rows, width))
    head_keys = split_heads(keys_all)
    head_values = split_heads(values_all)
    rel_queries = split_table(query_rel)
    rel_keys = split_table(key_rel)

    def forward_group(carry, group):
        g_query, g_key, g_value, g_qrel, g_krel = group
        total, near_pull, far_pull, window = relative_scores(
            g_query, g_key, g_krel, g_qrel, offset, full_len
        )
        scores = jnp.where(same_doc, total * score_scale, masked_score)
        highest = jnp.max(scores, axis=-1, keepdims=True)
        exponent = jnp.exp(scores - highest)
        denominator = jnp.sum(exponent, axis=-1, keepdims=True)
        weights_low = (exponent / denominator).astype(jnp.bfloat16)
        context = jnp.einsum(
            "rgij,rgjd->rgid", weights_low, g_value, preferred_element_type=jnp.float32
        )
        return (carry, (context, (highest + jnp.log(denominator))[..., 0]))

    unused, (context_groups, log_totals) = lax.scan(
        forward_group, None, (head_queries, head_keys, head_values, rel_queries, rel_keys)
    )
    context_low = join_heads(context_groups).reshape(tokens_here, width).astype(jnp.bfloat16)
    pre_norm = (
        flat_input.astype(jnp.float32)
        + jnp.dot(context_low, m_mix, preferred_element_type=jnp.float32)
        + biases[3]
    )
    hidden, norm1_pull = jax.vjp(
        normalize, pre_norm, gains[0].astype(jnp.float32), shifts[0].astype(jnp.float32)
    )
    hidden_low = hidden.astype(jnp.bfloat16)

    def spread_rows(rows_low):
        return lax.all_gather(rows_low, "seq", axis=0, tiled=True)

    def hidden_sums(make_term):
        return lax.psum_scatter(
            make_term(jnp.int32(0), tokens_here * lax.axis_size("seq")),
            "seq",
            scatter_dimension=0,
            tiled=True,
        )

    hidden_rows = spread_rows(hidden_low)
    inner = jnp.dot(hidden_rows, w_up, preferred_element_type=jnp.float32) + up_bias
    act, gelu_pull = jax.vjp(exact_gelu, inner)
    act_low = act.astype(jnp.bfloat16)

    def down_rows(start, count):
        return jnp.dot(act_low, w_down, preferred_element_type=jnp.float32)

    ffn_result = hidden_sums(down_rows)
    mixed = hidden + ffn_result + bias_down
    output, norm2_pull = jax.vjp(
        normalize, mixed, gains[1].astype(jnp.float32), shifts[1].astype(jnp.float32)
    )
    flat_grad = jnp.swapaxes(out_grad, 0, 1).reshape(tokens_here, width).astype(jnp.float32)
    mixed_grad, gain2_grad, shift2_grad = norm2_pull(flat_grad)
    ffn_grad_low = mixed_grad.astype(jnp.bfloat16)
    grad_rows = spread_rows(ffn_grad_low)
    act_grad = jnp.einsum("nd,fd->nf", grad_rows, w_down, preferred_element_type=jnp.float32)
    inner_low = gelu_pull(act_grad)[0].astype(jnp.bfloat16)
    up_part = jnp.einsum("nd,nf->df", hidden_rows, inner_low, preferred_element_type=jnp.float32)
    upb_part = jnp.sum(inner_low.astype(jnp.float32), axis=0)
    down_part = jnp.einsum("nf,nd->fd", act_low, grad_rows, preferred_element_type=jnp.float32)

    def back_rows(start, count):
        return jnp.einsum("nf,df->nd", inner_low, w_up, preferred_element_type=jnp.float32)

    hidden_grad = mixed_grad + hidden_sums(back_rows)
    pre_grad, gain1_grad, shift1_grad = norm1_pull(hidden_grad)
    attn_low = pre_grad.astype(jnp.bfloat16)
    mix_whole = jnp.einsum("nd,ne->de", context_low, attn_low, preferred_element_type=jnp.float32)
    context_grad = jnp.einsum(
        "ne,de->nd", attn_low, m_mix, preferred_element_type=jnp.float32
    ).astype(jnp.bfloat16)
    head_context_grad = split_heads(context_grad.reshape(local_len, rows, width))

    def query_side(group):
        g_query, g_key, g_value, g_qrel, g_krel, g_dctx, g_lse = group
        total, near_pull, far_pull, window = relative_scores(
            g_query, g_key, g_krel, g_qrel, offset, full_len
        )
        scores = jnp.where(same_doc, total * score_scale, masked_score)
        weights_now = jnp.exp(scores - g_lse[..., None])
        prob_grad = jnp.einsum(
            "rgid,rgjd->rgij", g_dctx, g_value, preferred_element_type=jnp.float32
        )
        inner_sum = jnp.sum(weights_now * prob_grad, axis=-1)
        score_grad = (weights_now * (prob_grad - inner_sum[..., None])).astype(jnp.bfloat16)
        grad_wide = score_grad.astype(jnp.float32)
        near_grad = near_pull(grad_wide)[0]
        near_low = jnp.where(inner_cols, near_grad, 0.0).astype(jnp.bfloat16)
        near_ends = end_columns(near_grad)
        query_part = jnp.einsum(
            "rgij,rgjd->rgid", score_grad, g_key, preferred_element_type=jnp.float32
        )
        query_part = (
            query_part
            + jnp.einsum("rgib,gbd->rgid", near_low, g_krel, preferred_element_type=jnp.float32)
            + end_terms(near_ends, g_krel)
        )
        krel_part = with_ends(
            jnp.einsum("rgib,rgid->gbd", near_low, g_query, preferred_element_type=jnp.float32),
            end_rows(near_ends, g_query),
        )
        return (
            weights_now,
            score_grad,
            grad_wide,
            far_pull,
            window,
            inner_sum,
            query_part * score_scale,
            krel_part * score_scale,
        )

    query_groups = (
        head_queries,
        head_keys,
        head_values,
        rel_queries,
        rel_keys,
        head_context_grad,
        log_totals,
    )

    def all_grads(carry, group):
        weights_now, score_grad, grad_wide, far_pull, window, inner_sum, query_part, krel_part = (
            query_side(group)
        )
        g_query, g_key, g_value, g_qrel, g_krel, g_dctx, g_lse = group
        cross_grad, end_grad = far_pull(grad_wide)
        cross_low = cross_grad.astype(jnp.bfloat16)
        key_part = jnp.einsum(
            "rgij,rgid->rgjd", score_grad, g_query, preferred_element_type=jnp.float32
        )
        band_part = jnp.einsum(
            "rgmb,gbd->rgmd", cross_low, g_qrel, preferred_element_type=jnp.float32
        )
        key_part = (
            key_part
            + unband(band_part, offset, full_len, buckets // 2)
            + end_terms(end_grad, g_qrel)
        )
        value_part = jnp.einsum(
            "rgij,rgid->rgjd",
            weights_now.astype(jnp.bfloat16),
            g_dctx,
            preferred_element_type=jnp.float32,
        )
        qrel_part = with_ends(
            jnp.einsum("rgmb,rgmd->gbd", cross_low, window, preferred_element_type=jnp.float32),
            end_rows(end_grad, g_key),
        )
        return (
            carry,
            (query_part, key_part * score_scale, value_part, qrel_part * score_scale, krel_part),
        )

    unused, (dq_groups, dk_groups, dv_groups, dqrel_groups, dkrel_groups) = lax.scan(
        all_grads, None, query_groups
    )
    key_sum, value_sum = (
        lax.psum_scatter(join_heads(dk_groups), "seq", scatter_dimension=0, tiled=True),
        lax.psum_scatter(join_heads(dv_groups), "seq", scatter_dimension=0, tiled=True),
    )
    key_grads = key_sum.reshape(tokens_here, width).astype(jnp.bfloat16)
    value_grads = value_sum.reshape(tokens_here, width).astype(jnp.bfloat16)
    query_grads = join_heads(dq_groups).reshape(tokens_here, width).astype(jnp.bfloat16)
    qrel_grad = join_table(dqrel_groups)
    krel_grad = join_table(dkrel_groups)
    input_grad = pre_grad + jnp.einsum(
        "ne,de->nd", query_grads, m_query, preferred_element_type=jnp.float32
    )
    input_grad = input_grad + jnp.einsum(
        "ne,de->nd", key_grads, m_key, preferred_element_type=jnp.float32
    )
    input_grad = input_grad + jnp.einsum(
        "ne,de->nd", value_grads, m_value, preferred_element_type=jnp.float32
    )
    query_whole = jnp.einsum(
        "nd,ne->de", flat_input, query_grads, preferred_element_type=jnp.float32
    ) + jnp.einsum(
        "bd,be->de", table, qrel_grad, precision=highest_prec, preferred_element_type=jnp.float32
    )
    key_whole = jnp.einsum(
        "nd,ne->de", flat_input, key_grads, preferred_element_type=jnp.float32
    ) + jnp.einsum(
        "bd,be->de", table, krel_grad, precision=highest_prec, preferred_element_type=jnp.float32
    )
    value_whole = jnp.einsum(
        "nd,ne->de", flat_input, value_grads, preferred_element_type=jnp.float32
    )
    table_whole = jnp.einsum(
        "be,de->bd", qrel_grad, m_query, precision=highest_prec, preferred_element_type=jnp.float32
    ) + jnp.einsum(
        "be,de->bd", krel_grad, m_key, precision=highest_prec, preferred_element_type=jnp.float32
    )
    bias_whole = jnp.stack(
        [
            jnp.sum(query_grads.astype(jnp.float32), axis=0) + jnp.sum(qrel_grad, axis=0),
            jnp.sum(key_grads.astype(jnp.float32), axis=0) + jnp.sum(krel_grad, axis=0),
            jnp.sum(value_grads.astype(jnp.float32), axis=0),
            jnp.sum(pre_grad, axis=0),
        ]
    )
    gain_whole = jnp.stack([gain1_grad, gain2_grad])
    shift_whole = jnp.stack([shift1_grad, shift2_grad])
    downb_whole = jnp.sum(mixed_grad, axis=0)
    seq_parts = (
        lax.psum_scatter(query_whole, "seq", scatter_dimension=0, tiled=True),
        lax.psum_scatter(key_whole, "seq", scatter_dimension=0, tiled=True),
        lax.psum_scatter(value_whole, "seq", scatter_dimension=0, tiled=True),
        lax.psum_scatter(mix_whole, "seq", scatter_dimension=0, tiled=True),
        lax.psum_scatter(table_whole, "seq", scatter_dimension=0, tiled=True),
        lax.psum_scatter(bias_whole, "seq", scatter_dimension=1, tiled=True),
        lax.psum_scatter(gain_whole, "seq", scatter_dimension=1, tiled=True),
        lax.psum_scatter(shift_whole, "seq", scatter_dimension=1, tiled=True),
        lax.psum_scatter(downb_whole, "seq", scatter_dimension=0, tiled=True),
    )
    batch_parts = (
        lax.psum_scatter(seq_parts[0], "batch", scatter_dimension=1, tiled=True),
        lax.psum_scatter(seq_parts[1], "batch", scatter_dimension=1, tiled=True),
        lax.psum_scatter(seq_parts[2], "batch", scatter_dimension=1, tiled=True),
        lax.psum_scatter(seq_parts[3], "batch", scatter_dimension=1, tiled=True),
        lax.psum_scatter(seq_parts[4], "batch", scatter_dimension=1, tiled=True),
        lax.psum_scatter(up_part, "batch", scatter_dimension=0, tiled=True),
        lax.psum_scatter(down_part, "batch", scatter_dimension=1, tiled=True),
    )
    small_parts = lax.psum(
        (seq_parts[5], seq_parts[6], seq_parts[7], seq_parts[8], upb_part), "batch"
    )
    layer_output = jnp.swapaxes(output.reshape(local_len, rows, width), 0, 1).astype(jnp.bfloat16)
    input_back = jnp.swapaxes(input_grad.reshape(local_len, rows, width), 0, 1)
    return (
        layer_output,
        input_back,
        batch_parts[0],
        batch_parts[1],
        batch_parts[2],
        batch_parts[3],
        batch_parts[4],
        small_parts[0],
        small_parts[1],
        small_parts[2],
        batch_parts[5],
        small_parts[4],
        batch_parts[6],
        small_parts[3],
    )


def solution(mesh):
    return jax.shard_map(
        body,
        mesh=mesh,
        in_specs=(
            P("batch", "seq", None),
            P("batch", "seq"),
            P("seq", "batch"),
            P("seq", "batch"),
            P("seq", "batch"),
            P("seq", "batch"),
            P("seq", "batch"),
            P(None, "seq"),
            P(None, "seq"),
            P(None, "seq"),
            P(None, "seq"),
            P("seq"),
            P("seq", None),
            P("seq"),
            P("batch", "seq", None),
        ),
        out_specs=(
            P("batch", "seq", None),
            P("batch", "seq", None),
            P("seq", "batch"),
            P("seq", "batch"),
            P("seq", "batch"),
            P("seq", "batch"),
            P("seq", "batch"),
            P(None, "seq"),
            P(None, "seq"),
            P(None, "seq"),
            P("batch", "seq"),
            P("seq"),
            P("seq", "batch"),
            P("seq"),
        ),
        check_vma=False,
    )
```

```python
import math

import jax
import jax.numpy as jnp
from jax import lax
from jax.experimental import pallas as pl
from jax.experimental.pallas import tpu as pltpu
from jax.sharding import PartitionSpec as P

DH = 64


masked_score = -1e30
norm_eps = 1e-06
pair_heads = 2


def normalize(values, gain, shift):
    average = jnp.mean(values, axis=-1, keepdims=True)
    centered = values - average
    variance = jnp.mean(centered * centered, axis=-1, keepdims=True)
    return centered * lax.rsqrt(variance + norm_eps) * gain + shift


def exact_gelu(values):
    return jax.nn.gelu(values, approximate=False)


def split_heads(matrix):
    length, rows, width = matrix.shape
    groups = width // (pair_heads * DH)
    return matrix.reshape(length, rows, groups, pair_heads, DH).transpose(2, 1, 3, 0, 4)


def join_heads(matrix):
    groups, rows, pair, length, depth = matrix.shape
    return matrix.transpose(3, 1, 0, 2, 4).reshape(length, rows, groups * pair * depth)


def split_table(matrix):
    buckets, width = matrix.shape
    return matrix.reshape(buckets, width // (pair_heads * DH), pair_heads, DH).transpose(1, 2, 0, 3)


def join_table(matrix):
    groups, pair, buckets, depth = matrix.shape
    return matrix.transpose(2, 0, 1, 3).reshape(buckets, groups * pair * depth)


def table_ends(table):
    return jnp.stack([table[:, 0], table[:, -1]], axis=1)


def near_skew(table_prod, offset, full_len):
    lead = table_prod.shape[:-2]
    count, buckets = table_prod.shape[-2:]
    span = buckets // 2
    lead_pad = [(0, 0)] * len(lead)
    flipped = jnp.pad(table_prod[..., ::-1], lead_pad + [(0, 0), (0, count)])
    sheared = flipped.reshape(lead + (count * (buckets + count),))[
        ..., : count * (buckets + count - 1)
    ]
    sheared = sheared.reshape(lead + (count, buckets + count - 1))
    spread = jnp.pad(sheared, lead_pad + [(0, 0), (full_len, full_len)])
    band = lax.dynamic_slice_in_dim(
        spread, full_len + span - 1 - offset, full_len, axis=len(lead) + 1
    )
    distance = (offset + jnp.arange(count, dtype=jnp.int32))[:, None] - jnp.arange(
        full_len, dtype=jnp.int32
    )[None, :]
    return jnp.where(
        distance <= -span,
        table_prod[..., 0:1],
        jnp.where(distance >= span - 1, table_prod[..., buckets - 1 :], band),
    )


def far_place(cross, end_vals, offset, count, full_len):
    lead = cross.shape[:-2]
    band_len, buckets = cross.shape[-2:]
    span = buckets // 2
    lead_pad = [(0, 0)] * len(lead)
    turned = jnp.swapaxes(cross, -1, -2).reshape(lead + (buckets * band_len,))
    turned = jnp.pad(turned, lead_pad + [(0, buckets)])
    diagonal = turned.reshape(lead + (buckets, band_len + 1))[..., :count]
    aligned = jnp.pad(jnp.swapaxes(diagonal, -1, -2), lead_pad + [(0, 0), (0, count)])
    sheared = aligned.reshape(lead + (count * (buckets + count),))[
        ..., : count * (buckets + count - 1)
    ]
    sheared = sheared.reshape(lead + (count, buckets + count - 1))
    spread = jnp.pad(sheared, lead_pad + [(0, 0), (full_len, full_len)])
    band = lax.dynamic_slice_in_dim(spread, full_len + span - offset, full_len, axis=len(lead) + 1)
    distance = (
        jnp.arange(full_len, dtype=jnp.int32)[None, :]
        - (offset + jnp.arange(count, dtype=jnp.int32))[:, None]
    )
    return jnp.where(
        distance <= -span,
        end_vals[..., 0:1, :],
        jnp.where(distance >= span - 1, end_vals[..., 1:2, :], band),
    )


def band_rows(all_rows, offset, count, span):
    padded = jnp.pad(all_rows, [(0, 0), (0, 0), (span, span), (0, 0)])
    return lax.dynamic_slice_in_dim(padded, offset, count + 2 * span - 1, axis=2)


def unband(values, offset, full_len, span):
    lead = values.shape[:2]
    room = jnp.zeros(lead + (full_len + 2 * span, values.shape[3]), jnp.float32)
    placed = lax.dynamic_update_slice_in_dim(room, values, offset, axis=2)
    return placed[:, :, span : span + full_len]


def relative_scores(own_rows, all_rows, own_table, all_table, offset, full_len):
    count = own_rows.shape[2]
    content = jnp.einsum("rgid,rgjd->rgij", own_rows, all_rows, preferred_element_type=jnp.float32)
    own_prod = jnp.einsum("rgid,gbd->rgib", own_rows, own_table, preferred_element_type=jnp.float32)
    window = band_rows(all_rows, offset, count, all_table.shape[1] // 2)
    cross = jnp.einsum("rgmd,gbd->rgmb", window, all_table, preferred_element_type=jnp.float32)
    end_vals = jnp.einsum(
        "rgjd,ged->rgej", all_rows, table_ends(all_table), preferred_element_type=jnp.float32
    )
    near_vals, near_pull = jax.vjp(lambda product: near_skew(product, offset, full_len), own_prod)
    far_vals, far_pull = jax.vjp(
        lambda part, ends: far_place(part, ends, offset, count, full_len), cross, end_vals
    )
    return (content + near_vals + far_vals, near_pull, far_pull, window)


def end_columns(grad):
    return jnp.stack([grad[..., 0], grad[..., -1]], axis=2)


def end_terms(ends, table):
    return jnp.einsum(
        "rgei,ged->rgid",
        ends,
        table_ends(table),
        precision=lax.Precision.HIGHEST,
        preferred_element_type=jnp.float32,
    )


def end_rows(ends, rows_low):
    return jnp.einsum(
        "rgei,rgid->ged",
        ends,
        rows_low,
        precision=lax.Precision.HIGHEST,
        preferred_element_type=jnp.float32,
    )


def with_ends(inner_part, edge_rows):
    buckets = inner_part.shape[1]
    place = jnp.arange(buckets, dtype=jnp.int32)[None, :, None]
    return (
        inner_part
        + jnp.where(place == 0, edge_rows[:, 0:1], 0.0)
        + jnp.where(place == buckets - 1, edge_rows[:, 1:2], 0.0)
    )


BLOCK = 128
MIB = 1024 * 1024
ATTEND_VMEM = 26 * MIB
BACK_VMEM = 26 * MIB
FEED_VMEM = 26 * MIB
COMM_VMEM = 16 * MIB


def dot_nn(a, b):
    return lax.dot_general(a, b, (((1,), (0,)), ((), ())), preferred_element_type=jnp.float32)


def dot_nt(a, b):
    return lax.dot_general(a, b, (((1,), (1,)), ((), ())), preferred_element_type=jnp.float32)


def dot_tn(a, b):
    return lax.dot_general(a, b, (((0,), (0,)), ((), ())), preferred_element_type=jnp.float32)


def turn_matrix(buckets):
    row = lax.broadcasted_iota(jnp.int32, (buckets, buckets), 0)
    col = lax.broadcasted_iota(jnp.int32, (buckets, buckets), 1)
    return (row + col == buckets - 1).astype(jnp.bfloat16)


def skew_band(product):
    count, buckets = product.shape
    row = lax.broadcasted_iota(jnp.int32, (count, BLOCK), 0)
    lane = lax.broadcasted_iota(jnp.int32, (count, BLOCK), 1)
    edge = jnp.where(row + lane <= BLOCK - 2, product[:, buckets - 1 :], product[:, 0:1])
    wide = jnp.concatenate([product, edge], axis=1)
    return pltpu.roll(wide, 1, 1, stride=1, stride_axis=0)


def skew_back(turned, buckets):
    return pltpu.roll(turned, turned.shape[1] - BLOCK, 1, stride=1, stride_axis=0)[:, :buckets]


def chip_columns(vec_ref, chip, index, core):
    width = 3 * DH // 2
    both = jnp.concatenate(
        [
            vec_ref[2 * chip, index : index + 1, :width].astype(jnp.float32),
            vec_ref[2 * chip + 1, index : index + 1, :width].astype(jnp.float32),
        ],
        axis=1,
    )
    return jnp.where(core == 0, both[:, : 2 * DH], both[:, DH:])


def attend_kernel(
    xs_ref,
    qkvs_ref,
    tables_ref,
    vecs_ref,
    q_ref,
    k_ref,
    v_ref,
    qrev_ref,
    krev_ref,
    p_ref,
    ctx_ref,
    w_ref,
    table_ref,
    segc_ref,
    place_ref,
    wide_ref,
    ends_ref,
    held_ref,
):
    at = Place()
    full_len = xs_ref.shape[0] * xs_ref.shape[1]
    buckets = table_ref.shape[0]
    blocks = full_len // BLOCK
    span = buckets // 2
    side = span // BLOCK
    band_width = buckets + BLOCK
    band_blocks = band_width // BLOCK
    group = 2 * DH
    scale = 1.0 / math.sqrt(3.0 * DH)
    units = p_ref.shape[0]
    shard_rows = qkvs_ref.shape[2]
    table_rows = tables_ref.shape[3]
    batches = tables_ref.shape[1]
    for part in range(at.tokens):
        pieces = []
        for i in range(3):
            piece = qkvs_ref[part, i]
            pieces.append(jnp.where(at.core == 0, piece[:, :group], piece[:, DH:]))
        w_ref[part * shard_rows : (part + 1) * shard_rows] = jnp.concatenate(pieces, axis=1)
        core, chip = part % 2, part // 2
        table_ref[part * table_rows : (part + 1) * table_rows] = jnp.concatenate(
            [tables_ref[core, row, chip] for row in range(batches)], axis=1
        )
        own_seg = vecs_ref[part, 9:10].astype(jnp.float32)
        segc_ref[part * BLOCK : (part + 1) * BLOCK] = jnp.broadcast_to(own_seg, (BLOCK, BLOCK)).T
    seg_row = jnp.concatenate(
        [vecs_ref[part, 9:10].astype(jnp.float32) for part in range(at.tokens)], axis=1
    )
    bias = jnp.concatenate(
        [chip_columns(vecs_ref, at.chip, i, at.core) for i in range(3)], axis=1
    )
    tokens_all = xs_ref[...].reshape(full_len, xs_ref.shape[2])
    proj = (dot_nn(tokens_all, w_ref[...]) + bias).astype(jnp.bfloat16)
    rel = (dot_nn(table_ref[...], w_ref[:, : 2 * group]) + bias[:, : 2 * group]).astype(
        jnp.bfloat16
    )
    rel = dot_nn(turn_matrix(buckets), rel).astype(jnp.bfloat16)
    for slot in range(2):
        lo, hi = slot * DH, (slot + 1) * DH
        q_ref[slot] = proj[:, lo:hi]
        k_ref[slot] = proj[:, group + lo : group + hi]
        v_ref[slot] = proj[:, 2 * group + lo : 2 * group + hi]
        qrev_ref[slot] = rel[:, lo:hi]
        krev_ref[slot] = rel[:, group + lo : group + hi]
    held_ref[...] = jnp.zeros_like(held_ref)
    for slot in range(2):
        ends_ref[slot, 0] = dot_nt(qrev_ref[slot, 0:16], k_ref[slot])
        ends_ref[slot, 1] = dot_nt(qrev_ref[slot, buckets - 16 : buckets], k_ref[slot])

        def key_block(kb, carry):
            rows = k_ref[slot, pl.ds(pl.multiple_of(kb * BLOCK, BLOCK), BLOCK)]
            band = skew_band(dot_nt(rows, qrev_ref[slot]))
            for e in range(band_blocks):
                place_ref[
                    slot,
                    kb + e,
                    :,
                    (band_blocks - 1 - e) * BLOCK : (band_blocks - e) * BLOCK,
                ] = band[:, e * BLOCK : (e + 1) * BLOCK].T
            return carry

        lax.fori_loop(0, blocks, key_block, 0, unroll=8)

    first = at.core * (blocks // 2)

    def unit(u, carry):
        g = u + first
        slot = g // blocks
        qb = g % blocks
        start = pl.multiple_of(qb * BLOCK, BLOCK)
        rows = q_ref[slot, pl.ds(start, BLOCK)]
        own = dot_nt(rows, krev_ref[slot])
        band = skew_band(own) + place_ref[slot, qb + side]
        wide_ref[u % 2, :, pl.ds(start, band_width)] = band
        content = dot_nt(rows, k_ref[slot])
        lane = lax.broadcasted_iota(jnp.int32, (BLOCK, full_len), 1)
        near = jnp.where(
            lane < start - span,
            own[:, 0:1] + ends_ref[slot, 1, 15:16],
            jnp.where(
                lane >= start + band_width - span,
                own[:, buckets - 1 :] + ends_ref[slot, 0, 0:1],
                wide_ref[u % 2, :, span : span + full_len],
            ),
        )
        same = segc_ref[pl.ds(start, BLOCK), 0:1] == seg_row
        scores = jnp.where(same, (content + near) * scale, masked_score)
        highest = jnp.max(scores, axis=-1, keepdims=True)
        exponent = jnp.exp(scores - highest)
        total = jnp.sum(exponent, axis=-1, keepdims=True)
        probs = (exponent / total).astype(jnp.bfloat16)
        p_ref[u] = probs
        held_ref[slot, pl.ds(start, BLOCK)] = dot_nn(probs, v_ref[slot]).astype(jnp.bfloat16)
        return carry

    lax.fori_loop(0, units, unit, 0, unroll=4)
    for part in range(at.tokens):
        rows = slice(part * BLOCK, (part + 1) * BLOCK)
        ctx_ref[part] = jnp.concatenate([held_ref[0, rows], held_ref[1, rows]], axis=1)


def attend(xs, qkvs, tables, vecs):
    tokens, local_len, width = xs.shape
    full_len = tokens * local_len
    buckets = tokens * tables.shape[3]
    blocks = full_len // BLOCK
    units = 3 * blocks // 2
    band_width = buckets + BLOCK
    low, wide = jnp.bfloat16, jnp.float32
    pad_blocks = blocks + band_width // BLOCK - 1
    return pl.pallas_call(
        attend_kernel,
        out_shape=(
            jax.ShapeDtypeStruct((2, full_len, DH), low),
            jax.ShapeDtypeStruct((2, full_len, DH), low),
            jax.ShapeDtypeStruct((2, full_len, DH), low),
            jax.ShapeDtypeStruct((2, buckets, DH), low),
            jax.ShapeDtypeStruct((2, buckets, DH), low),
            jax.ShapeDtypeStruct((units, BLOCK, full_len), low),
            jax.ShapeDtypeStruct((tokens, local_len, 2 * DH), low),
            jax.ShapeDtypeStruct((width, 6 * DH), low),
            jax.ShapeDtypeStruct((buckets, width), low),
        ),
        in_specs=[pl.BlockSpec(memory_space=pltpu.VMEM)] * 4,
        out_specs=[pl.BlockSpec(memory_space=pltpu.VMEM)] * 9,
        scratch_shapes=[
            pltpu.VMEM((full_len, BLOCK), wide),
            pltpu.VMEM((2, pad_blocks, BLOCK, band_width), wide),
            pltpu.VMEM((2, BLOCK, full_len + buckets), wide),
            pltpu.VMEM((2, 2, 16, full_len), wide),
            pltpu.VMEM((2, full_len, DH), low),
        ],
        compiler_params=pltpu.CompilerParams(vmem_limit_bytes=ATTEND_VMEM),
        name="attend",
    )(xs, qkvs, tables, vecs)


def attend_back_kernel(
    q_ref,
    k_ref,
    v_ref,
    qrev_ref,
    krev_ref,
    p_ref,
    mix_ref,
    attn_ref,
    dcat_ref,
    rel_ref,
    sum_ref,
    heads_ref,
    wide_ref,
    low_ref,
    place_ref,
    dq_ref,
    dkt_ref,
    dvt_ref,
    far_ref,
    dkr_ref,
    dqr_ref,
):
    full_len = q_ref.shape[1]
    buckets = qrev_ref.shape[1]
    blocks = full_len // BLOCK
    span = buckets // 2
    side = span // BLOCK
    band_width = buckets + BLOCK
    band_blocks = band_width // BLOCK
    scale = 1.0 / math.sqrt(3.0 * DH)
    units = p_ref.shape[0]
    for ref in (wide_ref, low_ref, place_ref, dq_ref, dkt_ref, dvt_ref, far_ref, dkr_ref, dqr_ref):
        ref[...] = jnp.zeros_like(ref)
    at = Place()
    group = 2 * DH
    first_row = pl.multiple_of((3 * at.chip + at.core) * DH, DH)
    mix_rows = mix_ref[pl.ds(first_row, group)]
    dctx = dot_nt(attn_ref[...].reshape(full_len, attn_ref.shape[2]), mix_rows)
    for slot in range(2):
        heads_ref[slot] = dctx[:, slot * DH : (slot + 1) * DH].astype(jnp.bfloat16)
    first = at.core * (blocks // 2)
    turn = turn_matrix(BLOCK)
    place8 = lax.broadcasted_iota(jnp.int32, (8, full_len), 0)

    def unit(u, carry):
        g = u + first
        slot = g // blocks
        qb = g % blocks
        start = pl.multiple_of(qb * BLOCK, BLOCK)
        rows = q_ref[slot, pl.ds(start, BLOCK)]
        grad = heads_ref[slot, pl.ds(start, BLOCK)]
        probs = p_ref[u]
        wide_probs = probs.astype(jnp.float32)
        prob_grad = dot_nt(grad, v_ref[slot])
        inner = jnp.sum(wide_probs * prob_grad, axis=-1, keepdims=True)
        low_grad = (wide_probs * (prob_grad - inner)).astype(jnp.bfloat16)
        score_grad = low_grad.astype(jnp.float32)
        wide_ref[u % 2, :, span : span + full_len] = dot_nn(turn, low_grad)
        low_ref[u % 2, :, span : span + full_len] = low_grad
        dvt_ref[slot] += dot_tn(grad, probs)
        dkt_ref[slot] += dot_tn(rows, low_grad)
        row = lax.broadcasted_iota(jnp.int32, (BLOCK, full_len), 0)
        lane = lax.broadcasted_iota(jnp.int32, (BLOCK, full_len), 1)
        gap = lane - row - start
        right = jnp.where(gap > span, score_grad, 0.0)
        left = jnp.where(gap < 1 - span, score_grad, 0.0)
        end_right = jnp.sum(right, axis=-1, keepdims=True)
        end_left = jnp.sum(left, axis=-1, keepdims=True)
        far_right = jnp.sum(jnp.where(gap >= span, score_grad, 0.0), axis=0, keepdims=True)
        far_left = jnp.sum(jnp.where(gap < -span, score_grad, 0.0), axis=0, keepdims=True)
        far_ref[slot] += jnp.where(place8 == 0, far_right, jnp.where(place8 == 1, far_left, 0.0))
        band = wide_ref[u % 2, :, pl.ds(start, band_width)]
        near = dot_nn(turn, skew_back(band, buckets).astype(jnp.bfloat16))
        bucket = lax.broadcasted_iota(jnp.int32, (BLOCK, buckets), 1)
        near = near + jnp.where(
            bucket == 0, end_left, jnp.where(bucket == buckets - 1, end_right, 0.0)
        )
        near_low = near.astype(jnp.bfloat16)
        dq = dot_nn(low_grad, k_ref[slot]) + dot_nn(near_low, krev_ref[slot])
        dq_ref[slot, pl.ds(start, BLOCK)] = dq
        dkr_ref[slot] += dot_tn(rows, near_low)
        for e in range(band_blocks):
            keys_at = pl.multiple_of(start + e * BLOCK, BLOCK)
            place_ref[
                slot, qb + e, :, (band_blocks - 1 - e) * BLOCK : (band_blocks - e) * BLOCK
            ] = dot_nt(turn, low_ref[u % 2, :, pl.ds(keys_at, BLOCK)])
        return carry

    lax.fori_loop(0, units, unit, 0, unroll=4)
    parts_q, parts_k, parts_v = [], [], []
    parts_r = [None] * 4
    for slot in range(2):
        far_low = far_ref[slot].astype(jnp.bfloat16)
        mark = lax.broadcasted_iota(jnp.int32, (8, DH), 0)
        ends = jnp.where(
            mark == 0,
            qrev_ref[slot, 0:1].astype(jnp.float32),
            jnp.where(mark == 1, qrev_ref[slot, buckets - 1 : buckets].astype(jnp.float32), 0.0),
        ).astype(jnp.bfloat16)
        end_keys = dot_tn(ends, far_low)
        end_rows = dot_nn(far_low, k_ref[slot])

        whole_k = (dkt_ref[slot] + end_keys).T

        def key_side(kb, carry):
            start = pl.multiple_of(kb * BLOCK, BLOCK)
            far = skew_back(place_ref[slot, kb + side], buckets).astype(jnp.bfloat16)
            far = dot_nn(turn, far).astype(jnp.bfloat16)
            keys = k_ref[slot, pl.ds(start, BLOCK)]
            dqr_ref[slot] += dot_tn(keys, far)
            dq_ref[2 + slot, pl.ds(start, BLOCK)] = dot_nn(far, qrev_ref[slot])
            return carry

        lax.fori_loop(0, blocks, key_side, 0, unroll=8)
        parts_q.append((dq_ref[slot] * scale).astype(jnp.bfloat16))
        parts_k.append(((dq_ref[2 + slot] + whole_k) * scale).astype(jnp.bfloat16))
        parts_v.append(dvt_ref[slot].T.astype(jnp.bfloat16))
        bucket = lax.broadcasted_iota(jnp.int32, (buckets, DH), 0)
        qr = dqr_ref[slot].T + jnp.where(
            bucket == 0, end_rows[0:1], jnp.where(bucket == buckets - 1, end_rows[1:2], 0.0)
        )
        dqr_out = qr * scale
        dkr_out = dkr_ref[slot].T * scale
        parts_r[slot] = dqr_out
        parts_r[2 + slot] = dkr_out
    dcat = jnp.concatenate(parts_q + parts_k + parts_v, axis=1)
    dcat_ref[...] = dcat
    rel = jnp.concatenate(parts_r, axis=1)
    rel_ref[...] = dot_nn(turn_matrix(buckets), rel.astype(jnp.bfloat16)).astype(jnp.bfloat16)
    rel_sum = jnp.sum(rel, axis=0, keepdims=True)
    rel_sum = jnp.concatenate([rel_sum, jnp.zeros((1, 2 * DH), jnp.float32)], axis=1)
    sums = jnp.sum(dcat.astype(jnp.float32), axis=0, keepdims=True) + rel_sum
    sum_ref[...] = jnp.broadcast_to(sums, sum_ref.shape)


def attend_back(q, k, v, qrev, krev, probs, m_mix, attn_all):
    full_len = q.shape[1]
    buckets = qrev.shape[1]
    blocks = full_len // BLOCK
    band_width = buckets + BLOCK
    low, wide = jnp.bfloat16, jnp.float32
    pad_blocks = blocks + band_width // BLOCK - 1
    return pl.pallas_call(
        attend_back_kernel,
        out_shape=(
            jax.ShapeDtypeStruct((full_len, 6 * DH), low),
            jax.ShapeDtypeStruct((buckets, 4 * DH), low),
            jax.ShapeDtypeStruct((8, 6 * DH), wide),
        ),
        in_specs=[pl.BlockSpec(memory_space=pltpu.VMEM)] * 8,
        out_specs=[pl.BlockSpec(memory_space=pltpu.VMEM)] * 3,
        scratch_shapes=[
            pltpu.VMEM((2, full_len, DH), low),
            pltpu.VMEM((2, BLOCK, full_len + buckets), wide),
            pltpu.VMEM((2, BLOCK, full_len + buckets), low),
            pltpu.VMEM((2, pad_blocks, BLOCK, band_width), wide),
            pltpu.VMEM((4, full_len, DH), wide),
            pltpu.VMEM((2, DH, full_len), wide),
            pltpu.VMEM((2, DH, full_len), wide),
            pltpu.VMEM((2, 8, full_len), wide),
            pltpu.VMEM((2, DH, buckets), wide),
            pltpu.VMEM((2, DH, buckets), wide),
        ],
        compiler_params=pltpu.CompilerParams(vmem_limit_bytes=BACK_VMEM),
        name="attend_back",
    )(q, k, v, qrev, krev, probs, m_mix, attn_all)


MESH = pl.DeviceIdType.MESH
VMEM_SPEC = pl.BlockSpec(memory_space=pltpu.VMEM)
HBM_SPEC = pl.BlockSpec(memory_space=pltpu.HBM)
CHUNKS = 4


class Place:
    def __init__(self):
        self.batches = lax.axis_size("batch")
        self.tokens = lax.axis_size("seq")
        self.chips = self.tokens // 2
        self.row = lax.axis_index("batch")
        self.part = lax.axis_index("seq")
        self.chip = self.part // 2
        self.core = self.part % 2

    def along_chips(self, k):
        chip = lax.rem(self.chip + k, self.chips)
        return chip, (self.row, 2 * chip + self.core)

    def from_chips(self, k):
        return lax.rem(self.chip + self.chips - k, self.chips)

    def partner(self):
        return (self.row, self.part + 1 - 2 * self.core)

    def along_rows(self, k):
        row = lax.rem(self.row + k, self.batches)
        return row, (row, self.part)

    def from_rows(self, k):
        return lax.rem(self.row + self.batches - k, self.batches)

    def along_seq(self, k):
        part = lax.rem(self.part + k, self.tokens)
        return part, (self.row, part)

    def along_plane(self, k):
        index = lax.rem(2 * self.row + self.core + k, 2 * self.batches)
        row, core = index // 2, index % 2
        return row, core, (row, 2 * self.chip + core)

    def chip_peers(self):
        return [self.along_chips(k)[1] for k in range(1, self.chips)]

    def row_peers(self):
        return [self.along_rows(k)[1] for k in range(1, self.batches)]

    def cross_peers(self):
        other = self.part + 1 - 2 * self.core
        return [(self.along_rows(k)[0], other) for k in range(1, self.batches)]

    def cross_row_peers(self):
        return self.row_peers() + self.cross_peers()

    def all_peers(self):
        peers = []
        for i in range(self.batches):
            row = lax.rem(self.row + i, self.batches)
            for j in range(self.tokens):
                if i or j:
                    peers.append((row, lax.rem(self.part + j, self.tokens)))
        return peers

    def seq_peers(self):
        return [self.along_seq(k)[1] for k in range(1, self.tokens)]

    def plane_peers(self):
        return [self.along_plane(k)[2] for k in range(1, 2 * self.batches)]


def meet(peers):
    barrier = pltpu.get_barrier_semaphore()
    for peer in peers:
        pl.semaphore_signal(barrier, inc=1, device_id=peer, device_id_type=MESH)
    pl.semaphore_wait(barrier, len(peers))


class Wires:
    def __init__(self, send_sems, recv_sems, local_sems):
        self.sems = (send_sems, recv_sems, local_sems)
        self.used = [0, 0]
        self.ends = []

    def send(self, src, dst, peer):
        k = self.used[0]
        self.used[0] += 1
        copy = pltpu.make_async_remote_copy(
            src_ref=src,
            dst_ref=dst,
            send_sem=self.sems[0].at[k],
            recv_sem=self.sems[1].at[k],
            device_id=peer,
            device_id_type=MESH,
        )
        copy.start()
        self.ends.append(copy.wait_send)
        return copy

    def local(self, src, dst):
        k = self.used[1]
        self.used[1] += 1
        copy = pltpu.make_async_copy(src, dst, self.sems[2].at[k])
        copy.start()
        return copy

    def finish(self):
        for end in self.ends:
            end()


def wire_scratch(sends, locals_count):
    return [
        pltpu.SemaphoreType.DMA((sends,)),
        pltpu.SemaphoreType.DMA((sends,)),
        pltpu.SemaphoreType.DMA((locals_count,)),
    ]


def comm_call(kernel, name, ident, out_shapes, inputs, sends, locals_count, scratch=(), spec=VMEM_SPEC):
    return pl.pallas_call(
        kernel,
        out_shape=tuple(out_shapes),
        in_specs=[spec] * len(inputs),
        out_specs=tuple([VMEM_SPEC] * len(out_shapes)),
        scratch_shapes=list(scratch) + wire_scratch(sends, locals_count),
        compiler_params=pltpu.CompilerParams(
            collective_id=ident, has_side_effects=True, vmem_limit_bytes=COMM_VMEM
        ),
        name=name,
    )(*inputs)


def like(array, *lead):
    return jax.ShapeDtypeStruct(tuple(lead) + tuple(array.shape), array.dtype)


def pick(values, index):
    out = jnp.int32(values[0])
    for i in range(1, len(values)):
        out = jnp.where(index == i, jnp.int32(values[i]), out)
    return out


def arrival_order(at):
    chips = range(at.chips)
    lists = [sorted((j for j in chips if j != z), key=lambda j: (abs(j - z), j)) for z in chips]
    return [pick([lists[z][t] for z in chips], at.chip) for t in range(at.chips - 1)]


def return_order(at):
    chips = range(at.chips)

    def away(j, z):
        end = at.chips - 1 if j < z else 0
        return (abs(j - end) + abs(end - z), j)

    lists = [sorted((j for j in chips if j != z), key=lambda j: away(j, z)) for z in chips]
    return [pick([lists[z][t] for z in chips], at.chip) for t in range(at.chips - 1)]


def far_order(at):
    chips = range(at.chips)
    lists = [sorted((j for j in chips if j != z), key=lambda j: (-abs(j - z), j)) for z in chips]
    return [pick([lists[z][t] for z in chips], at.chip) for t in range(at.chips - 1)]


def goes_on(at, j):
    above = jnp.logical_and(j < at.chip, at.chip < at.chips - 1)
    below = jnp.logical_and(j > at.chip, at.chip > 0)
    return jnp.logical_or(above, below)


def line_peer(at, step):
    return (at.row, 2 * (at.chip + step) + at.core)


class LineGather:
    def __init__(self, at, buf, slot, sems, own=None):
        self.at, self.buf, self.slot, self.own = at, buf, slot, own
        self.send_sems, self.recv_sems = sems
        self.rows = buf.shape[1] // CHUNKS

    def copy(self, j, h, step, k, own=False):
        window = pl.ds(h * self.rows, self.rows)
        home = self.buf.at[self.slot(j), window]
        src = self.own.at[window] if own and self.own is not None else home
        return pltpu.make_async_remote_copy(
            src_ref=src,
            dst_ref=home,
            send_sem=self.send_sems.at[k * CHUNKS + h],
            recv_sem=self.recv_sems.at[j * CHUNKS + h],
            device_id=line_peer(self.at, step),
            device_id_type=MESH,
        )

    def own_each(self, act):
        z, n = self.at.chip, self.at.chips
        for h in range(CHUNKS):

            @pl.when(z < n - 1)
            def _():
                act(self.copy(z, h, 1, z, own=True))

            @pl.when(z > 0)
            def _():
                act(self.copy(z, h, -1, n, own=True))

    def start(self):
        self.own_each(lambda copy: copy.start())

    def arrive(self, j):
        step = jnp.where(j < self.at.chip, 1, -1)
        for h in range(CHUNKS):
            self.copy(j, h, -step, j).wait_recv()

            @pl.when(goes_on(self.at, j))
            def _():
                self.copy(j, h, step, j).start()

    def drain(self, order):
        self.own_each(lambda copy: copy.wait_send())
        for j in order:
            step = jnp.where(j < self.at.chip, 1, -1)

            @pl.when(goes_on(self.at, j))
            def _():
                for h in range(CHUNKS):
                    self.copy(j, h, step, j).wait_send()


class LineReduce:
    def __init__(self, at, part, got, sems):
        self.at, self.part, self.got = at, part, got
        self.send_sems, self.recv_sems = sems
        self.rows = part.shape[1] // CHUNKS

    def copy(self, j, h):
        z, n = self.at.chip, self.at.chips
        window = pl.ds(h * self.rows, self.rows)
        slot = jnp.where(z + 1 == j, n, j)
        return pltpu.make_async_remote_copy(
            src_ref=self.part.at[j, window],
            dst_ref=self.got.at[slot, window],
            send_sem=self.send_sems.at[j * CHUNKS + h],
            recv_sem=self.recv_sems.at[slot * CHUNKS + h],
            device_id=line_peer(self.at, jnp.where(j < z, -1, 1)),
            device_id_type=MESH,
        )

    def landed(self, slot, h, step):
        window = pl.ds(h * self.rows, self.rows)
        return pltpu.make_async_remote_copy(
            src_ref=self.got.at[slot, window],
            dst_ref=self.got.at[slot, window],
            send_sem=self.send_sems.at[h],
            recv_sem=self.recv_sems.at[slot * CHUNKS + h],
            device_id=line_peer(self.at, step),
            device_id_type=MESH,
        )

    def send(self, j):
        for h in range(CHUNKS):
            self.copy(j, h).start()

    def send_last(self, j):
        @pl.when(jnp.logical_not(goes_on(self.at, j)))
        def _():
            self.send(j)

    def pass_on(self, order):
        z, n = self.at.chip, self.at.chips
        wide = jnp.float32

        @pl.when(jnp.logical_and(z > 0, z < n - 1))
        def _():
            for j in order:
                step = jnp.where(j < z, 1, -1)
                for h in range(CHUNKS):
                    self.landed(j, h, step).wait_recv()
                    window = pl.ds(h * self.rows, self.rows)
                    total = self.part[j, window].astype(wide) + self.got[j, window].astype(wide)
                    self.part[j, window] = total.astype(self.part.dtype)
                    self.copy(j, h).start()

    def clear(self):
        z, n = self.at.chip, self.at.chips

        @pl.when(z == n - 1)
        def _():
            self.got[z] = jnp.zeros(self.got.shape[1:], self.got.dtype)

        @pl.when(z == 0)
        def _():
            self.got[n] = jnp.zeros(self.got.shape[1:], self.got.dtype)

    def collect(self):
        z, n = self.at.chip, self.at.chips
        for h in range(CHUNKS):

            @pl.when(z < n - 1)
            def _():
                self.landed(z, h, 1).wait_recv()

            @pl.when(z > 0)
            def _():
                self.landed(n, h, -1).wait_recv()

        return self.got[z].astype(jnp.float32) + self.got[n].astype(jnp.float32)

    def drain(self, order):
        for j in order:
            for h in range(CHUNKS):
                self.copy(j, h).wait_send()


def gather_sems(chips):
    return [
        pltpu.SemaphoreType.DMA(((chips + 1) * CHUNKS,)),
        pltpu.SemaphoreType.DMA((chips * CHUNKS,)),
    ]


def reduce_sems(chips):
    return [
        pltpu.SemaphoreType.DMA((chips * CHUNKS,)),
        pltpu.SemaphoreType.DMA(((chips + 1) * CHUNKS,)),
    ]


def gather_kernel(
    x_ref, wq_ref, wk_ref, wv_ref, mix_ref, table_ref, vec_ref, up_ref, down_ref,
    xs_ref, qkvs_ref, mixs_ref, tables_ref, vecs_ref, up2_ref, down2_ref,
    line_send, line_recv, *sems,
):
    at = Place()
    wires = Wires(*sems)
    b, s, z, c = at.row, at.part, at.chip, at.core
    off_diagonal = b != z
    turned = (z, 2 * b + c)
    peers = at.seq_peers() + at.row_peers()
    barrier = pltpu.get_barrier_semaphore()
    for peer in peers:
        pl.semaphore_signal(barrier, inc=1, device_id=peer, device_id_type=MESH)

    @pl.when(off_diagonal)
    def _():
        pl.semaphore_signal(barrier, inc=1, device_id=turned, device_id_type=MESH)

    pl.semaphore_wait(barrier, len(peers) + off_diagonal.astype(jnp.int32))

    swaps, stays = [], []
    for i, ref in enumerate((wq_ref, wk_ref, wv_ref)):
        k = wires.used[0]
        wires.used[0] += 1
        swaps.append(
            pltpu.make_async_remote_copy(
                src_ref=ref,
                dst_ref=qkvs_ref.at[2 * z + c, i],
                send_sem=sems[0].at[k],
                recv_sem=sems[1].at[k],
                device_id=turned,
                device_id_type=MESH,
            )
        )
        stays.append(pltpu.make_async_copy(ref, qkvs_ref.at[2 * b + c, i], sems[2].at[i]))
        wires.used[1] += 1

    @pl.when(off_diagonal)
    def _():
        for swap in swaps:
            swap.start()

    @pl.when(jnp.logical_not(off_diagonal))
    def _():
        for stay in stays:
            stay.start()

    table_home = tables_ref.at[c, b, z]
    mix_home = mixs_ref.at[c, b, z]
    table_sends = [
        wires.send(table_ref, table_home, at.along_chips(k)[1]) for k in range(1, at.chips)
    ]
    kept = [wires.local(table_ref, table_home), wires.local(mix_ref, mix_home)]
    line = LineGather(at, xs_ref, lambda j: 2 * j + c, (line_send, line_recv), own=x_ref)
    line.start()
    last = [wires.send(vec_ref, vecs_ref.at[s], at.along_seq(k)[1]) for k in range(1, at.tokens)]
    mix_sends = [
        wires.send(mix_ref, mix_home, at.along_chips(k)[1]) for k in range(1, at.chips)
    ]
    last += [
        wires.send(x_ref, xs_ref.at[s], at.partner()),
        wires.send(up_ref, up2_ref, at.partner()),
        wires.send(down_ref, down2_ref, at.partner()),
    ]
    own = [
        wires.local(x_ref, xs_ref.at[s]),
        wires.local(vec_ref, vecs_ref.at[s]),
    ]

    @pl.when(off_diagonal)
    def _():
        for swap in swaps:
            swap.wait_recv()

    @pl.when(jnp.logical_not(off_diagonal))
    def _():
        for stay in stays:
            stay.wait()

    mine = qkvs_ref.at[2 * b + c]
    qkv_sends = [wires.send(mine, mine, at.along_rows(k)[1]) for k in range(1, at.batches)]
    last.append(wires.send(mine, mine, at.partner()))
    for copy in table_sends:
        copy.wait_recv()
    for copy in kept:
        copy.wait()
    mine = tables_ref.at[c, b]
    row_sends = [wires.send(mine, mine, at.along_rows(k)[1]) for k in range(1, at.batches)]
    last.append(wires.send(mine, mine, at.partner()))
    order = arrival_order(at)

    def arrived(j):
        line.arrive(j)
        home = xs_ref.at[2 * j + c]
        last.append(wires.send(home, home, at.partner()))

    arrived(order[0])
    for copy in mix_sends:
        copy.wait_recv()
    mine = mixs_ref.at[c, b]
    mix_rows = [wires.send(mine, mine, at.along_rows(k)[1]) for k in range(1, at.batches)]
    last.append(wires.send(mine, mine, at.partner()))
    arrived(order[1])
    for k in range(1, at.batches):
        qkv_sends[k - 1].wait_recv()
        home = qkvs_ref.at[2 * at.from_rows(k) + c]
        last.append(wires.send(home, home, at.partner()))
    for k in range(1, at.batches):
        row_sends[k - 1].wait_recv()
        home = tables_ref.at[c, at.from_rows(k)]
        last.append(wires.send(home, home, at.partner()))
    for j in order[2:]:
        arrived(j)
    for k in range(1, at.batches):
        mix_rows[k - 1].wait_recv()
        home = mixs_ref.at[c, at.from_rows(k)]
        last.append(wires.send(home, home, at.partner()))
    for copy in last:
        copy.wait_recv()
    for copy in own:
        copy.wait()
    wires.finish()
    line.drain(order)

    @pl.when(off_diagonal)
    def _():
        for swap in swaps:
            swap.wait_send()


def gather_inputs(x, w_query, w_key, w_value, w_mix, rel_table, vec, up, down):
    tokens, batches = lax.axis_size("seq"), lax.axis_size("batch")
    chips = tokens // 2
    outs = (
        like(x, tokens),
        like(w_query, tokens, 3),
        like(w_mix, 2, batches, chips),
        like(rel_table, 2, batches, chips),
        like(vec, tokens),
        like(up),
        like(down),
    )
    sends = 3 + 2 * (chips - 1) + tokens - 1 + 3 + 6 * (batches - 1) + 3 + chips - 1
    inputs = (x, w_query, w_key, w_value, w_mix, rel_table, vec, up, down)
    return comm_call(
        gather_kernel,
        "gather_inputs",
        0,
        outs,
        inputs,
        sends,
        7,
        scratch=gather_sems(chips),
        spec=HBM_SPEC,
    )


def norm_parts(values):
    average = jnp.mean(values, axis=-1, keepdims=True)
    centered = values - average
    variance = jnp.mean(centered * centered, axis=-1, keepdims=True)
    scale = lax.rsqrt(variance + norm_eps)
    return centered * scale, scale


def norm_back(grad, gain, unit, scale):
    inner = grad * gain
    mean = jnp.mean(inner, axis=-1, keepdims=True)
    slope = jnp.mean(inner * unit, axis=-1, keepdims=True)
    return scale * (inner - mean - unit * slope)


def line_pass(gather, reduce, order, work):
    def finish(j):
        work(j)
        reduce.send_last(j)

    for j in order:
        gather.arrive(j)
        finish(j)


def feed_kernel(
    ctx_ref, x_ref, mixs_ref, vecs_ref, up_ref, down_ref, up2_ref, down2_ref, out_grad_ref,
    output_ref, pre_grad_ref, sums_ref, attn_ref, mix_ref, ups_ref, downs_ref, upbs_ref,
    got_ref, hid_ref, act_ref, slope_ref, part_ref, ffn_ref, grad_ref, inner_ref,
    back_ref, backs_ref, up_away_ref, down_away_ref, upb_away_ref,
    up_got_ref, down_got_ref, upb_got_ref, upg_ref, downg_ref, upb_ref, vec_ref,
    hid_send, hid_recv, ffn_send, ffn_recv, grad_send, grad_recv, back_send, back_recv,
    attn_send, attn_recv, *sems,
):
    at = Place()
    wires = Wires(*sems)
    low, wide = jnp.bfloat16, jnp.float32
    b, s, z, c = at.row, at.part, at.chip, at.core
    order, returns = arrival_order(at), return_order(at)
    meet(at.seq_peers() + at.row_peers())
    last, own = [], []
    swaps = []
    for k in range(1, at.tokens):
        part, peer = at.along_seq(k)
        swaps.append(wires.send(ctx_ref.at[part], got_ref.at[s], peer))
    kept = wires.local(ctx_ref.at[s], got_ref.at[s])
    lanes = x_ref.shape[1] // at.tokens
    hidden_here = up_ref.shape[1]
    vec_ref[...] = jnp.concatenate(
        [vecs_ref[part, :, :lanes].astype(wide) for part in range(at.tokens)], axis=1
    )
    bias3 = vec_ref[3:4]
    gain1, gain2 = vec_ref[4:5], vec_ref[5:6]
    shift1, shift2 = vec_ref[6:7], vec_ref[7:8]
    bias_down = vec_ref[8:9]
    partner = s + 1 - 2 * c
    up_rows = hidden_here // BLOCK
    bias_up = jnp.concatenate(
        [vecs_ref[s, 10 + i : 11 + i].astype(wide) for i in range(up_rows)]
        + [vecs_ref[partner, 10 + i : 11 + i].astype(wide) for i in range(up_rows)],
        axis=1,
    )
    shard_rows = mixs_ref.shape[3]
    for part in range(at.tokens):
        mix_ref[part * shard_rows : (part + 1) * shard_rows] = jnp.concatenate(
            [mixs_ref[part % 2, row, part // 2] for row in range(at.batches)], axis=1
        )
    for copy in swaps:
        copy.wait_recv()
    kept.wait()
    pieces = []
    for chip in range(at.chips):
        left, right = got_ref[2 * chip], got_ref[2 * chip + 1]
        middle = left[:, DH:].astype(wide) + right[:, :DH].astype(wide)
        pieces += [left[:, :DH], middle.astype(low), right[:, DH:]]
    context = jnp.concatenate(pieces, axis=1)
    pre_norm = x_ref[...].astype(wide) + dot_nn(context, mix_ref[...]) + bias3
    unit1, scale1 = norm_parts(pre_norm)
    hidden = unit1 * gain1 + shift1
    hid_ref[z] = hidden.astype(low)
    hid_line = LineGather(at, hid_ref, lambda j: j, (hid_send, hid_recv))
    ffn_line = LineReduce(at, part_ref, ffn_ref, (ffn_send, ffn_recv))
    hid_line.start()
    ffn_line.clear()

    def ffn(chip):
        rows = hid_ref[chip]
        inner = jnp.concatenate(
            [dot_nn(rows, up_ref[...]), dot_nn(rows, up2_ref[...])], axis=1
        )
        inner = inner + bias_up
        cdf = 0.5 * (1.0 + lax.erf(inner * math.sqrt(0.5)))
        act = (inner * cdf).astype(low)
        slope_ref[chip] = cdf + inner * (
            jnp.exp(-0.5 * inner * inner) * (1.0 / math.sqrt(2.0 * math.pi))
        )
        act_ref[chip] = act
        part_ref[chip] = (
            dot_nn(act[:, :hidden_here], down_ref[...])
            + dot_nn(act[:, hidden_here:], down2_ref[...])
        ).astype(low)

    ffn(z)
    line_pass(hid_line, ffn_line, order, ffn)
    ffn_line.pass_on(returns)
    total = part_ref[z].astype(wide) + ffn_line.collect()
    mixed = hidden + total + bias_down
    unit2, scale2 = norm_parts(mixed)
    output_ref[...] = (unit2 * gain2 + shift2).astype(low)
    out_grad = out_grad_ref[...].astype(wide)
    mixed_grad = norm_back(out_grad, gain2, unit2, scale2)
    grad_ref[z] = mixed_grad.astype(low)
    grad_line = LineGather(at, grad_ref, lambda j: j, (grad_send, grad_recv))
    back_line = LineReduce(at, back_ref, backs_ref, (back_send, back_recv))
    grad_line.start()
    back_line.clear()
    gain2_grad = jnp.sum(out_grad * unit2, axis=0, keepdims=True)
    shift2_grad = jnp.sum(out_grad, axis=0, keepdims=True)
    downb_grad = jnp.sum(mixed_grad, axis=0, keepdims=True)

    def back(chip):
        rows = grad_ref[chip]
        act_grad = jnp.concatenate(
            [dot_nt(rows, down_ref[...]), dot_nt(rows, down2_ref[...])], axis=1
        )
        inner_low = (act_grad * slope_ref[chip]).astype(low)
        inner_ref[chip] = inner_low
        back_ref[chip] = (
            dot_nt(inner_low[:, :hidden_here], up_ref[...])
            + dot_nt(inner_low[:, hidden_here:], up2_ref[...])
        ).astype(low)

    back(z)
    line_pass(grad_line, back_line, order, back)
    width = x_ref.shape[1]
    columns = width // at.batches
    inner_all = inner_ref[...].reshape(at.chips * BLOCK, 2 * hidden_here)
    act_all = act_ref[...].reshape(at.chips * BLOCK, 2 * hidden_here)
    hid_all = hid_ref[...].reshape(at.chips * BLOCK, width)
    grad_all = grad_ref[...].reshape(at.chips * BLOCK, width)
    near, away = slice(0, hidden_here), slice(hidden_here, 2 * hidden_here)
    up_grad = dot_tn(hid_all, inner_all)
    up_away_ref[...] = up_grad[:, away].astype(low)
    down_grad = dot_tn(grad_all, act_all)
    down_away_ref[...] = down_grad[:, away].astype(low)
    upb_grad = jnp.sum(inner_all.astype(wide), axis=0, keepdims=True)
    upb_away_ref[...] = jnp.broadcast_to(upb_grad[:, away], upb_away_ref.shape)
    halves = [
        wires.send(up_away_ref, up_got_ref, at.partner()),
        wires.send(down_away_ref, down_got_ref, at.partner()),
        wires.send(upb_away_ref, upb_got_ref, at.partner()),
    ]
    back_line.pass_on(returns)
    for copy in halves:
        copy.wait_recv()
    upb_ref[...] = jnp.broadcast_to(upb_grad[:, near], upb_ref.shape) + upb_got_ref[...]
    up_sum = (up_grad[:, near] + up_got_ref[...].astype(wide)).astype(low)
    down_sum = (down_grad[:, near] + down_got_ref[...].astype(wide)).astype(low)
    for row in range(at.batches):
        upg_ref[row] = up_sum[row * columns : (row + 1) * columns]
        downg_ref[row] = down_sum[row * columns : (row + 1) * columns]
    for k in range(1, at.batches):
        row, peer = at.along_rows(k)
        last.append(wires.send(upg_ref.at[row], ups_ref.at[b], peer))
        last.append(wires.send(downg_ref.at[row], downs_ref.at[b], peer))
        last.append(wires.send(upb_ref, upbs_ref.at[b], peer))
    own.append(wires.local(upg_ref.at[b], ups_ref.at[b]))
    own.append(wires.local(downg_ref.at[b], downs_ref.at[b]))
    own.append(wires.local(upb_ref, upbs_ref.at[b]))
    total = back_ref[z].astype(wide) + back_line.collect()
    hidden_grad = mixed_grad + total
    pre_grad = norm_back(hidden_grad, gain1, unit1, scale1)
    attn_ref[s] = pre_grad.astype(low)
    attn_line = LineGather(at, attn_ref, lambda j: 2 * j + c, (attn_send, attn_recv))
    attn_line.start()
    last.append(wires.send(attn_ref.at[s], attn_ref.at[s], at.partner()))
    pre_grad_ref[...] = pre_grad
    gain1_grad = jnp.sum(hidden_grad * unit1, axis=0, keepdims=True)
    shift1_grad = jnp.sum(hidden_grad, axis=0, keepdims=True)
    bias3_grad = jnp.sum(pre_grad, axis=0, keepdims=True)
    sums = jnp.concatenate(
        [bias3_grad, gain1_grad, gain2_grad, shift1_grad, shift2_grad, downb_grad]
        + [jnp.zeros((2, width), wide)],
        axis=0,
    )
    spare = jnp.zeros((8, BLOCK - lanes), wide)
    for part in range(at.tokens):
        sums_ref[part] = jnp.concatenate(
            [sums[:, part * lanes : (part + 1) * lanes], spare], axis=1
        )
    for j in order:
        attn_line.arrive(j)
        home = attn_ref.at[2 * j + c]
        last.append(wires.send(home, home, at.partner()))
    for copy in last:
        copy.wait_recv()
    for copy in own:
        copy.wait()
    wires.finish()
    for line in (hid_line, ffn_line, grad_line, back_line, attn_line):
        line.drain(order)


def feed_forward(ctx, x, mixs, vecs, up, down, up2, down2, out_grad, ident):
    tokens, batches = lax.axis_size("seq"), lax.axis_size("batch")
    chips = tokens // 2
    width = x.shape[1]
    columns = width // batches
    hidden_here = up.shape[1]
    low, wide = jnp.bfloat16, jnp.float32
    outs = (
        jax.ShapeDtypeStruct(x.shape, low),
        jax.ShapeDtypeStruct(x.shape, wide),
        jax.ShapeDtypeStruct((tokens, 8, BLOCK), wide),
        jax.ShapeDtypeStruct((tokens,) + x.shape, low),
        jax.ShapeDtypeStruct((width, width), low),
        jax.ShapeDtypeStruct((batches, columns, hidden_here), low),
        jax.ShapeDtypeStruct((batches, columns, hidden_here), low),
        jax.ShapeDtypeStruct((batches, 8, hidden_here), wide),
    )
    block = (chips,) + x.shape
    wide_block = (chips, x.shape[0], 2 * hidden_here)
    slots = (chips + 1,) + x.shape
    up_half, bias_half = (width, hidden_here), (8, hidden_here)
    down_half = up_half
    scratch = [
        pltpu.VMEM(ctx.shape, low),
        pltpu.VMEM(block, low),
        pltpu.VMEM(wide_block, low),
        pltpu.VMEM(wide_block, wide),
        pltpu.VMEM(block, low),
        pltpu.VMEM(slots, low),
        pltpu.VMEM(block, low),
        pltpu.VMEM(wide_block, low),
        pltpu.VMEM(block, low),
        pltpu.VMEM(slots, low),
        pltpu.VMEM(up_half, low),
        pltpu.VMEM(down_half, low),
        pltpu.VMEM(bias_half, wide),
        pltpu.VMEM(up_half, low),
        pltpu.VMEM(down_half, low),
        pltpu.VMEM(bias_half, wide),
        pltpu.VMEM((batches, columns, hidden_here), low),
        pltpu.VMEM((batches, columns, hidden_here), low),
        pltpu.VMEM(bias_half, wide),
        pltpu.VMEM((16, width), wide),
    ]
    scratch += (gather_sems(chips) + reduce_sems(chips)) * 2 + gather_sems(chips)
    inputs = (ctx, x, mixs, vecs, up, down, up2, down2, out_grad)
    sends = tokens - 1 + 2 * batches - 1 + 3 + 3 * (batches - 1) + chips
    return pl.pallas_call(
        feed_kernel,
        out_shape=outs,
        in_specs=[VMEM_SPEC] * len(inputs),
        out_specs=(VMEM_SPEC,) * len(outs),
        scratch_shapes=scratch + wire_scratch(sends, 5),
        compiler_params=pltpu.CompilerParams(
            collective_id=ident, has_side_effects=True, vmem_limit_bytes=FEED_VMEM
        ),
        name="feed_forward",
    )(*inputs)


def settle_kernel(
    vec_ref, col_ref, dcat_ref, rel_ref, w_ref, xs_ref, table_ref, ctx_ref, attn_ref,
    ins_ref, vec_all_ref, cols_ref, dw_all_ref, tab_all_ref, mix_all_ref,
    in_ref, dw_ref, tab_ref, mix_ref, half_ref, sum_ref, got_ref, vecs_ref, vec_low_ref,
    dws_ref, dw_low_ref, rels_ref, rel_low_ref, mixs_ref, mix_low_ref,
    line_send, line_recv, tab_send, tab_recv, *sems,
):
    at = Place()
    wires = Wires(*sems)
    low, wide = jnp.bfloat16, jnp.float32
    b, s, z, c = at.row, at.part, at.chip, at.core
    off_diagonal = b != z
    same, cross = (z, 2 * b + c), (z, 2 * b + 1 - c)
    meet(at.all_peers())
    width = w_ref.shape[0]
    columns = width // at.batches
    full_len = dcat_ref.shape[0]
    group = 2 * DH
    buckets = table_ref.shape[0]
    bucket_rows = buckets // at.batches

    dw_sends, mix_sends, vec_sends, rel_sends, last, own = [], [], [], [], [], []
    for k in range(1, at.batches):
        row, peer = at.along_rows(k)
        rows = pl.ds(pl.multiple_of(row * bucket_rows, bucket_rows), bucket_rows)
        rel_sends.append(wires.send(rel_ref.at[rows], rels_ref.at[k - 1], peer))

    for k in range(1, at.tokens):
        part, peer = at.along_seq(k)
        vec_sends.append(wires.send(vec_ref.at[part], vecs_ref.at[k - 1], peer))
    mine = 2 * b + c
    for k in range(1, 2 * at.batches):
        last.append(wires.send(col_ref, cols_ref.at[mine], at.along_plane(k)[2]))
    own.append(wires.local(col_ref, cols_ref.at[mine]))

    def input_part(chip, core):
        start = pl.multiple_of((2 * chip + core) * BLOCK, BLOCK)
        in_ref[chip, core] = dot_nt(dcat_ref[pl.ds(start, BLOCK)], w_ref[...]).astype(low)

    order = far_order(at)
    places = order + [z]
    halves = []
    for chip in places:
        input_part(chip, 1 - c)
        halves.append(wires.send(in_ref.at[chip, 1 - c], half_ref.at[chip], at.partner()))
    line = LineReduce(at, sum_ref, got_ref, (line_send, line_recv))
    line.clear()
    for i, chip in enumerate(places):
        input_part(chip, c)
        halves[i].wait_recv()
        total = in_ref[chip, c].astype(wide) + half_ref[chip].astype(wide)
        sum_ref[chip] = total.astype(low)
        if i < len(order):
            line.send_last(chip)

    whole = xs_ref[...].reshape(full_len, width)
    dw = dot_tn(whole, dcat_ref[...])
    dw_rel = dot_tn(table_ref[...], rel_ref[...])
    dw = jnp.concatenate([dw[:, : 2 * group] + dw_rel, dw[:, 2 * group :]], axis=1)
    for row in range(at.batches):
        dw_ref[row] = dw[row * columns : (row + 1) * columns].astype(low)
    for k in range(1, at.batches):
        row, peer = at.along_rows(k)
        dw_sends.append(wires.send(dw_ref.at[row], dws_ref.at[k - 1], peer))

    rows = pl.ds(pl.multiple_of(b * bucket_rows, bucket_rows), bucket_rows)
    total = rel_ref[rows].astype(wide)
    for k in range(1, at.batches):
        rel_sends[k - 1].wait_recv()
        total = total + rels_ref[k - 1].astype(wide)
    rel_low_ref[...] = total.astype(low)
    table_rows = bucket_rows // 2
    for row in range(at.batches):
        piece = dot_nt(rel_low_ref[...], w_ref[row * columns : (row + 1) * columns, : 2 * group])
        for core in range(2):
            tab_ref[core, row] = piece[core * table_rows : (core + 1) * table_rows].astype(low)

    def tab_copy(k, d):
        row = lax.rem(b + k, at.batches)
        core = jnp.where(d == 0, c, 1 - c)
        return pltpu.make_async_remote_copy(
            src_ref=tab_ref.at[core, row],
            dst_ref=tab_all_ref.at[s],
            send_sem=tab_send.at[2 * k + d],
            recv_sem=tab_recv.at[s],
            device_id=(row, 2 * b + core),
            device_id_type=MESH,
        )

    tab_stay = pltpu.make_async_copy(
        tab_ref.at[c, b], tab_all_ref.at[s], sems[2].at[wires.used[1]]
    )
    wires.used[1] += 1
    for k in range(at.batches):
        for d in range(2):
            if k or d:
                tab_copy(k, d).start()

    @pl.when(off_diagonal)
    def _():
        tab_copy(0, 0).start()

    @pl.when(jnp.logical_not(off_diagonal))
    def _():
        tab_stay.start()

    line.pass_on(order[:1])
    mix = dot_tn(
        ctx_ref[...].reshape(full_len, group), attn_ref[...].reshape(full_len, width)
    )
    for row in range(at.batches):
        mix_ref[row] = mix[:, row * columns : (row + 1) * columns].astype(low)
    for k in range(1, at.batches):
        row, peer = at.along_rows(k)
        mix_sends.append(wires.send(mix_ref.at[row], mixs_ref.at[k - 1], peer))

    line.pass_on(order[1:2])
    total = dw_ref[b].astype(wide)
    for k in range(1, at.batches):
        dw_sends[k - 1].wait_recv()
        total = total + dws_ref[k - 1].astype(wide)
    shard_rows = dw_low_ref.shape[1]
    for half in range(2):
        dw_low_ref[half] = total[half * shard_rows : (half + 1) * shard_rows].astype(low)
    k = wires.used[0]
    wires.used[0] += 1
    move = pltpu.make_async_remote_copy(
        src_ref=dw_low_ref.at[c],
        dst_ref=dw_all_ref.at[c],
        send_sem=sems[0].at[k],
        recv_sem=sems[1].at[k],
        device_id=same,
        device_id_type=MESH,
    )
    stay = pltpu.make_async_copy(
        dw_low_ref.at[c], dw_all_ref.at[c], sems[2].at[wires.used[1]]
    )
    wires.used[1] += 1

    @pl.when(off_diagonal)
    def _():
        move.start()

    @pl.when(jnp.logical_not(off_diagonal))
    def _():
        stay.start()

    last.append(wires.send(dw_low_ref.at[1 - c], dw_all_ref.at[c], cross))

    line.pass_on(order[2:])
    total = mix_ref[b].astype(wide)
    for k in range(1, at.batches):
        mix_sends[k - 1].wait_recv()
        total = total + mixs_ref[k - 1].astype(wide)
    mix_low_ref[...] = total.astype(low)
    last.append(wires.send(mix_low_ref, mix_all_ref.at[c], at.partner()))
    own.append(wires.local(mix_low_ref, mix_all_ref.at[c]))

    total = vec_ref[s]
    for k in range(1, at.tokens):
        vec_sends[k - 1].wait_recv()
        total = total + vecs_ref[k - 1]
    vec_low_ref[...] = total
    for k in range(1, at.batches):
        last.append(wires.send(vec_low_ref, vec_all_ref.at[b], at.along_rows(k)[1]))
    own.append(wires.local(vec_low_ref, vec_all_ref.at[b]))

    ins_ref[...] = sum_ref[z].astype(wide) + line.collect()
    for copy in last:
        copy.wait_recv()
    for copy in own:
        copy.wait()
    wires.finish()
    line.drain(order)
    for part in range(at.tokens):
        landed = pltpu.make_async_remote_copy(
            src_ref=tab_all_ref.at[part],
            dst_ref=tab_all_ref.at[part],
            send_sem=tab_send.at[0],
            recv_sem=tab_recv.at[part],
            device_id=at.partner(),
            device_id_type=MESH,
        )

        @pl.when(jnp.logical_or(off_diagonal, s != part))
        def _():
            landed.wait_recv()

    for k in range(at.batches):
        for d in range(2):
            if k or d:
                tab_copy(k, d).wait_send()

    @pl.when(off_diagonal)
    def _():
        tab_copy(0, 0).wait_send()
        move.wait()

    @pl.when(jnp.logical_not(off_diagonal))
    def _():
        tab_stay.wait()
        stay.wait()


def settle_grads(vec, cols, dcat, rel, w_cat, xs, table, ctx, attn_all, ident):
    tokens, batches = lax.axis_size("seq"), lax.axis_size("batch")
    chips = tokens // 2
    low, wide = jnp.bfloat16, jnp.float32
    local_len, width = xs.shape[1:]
    columns, group = width // batches, dcat.shape[1]
    buckets = table.shape[0]
    half = (chips, local_len, width)
    dw_pieces = (2, columns // 2, group)
    mix_piece = (2 * DH, columns)
    dw_piece, rel_piece = (columns, group), (buckets // batches, rel.shape[1])
    outs = (
        jax.ShapeDtypeStruct((local_len, width), wide),
        jax.ShapeDtypeStruct((batches,) + vec.shape[1:], wide),
        like(cols, 2 * batches),
        jax.ShapeDtypeStruct(dw_pieces, low),
        jax.ShapeDtypeStruct((tokens, buckets // tokens, columns), low),
        jax.ShapeDtypeStruct((2,) + mix_piece, low),
    )
    scratch = [
        pltpu.VMEM((chips, 2, local_len, width), low),
        pltpu.VMEM((batches,) + dw_piece, low),
        pltpu.VMEM((2, batches, buckets // tokens, columns), low),
        pltpu.VMEM((batches,) + mix_piece, low),
        pltpu.VMEM(half, low),
        pltpu.VMEM(half, low),
        pltpu.VMEM((chips + 1, local_len, width), low),
        pltpu.VMEM((tokens - 1,) + vec.shape[1:], wide),
        pltpu.VMEM(vec.shape[1:], wide),
        pltpu.VMEM((batches - 1,) + dw_piece, low),
        pltpu.VMEM(dw_pieces, low),
        pltpu.VMEM((batches - 1,) + rel_piece, low),
        pltpu.VMEM(rel_piece, low),
        pltpu.VMEM((batches - 1,) + mix_piece, low),
        pltpu.VMEM(mix_piece, low),
    ]
    scratch += reduce_sems(chips)
    scratch += [pltpu.SemaphoreType.DMA((2 * batches,)), pltpu.SemaphoreType.DMA((tokens,))]
    sends = 4 * (batches - 1) + chips + tokens - 1 + 2 * batches - 1 + 3
    inputs = (vec, cols, dcat, rel, w_cat, xs, table, ctx, attn_all)
    return comm_call(settle_kernel, "settle_grads", ident, outs, inputs, sends, 6, scratch=scratch)


def finish_kernel(
    pre_ref, ins_ref, vecs_ref, cols_ref, dws_ref, tabs_ref, mixs_ref, ups_ref, downs_ref,
    upbs_ref, last_ref,
    output_ref, input_ref, dq_ref, dk_ref, dv_ref, mix_ref, table_ref, bias_ref, gain_ref, shift_ref,
    up_ref, upb_ref, down_ref, downb_ref,
):
    at = Place()
    wide = jnp.float32

    def total(ref):
        out = ref[0].astype(wide)
        for k in range(1, ref.shape[0]):
            out = out + ref[k].astype(wide)
        return out

    output_ref[...] = last_ref[...]
    input_ref[...] = pre_ref[...] + ins_ref[...]
    up_ref[...] = total(ups_ref)
    down_ref[...] = total(downs_ref)
    upb_ref[...] = total(upbs_ref)[0:1]
    table_ref[...] = total(tabs_ref)
    group = 2 * DH
    spare = jnp.zeros((dws_ref.shape[1], DH), wide)
    for i, ref in enumerate((dq_ref, dk_ref, dv_ref)):
        lower = dws_ref[0, :, i * group : (i + 1) * group].astype(wide)
        upper = dws_ref[1, :, i * group : (i + 1) * group].astype(wide)
        ref[...] = jnp.concatenate([lower, spare], axis=1) + jnp.concatenate(
            [spare, upper], axis=1
        )
    rows = mix_ref.shape[0]
    lower, upper = mixs_ref[0].astype(wide), mixs_ref[1].astype(wide)
    spare = jnp.zeros((DH, lower.shape[1]), wide)
    whole = jnp.concatenate([lower, spare], axis=0) + jnp.concatenate([spare, upper], axis=0)
    mix_ref[...] = jnp.where(at.core == 0, whole[:rows], whole[rows:])
    small = total(vecs_ref)
    lanes = bias_ref.shape[1]
    cols = [cols_ref[core, 0:1] for core in range(2)]
    for row in range(1, at.batches):
        cols = [cols[core] + cols_ref[2 * row + core, 0:1] for core in range(2)]
    spare = jnp.zeros((1, DH), wide)
    biases = []
    for i in range(3):
        lower, upper = [part[:, i * group : (i + 1) * group] for part in cols]
        both = jnp.concatenate([lower, spare], axis=1) + jnp.concatenate([spare, upper], axis=1)
        biases.append(jnp.where(at.core == 0, both[:, :lanes], both[:, lanes:]))
    bias_ref[...] = jnp.concatenate(biases + [small[0:1, :lanes]], axis=0)
    gain_ref[...] = small[1:3, :lanes]
    shift_ref[...] = small[3:5, :lanes]
    downb_ref[...] = small[5:6, :lanes]


def finish(pre_grad, parts, shapes):
    inputs = (pre_grad,) + tuple(parts)
    return pl.pallas_call(
        finish_kernel,
        out_shape=(like(parts[-1]),)
        + tuple(jax.ShapeDtypeStruct(shape, jnp.float32) for shape in shapes),
        in_specs=[VMEM_SPEC] * len(inputs),
        out_specs=(VMEM_SPEC,) * (len(shapes) + 1),
        compiler_params=pltpu.CompilerParams(vmem_limit_bytes=COMM_VMEM),
        name="finish",
    )(*inputs)


def fits_fast(layer_input, table_shard, hidden_here):
    rows, local_len, width = layer_input.shape
    tokens, batches = lax.axis_size("seq"), lax.axis_size("batch")
    return (
        rows == 1
        and local_len == BLOCK
        and tokens == 2 * batches
        and width == 3 * DH * batches
        and (table_shard.shape[0] * tokens) % (4 * BLOCK) == 0
        and tokens == 8
        and 10 + hidden_here // BLOCK <= 16
        and hidden_here % BLOCK == 0
    )


def fast_body(
    layer_input, segment_ids, w_query, w_key, w_value, w_mix, rel_table, attn_biases,
    norm_gains, norm_shifts, w_up, up_bias, w_down, down_bias, out_grad,
):
    local_len, width = layer_input.shape[1:]
    low = jnp.bfloat16
    shard_rows, shard_cols = w_query.shape
    lanes = attn_biases.shape[1]
    hidden_here = w_up.shape[1]
    x = layer_input[0]
    pack = jnp.concatenate([attn_biases, norm_gains, norm_shifts, down_bias[None]], axis=0)
    pack = jnp.pad(pack, ((0, 0), (0, BLOCK - lanes)))
    pack = jnp.concatenate(
        [pack, segment_ids.astype(low), up_bias.reshape(hidden_here // BLOCK, BLOCK)], axis=0
    )
    pack = jnp.pad(pack, ((0, 16 - pack.shape[0]), (0, 0)))
    weights = (w_query, w_key, w_value, w_mix, rel_table, pack, w_up, w_down)
    xs, qkvs, mixs, tables, vecs, up2, down2 = gather_inputs(
        *[pltpu.with_memory_space_constraint(a, pltpu.HBM) for a in (x,) + weights]
    )
    q, k, v, qrev, krev, probs, ctx, w_cat, table = attend(xs, qkvs, tables, vecs)
    output, pre_grad, sums, attn_all, m_mix, ups, downs, upbs = feed_forward(
        ctx, x, mixs, vecs, w_up, w_down, up2, down2, out_grad[0], 1
    )
    dcat, rel_grad, cols = attend_back(q, k, v, qrev, krev, probs, m_mix, attn_all)
    ins, vec_all, cols_all, dw_all, tab_all, mix_all = settle_grads(
        sums, cols, dcat, rel_grad, w_cat, xs, table, ctx, attn_all, 2
    )
    shard = (shard_rows, shard_cols)
    shapes = (
        x.shape, shard, shard, shard, shard, rel_table.shape, (4, lanes), (2, lanes), (2, lanes),
        (width // lax.axis_size("batch"), hidden_here), (1, hidden_here),
        (width // lax.axis_size("batch"), hidden_here), (1, lanes),
    )
    grads = finish(
        pre_grad,
        (ins, vec_all, cols_all, dw_all, tab_all, mix_all, ups, downs, upbs, output),
        shapes,
    )
    output, input_grad, dq, dk, dv, dmix, dtable = grads[:7]
    dbias, dgain, dshift, dup, dupb, ddown, ddownb = grads[7:]
    return (
        output[None], input_grad[None], dq, dk, dv, dmix, dtable, dbias, dgain, dshift,
        dup, dupb.reshape(hidden_here), ddown.T, ddownb.reshape(lanes),
    )


def body(
    layer_input,
    segment_ids,
    w_query,
    w_key,
    w_value,
    w_mix,
    rel_table,
    attn_biases,
    norm_gains,
    norm_shifts,
    w_up,
    up_bias,
    w_down,
    down_bias,
    out_grad,
):
    if fits_fast(layer_input, rel_table, w_up.shape[1]):
        return fast_body(
            layer_input, segment_ids, w_query, w_key, w_value, w_mix, rel_table, attn_biases,
            norm_gains, norm_shifts, w_up, up_bias, w_down, down_bias, out_grad,
        )
    rows, local_len, width = layer_input.shape
    full_len = local_len * lax.axis_size("seq")
    tokens_here = local_len * rows
    highest_prec = lax.Precision.HIGHEST
    parts = (
        lax.all_gather(w_query, "batch", axis=1, tiled=True),
        lax.all_gather(w_key, "batch", axis=1, tiled=True),
        lax.all_gather(w_value, "batch", axis=1, tiled=True),
        lax.all_gather(w_mix, "batch", axis=1, tiled=True),
        lax.all_gather(rel_table, "batch", axis=1, tiled=True),
    )
    whole = (
        lax.all_gather(parts[0], "seq", axis=0, tiled=True),
        lax.all_gather(parts[1], "seq", axis=0, tiled=True),
        lax.all_gather(parts[2], "seq", axis=0, tiled=True),
        lax.all_gather(parts[3], "seq", axis=0, tiled=True),
        lax.all_gather(parts[4], "seq", axis=0, tiled=True),
        lax.all_gather(attn_biases, "seq", axis=1, tiled=True),
        lax.all_gather(norm_gains, "seq", axis=1, tiled=True),
        lax.all_gather(norm_shifts, "seq", axis=1, tiled=True),
        lax.all_gather(down_bias, "seq", axis=0, tiled=True),
    )
    m_query, m_key, m_value, m_mix, table, biases, gains, shifts, bias_down = whole
    flat_input = jnp.swapaxes(layer_input, 0, 1).reshape(tokens_here, width)
    queries = (jnp.dot(flat_input, m_query, preferred_element_type=jnp.float32) + biases[0]).astype(
        jnp.bfloat16
    )
    keys_here = (jnp.dot(flat_input, m_key, preferred_element_type=jnp.float32) + biases[1]).astype(
        jnp.bfloat16
    )
    values_here = (
        jnp.dot(flat_input, m_value, preferred_element_type=jnp.float32) + biases[2]
    ).astype(jnp.bfloat16)
    query_rel = (jnp.dot(table, m_query, preferred_element_type=jnp.float32) + biases[0]).astype(
        jnp.bfloat16
    )
    key_rel = (jnp.dot(table, m_key, preferred_element_type=jnp.float32) + biases[1]).astype(
        jnp.bfloat16
    )
    local_seg = jnp.swapaxes(segment_ids, 0, 1).astype(jnp.bfloat16)
    keys_all, values_all, seg_all = (
        lax.all_gather(keys_here.reshape(local_len, rows, width), "seq", axis=0, tiled=True),
        lax.all_gather(values_here.reshape(local_len, rows, width), "seq", axis=0, tiled=True),
        lax.all_gather(local_seg, "seq", axis=0, tiled=True),
    )
    buckets = table.shape[0]
    offset = lax.axis_index("seq") * local_len
    bucket_iota = jnp.arange(buckets, dtype=jnp.int32)
    inner_cols = (bucket_iota > 0) & (bucket_iota < buckets - 1)
    same_doc = (
        jnp.swapaxes(local_seg, 0, 1)[:, None, :, None]
        == jnp.swapaxes(seg_all, 0, 1)[:, None, None, :]
    )
    score_scale = 1.0 / math.sqrt(3.0 * DH)
    head_queries = split_heads(queries.reshape(local_len, rows, width))
    head_keys = split_heads(keys_all)
    head_values = split_heads(values_all)
    rel_queries = split_table(query_rel)
    rel_keys = split_table(key_rel)

    def forward_group(carry, group):
        g_query, g_key, g_value, g_qrel, g_krel = group
        total, near_pull, far_pull, window = relative_scores(
            g_query, g_key, g_krel, g_qrel, offset, full_len
        )
        scores = jnp.where(same_doc, total * score_scale, masked_score)
        highest = jnp.max(scores, axis=-1, keepdims=True)
        exponent = jnp.exp(scores - highest)
        denominator = jnp.sum(exponent, axis=-1, keepdims=True)
        weights_low = (exponent / denominator).astype(jnp.bfloat16)
        context = jnp.einsum(
            "rgij,rgjd->rgid", weights_low, g_value, preferred_element_type=jnp.float32
        )
        return (carry, (context, (highest + jnp.log(denominator))[..., 0]))

    unused, (context_groups, log_totals) = lax.scan(
        forward_group, None, (head_queries, head_keys, head_values, rel_queries, rel_keys)
    )
    context_low = join_heads(context_groups).reshape(tokens_here, width).astype(jnp.bfloat16)
    pre_norm = (
        flat_input.astype(jnp.float32)
        + jnp.dot(context_low, m_mix, preferred_element_type=jnp.float32)
        + biases[3]
    )
    hidden, norm1_pull = jax.vjp(
        normalize, pre_norm, gains[0].astype(jnp.float32), shifts[0].astype(jnp.float32)
    )
    hidden_low = hidden.astype(jnp.bfloat16)

    def spread_rows(rows_low):
        return lax.all_gather(rows_low, "seq", axis=0, tiled=True)

    def hidden_sums(make_term):
        return lax.psum_scatter(
            make_term(jnp.int32(0), tokens_here * lax.axis_size("seq")),
            "seq",
            scatter_dimension=0,
            tiled=True,
        )

    hidden_rows = spread_rows(hidden_low)
    inner = jnp.dot(hidden_rows, w_up, preferred_element_type=jnp.float32) + up_bias
    act, gelu_pull = jax.vjp(exact_gelu, inner)
    act_low = act.astype(jnp.bfloat16)

    def down_rows(start, count):
        return jnp.dot(act_low, w_down, preferred_element_type=jnp.float32)

    ffn_result = hidden_sums(down_rows)
    mixed = hidden + ffn_result + bias_down
    output, norm2_pull = jax.vjp(
        normalize, mixed, gains[1].astype(jnp.float32), shifts[1].astype(jnp.float32)
    )
    flat_grad = jnp.swapaxes(out_grad, 0, 1).reshape(tokens_here, width).astype(jnp.float32)
    mixed_grad, gain2_grad, shift2_grad = norm2_pull(flat_grad)
    ffn_grad_low = mixed_grad.astype(jnp.bfloat16)
    grad_rows = spread_rows(ffn_grad_low)
    act_grad = jnp.einsum("nd,fd->nf", grad_rows, w_down, preferred_element_type=jnp.float32)
    inner_low = gelu_pull(act_grad)[0].astype(jnp.bfloat16)
    up_part = jnp.einsum("nd,nf->df", hidden_rows, inner_low, preferred_element_type=jnp.float32)
    upb_part = jnp.sum(inner_low.astype(jnp.float32), axis=0)
    down_part = jnp.einsum("nf,nd->fd", act_low, grad_rows, preferred_element_type=jnp.float32)

    def back_rows(start, count):
        return jnp.einsum("nf,df->nd", inner_low, w_up, preferred_element_type=jnp.float32)

    hidden_grad = mixed_grad + hidden_sums(back_rows)
    pre_grad, gain1_grad, shift1_grad = norm1_pull(hidden_grad)
    attn_low = pre_grad.astype(jnp.bfloat16)
    mix_whole = jnp.einsum("nd,ne->de", context_low, attn_low, preferred_element_type=jnp.float32)
    context_grad = jnp.einsum(
        "ne,de->nd", attn_low, m_mix, preferred_element_type=jnp.float32
    ).astype(jnp.bfloat16)
    head_context_grad = split_heads(context_grad.reshape(local_len, rows, width))

    def query_side(group):
        g_query, g_key, g_value, g_qrel, g_krel, g_dctx, g_lse = group
        total, near_pull, far_pull, window = relative_scores(
            g_query, g_key, g_krel, g_qrel, offset, full_len
        )
        scores = jnp.where(same_doc, total * score_scale, masked_score)
        weights_now = jnp.exp(scores - g_lse[..., None])
        prob_grad = jnp.einsum(
            "rgid,rgjd->rgij", g_dctx, g_value, preferred_element_type=jnp.float32
        )
        inner_sum = jnp.sum(weights_now * prob_grad, axis=-1)
        score_grad = (weights_now * (prob_grad - inner_sum[..., None])).astype(jnp.bfloat16)
        grad_wide = score_grad.astype(jnp.float32)
        near_grad = near_pull(grad_wide)[0]
        near_low = jnp.where(inner_cols, near_grad, 0.0).astype(jnp.bfloat16)
        near_ends = end_columns(near_grad)
        query_part = jnp.einsum(
            "rgij,rgjd->rgid", score_grad, g_key, preferred_element_type=jnp.float32
        )
        query_part = (
            query_part
            + jnp.einsum("rgib,gbd->rgid", near_low, g_krel, preferred_element_type=jnp.float32)
            + end_terms(near_ends, g_krel)
        )
        krel_part = with_ends(
            jnp.einsum("rgib,rgid->gbd", near_low, g_query, preferred_element_type=jnp.float32),
            end_rows(near_ends, g_query),
        )
        return (
            weights_now,
            score_grad,
            grad_wide,
            far_pull,
            window,
            inner_sum,
            query_part * score_scale,
            krel_part * score_scale,
        )

    query_groups = (
        head_queries,
        head_keys,
        head_values,
        rel_queries,
        rel_keys,
        head_context_grad,
        log_totals,
    )

    def all_grads(carry, group):
        weights_now, score_grad, grad_wide, far_pull, window, inner_sum, query_part, krel_part = (
            query_side(group)
        )
        g_query, g_key, g_value, g_qrel, g_krel, g_dctx, g_lse = group
        cross_grad, end_grad = far_pull(grad_wide)
        cross_low = cross_grad.astype(jnp.bfloat16)
        key_part = jnp.einsum(
            "rgij,rgid->rgjd", score_grad, g_query, preferred_element_type=jnp.float32
        )
        band_part = jnp.einsum(
            "rgmb,gbd->rgmd", cross_low, g_qrel, preferred_element_type=jnp.float32
        )
        key_part = (
            key_part
            + unband(band_part, offset, full_len, buckets // 2)
            + end_terms(end_grad, g_qrel)
        )
        value_part = jnp.einsum(
            "rgij,rgid->rgjd",
            weights_now.astype(jnp.bfloat16),
            g_dctx,
            preferred_element_type=jnp.float32,
        )
        qrel_part = with_ends(
            jnp.einsum("rgmb,rgmd->gbd", cross_low, window, preferred_element_type=jnp.float32),
            end_rows(end_grad, g_key),
        )
        return (
            carry,
            (query_part, key_part * score_scale, value_part, qrel_part * score_scale, krel_part),
        )

    unused, (dq_groups, dk_groups, dv_groups, dqrel_groups, dkrel_groups) = lax.scan(
        all_grads, None, query_groups
    )
    key_sum, value_sum = (
        lax.psum_scatter(join_heads(dk_groups), "seq", scatter_dimension=0, tiled=True),
        lax.psum_scatter(join_heads(dv_groups), "seq", scatter_dimension=0, tiled=True),
    )
    key_grads = key_sum.reshape(tokens_here, width).astype(jnp.bfloat16)
    value_grads = value_sum.reshape(tokens_here, width).astype(jnp.bfloat16)
    query_grads = join_heads(dq_groups).reshape(tokens_here, width).astype(jnp.bfloat16)
    qrel_grad = join_table(dqrel_groups)
    krel_grad = join_table(dkrel_groups)
    input_grad = pre_grad + jnp.einsum(
        "ne,de->nd", query_grads, m_query, preferred_element_type=jnp.float32
    )
    input_grad = input_grad + jnp.einsum(
        "ne,de->nd", key_grads, m_key, preferred_element_type=jnp.float32
    )
    input_grad = input_grad + jnp.einsum(
        "ne,de->nd", value_grads, m_value, preferred_element_type=jnp.float32
    )
    query_whole = jnp.einsum(
        "nd,ne->de", flat_input, query_grads, preferred_element_type=jnp.float32
    ) + jnp.einsum(
        "bd,be->de", table, qrel_grad, precision=highest_prec, preferred_element_type=jnp.float32
    )
    key_whole = jnp.einsum(
        "nd,ne->de", flat_input, key_grads, preferred_element_type=jnp.float32
    ) + jnp.einsum(
        "bd,be->de", table, krel_grad, precision=highest_prec, preferred_element_type=jnp.float32
    )
    value_whole = jnp.einsum(
        "nd,ne->de", flat_input, value_grads, preferred_element_type=jnp.float32
    )
    table_whole = jnp.einsum(
        "be,de->bd", qrel_grad, m_query, precision=highest_prec, preferred_element_type=jnp.float32
    ) + jnp.einsum(
        "be,de->bd", krel_grad, m_key, precision=highest_prec, preferred_element_type=jnp.float32
    )
    bias_whole = jnp.stack(
        [
            jnp.sum(query_grads.astype(jnp.float32), axis=0) + jnp.sum(qrel_grad, axis=0),
            jnp.sum(key_grads.astype(jnp.float32), axis=0) + jnp.sum(krel_grad, axis=0),
            jnp.sum(value_grads.astype(jnp.float32), axis=0),
            jnp.sum(pre_grad, axis=0),
        ]
    )
    gain_whole = jnp.stack([gain1_grad, gain2_grad])
    shift_whole = jnp.stack([shift1_grad, shift2_grad])
    downb_whole = jnp.sum(mixed_grad, axis=0)
    seq_parts = (
        lax.psum_scatter(query_whole, "seq", scatter_dimension=0, tiled=True),
        lax.psum_scatter(key_whole, "seq", scatter_dimension=0, tiled=True),
        lax.psum_scatter(value_whole, "seq", scatter_dimension=0, tiled=True),
        lax.psum_scatter(mix_whole, "seq", scatter_dimension=0, tiled=True),
        lax.psum_scatter(table_whole, "seq", scatter_dimension=0, tiled=True),
        lax.psum_scatter(bias_whole, "seq", scatter_dimension=1, tiled=True),
        lax.psum_scatter(gain_whole, "seq", scatter_dimension=1, tiled=True),
        lax.psum_scatter(shift_whole, "seq", scatter_dimension=1, tiled=True),
        lax.psum_scatter(downb_whole, "seq", scatter_dimension=0, tiled=True),
    )
    batch_parts = (
        lax.psum_scatter(seq_parts[0], "batch", scatter_dimension=1, tiled=True),
        lax.psum_scatter(seq_parts[1], "batch", scatter_dimension=1, tiled=True),
        lax.psum_scatter(seq_parts[2], "batch", scatter_dimension=1, tiled=True),
        lax.psum_scatter(seq_parts[3], "batch", scatter_dimension=1, tiled=True),
        lax.psum_scatter(seq_parts[4], "batch", scatter_dimension=1, tiled=True),
        lax.psum_scatter(up_part, "batch", scatter_dimension=0, tiled=True),
        lax.psum_scatter(down_part, "batch", scatter_dimension=1, tiled=True),
    )
    small_parts = lax.psum(
        (seq_parts[5], seq_parts[6], seq_parts[7], seq_parts[8], upb_part), "batch"
    )
    layer_output = jnp.swapaxes(output.reshape(local_len, rows, width), 0, 1).astype(jnp.bfloat16)
    input_back = jnp.swapaxes(input_grad.reshape(local_len, rows, width), 0, 1)
    return (
        layer_output,
        input_back,
        batch_parts[0],
        batch_parts[1],
        batch_parts[2],
        batch_parts[3],
        batch_parts[4],
        small_parts[0],
        small_parts[1],
        small_parts[2],
        batch_parts[5],
        small_parts[4],
        batch_parts[6],
        small_parts[3],
    )


def solution(mesh):
    return jax.shard_map(
        body,
        mesh=mesh,
        in_specs=(
            P("batch", "seq", None),
            P("batch", "seq"),
            P("seq", "batch"),
            P("seq", "batch"),
            P("seq", "batch"),
            P("seq", "batch"),
            P("seq", "batch"),
            P(None, "seq"),
            P(None, "seq"),
            P(None, "seq"),
            P(None, "seq"),
            P("seq"),
            P("seq", None),
            P("seq"),
            P("batch", "seq", None),
        ),
        out_specs=(
            P("batch", "seq", None),
            P("batch", "seq", None),
            P("seq", "batch"),
            P("seq", "batch"),
            P("seq", "batch"),
            P("seq", "batch"),
            P("seq", "batch"),
            P(None, "seq"),
            P(None, "seq"),
            P(None, "seq"),
            P("batch", "seq"),
            P("seq"),
            P("seq", "batch"),
            P("seq"),
        ),
        check_vma=False,
    )
```

```python
import math

import jax
import jax.numpy as jnp
from jax import lax
from jax.experimental import pallas as pl
from jax.experimental.pallas import tpu as pltpu
from jax.sharding import PartitionSpec as P

DH = 64


masked_score = -1e30
norm_eps = 1e-06
pair_heads = 2


def normalize(values, gain, shift):
    average = jnp.mean(values, axis=-1, keepdims=True)
    centered = values - average
    variance = jnp.mean(centered * centered, axis=-1, keepdims=True)
    return centered * lax.rsqrt(variance + norm_eps) * gain + shift


def exact_gelu(values):
    return jax.nn.gelu(values, approximate=False)


def split_heads(matrix):
    length, rows, width = matrix.shape
    groups = width // (pair_heads * DH)
    return matrix.reshape(length, rows, groups, pair_heads, DH).transpose(2, 1, 3, 0, 4)


def join_heads(matrix):
    groups, rows, pair, length, depth = matrix.shape
    return matrix.transpose(3, 1, 0, 2, 4).reshape(length, rows, groups * pair * depth)


def split_table(matrix):
    buckets, width = matrix.shape
    return matrix.reshape(buckets, width // (pair_heads * DH), pair_heads, DH).transpose(1, 2, 0, 3)


def join_table(matrix):
    groups, pair, buckets, depth = matrix.shape
    return matrix.transpose(2, 0, 1, 3).reshape(buckets, groups * pair * depth)


def table_ends(table):
    return jnp.stack([table[:, 0], table[:, -1]], axis=1)


def near_skew(table_prod, offset, full_len):
    lead = table_prod.shape[:-2]
    count, buckets = table_prod.shape[-2:]
    span = buckets // 2
    lead_pad = [(0, 0)] * len(lead)
    flipped = jnp.pad(table_prod[..., ::-1], lead_pad + [(0, 0), (0, count)])
    sheared = flipped.reshape(lead + (count * (buckets + count),))[
        ..., : count * (buckets + count - 1)
    ]
    sheared = sheared.reshape(lead + (count, buckets + count - 1))
    spread = jnp.pad(sheared, lead_pad + [(0, 0), (full_len, full_len)])
    band = lax.dynamic_slice_in_dim(
        spread, full_len + span - 1 - offset, full_len, axis=len(lead) + 1
    )
    distance = (offset + jnp.arange(count, dtype=jnp.int32))[:, None] - jnp.arange(
        full_len, dtype=jnp.int32
    )[None, :]
    return jnp.where(
        distance <= -span,
        table_prod[..., 0:1],
        jnp.where(distance >= span - 1, table_prod[..., buckets - 1 :], band),
    )


def far_place(cross, end_vals, offset, count, full_len):
    lead = cross.shape[:-2]
    band_len, buckets = cross.shape[-2:]
    span = buckets // 2
    lead_pad = [(0, 0)] * len(lead)
    turned = jnp.swapaxes(cross, -1, -2).reshape(lead + (buckets * band_len,))
    turned = jnp.pad(turned, lead_pad + [(0, buckets)])
    diagonal = turned.reshape(lead + (buckets, band_len + 1))[..., :count]
    aligned = jnp.pad(jnp.swapaxes(diagonal, -1, -2), lead_pad + [(0, 0), (0, count)])
    sheared = aligned.reshape(lead + (count * (buckets + count),))[
        ..., : count * (buckets + count - 1)
    ]
    sheared = sheared.reshape(lead + (count, buckets + count - 1))
    spread = jnp.pad(sheared, lead_pad + [(0, 0), (full_len, full_len)])
    band = lax.dynamic_slice_in_dim(spread, full_len + span - offset, full_len, axis=len(lead) + 1)
    distance = (
        jnp.arange(full_len, dtype=jnp.int32)[None, :]
        - (offset + jnp.arange(count, dtype=jnp.int32))[:, None]
    )
    return jnp.where(
        distance <= -span,
        end_vals[..., 0:1, :],
        jnp.where(distance >= span - 1, end_vals[..., 1:2, :], band),
    )


def band_rows(all_rows, offset, count, span):
    padded = jnp.pad(all_rows, [(0, 0), (0, 0), (span, span), (0, 0)])
    return lax.dynamic_slice_in_dim(padded, offset, count + 2 * span - 1, axis=2)


def unband(values, offset, full_len, span):
    lead = values.shape[:2]
    room = jnp.zeros(lead + (full_len + 2 * span, values.shape[3]), jnp.float32)
    placed = lax.dynamic_update_slice_in_dim(room, values, offset, axis=2)
    return placed[:, :, span : span + full_len]


def relative_scores(own_rows, all_rows, own_table, all_table, offset, full_len):
    count = own_rows.shape[2]
    content = jnp.einsum("rgid,rgjd->rgij", own_rows, all_rows, preferred_element_type=jnp.float32)
    own_prod = jnp.einsum("rgid,gbd->rgib", own_rows, own_table, preferred_element_type=jnp.float32)
    window = band_rows(all_rows, offset, count, all_table.shape[1] // 2)
    cross = jnp.einsum("rgmd,gbd->rgmb", window, all_table, preferred_element_type=jnp.float32)
    end_vals = jnp.einsum(
        "rgjd,ged->rgej", all_rows, table_ends(all_table), preferred_element_type=jnp.float32
    )
    near_vals, near_pull = jax.vjp(lambda product: near_skew(product, offset, full_len), own_prod)
    far_vals, far_pull = jax.vjp(
        lambda part, ends: far_place(part, ends, offset, count, full_len), cross, end_vals
    )
    return (content + near_vals + far_vals, near_pull, far_pull, window)


def end_columns(grad):
    return jnp.stack([grad[..., 0], grad[..., -1]], axis=2)


def end_terms(ends, table):
    return jnp.einsum(
        "rgei,ged->rgid",
        ends,
        table_ends(table),
        precision=lax.Precision.HIGHEST,
        preferred_element_type=jnp.float32,
    )


def end_rows(ends, rows_low):
    return jnp.einsum(
        "rgei,rgid->ged",
        ends,
        rows_low,
        precision=lax.Precision.HIGHEST,
        preferred_element_type=jnp.float32,
    )


def with_ends(inner_part, edge_rows):
    buckets = inner_part.shape[1]
    place = jnp.arange(buckets, dtype=jnp.int32)[None, :, None]
    return (
        inner_part
        + jnp.where(place == 0, edge_rows[:, 0:1], 0.0)
        + jnp.where(place == buckets - 1, edge_rows[:, 1:2], 0.0)
    )


BLOCK = 128
MIB = 1024 * 1024
ATTEND_VMEM = 26 * MIB
BACK_VMEM = 40 * MIB
FEED_VMEM = 26 * MIB
COMM_VMEM = 16 * MIB


def dot_nn(a, b):
    return lax.dot_general(a, b, (((1,), (0,)), ((), ())), preferred_element_type=jnp.float32)


def dot_nt(a, b):
    return lax.dot_general(a, b, (((1,), (1,)), ((), ())), preferred_element_type=jnp.float32)


def dot_tn(a, b):
    return lax.dot_general(a, b, (((0,), (0,)), ((), ())), preferred_element_type=jnp.float32)


def turn_matrix(buckets):
    row = lax.broadcasted_iota(jnp.int32, (buckets, buckets), 0)
    col = lax.broadcasted_iota(jnp.int32, (buckets, buckets), 1)
    return (row + col == buckets - 1).astype(jnp.bfloat16)


def skew_band(product):
    count, buckets = product.shape
    row = lax.broadcasted_iota(jnp.int32, (count, BLOCK), 0)
    lane = lax.broadcasted_iota(jnp.int32, (count, BLOCK), 1)
    edge = jnp.where(row + lane <= BLOCK - 2, product[:, buckets - 1 :], product[:, 0:1])
    wide = jnp.concatenate([product, edge], axis=1)
    return pltpu.roll(wide, 1, 1, stride=1, stride_axis=0)


def skew_back(turned, buckets):
    return pltpu.roll(turned, turned.shape[1] - BLOCK, 1, stride=1, stride_axis=0)[:, :buckets]


def chip_columns(vec_ref, chip, index, core):
    width = 3 * DH // 2
    both = jnp.concatenate(
        [
            vec_ref[2 * chip, index : index + 1, :width].astype(jnp.float32),
            vec_ref[2 * chip + 1, index : index + 1, :width].astype(jnp.float32),
        ],
        axis=1,
    )
    return jnp.where(core == 0, both[:, : 2 * DH], both[:, DH:])


def attend_kernel(
    xs_ref,
    qkvs_ref,
    tables_ref,
    vecs_ref,
    q_ref,
    k_ref,
    v_ref,
    qrev_ref,
    krev_ref,
    p_ref,
    ctx_ref,
    w_ref,
    table_ref,
    segc_ref,
    place_ref,
    wide_ref,
    ends_ref,
    held_ref,
):
    at = Place()
    full_len = xs_ref.shape[0] * xs_ref.shape[1]
    buckets = table_ref.shape[0]
    blocks = full_len // BLOCK
    span = buckets // 2
    side = span // BLOCK
    band_width = buckets + BLOCK
    band_blocks = band_width // BLOCK
    group = 2 * DH
    scale = 1.0 / math.sqrt(3.0 * DH)
    units = p_ref.shape[0]
    shard_rows = qkvs_ref.shape[2]
    table_rows = tables_ref.shape[3]
    batches = tables_ref.shape[1]
    for part in range(at.tokens):
        pieces = []
        for i in range(3):
            piece = qkvs_ref[part, i]
            pieces.append(jnp.where(at.core == 0, piece[:, :group], piece[:, DH:]))
        w_ref[part * shard_rows : (part + 1) * shard_rows] = jnp.concatenate(pieces, axis=1)
        core, chip = part % 2, part // 2
        table_ref[part * table_rows : (part + 1) * table_rows] = jnp.concatenate(
            [tables_ref[core, row, chip] for row in range(batches)], axis=1
        )
        own_seg = vecs_ref[part, 9:10].astype(jnp.float32)
        segc_ref[part * BLOCK : (part + 1) * BLOCK] = jnp.broadcast_to(own_seg, (BLOCK, BLOCK)).T
    seg_row = jnp.concatenate(
        [vecs_ref[part, 9:10].astype(jnp.float32) for part in range(at.tokens)], axis=1
    )
    bias = jnp.concatenate(
        [chip_columns(vecs_ref, at.chip, i, at.core) for i in range(3)], axis=1
    )
    tokens_all = xs_ref[...].reshape(full_len, xs_ref.shape[2])
    proj = (dot_nn(tokens_all, w_ref[...]) + bias).astype(jnp.bfloat16)
    rel = (dot_nn(table_ref[...], w_ref[:, : 2 * group]) + bias[:, : 2 * group]).astype(
        jnp.bfloat16
    )
    rel = dot_nn(turn_matrix(buckets), rel).astype(jnp.bfloat16)
    for slot in range(2):
        lo, hi = slot * DH, (slot + 1) * DH
        q_ref[slot] = proj[:, lo:hi]
        k_ref[slot] = proj[:, group + lo : group + hi]
        v_ref[slot] = proj[:, 2 * group + lo : 2 * group + hi]
        qrev_ref[slot] = rel[:, lo:hi]
        krev_ref[slot] = rel[:, group + lo : group + hi]
    held_ref[...] = jnp.zeros_like(held_ref)
    for slot in range(2):
        ends_ref[slot, 0] = dot_nt(qrev_ref[slot, 0:16], k_ref[slot])
        ends_ref[slot, 1] = dot_nt(qrev_ref[slot, buckets - 16 : buckets], k_ref[slot])

        def key_block(kb, carry):
            rows = k_ref[slot, pl.ds(pl.multiple_of(kb * BLOCK, BLOCK), BLOCK)]
            band = skew_band(dot_nt(rows, qrev_ref[slot]))
            for e in range(band_blocks):
                place_ref[
                    slot,
                    kb + e,
                    :,
                    (band_blocks - 1 - e) * BLOCK : (band_blocks - e) * BLOCK,
                ] = band[:, e * BLOCK : (e + 1) * BLOCK].T
            return carry

        lax.fori_loop(0, blocks, key_block, 0, unroll=8)

    first = at.core * (blocks // 2)

    def unit(u, carry):
        g = u + first
        slot = g // blocks
        qb = g % blocks
        start = pl.multiple_of(qb * BLOCK, BLOCK)
        rows = q_ref[slot, pl.ds(start, BLOCK)]
        own = dot_nt(rows, krev_ref[slot])
        band = skew_band(own) + place_ref[slot, qb + side]
        wide_ref[u % 2, :, pl.ds(start, band_width)] = band
        content = dot_nt(rows, k_ref[slot])
        lane = lax.broadcasted_iota(jnp.int32, (BLOCK, full_len), 1)
        near = jnp.where(
            lane < start - span,
            own[:, 0:1] + ends_ref[slot, 1, 15:16],
            jnp.where(
                lane >= start + band_width - span,
                own[:, buckets - 1 :] + ends_ref[slot, 0, 0:1],
                wide_ref[u % 2, :, span : span + full_len],
            ),
        )
        same = segc_ref[pl.ds(start, BLOCK), 0:1] == seg_row
        scores = jnp.where(same, (content + near) * scale, masked_score)
        highest = jnp.max(scores, axis=-1, keepdims=True)
        exponent = jnp.exp(scores - highest)
        total = jnp.sum(exponent, axis=-1, keepdims=True)
        probs = (exponent / total).astype(jnp.bfloat16)
        p_ref[u] = probs
        held_ref[slot, pl.ds(start, BLOCK)] = dot_nn(probs, v_ref[slot]).astype(jnp.bfloat16)
        return carry

    lax.fori_loop(0, units, unit, 0, unroll=4)
    for part in range(at.tokens):
        rows = slice(part * BLOCK, (part + 1) * BLOCK)
        ctx_ref[part] = jnp.concatenate([held_ref[0, rows], held_ref[1, rows]], axis=1)


def attend(xs, qkvs, tables, vecs):
    tokens, local_len, width = xs.shape
    full_len = tokens * local_len
    buckets = tokens * tables.shape[3]
    blocks = full_len // BLOCK
    units = 3 * blocks // 2
    band_width = buckets + BLOCK
    low, wide = jnp.bfloat16, jnp.float32
    pad_blocks = blocks + band_width // BLOCK - 1
    return pl.pallas_call(
        attend_kernel,
        out_shape=(
            jax.ShapeDtypeStruct((2, full_len, DH), low),
            jax.ShapeDtypeStruct((2, full_len, DH), low),
            jax.ShapeDtypeStruct((2, full_len, DH), low),
            jax.ShapeDtypeStruct((2, buckets, DH), low),
            jax.ShapeDtypeStruct((2, buckets, DH), low),
            jax.ShapeDtypeStruct((units, BLOCK, full_len), low),
            jax.ShapeDtypeStruct((tokens, local_len, 2 * DH), low),
            jax.ShapeDtypeStruct((width, 6 * DH), low),
            jax.ShapeDtypeStruct((buckets, width), low),
        ),
        in_specs=[pl.BlockSpec(memory_space=pltpu.VMEM)] * 4,
        out_specs=[pl.BlockSpec(memory_space=pltpu.VMEM)] * 9,
        scratch_shapes=[
            pltpu.VMEM((full_len, BLOCK), wide),
            pltpu.VMEM((2, pad_blocks, BLOCK, band_width), wide),
            pltpu.VMEM((2, BLOCK, full_len + buckets), wide),
            pltpu.VMEM((2, 2, 16, full_len), wide),
            pltpu.VMEM((2, full_len, DH), low),
        ],
        compiler_params=pltpu.CompilerParams(vmem_limit_bytes=ATTEND_VMEM),
        name="attend",
    )(xs, qkvs, tables, vecs)


def attend_back_kernel(
    q_ref,
    k_ref,
    v_ref,
    qrev_ref,
    krev_ref,
    p_ref,
    mix_ref,
    attn_ref,
    dcat_ref,
    rel_ref,
    sum_ref,
    heads_ref,
    wide_ref,
    low_ref,
    place_ref,
    dq_ref,
    dkt_ref,
    dvt_ref,
    far_ref,
    dkr_ref,
    dqr_ref,
):
    full_len = q_ref.shape[1]
    buckets = qrev_ref.shape[1]
    blocks = full_len // BLOCK
    span = buckets // 2
    side = span // BLOCK
    band_width = buckets + BLOCK
    band_blocks = band_width // BLOCK
    scale = 1.0 / math.sqrt(3.0 * DH)
    units = p_ref.shape[0]
    for ref in (wide_ref, low_ref, place_ref, dq_ref, dkt_ref, dvt_ref, far_ref, dkr_ref, dqr_ref):
        ref[...] = jnp.zeros_like(ref)
    at = Place()
    group = 2 * DH
    first_row = pl.multiple_of((3 * at.chip + at.core) * DH, DH)
    mix_rows = mix_ref[pl.ds(first_row, group)]
    dctx = dot_nt(attn_ref[...].reshape(full_len, attn_ref.shape[2]), mix_rows)
    for slot in range(2):
        heads_ref[slot] = dctx[:, slot * DH : (slot + 1) * DH].astype(jnp.bfloat16)
    first = at.core * (blocks // 2)
    turn = turn_matrix(BLOCK)
    place8 = lax.broadcasted_iota(jnp.int32, (8, full_len), 0)

    def unit(u, carry):
        g = u + first
        slot = g // blocks
        qb = g % blocks
        start = pl.multiple_of(qb * BLOCK, BLOCK)
        rows = q_ref[slot, pl.ds(start, BLOCK)]
        grad = heads_ref[slot, pl.ds(start, BLOCK)]
        probs = p_ref[u]
        wide_probs = probs.astype(jnp.float32)
        prob_grad = dot_nt(grad, v_ref[slot])
        inner = jnp.sum(wide_probs * prob_grad, axis=-1, keepdims=True)
        low_grad = (wide_probs * (prob_grad - inner)).astype(jnp.bfloat16)
        score_grad = low_grad.astype(jnp.float32)
        wide_ref[u % 2, :, span : span + full_len] = dot_nn(turn, low_grad)
        low_ref[u % 2, :, span : span + full_len] = low_grad
        dvt_ref[slot] += dot_tn(grad, probs)
        dkt_ref[slot] += dot_tn(rows, low_grad)
        row = lax.broadcasted_iota(jnp.int32, (BLOCK, full_len), 0)
        lane = lax.broadcasted_iota(jnp.int32, (BLOCK, full_len), 1)
        gap = lane - row - start
        right = jnp.where(gap > span, score_grad, 0.0)
        left = jnp.where(gap < 1 - span, score_grad, 0.0)
        end_right = jnp.sum(right, axis=-1, keepdims=True)
        end_left = jnp.sum(left, axis=-1, keepdims=True)
        far_right = jnp.sum(jnp.where(gap >= span, score_grad, 0.0), axis=0, keepdims=True)
        far_left = jnp.sum(jnp.where(gap < -span, score_grad, 0.0), axis=0, keepdims=True)
        far_ref[slot] += jnp.where(place8 == 0, far_right, jnp.where(place8 == 1, far_left, 0.0))
        band = wide_ref[u % 2, :, pl.ds(start, band_width)]
        near = dot_nn(turn, skew_back(band, buckets).astype(jnp.bfloat16))
        bucket = lax.broadcasted_iota(jnp.int32, (BLOCK, buckets), 1)
        near = near + jnp.where(
            bucket == 0, end_left, jnp.where(bucket == buckets - 1, end_right, 0.0)
        )
        near_low = near.astype(jnp.bfloat16)
        dq = dot_nn(low_grad, k_ref[slot]) + dot_nn(near_low, krev_ref[slot])
        dq_ref[slot, pl.ds(start, BLOCK)] = dq
        dkr_ref[slot] += dot_tn(rows, near_low)
        for e in range(band_blocks):
            keys_at = pl.multiple_of(start + e * BLOCK, BLOCK)
            place_ref[
                slot, qb + e, :, (band_blocks - 1 - e) * BLOCK : (band_blocks - e) * BLOCK
            ] = dot_nt(turn, low_ref[u % 2, :, pl.ds(keys_at, BLOCK)])
        return carry

    lax.fori_loop(0, units, unit, 0, unroll=4)
    parts_q, parts_k, parts_v = [], [], []
    parts_r = [None] * 4
    for slot in range(2):
        far_low = far_ref[slot].astype(jnp.bfloat16)
        mark = lax.broadcasted_iota(jnp.int32, (8, DH), 0)
        ends = jnp.where(
            mark == 0,
            qrev_ref[slot, 0:1].astype(jnp.float32),
            jnp.where(mark == 1, qrev_ref[slot, buckets - 1 : buckets].astype(jnp.float32), 0.0),
        ).astype(jnp.bfloat16)
        end_keys = dot_tn(ends, far_low)
        end_rows = dot_nn(far_low, k_ref[slot])

        whole_k = (dkt_ref[slot] + end_keys).T

        def key_side(kb, carry):
            start = pl.multiple_of(kb * BLOCK, BLOCK)
            far = skew_back(place_ref[slot, kb + side], buckets).astype(jnp.bfloat16)
            far = dot_nn(turn, far).astype(jnp.bfloat16)
            keys = k_ref[slot, pl.ds(start, BLOCK)]
            dqr_ref[slot] += dot_tn(keys, far)
            dq_ref[2 + slot, pl.ds(start, BLOCK)] = dot_nn(far, qrev_ref[slot])
            return carry

        lax.fori_loop(0, blocks, key_side, 0, unroll=8)
        parts_q.append((dq_ref[slot] * scale).astype(jnp.bfloat16))
        parts_k.append(((dq_ref[2 + slot] + whole_k) * scale).astype(jnp.bfloat16))
        parts_v.append(dvt_ref[slot].T.astype(jnp.bfloat16))
        bucket = lax.broadcasted_iota(jnp.int32, (buckets, DH), 0)
        qr = dqr_ref[slot].T + jnp.where(
            bucket == 0, end_rows[0:1], jnp.where(bucket == buckets - 1, end_rows[1:2], 0.0)
        )
        dqr_out = qr * scale
        dkr_out = dkr_ref[slot].T * scale
        parts_r[slot] = dqr_out
        parts_r[2 + slot] = dkr_out
    dcat = jnp.concatenate(parts_q + parts_k + parts_v, axis=1)
    dcat_ref[...] = dcat
    rel = jnp.concatenate(parts_r, axis=1)
    rel_ref[...] = dot_nn(turn_matrix(buckets), rel.astype(jnp.bfloat16)).astype(jnp.bfloat16)
    rel_sum = jnp.sum(rel, axis=0, keepdims=True)
    rel_sum = jnp.concatenate([rel_sum, jnp.zeros((1, 2 * DH), jnp.float32)], axis=1)
    sums = jnp.sum(dcat.astype(jnp.float32), axis=0, keepdims=True) + rel_sum
    sum_ref[...] = jnp.broadcast_to(sums, sum_ref.shape)


MESH = pl.DeviceIdType.MESH
VMEM_SPEC = pl.BlockSpec(memory_space=pltpu.VMEM)
HBM_SPEC = pl.BlockSpec(memory_space=pltpu.HBM)
CHUNKS = 4


class Place:
    def __init__(self):
        self.batches = lax.axis_size("batch")
        self.tokens = lax.axis_size("seq")
        self.chips = self.tokens // 2
        self.row = lax.axis_index("batch")
        self.part = lax.axis_index("seq")
        self.chip = self.part // 2
        self.core = self.part % 2

    def along_chips(self, k):
        chip = lax.rem(self.chip + k, self.chips)
        return chip, (self.row, 2 * chip + self.core)

    def from_chips(self, k):
        return lax.rem(self.chip + self.chips - k, self.chips)

    def partner(self):
        return (self.row, self.part + 1 - 2 * self.core)

    def along_rows(self, k):
        row = lax.rem(self.row + k, self.batches)
        return row, (row, self.part)

    def from_rows(self, k):
        return lax.rem(self.row + self.batches - k, self.batches)

    def along_seq(self, k):
        part = lax.rem(self.part + k, self.tokens)
        return part, (self.row, part)

    def along_plane(self, k):
        index = lax.rem(2 * self.row + self.core + k, 2 * self.batches)
        row, core = index // 2, index % 2
        return row, core, (row, 2 * self.chip + core)

    def chip_peers(self):
        return [self.along_chips(k)[1] for k in range(1, self.chips)]

    def row_peers(self):
        return [self.along_rows(k)[1] for k in range(1, self.batches)]

    def cross_peers(self):
        other = self.part + 1 - 2 * self.core
        return [(self.along_rows(k)[0], other) for k in range(1, self.batches)]

    def cross_row_peers(self):
        return self.row_peers() + self.cross_peers()

    def all_peers(self):
        peers = []
        for i in range(self.batches):
            row = lax.rem(self.row + i, self.batches)
            for j in range(self.tokens):
                if i or j:
                    peers.append((row, lax.rem(self.part + j, self.tokens)))
        return peers

    def seq_peers(self):
        return [self.along_seq(k)[1] for k in range(1, self.tokens)]

    def plane_peers(self):
        return [self.along_plane(k)[2] for k in range(1, 2 * self.batches)]


def meet(peers):
    barrier = pltpu.get_barrier_semaphore()
    for peer in peers:
        pl.semaphore_signal(barrier, inc=1, device_id=peer, device_id_type=MESH)
    pl.semaphore_wait(barrier, len(peers))


class Wires:
    def __init__(self, send_sems, recv_sems, local_sems):
        self.sems = (send_sems, recv_sems, local_sems)
        self.used = [0, 0]
        self.ends = []

    def send(self, src, dst, peer):
        k = self.used[0]
        self.used[0] += 1
        copy = pltpu.make_async_remote_copy(
            src_ref=src,
            dst_ref=dst,
            send_sem=self.sems[0].at[k],
            recv_sem=self.sems[1].at[k],
            device_id=peer,
            device_id_type=MESH,
        )
        copy.start()
        self.ends.append(copy.wait_send)
        return copy

    def local(self, src, dst):
        k = self.used[1]
        self.used[1] += 1
        copy = pltpu.make_async_copy(src, dst, self.sems[2].at[k])
        copy.start()
        return copy

    def finish(self):
        for end in self.ends:
            end()


def wire_scratch(sends, locals_count):
    return [
        pltpu.SemaphoreType.DMA((sends,)),
        pltpu.SemaphoreType.DMA((sends,)),
        pltpu.SemaphoreType.DMA((locals_count,)),
    ]


def comm_call(kernel, name, ident, out_shapes, inputs, sends, locals_count, scratch=(), spec=VMEM_SPEC, limit=None):
    return pl.pallas_call(
        kernel,
        out_shape=tuple(out_shapes),
        in_specs=[spec] * len(inputs),
        out_specs=tuple([VMEM_SPEC] * len(out_shapes)),
        scratch_shapes=list(scratch) + wire_scratch(sends, locals_count),
        compiler_params=pltpu.CompilerParams(
            collective_id=ident, has_side_effects=True, vmem_limit_bytes=limit or COMM_VMEM
        ),
        name=name,
    )(*inputs)


def like(array, *lead):
    return jax.ShapeDtypeStruct(tuple(lead) + tuple(array.shape), array.dtype)


def pick(values, index):
    out = jnp.int32(values[0])
    for i in range(1, len(values)):
        out = jnp.where(index == i, jnp.int32(values[i]), out)
    return out


def arrival_order(at):
    chips = range(at.chips)
    lists = [sorted((j for j in chips if j != z), key=lambda j: (abs(j - z), j)) for z in chips]
    return [pick([lists[z][t] for z in chips], at.chip) for t in range(at.chips - 1)]


def return_order(at):
    chips = range(at.chips)

    def away(j, z):
        end = at.chips - 1 if j < z else 0
        return (abs(j - end) + abs(end - z), j)

    lists = [sorted((j for j in chips if j != z), key=lambda j: away(j, z)) for z in chips]
    return [pick([lists[z][t] for z in chips], at.chip) for t in range(at.chips - 1)]


def far_order(at):
    chips = range(at.chips)
    lists = [sorted((j for j in chips if j != z), key=lambda j: (-abs(j - z), j)) for z in chips]
    return [pick([lists[z][t] for z in chips], at.chip) for t in range(at.chips - 1)]


def goes_on(at, j):
    above = jnp.logical_and(j < at.chip, at.chip < at.chips - 1)
    below = jnp.logical_and(j > at.chip, at.chip > 0)
    return jnp.logical_or(above, below)


def line_peer(at, step):
    return (at.row, 2 * (at.chip + step) + at.core)


class LineGather:
    def __init__(self, at, buf, slot, sems, own=None):
        self.at, self.buf, self.slot, self.own = at, buf, slot, own
        self.send_sems, self.recv_sems = sems
        self.rows = buf.shape[1] // CHUNKS

    def copy(self, j, h, step, k, own=False):
        window = pl.ds(h * self.rows, self.rows)
        home = self.buf.at[self.slot(j), window]
        src = self.own.at[window] if own and self.own is not None else home
        return pltpu.make_async_remote_copy(
            src_ref=src,
            dst_ref=home,
            send_sem=self.send_sems.at[k * CHUNKS + h],
            recv_sem=self.recv_sems.at[j * CHUNKS + h],
            device_id=line_peer(self.at, step),
            device_id_type=MESH,
        )

    def own_each(self, act):
        z, n = self.at.chip, self.at.chips
        for h in range(CHUNKS):

            @pl.when(z < n - 1)
            def _():
                act(self.copy(z, h, 1, z, own=True))

            @pl.when(z > 0)
            def _():
                act(self.copy(z, h, -1, n, own=True))

    def start(self):
        self.own_each(lambda copy: copy.start())

    def arrive(self, j):
        step = jnp.where(j < self.at.chip, 1, -1)
        for h in range(CHUNKS):
            self.copy(j, h, -step, j).wait_recv()

            @pl.when(goes_on(self.at, j))
            def _():
                self.copy(j, h, step, j).start()

    def drain(self, order):
        self.own_each(lambda copy: copy.wait_send())
        for j in order:
            step = jnp.where(j < self.at.chip, 1, -1)

            @pl.when(goes_on(self.at, j))
            def _():
                for h in range(CHUNKS):
                    self.copy(j, h, step, j).wait_send()


class LineReduce:
    def __init__(self, at, part, got, sems):
        self.at, self.part, self.got = at, part, got
        self.send_sems, self.recv_sems = sems
        self.rows = part.shape[1] // CHUNKS

    def copy(self, j, h):
        z, n = self.at.chip, self.at.chips
        window = pl.ds(h * self.rows, self.rows)
        slot = jnp.where(z + 1 == j, n, j)
        return pltpu.make_async_remote_copy(
            src_ref=self.part.at[j, window],
            dst_ref=self.got.at[slot, window],
            send_sem=self.send_sems.at[j * CHUNKS + h],
            recv_sem=self.recv_sems.at[slot * CHUNKS + h],
            device_id=line_peer(self.at, jnp.where(j < z, -1, 1)),
            device_id_type=MESH,
        )

    def landed(self, slot, h, step):
        window = pl.ds(h * self.rows, self.rows)
        return pltpu.make_async_remote_copy(
            src_ref=self.got.at[slot, window],
            dst_ref=self.got.at[slot, window],
            send_sem=self.send_sems.at[h],
            recv_sem=self.recv_sems.at[slot * CHUNKS + h],
            device_id=line_peer(self.at, step),
            device_id_type=MESH,
        )

    def send(self, j):
        for h in range(CHUNKS):
            self.copy(j, h).start()

    def send_last(self, j):
        @pl.when(jnp.logical_not(goes_on(self.at, j)))
        def _():
            self.send(j)

    def pass_on(self, order):
        z, n = self.at.chip, self.at.chips
        wide = jnp.float32

        @pl.when(jnp.logical_and(z > 0, z < n - 1))
        def _():
            for j in order:
                step = jnp.where(j < z, 1, -1)
                for h in range(CHUNKS):
                    self.landed(j, h, step).wait_recv()
                    window = pl.ds(h * self.rows, self.rows)
                    total = self.part[j, window].astype(wide) + self.got[j, window].astype(wide)
                    self.part[j, window] = total.astype(self.part.dtype)
                    self.copy(j, h).start()

    def clear(self):
        z, n = self.at.chip, self.at.chips

        @pl.when(z == n - 1)
        def _():
            self.got[z] = jnp.zeros(self.got.shape[1:], self.got.dtype)

        @pl.when(z == 0)
        def _():
            self.got[n] = jnp.zeros(self.got.shape[1:], self.got.dtype)

    def collect(self):
        z, n = self.at.chip, self.at.chips
        for h in range(CHUNKS):

            @pl.when(z < n - 1)
            def _():
                self.landed(z, h, 1).wait_recv()

            @pl.when(z > 0)
            def _():
                self.landed(n, h, -1).wait_recv()

        return self.got[z].astype(jnp.float32) + self.got[n].astype(jnp.float32)

    def drain(self, order):
        for j in order:
            for h in range(CHUNKS):
                self.copy(j, h).wait_send()


def gather_sems(chips):
    return [
        pltpu.SemaphoreType.DMA(((chips + 1) * CHUNKS,)),
        pltpu.SemaphoreType.DMA((chips * CHUNKS,)),
    ]


def reduce_sems(chips):
    return [
        pltpu.SemaphoreType.DMA((chips * CHUNKS,)),
        pltpu.SemaphoreType.DMA(((chips + 1) * CHUNKS,)),
    ]


def gather_kernel(
    x_ref, wq_ref, wk_ref, wv_ref, mix_ref, table_ref, vec_ref, up_ref, down_ref,
    xs_ref, qkvs_ref, mixs_ref, tables_ref, vecs_ref, up2_ref, down2_ref,
    line_send, line_recv, *sems,
):
    at = Place()
    wires = Wires(*sems)
    b, s, z, c = at.row, at.part, at.chip, at.core
    off_diagonal = b != z
    turned = (z, 2 * b + c)
    peers = at.seq_peers() + at.row_peers()
    barrier = pltpu.get_barrier_semaphore()
    for peer in peers:
        pl.semaphore_signal(barrier, inc=1, device_id=peer, device_id_type=MESH)

    @pl.when(off_diagonal)
    def _():
        pl.semaphore_signal(barrier, inc=1, device_id=turned, device_id_type=MESH)

    pl.semaphore_wait(barrier, len(peers) + off_diagonal.astype(jnp.int32))

    swaps, stays = [], []
    for i, ref in enumerate((wq_ref, wk_ref, wv_ref)):
        k = wires.used[0]
        wires.used[0] += 1
        swaps.append(
            pltpu.make_async_remote_copy(
                src_ref=ref,
                dst_ref=qkvs_ref.at[2 * z + c, i],
                send_sem=sems[0].at[k],
                recv_sem=sems[1].at[k],
                device_id=turned,
                device_id_type=MESH,
            )
        )
        stays.append(pltpu.make_async_copy(ref, qkvs_ref.at[2 * b + c, i], sems[2].at[i]))
        wires.used[1] += 1

    @pl.when(off_diagonal)
    def _():
        for swap in swaps:
            swap.start()

    @pl.when(jnp.logical_not(off_diagonal))
    def _():
        for stay in stays:
            stay.start()

    table_home = tables_ref.at[c, b, z]
    mix_home = mixs_ref.at[c, b, z]
    table_sends = [
        wires.send(table_ref, table_home, at.along_chips(k)[1]) for k in range(1, at.chips)
    ]
    kept = [wires.local(table_ref, table_home), wires.local(mix_ref, mix_home)]
    line = LineGather(at, xs_ref, lambda j: 2 * j + c, (line_send, line_recv), own=x_ref)
    line.start()
    last = [wires.send(vec_ref, vecs_ref.at[s], at.along_seq(k)[1]) for k in range(1, at.tokens)]
    mix_sends = [
        wires.send(mix_ref, mix_home, at.along_chips(k)[1]) for k in range(1, at.chips)
    ]
    last += [
        wires.send(x_ref, xs_ref.at[s], at.partner()),
        wires.send(up_ref, up2_ref, at.partner()),
        wires.send(down_ref, down2_ref, at.partner()),
    ]
    own = [
        wires.local(x_ref, xs_ref.at[s]),
        wires.local(vec_ref, vecs_ref.at[s]),
    ]

    @pl.when(off_diagonal)
    def _():
        for swap in swaps:
            swap.wait_recv()

    @pl.when(jnp.logical_not(off_diagonal))
    def _():
        for stay in stays:
            stay.wait()

    mine = qkvs_ref.at[2 * b + c]
    qkv_sends = [wires.send(mine, mine, at.along_rows(k)[1]) for k in range(1, at.batches)]
    last.append(wires.send(mine, mine, at.partner()))
    for copy in table_sends:
        copy.wait_recv()
    for copy in kept:
        copy.wait()
    mine = tables_ref.at[c, b]
    row_sends = [wires.send(mine, mine, at.along_rows(k)[1]) for k in range(1, at.batches)]
    last.append(wires.send(mine, mine, at.partner()))
    order = arrival_order(at)

    def arrived(j):
        line.arrive(j)
        home = xs_ref.at[2 * j + c]
        last.append(wires.send(home, home, at.partner()))

    arrived(order[0])
    for copy in mix_sends:
        copy.wait_recv()
    mine = mixs_ref.at[c, b]
    mix_rows = [wires.send(mine, mine, at.along_rows(k)[1]) for k in range(1, at.batches)]
    last.append(wires.send(mine, mine, at.partner()))
    arrived(order[1])
    for k in range(1, at.batches):
        qkv_sends[k - 1].wait_recv()
        home = qkvs_ref.at[2 * at.from_rows(k) + c]
        last.append(wires.send(home, home, at.partner()))
    for k in range(1, at.batches):
        row_sends[k - 1].wait_recv()
        home = tables_ref.at[c, at.from_rows(k)]
        last.append(wires.send(home, home, at.partner()))
    for j in order[2:]:
        arrived(j)
    for k in range(1, at.batches):
        mix_rows[k - 1].wait_recv()
        home = mixs_ref.at[c, at.from_rows(k)]
        last.append(wires.send(home, home, at.partner()))
    for copy in last:
        copy.wait_recv()
    for copy in own:
        copy.wait()
    wires.finish()
    line.drain(order)

    @pl.when(off_diagonal)
    def _():
        for swap in swaps:
            swap.wait_send()


def gather_inputs(x, w_query, w_key, w_value, w_mix, rel_table, vec, up, down):
    tokens, batches = lax.axis_size("seq"), lax.axis_size("batch")
    chips = tokens // 2
    outs = (
        like(x, tokens),
        like(w_query, tokens, 3),
        like(w_mix, 2, batches, chips),
        like(rel_table, 2, batches, chips),
        like(vec, tokens),
        like(up),
        like(down),
    )
    sends = 3 + 2 * (chips - 1) + tokens - 1 + 3 + 6 * (batches - 1) + 3 + chips - 1
    inputs = (x, w_query, w_key, w_value, w_mix, rel_table, vec, up, down)
    return comm_call(
        gather_kernel,
        "gather_inputs",
        0,
        outs,
        inputs,
        sends,
        7,
        scratch=gather_sems(chips),
        spec=HBM_SPEC,
    )


def norm_parts(values):
    average = jnp.mean(values, axis=-1, keepdims=True)
    centered = values - average
    variance = jnp.mean(centered * centered, axis=-1, keepdims=True)
    scale = lax.rsqrt(variance + norm_eps)
    return centered * scale, scale


def norm_back(grad, gain, unit, scale):
    inner = grad * gain
    mean = jnp.mean(inner, axis=-1, keepdims=True)
    slope = jnp.mean(inner * unit, axis=-1, keepdims=True)
    return scale * (inner - mean - unit * slope)


def line_pass(gather, reduce, order, work, after=None):
    for j in order:
        gather.arrive(j)
        work(j)
        reduce.send_last(j)
        if after is not None:
            after(j)


def feed_kernel(
    ctx_ref, x_ref, mixs_ref, vecs_ref, up_ref, down_ref, up2_ref, down2_ref, out_grad_ref,
    output_ref, pre_grad_ref, sums_ref, attn_ref, mix_ref, ups_ref, downs_ref, upbs_ref,
    got_ref, hid_ref, act_ref, slope_ref, part_ref, ffn_ref, grad_ref, inner_ref,
    back_ref, backs_ref, up_acc_ref, down_acc_ref, up_away_ref, down_away_ref, upb_away_ref,
    up_got_ref, down_got_ref, upb_got_ref, upg_ref, downg_ref, upb_ref, vec_ref,
    hid_send, hid_recv, ffn_send, ffn_recv, grad_send, grad_recv, back_send, back_recv,
    attn_send, attn_recv, *sems,
):
    at = Place()
    wires = Wires(*sems)
    low, wide = jnp.bfloat16, jnp.float32
    b, s, z, c = at.row, at.part, at.chip, at.core
    order, returns = arrival_order(at), return_order(at)
    meet(at.seq_peers() + at.row_peers())
    last, own = [], []
    swaps = []
    for k in range(1, at.tokens):
        part, peer = at.along_seq(k)
        swaps.append(wires.send(ctx_ref.at[part], got_ref.at[s], peer))
    kept = wires.local(ctx_ref.at[s], got_ref.at[s])
    lanes = x_ref.shape[1] // at.tokens
    hidden_here = up_ref.shape[1]
    vec_ref[...] = jnp.concatenate(
        [vecs_ref[part, :, :lanes].astype(wide) for part in range(at.tokens)], axis=1
    )
    bias3 = vec_ref[3:4]
    gain1, gain2 = vec_ref[4:5], vec_ref[5:6]
    shift1, shift2 = vec_ref[6:7], vec_ref[7:8]
    bias_down = vec_ref[8:9]
    partner = s + 1 - 2 * c
    up_rows = hidden_here // BLOCK
    bias_up = jnp.concatenate(
        [vecs_ref[s, 10 + i : 11 + i].astype(wide) for i in range(up_rows)]
        + [vecs_ref[partner, 10 + i : 11 + i].astype(wide) for i in range(up_rows)],
        axis=1,
    )
    shard_rows = mixs_ref.shape[3]
    for part in range(at.tokens):
        mix_ref[part * shard_rows : (part + 1) * shard_rows] = jnp.concatenate(
            [mixs_ref[part % 2, row, part // 2] for row in range(at.batches)], axis=1
        )
    for copy in swaps:
        copy.wait_recv()
    kept.wait()
    pieces = []
    for chip in range(at.chips):
        left, right = got_ref[2 * chip], got_ref[2 * chip + 1]
        middle = left[:, DH:].astype(wide) + right[:, :DH].astype(wide)
        pieces += [left[:, :DH], middle.astype(low), right[:, DH:]]
    context = jnp.concatenate(pieces, axis=1)
    pre_norm = x_ref[...].astype(wide) + dot_nn(context, mix_ref[...]) + bias3
    unit1, scale1 = norm_parts(pre_norm)
    hidden = unit1 * gain1 + shift1
    hid_ref[z] = hidden.astype(low)
    hid_line = LineGather(at, hid_ref, lambda j: j, (hid_send, hid_recv))
    ffn_line = LineReduce(at, part_ref, ffn_ref, (ffn_send, ffn_recv))
    hid_line.start()
    ffn_line.clear()

    def ffn(chip):
        rows = hid_ref[chip]
        inner = jnp.concatenate(
            [dot_nn(rows, up_ref[...]), dot_nn(rows, up2_ref[...])], axis=1
        )
        inner = inner + bias_up
        cdf = 0.5 * (1.0 + lax.erf(inner * math.sqrt(0.5)))
        act = (inner * cdf).astype(low)
        slope_ref[chip] = cdf + inner * (
            jnp.exp(-0.5 * inner * inner) * (1.0 / math.sqrt(2.0 * math.pi))
        )
        act_ref[chip] = act
        part_ref[chip] = (
            dot_nn(act[:, :hidden_here], down_ref[...])
            + dot_nn(act[:, hidden_here:], down2_ref[...])
        ).astype(low)

    ffn(z)
    line_pass(hid_line, ffn_line, order, ffn)
    ffn_line.pass_on(returns)
    total = part_ref[z].astype(wide) + ffn_line.collect()
    mixed = hidden + total + bias_down
    unit2, scale2 = norm_parts(mixed)
    output_ref[...] = (unit2 * gain2 + shift2).astype(low)
    out_grad = out_grad_ref[...].astype(wide)
    mixed_grad = norm_back(out_grad, gain2, unit2, scale2)
    grad_ref[z] = mixed_grad.astype(low)
    grad_line = LineGather(at, grad_ref, lambda j: j, (grad_send, grad_recv))
    back_line = LineReduce(at, back_ref, backs_ref, (back_send, back_recv))
    grad_line.start()
    back_line.clear()
    gain2_grad = jnp.sum(out_grad * unit2, axis=0, keepdims=True)
    shift2_grad = jnp.sum(out_grad, axis=0, keepdims=True)
    downb_grad = jnp.sum(mixed_grad, axis=0, keepdims=True)

    def back(chip):
        rows = grad_ref[chip]
        act_grad = jnp.concatenate(
            [dot_nt(rows, down_ref[...]), dot_nt(rows, down2_ref[...])], axis=1
        )
        inner_low = (act_grad * slope_ref[chip]).astype(low)
        inner_ref[chip] = inner_low
        back_ref[chip] = (
            dot_nt(inner_low[:, :hidden_here], up_ref[...])
            + dot_nt(inner_low[:, hidden_here:], up2_ref[...])
        ).astype(low)

    def weight_grads(chip):
        up_acc_ref[...] += dot_tn(hid_ref[chip], inner_ref[chip])
        down_acc_ref[...] += dot_tn(grad_ref[chip], act_ref[chip])

    back(z)
    up_acc_ref[...] = dot_tn(hid_ref[z], inner_ref[z])
    down_acc_ref[...] = dot_tn(grad_ref[z], act_ref[z])
    line_pass(grad_line, back_line, order, back, weight_grads)
    width = x_ref.shape[1]
    columns = width // at.batches
    inner_all = inner_ref[...].reshape(at.chips * BLOCK, 2 * hidden_here)
    near, away = slice(0, hidden_here), slice(hidden_here, 2 * hidden_here)
    up_away_ref[...] = up_acc_ref[:, away].astype(low)
    down_away_ref[...] = down_acc_ref[:, away].astype(low)
    upb_grad = jnp.sum(inner_all.astype(wide), axis=0, keepdims=True)
    upb_away_ref[...] = jnp.broadcast_to(upb_grad[:, away], upb_away_ref.shape)
    halves = [
        wires.send(up_away_ref, up_got_ref, at.partner()),
        wires.send(down_away_ref, down_got_ref, at.partner()),
        wires.send(upb_away_ref, upb_got_ref, at.partner()),
    ]
    back_line.pass_on(returns)
    for copy in halves:
        copy.wait_recv()
    upb_ref[...] = jnp.broadcast_to(upb_grad[:, near], upb_ref.shape) + upb_got_ref[...]
    up_sum = (up_acc_ref[:, near] + up_got_ref[...].astype(wide)).astype(low)
    down_sum = (down_acc_ref[:, near] + down_got_ref[...].astype(wide)).astype(low)
    for row in range(at.batches):
        upg_ref[row] = up_sum[row * columns : (row + 1) * columns]
        downg_ref[row] = down_sum[row * columns : (row + 1) * columns]
    for k in range(1, at.batches):
        row, peer = at.along_rows(k)
        last.append(wires.send(upg_ref.at[row], ups_ref.at[b], peer))
        last.append(wires.send(downg_ref.at[row], downs_ref.at[b], peer))
        last.append(wires.send(upb_ref, upbs_ref.at[b], peer))
    own.append(wires.local(upg_ref.at[b], ups_ref.at[b]))
    own.append(wires.local(downg_ref.at[b], downs_ref.at[b]))
    own.append(wires.local(upb_ref, upbs_ref.at[b]))
    total = back_ref[z].astype(wide) + back_line.collect()
    hidden_grad = mixed_grad + total
    pre_grad = norm_back(hidden_grad, gain1, unit1, scale1)
    attn_ref[s] = pre_grad.astype(low)
    attn_line = LineGather(at, attn_ref, lambda j: 2 * j + c, (attn_send, attn_recv))
    attn_line.start()
    last.append(wires.send(attn_ref.at[s], attn_ref.at[s], at.partner()))
    pre_grad_ref[...] = pre_grad
    gain1_grad = jnp.sum(hidden_grad * unit1, axis=0, keepdims=True)
    shift1_grad = jnp.sum(hidden_grad, axis=0, keepdims=True)
    bias3_grad = jnp.sum(pre_grad, axis=0, keepdims=True)
    sums = jnp.concatenate(
        [bias3_grad, gain1_grad, gain2_grad, shift1_grad, shift2_grad, downb_grad]
        + [jnp.zeros((2, width), wide)],
        axis=0,
    )
    spare = jnp.zeros((8, BLOCK - lanes), wide)
    for part in range(at.tokens):
        sums_ref[part] = jnp.concatenate(
            [sums[:, part * lanes : (part + 1) * lanes], spare], axis=1
        )
    for j in order:
        attn_line.arrive(j)
        home = attn_ref.at[2 * j + c]
        last.append(wires.send(home, home, at.partner()))
    for copy in last:
        copy.wait_recv()
    for copy in own:
        copy.wait()
    wires.finish()
    for line in (hid_line, ffn_line, grad_line, back_line, attn_line):
        line.drain(order)


def feed_forward(ctx, x, mixs, vecs, up, down, up2, down2, out_grad, ident):
    tokens, batches = lax.axis_size("seq"), lax.axis_size("batch")
    chips = tokens // 2
    width = x.shape[1]
    columns = width // batches
    hidden_here = up.shape[1]
    low, wide = jnp.bfloat16, jnp.float32
    outs = (
        jax.ShapeDtypeStruct(x.shape, low),
        jax.ShapeDtypeStruct(x.shape, wide),
        jax.ShapeDtypeStruct((tokens, 8, BLOCK), wide),
        jax.ShapeDtypeStruct((tokens,) + x.shape, low),
        jax.ShapeDtypeStruct((width, width), low),
        jax.ShapeDtypeStruct((batches, columns, hidden_here), low),
        jax.ShapeDtypeStruct((batches, columns, hidden_here), low),
        jax.ShapeDtypeStruct((batches, 8, hidden_here), wide),
    )
    block = (chips,) + x.shape
    wide_block = (chips, x.shape[0], 2 * hidden_here)
    slots = (chips + 1,) + x.shape
    up_half, bias_half = (width, hidden_here), (8, hidden_here)
    down_half = up_half
    scratch = [
        pltpu.VMEM(ctx.shape, low),
        pltpu.VMEM(block, low),
        pltpu.VMEM(wide_block, low),
        pltpu.VMEM(wide_block, wide),
        pltpu.VMEM(block, low),
        pltpu.VMEM(slots, low),
        pltpu.VMEM(block, low),
        pltpu.VMEM(wide_block, low),
        pltpu.VMEM(block, low),
        pltpu.VMEM(slots, low),
        pltpu.VMEM((width, 2 * hidden_here), wide),
        pltpu.VMEM((width, 2 * hidden_here), wide),
        pltpu.VMEM(up_half, low),
        pltpu.VMEM(down_half, low),
        pltpu.VMEM(bias_half, wide),
        pltpu.VMEM(up_half, low),
        pltpu.VMEM(down_half, low),
        pltpu.VMEM(bias_half, wide),
        pltpu.VMEM((batches, columns, hidden_here), low),
        pltpu.VMEM((batches, columns, hidden_here), low),
        pltpu.VMEM(bias_half, wide),
        pltpu.VMEM((16, width), wide),
    ]
    scratch += (gather_sems(chips) + reduce_sems(chips)) * 2 + gather_sems(chips)
    inputs = (ctx, x, mixs, vecs, up, down, up2, down2, out_grad)
    sends = tokens - 1 + 2 * batches - 1 + 3 + 3 * (batches - 1) + chips
    return pl.pallas_call(
        feed_kernel,
        out_shape=outs,
        in_specs=[VMEM_SPEC] * len(inputs),
        out_specs=(VMEM_SPEC,) * len(outs),
        scratch_shapes=scratch + wire_scratch(sends, 5),
        compiler_params=pltpu.CompilerParams(
            collective_id=ident, has_side_effects=True, vmem_limit_bytes=FEED_VMEM
        ),
        name="feed_forward",
    )(*inputs)


def settle_kernel(
    q_ref, k_ref, v_ref, qrev_ref, krev_ref, p_ref, mix_all_rows_ref,
    vec_ref, w_ref, xs_ref, table_ref, ctx_ref, attn_ref,
    ins_ref, vec_all_ref, cols_ref, dw_all_ref, tab_all_ref, mix_all_ref,
    in_ref, dw_ref, tab_ref, mix_ref, half_ref, sum_ref, got_ref, vecs_ref, vec_low_ref,
    dws_ref, dw_low_ref, rels_ref, rel_low_ref, mixs_ref, mix_low_ref,
    dcat_ref, rel_ref, col_ref, heads_ref, wide_ref, low_ref, place_ref, dq_ref, dkt_ref,
    dvt_ref, far_ref, dkr_ref, dqr_ref,
    line_send, line_recv, tab_send, tab_recv, *sems,
):
    at = Place()
    wires = Wires(*sems)
    low, wide = jnp.bfloat16, jnp.float32
    b, s, z, c = at.row, at.part, at.chip, at.core
    off_diagonal = b != z
    same, cross = (z, 2 * b + c), (z, 2 * b + 1 - c)
    peers = at.all_peers()
    barrier = pltpu.get_barrier_semaphore()
    for peer in peers:
        pl.semaphore_signal(barrier, inc=1, device_id=peer, device_id_type=MESH)
    attend_back_kernel(
        q_ref, k_ref, v_ref, qrev_ref, krev_ref, p_ref, mix_all_rows_ref, attn_ref,
        dcat_ref, rel_ref, col_ref, heads_ref, wide_ref, low_ref, place_ref, dq_ref, dkt_ref,
        dvt_ref, far_ref, dkr_ref, dqr_ref,
    )
    pl.semaphore_wait(barrier, len(peers))
    width = w_ref.shape[0]
    columns = width // at.batches
    full_len = dcat_ref.shape[0]
    group = 2 * DH
    buckets = table_ref.shape[0]
    bucket_rows = buckets // at.batches

    dw_sends, mix_sends, vec_sends, rel_sends, last, own = [], [], [], [], [], []
    for k in range(1, at.batches):
        row, peer = at.along_rows(k)
        rows = pl.ds(pl.multiple_of(row * bucket_rows, bucket_rows), bucket_rows)
        rel_sends.append(wires.send(rel_ref.at[rows], rels_ref.at[k - 1], peer))

    for k in range(1, at.tokens):
        part, peer = at.along_seq(k)
        vec_sends.append(wires.send(vec_ref.at[part], vecs_ref.at[k - 1], peer))
    mine = 2 * b + c
    for k in range(1, 2 * at.batches):
        last.append(wires.send(col_ref, cols_ref.at[mine], at.along_plane(k)[2]))
    own.append(wires.local(col_ref, cols_ref.at[mine]))

    def input_part(chip, core):
        start = pl.multiple_of((2 * chip + core) * BLOCK, BLOCK)
        in_ref[chip, core] = dot_nt(dcat_ref[pl.ds(start, BLOCK)], w_ref[...]).astype(low)

    order = far_order(at)
    places = order + [z]
    halves = []
    for chip in places:
        input_part(chip, 1 - c)
        halves.append(wires.send(in_ref.at[chip, 1 - c], half_ref.at[chip], at.partner()))
    line = LineReduce(at, sum_ref, got_ref, (line_send, line_recv))
    line.clear()
    for i, chip in enumerate(places):
        input_part(chip, c)
        halves[i].wait_recv()
        total = in_ref[chip, c].astype(wide) + half_ref[chip].astype(wide)
        sum_ref[chip] = total.astype(low)
        if i < len(order):
            line.send_last(chip)

    whole = xs_ref[...].reshape(full_len, width)
    dw = dot_tn(whole, dcat_ref[...])
    dw_rel = dot_tn(table_ref[...], rel_ref[...])
    dw = jnp.concatenate([dw[:, : 2 * group] + dw_rel, dw[:, 2 * group :]], axis=1)
    for row in range(at.batches):
        dw_ref[row] = dw[row * columns : (row + 1) * columns].astype(low)
    for k in range(1, at.batches):
        row, peer = at.along_rows(k)
        dw_sends.append(wires.send(dw_ref.at[row], dws_ref.at[k - 1], peer))

    rows = pl.ds(pl.multiple_of(b * bucket_rows, bucket_rows), bucket_rows)
    total = rel_ref[rows].astype(wide)
    for k in range(1, at.batches):
        rel_sends[k - 1].wait_recv()
        total = total + rels_ref[k - 1].astype(wide)
    rel_low_ref[...] = total.astype(low)
    table_rows = bucket_rows // 2
    for row in range(at.batches):
        piece = dot_nt(rel_low_ref[...], w_ref[row * columns : (row + 1) * columns, : 2 * group])
        for core in range(2):
            tab_ref[core, row] = piece[core * table_rows : (core + 1) * table_rows].astype(low)

    def tab_copy(k, d):
        row = lax.rem(b + k, at.batches)
        core = jnp.where(d == 0, c, 1 - c)
        return pltpu.make_async_remote_copy(
            src_ref=tab_ref.at[core, row],
            dst_ref=tab_all_ref.at[s],
            send_sem=tab_send.at[2 * k + d],
            recv_sem=tab_recv.at[s],
            device_id=(row, 2 * b + core),
            device_id_type=MESH,
        )

    tab_stay = pltpu.make_async_copy(
        tab_ref.at[c, b], tab_all_ref.at[s], sems[2].at[wires.used[1]]
    )
    wires.used[1] += 1
    for k in range(at.batches):
        for d in range(2):
            if k or d:
                tab_copy(k, d).start()

    @pl.when(off_diagonal)
    def _():
        tab_copy(0, 0).start()

    @pl.when(jnp.logical_not(off_diagonal))
    def _():
        tab_stay.start()

    line.pass_on(order[:1])
    mix = dot_tn(
        ctx_ref[...].reshape(full_len, group), attn_ref[...].reshape(full_len, width)
    )
    for row in range(at.batches):
        mix_ref[row] = mix[:, row * columns : (row + 1) * columns].astype(low)
    for k in range(1, at.batches):
        row, peer = at.along_rows(k)
        mix_sends.append(wires.send(mix_ref.at[row], mixs_ref.at[k - 1], peer))

    line.pass_on(order[1:2])
    total = dw_ref[b].astype(wide)
    for k in range(1, at.batches):
        dw_sends[k - 1].wait_recv()
        total = total + dws_ref[k - 1].astype(wide)
    shard_rows = dw_low_ref.shape[1]
    for half in range(2):
        dw_low_ref[half] = total[half * shard_rows : (half + 1) * shard_rows].astype(low)
    k = wires.used[0]
    wires.used[0] += 1
    move = pltpu.make_async_remote_copy(
        src_ref=dw_low_ref.at[c],
        dst_ref=dw_all_ref.at[c],
        send_sem=sems[0].at[k],
        recv_sem=sems[1].at[k],
        device_id=same,
        device_id_type=MESH,
    )
    stay = pltpu.make_async_copy(
        dw_low_ref.at[c], dw_all_ref.at[c], sems[2].at[wires.used[1]]
    )
    wires.used[1] += 1

    @pl.when(off_diagonal)
    def _():
        move.start()

    @pl.when(jnp.logical_not(off_diagonal))
    def _():
        stay.start()

    last.append(wires.send(dw_low_ref.at[1 - c], dw_all_ref.at[c], cross))

    line.pass_on(order[2:])
    total = mix_ref[b].astype(wide)
    for k in range(1, at.batches):
        mix_sends[k - 1].wait_recv()
        total = total + mixs_ref[k - 1].astype(wide)
    mix_low_ref[...] = total.astype(low)
    last.append(wires.send(mix_low_ref, mix_all_ref.at[c], at.partner()))
    own.append(wires.local(mix_low_ref, mix_all_ref.at[c]))

    total = vec_ref[s]
    for k in range(1, at.tokens):
        vec_sends[k - 1].wait_recv()
        total = total + vecs_ref[k - 1]
    vec_low_ref[...] = total
    for k in range(1, at.batches):
        last.append(wires.send(vec_low_ref, vec_all_ref.at[b], at.along_rows(k)[1]))
    own.append(wires.local(vec_low_ref, vec_all_ref.at[b]))

    ins_ref[...] = sum_ref[z].astype(wide) + line.collect()
    for copy in last:
        copy.wait_recv()
    for copy in own:
        copy.wait()
    wires.finish()
    line.drain(order)
    for part in range(at.tokens):
        landed = pltpu.make_async_remote_copy(
            src_ref=tab_all_ref.at[part],
            dst_ref=tab_all_ref.at[part],
            send_sem=tab_send.at[0],
            recv_sem=tab_recv.at[part],
            device_id=at.partner(),
            device_id_type=MESH,
        )

        @pl.when(jnp.logical_or(off_diagonal, s != part))
        def _():
            landed.wait_recv()

    for k in range(at.batches):
        for d in range(2):
            if k or d:
                tab_copy(k, d).wait_send()

    @pl.when(off_diagonal)
    def _():
        tab_copy(0, 0).wait_send()
        move.wait()

    @pl.when(jnp.logical_not(off_diagonal))
    def _():
        tab_stay.wait()
        stay.wait()


def settle_grads(q, k, v, qrev, krev, probs, m_mix, vec, w_cat, xs, table, ctx, attn_all, ident):
    tokens, batches = lax.axis_size("seq"), lax.axis_size("batch")
    chips = tokens // 2
    low, wide = jnp.bfloat16, jnp.float32
    local_len, width = xs.shape[1:]
    columns, group = width // batches, 6 * DH
    buckets = table.shape[0]
    full_len = tokens * local_len
    band_width = buckets + BLOCK
    pad_blocks = full_len // BLOCK + band_width // BLOCK - 1
    half = (chips, local_len, width)
    dw_pieces = (2, columns // 2, group)
    mix_piece = (2 * DH, columns)
    dw_piece, rel_piece = (columns, group), (buckets // batches, 4 * DH)
    outs = (
        jax.ShapeDtypeStruct((local_len, width), wide),
        jax.ShapeDtypeStruct((batches,) + vec.shape[1:], wide),
        jax.ShapeDtypeStruct((2 * batches, 8, group), wide),
        jax.ShapeDtypeStruct(dw_pieces, low),
        jax.ShapeDtypeStruct((tokens, buckets // tokens, columns), low),
        jax.ShapeDtypeStruct((2,) + mix_piece, low),
    )
    scratch = [
        pltpu.VMEM((chips, 2, local_len, width), low),
        pltpu.VMEM((batches,) + dw_piece, low),
        pltpu.VMEM((2, batches, buckets // tokens, columns), low),
        pltpu.VMEM((batches,) + mix_piece, low),
        pltpu.VMEM(half, low),
        pltpu.VMEM(half, low),
        pltpu.VMEM((chips + 1, local_len, width), low),
        pltpu.VMEM((tokens - 1,) + vec.shape[1:], wide),
        pltpu.VMEM(vec.shape[1:], wide),
        pltpu.VMEM((batches - 1,) + dw_piece, low),
        pltpu.VMEM(dw_pieces, low),
        pltpu.VMEM((batches - 1,) + rel_piece, low),
        pltpu.VMEM(rel_piece, low),
        pltpu.VMEM((batches - 1,) + mix_piece, low),
        pltpu.VMEM(mix_piece, low),
        pltpu.VMEM((full_len, group), low),
        pltpu.VMEM((buckets, 4 * DH), low),
        pltpu.VMEM((8, group), wide),
        pltpu.VMEM((2, full_len, DH), low),
        pltpu.VMEM((2, BLOCK, full_len + buckets), wide),
        pltpu.VMEM((2, BLOCK, full_len + buckets), low),
        pltpu.VMEM((2, pad_blocks, BLOCK, band_width), wide),
        pltpu.VMEM((4, full_len, DH), wide),
        pltpu.VMEM((2, DH, full_len), wide),
        pltpu.VMEM((2, DH, full_len), wide),
        pltpu.VMEM((2, 8, full_len), wide),
        pltpu.VMEM((2, DH, buckets), wide),
        pltpu.VMEM((2, DH, buckets), wide),
    ]
    scratch += reduce_sems(chips)
    scratch += [pltpu.SemaphoreType.DMA((2 * batches,)), pltpu.SemaphoreType.DMA((tokens,))]
    sends = 4 * (batches - 1) + chips + tokens - 1 + 2 * batches - 1 + 3
    inputs = (q, k, v, qrev, krev, probs, m_mix, vec, w_cat, xs, table, ctx, attn_all)
    return comm_call(
        settle_kernel,
        "settle_grads",
        ident,
        outs,
        inputs,
        sends,
        6,
        scratch=scratch,
        limit=BACK_VMEM,
    )


def finish_kernel(
    pre_ref, ins_ref, vecs_ref, cols_ref, dws_ref, tabs_ref, mixs_ref, ups_ref, downs_ref,
    upbs_ref, last_ref,
    output_ref, input_ref, dq_ref, dk_ref, dv_ref, mix_ref, table_ref, bias_ref, gain_ref, shift_ref,
    up_ref, upb_ref, down_ref, downb_ref,
):
    at = Place()
    wide = jnp.float32

    def total(ref):
        out = ref[0].astype(wide)
        for k in range(1, ref.shape[0]):
            out = out + ref[k].astype(wide)
        return out

    output_ref[...] = last_ref[...]
    input_ref[...] = pre_ref[...] + ins_ref[...]
    up_ref[...] = total(ups_ref)
    down_ref[...] = total(downs_ref)
    upb_ref[...] = total(upbs_ref)[0:1]
    table_ref[...] = total(tabs_ref)
    group = 2 * DH
    spare = jnp.zeros((dws_ref.shape[1], DH), wide)
    for i, ref in enumerate((dq_ref, dk_ref, dv_ref)):
        lower = dws_ref[0, :, i * group : (i + 1) * group].astype(wide)
        upper = dws_ref[1, :, i * group : (i + 1) * group].astype(wide)
        ref[...] = jnp.concatenate([lower, spare], axis=1) + jnp.concatenate(
            [spare, upper], axis=1
        )
    rows = mix_ref.shape[0]
    lower, upper = mixs_ref[0].astype(wide), mixs_ref[1].astype(wide)
    spare = jnp.zeros((DH, lower.shape[1]), wide)
    whole = jnp.concatenate([lower, spare], axis=0) + jnp.concatenate([spare, upper], axis=0)
    mix_ref[...] = jnp.where(at.core == 0, whole[:rows], whole[rows:])
    small = total(vecs_ref)
    lanes = bias_ref.shape[1]
    cols = [cols_ref[core, 0:1] for core in range(2)]
    for row in range(1, at.batches):
        cols = [cols[core] + cols_ref[2 * row + core, 0:1] for core in range(2)]
    spare = jnp.zeros((1, DH), wide)
    biases = []
    for i in range(3):
        lower, upper = [part[:, i * group : (i + 1) * group] for part in cols]
        both = jnp.concatenate([lower, spare], axis=1) + jnp.concatenate([spare, upper], axis=1)
        biases.append(jnp.where(at.core == 0, both[:, :lanes], both[:, lanes:]))
    bias_ref[...] = jnp.concatenate(biases + [small[0:1, :lanes]], axis=0)
    gain_ref[...] = small[1:3, :lanes]
    shift_ref[...] = small[3:5, :lanes]
    downb_ref[...] = small[5:6, :lanes]


def finish(pre_grad, parts, shapes):
    inputs = (pre_grad,) + tuple(parts)
    return pl.pallas_call(
        finish_kernel,
        out_shape=(like(parts[-1]),)
        + tuple(jax.ShapeDtypeStruct(shape, jnp.float32) for shape in shapes),
        in_specs=[VMEM_SPEC] * len(inputs),
        out_specs=(VMEM_SPEC,) * (len(shapes) + 1),
        compiler_params=pltpu.CompilerParams(vmem_limit_bytes=COMM_VMEM),
        name="finish",
    )(*inputs)


def fits_fast(layer_input, table_shard, hidden_here):
    rows, local_len, width = layer_input.shape
    tokens, batches = lax.axis_size("seq"), lax.axis_size("batch")
    return (
        rows == 1
        and local_len == BLOCK
        and tokens == 2 * batches
        and width == 3 * DH * batches
        and (table_shard.shape[0] * tokens) % (4 * BLOCK) == 0
        and tokens == 8
        and 10 + hidden_here // BLOCK <= 16
        and hidden_here % BLOCK == 0
    )


def fast_body(
    layer_input, segment_ids, w_query, w_key, w_value, w_mix, rel_table, attn_biases,
    norm_gains, norm_shifts, w_up, up_bias, w_down, down_bias, out_grad,
):
    local_len, width = layer_input.shape[1:]
    low = jnp.bfloat16
    shard_rows, shard_cols = w_query.shape
    lanes = attn_biases.shape[1]
    hidden_here = w_up.shape[1]
    x = layer_input[0]
    pack = jnp.concatenate([attn_biases, norm_gains, norm_shifts, down_bias[None]], axis=0)
    pack = jnp.pad(pack, ((0, 0), (0, BLOCK - lanes)))
    pack = jnp.concatenate(
        [pack, segment_ids.astype(low), up_bias.reshape(hidden_here // BLOCK, BLOCK)], axis=0
    )
    pack = jnp.pad(pack, ((0, 16 - pack.shape[0]), (0, 0)))
    weights = (w_query, w_key, w_value, w_mix, rel_table, pack, w_up, w_down)
    xs, qkvs, mixs, tables, vecs, up2, down2 = gather_inputs(
        *[pltpu.with_memory_space_constraint(a, pltpu.HBM) for a in (x,) + weights]
    )
    q, k, v, qrev, krev, probs, ctx, w_cat, table = attend(xs, qkvs, tables, vecs)
    output, pre_grad, sums, attn_all, m_mix, ups, downs, upbs = feed_forward(
        ctx, x, mixs, vecs, w_up, w_down, up2, down2, out_grad[0], 1
    )
    ins, vec_all, cols_all, dw_all, tab_all, mix_all = settle_grads(
        q, k, v, qrev, krev, probs, m_mix, sums, w_cat, xs, table, ctx, attn_all, 2
    )
    shard = (shard_rows, shard_cols)
    shapes = (
        x.shape, shard, shard, shard, shard, rel_table.shape, (4, lanes), (2, lanes), (2, lanes),
        (width // lax.axis_size("batch"), hidden_here), (1, hidden_here),
        (width // lax.axis_size("batch"), hidden_here), (1, lanes),
    )
    grads = finish(
        pre_grad,
        (ins, vec_all, cols_all, dw_all, tab_all, mix_all, ups, downs, upbs, output),
        shapes,
    )
    output, input_grad, dq, dk, dv, dmix, dtable = grads[:7]
    dbias, dgain, dshift, dup, dupb, ddown, ddownb = grads[7:]
    return (
        output[None], input_grad[None], dq, dk, dv, dmix, dtable, dbias, dgain, dshift,
        dup, dupb.reshape(hidden_here), ddown.T, ddownb.reshape(lanes),
    )


def body(
    layer_input,
    segment_ids,
    w_query,
    w_key,
    w_value,
    w_mix,
    rel_table,
    attn_biases,
    norm_gains,
    norm_shifts,
    w_up,
    up_bias,
    w_down,
    down_bias,
    out_grad,
):
    if fits_fast(layer_input, rel_table, w_up.shape[1]):
        return fast_body(
            layer_input, segment_ids, w_query, w_key, w_value, w_mix, rel_table, attn_biases,
            norm_gains, norm_shifts, w_up, up_bias, w_down, down_bias, out_grad,
        )
    rows, local_len, width = layer_input.shape
    full_len = local_len * lax.axis_size("seq")
    tokens_here = local_len * rows
    highest_prec = lax.Precision.HIGHEST
    parts = (
        lax.all_gather(w_query, "batch", axis=1, tiled=True),
        lax.all_gather(w_key, "batch", axis=1, tiled=True),
        lax.all_gather(w_value, "batch", axis=1, tiled=True),
        lax.all_gather(w_mix, "batch", axis=1, tiled=True),
        lax.all_gather(rel_table, "batch", axis=1, tiled=True),
    )
    whole = (
        lax.all_gather(parts[0], "seq", axis=0, tiled=True),
        lax.all_gather(parts[1], "seq", axis=0, tiled=True),
        lax.all_gather(parts[2], "seq", axis=0, tiled=True),
        lax.all_gather(parts[3], "seq", axis=0, tiled=True),
        lax.all_gather(parts[4], "seq", axis=0, tiled=True),
        lax.all_gather(attn_biases, "seq", axis=1, tiled=True),
        lax.all_gather(norm_gains, "seq", axis=1, tiled=True),
        lax.all_gather(norm_shifts, "seq", axis=1, tiled=True),
        lax.all_gather(down_bias, "seq", axis=0, tiled=True),
    )
    m_query, m_key, m_value, m_mix, table, biases, gains, shifts, bias_down = whole
    flat_input = jnp.swapaxes(layer_input, 0, 1).reshape(tokens_here, width)
    queries = (jnp.dot(flat_input, m_query, preferred_element_type=jnp.float32) + biases[0]).astype(
        jnp.bfloat16
    )
    keys_here = (jnp.dot(flat_input, m_key, preferred_element_type=jnp.float32) + biases[1]).astype(
        jnp.bfloat16
    )
    values_here = (
        jnp.dot(flat_input, m_value, preferred_element_type=jnp.float32) + biases[2]
    ).astype(jnp.bfloat16)
    query_rel = (jnp.dot(table, m_query, preferred_element_type=jnp.float32) + biases[0]).astype(
        jnp.bfloat16
    )
    key_rel = (jnp.dot(table, m_key, preferred_element_type=jnp.float32) + biases[1]).astype(
        jnp.bfloat16
    )
    local_seg = jnp.swapaxes(segment_ids, 0, 1).astype(jnp.bfloat16)
    keys_all, values_all, seg_all = (
        lax.all_gather(keys_here.reshape(local_len, rows, width), "seq", axis=0, tiled=True),
        lax.all_gather(values_here.reshape(local_len, rows, width), "seq", axis=0, tiled=True),
        lax.all_gather(local_seg, "seq", axis=0, tiled=True),
    )
    buckets = table.shape[0]
    offset = lax.axis_index("seq") * local_len
    bucket_iota = jnp.arange(buckets, dtype=jnp.int32)
    inner_cols = (bucket_iota > 0) & (bucket_iota < buckets - 1)
    same_doc = (
        jnp.swapaxes(local_seg, 0, 1)[:, None, :, None]
        == jnp.swapaxes(seg_all, 0, 1)[:, None, None, :]
    )
    score_scale = 1.0 / math.sqrt(3.0 * DH)
    head_queries = split_heads(queries.reshape(local_len, rows, width))
    head_keys = split_heads(keys_all)
    head_values = split_heads(values_all)
    rel_queries = split_table(query_rel)
    rel_keys = split_table(key_rel)

    def forward_group(carry, group):
        g_query, g_key, g_value, g_qrel, g_krel = group
        total, near_pull, far_pull, window = relative_scores(
            g_query, g_key, g_krel, g_qrel, offset, full_len
        )
        scores = jnp.where(same_doc, total * score_scale, masked_score)
        highest = jnp.max(scores, axis=-1, keepdims=True)
        exponent = jnp.exp(scores - highest)
        denominator = jnp.sum(exponent, axis=-1, keepdims=True)
        weights_low = (exponent / denominator).astype(jnp.bfloat16)
        context = jnp.einsum(
            "rgij,rgjd->rgid", weights_low, g_value, preferred_element_type=jnp.float32
        )
        return (carry, (context, (highest + jnp.log(denominator))[..., 0]))

    unused, (context_groups, log_totals) = lax.scan(
        forward_group, None, (head_queries, head_keys, head_values, rel_queries, rel_keys)
    )
    context_low = join_heads(context_groups).reshape(tokens_here, width).astype(jnp.bfloat16)
    pre_norm = (
        flat_input.astype(jnp.float32)
        + jnp.dot(context_low, m_mix, preferred_element_type=jnp.float32)
        + biases[3]
    )
    hidden, norm1_pull = jax.vjp(
        normalize, pre_norm, gains[0].astype(jnp.float32), shifts[0].astype(jnp.float32)
    )
    hidden_low = hidden.astype(jnp.bfloat16)

    def spread_rows(rows_low):
        return lax.all_gather(rows_low, "seq", axis=0, tiled=True)

    def hidden_sums(make_term):
        return lax.psum_scatter(
            make_term(jnp.int32(0), tokens_here * lax.axis_size("seq")),
            "seq",
            scatter_dimension=0,
            tiled=True,
        )

    hidden_rows = spread_rows(hidden_low)
    inner = jnp.dot(hidden_rows, w_up, preferred_element_type=jnp.float32) + up_bias
    act, gelu_pull = jax.vjp(exact_gelu, inner)
    act_low = act.astype(jnp.bfloat16)

    def down_rows(start, count):
        return jnp.dot(act_low, w_down, preferred_element_type=jnp.float32)

    ffn_result = hidden_sums(down_rows)
    mixed = hidden + ffn_result + bias_down
    output, norm2_pull = jax.vjp(
        normalize, mixed, gains[1].astype(jnp.float32), shifts[1].astype(jnp.float32)
    )
    flat_grad = jnp.swapaxes(out_grad, 0, 1).reshape(tokens_here, width).astype(jnp.float32)
    mixed_grad, gain2_grad, shift2_grad = norm2_pull(flat_grad)
    ffn_grad_low = mixed_grad.astype(jnp.bfloat16)
    grad_rows = spread_rows(ffn_grad_low)
    act_grad = jnp.einsum("nd,fd->nf", grad_rows, w_down, preferred_element_type=jnp.float32)
    inner_low = gelu_pull(act_grad)[0].astype(jnp.bfloat16)
    up_part = jnp.einsum("nd,nf->df", hidden_rows, inner_low, preferred_element_type=jnp.float32)
    upb_part = jnp.sum(inner_low.astype(jnp.float32), axis=0)
    down_part = jnp.einsum("nf,nd->fd", act_low, grad_rows, preferred_element_type=jnp.float32)

    def back_rows(start, count):
        return jnp.einsum("nf,df->nd", inner_low, w_up, preferred_element_type=jnp.float32)

    hidden_grad = mixed_grad + hidden_sums(back_rows)
    pre_grad, gain1_grad, shift1_grad = norm1_pull(hidden_grad)
    attn_low = pre_grad.astype(jnp.bfloat16)
    mix_whole = jnp.einsum("nd,ne->de", context_low, attn_low, preferred_element_type=jnp.float32)
    context_grad = jnp.einsum(
        "ne,de->nd", attn_low, m_mix, preferred_element_type=jnp.float32
    ).astype(jnp.bfloat16)
    head_context_grad = split_heads(context_grad.reshape(local_len, rows, width))

    def query_side(group):
        g_query, g_key, g_value, g_qrel, g_krel, g_dctx, g_lse = group
        total, near_pull, far_pull, window = relative_scores(
            g_query, g_key, g_krel, g_qrel, offset, full_len
        )
        scores = jnp.where(same_doc, total * score_scale, masked_score)
        weights_now = jnp.exp(scores - g_lse[..., None])
        prob_grad = jnp.einsum(
            "rgid,rgjd->rgij", g_dctx, g_value, preferred_element_type=jnp.float32
        )
        inner_sum = jnp.sum(weights_now * prob_grad, axis=-1)
        score_grad = (weights_now * (prob_grad - inner_sum[..., None])).astype(jnp.bfloat16)
        grad_wide = score_grad.astype(jnp.float32)
        near_grad = near_pull(grad_wide)[0]
        near_low = jnp.where(inner_cols, near_grad, 0.0).astype(jnp.bfloat16)
        near_ends = end_columns(near_grad)
        query_part = jnp.einsum(
            "rgij,rgjd->rgid", score_grad, g_key, preferred_element_type=jnp.float32
        )
        query_part = (
            query_part
            + jnp.einsum("rgib,gbd->rgid", near_low, g_krel, preferred_element_type=jnp.float32)
            + end_terms(near_ends, g_krel)
        )
        krel_part = with_ends(
            jnp.einsum("rgib,rgid->gbd", near_low, g_query, preferred_element_type=jnp.float32),
            end_rows(near_ends, g_query),
        )
        return (
            weights_now,
            score_grad,
            grad_wide,
            far_pull,
            window,
            inner_sum,
            query_part * score_scale,
            krel_part * score_scale,
        )

    query_groups = (
        head_queries,
        head_keys,
        head_values,
        rel_queries,
        rel_keys,
        head_context_grad,
        log_totals,
    )

    def all_grads(carry, group):
        weights_now, score_grad, grad_wide, far_pull, window, inner_sum, query_part, krel_part = (
            query_side(group)
        )
        g_query, g_key, g_value, g_qrel, g_krel, g_dctx, g_lse = group
        cross_grad, end_grad = far_pull(grad_wide)
        cross_low = cross_grad.astype(jnp.bfloat16)
        key_part = jnp.einsum(
            "rgij,rgid->rgjd", score_grad, g_query, preferred_element_type=jnp.float32
        )
        band_part = jnp.einsum(
            "rgmb,gbd->rgmd", cross_low, g_qrel, preferred_element_type=jnp.float32
        )
        key_part = (
            key_part
            + unband(band_part, offset, full_len, buckets // 2)
            + end_terms(end_grad, g_qrel)
        )
        value_part = jnp.einsum(
            "rgij,rgid->rgjd",
            weights_now.astype(jnp.bfloat16),
            g_dctx,
            preferred_element_type=jnp.float32,
        )
        qrel_part = with_ends(
            jnp.einsum("rgmb,rgmd->gbd", cross_low, window, preferred_element_type=jnp.float32),
            end_rows(end_grad, g_key),
        )
        return (
            carry,
            (query_part, key_part * score_scale, value_part, qrel_part * score_scale, krel_part),
        )

    unused, (dq_groups, dk_groups, dv_groups, dqrel_groups, dkrel_groups) = lax.scan(
        all_grads, None, query_groups
    )
    key_sum, value_sum = (
        lax.psum_scatter(join_heads(dk_groups), "seq", scatter_dimension=0, tiled=True),
        lax.psum_scatter(join_heads(dv_groups), "seq", scatter_dimension=0, tiled=True),
    )
    key_grads = key_sum.reshape(tokens_here, width).astype(jnp.bfloat16)
    value_grads = value_sum.reshape(tokens_here, width).astype(jnp.bfloat16)
    query_grads = join_heads(dq_groups).reshape(tokens_here, width).astype(jnp.bfloat16)
    qrel_grad = join_table(dqrel_groups)
    krel_grad = join_table(dkrel_groups)
    input_grad = pre_grad + jnp.einsum(
        "ne,de->nd", query_grads, m_query, preferred_element_type=jnp.float32
    )
    input_grad = input_grad + jnp.einsum(
        "ne,de->nd", key_grads, m_key, preferred_element_type=jnp.float32
    )
    input_grad = input_grad + jnp.einsum(
        "ne,de->nd", value_grads, m_value, preferred_element_type=jnp.float32
    )
    query_whole = jnp.einsum(
        "nd,ne->de", flat_input, query_grads, preferred_element_type=jnp.float32
    ) + jnp.einsum(
        "bd,be->de", table, qrel_grad, precision=highest_prec, preferred_element_type=jnp.float32
    )
    key_whole = jnp.einsum(
        "nd,ne->de", flat_input, key_grads, preferred_element_type=jnp.float32
    ) + jnp.einsum(
        "bd,be->de", table, krel_grad, precision=highest_prec, preferred_element_type=jnp.float32
    )
    value_whole = jnp.einsum(
        "nd,ne->de", flat_input, value_grads, preferred_element_type=jnp.float32
    )
    table_whole = jnp.einsum(
        "be,de->bd", qrel_grad, m_query, precision=highest_prec, preferred_element_type=jnp.float32
    ) + jnp.einsum(
        "be,de->bd", krel_grad, m_key, precision=highest_prec, preferred_element_type=jnp.float32
    )
    bias_whole = jnp.stack(
        [
            jnp.sum(query_grads.astype(jnp.float32), axis=0) + jnp.sum(qrel_grad, axis=0),
            jnp.sum(key_grads.astype(jnp.float32), axis=0) + jnp.sum(krel_grad, axis=0),
            jnp.sum(value_grads.astype(jnp.float32), axis=0),
            jnp.sum(pre_grad, axis=0),
        ]
    )
    gain_whole = jnp.stack([gain1_grad, gain2_grad])
    shift_whole = jnp.stack([shift1_grad, shift2_grad])
    downb_whole = jnp.sum(mixed_grad, axis=0)
    seq_parts = (
        lax.psum_scatter(query_whole, "seq", scatter_dimension=0, tiled=True),
        lax.psum_scatter(key_whole, "seq", scatter_dimension=0, tiled=True),
        lax.psum_scatter(value_whole, "seq", scatter_dimension=0, tiled=True),
        lax.psum_scatter(mix_whole, "seq", scatter_dimension=0, tiled=True),
        lax.psum_scatter(table_whole, "seq", scatter_dimension=0, tiled=True),
        lax.psum_scatter(bias_whole, "seq", scatter_dimension=1, tiled=True),
        lax.psum_scatter(gain_whole, "seq", scatter_dimension=1, tiled=True),
        lax.psum_scatter(shift_whole, "seq", scatter_dimension=1, tiled=True),
        lax.psum_scatter(downb_whole, "seq", scatter_dimension=0, tiled=True),
    )
    batch_parts = (
        lax.psum_scatter(seq_parts[0], "batch", scatter_dimension=1, tiled=True),
        lax.psum_scatter(seq_parts[1], "batch", scatter_dimension=1, tiled=True),
        lax.psum_scatter(seq_parts[2], "batch", scatter_dimension=1, tiled=True),
        lax.psum_scatter(seq_parts[3], "batch", scatter_dimension=1, tiled=True),
        lax.psum_scatter(seq_parts[4], "batch", scatter_dimension=1, tiled=True),
        lax.psum_scatter(up_part, "batch", scatter_dimension=0, tiled=True),
        lax.psum_scatter(down_part, "batch", scatter_dimension=1, tiled=True),
    )
    small_parts = lax.psum(
        (seq_parts[5], seq_parts[6], seq_parts[7], seq_parts[8], upb_part), "batch"
    )
    layer_output = jnp.swapaxes(output.reshape(local_len, rows, width), 0, 1).astype(jnp.bfloat16)
    input_back = jnp.swapaxes(input_grad.reshape(local_len, rows, width), 0, 1)
    return (
        layer_output,
        input_back,
        batch_parts[0],
        batch_parts[1],
        batch_parts[2],
        batch_parts[3],
        batch_parts[4],
        small_parts[0],
        small_parts[1],
        small_parts[2],
        batch_parts[5],
        small_parts[4],
        batch_parts[6],
        small_parts[3],
    )


def solution(mesh):
    return jax.shard_map(
        body,
        mesh=mesh,
        in_specs=(
            P("batch", "seq", None),
            P("batch", "seq"),
            P("seq", "batch"),
            P("seq", "batch"),
            P("seq", "batch"),
            P("seq", "batch"),
            P("seq", "batch"),
            P(None, "seq"),
            P(None, "seq"),
            P(None, "seq"),
            P(None, "seq"),
            P("seq"),
            P("seq", None),
            P("seq"),
            P("batch", "seq", None),
        ),
        out_specs=(
            P("batch", "seq", None),
            P("batch", "seq", None),
            P("seq", "batch"),
            P("seq", "batch"),
            P("seq", "batch"),
            P("seq", "batch"),
            P("seq", "batch"),
            P(None, "seq"),
            P(None, "seq"),
            P(None, "seq"),
            P("batch", "seq"),
            P("seq"),
            P("seq", "batch"),
            P("seq"),
        ),
        check_vma=False,
    )
```

```python
import math

import jax
import jax.numpy as jnp
from jax import lax
from jax.experimental import pallas as pl
from jax.experimental.pallas import tpu as pltpu
from jax.sharding import PartitionSpec as P

DH = 64


masked_score = -1e30
norm_eps = 1e-06
pair_heads = 2


def normalize(values, gain, shift):
    average = jnp.mean(values, axis=-1, keepdims=True)
    centered = values - average
    variance = jnp.mean(centered * centered, axis=-1, keepdims=True)
    return centered * lax.rsqrt(variance + norm_eps) * gain + shift


def exact_gelu(values):
    return jax.nn.gelu(values, approximate=False)


def split_heads(matrix):
    length, rows, width = matrix.shape
    groups = width // (pair_heads * DH)
    return matrix.reshape(length, rows, groups, pair_heads, DH).transpose(2, 1, 3, 0, 4)


def join_heads(matrix):
    groups, rows, pair, length, depth = matrix.shape
    return matrix.transpose(3, 1, 0, 2, 4).reshape(length, rows, groups * pair * depth)


def split_table(matrix):
    buckets, width = matrix.shape
    return matrix.reshape(buckets, width // (pair_heads * DH), pair_heads, DH).transpose(1, 2, 0, 3)


def join_table(matrix):
    groups, pair, buckets, depth = matrix.shape
    return matrix.transpose(2, 0, 1, 3).reshape(buckets, groups * pair * depth)


def table_ends(table):
    return jnp.stack([table[:, 0], table[:, -1]], axis=1)


def near_skew(table_prod, offset, full_len):
    lead = table_prod.shape[:-2]
    count, buckets = table_prod.shape[-2:]
    span = buckets // 2
    lead_pad = [(0, 0)] * len(lead)
    flipped = jnp.pad(table_prod[..., ::-1], lead_pad + [(0, 0), (0, count)])
    sheared = flipped.reshape(lead + (count * (buckets + count),))[
        ..., : count * (buckets + count - 1)
    ]
    sheared = sheared.reshape(lead + (count, buckets + count - 1))
    spread = jnp.pad(sheared, lead_pad + [(0, 0), (full_len, full_len)])
    band = lax.dynamic_slice_in_dim(
        spread, full_len + span - 1 - offset, full_len, axis=len(lead) + 1
    )
    distance = (offset + jnp.arange(count, dtype=jnp.int32))[:, None] - jnp.arange(
        full_len, dtype=jnp.int32
    )[None, :]
    return jnp.where(
        distance <= -span,
        table_prod[..., 0:1],
        jnp.where(distance >= span - 1, table_prod[..., buckets - 1 :], band),
    )


def far_place(cross, end_vals, offset, count, full_len):
    lead = cross.shape[:-2]
    band_len, buckets = cross.shape[-2:]
    span = buckets // 2
    lead_pad = [(0, 0)] * len(lead)
    turned = jnp.swapaxes(cross, -1, -2).reshape(lead + (buckets * band_len,))
    turned = jnp.pad(turned, lead_pad + [(0, buckets)])
    diagonal = turned.reshape(lead + (buckets, band_len + 1))[..., :count]
    aligned = jnp.pad(jnp.swapaxes(diagonal, -1, -2), lead_pad + [(0, 0), (0, count)])
    sheared = aligned.reshape(lead + (count * (buckets + count),))[
        ..., : count * (buckets + count - 1)
    ]
    sheared = sheared.reshape(lead + (count, buckets + count - 1))
    spread = jnp.pad(sheared, lead_pad + [(0, 0), (full_len, full_len)])
    band = lax.dynamic_slice_in_dim(spread, full_len + span - offset, full_len, axis=len(lead) + 1)
    distance = (
        jnp.arange(full_len, dtype=jnp.int32)[None, :]
        - (offset + jnp.arange(count, dtype=jnp.int32))[:, None]
    )
    return jnp.where(
        distance <= -span,
        end_vals[..., 0:1, :],
        jnp.where(distance >= span - 1, end_vals[..., 1:2, :], band),
    )


def band_rows(all_rows, offset, count, span):
    padded = jnp.pad(all_rows, [(0, 0), (0, 0), (span, span), (0, 0)])
    return lax.dynamic_slice_in_dim(padded, offset, count + 2 * span - 1, axis=2)


def unband(values, offset, full_len, span):
    lead = values.shape[:2]
    room = jnp.zeros(lead + (full_len + 2 * span, values.shape[3]), jnp.float32)
    placed = lax.dynamic_update_slice_in_dim(room, values, offset, axis=2)
    return placed[:, :, span : span + full_len]


def relative_scores(own_rows, all_rows, own_table, all_table, offset, full_len):
    count = own_rows.shape[2]
    content = jnp.einsum("rgid,rgjd->rgij", own_rows, all_rows, preferred_element_type=jnp.float32)
    own_prod = jnp.einsum("rgid,gbd->rgib", own_rows, own_table, preferred_element_type=jnp.float32)
    window = band_rows(all_rows, offset, count, all_table.shape[1] // 2)
    cross = jnp.einsum("rgmd,gbd->rgmb", window, all_table, preferred_element_type=jnp.float32)
    end_vals = jnp.einsum(
        "rgjd,ged->rgej", all_rows, table_ends(all_table), preferred_element_type=jnp.float32
    )
    near_vals, near_pull = jax.vjp(lambda product: near_skew(product, offset, full_len), own_prod)
    far_vals, far_pull = jax.vjp(
        lambda part, ends: far_place(part, ends, offset, count, full_len), cross, end_vals
    )
    return (content + near_vals + far_vals, near_pull, far_pull, window)


def end_columns(grad):
    return jnp.stack([grad[..., 0], grad[..., -1]], axis=2)


def end_terms(ends, table):
    return jnp.einsum(
        "rgei,ged->rgid",
        ends,
        table_ends(table),
        precision=lax.Precision.HIGHEST,
        preferred_element_type=jnp.float32,
    )


def end_rows(ends, rows_low):
    return jnp.einsum(
        "rgei,rgid->ged",
        ends,
        rows_low,
        precision=lax.Precision.HIGHEST,
        preferred_element_type=jnp.float32,
    )


def with_ends(inner_part, edge_rows):
    buckets = inner_part.shape[1]
    place = jnp.arange(buckets, dtype=jnp.int32)[None, :, None]
    return (
        inner_part
        + jnp.where(place == 0, edge_rows[:, 0:1], 0.0)
        + jnp.where(place == buckets - 1, edge_rows[:, 1:2], 0.0)
    )


BLOCK = 128
MIB = 1024 * 1024
ATTEND_VMEM = 26 * MIB
BACK_VMEM = 40 * MIB
FEED_VMEM = 26 * MIB
COMM_VMEM = 16 * MIB


def dot_nn(a, b):
    return lax.dot_general(a, b, (((1,), (0,)), ((), ())), preferred_element_type=jnp.float32)


def dot_nt(a, b):
    return lax.dot_general(a, b, (((1,), (1,)), ((), ())), preferred_element_type=jnp.float32)


def dot_tn(a, b):
    return lax.dot_general(a, b, (((0,), (0,)), ((), ())), preferred_element_type=jnp.float32)


def turn_matrix(buckets):
    row = lax.broadcasted_iota(jnp.int32, (buckets, buckets), 0)
    col = lax.broadcasted_iota(jnp.int32, (buckets, buckets), 1)
    return (row + col == buckets - 1).astype(jnp.bfloat16)


def skew_band(product):
    count, buckets = product.shape
    row = lax.broadcasted_iota(jnp.int32, (count, BLOCK), 0)
    lane = lax.broadcasted_iota(jnp.int32, (count, BLOCK), 1)
    edge = jnp.where(row + lane <= BLOCK - 2, product[:, buckets - 1 :], product[:, 0:1])
    wide = jnp.concatenate([product, edge], axis=1)
    return pltpu.roll(wide, 1, 1, stride=1, stride_axis=0)


def skew_back(turned, buckets):
    return pltpu.roll(turned, turned.shape[1] - BLOCK, 1, stride=1, stride_axis=0)[:, :buckets]


def chip_columns(vec_ref, chip, index, core):
    width = 3 * DH // 2
    both = jnp.concatenate(
        [
            vec_ref[2 * chip, index : index + 1, :width].astype(jnp.float32),
            vec_ref[2 * chip + 1, index : index + 1, :width].astype(jnp.float32),
        ],
        axis=1,
    )
    return jnp.where(core == 0, both[:, : 2 * DH], both[:, DH:])


def attend_kernel(
    xs_ref,
    qkvs_ref,
    tables_ref,
    vecs_ref,
    q_ref,
    k_ref,
    v_ref,
    qrev_ref,
    krev_ref,
    p_ref,
    ctx_ref,
    w_ref,
    table_ref,
    segc_ref,
    place_ref,
    wide_ref,
    ends_ref,
    held_ref,
):
    at = Place()
    full_len = xs_ref.shape[0] * xs_ref.shape[1]
    buckets = table_ref.shape[0]
    blocks = full_len // BLOCK
    span = buckets // 2
    side = span // BLOCK
    band_width = buckets + BLOCK
    band_blocks = band_width // BLOCK
    group = 2 * DH
    scale = 1.0 / math.sqrt(3.0 * DH)
    units = p_ref.shape[0]
    shard_rows = qkvs_ref.shape[2]
    table_rows = tables_ref.shape[3]
    batches = tables_ref.shape[1]
    for part in range(at.tokens):
        pieces = []
        for i in range(3):
            piece = qkvs_ref[part, i]
            pieces.append(jnp.where(at.core == 0, piece[:, :group], piece[:, DH:]))
        w_ref[part * shard_rows : (part + 1) * shard_rows] = jnp.concatenate(pieces, axis=1)
        core, chip = part % 2, part // 2
        table_ref[part * table_rows : (part + 1) * table_rows] = jnp.concatenate(
            [tables_ref[core, row, chip] for row in range(batches)], axis=1
        )
        own_seg = vecs_ref[part, 9:10].astype(jnp.float32)
        segc_ref[part * BLOCK : (part + 1) * BLOCK] = jnp.broadcast_to(own_seg, (BLOCK, BLOCK)).T
    seg_row = jnp.concatenate(
        [vecs_ref[part, 9:10].astype(jnp.float32) for part in range(at.tokens)], axis=1
    )
    bias = jnp.concatenate(
        [chip_columns(vecs_ref, at.chip, i, at.core) for i in range(3)], axis=1
    )
    tokens_all = xs_ref[...].reshape(full_len, xs_ref.shape[2])
    proj = (dot_nn(tokens_all, w_ref[...]) + bias).astype(jnp.bfloat16)
    rel = (dot_nn(table_ref[...], w_ref[:, : 2 * group]) + bias[:, : 2 * group]).astype(
        jnp.bfloat16
    )
    rel = dot_nn(turn_matrix(buckets), rel).astype(jnp.bfloat16)
    for slot in range(2):
        lo, hi = slot * DH, (slot + 1) * DH
        q_ref[slot] = proj[:, lo:hi]
        k_ref[slot] = proj[:, group + lo : group + hi]
        v_ref[slot] = proj[:, 2 * group + lo : 2 * group + hi]
        qrev_ref[slot] = rel[:, lo:hi]
        krev_ref[slot] = rel[:, group + lo : group + hi]
    held_ref[...] = jnp.zeros_like(held_ref)
    for slot in range(2):
        ends_ref[slot, 0] = dot_nt(qrev_ref[slot, 0:16], k_ref[slot])
        ends_ref[slot, 1] = dot_nt(qrev_ref[slot, buckets - 16 : buckets], k_ref[slot])

        def key_block(kb, carry):
            rows = k_ref[slot, pl.ds(pl.multiple_of(kb * BLOCK, BLOCK), BLOCK)]
            band = skew_band(dot_nt(rows, qrev_ref[slot]))
            for e in range(band_blocks):
                place_ref[
                    slot,
                    kb + e,
                    :,
                    (band_blocks - 1 - e) * BLOCK : (band_blocks - e) * BLOCK,
                ] = band[:, e * BLOCK : (e + 1) * BLOCK].T
            return carry

        lax.fori_loop(0, blocks, key_block, 0, unroll=8)

    first = at.core * (blocks // 2)

    def unit(u, carry):
        g = u + first
        slot = g // blocks
        qb = g % blocks
        start = pl.multiple_of(qb * BLOCK, BLOCK)
        rows = q_ref[slot, pl.ds(start, BLOCK)]
        own = dot_nt(rows, krev_ref[slot])
        band = skew_band(own) + place_ref[slot, qb + side]
        wide_ref[u % 2, :, pl.ds(start, band_width)] = band
        content = dot_nt(rows, k_ref[slot])
        lane = lax.broadcasted_iota(jnp.int32, (BLOCK, full_len), 1)
        near = jnp.where(
            lane < start - span,
            own[:, 0:1] + ends_ref[slot, 1, 15:16],
            jnp.where(
                lane >= start + band_width - span,
                own[:, buckets - 1 :] + ends_ref[slot, 0, 0:1],
                wide_ref[u % 2, :, span : span + full_len],
            ),
        )
        same = segc_ref[pl.ds(start, BLOCK), 0:1] == seg_row
        scores = jnp.where(same, (content + near) * scale, masked_score)
        highest = jnp.max(scores, axis=-1, keepdims=True)
        exponent = jnp.exp(scores - highest)
        total = jnp.sum(exponent, axis=-1, keepdims=True)
        probs = (exponent / total).astype(jnp.bfloat16)
        p_ref[u] = probs
        held_ref[slot, pl.ds(start, BLOCK)] = dot_nn(probs, v_ref[slot]).astype(jnp.bfloat16)
        return carry

    lax.fori_loop(0, units, unit, 0, unroll=4)
    for part in range(at.tokens):
        rows = slice(part * BLOCK, (part + 1) * BLOCK)
        ctx_ref[part] = jnp.concatenate([held_ref[0, rows], held_ref[1, rows]], axis=1)


def attend(xs, qkvs, tables, vecs):
    tokens, local_len, width = xs.shape
    full_len = tokens * local_len
    buckets = tokens * tables.shape[3]
    blocks = full_len // BLOCK
    units = 3 * blocks // 2
    band_width = buckets + BLOCK
    low, wide = jnp.bfloat16, jnp.float32
    pad_blocks = blocks + band_width // BLOCK - 1
    return pl.pallas_call(
        attend_kernel,
        out_shape=(
            jax.ShapeDtypeStruct((2, full_len, DH), low),
            jax.ShapeDtypeStruct((2, full_len, DH), low),
            jax.ShapeDtypeStruct((2, full_len, DH), low),
            jax.ShapeDtypeStruct((2, buckets, DH), low),
            jax.ShapeDtypeStruct((2, buckets, DH), low),
            jax.ShapeDtypeStruct((units, BLOCK, full_len), low),
            jax.ShapeDtypeStruct((tokens, local_len, 2 * DH), low),
            jax.ShapeDtypeStruct((width, 6 * DH), low),
            jax.ShapeDtypeStruct((buckets, width), low),
        ),
        in_specs=[pl.BlockSpec(memory_space=pltpu.VMEM)] * 4,
        out_specs=[pl.BlockSpec(memory_space=pltpu.VMEM)] * 9,
        scratch_shapes=[
            pltpu.VMEM((full_len, BLOCK), wide),
            pltpu.VMEM((2, pad_blocks, BLOCK, band_width), wide),
            pltpu.VMEM((2, BLOCK, full_len + buckets), wide),
            pltpu.VMEM((2, 2, 16, full_len), wide),
            pltpu.VMEM((2, full_len, DH), low),
        ],
        compiler_params=pltpu.CompilerParams(vmem_limit_bytes=ATTEND_VMEM),
        name="attend",
    )(xs, qkvs, tables, vecs)


def attend_back_kernel(
    q_ref,
    k_ref,
    v_ref,
    qrev_ref,
    krev_ref,
    p_ref,
    mix_ref,
    attn_ref,
    dcat_ref,
    rel_ref,
    sum_ref,
    heads_ref,
    wide_ref,
    low_ref,
    place_ref,
    dq_ref,
    dkt_ref,
    dvt_ref,
    far_ref,
    dkr_ref,
    dqr_ref,
):
    full_len = q_ref.shape[1]
    buckets = qrev_ref.shape[1]
    blocks = full_len // BLOCK
    span = buckets // 2
    side = span // BLOCK
    band_width = buckets + BLOCK
    band_blocks = band_width // BLOCK
    scale = 1.0 / math.sqrt(3.0 * DH)
    units = p_ref.shape[0]
    for ref in (wide_ref, low_ref, place_ref, dq_ref, dkt_ref, dvt_ref, far_ref, dkr_ref, dqr_ref):
        ref[...] = jnp.zeros_like(ref)
    at = Place()
    group = 2 * DH
    first_row = pl.multiple_of((3 * at.chip + at.core) * DH, DH)
    mix_rows = mix_ref[pl.ds(first_row, group)]
    dctx = dot_nt(attn_ref[...].reshape(full_len, attn_ref.shape[2]), mix_rows)
    for slot in range(2):
        heads_ref[slot] = dctx[:, slot * DH : (slot + 1) * DH].astype(jnp.bfloat16)
    first = at.core * (blocks // 2)
    turn = turn_matrix(BLOCK)
    place8 = lax.broadcasted_iota(jnp.int32, (8, full_len), 0)

    def unit(u, carry):
        g = u + first
        slot = g // blocks
        qb = g % blocks
        start = pl.multiple_of(qb * BLOCK, BLOCK)
        rows = q_ref[slot, pl.ds(start, BLOCK)]
        grad = heads_ref[slot, pl.ds(start, BLOCK)]
        probs = p_ref[u]
        wide_probs = probs.astype(jnp.float32)
        prob_grad = dot_nt(grad, v_ref[slot])
        inner = jnp.sum(wide_probs * prob_grad, axis=-1, keepdims=True)
        low_grad = (wide_probs * (prob_grad - inner)).astype(jnp.bfloat16)
        score_grad = low_grad.astype(jnp.float32)
        wide_ref[u % 2, :, span : span + full_len] = dot_nn(turn, low_grad)
        low_ref[u % 2, :, span : span + full_len] = low_grad
        dvt_ref[slot] += dot_tn(grad, probs)
        dkt_ref[slot] += dot_tn(rows, low_grad)
        row = lax.broadcasted_iota(jnp.int32, (BLOCK, full_len), 0)
        lane = lax.broadcasted_iota(jnp.int32, (BLOCK, full_len), 1)
        gap = lane - row - start
        right = jnp.where(gap > span, score_grad, 0.0)
        left = jnp.where(gap < 1 - span, score_grad, 0.0)
        end_right = jnp.sum(right, axis=-1, keepdims=True)
        end_left = jnp.sum(left, axis=-1, keepdims=True)
        far_right = jnp.sum(jnp.where(gap >= span, score_grad, 0.0), axis=0, keepdims=True)
        far_left = jnp.sum(jnp.where(gap < -span, score_grad, 0.0), axis=0, keepdims=True)
        far_ref[slot] += jnp.where(place8 == 0, far_right, jnp.where(place8 == 1, far_left, 0.0))
        band = wide_ref[u % 2, :, pl.ds(start, band_width)]
        near = dot_nn(turn, skew_back(band, buckets).astype(jnp.bfloat16))
        bucket = lax.broadcasted_iota(jnp.int32, (BLOCK, buckets), 1)
        near = near + jnp.where(
            bucket == 0, end_left, jnp.where(bucket == buckets - 1, end_right, 0.0)
        )
        near_low = near.astype(jnp.bfloat16)
        dq = dot_nn(low_grad, k_ref[slot]) + dot_nn(near_low, krev_ref[slot])
        dq_ref[slot, pl.ds(start, BLOCK)] = dq
        dkr_ref[slot] += dot_tn(rows, near_low)
        for e in range(band_blocks):
            keys_at = pl.multiple_of(start + e * BLOCK, BLOCK)
            place_ref[
                slot, qb + e, :, (band_blocks - 1 - e) * BLOCK : (band_blocks - e) * BLOCK
            ] = dot_nt(turn, low_ref[u % 2, :, pl.ds(keys_at, BLOCK)])
        return carry

    lax.fori_loop(0, units, unit, 0, unroll=4)
    parts_q, parts_k, parts_v = [], [], []
    parts_r = [None] * 4
    for slot in range(2):
        far_low = far_ref[slot].astype(jnp.bfloat16)
        mark = lax.broadcasted_iota(jnp.int32, (8, DH), 0)
        ends = jnp.where(
            mark == 0,
            qrev_ref[slot, 0:1].astype(jnp.float32),
            jnp.where(mark == 1, qrev_ref[slot, buckets - 1 : buckets].astype(jnp.float32), 0.0),
        ).astype(jnp.bfloat16)
        end_keys = dot_tn(ends, far_low)
        end_rows = dot_nn(far_low, k_ref[slot])

        whole_k = (dkt_ref[slot] + end_keys).T

        def key_side(kb, carry):
            start = pl.multiple_of(kb * BLOCK, BLOCK)
            far = skew_back(place_ref[slot, kb + side], buckets).astype(jnp.bfloat16)
            far = dot_nn(turn, far).astype(jnp.bfloat16)
            keys = k_ref[slot, pl.ds(start, BLOCK)]
            dqr_ref[slot] += dot_tn(keys, far)
            dq_ref[2 + slot, pl.ds(start, BLOCK)] = dot_nn(far, qrev_ref[slot])
            return carry

        lax.fori_loop(0, blocks, key_side, 0, unroll=8)
        parts_q.append((dq_ref[slot] * scale).astype(jnp.bfloat16))
        parts_k.append(((dq_ref[2 + slot] + whole_k) * scale).astype(jnp.bfloat16))
        parts_v.append(dvt_ref[slot].T.astype(jnp.bfloat16))
        bucket = lax.broadcasted_iota(jnp.int32, (buckets, DH), 0)
        qr = dqr_ref[slot].T + jnp.where(
            bucket == 0, end_rows[0:1], jnp.where(bucket == buckets - 1, end_rows[1:2], 0.0)
        )
        dqr_out = qr * scale
        dkr_out = dkr_ref[slot].T * scale
        parts_r[slot] = dqr_out
        parts_r[2 + slot] = dkr_out
    dcat = jnp.concatenate(parts_q + parts_k + parts_v, axis=1)
    dcat_ref[...] = dcat
    rel = jnp.concatenate(parts_r, axis=1)
    rel_ref[...] = dot_nn(turn_matrix(buckets), rel.astype(jnp.bfloat16)).astype(jnp.bfloat16)
    rel_sum = jnp.sum(rel, axis=0, keepdims=True)
    rel_sum = jnp.concatenate([rel_sum, jnp.zeros((1, 2 * DH), jnp.float32)], axis=1)
    sums = jnp.sum(dcat.astype(jnp.float32), axis=0, keepdims=True) + rel_sum
    sum_ref[...] = jnp.broadcast_to(sums, sum_ref.shape)


MESH = pl.DeviceIdType.MESH
VMEM_SPEC = pl.BlockSpec(memory_space=pltpu.VMEM)
HBM_SPEC = pl.BlockSpec(memory_space=pltpu.HBM)
CHUNKS = 4


class Place:
    def __init__(self):
        self.batches = lax.axis_size("batch")
        self.tokens = lax.axis_size("seq")
        self.chips = self.tokens // 2
        self.row = lax.axis_index("batch")
        self.part = lax.axis_index("seq")
        self.chip = self.part // 2
        self.core = self.part % 2

    def inside(self):
        return jnp.logical_and(self.chip > 0, self.chip < self.chips - 1)

    def along_chips(self, k):
        chip = lax.rem(self.chip + k, self.chips)
        return chip, (self.row, 2 * chip + self.core)

    def from_chips(self, k):
        return lax.rem(self.chip + self.chips - k, self.chips)

    def partner(self):
        return (self.row, self.part + 1 - 2 * self.core)

    def along_rows(self, k):
        row = lax.rem(self.row + k, self.batches)
        return row, (row, self.part)

    def from_rows(self, k):
        return lax.rem(self.row + self.batches - k, self.batches)

    def along_seq(self, k):
        part = lax.rem(self.part + k, self.tokens)
        return part, (self.row, part)

    def along_plane(self, k):
        index = lax.rem(2 * self.row + self.core + k, 2 * self.batches)
        row, core = index // 2, index % 2
        return row, core, (row, 2 * self.chip + core)

    def chip_peers(self):
        return [self.along_chips(k)[1] for k in range(1, self.chips)]

    def row_peers(self):
        return [self.along_rows(k)[1] for k in range(1, self.batches)]

    def cross_peers(self):
        other = self.part + 1 - 2 * self.core
        return [(self.along_rows(k)[0], other) for k in range(1, self.batches)]

    def cross_row_peers(self):
        return self.row_peers() + self.cross_peers()

    def all_peers(self):
        peers = []
        for i in range(self.batches):
            row = lax.rem(self.row + i, self.batches)
            for j in range(self.tokens):
                if i or j:
                    peers.append((row, lax.rem(self.part + j, self.tokens)))
        return peers

    def seq_peers(self):
        return [self.along_seq(k)[1] for k in range(1, self.tokens)]

    def plane_peers(self):
        return [self.along_plane(k)[2] for k in range(1, 2 * self.batches)]


def meet(peers):
    barrier = pltpu.get_barrier_semaphore()
    for peer in peers:
        pl.semaphore_signal(barrier, inc=1, device_id=peer, device_id_type=MESH)
    pl.semaphore_wait(barrier, len(peers))


class Wires:
    def __init__(self, send_sems, recv_sems, local_sems):
        self.sems = (send_sems, recv_sems, local_sems)
        self.used = [0, 0]
        self.ends = []

    def send(self, src, dst, peer):
        k = self.used[0]
        self.used[0] += 1
        copy = pltpu.make_async_remote_copy(
            src_ref=src,
            dst_ref=dst,
            send_sem=self.sems[0].at[k],
            recv_sem=self.sems[1].at[k],
            device_id=peer,
            device_id_type=MESH,
        )
        copy.start()
        self.ends.append(copy.wait_send)
        return copy

    def local(self, src, dst):
        k = self.used[1]
        self.used[1] += 1
        copy = pltpu.make_async_copy(src, dst, self.sems[2].at[k])
        copy.start()
        return copy

    def finish(self):
        for end in self.ends:
            end()


def wire_scratch(sends, locals_count):
    return [
        pltpu.SemaphoreType.DMA((sends,)),
        pltpu.SemaphoreType.DMA((sends,)),
        pltpu.SemaphoreType.DMA((locals_count,)),
    ]


def comm_call(kernel, name, ident, out_shapes, inputs, sends, locals_count, scratch=(), spec=VMEM_SPEC, limit=None):
    return pl.pallas_call(
        kernel,
        out_shape=tuple(out_shapes),
        in_specs=[spec] * len(inputs),
        out_specs=tuple([VMEM_SPEC] * len(out_shapes)),
        scratch_shapes=list(scratch) + wire_scratch(sends, locals_count),
        compiler_params=pltpu.CompilerParams(
            collective_id=ident, has_side_effects=True, vmem_limit_bytes=limit or COMM_VMEM
        ),
        name=name,
    )(*inputs)


def like(array, *lead):
    return jax.ShapeDtypeStruct(tuple(lead) + tuple(array.shape), array.dtype)


def pick(values, index):
    out = jnp.int32(values[0])
    for i in range(1, len(values)):
        out = jnp.where(index == i, jnp.int32(values[i]), out)
    return out


def arrival_order(at):
    chips = range(at.chips)
    lists = [sorted((j for j in chips if j != z), key=lambda j: (abs(j - z), j)) for z in chips]
    return [pick([lists[z][t] for z in chips], at.chip) for t in range(at.chips - 1)]


def return_order(at):
    chips = range(at.chips)

    def away(j, z):
        end = at.chips - 1 if j < z else 0
        return (abs(j - end) + abs(end - z), j)

    lists = [sorted((j for j in chips if j != z), key=lambda j: away(j, z)) for z in chips]
    return [pick([lists[z][t] for z in chips], at.chip) for t in range(at.chips - 1)]


def far_order(at):
    chips = range(at.chips)
    lists = [sorted((j for j in chips if j != z), key=lambda j: (-abs(j - z), j)) for z in chips]
    return [pick([lists[z][t] for z in chips], at.chip) for t in range(at.chips - 1)]


def goes_on(at, j):
    above = jnp.logical_and(j < at.chip, at.chip < at.chips - 1)
    below = jnp.logical_and(j > at.chip, at.chip > 0)
    return jnp.logical_or(above, below)


def line_peer(at, step):
    return (at.row, 2 * (at.chip + step) + at.core)


class LineGather:
    def __init__(self, at, buf, slot, sems, own=None):
        self.at, self.buf, self.slot, self.own = at, buf, slot, own
        self.send_sems, self.recv_sems = sems
        self.rows = buf.shape[1] // CHUNKS

    def copy(self, j, h, step, k, own=False):
        window = pl.ds(h * self.rows, self.rows)
        home = self.buf.at[self.slot(j), window]
        src = self.own.at[window] if own and self.own is not None else home
        return pltpu.make_async_remote_copy(
            src_ref=src,
            dst_ref=home,
            send_sem=self.send_sems.at[k * CHUNKS + h],
            recv_sem=self.recv_sems.at[j * CHUNKS + h],
            device_id=line_peer(self.at, step),
            device_id_type=MESH,
        )

    def own_each(self, act):
        z, n = self.at.chip, self.at.chips
        for h in range(CHUNKS):

            @pl.when(z < n - 1)
            def _():
                act(self.copy(z, h, 1, z, own=True))

            @pl.when(z > 0)
            def _():
                act(self.copy(z, h, -1, n, own=True))

    def start(self):
        self.own_each(lambda copy: copy.start())

    def arrive_chunk(self, j, h):
        step = jnp.where(j < self.at.chip, 1, -1)
        self.copy(j, h, -step, j).wait_recv()

        @pl.when(goes_on(self.at, j))
        def _():
            self.copy(j, h, step, j).start()

    def arrive(self, order, t):
        if t == 0:

            @pl.when(self.at.inside())
            def _():
                for h in range(CHUNKS):
                    self.arrive_chunk(order[0], h)
                    self.arrive_chunk(order[1], h)

        if t < 2:

            @pl.when(jnp.logical_not(self.at.inside()))
            def _():
                for h in range(CHUNKS):
                    self.arrive_chunk(order[t], h)

        else:
            for h in range(CHUNKS):
                self.arrive_chunk(order[t], h)

    def drain(self, order):
        self.own_each(lambda copy: copy.wait_send())
        for j in order:
            step = jnp.where(j < self.at.chip, 1, -1)

            @pl.when(goes_on(self.at, j))
            def _():
                for h in range(CHUNKS):
                    self.copy(j, h, step, j).wait_send()


class LineReduce:
    def __init__(self, at, part, got, sems):
        self.at, self.part, self.got = at, part, got
        self.send_sems, self.recv_sems = sems
        self.rows = part.shape[1] // CHUNKS

    def copy(self, j, h):
        z, n = self.at.chip, self.at.chips
        window = pl.ds(h * self.rows, self.rows)
        slot = jnp.where(z + 1 == j, n, j)
        return pltpu.make_async_remote_copy(
            src_ref=self.part.at[j, window],
            dst_ref=self.got.at[slot, window],
            send_sem=self.send_sems.at[j * CHUNKS + h],
            recv_sem=self.recv_sems.at[slot * CHUNKS + h],
            device_id=line_peer(self.at, jnp.where(j < z, -1, 1)),
            device_id_type=MESH,
        )

    def landed(self, slot, h, step):
        window = pl.ds(h * self.rows, self.rows)
        return pltpu.make_async_remote_copy(
            src_ref=self.got.at[slot, window],
            dst_ref=self.got.at[slot, window],
            send_sem=self.send_sems.at[h],
            recv_sem=self.recv_sems.at[slot * CHUNKS + h],
            device_id=line_peer(self.at, step),
            device_id_type=MESH,
        )

    def send(self, j):
        for h in range(CHUNKS):
            self.copy(j, h).start()

    def send_last(self, j):
        @pl.when(jnp.logical_not(goes_on(self.at, j)))
        def _():
            self.send(j)

    def pass_chunk(self, j, h):
        wide = jnp.float32
        step = jnp.where(j < self.at.chip, 1, -1)
        self.landed(j, h, step).wait_recv()
        window = pl.ds(h * self.rows, self.rows)
        total = self.part[j, window].astype(wide) + self.got[j, window].astype(wide)
        self.part[j, window] = total.astype(self.part.dtype)
        self.copy(j, h).start()

    def pass_on(self, order):
        @pl.when(self.at.inside())
        def _():
            for h in range(CHUNKS):
                for j in order:
                    self.pass_chunk(j, h)

    def clear(self):
        z, n = self.at.chip, self.at.chips

        @pl.when(z == n - 1)
        def _():
            self.got[z] = jnp.zeros(self.got.shape[1:], self.got.dtype)

        @pl.when(z == 0)
        def _():
            self.got[n] = jnp.zeros(self.got.shape[1:], self.got.dtype)

    def collect(self):
        z, n = self.at.chip, self.at.chips
        for h in range(CHUNKS):

            @pl.when(z < n - 1)
            def _():
                self.landed(z, h, 1).wait_recv()

            @pl.when(z > 0)
            def _():
                self.landed(n, h, -1).wait_recv()

        return self.got[z].astype(jnp.float32) + self.got[n].astype(jnp.float32)

    def drain(self, order):
        for j in order:
            for h in range(CHUNKS):
                self.copy(j, h).wait_send()


def gather_sems(chips):
    return [
        pltpu.SemaphoreType.DMA(((chips + 1) * CHUNKS,)),
        pltpu.SemaphoreType.DMA((chips * CHUNKS,)),
    ]


def reduce_sems(chips):
    return [
        pltpu.SemaphoreType.DMA((chips * CHUNKS,)),
        pltpu.SemaphoreType.DMA(((chips + 1) * CHUNKS,)),
    ]


def gather_kernel(
    x_ref, wq_ref, wk_ref, wv_ref, mix_ref, table_ref, vec_ref, up_ref, down_ref,
    xs_ref, qkvs_ref, mixs_ref, tables_ref, vecs_ref, up2_ref, down2_ref,
    line_send, line_recv, *sems,
):
    at = Place()
    wires = Wires(*sems)
    b, s, z, c = at.row, at.part, at.chip, at.core
    off_diagonal = b != z
    turned = (z, 2 * b + c)
    peers = at.seq_peers() + at.row_peers()
    barrier = pltpu.get_barrier_semaphore()
    for peer in peers:
        pl.semaphore_signal(barrier, inc=1, device_id=peer, device_id_type=MESH)

    @pl.when(off_diagonal)
    def _():
        pl.semaphore_signal(barrier, inc=1, device_id=turned, device_id_type=MESH)

    pl.semaphore_wait(barrier, len(peers) + off_diagonal.astype(jnp.int32))

    swaps, stays = [], []
    for i, ref in enumerate((wq_ref, wk_ref, wv_ref)):
        k = wires.used[0]
        wires.used[0] += 1
        swaps.append(
            pltpu.make_async_remote_copy(
                src_ref=ref,
                dst_ref=qkvs_ref.at[2 * z + c, i],
                send_sem=sems[0].at[k],
                recv_sem=sems[1].at[k],
                device_id=turned,
                device_id_type=MESH,
            )
        )
        stays.append(pltpu.make_async_copy(ref, qkvs_ref.at[2 * b + c, i], sems[2].at[i]))
        wires.used[1] += 1

    @pl.when(off_diagonal)
    def _():
        for swap in swaps:
            swap.start()

    @pl.when(jnp.logical_not(off_diagonal))
    def _():
        for stay in stays:
            stay.start()

    table_home = tables_ref.at[c, b, z]
    mix_home = mixs_ref.at[c, b, z]
    table_sends = [
        wires.send(table_ref, table_home, at.along_chips(k)[1]) for k in range(1, at.chips)
    ]
    kept = [wires.local(table_ref, table_home), wires.local(mix_ref, mix_home)]
    line = LineGather(at, xs_ref, lambda j: 2 * j + c, (line_send, line_recv), own=x_ref)
    line.start()
    last = [wires.send(vec_ref, vecs_ref.at[s], at.along_seq(k)[1]) for k in range(1, at.tokens)]
    mix_sends = [
        wires.send(mix_ref, mix_home, at.along_chips(k)[1]) for k in range(1, at.chips)
    ]
    last += [
        wires.send(x_ref, xs_ref.at[s], at.partner()),
        wires.send(up_ref, up2_ref, at.partner()),
        wires.send(down_ref, down2_ref, at.partner()),
    ]
    own = [
        wires.local(x_ref, xs_ref.at[s]),
        wires.local(vec_ref, vecs_ref.at[s]),
    ]

    @pl.when(off_diagonal)
    def _():
        for swap in swaps:
            swap.wait_recv()

    @pl.when(jnp.logical_not(off_diagonal))
    def _():
        for stay in stays:
            stay.wait()

    mine = qkvs_ref.at[2 * b + c]
    qkv_sends = [wires.send(mine, mine, at.along_rows(k)[1]) for k in range(1, at.batches)]
    last.append(wires.send(mine, mine, at.partner()))
    for copy in table_sends:
        copy.wait_recv()
    for copy in kept:
        copy.wait()
    mine = tables_ref.at[c, b]
    row_sends = [wires.send(mine, mine, at.along_rows(k)[1]) for k in range(1, at.batches)]
    last.append(wires.send(mine, mine, at.partner()))
    order = arrival_order(at)

    def arrived(t):
        line.arrive(order, t)
        home = xs_ref.at[2 * order[t] + c]
        last.append(wires.send(home, home, at.partner()))

    arrived(0)
    for copy in mix_sends:
        copy.wait_recv()
    mine = mixs_ref.at[c, b]
    mix_rows = [wires.send(mine, mine, at.along_rows(k)[1]) for k in range(1, at.batches)]
    last.append(wires.send(mine, mine, at.partner()))
    arrived(1)
    for k in range(1, at.batches):
        qkv_sends[k - 1].wait_recv()
        home = qkvs_ref.at[2 * at.from_rows(k) + c]
        last.append(wires.send(home, home, at.partner()))
    for k in range(1, at.batches):
        row_sends[k - 1].wait_recv()
        home = tables_ref.at[c, at.from_rows(k)]
        last.append(wires.send(home, home, at.partner()))
    for t in range(2, at.chips - 1):
        arrived(t)
    for k in range(1, at.batches):
        mix_rows[k - 1].wait_recv()
        home = mixs_ref.at[c, at.from_rows(k)]
        last.append(wires.send(home, home, at.partner()))
    for copy in last:
        copy.wait_recv()
    for copy in own:
        copy.wait()
    wires.finish()
    line.drain(order)

    @pl.when(off_diagonal)
    def _():
        for swap in swaps:
            swap.wait_send()


def gather_inputs(x, w_query, w_key, w_value, w_mix, rel_table, vec, up, down):
    tokens, batches = lax.axis_size("seq"), lax.axis_size("batch")
    chips = tokens // 2
    outs = (
        like(x, tokens),
        like(w_query, tokens, 3),
        like(w_mix, 2, batches, chips),
        like(rel_table, 2, batches, chips),
        like(vec, tokens),
        like(up),
        like(down),
    )
    sends = 3 + 2 * (chips - 1) + tokens - 1 + 3 + 6 * (batches - 1) + 3 + chips - 1
    inputs = (x, w_query, w_key, w_value, w_mix, rel_table, vec, up, down)
    return comm_call(
        gather_kernel,
        "gather_inputs",
        0,
        outs,
        inputs,
        sends,
        7,
        scratch=gather_sems(chips),
        spec=HBM_SPEC,
    )


def norm_parts(values):
    average = jnp.mean(values, axis=-1, keepdims=True)
    centered = values - average
    variance = jnp.mean(centered * centered, axis=-1, keepdims=True)
    scale = lax.rsqrt(variance + norm_eps)
    return centered * scale, scale


def norm_back(grad, gain, unit, scale):
    inner = grad * gain
    mean = jnp.mean(inner, axis=-1, keepdims=True)
    slope = jnp.mean(inner * unit, axis=-1, keepdims=True)
    return scale * (inner - mean - unit * slope)


def line_pass(gather, reduce, order, work):
    for t, j in enumerate(order):
        gather.arrive(order, t)
        work(j)
        reduce.send_last(j)


def feed_kernel(
    ctx_ref, x_ref, mixs_ref, vecs_ref, up_ref, down_ref, up2_ref, down2_ref, out_grad_ref,
    output_ref, pre_grad_ref, sums_ref, attn_ref, mix_ref, ups_ref, downs_ref, upbs_ref,
    got_ref, hid_ref, act_ref, slope_ref, part_ref, ffn_ref, grad_ref, inner_ref,
    back_ref, backs_ref, up_acc_ref, down_acc_ref, up_away_ref, down_away_ref, upb_away_ref,
    up_got_ref, down_got_ref, upb_got_ref, upg_ref, downg_ref, upb_ref, vec_ref,
    hid_send, hid_recv, ffn_send, ffn_recv, grad_send, grad_recv, back_send, back_recv,
    attn_send, attn_recv, *sems,
):
    at = Place()
    wires = Wires(*sems)
    low, wide = jnp.bfloat16, jnp.float32
    b, s, z, c = at.row, at.part, at.chip, at.core
    order, returns = arrival_order(at), return_order(at)
    meet(at.seq_peers() + at.row_peers())
    last, own = [], []
    swaps = []
    for k in range(1, at.tokens):
        part, peer = at.along_seq(k)
        swaps.append(wires.send(ctx_ref.at[part], got_ref.at[s], peer))
    kept = wires.local(ctx_ref.at[s], got_ref.at[s])
    lanes = x_ref.shape[1] // at.tokens
    hidden_here = up_ref.shape[1]
    vec_ref[...] = jnp.concatenate(
        [vecs_ref[part, :, :lanes].astype(wide) for part in range(at.tokens)], axis=1
    )
    bias3 = vec_ref[3:4]
    gain1, gain2 = vec_ref[4:5], vec_ref[5:6]
    shift1, shift2 = vec_ref[6:7], vec_ref[7:8]
    bias_down = vec_ref[8:9]
    partner = s + 1 - 2 * c
    up_rows = hidden_here // BLOCK
    bias_up = jnp.concatenate(
        [vecs_ref[s, 10 + i : 11 + i].astype(wide) for i in range(up_rows)]
        + [vecs_ref[partner, 10 + i : 11 + i].astype(wide) for i in range(up_rows)],
        axis=1,
    )
    shard_rows = mixs_ref.shape[3]
    for part in range(at.tokens):
        mix_ref[part * shard_rows : (part + 1) * shard_rows] = jnp.concatenate(
            [mixs_ref[part % 2, row, part // 2] for row in range(at.batches)], axis=1
        )
    for copy in swaps:
        copy.wait_recv()
    kept.wait()
    pieces = []
    for chip in range(at.chips):
        left, right = got_ref[2 * chip], got_ref[2 * chip + 1]
        middle = left[:, DH:].astype(wide) + right[:, :DH].astype(wide)
        pieces += [left[:, :DH], middle.astype(low), right[:, DH:]]
    context = jnp.concatenate(pieces, axis=1)
    pre_norm = x_ref[...].astype(wide) + dot_nn(context, mix_ref[...]) + bias3
    unit1, scale1 = norm_parts(pre_norm)
    hidden = unit1 * gain1 + shift1
    hid_ref[z] = hidden.astype(low)
    hid_line = LineGather(at, hid_ref, lambda j: j, (hid_send, hid_recv))
    ffn_line = LineReduce(at, part_ref, ffn_ref, (ffn_send, ffn_recv))
    hid_line.start()
    ffn_line.clear()

    def ffn(chip):
        rows = hid_ref[chip]
        inner = jnp.concatenate(
            [dot_nn(rows, up_ref[...]), dot_nn(rows, up2_ref[...])], axis=1
        )
        inner = inner + bias_up
        cdf = 0.5 * (1.0 + lax.erf(inner * math.sqrt(0.5)))
        act = (inner * cdf).astype(low)
        slope_ref[chip] = cdf + inner * (
            jnp.exp(-0.5 * inner * inner) * (1.0 / math.sqrt(2.0 * math.pi))
        )
        act_ref[chip] = act
        part_ref[chip] = (
            dot_nn(act[:, :hidden_here], down_ref[...])
            + dot_nn(act[:, hidden_here:], down2_ref[...])
        ).astype(low)

    ffn(z)
    line_pass(hid_line, ffn_line, order, ffn)
    ffn_line.pass_on(returns[:1])
    ffn_line.pass_on(returns[1:])
    total = part_ref[z].astype(wide) + ffn_line.collect()
    mixed = hidden + total + bias_down
    unit2, scale2 = norm_parts(mixed)
    output_ref[...] = (unit2 * gain2 + shift2).astype(low)
    out_grad = out_grad_ref[...].astype(wide)
    mixed_grad = norm_back(out_grad, gain2, unit2, scale2)
    grad_ref[z] = mixed_grad.astype(low)
    grad_line = LineGather(at, grad_ref, lambda j: j, (grad_send, grad_recv))
    back_line = LineReduce(at, back_ref, backs_ref, (back_send, back_recv))
    grad_line.start()
    back_line.clear()
    gain2_grad = jnp.sum(out_grad * unit2, axis=0, keepdims=True)
    shift2_grad = jnp.sum(out_grad, axis=0, keepdims=True)
    downb_grad = jnp.sum(mixed_grad, axis=0, keepdims=True)

    def back(chip):
        rows = grad_ref[chip]
        act_grad = jnp.concatenate(
            [dot_nt(rows, down_ref[...]), dot_nt(rows, down2_ref[...])], axis=1
        )
        inner_low = (act_grad * slope_ref[chip]).astype(low)
        inner_ref[chip] = inner_low
        back_ref[chip] = (
            dot_nt(inner_low[:, :hidden_here], up_ref[...])
            + dot_nt(inner_low[:, hidden_here:], up2_ref[...])
        ).astype(low)

    def weight_grads(chip):
        up_acc_ref[...] += dot_tn(hid_ref[chip], inner_ref[chip])
        down_acc_ref[...] += dot_tn(grad_ref[chip], act_ref[chip])

    back(z)
    up_acc_ref[...] = dot_tn(hid_ref[z], inner_ref[z])
    down_acc_ref[...] = dot_tn(grad_ref[z], act_ref[z])
    line_pass(grad_line, back_line, order, back)
    back_line.pass_on(returns[:1])
    back_line.pass_on(returns[1:])
    for j in order:
        weight_grads(j)
    width = x_ref.shape[1]
    columns = width // at.batches
    inner_all = inner_ref[...].reshape(at.chips * BLOCK, 2 * hidden_here)
    near, away = slice(0, hidden_here), slice(hidden_here, 2 * hidden_here)
    up_away_ref[...] = up_acc_ref[:, away].astype(low)
    down_away_ref[...] = down_acc_ref[:, away].astype(low)
    upb_grad = jnp.sum(inner_all.astype(wide), axis=0, keepdims=True)
    upb_away_ref[...] = jnp.broadcast_to(upb_grad[:, away], upb_away_ref.shape)
    halves = [
        wires.send(up_away_ref, up_got_ref, at.partner()),
        wires.send(down_away_ref, down_got_ref, at.partner()),
        wires.send(upb_away_ref, upb_got_ref, at.partner()),
    ]
    for copy in halves:
        copy.wait_recv()
    upb_ref[...] = jnp.broadcast_to(upb_grad[:, near], upb_ref.shape) + upb_got_ref[...]
    up_sum = (up_acc_ref[:, near] + up_got_ref[...].astype(wide)).astype(low)
    down_sum = (down_acc_ref[:, near] + down_got_ref[...].astype(wide)).astype(low)
    for row in range(at.batches):
        upg_ref[row] = up_sum[row * columns : (row + 1) * columns]
        downg_ref[row] = down_sum[row * columns : (row + 1) * columns]
    for k in range(1, at.batches):
        row, peer = at.along_rows(k)
        last.append(wires.send(upg_ref.at[row], ups_ref.at[b], peer))
        last.append(wires.send(downg_ref.at[row], downs_ref.at[b], peer))
        last.append(wires.send(upb_ref, upbs_ref.at[b], peer))
    own.append(wires.local(upg_ref.at[b], ups_ref.at[b]))
    own.append(wires.local(downg_ref.at[b], downs_ref.at[b]))
    own.append(wires.local(upb_ref, upbs_ref.at[b]))
    total = back_ref[z].astype(wide) + back_line.collect()
    hidden_grad = mixed_grad + total
    pre_grad = norm_back(hidden_grad, gain1, unit1, scale1)
    attn_ref[s] = pre_grad.astype(low)
    attn_line = LineGather(at, attn_ref, lambda j: 2 * j + c, (attn_send, attn_recv))
    attn_line.start()
    last.append(wires.send(attn_ref.at[s], attn_ref.at[s], at.partner()))
    pre_grad_ref[...] = pre_grad
    gain1_grad = jnp.sum(hidden_grad * unit1, axis=0, keepdims=True)
    shift1_grad = jnp.sum(hidden_grad, axis=0, keepdims=True)
    bias3_grad = jnp.sum(pre_grad, axis=0, keepdims=True)
    sums = jnp.concatenate(
        [bias3_grad, gain1_grad, gain2_grad, shift1_grad, shift2_grad, downb_grad]
        + [jnp.zeros((2, width), wide)],
        axis=0,
    )
    spare = jnp.zeros((8, BLOCK - lanes), wide)
    for part in range(at.tokens):
        sums_ref[part] = jnp.concatenate(
            [sums[:, part * lanes : (part + 1) * lanes], spare], axis=1
        )
    for t, j in enumerate(order):
        attn_line.arrive(order, t)
        home = attn_ref.at[2 * j + c]
        last.append(wires.send(home, home, at.partner()))
    for copy in last:
        copy.wait_recv()
    for copy in own:
        copy.wait()
    wires.finish()
    for line in (hid_line, ffn_line, grad_line, back_line, attn_line):
        line.drain(order)


def feed_forward(ctx, x, mixs, vecs, up, down, up2, down2, out_grad, ident):
    tokens, batches = lax.axis_size("seq"), lax.axis_size("batch")
    chips = tokens // 2
    width = x.shape[1]
    columns = width // batches
    hidden_here = up.shape[1]
    low, wide = jnp.bfloat16, jnp.float32
    outs = (
        jax.ShapeDtypeStruct(x.shape, low),
        jax.ShapeDtypeStruct(x.shape, wide),
        jax.ShapeDtypeStruct((tokens, 8, BLOCK), wide),
        jax.ShapeDtypeStruct((tokens,) + x.shape, low),
        jax.ShapeDtypeStruct((width, width), low),
        jax.ShapeDtypeStruct((batches, columns, hidden_here), low),
        jax.ShapeDtypeStruct((batches, columns, hidden_here), low),
        jax.ShapeDtypeStruct((batches, 8, hidden_here), wide),
    )
    block = (chips,) + x.shape
    wide_block = (chips, x.shape[0], 2 * hidden_here)
    slots = (chips + 1,) + x.shape
    up_half, bias_half = (width, hidden_here), (8, hidden_here)
    down_half = up_half
    scratch = [
        pltpu.VMEM(ctx.shape, low),
        pltpu.VMEM(block, low),
        pltpu.VMEM(wide_block, low),
        pltpu.VMEM(wide_block, wide),
        pltpu.VMEM(block, low),
        pltpu.VMEM(slots, low),
        pltpu.VMEM(block, low),
        pltpu.VMEM(wide_block, low),
        pltpu.VMEM(block, low),
        pltpu.VMEM(slots, low),
        pltpu.VMEM((width, 2 * hidden_here), wide),
        pltpu.VMEM((width, 2 * hidden_here), wide),
        pltpu.VMEM(up_half, low),
        pltpu.VMEM(down_half, low),
        pltpu.VMEM(bias_half, wide),
        pltpu.VMEM(up_half, low),
        pltpu.VMEM(down_half, low),
        pltpu.VMEM(bias_half, wide),
        pltpu.VMEM((batches, columns, hidden_here), low),
        pltpu.VMEM((batches, columns, hidden_here), low),
        pltpu.VMEM(bias_half, wide),
        pltpu.VMEM((16, width), wide),
    ]
    scratch += (gather_sems(chips) + reduce_sems(chips)) * 2 + gather_sems(chips)
    inputs = (ctx, x, mixs, vecs, up, down, up2, down2, out_grad)
    sends = tokens - 1 + 2 * batches - 1 + 3 + 3 * (batches - 1) + chips
    return pl.pallas_call(
        feed_kernel,
        out_shape=outs,
        in_specs=[VMEM_SPEC] * len(inputs),
        out_specs=(VMEM_SPEC,) * len(outs),
        scratch_shapes=scratch + wire_scratch(sends, 5),
        compiler_params=pltpu.CompilerParams(
            collective_id=ident, has_side_effects=True, vmem_limit_bytes=FEED_VMEM
        ),
        name="feed_forward",
    )(*inputs)


def settle_kernel(
    q_ref, k_ref, v_ref, qrev_ref, krev_ref, p_ref, mix_all_rows_ref,
    vec_ref, w_ref, xs_ref, table_ref, ctx_ref, attn_ref,
    ins_ref, vec_all_ref, cols_ref, dw_all_ref, tab_all_ref, mix_all_ref,
    in_ref, dw_ref, tab_ref, mix_ref, half_ref, sum_ref, got_ref, vecs_ref, vec_low_ref,
    dws_ref, dw_low_ref, rels_ref, rel_low_ref, mixs_ref, mix_low_ref,
    dcat_ref, rel_ref, col_ref, heads_ref, wide_ref, low_ref, place_ref, dq_ref, dkt_ref,
    dvt_ref, far_ref, dkr_ref, dqr_ref,
    line_send, line_recv, tab_send, tab_recv, *sems,
):
    at = Place()
    wires = Wires(*sems)
    low, wide = jnp.bfloat16, jnp.float32
    b, s, z, c = at.row, at.part, at.chip, at.core
    off_diagonal = b != z
    same, cross = (z, 2 * b + c), (z, 2 * b + 1 - c)
    peers = at.all_peers()
    barrier = pltpu.get_barrier_semaphore()
    for peer in peers:
        pl.semaphore_signal(barrier, inc=1, device_id=peer, device_id_type=MESH)
    attend_back_kernel(
        q_ref, k_ref, v_ref, qrev_ref, krev_ref, p_ref, mix_all_rows_ref, attn_ref,
        dcat_ref, rel_ref, col_ref, heads_ref, wide_ref, low_ref, place_ref, dq_ref, dkt_ref,
        dvt_ref, far_ref, dkr_ref, dqr_ref,
    )
    pl.semaphore_wait(barrier, len(peers))
    width = w_ref.shape[0]
    columns = width // at.batches
    full_len = dcat_ref.shape[0]
    group = 2 * DH
    buckets = table_ref.shape[0]
    bucket_rows = buckets // at.batches

    dw_sends, mix_sends, vec_sends, rel_sends, last, own = [], [], [], [], [], []
    for k in range(1, at.batches):
        row, peer = at.along_rows(k)
        rows = pl.ds(pl.multiple_of(row * bucket_rows, bucket_rows), bucket_rows)
        rel_sends.append(wires.send(rel_ref.at[rows], rels_ref.at[k - 1], peer))

    for k in range(1, at.tokens):
        part, peer = at.along_seq(k)
        vec_sends.append(wires.send(vec_ref.at[part], vecs_ref.at[k - 1], peer))
    mine = 2 * b + c
    for k in range(1, 2 * at.batches):
        last.append(wires.send(col_ref, cols_ref.at[mine], at.along_plane(k)[2]))
    own.append(wires.local(col_ref, cols_ref.at[mine]))

    def input_part(chip, core):
        start = pl.multiple_of((2 * chip + core) * BLOCK, BLOCK)
        in_ref[chip, core] = dot_nt(dcat_ref[pl.ds(start, BLOCK)], w_ref[...]).astype(low)

    order = far_order(at)
    places = order + [z]
    halves = []
    for chip in places:
        input_part(chip, 1 - c)
        halves.append(wires.send(in_ref.at[chip, 1 - c], half_ref.at[chip], at.partner()))
    line = LineReduce(at, sum_ref, got_ref, (line_send, line_recv))
    line.clear()
    for i, chip in enumerate(places):
        input_part(chip, c)
        halves[i].wait_recv()
        total = in_ref[chip, c].astype(wide) + half_ref[chip].astype(wide)
        sum_ref[chip] = total.astype(low)
        if i < len(order):
            line.send_last(chip)

    whole = xs_ref[...].reshape(full_len, width)
    dw = dot_tn(whole, dcat_ref[...])
    dw_rel = dot_tn(table_ref[...], rel_ref[...])
    dw = jnp.concatenate([dw[:, : 2 * group] + dw_rel, dw[:, 2 * group :]], axis=1)
    for row in range(at.batches):
        dw_ref[row] = dw[row * columns : (row + 1) * columns].astype(low)
    for k in range(1, at.batches):
        row, peer = at.along_rows(k)
        dw_sends.append(wires.send(dw_ref.at[row], dws_ref.at[k - 1], peer))

    rows = pl.ds(pl.multiple_of(b * bucket_rows, bucket_rows), bucket_rows)
    total = rel_ref[rows].astype(wide)
    for k in range(1, at.batches):
        rel_sends[k - 1].wait_recv()
        total = total + rels_ref[k - 1].astype(wide)
    rel_low_ref[...] = total.astype(low)
    table_rows = bucket_rows // 2
    for row in range(at.batches):
        piece = dot_nt(rel_low_ref[...], w_ref[row * columns : (row + 1) * columns, : 2 * group])
        for core in range(2):
            tab_ref[core, row] = piece[core * table_rows : (core + 1) * table_rows].astype(low)

    def tab_copy(k, d):
        row = lax.rem(b + k, at.batches)
        core = jnp.where(d == 0, c, 1 - c)
        return pltpu.make_async_remote_copy(
            src_ref=tab_ref.at[core, row],
            dst_ref=tab_all_ref.at[s],
            send_sem=tab_send.at[2 * k + d],
            recv_sem=tab_recv.at[s],
            device_id=(row, 2 * b + core),
            device_id_type=MESH,
        )

    tab_stay = pltpu.make_async_copy(
        tab_ref.at[c, b], tab_all_ref.at[s], sems[2].at[wires.used[1]]
    )
    wires.used[1] += 1
    for k in range(at.batches):
        for d in range(2):
            if k or d:
                tab_copy(k, d).start()

    @pl.when(off_diagonal)
    def _():
        tab_copy(0, 0).start()

    @pl.when(jnp.logical_not(off_diagonal))
    def _():
        tab_stay.start()

    line.pass_on(order[:1])
    mix = dot_tn(
        ctx_ref[...].reshape(full_len, group), attn_ref[...].reshape(full_len, width)
    )
    for row in range(at.batches):
        mix_ref[row] = mix[:, row * columns : (row + 1) * columns].astype(low)
    for k in range(1, at.batches):
        row, peer = at.along_rows(k)
        mix_sends.append(wires.send(mix_ref.at[row], mixs_ref.at[k - 1], peer))

    line.pass_on(order[1:])
    total = dw_ref[b].astype(wide)
    for k in range(1, at.batches):
        dw_sends[k - 1].wait_recv()
        total = total + dws_ref[k - 1].astype(wide)
    shard_rows = dw_low_ref.shape[1]
    for half in range(2):
        dw_low_ref[half] = total[half * shard_rows : (half + 1) * shard_rows].astype(low)
    k = wires.used[0]
    wires.used[0] += 1
    move = pltpu.make_async_remote_copy(
        src_ref=dw_low_ref.at[c],
        dst_ref=dw_all_ref.at[c],
        send_sem=sems[0].at[k],
        recv_sem=sems[1].at[k],
        device_id=same,
        device_id_type=MESH,
    )
    stay = pltpu.make_async_copy(
        dw_low_ref.at[c], dw_all_ref.at[c], sems[2].at[wires.used[1]]
    )
    wires.used[1] += 1

    @pl.when(off_diagonal)
    def _():
        move.start()

    @pl.when(jnp.logical_not(off_diagonal))
    def _():
        stay.start()

    last.append(wires.send(dw_low_ref.at[1 - c], dw_all_ref.at[c], cross))

    total = mix_ref[b].astype(wide)
    for k in range(1, at.batches):
        mix_sends[k - 1].wait_recv()
        total = total + mixs_ref[k - 1].astype(wide)
    mix_low_ref[...] = total.astype(low)
    last.append(wires.send(mix_low_ref, mix_all_ref.at[c], at.partner()))
    own.append(wires.local(mix_low_ref, mix_all_ref.at[c]))

    total = vec_ref[s]
    for k in range(1, at.tokens):
        vec_sends[k - 1].wait_recv()
        total = total + vecs_ref[k - 1]
    vec_low_ref[...] = total
    for k in range(1, at.batches):
        last.append(wires.send(vec_low_ref, vec_all_ref.at[b], at.along_rows(k)[1]))
    own.append(wires.local(vec_low_ref, vec_all_ref.at[b]))

    ins_ref[...] = sum_ref[z].astype(wide) + line.collect()
    for copy in last:
        copy.wait_recv()
    for copy in own:
        copy.wait()
    wires.finish()
    line.drain(order)
    for part in range(at.tokens):
        landed = pltpu.make_async_remote_copy(
            src_ref=tab_all_ref.at[part],
            dst_ref=tab_all_ref.at[part],
            send_sem=tab_send.at[0],
            recv_sem=tab_recv.at[part],
            device_id=at.partner(),
            device_id_type=MESH,
        )

        @pl.when(jnp.logical_or(off_diagonal, s != part))
        def _():
            landed.wait_recv()

    for k in range(at.batches):
        for d in range(2):
            if k or d:
                tab_copy(k, d).wait_send()

    @pl.when(off_diagonal)
    def _():
        tab_copy(0, 0).wait_send()
        move.wait()

    @pl.when(jnp.logical_not(off_diagonal))
    def _():
        tab_stay.wait()
        stay.wait()


def settle_grads(q, k, v, qrev, krev, probs, m_mix, vec, w_cat, xs, table, ctx, attn_all, ident):
    tokens, batches = lax.axis_size("seq"), lax.axis_size("batch")
    chips = tokens // 2
    low, wide = jnp.bfloat16, jnp.float32
    local_len, width = xs.shape[1:]
    columns, group = width // batches, 6 * DH
    buckets = table.shape[0]
    full_len = tokens * local_len
    band_width = buckets + BLOCK
    pad_blocks = full_len // BLOCK + band_width // BLOCK - 1
    half = (chips, local_len, width)
    dw_pieces = (2, columns // 2, group)
    mix_piece = (2 * DH, columns)
    dw_piece, rel_piece = (columns, group), (buckets // batches, 4 * DH)
    outs = (
        jax.ShapeDtypeStruct((local_len, width), wide),
        jax.ShapeDtypeStruct((batches,) + vec.shape[1:], wide),
        jax.ShapeDtypeStruct((2 * batches, 8, group), wide),
        jax.ShapeDtypeStruct(dw_pieces, low),
        jax.ShapeDtypeStruct((tokens, buckets // tokens, columns), low),
        jax.ShapeDtypeStruct((2,) + mix_piece, low),
    )
    scratch = [
        pltpu.VMEM((chips, 2, local_len, width), low),
        pltpu.VMEM((batches,) + dw_piece, low),
        pltpu.VMEM((2, batches, buckets // tokens, columns), low),
        pltpu.VMEM((batches,) + mix_piece, low),
        pltpu.VMEM(half, low),
        pltpu.VMEM(half, low),
        pltpu.VMEM((chips + 1, local_len, width), low),
        pltpu.VMEM((tokens - 1,) + vec.shape[1:], wide),
        pltpu.VMEM(vec.shape[1:], wide),
        pltpu.VMEM((batches - 1,) + dw_piece, low),
        pltpu.VMEM(dw_pieces, low),
        pltpu.VMEM((batches - 1,) + rel_piece, low),
        pltpu.VMEM(rel_piece, low),
        pltpu.VMEM((batches - 1,) + mix_piece, low),
        pltpu.VMEM(mix_piece, low),
        pltpu.VMEM((full_len, group), low),
        pltpu.VMEM((buckets, 4 * DH), low),
        pltpu.VMEM((8, group), wide),
        pltpu.VMEM((2, full_len, DH), low),
        pltpu.VMEM((2, BLOCK, full_len + buckets), wide),
        pltpu.VMEM((2, BLOCK, full_len + buckets), low),
        pltpu.VMEM((2, pad_blocks, BLOCK, band_width), wide),
        pltpu.VMEM((4, full_len, DH), wide),
        pltpu.VMEM((2, DH, full_len), wide),
        pltpu.VMEM((2, DH, full_len), wide),
        pltpu.VMEM((2, 8, full_len), wide),
        pltpu.VMEM((2, DH, buckets), wide),
        pltpu.VMEM((2, DH, buckets), wide),
    ]
    scratch += reduce_sems(chips)
    scratch += [pltpu.SemaphoreType.DMA((2 * batches,)), pltpu.SemaphoreType.DMA((tokens,))]
    sends = 4 * (batches - 1) + chips + tokens - 1 + 2 * batches - 1 + 3
    inputs = (q, k, v, qrev, krev, probs, m_mix, vec, w_cat, xs, table, ctx, attn_all)
    return comm_call(
        settle_kernel,
        "settle_grads",
        ident,
        outs,
        inputs,
        sends,
        6,
        scratch=scratch,
        limit=BACK_VMEM,
    )


def finish_kernel(
    pre_ref, ins_ref, vecs_ref, cols_ref, dws_ref, tabs_ref, mixs_ref, ups_ref, downs_ref,
    upbs_ref, last_ref,
    output_ref, input_ref, dq_ref, dk_ref, dv_ref, mix_ref, table_ref, bias_ref, gain_ref, shift_ref,
    up_ref, upb_ref, down_ref, downb_ref,
):
    at = Place()
    wide = jnp.float32

    def total(ref):
        out = ref[0].astype(wide)
        for k in range(1, ref.shape[0]):
            out = out + ref[k].astype(wide)
        return out

    output_ref[...] = last_ref[...]
    input_ref[...] = pre_ref[...] + ins_ref[...]
    up_ref[...] = total(ups_ref)
    down_ref[...] = total(downs_ref)
    upb_ref[...] = total(upbs_ref)[0:1]
    table_ref[...] = total(tabs_ref)
    group = 2 * DH
    spare = jnp.zeros((dws_ref.shape[1], DH), wide)
    for i, ref in enumerate((dq_ref, dk_ref, dv_ref)):
        lower = dws_ref[0, :, i * group : (i + 1) * group].astype(wide)
        upper = dws_ref[1, :, i * group : (i + 1) * group].astype(wide)
        ref[...] = jnp.concatenate([lower, spare], axis=1) + jnp.concatenate(
            [spare, upper], axis=1
        )
    rows = mix_ref.shape[0]
    lower, upper = mixs_ref[0].astype(wide), mixs_ref[1].astype(wide)
    spare = jnp.zeros((DH, lower.shape[1]), wide)
    whole = jnp.concatenate([lower, spare], axis=0) + jnp.concatenate([spare, upper], axis=0)
    mix_ref[...] = jnp.where(at.core == 0, whole[:rows], whole[rows:])
    small = total(vecs_ref)
    lanes = bias_ref.shape[1]
    cols = [cols_ref[core, 0:1] for core in range(2)]
    for row in range(1, at.batches):
        cols = [cols[core] + cols_ref[2 * row + core, 0:1] for core in range(2)]
    spare = jnp.zeros((1, DH), wide)
    biases = []
    for i in range(3):
        lower, upper = [part[:, i * group : (i + 1) * group] for part in cols]
        both = jnp.concatenate([lower, spare], axis=1) + jnp.concatenate([spare, upper], axis=1)
        biases.append(jnp.where(at.core == 0, both[:, :lanes], both[:, lanes:]))
    bias_ref[...] = jnp.concatenate(biases + [small[0:1, :lanes]], axis=0)
    gain_ref[...] = small[1:3, :lanes]
    shift_ref[...] = small[3:5, :lanes]
    downb_ref[...] = small[5:6, :lanes]


def finish(pre_grad, parts, shapes):
    inputs = (pre_grad,) + tuple(parts)
    return pl.pallas_call(
        finish_kernel,
        out_shape=(like(parts[-1]),)
        + tuple(jax.ShapeDtypeStruct(shape, jnp.float32) for shape in shapes),
        in_specs=[VMEM_SPEC] * len(inputs),
        out_specs=(VMEM_SPEC,) * (len(shapes) + 1),
        compiler_params=pltpu.CompilerParams(vmem_limit_bytes=COMM_VMEM),
        name="finish",
    )(*inputs)


def fits_fast(layer_input, table_shard, hidden_here):
    rows, local_len, width = layer_input.shape
    tokens, batches = lax.axis_size("seq"), lax.axis_size("batch")
    return (
        rows == 1
        and local_len == BLOCK
        and tokens == 2 * batches
        and width == 3 * DH * batches
        and (table_shard.shape[0] * tokens) % (4 * BLOCK) == 0
        and tokens == 8
        and 10 + hidden_here // BLOCK <= 16
        and hidden_here % BLOCK == 0
    )


def fast_body(
    layer_input, segment_ids, w_query, w_key, w_value, w_mix, rel_table, attn_biases,
    norm_gains, norm_shifts, w_up, up_bias, w_down, down_bias, out_grad,
):
    local_len, width = layer_input.shape[1:]
    low = jnp.bfloat16
    shard_rows, shard_cols = w_query.shape
    lanes = attn_biases.shape[1]
    hidden_here = w_up.shape[1]
    x = layer_input[0]
    pack = jnp.concatenate([attn_biases, norm_gains, norm_shifts, down_bias[None]], axis=0)
    pack = jnp.pad(pack, ((0, 0), (0, BLOCK - lanes)))
    pack = jnp.concatenate(
        [pack, segment_ids.astype(low), up_bias.reshape(hidden_here // BLOCK, BLOCK)], axis=0
    )
    pack = jnp.pad(pack, ((0, 16 - pack.shape[0]), (0, 0)))
    weights = (w_query, w_key, w_value, w_mix, rel_table, pack, w_up, w_down)
    xs, qkvs, mixs, tables, vecs, up2, down2 = gather_inputs(
        *[pltpu.with_memory_space_constraint(a, pltpu.HBM) for a in (x,) + weights]
    )
    q, k, v, qrev, krev, probs, ctx, w_cat, table = attend(xs, qkvs, tables, vecs)
    output, pre_grad, sums, attn_all, m_mix, ups, downs, upbs = feed_forward(
        ctx, x, mixs, vecs, w_up, w_down, up2, down2, out_grad[0], 1
    )
    ins, vec_all, cols_all, dw_all, tab_all, mix_all = settle_grads(
        q, k, v, qrev, krev, probs, m_mix, sums, w_cat, xs, table, ctx, attn_all, 2
    )
    shard = (shard_rows, shard_cols)
    shapes = (
        x.shape, shard, shard, shard, shard, rel_table.shape, (4, lanes), (2, lanes), (2, lanes),
        (width // lax.axis_size("batch"), hidden_here), (1, hidden_here),
        (width // lax.axis_size("batch"), hidden_here), (1, lanes),
    )
    grads = finish(
        pre_grad,
        (ins, vec_all, cols_all, dw_all, tab_all, mix_all, ups, downs, upbs, output),
        shapes,
    )
    output, input_grad, dq, dk, dv, dmix, dtable = grads[:7]
    dbias, dgain, dshift, dup, dupb, ddown, ddownb = grads[7:]
    return (
        output[None], input_grad[None], dq, dk, dv, dmix, dtable, dbias, dgain, dshift,
        dup, dupb.reshape(hidden_here), ddown.T, ddownb.reshape(lanes),
    )


def body(
    layer_input,
    segment_ids,
    w_query,
    w_key,
    w_value,
    w_mix,
    rel_table,
    attn_biases,
    norm_gains,
    norm_shifts,
    w_up,
    up_bias,
    w_down,
    down_bias,
    out_grad,
):
    if fits_fast(layer_input, rel_table, w_up.shape[1]):
        return fast_body(
            layer_input, segment_ids, w_query, w_key, w_value, w_mix, rel_table, attn_biases,
            norm_gains, norm_shifts, w_up, up_bias, w_down, down_bias, out_grad,
        )
    rows, local_len, width = layer_input.shape
    full_len = local_len * lax.axis_size("seq")
    tokens_here = local_len * rows
    highest_prec = lax.Precision.HIGHEST
    parts = (
        lax.all_gather(w_query, "batch", axis=1, tiled=True),
        lax.all_gather(w_key, "batch", axis=1, tiled=True),
        lax.all_gather(w_value, "batch", axis=1, tiled=True),
        lax.all_gather(w_mix, "batch", axis=1, tiled=True),
        lax.all_gather(rel_table, "batch", axis=1, tiled=True),
    )
    whole = (
        lax.all_gather(parts[0], "seq", axis=0, tiled=True),
        lax.all_gather(parts[1], "seq", axis=0, tiled=True),
        lax.all_gather(parts[2], "seq", axis=0, tiled=True),
        lax.all_gather(parts[3], "seq", axis=0, tiled=True),
        lax.all_gather(parts[4], "seq", axis=0, tiled=True),
        lax.all_gather(attn_biases, "seq", axis=1, tiled=True),
        lax.all_gather(norm_gains, "seq", axis=1, tiled=True),
        lax.all_gather(norm_shifts, "seq", axis=1, tiled=True),
        lax.all_gather(down_bias, "seq", axis=0, tiled=True),
    )
    m_query, m_key, m_value, m_mix, table, biases, gains, shifts, bias_down = whole
    flat_input = jnp.swapaxes(layer_input, 0, 1).reshape(tokens_here, width)
    queries = (jnp.dot(flat_input, m_query, preferred_element_type=jnp.float32) + biases[0]).astype(
        jnp.bfloat16
    )
    keys_here = (jnp.dot(flat_input, m_key, preferred_element_type=jnp.float32) + biases[1]).astype(
        jnp.bfloat16
    )
    values_here = (
        jnp.dot(flat_input, m_value, preferred_element_type=jnp.float32) + biases[2]
    ).astype(jnp.bfloat16)
    query_rel = (jnp.dot(table, m_query, preferred_element_type=jnp.float32) + biases[0]).astype(
        jnp.bfloat16
    )
    key_rel = (jnp.dot(table, m_key, preferred_element_type=jnp.float32) + biases[1]).astype(
        jnp.bfloat16
    )
    local_seg = jnp.swapaxes(segment_ids, 0, 1).astype(jnp.bfloat16)
    keys_all, values_all, seg_all = (
        lax.all_gather(keys_here.reshape(local_len, rows, width), "seq", axis=0, tiled=True),
        lax.all_gather(values_here.reshape(local_len, rows, width), "seq", axis=0, tiled=True),
        lax.all_gather(local_seg, "seq", axis=0, tiled=True),
    )
    buckets = table.shape[0]
    offset = lax.axis_index("seq") * local_len
    bucket_iota = jnp.arange(buckets, dtype=jnp.int32)
    inner_cols = (bucket_iota > 0) & (bucket_iota < buckets - 1)
    same_doc = (
        jnp.swapaxes(local_seg, 0, 1)[:, None, :, None]
        == jnp.swapaxes(seg_all, 0, 1)[:, None, None, :]
    )
    score_scale = 1.0 / math.sqrt(3.0 * DH)
    head_queries = split_heads(queries.reshape(local_len, rows, width))
    head_keys = split_heads(keys_all)
    head_values = split_heads(values_all)
    rel_queries = split_table(query_rel)
    rel_keys = split_table(key_rel)

    def forward_group(carry, group):
        g_query, g_key, g_value, g_qrel, g_krel = group
        total, near_pull, far_pull, window = relative_scores(
            g_query, g_key, g_krel, g_qrel, offset, full_len
        )
        scores = jnp.where(same_doc, total * score_scale, masked_score)
        highest = jnp.max(scores, axis=-1, keepdims=True)
        exponent = jnp.exp(scores - highest)
        denominator = jnp.sum(exponent, axis=-1, keepdims=True)
        weights_low = (exponent / denominator).astype(jnp.bfloat16)
        context = jnp.einsum(
            "rgij,rgjd->rgid", weights_low, g_value, preferred_element_type=jnp.float32
        )
        return (carry, (context, (highest + jnp.log(denominator))[..., 0]))

    unused, (context_groups, log_totals) = lax.scan(
        forward_group, None, (head_queries, head_keys, head_values, rel_queries, rel_keys)
    )
    context_low = join_heads(context_groups).reshape(tokens_here, width).astype(jnp.bfloat16)
    pre_norm = (
        flat_input.astype(jnp.float32)
        + jnp.dot(context_low, m_mix, preferred_element_type=jnp.float32)
        + biases[3]
    )
    hidden, norm1_pull = jax.vjp(
        normalize, pre_norm, gains[0].astype(jnp.float32), shifts[0].astype(jnp.float32)
    )
    hidden_low = hidden.astype(jnp.bfloat16)

    def spread_rows(rows_low):
        return lax.all_gather(rows_low, "seq", axis=0, tiled=True)

    def hidden_sums(make_term):
        return lax.psum_scatter(
            make_term(jnp.int32(0), tokens_here * lax.axis_size("seq")),
            "seq",
            scatter_dimension=0,
            tiled=True,
        )

    hidden_rows = spread_rows(hidden_low)
    inner = jnp.dot(hidden_rows, w_up, preferred_element_type=jnp.float32) + up_bias
    act, gelu_pull = jax.vjp(exact_gelu, inner)
    act_low = act.astype(jnp.bfloat16)

    def down_rows(start, count):
        return jnp.dot(act_low, w_down, preferred_element_type=jnp.float32)

    ffn_result = hidden_sums(down_rows)
    mixed = hidden + ffn_result + bias_down
    output, norm2_pull = jax.vjp(
        normalize, mixed, gains[1].astype(jnp.float32), shifts[1].astype(jnp.float32)
    )
    flat_grad = jnp.swapaxes(out_grad, 0, 1).reshape(tokens_here, width).astype(jnp.float32)
    mixed_grad, gain2_grad, shift2_grad = norm2_pull(flat_grad)
    ffn_grad_low = mixed_grad.astype(jnp.bfloat16)
    grad_rows = spread_rows(ffn_grad_low)
    act_grad = jnp.einsum("nd,fd->nf", grad_rows, w_down, preferred_element_type=jnp.float32)
    inner_low = gelu_pull(act_grad)[0].astype(jnp.bfloat16)
    up_part = jnp.einsum("nd,nf->df", hidden_rows, inner_low, preferred_element_type=jnp.float32)
    upb_part = jnp.sum(inner_low.astype(jnp.float32), axis=0)
    down_part = jnp.einsum("nf,nd->fd", act_low, grad_rows, preferred_element_type=jnp.float32)

    def back_rows(start, count):
        return jnp.einsum("nf,df->nd", inner_low, w_up, preferred_element_type=jnp.float32)

    hidden_grad = mixed_grad + hidden_sums(back_rows)
    pre_grad, gain1_grad, shift1_grad = norm1_pull(hidden_grad)
    attn_low = pre_grad.astype(jnp.bfloat16)
    mix_whole = jnp.einsum("nd,ne->de", context_low, attn_low, preferred_element_type=jnp.float32)
    context_grad = jnp.einsum(
        "ne,de->nd", attn_low, m_mix, preferred_element_type=jnp.float32
    ).astype(jnp.bfloat16)
    head_context_grad = split_heads(context_grad.reshape(local_len, rows, width))

    def query_side(group):
        g_query, g_key, g_value, g_qrel, g_krel, g_dctx, g_lse = group
        total, near_pull, far_pull, window = relative_scores(
            g_query, g_key, g_krel, g_qrel, offset, full_len
        )
        scores = jnp.where(same_doc, total * score_scale, masked_score)
        weights_now = jnp.exp(scores - g_lse[..., None])
        prob_grad = jnp.einsum(
            "rgid,rgjd->rgij", g_dctx, g_value, preferred_element_type=jnp.float32
        )
        inner_sum = jnp.sum(weights_now * prob_grad, axis=-1)
        score_grad = (weights_now * (prob_grad - inner_sum[..., None])).astype(jnp.bfloat16)
        grad_wide = score_grad.astype(jnp.float32)
        near_grad = near_pull(grad_wide)[0]
        near_low = jnp.where(inner_cols, near_grad, 0.0).astype(jnp.bfloat16)
        near_ends = end_columns(near_grad)
        query_part = jnp.einsum(
            "rgij,rgjd->rgid", score_grad, g_key, preferred_element_type=jnp.float32
        )
        query_part = (
            query_part
            + jnp.einsum("rgib,gbd->rgid", near_low, g_krel, preferred_element_type=jnp.float32)
            + end_terms(near_ends, g_krel)
        )
        krel_part = with_ends(
            jnp.einsum("rgib,rgid->gbd", near_low, g_query, preferred_element_type=jnp.float32),
            end_rows(near_ends, g_query),
        )
        return (
            weights_now,
            score_grad,
            grad_wide,
            far_pull,
            window,
            inner_sum,
            query_part * score_scale,
            krel_part * score_scale,
        )

    query_groups = (
        head_queries,
        head_keys,
        head_values,
        rel_queries,
        rel_keys,
        head_context_grad,
        log_totals,
    )

    def all_grads(carry, group):
        weights_now, score_grad, grad_wide, far_pull, window, inner_sum, query_part, krel_part = (
            query_side(group)
        )
        g_query, g_key, g_value, g_qrel, g_krel, g_dctx, g_lse = group
        cross_grad, end_grad = far_pull(grad_wide)
        cross_low = cross_grad.astype(jnp.bfloat16)
        key_part = jnp.einsum(
            "rgij,rgid->rgjd", score_grad, g_query, preferred_element_type=jnp.float32
        )
        band_part = jnp.einsum(
            "rgmb,gbd->rgmd", cross_low, g_qrel, preferred_element_type=jnp.float32
        )
        key_part = (
            key_part
            + unband(band_part, offset, full_len, buckets // 2)
            + end_terms(end_grad, g_qrel)
        )
        value_part = jnp.einsum(
            "rgij,rgid->rgjd",
            weights_now.astype(jnp.bfloat16),
            g_dctx,
            preferred_element_type=jnp.float32,
        )
        qrel_part = with_ends(
            jnp.einsum("rgmb,rgmd->gbd", cross_low, window, preferred_element_type=jnp.float32),
            end_rows(end_grad, g_key),
        )
        return (
            carry,
            (query_part, key_part * score_scale, value_part, qrel_part * score_scale, krel_part),
        )

    unused, (dq_groups, dk_groups, dv_groups, dqrel_groups, dkrel_groups) = lax.scan(
        all_grads, None, query_groups
    )
    key_sum, value_sum = (
        lax.psum_scatter(join_heads(dk_groups), "seq", scatter_dimension=0, tiled=True),
        lax.psum_scatter(join_heads(dv_groups), "seq", scatter_dimension=0, tiled=True),
    )
    key_grads = key_sum.reshape(tokens_here, width).astype(jnp.bfloat16)
    value_grads = value_sum.reshape(tokens_here, width).astype(jnp.bfloat16)
    query_grads = join_heads(dq_groups).reshape(tokens_here, width).astype(jnp.bfloat16)
    qrel_grad = join_table(dqrel_groups)
    krel_grad = join_table(dkrel_groups)
    input_grad = pre_grad + jnp.einsum(
        "ne,de->nd", query_grads, m_query, preferred_element_type=jnp.float32
    )
    input_grad = input_grad + jnp.einsum(
        "ne,de->nd", key_grads, m_key, preferred_element_type=jnp.float32
    )
    input_grad = input_grad + jnp.einsum(
        "ne,de->nd", value_grads, m_value, preferred_element_type=jnp.float32
    )
    query_whole = jnp.einsum(
        "nd,ne->de", flat_input, query_grads, preferred_element_type=jnp.float32
    ) + jnp.einsum(
        "bd,be->de", table, qrel_grad, precision=highest_prec, preferred_element_type=jnp.float32
    )
    key_whole = jnp.einsum(
        "nd,ne->de", flat_input, key_grads, preferred_element_type=jnp.float32
    ) + jnp.einsum(
        "bd,be->de", table, krel_grad, precision=highest_prec, preferred_element_type=jnp.float32
    )
    value_whole = jnp.einsum(
        "nd,ne->de", flat_input, value_grads, preferred_element_type=jnp.float32
    )
    table_whole = jnp.einsum(
        "be,de->bd", qrel_grad, m_query, precision=highest_prec, preferred_element_type=jnp.float32
    ) + jnp.einsum(
        "be,de->bd", krel_grad, m_key, precision=highest_prec, preferred_element_type=jnp.float32
    )
    bias_whole = jnp.stack(
        [
            jnp.sum(query_grads.astype(jnp.float32), axis=0) + jnp.sum(qrel_grad, axis=0),
            jnp.sum(key_grads.astype(jnp.float32), axis=0) + jnp.sum(krel_grad, axis=0),
            jnp.sum(value_grads.astype(jnp.float32), axis=0),
            jnp.sum(pre_grad, axis=0),
        ]
    )
    gain_whole = jnp.stack([gain1_grad, gain2_grad])
    shift_whole = jnp.stack([shift1_grad, shift2_grad])
    downb_whole = jnp.sum(mixed_grad, axis=0)
    seq_parts = (
        lax.psum_scatter(query_whole, "seq", scatter_dimension=0, tiled=True),
        lax.psum_scatter(key_whole, "seq", scatter_dimension=0, tiled=True),
        lax.psum_scatter(value_whole, "seq", scatter_dimension=0, tiled=True),
        lax.psum_scatter(mix_whole, "seq", scatter_dimension=0, tiled=True),
        lax.psum_scatter(table_whole, "seq", scatter_dimension=0, tiled=True),
        lax.psum_scatter(bias_whole, "seq", scatter_dimension=1, tiled=True),
        lax.psum_scatter(gain_whole, "seq", scatter_dimension=1, tiled=True),
        lax.psum_scatter(shift_whole, "seq", scatter_dimension=1, tiled=True),
        lax.psum_scatter(downb_whole, "seq", scatter_dimension=0, tiled=True),
    )
    batch_parts = (
        lax.psum_scatter(seq_parts[0], "batch", scatter_dimension=1, tiled=True),
        lax.psum_scatter(seq_parts[1], "batch", scatter_dimension=1, tiled=True),
        lax.psum_scatter(seq_parts[2], "batch", scatter_dimension=1, tiled=True),
        lax.psum_scatter(seq_parts[3], "batch", scatter_dimension=1, tiled=True),
        lax.psum_scatter(seq_parts[4], "batch", scatter_dimension=1, tiled=True),
        lax.psum_scatter(up_part, "batch", scatter_dimension=0, tiled=True),
        lax.psum_scatter(down_part, "batch", scatter_dimension=1, tiled=True),
    )
    small_parts = lax.psum(
        (seq_parts[5], seq_parts[6], seq_parts[7], seq_parts[8], upb_part), "batch"
    )
    layer_output = jnp.swapaxes(output.reshape(local_len, rows, width), 0, 1).astype(jnp.bfloat16)
    input_back = jnp.swapaxes(input_grad.reshape(local_len, rows, width), 0, 1)
    return (
        layer_output,
        input_back,
        batch_parts[0],
        batch_parts[1],
        batch_parts[2],
        batch_parts[3],
        batch_parts[4],
        small_parts[0],
        small_parts[1],
        small_parts[2],
        batch_parts[5],
        small_parts[4],
        batch_parts[6],
        small_parts[3],
    )


def solution(mesh):
    return jax.shard_map(
        body,
        mesh=mesh,
        in_specs=(
            P("batch", "seq", None),
            P("batch", "seq"),
            P("seq", "batch"),
            P("seq", "batch"),
            P("seq", "batch"),
            P("seq", "batch"),
            P("seq", "batch"),
            P(None, "seq"),
            P(None, "seq"),
            P(None, "seq"),
            P(None, "seq"),
            P("seq"),
            P("seq", None),
            P("seq"),
            P("batch", "seq", None),
        ),
        out_specs=(
            P("batch", "seq", None),
            P("batch", "seq", None),
            P("seq", "batch"),
            P("seq", "batch"),
            P("seq", "batch"),
            P("seq", "batch"),
            P("seq", "batch"),
            P(None, "seq"),
            P(None, "seq"),
            P(None, "seq"),
            P("batch", "seq"),
            P("seq"),
            P("seq", "batch"),
            P("seq"),
        ),
        check_vma=False,
    )
```

```python
import math

import jax
import jax.numpy as jnp
from jax import lax
from jax.experimental import pallas as pl
from jax.experimental.pallas import tpu as pltpu
from jax.sharding import PartitionSpec as P

DH = 64


masked_score = -1e30
norm_eps = 1e-06
pair_heads = 2


def normalize(values, gain, shift):
    average = jnp.mean(values, axis=-1, keepdims=True)
    centered = values - average
    variance = jnp.mean(centered * centered, axis=-1, keepdims=True)
    return centered * lax.rsqrt(variance + norm_eps) * gain + shift


def exact_gelu(values):
    return jax.nn.gelu(values, approximate=False)


def split_heads(matrix):
    length, rows, width = matrix.shape
    groups = width // (pair_heads * DH)
    return matrix.reshape(length, rows, groups, pair_heads, DH).transpose(2, 1, 3, 0, 4)


def join_heads(matrix):
    groups, rows, pair, length, depth = matrix.shape
    return matrix.transpose(3, 1, 0, 2, 4).reshape(length, rows, groups * pair * depth)


def split_table(matrix):
    buckets, width = matrix.shape
    return matrix.reshape(buckets, width // (pair_heads * DH), pair_heads, DH).transpose(1, 2, 0, 3)


def join_table(matrix):
    groups, pair, buckets, depth = matrix.shape
    return matrix.transpose(2, 0, 1, 3).reshape(buckets, groups * pair * depth)


def table_ends(table):
    return jnp.stack([table[:, 0], table[:, -1]], axis=1)


def near_skew(table_prod, offset, full_len):
    lead = table_prod.shape[:-2]
    count, buckets = table_prod.shape[-2:]
    span = buckets // 2
    lead_pad = [(0, 0)] * len(lead)
    flipped = jnp.pad(table_prod[..., ::-1], lead_pad + [(0, 0), (0, count)])
    sheared = flipped.reshape(lead + (count * (buckets + count),))[
        ..., : count * (buckets + count - 1)
    ]
    sheared = sheared.reshape(lead + (count, buckets + count - 1))
    spread = jnp.pad(sheared, lead_pad + [(0, 0), (full_len, full_len)])
    band = lax.dynamic_slice_in_dim(
        spread, full_len + span - 1 - offset, full_len, axis=len(lead) + 1
    )
    distance = (offset + jnp.arange(count, dtype=jnp.int32))[:, None] - jnp.arange(
        full_len, dtype=jnp.int32
    )[None, :]
    return jnp.where(
        distance <= -span,
        table_prod[..., 0:1],
        jnp.where(distance >= span - 1, table_prod[..., buckets - 1 :], band),
    )


def far_place(cross, end_vals, offset, count, full_len):
    lead = cross.shape[:-2]
    band_len, buckets = cross.shape[-2:]
    span = buckets // 2
    lead_pad = [(0, 0)] * len(lead)
    turned = jnp.swapaxes(cross, -1, -2).reshape(lead + (buckets * band_len,))
    turned = jnp.pad(turned, lead_pad + [(0, buckets)])
    diagonal = turned.reshape(lead + (buckets, band_len + 1))[..., :count]
    aligned = jnp.pad(jnp.swapaxes(diagonal, -1, -2), lead_pad + [(0, 0), (0, count)])
    sheared = aligned.reshape(lead + (count * (buckets + count),))[
        ..., : count * (buckets + count - 1)
    ]
    sheared = sheared.reshape(lead + (count, buckets + count - 1))
    spread = jnp.pad(sheared, lead_pad + [(0, 0), (full_len, full_len)])
    band = lax.dynamic_slice_in_dim(spread, full_len + span - offset, full_len, axis=len(lead) + 1)
    distance = (
        jnp.arange(full_len, dtype=jnp.int32)[None, :]
        - (offset + jnp.arange(count, dtype=jnp.int32))[:, None]
    )
    return jnp.where(
        distance <= -span,
        end_vals[..., 0:1, :],
        jnp.where(distance >= span - 1, end_vals[..., 1:2, :], band),
    )


def band_rows(all_rows, offset, count, span):
    padded = jnp.pad(all_rows, [(0, 0), (0, 0), (span, span), (0, 0)])
    return lax.dynamic_slice_in_dim(padded, offset, count + 2 * span - 1, axis=2)


def unband(values, offset, full_len, span):
    lead = values.shape[:2]
    room = jnp.zeros(lead + (full_len + 2 * span, values.shape[3]), jnp.float32)
    placed = lax.dynamic_update_slice_in_dim(room, values, offset, axis=2)
    return placed[:, :, span : span + full_len]


def relative_scores(own_rows, all_rows, own_table, all_table, offset, full_len):
    count = own_rows.shape[2]
    content = jnp.einsum("rgid,rgjd->rgij", own_rows, all_rows, preferred_element_type=jnp.float32)
    own_prod = jnp.einsum("rgid,gbd->rgib", own_rows, own_table, preferred_element_type=jnp.float32)
    window = band_rows(all_rows, offset, count, all_table.shape[1] // 2)
    cross = jnp.einsum("rgmd,gbd->rgmb", window, all_table, preferred_element_type=jnp.float32)
    end_vals = jnp.einsum(
        "rgjd,ged->rgej", all_rows, table_ends(all_table), preferred_element_type=jnp.float32
    )
    near_vals, near_pull = jax.vjp(lambda product: near_skew(product, offset, full_len), own_prod)
    far_vals, far_pull = jax.vjp(
        lambda part, ends: far_place(part, ends, offset, count, full_len), cross, end_vals
    )
    return (content + near_vals + far_vals, near_pull, far_pull, window)


def end_columns(grad):
    return jnp.stack([grad[..., 0], grad[..., -1]], axis=2)


def end_terms(ends, table):
    return jnp.einsum(
        "rgei,ged->rgid",
        ends,
        table_ends(table),
        precision=lax.Precision.HIGHEST,
        preferred_element_type=jnp.float32,
    )


def end_rows(ends, rows_low):
    return jnp.einsum(
        "rgei,rgid->ged",
        ends,
        rows_low,
        precision=lax.Precision.HIGHEST,
        preferred_element_type=jnp.float32,
    )


def with_ends(inner_part, edge_rows):
    buckets = inner_part.shape[1]
    place = jnp.arange(buckets, dtype=jnp.int32)[None, :, None]
    return (
        inner_part
        + jnp.where(place == 0, edge_rows[:, 0:1], 0.0)
        + jnp.where(place == buckets - 1, edge_rows[:, 1:2], 0.0)
    )


BLOCK = 128
MIB = 1024 * 1024
ATTEND_VMEM = 26 * MIB
BACK_VMEM = 40 * MIB
FEED_VMEM = 26 * MIB
COMM_VMEM = 16 * MIB


def dot_nn(a, b):
    return lax.dot_general(a, b, (((1,), (0,)), ((), ())), preferred_element_type=jnp.float32)


def dot_nt(a, b):
    return lax.dot_general(a, b, (((1,), (1,)), ((), ())), preferred_element_type=jnp.float32)


def dot_tn(a, b):
    return lax.dot_general(a, b, (((0,), (0,)), ((), ())), preferred_element_type=jnp.float32)


def turn_matrix(buckets):
    row = lax.broadcasted_iota(jnp.int32, (buckets, buckets), 0)
    col = lax.broadcasted_iota(jnp.int32, (buckets, buckets), 1)
    return (row + col == buckets - 1).astype(jnp.bfloat16)


def skew_band(product):
    count, buckets = product.shape
    row = lax.broadcasted_iota(jnp.int32, (count, BLOCK), 0)
    lane = lax.broadcasted_iota(jnp.int32, (count, BLOCK), 1)
    edge = jnp.where(row + lane <= BLOCK - 2, product[:, buckets - 1 :], product[:, 0:1])
    wide = jnp.concatenate([product, edge], axis=1)
    return pltpu.roll(wide, 1, 1, stride=1, stride_axis=0)


def skew_back(turned, buckets):
    return pltpu.roll(turned, turned.shape[1] - BLOCK, 1, stride=1, stride_axis=0)[:, :buckets]


def chip_columns(vec_ref, chip, index, core):
    width = 3 * DH // 2
    both = jnp.concatenate(
        [
            vec_ref[2 * chip, index : index + 1, :width].astype(jnp.float32),
            vec_ref[2 * chip + 1, index : index + 1, :width].astype(jnp.float32),
        ],
        axis=1,
    )
    return jnp.where(core == 0, both[:, : 2 * DH], both[:, DH:])


def attend_kernel(
    xs_ref,
    qkvs_ref,
    tables_ref,
    vecs_ref,
    q_ref,
    k_ref,
    v_ref,
    qrev_ref,
    krev_ref,
    p_ref,
    ctx_ref,
    w_ref,
    table_ref,
    segc_ref,
    place_ref,
    wide_ref,
    ends_ref,
    held_ref,
    between,
):
    at = Place()
    full_len = xs_ref.shape[0] * xs_ref.shape[1]
    buckets = table_ref.shape[0]
    blocks = full_len // BLOCK
    span = buckets // 2
    side = span // BLOCK
    band_width = buckets + BLOCK
    band_blocks = band_width // BLOCK
    group = 2 * DH
    scale = 1.0 / math.sqrt(3.0 * DH)
    units = p_ref.shape[0]
    shard_rows = qkvs_ref.shape[2]
    table_rows = tables_ref.shape[3]
    batches = tables_ref.shape[1]
    for part in range(at.tokens):
        pieces = []
        for i in range(3):
            piece = qkvs_ref[part, i]
            pieces.append(jnp.where(at.core == 0, piece[:, :group], piece[:, DH:]))
        w_ref[part * shard_rows : (part + 1) * shard_rows] = jnp.concatenate(pieces, axis=1)
        core, chip = part % 2, part // 2
        table_ref[part * table_rows : (part + 1) * table_rows] = jnp.concatenate(
            [tables_ref[core, row, chip] for row in range(batches)], axis=1
        )
        own_seg = vecs_ref[part, 9:10].astype(jnp.float32)
        segc_ref[part * BLOCK : (part + 1) * BLOCK] = jnp.broadcast_to(own_seg, (BLOCK, BLOCK)).T
    seg_row = jnp.concatenate(
        [vecs_ref[part, 9:10].astype(jnp.float32) for part in range(at.tokens)], axis=1
    )
    bias = jnp.concatenate(
        [chip_columns(vecs_ref, at.chip, i, at.core) for i in range(3)], axis=1
    )
    tokens_all = xs_ref[...].reshape(full_len, xs_ref.shape[2])
    proj = (dot_nn(tokens_all, w_ref[...]) + bias).astype(jnp.bfloat16)
    rel = (dot_nn(table_ref[...], w_ref[:, : 2 * group]) + bias[:, : 2 * group]).astype(
        jnp.bfloat16
    )
    rel = dot_nn(turn_matrix(buckets), rel).astype(jnp.bfloat16)
    for slot in range(2):
        lo, hi = slot * DH, (slot + 1) * DH
        q_ref[slot] = proj[:, lo:hi]
        k_ref[slot] = proj[:, group + lo : group + hi]
        v_ref[slot] = proj[:, 2 * group + lo : 2 * group + hi]
        qrev_ref[slot] = rel[:, lo:hi]
        krev_ref[slot] = rel[:, group + lo : group + hi]
    held_ref[...] = jnp.zeros_like(held_ref)
    for slot in range(2):
        ends_ref[slot, 0] = dot_nt(qrev_ref[slot, 0:16], k_ref[slot])
        ends_ref[slot, 1] = dot_nt(qrev_ref[slot, buckets - 16 : buckets], k_ref[slot])

        def key_block(kb, carry):
            rows = k_ref[slot, pl.ds(pl.multiple_of(kb * BLOCK, BLOCK), BLOCK)]
            band = skew_band(dot_nt(rows, qrev_ref[slot]))
            for e in range(band_blocks):
                place_ref[
                    slot,
                    kb + e,
                    :,
                    (band_blocks - 1 - e) * BLOCK : (band_blocks - e) * BLOCK,
                ] = band[:, e * BLOCK : (e + 1) * BLOCK].T
            return carry

        lax.fori_loop(0, blocks, key_block, 0, unroll=8)

    first = at.core * (blocks // 2)
    between()

    def unit(u, carry):
        g = u + first
        slot = g // blocks
        qb = g % blocks
        start = pl.multiple_of(qb * BLOCK, BLOCK)
        rows = q_ref[slot, pl.ds(start, BLOCK)]
        own = dot_nt(rows, krev_ref[slot])
        band = skew_band(own) + place_ref[slot, qb + side]
        wide_ref[u % 2, :, pl.ds(start, band_width)] = band
        content = dot_nt(rows, k_ref[slot])
        lane = lax.broadcasted_iota(jnp.int32, (BLOCK, full_len), 1)
        near = jnp.where(
            lane < start - span,
            own[:, 0:1] + ends_ref[slot, 1, 15:16],
            jnp.where(
                lane >= start + band_width - span,
                own[:, buckets - 1 :] + ends_ref[slot, 0, 0:1],
                wide_ref[u % 2, :, span : span + full_len],
            ),
        )
        same = segc_ref[pl.ds(start, BLOCK), 0:1] == seg_row
        scores = jnp.where(same, (content + near) * scale, masked_score)
        highest = jnp.max(scores, axis=-1, keepdims=True)
        exponent = jnp.exp(scores - highest)
        total = jnp.sum(exponent, axis=-1, keepdims=True)
        probs = (exponent / total).astype(jnp.bfloat16)
        p_ref[u] = probs
        held_ref[slot, pl.ds(start, BLOCK)] = dot_nn(probs, v_ref[slot]).astype(jnp.bfloat16)
        return carry

    lax.fori_loop(0, units, unit, 0, unroll=4)
    for part in range(at.tokens):
        rows = slice(part * BLOCK, (part + 1) * BLOCK)
        ctx_ref[part] = jnp.concatenate([held_ref[0, rows], held_ref[1, rows]], axis=1)


def attend_back_kernel(
    q_ref,
    k_ref,
    v_ref,
    qrev_ref,
    krev_ref,
    p_ref,
    mix_ref,
    attn_ref,
    dcat_ref,
    rel_ref,
    sum_ref,
    heads_ref,
    wide_ref,
    low_ref,
    place_ref,
    dq_ref,
    dkt_ref,
    dvt_ref,
    far_ref,
    dkr_ref,
    dqr_ref,
):
    full_len = q_ref.shape[1]
    buckets = qrev_ref.shape[1]
    blocks = full_len // BLOCK
    span = buckets // 2
    side = span // BLOCK
    band_width = buckets + BLOCK
    band_blocks = band_width // BLOCK
    scale = 1.0 / math.sqrt(3.0 * DH)
    units = p_ref.shape[0]
    for ref in (wide_ref, low_ref, place_ref, dq_ref, dkt_ref, dvt_ref, far_ref, dkr_ref, dqr_ref):
        ref[...] = jnp.zeros_like(ref)
    at = Place()
    group = 2 * DH
    first_row = pl.multiple_of((3 * at.chip + at.core) * DH, DH)
    mix_rows = mix_ref[pl.ds(first_row, group)]
    dctx = dot_nt(attn_ref[...].reshape(full_len, attn_ref.shape[2]), mix_rows)
    for slot in range(2):
        heads_ref[slot] = dctx[:, slot * DH : (slot + 1) * DH].astype(jnp.bfloat16)
    first = at.core * (blocks // 2)
    turn = turn_matrix(BLOCK)
    place8 = lax.broadcasted_iota(jnp.int32, (8, full_len), 0)

    def unit(u, carry):
        g = u + first
        slot = g // blocks
        qb = g % blocks
        start = pl.multiple_of(qb * BLOCK, BLOCK)
        rows = q_ref[slot, pl.ds(start, BLOCK)]
        grad = heads_ref[slot, pl.ds(start, BLOCK)]
        probs = p_ref[u]
        wide_probs = probs.astype(jnp.float32)
        prob_grad = dot_nt(grad, v_ref[slot])
        inner = jnp.sum(wide_probs * prob_grad, axis=-1, keepdims=True)
        low_grad = (wide_probs * (prob_grad - inner)).astype(jnp.bfloat16)
        score_grad = low_grad.astype(jnp.float32)
        wide_ref[u % 2, :, span : span + full_len] = dot_nn(turn, low_grad)
        low_ref[u % 2, :, span : span + full_len] = low_grad
        dvt_ref[slot] += dot_tn(grad, probs)
        dkt_ref[slot] += dot_tn(rows, low_grad)
        row = lax.broadcasted_iota(jnp.int32, (BLOCK, full_len), 0)
        lane = lax.broadcasted_iota(jnp.int32, (BLOCK, full_len), 1)
        gap = lane - row - start
        right = jnp.where(gap > span, score_grad, 0.0)
        left = jnp.where(gap < 1 - span, score_grad, 0.0)
        end_right = jnp.sum(right, axis=-1, keepdims=True)
        end_left = jnp.sum(left, axis=-1, keepdims=True)
        far_right = jnp.sum(jnp.where(gap >= span, score_grad, 0.0), axis=0, keepdims=True)
        far_left = jnp.sum(jnp.where(gap < -span, score_grad, 0.0), axis=0, keepdims=True)
        far_ref[slot] += jnp.where(place8 == 0, far_right, jnp.where(place8 == 1, far_left, 0.0))
        band = wide_ref[u % 2, :, pl.ds(start, band_width)]
        near = dot_nn(turn, skew_back(band, buckets).astype(jnp.bfloat16))
        bucket = lax.broadcasted_iota(jnp.int32, (BLOCK, buckets), 1)
        near = near + jnp.where(
            bucket == 0, end_left, jnp.where(bucket == buckets - 1, end_right, 0.0)
        )
        near_low = near.astype(jnp.bfloat16)
        dq = dot_nn(low_grad, k_ref[slot]) + dot_nn(near_low, krev_ref[slot])
        dq_ref[slot, pl.ds(start, BLOCK)] = dq
        dkr_ref[slot] += dot_tn(rows, near_low)
        for e in range(band_blocks):
            keys_at = pl.multiple_of(start + e * BLOCK, BLOCK)
            place_ref[
                slot, qb + e, :, (band_blocks - 1 - e) * BLOCK : (band_blocks - e) * BLOCK
            ] = dot_nt(turn, low_ref[u % 2, :, pl.ds(keys_at, BLOCK)])
        return carry

    lax.fori_loop(0, units, unit, 0, unroll=4)
    parts_q, parts_k, parts_v = [], [], []
    parts_r = [None] * 4
    for slot in range(2):
        far_low = far_ref[slot].astype(jnp.bfloat16)
        mark = lax.broadcasted_iota(jnp.int32, (8, DH), 0)
        ends = jnp.where(
            mark == 0,
            qrev_ref[slot, 0:1].astype(jnp.float32),
            jnp.where(mark == 1, qrev_ref[slot, buckets - 1 : buckets].astype(jnp.float32), 0.0),
        ).astype(jnp.bfloat16)
        end_keys = dot_tn(ends, far_low)
        end_rows = dot_nn(far_low, k_ref[slot])

        whole_k = (dkt_ref[slot] + end_keys).T

        def key_side(kb, carry):
            start = pl.multiple_of(kb * BLOCK, BLOCK)
            far = skew_back(place_ref[slot, kb + side], buckets).astype(jnp.bfloat16)
            far = dot_nn(turn, far).astype(jnp.bfloat16)
            keys = k_ref[slot, pl.ds(start, BLOCK)]
            dqr_ref[slot] += dot_tn(keys, far)
            dq_ref[2 + slot, pl.ds(start, BLOCK)] = dot_nn(far, qrev_ref[slot])
            return carry

        lax.fori_loop(0, blocks, key_side, 0, unroll=8)
        parts_q.append((dq_ref[slot] * scale).astype(jnp.bfloat16))
        parts_k.append(((dq_ref[2 + slot] + whole_k) * scale).astype(jnp.bfloat16))
        parts_v.append(dvt_ref[slot].T.astype(jnp.bfloat16))
        bucket = lax.broadcasted_iota(jnp.int32, (buckets, DH), 0)
        qr = dqr_ref[slot].T + jnp.where(
            bucket == 0, end_rows[0:1], jnp.where(bucket == buckets - 1, end_rows[1:2], 0.0)
        )
        dqr_out = qr * scale
        dkr_out = dkr_ref[slot].T * scale
        parts_r[slot] = dqr_out
        parts_r[2 + slot] = dkr_out
    dcat = jnp.concatenate(parts_q + parts_k + parts_v, axis=1)
    dcat_ref[...] = dcat
    rel = jnp.concatenate(parts_r, axis=1)
    rel_ref[...] = dot_nn(turn_matrix(buckets), rel.astype(jnp.bfloat16)).astype(jnp.bfloat16)
    rel_sum = jnp.sum(rel, axis=0, keepdims=True)
    rel_sum = jnp.concatenate([rel_sum, jnp.zeros((1, 2 * DH), jnp.float32)], axis=1)
    sums = jnp.sum(dcat.astype(jnp.float32), axis=0, keepdims=True) + rel_sum
    sum_ref[...] = jnp.broadcast_to(sums, sum_ref.shape)


MESH = pl.DeviceIdType.MESH
VMEM_SPEC = pl.BlockSpec(memory_space=pltpu.VMEM)
HBM_SPEC = pl.BlockSpec(memory_space=pltpu.HBM)
CHUNKS = 4


class Place:
    def __init__(self):
        self.batches = lax.axis_size("batch")
        self.tokens = lax.axis_size("seq")
        self.chips = self.tokens // 2
        self.row = lax.axis_index("batch")
        self.part = lax.axis_index("seq")
        self.chip = self.part // 2
        self.core = self.part % 2

    def inside(self):
        return jnp.logical_and(self.chip > 0, self.chip < self.chips - 1)

    def along_chips(self, k):
        chip = lax.rem(self.chip + k, self.chips)
        return chip, (self.row, 2 * chip + self.core)

    def from_chips(self, k):
        return lax.rem(self.chip + self.chips - k, self.chips)

    def partner(self):
        return (self.row, self.part + 1 - 2 * self.core)

    def along_rows(self, k):
        row = lax.rem(self.row + k, self.batches)
        return row, (row, self.part)

    def from_rows(self, k):
        return lax.rem(self.row + self.batches - k, self.batches)

    def along_seq(self, k):
        part = lax.rem(self.part + k, self.tokens)
        return part, (self.row, part)

    def along_plane(self, k):
        index = lax.rem(2 * self.row + self.core + k, 2 * self.batches)
        row, core = index // 2, index % 2
        return row, core, (row, 2 * self.chip + core)

    def chip_peers(self):
        return [self.along_chips(k)[1] for k in range(1, self.chips)]

    def row_peers(self):
        return [self.along_rows(k)[1] for k in range(1, self.batches)]

    def cross_peers(self):
        other = self.part + 1 - 2 * self.core
        return [(self.along_rows(k)[0], other) for k in range(1, self.batches)]

    def cross_row_peers(self):
        return self.row_peers() + self.cross_peers()

    def all_peers(self):
        peers = []
        for i in range(self.batches):
            row = lax.rem(self.row + i, self.batches)
            for j in range(self.tokens):
                if i or j:
                    peers.append((row, lax.rem(self.part + j, self.tokens)))
        return peers

    def seq_peers(self):
        return [self.along_seq(k)[1] for k in range(1, self.tokens)]

    def plane_peers(self):
        return [self.along_plane(k)[2] for k in range(1, 2 * self.batches)]


def meet(peers):
    barrier = pltpu.get_barrier_semaphore()
    for peer in peers:
        pl.semaphore_signal(barrier, inc=1, device_id=peer, device_id_type=MESH)
    pl.semaphore_wait(barrier, len(peers))


class Wires:
    def __init__(self, send_sems, recv_sems, local_sems):
        self.sems = (send_sems, recv_sems, local_sems)
        self.used = [0, 0]
        self.ends = []

    def send(self, src, dst, peer):
        k = self.used[0]
        self.used[0] += 1
        copy = pltpu.make_async_remote_copy(
            src_ref=src,
            dst_ref=dst,
            send_sem=self.sems[0].at[k],
            recv_sem=self.sems[1].at[k],
            device_id=peer,
            device_id_type=MESH,
        )
        copy.start()
        self.ends.append(copy.wait_send)
        return copy

    def local(self, src, dst):
        k = self.used[1]
        self.used[1] += 1
        copy = pltpu.make_async_copy(src, dst, self.sems[2].at[k])
        copy.start()
        return copy

    def finish(self):
        for end in self.ends:
            end()


def wire_scratch(sends, locals_count):
    return [
        pltpu.SemaphoreType.DMA((sends,)),
        pltpu.SemaphoreType.DMA((sends,)),
        pltpu.SemaphoreType.DMA((locals_count,)),
    ]


def comm_call(kernel, name, ident, out_shapes, inputs, sends, locals_count, scratch=(), spec=VMEM_SPEC, limit=None):
    return pl.pallas_call(
        kernel,
        out_shape=tuple(out_shapes),
        in_specs=[spec] * len(inputs),
        out_specs=tuple([VMEM_SPEC] * len(out_shapes)),
        scratch_shapes=list(scratch) + wire_scratch(sends, locals_count),
        compiler_params=pltpu.CompilerParams(
            collective_id=ident, has_side_effects=True, vmem_limit_bytes=limit or COMM_VMEM
        ),
        name=name,
    )(*inputs)


def like(array, *lead):
    return jax.ShapeDtypeStruct(tuple(lead) + tuple(array.shape), array.dtype)


def pick(values, index):
    out = jnp.int32(values[0])
    for i in range(1, len(values)):
        out = jnp.where(index == i, jnp.int32(values[i]), out)
    return out


def arrival_order(at):
    chips = range(at.chips)
    lists = [sorted((j for j in chips if j != z), key=lambda j: (abs(j - z), j)) for z in chips]
    return [pick([lists[z][t] for z in chips], at.chip) for t in range(at.chips - 1)]


def return_order(at):
    chips = range(at.chips)

    def away(j, z):
        end = at.chips - 1 if j < z else 0
        return (abs(j - end) + abs(end - z), j)

    lists = [sorted((j for j in chips if j != z), key=lambda j: away(j, z)) for z in chips]
    return [pick([lists[z][t] for z in chips], at.chip) for t in range(at.chips - 1)]


def far_order(at):
    chips = range(at.chips)
    lists = [sorted((j for j in chips if j != z), key=lambda j: (-abs(j - z), j)) for z in chips]
    return [pick([lists[z][t] for z in chips], at.chip) for t in range(at.chips - 1)]


def goes_on(at, j):
    above = jnp.logical_and(j < at.chip, at.chip < at.chips - 1)
    below = jnp.logical_and(j > at.chip, at.chip > 0)
    return jnp.logical_or(above, below)


def line_peer(at, step):
    return (at.row, 2 * (at.chip + step) + at.core)


class LineGather:
    def __init__(self, at, buf, slot, sems, own=None):
        self.at, self.buf, self.slot, self.own = at, buf, slot, own
        self.send_sems, self.recv_sems = sems
        self.rows = buf.shape[1] // CHUNKS

    def copy(self, j, h, step, k, own=False):
        window = pl.ds(h * self.rows, self.rows)
        home = self.buf.at[self.slot(j), window]
        src = self.own.at[window] if own and self.own is not None else home
        return pltpu.make_async_remote_copy(
            src_ref=src,
            dst_ref=home,
            send_sem=self.send_sems.at[k * CHUNKS + h],
            recv_sem=self.recv_sems.at[j * CHUNKS + h],
            device_id=line_peer(self.at, step),
            device_id_type=MESH,
        )

    def own_each(self, act):
        z, n = self.at.chip, self.at.chips
        for h in range(CHUNKS):

            @pl.when(z < n - 1)
            def _():
                act(self.copy(z, h, 1, z, own=True))

            @pl.when(z > 0)
            def _():
                act(self.copy(z, h, -1, n, own=True))

    def start(self):
        self.own_each(lambda copy: copy.start())

    def arrive_chunk(self, j, h):
        step = jnp.where(j < self.at.chip, 1, -1)
        self.copy(j, h, -step, j).wait_recv()

        @pl.when(goes_on(self.at, j))
        def _():
            self.copy(j, h, step, j).start()

    def arrive(self, order, t):
        if t == 0:

            @pl.when(self.at.inside())
            def _():
                for h in range(CHUNKS):
                    self.arrive_chunk(order[0], h)
                    self.arrive_chunk(order[1], h)

        if t < 2:

            @pl.when(jnp.logical_not(self.at.inside()))
            def _():
                for h in range(CHUNKS):
                    self.arrive_chunk(order[t], h)

        else:
            for h in range(CHUNKS):
                self.arrive_chunk(order[t], h)

    def drain(self, order):
        self.own_each(lambda copy: copy.wait_send())
        for j in order:
            step = jnp.where(j < self.at.chip, 1, -1)

            @pl.when(goes_on(self.at, j))
            def _():
                for h in range(CHUNKS):
                    self.copy(j, h, step, j).wait_send()


class LineReduce:
    def __init__(self, at, part, got, sems):
        self.at, self.part, self.got = at, part, got
        self.send_sems, self.recv_sems = sems
        self.rows = part.shape[1] // CHUNKS

    def copy(self, j, h):
        z, n = self.at.chip, self.at.chips
        window = pl.ds(h * self.rows, self.rows)
        slot = jnp.where(z + 1 == j, n, j)
        return pltpu.make_async_remote_copy(
            src_ref=self.part.at[j, window],
            dst_ref=self.got.at[slot, window],
            send_sem=self.send_sems.at[j * CHUNKS + h],
            recv_sem=self.recv_sems.at[slot * CHUNKS + h],
            device_id=line_peer(self.at, jnp.where(j < z, -1, 1)),
            device_id_type=MESH,
        )

    def landed(self, slot, h, step):
        window = pl.ds(h * self.rows, self.rows)
        return pltpu.make_async_remote_copy(
            src_ref=self.got.at[slot, window],
            dst_ref=self.got.at[slot, window],
            send_sem=self.send_sems.at[h],
            recv_sem=self.recv_sems.at[slot * CHUNKS + h],
            device_id=line_peer(self.at, step),
            device_id_type=MESH,
        )

    def send(self, j):
        for h in range(CHUNKS):
            self.copy(j, h).start()

    def send_last(self, j):
        @pl.when(jnp.logical_not(goes_on(self.at, j)))
        def _():
            self.send(j)

    def pass_chunk(self, j, h):
        wide = jnp.float32
        step = jnp.where(j < self.at.chip, 1, -1)
        self.landed(j, h, step).wait_recv()
        window = pl.ds(h * self.rows, self.rows)
        total = self.part[j, window].astype(wide) + self.got[j, window].astype(wide)
        self.part[j, window] = total.astype(self.part.dtype)
        self.copy(j, h).start()

    def pass_on(self, order):
        @pl.when(self.at.inside())
        def _():
            for j in order:
                for h in range(CHUNKS):
                    self.pass_chunk(j, h)

    def clear(self):
        z, n = self.at.chip, self.at.chips

        @pl.when(z == n - 1)
        def _():
            self.got[z] = jnp.zeros(self.got.shape[1:], self.got.dtype)

        @pl.when(z == 0)
        def _():
            self.got[n] = jnp.zeros(self.got.shape[1:], self.got.dtype)

    def collect(self):
        z, n = self.at.chip, self.at.chips
        for h in range(CHUNKS):

            @pl.when(z < n - 1)
            def _():
                self.landed(z, h, 1).wait_recv()

            @pl.when(z > 0)
            def _():
                self.landed(n, h, -1).wait_recv()

        return self.got[z].astype(jnp.float32) + self.got[n].astype(jnp.float32)

    def drain(self, order):
        for j in order:
            for h in range(CHUNKS):
                self.copy(j, h).wait_send()


def gather_sems(chips):
    return [
        pltpu.SemaphoreType.DMA(((chips + 1) * CHUNKS,)),
        pltpu.SemaphoreType.DMA((chips * CHUNKS,)),
    ]


def reduce_sems(chips):
    return [
        pltpu.SemaphoreType.DMA((chips * CHUNKS,)),
        pltpu.SemaphoreType.DMA(((chips + 1) * CHUNKS,)),
    ]


def gather_kernel(
    x_ref, wq_ref, wk_ref, wv_ref, mix_ref, table_ref, vec_ref, up_ref, down_ref,
    xs_ref, mixs_ref, vecs_ref, up2_ref, down2_ref,
    q_ref, k_ref, v_ref, qrev_ref, krev_ref, p_ref, ctx_ref, w_ref, table_all_ref,
    qkvs_ref, tables_ref, segc_ref, place_ref, wide_ref, ends_ref, held_ref,
    line_send, line_recv, *sems,
):
    at = Place()
    wires = Wires(*sems)
    b, s, z, c = at.row, at.part, at.chip, at.core
    off_diagonal = b != z
    turned = (z, 2 * b + c)
    peers = at.seq_peers() + at.row_peers()
    barrier = pltpu.get_barrier_semaphore()
    for peer in peers:
        pl.semaphore_signal(barrier, inc=1, device_id=peer, device_id_type=MESH)

    @pl.when(off_diagonal)
    def _():
        pl.semaphore_signal(barrier, inc=1, device_id=turned, device_id_type=MESH)

    pl.semaphore_wait(barrier, len(peers) + off_diagonal.astype(jnp.int32))

    swaps, stays = [], []
    for i, ref in enumerate((wq_ref, wk_ref, wv_ref)):
        k = wires.used[0]
        wires.used[0] += 1
        swaps.append(
            pltpu.make_async_remote_copy(
                src_ref=ref,
                dst_ref=qkvs_ref.at[2 * z + c, i],
                send_sem=sems[0].at[k],
                recv_sem=sems[1].at[k],
                device_id=turned,
                device_id_type=MESH,
            )
        )
        stays.append(pltpu.make_async_copy(ref, qkvs_ref.at[2 * b + c, i], sems[2].at[i]))
        wires.used[1] += 1

    @pl.when(off_diagonal)
    def _():
        for swap in swaps:
            swap.start()

    @pl.when(jnp.logical_not(off_diagonal))
    def _():
        for stay in stays:
            stay.start()

    table_home = tables_ref.at[c, b, z]
    mix_home = mixs_ref.at[c, b, z]
    table_sends = [
        wires.send(table_ref, table_home, at.along_chips(k)[1]) for k in range(1, at.chips)
    ]
    kept = [wires.local(table_ref, table_home), wires.local(mix_ref, mix_home)]
    line = LineGather(at, xs_ref, lambda j: 2 * j + c, (line_send, line_recv), own=x_ref)
    line.start()
    last = [wires.send(vec_ref, vecs_ref.at[s], at.along_seq(k)[1]) for k in range(1, at.tokens)]
    mix_sends = [
        wires.send(mix_ref, mix_home, at.along_chips(k)[1]) for k in range(1, at.chips)
    ]
    last += [
        wires.send(x_ref, xs_ref.at[s], at.partner()),
        wires.send(up_ref, up2_ref, at.partner()),
        wires.send(down_ref, down2_ref, at.partner()),
    ]
    own = [
        wires.local(x_ref, xs_ref.at[s]),
        wires.local(vec_ref, vecs_ref.at[s]),
    ]

    @pl.when(off_diagonal)
    def _():
        for swap in swaps:
            swap.wait_recv()

    @pl.when(jnp.logical_not(off_diagonal))
    def _():
        for stay in stays:
            stay.wait()

    mine = qkvs_ref.at[2 * b + c]
    qkv_sends = [wires.send(mine, mine, at.along_rows(k)[1]) for k in range(1, at.batches)]
    last.append(wires.send(mine, mine, at.partner()))
    for copy in table_sends:
        copy.wait_recv()
    for copy in kept:
        copy.wait()
    mine = tables_ref.at[c, b]
    row_sends = [wires.send(mine, mine, at.along_rows(k)[1]) for k in range(1, at.batches)]
    last.append(wires.send(mine, mine, at.partner()))
    order = arrival_order(at)

    def arrived(t):
        line.arrive(order, t)
        home = xs_ref.at[2 * order[t] + c]
        last.append(wires.send(home, home, at.partner()))

    arrived(0)
    arrived(1)
    for k in range(1, at.batches):
        qkv_sends[k - 1].wait_recv()
        home = qkvs_ref.at[2 * at.from_rows(k) + c]
        last.append(wires.send(home, home, at.partner()))
    for k in range(1, at.batches):
        row_sends[k - 1].wait_recv()
        home = tables_ref.at[c, at.from_rows(k)]
        last.append(wires.send(home, home, at.partner()))
    for t in range(2, at.chips - 1):
        arrived(t)
    for copy in last:
        copy.wait_recv()
    for copy in own:
        copy.wait()
    mix_rows, mix_last = [], []

    def between():
        for copy in mix_sends:
            copy.wait_recv()
        mine = mixs_ref.at[c, b]
        for k in range(1, at.batches):
            mix_rows.append(wires.send(mine, mine, at.along_rows(k)[1]))
        mix_last.append(wires.send(mine, mine, at.partner()))

    attend_kernel(
        xs_ref, qkvs_ref, tables_ref, vecs_ref, q_ref, k_ref, v_ref, qrev_ref, krev_ref, p_ref,
        ctx_ref, w_ref, table_all_ref, segc_ref, place_ref, wide_ref, ends_ref, held_ref, between,
    )
    for k in range(1, at.batches):
        mix_rows[k - 1].wait_recv()
        home = mixs_ref.at[c, at.from_rows(k)]
        mix_last.append(wires.send(home, home, at.partner()))
    for copy in mix_last:
        copy.wait_recv()
    wires.finish()
    line.drain(order)

    @pl.when(off_diagonal)
    def _():
        for swap in swaps:
            swap.wait_send()


def gather_inputs(x, w_query, w_key, w_value, w_mix, rel_table, vec, up, down):
    tokens, batches = lax.axis_size("seq"), lax.axis_size("batch")
    chips = tokens // 2
    local_len, width = x.shape
    full_len = tokens * local_len
    buckets = tokens * rel_table.shape[0]
    units = 3 * full_len // BLOCK // 2
    band_width = buckets + BLOCK
    pad_blocks = full_len // BLOCK + band_width // BLOCK - 1
    low, wide = jnp.bfloat16, jnp.float32
    outs = (
        like(x, tokens),
        like(w_mix, 2, batches, chips),
        like(vec, tokens),
        like(up),
        like(down),
        jax.ShapeDtypeStruct((2, full_len, DH), low),
        jax.ShapeDtypeStruct((2, full_len, DH), low),
        jax.ShapeDtypeStruct((2, full_len, DH), low),
        jax.ShapeDtypeStruct((2, buckets, DH), low),
        jax.ShapeDtypeStruct((2, buckets, DH), low),
        jax.ShapeDtypeStruct((units, BLOCK, full_len), low),
        jax.ShapeDtypeStruct((tokens, local_len, 2 * DH), low),
        jax.ShapeDtypeStruct((width, 6 * DH), low),
        jax.ShapeDtypeStruct((buckets, width), low),
    )
    scratch = [
        pltpu.VMEM((tokens, 3) + w_query.shape, low),
        pltpu.VMEM((2, batches, chips) + rel_table.shape, low),
        pltpu.VMEM((full_len, BLOCK), wide),
        pltpu.VMEM((2, pad_blocks, BLOCK, band_width), wide),
        pltpu.VMEM((2, BLOCK, full_len + buckets), wide),
        pltpu.VMEM((2, 2, 16, full_len), wide),
        pltpu.VMEM((2, full_len, DH), low),
    ]
    sends = 3 + 2 * (chips - 1) + tokens - 1 + 3 + 6 * (batches - 1) + 3 + chips - 1
    inputs = (x, w_query, w_key, w_value, w_mix, rel_table, vec, up, down)
    return comm_call(
        gather_kernel,
        "gather_inputs",
        0,
        outs,
        inputs,
        sends,
        7,
        scratch=scratch + gather_sems(chips),
        spec=HBM_SPEC,
        limit=ATTEND_VMEM,
    )


def norm_parts(values):
    average = jnp.mean(values, axis=-1, keepdims=True)
    centered = values - average
    variance = jnp.mean(centered * centered, axis=-1, keepdims=True)
    scale = lax.rsqrt(variance + norm_eps)
    return centered * scale, scale


def norm_back(grad, gain, unit, scale):
    inner = grad * gain
    mean = jnp.mean(inner, axis=-1, keepdims=True)
    slope = jnp.mean(inner * unit, axis=-1, keepdims=True)
    return scale * (inner - mean - unit * slope)


def line_pass(gather, reduce, order, work):
    for t, j in enumerate(order):
        gather.arrive(order, t)
        work(j)
        reduce.send_last(j)


def feed_kernel(
    ctx_ref, x_ref, mixs_ref, vecs_ref, up_ref, down_ref, up2_ref, down2_ref, out_grad_ref,
    output_ref, pre_grad_ref, sums_ref, attn_ref, mix_ref, ups_ref, downs_ref, upbs_ref,
    got_ref, hid_ref, act_ref, slope_ref, part_ref, ffn_ref, grad_ref, inner_ref,
    back_ref, backs_ref, up_acc_ref, down_acc_ref, up_away_ref, down_away_ref, upb_away_ref,
    up_got_ref, down_got_ref, upb_got_ref, upg_ref, downg_ref, upb_ref, vec_ref,
    hid_send, hid_recv, ffn_send, ffn_recv, grad_send, grad_recv, back_send, back_recv,
    attn_send, attn_recv, *sems,
):
    at = Place()
    wires = Wires(*sems)
    low, wide = jnp.bfloat16, jnp.float32
    b, s, z, c = at.row, at.part, at.chip, at.core
    order, returns = arrival_order(at), return_order(at)
    meet(at.seq_peers() + at.row_peers())
    last, own = [], []
    swaps = []
    for k in range(1, at.tokens):
        part, peer = at.along_seq(k)
        swaps.append(wires.send(ctx_ref.at[part], got_ref.at[s], peer))
    kept = wires.local(ctx_ref.at[s], got_ref.at[s])
    lanes = x_ref.shape[1] // at.tokens
    hidden_here = up_ref.shape[1]
    vec_ref[...] = jnp.concatenate(
        [vecs_ref[part, :, :lanes].astype(wide) for part in range(at.tokens)], axis=1
    )
    bias3 = vec_ref[3:4]
    gain1, gain2 = vec_ref[4:5], vec_ref[5:6]
    shift1, shift2 = vec_ref[6:7], vec_ref[7:8]
    bias_down = vec_ref[8:9]
    partner = s + 1 - 2 * c
    up_rows = hidden_here // BLOCK
    bias_up = jnp.concatenate(
        [vecs_ref[s, 10 + i : 11 + i].astype(wide) for i in range(up_rows)]
        + [vecs_ref[partner, 10 + i : 11 + i].astype(wide) for i in range(up_rows)],
        axis=1,
    )
    shard_rows = mixs_ref.shape[3]
    for part in range(at.tokens):
        mix_ref[part * shard_rows : (part + 1) * shard_rows] = jnp.concatenate(
            [mixs_ref[part % 2, row, part // 2] for row in range(at.batches)], axis=1
        )
    for copy in swaps:
        copy.wait_recv()
    kept.wait()
    pieces = []
    for chip in range(at.chips):
        left, right = got_ref[2 * chip], got_ref[2 * chip + 1]
        middle = left[:, DH:].astype(wide) + right[:, :DH].astype(wide)
        pieces += [left[:, :DH], middle.astype(low), right[:, DH:]]
    context = jnp.concatenate(pieces, axis=1)
    pre_norm = x_ref[...].astype(wide) + dot_nn(context, mix_ref[...]) + bias3
    unit1, scale1 = norm_parts(pre_norm)
    hidden = unit1 * gain1 + shift1
    hid_ref[z] = hidden.astype(low)
    hid_line = LineGather(at, hid_ref, lambda j: j, (hid_send, hid_recv))
    ffn_line = LineReduce(at, part_ref, ffn_ref, (ffn_send, ffn_recv))
    hid_line.start()
    ffn_line.clear()

    def ffn(chip):
        rows = hid_ref[chip]
        inner = jnp.concatenate(
            [dot_nn(rows, up_ref[...]), dot_nn(rows, up2_ref[...])], axis=1
        )
        inner = inner + bias_up
        cdf = 0.5 * (1.0 + lax.erf(inner * math.sqrt(0.5)))
        act = (inner * cdf).astype(low)
        slope_ref[chip] = cdf + inner * (
            jnp.exp(-0.5 * inner * inner) * (1.0 / math.sqrt(2.0 * math.pi))
        )
        act_ref[chip] = act
        part_ref[chip] = (
            dot_nn(act[:, :hidden_here], down_ref[...])
            + dot_nn(act[:, hidden_here:], down2_ref[...])
        ).astype(low)

    ffn(z)
    line_pass(hid_line, ffn_line, order, ffn)
    ffn_line.pass_on(returns[:1])
    ffn_line.pass_on(returns[1:])
    total = part_ref[z].astype(wide) + ffn_line.collect()
    mixed = hidden + total + bias_down
    unit2, scale2 = norm_parts(mixed)
    output_ref[...] = (unit2 * gain2 + shift2).astype(low)
    out_grad = out_grad_ref[...].astype(wide)
    mixed_grad = norm_back(out_grad, gain2, unit2, scale2)
    grad_ref[z] = mixed_grad.astype(low)
    grad_line = LineGather(at, grad_ref, lambda j: j, (grad_send, grad_recv))
    back_line = LineReduce(at, back_ref, backs_ref, (back_send, back_recv))
    grad_line.start()
    back_line.clear()
    gain2_grad = jnp.sum(out_grad * unit2, axis=0, keepdims=True)
    shift2_grad = jnp.sum(out_grad, axis=0, keepdims=True)
    downb_grad = jnp.sum(mixed_grad, axis=0, keepdims=True)

    def back(chip):
        rows = grad_ref[chip]
        act_grad = jnp.concatenate(
            [dot_nt(rows, down_ref[...]), dot_nt(rows, down2_ref[...])], axis=1
        )
        inner_low = (act_grad * slope_ref[chip]).astype(low)
        inner_ref[chip] = inner_low
        back_ref[chip] = (
            dot_nt(inner_low[:, :hidden_here], up_ref[...])
            + dot_nt(inner_low[:, hidden_here:], up2_ref[...])
        ).astype(low)

    def weight_grads(chip):
        up_acc_ref[...] += dot_tn(hid_ref[chip], inner_ref[chip])
        down_acc_ref[...] += dot_tn(grad_ref[chip], act_ref[chip])

    back(z)
    up_acc_ref[...] = dot_tn(hid_ref[z], inner_ref[z])
    down_acc_ref[...] = dot_tn(grad_ref[z], act_ref[z])
    line_pass(grad_line, back_line, order, back)
    for j in order:
        weight_grads(j)
    back_line.pass_on(returns[:1])
    back_line.pass_on(returns[1:])
    width = x_ref.shape[1]
    columns = width // at.batches
    inner_all = inner_ref[...].reshape(at.chips * BLOCK, 2 * hidden_here)
    near, away = slice(0, hidden_here), slice(hidden_here, 2 * hidden_here)
    up_away_ref[...] = up_acc_ref[:, away].astype(low)
    down_away_ref[...] = down_acc_ref[:, away].astype(low)
    upb_grad = jnp.sum(inner_all.astype(wide), axis=0, keepdims=True)
    upb_away_ref[...] = jnp.broadcast_to(upb_grad[:, away], upb_away_ref.shape)
    halves = [
        wires.send(up_away_ref, up_got_ref, at.partner()),
        wires.send(down_away_ref, down_got_ref, at.partner()),
        wires.send(upb_away_ref, upb_got_ref, at.partner()),
    ]
    for copy in halves:
        copy.wait_recv()
    upb_ref[...] = jnp.broadcast_to(upb_grad[:, near], upb_ref.shape) + upb_got_ref[...]
    up_sum = (up_acc_ref[:, near] + up_got_ref[...].astype(wide)).astype(low)
    down_sum = (down_acc_ref[:, near] + down_got_ref[...].astype(wide)).astype(low)
    for row in range(at.batches):
        upg_ref[row] = up_sum[row * columns : (row + 1) * columns]
        downg_ref[row] = down_sum[row * columns : (row + 1) * columns]
    for k in range(1, at.batches):
        row, peer = at.along_rows(k)
        last.append(wires.send(upg_ref.at[row], ups_ref.at[b], peer))
        last.append(wires.send(downg_ref.at[row], downs_ref.at[b], peer))
        last.append(wires.send(upb_ref, upbs_ref.at[b], peer))
    own.append(wires.local(upg_ref.at[b], ups_ref.at[b]))
    own.append(wires.local(downg_ref.at[b], downs_ref.at[b]))
    own.append(wires.local(upb_ref, upbs_ref.at[b]))
    total = back_ref[z].astype(wide) + back_line.collect()
    hidden_grad = mixed_grad + total
    pre_grad = norm_back(hidden_grad, gain1, unit1, scale1)
    attn_ref[s] = pre_grad.astype(low)
    attn_line = LineGather(at, attn_ref, lambda j: 2 * j + c, (attn_send, attn_recv))
    attn_line.start()
    last.append(wires.send(attn_ref.at[s], attn_ref.at[s], at.partner()))
    pre_grad_ref[...] = pre_grad
    gain1_grad = jnp.sum(hidden_grad * unit1, axis=0, keepdims=True)
    shift1_grad = jnp.sum(hidden_grad, axis=0, keepdims=True)
    bias3_grad = jnp.sum(pre_grad, axis=0, keepdims=True)
    sums = jnp.concatenate(
        [bias3_grad, gain1_grad, gain2_grad, shift1_grad, shift2_grad, downb_grad]
        + [jnp.zeros((2, width), wide)],
        axis=0,
    )
    spare = jnp.zeros((8, BLOCK - lanes), wide)
    for part in range(at.tokens):
        sums_ref[part] = jnp.concatenate(
            [sums[:, part * lanes : (part + 1) * lanes], spare], axis=1
        )
    for t, j in enumerate(order):
        attn_line.arrive(order, t)
        home = attn_ref.at[2 * j + c]
        last.append(wires.send(home, home, at.partner()))
    for copy in last:
        copy.wait_recv()
    for copy in own:
        copy.wait()
    wires.finish()
    for line in (hid_line, ffn_line, grad_line, back_line, attn_line):
        line.drain(order)


def feed_forward(ctx, x, mixs, vecs, up, down, up2, down2, out_grad, ident):
    tokens, batches = lax.axis_size("seq"), lax.axis_size("batch")
    chips = tokens // 2
    width = x.shape[1]
    columns = width // batches
    hidden_here = up.shape[1]
    low, wide = jnp.bfloat16, jnp.float32
    outs = (
        jax.ShapeDtypeStruct(x.shape, low),
        jax.ShapeDtypeStruct(x.shape, wide),
        jax.ShapeDtypeStruct((tokens, 8, BLOCK), wide),
        jax.ShapeDtypeStruct((tokens,) + x.shape, low),
        jax.ShapeDtypeStruct((width, width), low),
        jax.ShapeDtypeStruct((batches, columns, hidden_here), low),
        jax.ShapeDtypeStruct((batches, columns, hidden_here), low),
        jax.ShapeDtypeStruct((batches, 8, hidden_here), wide),
    )
    block = (chips,) + x.shape
    wide_block = (chips, x.shape[0], 2 * hidden_here)
    slots = (chips + 1,) + x.shape
    up_half, bias_half = (width, hidden_here), (8, hidden_here)
    down_half = up_half
    scratch = [
        pltpu.VMEM(ctx.shape, low),
        pltpu.VMEM(block, low),
        pltpu.VMEM(wide_block, low),
        pltpu.VMEM(wide_block, wide),
        pltpu.VMEM(block, low),
        pltpu.VMEM(slots, low),
        pltpu.VMEM(block, low),
        pltpu.VMEM(wide_block, low),
        pltpu.VMEM(block, low),
        pltpu.VMEM(slots, low),
        pltpu.VMEM((width, 2 * hidden_here), wide),
        pltpu.VMEM((width, 2 * hidden_here), wide),
        pltpu.VMEM(up_half, low),
        pltpu.VMEM(down_half, low),
        pltpu.VMEM(bias_half, wide),
        pltpu.VMEM(up_half, low),
        pltpu.VMEM(down_half, low),
        pltpu.VMEM(bias_half, wide),
        pltpu.VMEM((batches, columns, hidden_here), low),
        pltpu.VMEM((batches, columns, hidden_here), low),
        pltpu.VMEM(bias_half, wide),
        pltpu.VMEM((16, width), wide),
    ]
    scratch += (gather_sems(chips) + reduce_sems(chips)) * 2 + gather_sems(chips)
    inputs = (ctx, x, mixs, vecs, up, down, up2, down2, out_grad)
    sends = tokens - 1 + 2 * batches - 1 + 3 + 3 * (batches - 1) + chips
    return pl.pallas_call(
        feed_kernel,
        out_shape=outs,
        in_specs=[VMEM_SPEC] * len(inputs),
        out_specs=(VMEM_SPEC,) * len(outs),
        scratch_shapes=scratch + wire_scratch(sends, 5),
        compiler_params=pltpu.CompilerParams(
            collective_id=ident, has_side_effects=True, vmem_limit_bytes=FEED_VMEM
        ),
        name="feed_forward",
    )(*inputs)


def settle_kernel(
    q_ref, k_ref, v_ref, qrev_ref, krev_ref, p_ref, mix_all_rows_ref,
    vec_ref, w_ref, xs_ref, table_ref, ctx_ref, attn_ref,
    ins_ref, vec_all_ref, cols_ref, dw_all_ref, tab_all_ref, mix_all_ref,
    in_ref, dw_ref, tab_ref, mix_ref, half_ref, sum_ref, got_ref, vecs_ref, vec_low_ref,
    dws_ref, dw_low_ref, rels_ref, rel_low_ref, mixs_ref, mix_low_ref,
    dcat_ref, rel_ref, col_ref, heads_ref, wide_ref, low_ref, place_ref, dq_ref, dkt_ref,
    dvt_ref, far_ref, dkr_ref, dqr_ref,
    line_send, line_recv, tab_send, tab_recv, *sems,
):
    at = Place()
    wires = Wires(*sems)
    low, wide = jnp.bfloat16, jnp.float32
    b, s, z, c = at.row, at.part, at.chip, at.core
    off_diagonal = b != z
    same, cross = (z, 2 * b + c), (z, 2 * b + 1 - c)
    peers = at.all_peers()
    barrier = pltpu.get_barrier_semaphore()
    for peer in peers:
        pl.semaphore_signal(barrier, inc=1, device_id=peer, device_id_type=MESH)
    attend_back_kernel(
        q_ref, k_ref, v_ref, qrev_ref, krev_ref, p_ref, mix_all_rows_ref, attn_ref,
        dcat_ref, rel_ref, col_ref, heads_ref, wide_ref, low_ref, place_ref, dq_ref, dkt_ref,
        dvt_ref, far_ref, dkr_ref, dqr_ref,
    )
    pl.semaphore_wait(barrier, len(peers))
    width = w_ref.shape[0]
    columns = width // at.batches
    full_len = dcat_ref.shape[0]
    group = 2 * DH
    buckets = table_ref.shape[0]
    bucket_rows = buckets // at.batches

    dw_sends, mix_sends, vec_sends, rel_sends, last, own = [], [], [], [], [], []
    for k in range(1, at.batches):
        row, peer = at.along_rows(k)
        rows = pl.ds(pl.multiple_of(row * bucket_rows, bucket_rows), bucket_rows)
        rel_sends.append(wires.send(rel_ref.at[rows], rels_ref.at[k - 1], peer))

    for k in range(1, at.tokens):
        part, peer = at.along_seq(k)
        vec_sends.append(wires.send(vec_ref.at[part], vecs_ref.at[k - 1], peer))
    mine = 2 * b + c
    for k in range(1, 2 * at.batches):
        last.append(wires.send(col_ref, cols_ref.at[mine], at.along_plane(k)[2]))
    own.append(wires.local(col_ref, cols_ref.at[mine]))

    def input_part(chip, core):
        start = pl.multiple_of((2 * chip + core) * BLOCK, BLOCK)
        in_ref[chip, core] = dot_nt(dcat_ref[pl.ds(start, BLOCK)], w_ref[...]).astype(low)

    order = far_order(at)
    places = order + [z]
    halves = []
    for chip in places:
        input_part(chip, 1 - c)
        halves.append(wires.send(in_ref.at[chip, 1 - c], half_ref.at[chip], at.partner()))
    line = LineReduce(at, sum_ref, got_ref, (line_send, line_recv))
    line.clear()
    for i, chip in enumerate(places):
        input_part(chip, c)
        halves[i].wait_recv()
        total = in_ref[chip, c].astype(wide) + half_ref[chip].astype(wide)
        sum_ref[chip] = total.astype(low)
        if i < len(order):
            line.send_last(chip)

    whole = xs_ref[...].reshape(full_len, width)
    dw = dot_tn(whole, dcat_ref[...])
    dw_rel = dot_tn(table_ref[...], rel_ref[...])
    dw = jnp.concatenate([dw[:, : 2 * group] + dw_rel, dw[:, 2 * group :]], axis=1)
    for row in range(at.batches):
        dw_ref[row] = dw[row * columns : (row + 1) * columns].astype(low)
    for k in range(1, at.batches):
        row, peer = at.along_rows(k)
        dw_sends.append(wires.send(dw_ref.at[row], dws_ref.at[k - 1], peer))

    rows = pl.ds(pl.multiple_of(b * bucket_rows, bucket_rows), bucket_rows)
    total = rel_ref[rows].astype(wide)
    for k in range(1, at.batches):
        rel_sends[k - 1].wait_recv()
        total = total + rels_ref[k - 1].astype(wide)
    rel_low_ref[...] = total.astype(low)
    table_rows = bucket_rows // 2
    for row in range(at.batches):
        piece = dot_nt(rel_low_ref[...], w_ref[row * columns : (row + 1) * columns, : 2 * group])
        for core in range(2):
            tab_ref[core, row] = piece[core * table_rows : (core + 1) * table_rows].astype(low)

    def tab_copy(k, d):
        row = lax.rem(b + k, at.batches)
        core = jnp.where(d == 0, c, 1 - c)
        return pltpu.make_async_remote_copy(
            src_ref=tab_ref.at[core, row],
            dst_ref=tab_all_ref.at[s],
            send_sem=tab_send.at[2 * k + d],
            recv_sem=tab_recv.at[s],
            device_id=(row, 2 * b + core),
            device_id_type=MESH,
        )

    tab_stay = pltpu.make_async_copy(
        tab_ref.at[c, b], tab_all_ref.at[s], sems[2].at[wires.used[1]]
    )
    wires.used[1] += 1
    for k in range(at.batches):
        for d in range(2):
            if k or d:
                tab_copy(k, d).start()

    @pl.when(off_diagonal)
    def _():
        tab_copy(0, 0).start()

    @pl.when(jnp.logical_not(off_diagonal))
    def _():
        tab_stay.start()

    line.pass_on(order[:1])
    mix = dot_tn(
        ctx_ref[...].reshape(full_len, group), attn_ref[...].reshape(full_len, width)
    )
    for row in range(at.batches):
        mix_ref[row] = mix[:, row * columns : (row + 1) * columns].astype(low)
    for k in range(1, at.batches):
        row, peer = at.along_rows(k)
        mix_sends.append(wires.send(mix_ref.at[row], mixs_ref.at[k - 1], peer))

    line.pass_on(order[1:])
    total = dw_ref[b].astype(wide)
    for k in range(1, at.batches):
        dw_sends[k - 1].wait_recv()
        total = total + dws_ref[k - 1].astype(wide)
    shard_rows = dw_low_ref.shape[1]
    for half in range(2):
        dw_low_ref[half] = total[half * shard_rows : (half + 1) * shard_rows].astype(low)
    k = wires.used[0]
    wires.used[0] += 1
    move = pltpu.make_async_remote_copy(
        src_ref=dw_low_ref.at[c],
        dst_ref=dw_all_ref.at[c],
        send_sem=sems[0].at[k],
        recv_sem=sems[1].at[k],
        device_id=same,
        device_id_type=MESH,
    )
    stay = pltpu.make_async_copy(
        dw_low_ref.at[c], dw_all_ref.at[c], sems[2].at[wires.used[1]]
    )
    wires.used[1] += 1

    @pl.when(off_diagonal)
    def _():
        move.start()

    @pl.when(jnp.logical_not(off_diagonal))
    def _():
        stay.start()

    last.append(wires.send(dw_low_ref.at[1 - c], dw_all_ref.at[c], cross))

    total = mix_ref[b].astype(wide)
    for k in range(1, at.batches):
        mix_sends[k - 1].wait_recv()
        total = total + mixs_ref[k - 1].astype(wide)
    mix_low_ref[...] = total.astype(low)
    last.append(wires.send(mix_low_ref, mix_all_ref.at[c], at.partner()))
    own.append(wires.local(mix_low_ref, mix_all_ref.at[c]))

    total = vec_ref[s]
    for k in range(1, at.tokens):
        vec_sends[k - 1].wait_recv()
        total = total + vecs_ref[k - 1]
    vec_low_ref[...] = total
    for k in range(1, at.batches):
        last.append(wires.send(vec_low_ref, vec_all_ref.at[b], at.along_rows(k)[1]))
    own.append(wires.local(vec_low_ref, vec_all_ref.at[b]))

    ins_ref[...] = sum_ref[z].astype(wide) + line.collect()
    for copy in last:
        copy.wait_recv()
    for copy in own:
        copy.wait()
    wires.finish()
    line.drain(order)
    for part in range(at.tokens):
        landed = pltpu.make_async_remote_copy(
            src_ref=tab_all_ref.at[part],
            dst_ref=tab_all_ref.at[part],
            send_sem=tab_send.at[0],
            recv_sem=tab_recv.at[part],
            device_id=at.partner(),
            device_id_type=MESH,
        )

        @pl.when(jnp.logical_or(off_diagonal, s != part))
        def _():
            landed.wait_recv()

    for k in range(at.batches):
        for d in range(2):
            if k or d:
                tab_copy(k, d).wait_send()

    @pl.when(off_diagonal)
    def _():
        tab_copy(0, 0).wait_send()
        move.wait()

    @pl.when(jnp.logical_not(off_diagonal))
    def _():
        tab_stay.wait()
        stay.wait()


def settle_grads(q, k, v, qrev, krev, probs, m_mix, vec, w_cat, xs, table, ctx, attn_all, ident):
    tokens, batches = lax.axis_size("seq"), lax.axis_size("batch")
    chips = tokens // 2
    low, wide = jnp.bfloat16, jnp.float32
    local_len, width = xs.shape[1:]
    columns, group = width // batches, 6 * DH
    buckets = table.shape[0]
    full_len = tokens * local_len
    band_width = buckets + BLOCK
    pad_blocks = full_len // BLOCK + band_width // BLOCK - 1
    half = (chips, local_len, width)
    dw_pieces = (2, columns // 2, group)
    mix_piece = (2 * DH, columns)
    dw_piece, rel_piece = (columns, group), (buckets // batches, 4 * DH)
    outs = (
        jax.ShapeDtypeStruct((local_len, width), wide),
        jax.ShapeDtypeStruct((batches,) + vec.shape[1:], wide),
        jax.ShapeDtypeStruct((2 * batches, 8, group), wide),
        jax.ShapeDtypeStruct(dw_pieces, low),
        jax.ShapeDtypeStruct((tokens, buckets // tokens, columns), low),
        jax.ShapeDtypeStruct((2,) + mix_piece, low),
    )
    scratch = [
        pltpu.VMEM((chips, 2, local_len, width), low),
        pltpu.VMEM((batches,) + dw_piece, low),
        pltpu.VMEM((2, batches, buckets // tokens, columns), low),
        pltpu.VMEM((batches,) + mix_piece, low),
        pltpu.VMEM(half, low),
        pltpu.VMEM(half, low),
        pltpu.VMEM((chips + 1, local_len, width), low),
        pltpu.VMEM((tokens - 1,) + vec.shape[1:], wide),
        pltpu.VMEM(vec.shape[1:], wide),
        pltpu.VMEM((batches - 1,) + dw_piece, low),
        pltpu.VMEM(dw_pieces, low),
        pltpu.VMEM((batches - 1,) + rel_piece, low),
        pltpu.VMEM(rel_piece, low),
        pltpu.VMEM((batches - 1,) + mix_piece, low),
        pltpu.VMEM(mix_piece, low),
        pltpu.VMEM((full_len, group), low),
        pltpu.VMEM((buckets, 4 * DH), low),
        pltpu.VMEM((8, group), wide),
        pltpu.VMEM((2, full_len, DH), low),
        pltpu.VMEM((2, BLOCK, full_len + buckets), wide),
        pltpu.VMEM((2, BLOCK, full_len + buckets), low),
        pltpu.VMEM((2, pad_blocks, BLOCK, band_width), wide),
        pltpu.VMEM((4, full_len, DH), wide),
        pltpu.VMEM((2, DH, full_len), wide),
        pltpu.VMEM((2, DH, full_len), wide),
        pltpu.VMEM((2, 8, full_len), wide),
        pltpu.VMEM((2, DH, buckets), wide),
        pltpu.VMEM((2, DH, buckets), wide),
    ]
    scratch += reduce_sems(chips)
    scratch += [pltpu.SemaphoreType.DMA((2 * batches,)), pltpu.SemaphoreType.DMA((tokens,))]
    sends = 4 * (batches - 1) + chips + tokens - 1 + 2 * batches - 1 + 3
    inputs = (q, k, v, qrev, krev, probs, m_mix, vec, w_cat, xs, table, ctx, attn_all)
    return comm_call(
        settle_kernel,
        "settle_grads",
        ident,
        outs,
        inputs,
        sends,
        6,
        scratch=scratch,
        limit=BACK_VMEM,
    )


def finish_kernel(
    pre_ref, ins_ref, vecs_ref, cols_ref, dws_ref, tabs_ref, mixs_ref, ups_ref, downs_ref,
    upbs_ref, last_ref,
    output_ref, input_ref, dq_ref, dk_ref, dv_ref, mix_ref, table_ref, bias_ref, gain_ref, shift_ref,
    up_ref, upb_ref, down_ref, downb_ref,
):
    at = Place()
    wide = jnp.float32

    def total(ref):
        out = ref[0].astype(wide)
        for k in range(1, ref.shape[0]):
            out = out + ref[k].astype(wide)
        return out

    output_ref[...] = last_ref[...]
    input_ref[...] = pre_ref[...] + ins_ref[...]
    up_ref[...] = total(ups_ref)
    down_ref[...] = total(downs_ref)
    upb_ref[...] = total(upbs_ref)[0:1]
    table_ref[...] = total(tabs_ref)
    group = 2 * DH
    spare = jnp.zeros((dws_ref.shape[1], DH), wide)
    for i, ref in enumerate((dq_ref, dk_ref, dv_ref)):
        lower = dws_ref[0, :, i * group : (i + 1) * group].astype(wide)
        upper = dws_ref[1, :, i * group : (i + 1) * group].astype(wide)
        ref[...] = jnp.concatenate([lower, spare], axis=1) + jnp.concatenate(
            [spare, upper], axis=1
        )
    rows = mix_ref.shape[0]
    lower, upper = mixs_ref[0].astype(wide), mixs_ref[1].astype(wide)
    spare = jnp.zeros((DH, lower.shape[1]), wide)
    whole = jnp.concatenate([lower, spare], axis=0) + jnp.concatenate([spare, upper], axis=0)
    mix_ref[...] = jnp.where(at.core == 0, whole[:rows], whole[rows:])
    small = total(vecs_ref)
    lanes = bias_ref.shape[1]
    cols = [cols_ref[core, 0:1] for core in range(2)]
    for row in range(1, at.batches):
        cols = [cols[core] + cols_ref[2 * row + core, 0:1] for core in range(2)]
    spare = jnp.zeros((1, DH), wide)
    biases = []
    for i in range(3):
        lower, upper = [part[:, i * group : (i + 1) * group] for part in cols]
        both = jnp.concatenate([lower, spare], axis=1) + jnp.concatenate([spare, upper], axis=1)
        biases.append(jnp.where(at.core == 0, both[:, :lanes], both[:, lanes:]))
    bias_ref[...] = jnp.concatenate(biases + [small[0:1, :lanes]], axis=0)
    gain_ref[...] = small[1:3, :lanes]
    shift_ref[...] = small[3:5, :lanes]
    downb_ref[...] = small[5:6, :lanes]


def finish(pre_grad, parts, shapes):
    inputs = (pre_grad,) + tuple(parts)
    return pl.pallas_call(
        finish_kernel,
        out_shape=(like(parts[-1]),)
        + tuple(jax.ShapeDtypeStruct(shape, jnp.float32) for shape in shapes),
        in_specs=[VMEM_SPEC] * len(inputs),
        out_specs=(VMEM_SPEC,) * (len(shapes) + 1),
        compiler_params=pltpu.CompilerParams(vmem_limit_bytes=COMM_VMEM),
        name="finish",
    )(*inputs)


def fits_fast(layer_input, table_shard, hidden_here):
    rows, local_len, width = layer_input.shape
    tokens, batches = lax.axis_size("seq"), lax.axis_size("batch")
    return (
        rows == 1
        and local_len == BLOCK
        and tokens == 2 * batches
        and width == 3 * DH * batches
        and (table_shard.shape[0] * tokens) % (4 * BLOCK) == 0
        and tokens == 8
        and 10 + hidden_here // BLOCK <= 16
        and hidden_here % BLOCK == 0
    )


def fast_body(
    layer_input, segment_ids, w_query, w_key, w_value, w_mix, rel_table, attn_biases,
    norm_gains, norm_shifts, w_up, up_bias, w_down, down_bias, out_grad,
):
    local_len, width = layer_input.shape[1:]
    low = jnp.bfloat16
    shard_rows, shard_cols = w_query.shape
    lanes = attn_biases.shape[1]
    hidden_here = w_up.shape[1]
    x = layer_input[0]
    pack = jnp.concatenate([attn_biases, norm_gains, norm_shifts, down_bias[None]], axis=0)
    pack = jnp.pad(pack, ((0, 0), (0, BLOCK - lanes)))
    pack = jnp.concatenate(
        [pack, segment_ids.astype(low), up_bias.reshape(hidden_here // BLOCK, BLOCK)], axis=0
    )
    pack = jnp.pad(pack, ((0, 16 - pack.shape[0]), (0, 0)))
    weights = (w_query, w_key, w_value, w_mix, rel_table, pack, w_up, w_down)
    gathered = gather_inputs(
        *[pltpu.with_memory_space_constraint(a, pltpu.HBM) for a in (x,) + weights]
    )
    xs, mixs, vecs, up2, down2 = gathered[:5]
    q, k, v, qrev, krev, probs, ctx, w_cat, table = gathered[5:]
    output, pre_grad, sums, attn_all, m_mix, ups, downs, upbs = feed_forward(
        ctx, x, mixs, vecs, w_up, w_down, up2, down2, out_grad[0], 1
    )
    ins, vec_all, cols_all, dw_all, tab_all, mix_all = settle_grads(
        q, k, v, qrev, krev, probs, m_mix, sums, w_cat, xs, table, ctx, attn_all, 2
    )
    shard = (shard_rows, shard_cols)
    shapes = (
        x.shape, shard, shard, shard, shard, rel_table.shape, (4, lanes), (2, lanes), (2, lanes),
        (width // lax.axis_size("batch"), hidden_here), (1, hidden_here),
        (width // lax.axis_size("batch"), hidden_here), (1, lanes),
    )
    grads = finish(
        pre_grad,
        (ins, vec_all, cols_all, dw_all, tab_all, mix_all, ups, downs, upbs, output),
        shapes,
    )
    output, input_grad, dq, dk, dv, dmix, dtable = grads[:7]
    dbias, dgain, dshift, dup, dupb, ddown, ddownb = grads[7:]
    return (
        output[None], input_grad[None], dq, dk, dv, dmix, dtable, dbias, dgain, dshift,
        dup, dupb.reshape(hidden_here), ddown.T, ddownb.reshape(lanes),
    )


def body(
    layer_input,
    segment_ids,
    w_query,
    w_key,
    w_value,
    w_mix,
    rel_table,
    attn_biases,
    norm_gains,
    norm_shifts,
    w_up,
    up_bias,
    w_down,
    down_bias,
    out_grad,
):
    if fits_fast(layer_input, rel_table, w_up.shape[1]):
        return fast_body(
            layer_input, segment_ids, w_query, w_key, w_value, w_mix, rel_table, attn_biases,
            norm_gains, norm_shifts, w_up, up_bias, w_down, down_bias, out_grad,
        )
    rows, local_len, width = layer_input.shape
    full_len = local_len * lax.axis_size("seq")
    tokens_here = local_len * rows
    highest_prec = lax.Precision.HIGHEST
    parts = (
        lax.all_gather(w_query, "batch", axis=1, tiled=True),
        lax.all_gather(w_key, "batch", axis=1, tiled=True),
        lax.all_gather(w_value, "batch", axis=1, tiled=True),
        lax.all_gather(w_mix, "batch", axis=1, tiled=True),
        lax.all_gather(rel_table, "batch", axis=1, tiled=True),
    )
    whole = (
        lax.all_gather(parts[0], "seq", axis=0, tiled=True),
        lax.all_gather(parts[1], "seq", axis=0, tiled=True),
        lax.all_gather(parts[2], "seq", axis=0, tiled=True),
        lax.all_gather(parts[3], "seq", axis=0, tiled=True),
        lax.all_gather(parts[4], "seq", axis=0, tiled=True),
        lax.all_gather(attn_biases, "seq", axis=1, tiled=True),
        lax.all_gather(norm_gains, "seq", axis=1, tiled=True),
        lax.all_gather(norm_shifts, "seq", axis=1, tiled=True),
        lax.all_gather(down_bias, "seq", axis=0, tiled=True),
    )
    m_query, m_key, m_value, m_mix, table, biases, gains, shifts, bias_down = whole
    flat_input = jnp.swapaxes(layer_input, 0, 1).reshape(tokens_here, width)
    queries = (jnp.dot(flat_input, m_query, preferred_element_type=jnp.float32) + biases[0]).astype(
        jnp.bfloat16
    )
    keys_here = (jnp.dot(flat_input, m_key, preferred_element_type=jnp.float32) + biases[1]).astype(
        jnp.bfloat16
    )
    values_here = (
        jnp.dot(flat_input, m_value, preferred_element_type=jnp.float32) + biases[2]
    ).astype(jnp.bfloat16)
    query_rel = (jnp.dot(table, m_query, preferred_element_type=jnp.float32) + biases[0]).astype(
        jnp.bfloat16
    )
    key_rel = (jnp.dot(table, m_key, preferred_element_type=jnp.float32) + biases[1]).astype(
        jnp.bfloat16
    )
    local_seg = jnp.swapaxes(segment_ids, 0, 1).astype(jnp.bfloat16)
    keys_all, values_all, seg_all = (
        lax.all_gather(keys_here.reshape(local_len, rows, width), "seq", axis=0, tiled=True),
        lax.all_gather(values_here.reshape(local_len, rows, width), "seq", axis=0, tiled=True),
        lax.all_gather(local_seg, "seq", axis=0, tiled=True),
    )
    buckets = table.shape[0]
    offset = lax.axis_index("seq") * local_len
    bucket_iota = jnp.arange(buckets, dtype=jnp.int32)
    inner_cols = (bucket_iota > 0) & (bucket_iota < buckets - 1)
    same_doc = (
        jnp.swapaxes(local_seg, 0, 1)[:, None, :, None]
        == jnp.swapaxes(seg_all, 0, 1)[:, None, None, :]
    )
    score_scale = 1.0 / math.sqrt(3.0 * DH)
    head_queries = split_heads(queries.reshape(local_len, rows, width))
    head_keys = split_heads(keys_all)
    head_values = split_heads(values_all)
    rel_queries = split_table(query_rel)
    rel_keys = split_table(key_rel)

    def forward_group(carry, group):
        g_query, g_key, g_value, g_qrel, g_krel = group
        total, near_pull, far_pull, window = relative_scores(
            g_query, g_key, g_krel, g_qrel, offset, full_len
        )
        scores = jnp.where(same_doc, total * score_scale, masked_score)
        highest = jnp.max(scores, axis=-1, keepdims=True)
        exponent = jnp.exp(scores - highest)
        denominator = jnp.sum(exponent, axis=-1, keepdims=True)
        weights_low = (exponent / denominator).astype(jnp.bfloat16)
        context = jnp.einsum(
            "rgij,rgjd->rgid", weights_low, g_value, preferred_element_type=jnp.float32
        )
        return (carry, (context, (highest + jnp.log(denominator))[..., 0]))

    unused, (context_groups, log_totals) = lax.scan(
        forward_group, None, (head_queries, head_keys, head_values, rel_queries, rel_keys)
    )
    context_low = join_heads(context_groups).reshape(tokens_here, width).astype(jnp.bfloat16)
    pre_norm = (
        flat_input.astype(jnp.float32)
        + jnp.dot(context_low, m_mix, preferred_element_type=jnp.float32)
        + biases[3]
    )
    hidden, norm1_pull = jax.vjp(
        normalize, pre_norm, gains[0].astype(jnp.float32), shifts[0].astype(jnp.float32)
    )
    hidden_low = hidden.astype(jnp.bfloat16)

    def spread_rows(rows_low):
        return lax.all_gather(rows_low, "seq", axis=0, tiled=True)

    def hidden_sums(make_term):
        return lax.psum_scatter(
            make_term(jnp.int32(0), tokens_here * lax.axis_size("seq")),
            "seq",
            scatter_dimension=0,
            tiled=True,
        )

    hidden_rows = spread_rows(hidden_low)
    inner = jnp.dot(hidden_rows, w_up, preferred_element_type=jnp.float32) + up_bias
    act, gelu_pull = jax.vjp(exact_gelu, inner)
    act_low = act.astype(jnp.bfloat16)

    def down_rows(start, count):
        return jnp.dot(act_low, w_down, preferred_element_type=jnp.float32)

    ffn_result = hidden_sums(down_rows)
    mixed = hidden + ffn_result + bias_down
    output, norm2_pull = jax.vjp(
        normalize, mixed, gains[1].astype(jnp.float32), shifts[1].astype(jnp.float32)
    )
    flat_grad = jnp.swapaxes(out_grad, 0, 1).reshape(tokens_here, width).astype(jnp.float32)
    mixed_grad, gain2_grad, shift2_grad = norm2_pull(flat_grad)
    ffn_grad_low = mixed_grad.astype(jnp.bfloat16)
    grad_rows = spread_rows(ffn_grad_low)
    act_grad = jnp.einsum("nd,fd->nf", grad_rows, w_down, preferred_element_type=jnp.float32)
    inner_low = gelu_pull(act_grad)[0].astype(jnp.bfloat16)
    up_part = jnp.einsum("nd,nf->df", hidden_rows, inner_low, preferred_element_type=jnp.float32)
    upb_part = jnp.sum(inner_low.astype(jnp.float32), axis=0)
    down_part = jnp.einsum("nf,nd->fd", act_low, grad_rows, preferred_element_type=jnp.float32)

    def back_rows(start, count):
        return jnp.einsum("nf,df->nd", inner_low, w_up, preferred_element_type=jnp.float32)

    hidden_grad = mixed_grad + hidden_sums(back_rows)
    pre_grad, gain1_grad, shift1_grad = norm1_pull(hidden_grad)
    attn_low = pre_grad.astype(jnp.bfloat16)
    mix_whole = jnp.einsum("nd,ne->de", context_low, attn_low, preferred_element_type=jnp.float32)
    context_grad = jnp.einsum(
        "ne,de->nd", attn_low, m_mix, preferred_element_type=jnp.float32
    ).astype(jnp.bfloat16)
    head_context_grad = split_heads(context_grad.reshape(local_len, rows, width))

    def query_side(group):
        g_query, g_key, g_value, g_qrel, g_krel, g_dctx, g_lse = group
        total, near_pull, far_pull, window = relative_scores(
            g_query, g_key, g_krel, g_qrel, offset, full_len
        )
        scores = jnp.where(same_doc, total * score_scale, masked_score)
        weights_now = jnp.exp(scores - g_lse[..., None])
        prob_grad = jnp.einsum(
            "rgid,rgjd->rgij", g_dctx, g_value, preferred_element_type=jnp.float32
        )
        inner_sum = jnp.sum(weights_now * prob_grad, axis=-1)
        score_grad = (weights_now * (prob_grad - inner_sum[..., None])).astype(jnp.bfloat16)
        grad_wide = score_grad.astype(jnp.float32)
        near_grad = near_pull(grad_wide)[0]
        near_low = jnp.where(inner_cols, near_grad, 0.0).astype(jnp.bfloat16)
        near_ends = end_columns(near_grad)
        query_part = jnp.einsum(
            "rgij,rgjd->rgid", score_grad, g_key, preferred_element_type=jnp.float32
        )
        query_part = (
            query_part
            + jnp.einsum("rgib,gbd->rgid", near_low, g_krel, preferred_element_type=jnp.float32)
            + end_terms(near_ends, g_krel)
        )
        krel_part = with_ends(
            jnp.einsum("rgib,rgid->gbd", near_low, g_query, preferred_element_type=jnp.float32),
            end_rows(near_ends, g_query),
        )
        return (
            weights_now,
            score_grad,
            grad_wide,
            far_pull,
            window,
            inner_sum,
            query_part * score_scale,
            krel_part * score_scale,
        )

    query_groups = (
        head_queries,
        head_keys,
        head_values,
        rel_queries,
        rel_keys,
        head_context_grad,
        log_totals,
    )

    def all_grads(carry, group):
        weights_now, score_grad, grad_wide, far_pull, window, inner_sum, query_part, krel_part = (
            query_side(group)
        )
        g_query, g_key, g_value, g_qrel, g_krel, g_dctx, g_lse = group
        cross_grad, end_grad = far_pull(grad_wide)
        cross_low = cross_grad.astype(jnp.bfloat16)
        key_part = jnp.einsum(
            "rgij,rgid->rgjd", score_grad, g_query, preferred_element_type=jnp.float32
        )
        band_part = jnp.einsum(
            "rgmb,gbd->rgmd", cross_low, g_qrel, preferred_element_type=jnp.float32
        )
        key_part = (
            key_part
            + unband(band_part, offset, full_len, buckets // 2)
            + end_terms(end_grad, g_qrel)
        )
        value_part = jnp.einsum(
            "rgij,rgid->rgjd",
            weights_now.astype(jnp.bfloat16),
            g_dctx,
            preferred_element_type=jnp.float32,
        )
        qrel_part = with_ends(
            jnp.einsum("rgmb,rgmd->gbd", cross_low, window, preferred_element_type=jnp.float32),
            end_rows(end_grad, g_key),
        )
        return (
            carry,
            (query_part, key_part * score_scale, value_part, qrel_part * score_scale, krel_part),
        )

    unused, (dq_groups, dk_groups, dv_groups, dqrel_groups, dkrel_groups) = lax.scan(
        all_grads, None, query_groups
    )
    key_sum, value_sum = (
        lax.psum_scatter(join_heads(dk_groups), "seq", scatter_dimension=0, tiled=True),
        lax.psum_scatter(join_heads(dv_groups), "seq", scatter_dimension=0, tiled=True),
    )
    key_grads = key_sum.reshape(tokens_here, width).astype(jnp.bfloat16)
    value_grads = value_sum.reshape(tokens_here, width).astype(jnp.bfloat16)
    query_grads = join_heads(dq_groups).reshape(tokens_here, width).astype(jnp.bfloat16)
    qrel_grad = join_table(dqrel_groups)
    krel_grad = join_table(dkrel_groups)
    input_grad = pre_grad + jnp.einsum(
        "ne,de->nd", query_grads, m_query, preferred_element_type=jnp.float32
    )
    input_grad = input_grad + jnp.einsum(
        "ne,de->nd", key_grads, m_key, preferred_element_type=jnp.float32
    )
    input_grad = input_grad + jnp.einsum(
        "ne,de->nd", value_grads, m_value, preferred_element_type=jnp.float32
    )
    query_whole = jnp.einsum(
        "nd,ne->de", flat_input, query_grads, preferred_element_type=jnp.float32
    ) + jnp.einsum(
        "bd,be->de", table, qrel_grad, precision=highest_prec, preferred_element_type=jnp.float32
    )
    key_whole = jnp.einsum(
        "nd,ne->de", flat_input, key_grads, preferred_element_type=jnp.float32
    ) + jnp.einsum(
        "bd,be->de", table, krel_grad, precision=highest_prec, preferred_element_type=jnp.float32
    )
    value_whole = jnp.einsum(
        "nd,ne->de", flat_input, value_grads, preferred_element_type=jnp.float32
    )
    table_whole = jnp.einsum(
        "be,de->bd", qrel_grad, m_query, precision=highest_prec, preferred_element_type=jnp.float32
    ) + jnp.einsum(
        "be,de->bd", krel_grad, m_key, precision=highest_prec, preferred_element_type=jnp.float32
    )
    bias_whole = jnp.stack(
        [
            jnp.sum(query_grads.astype(jnp.float32), axis=0) + jnp.sum(qrel_grad, axis=0),
            jnp.sum(key_grads.astype(jnp.float32), axis=0) + jnp.sum(krel_grad, axis=0),
            jnp.sum(value_grads.astype(jnp.float32), axis=0),
            jnp.sum(pre_grad, axis=0),
        ]
    )
    gain_whole = jnp.stack([gain1_grad, gain2_grad])
    shift_whole = jnp.stack([shift1_grad, shift2_grad])
    downb_whole = jnp.sum(mixed_grad, axis=0)
    seq_parts = (
        lax.psum_scatter(query_whole, "seq", scatter_dimension=0, tiled=True),
        lax.psum_scatter(key_whole, "seq", scatter_dimension=0, tiled=True),
        lax.psum_scatter(value_whole, "seq", scatter_dimension=0, tiled=True),
        lax.psum_scatter(mix_whole, "seq", scatter_dimension=0, tiled=True),
        lax.psum_scatter(table_whole, "seq", scatter_dimension=0, tiled=True),
        lax.psum_scatter(bias_whole, "seq", scatter_dimension=1, tiled=True),
        lax.psum_scatter(gain_whole, "seq", scatter_dimension=1, tiled=True),
        lax.psum_scatter(shift_whole, "seq", scatter_dimension=1, tiled=True),
        lax.psum_scatter(downb_whole, "seq", scatter_dimension=0, tiled=True),
    )
    batch_parts = (
        lax.psum_scatter(seq_parts[0], "batch", scatter_dimension=1, tiled=True),
        lax.psum_scatter(seq_parts[1], "batch", scatter_dimension=1, tiled=True),
        lax.psum_scatter(seq_parts[2], "batch", scatter_dimension=1, tiled=True),
        lax.psum_scatter(seq_parts[3], "batch", scatter_dimension=1, tiled=True),
        lax.psum_scatter(seq_parts[4], "batch", scatter_dimension=1, tiled=True),
        lax.psum_scatter(up_part, "batch", scatter_dimension=0, tiled=True),
        lax.psum_scatter(down_part, "batch", scatter_dimension=1, tiled=True),
    )
    small_parts = lax.psum(
        (seq_parts[5], seq_parts[6], seq_parts[7], seq_parts[8], upb_part), "batch"
    )
    layer_output = jnp.swapaxes(output.reshape(local_len, rows, width), 0, 1).astype(jnp.bfloat16)
    input_back = jnp.swapaxes(input_grad.reshape(local_len, rows, width), 0, 1)
    return (
        layer_output,
        input_back,
        batch_parts[0],
        batch_parts[1],
        batch_parts[2],
        batch_parts[3],
        batch_parts[4],
        small_parts[0],
        small_parts[1],
        small_parts[2],
        batch_parts[5],
        small_parts[4],
        batch_parts[6],
        small_parts[3],
    )


def solution(mesh):
    return jax.shard_map(
        body,
        mesh=mesh,
        in_specs=(
            P("batch", "seq", None),
            P("batch", "seq"),
            P("seq", "batch"),
            P("seq", "batch"),
            P("seq", "batch"),
            P("seq", "batch"),
            P("seq", "batch"),
            P(None, "seq"),
            P(None, "seq"),
            P(None, "seq"),
            P(None, "seq"),
            P("seq"),
            P("seq", None),
            P("seq"),
            P("batch", "seq", None),
        ),
        out_specs=(
            P("batch", "seq", None),
            P("batch", "seq", None),
            P("seq", "batch"),
            P("seq", "batch"),
            P("seq", "batch"),
            P("seq", "batch"),
            P("seq", "batch"),
            P(None, "seq"),
            P(None, "seq"),
            P(None, "seq"),
            P("batch", "seq"),
            P("seq"),
            P("seq", "batch"),
            P("seq"),
        ),
        check_vma=False,
    )
```
